32 devices in a mesh: dp: 8 (over z, x), expert: 4 (over y, core).
Axes of the slice: x: 2, y: 2, z: 4, core: 2. Of those that a mesh axis runs over, the one named last changes fastest.
Arguments:
- tokens: bfloat16 [32, 1024, 768], P(('dp', 'expert')), may hold values from -6 to 6
- resid_logits: bfloat16 [32, 1024, 12], P(('dp', 'expert')), may hold values from -3 to 3
- routes: int32 [32, 1024, 2], P(('dp', 'expert')), may hold values from 0 to 11, all different within a row; in each aligned block of 1024 rows (0 to 1023, 1024 to 2047, ..., all dimensions but the last counted through in order) at most 256 rows name the same one
- doc_ids: int32 [32, 1024], P(('dp', 'expert')), may hold values from 0 to 3, never falling along the last dimension, each value on 1 to 512 neighbouring positions
- w_qkv: bfloat16 [768, 2304], P('dp'), may hold values from -0.21875 to 0.21875
- w_out: bfloat16 [768, 768], P('dp'), may hold values from -1.75 to 1.75
- gain_attn: bfloat16 [768], P('dp'), may hold values from 0.25 to 1.75
- gain_ffn: bfloat16 [768], P('dp'), may hold values from 0.25 to 1.75
- w_router: bfloat16 [768, 12], P('dp'), may hold values from -0.15625 to 0.15625
- w_const: bfloat16 [768, 4], P('dp'), may hold values from -0.21875 to 0.21875
- v_const: bfloat16 [768, 2], P('dp'), may hold values from -5 to 5
- w_gate_up: bfloat16 [8, 768, 4096], P('expert', 'dp'), may hold values from -0.21875 to 0.21875
- w_down: bfloat16 [8, 2048, 768], P('expert', 'dp'), may hold values from -0.1875 to 0.1875
- out_grad: bfloat16 [32, 1024, 768], P(('dp', 'expert')), may hold values from -6 to 6
Outputs:
- output: bfloat16 [32, 1024, 768], P(('dp', 'expert'))
- token_grad: bfloat16 [32, 1024, 768], P(('dp', 'expert'))
- logit_grad: bfloat16 [32, 1024, 12], P(('dp', 'expert'))
- grad_w_qkv: float32 [768, 2304], P('dp')
- grad_w_out: float32 [768, 768], P('dp')
- grad_gain_attn: float32 [768], P('dp')
- grad_gain_ffn: float32 [768], P('dp')
- grad_w_router: float32 [768, 12], P('dp')
- grad_w_const: float32 [768, 4], P('dp')
- grad_v_const: float32 [768, 2], P('dp')
- grad_w_gate_up: float32 [8, 768, 4096], P('expert', 'dp')
- grad_w_down: float32 [8, 2048, 768], P('expert', 'dp')
The draws below stay inside these ranges and needn't reach their ends.
Inputs may be any that keep to these rules, and one draw needn't show every extreme that they name: A token's two routes differ. Numbers below 8 are feed-forward experts, 8 the zero expert, 9 the copy expert, 10 + k constant expert k. Among the tokens of one device no number is named more than 256 times. `doc_ids`: Non-decreasing along each sequence; a document covers 1 to 512 positions.
All inputs are finite; a program needn't handle non-finite values.
Results may differ from the reference program's by a relative error of at most 0.02.
Values may be sent and summed in bfloat16 or wider, within the bound.
A program may use at most 320 MiB of HBM per device.

```python
import math
import jax
import jax.numpy as jnp
import numpy as np
from jax import lax

D = 768
HEADS = 12
FF = 2048
EXPERTS = 8
NCONST = 2
CHOICES = 12
BLOCK = 256
SEQ_LEN = 1024
DOCS = 4
TOK_DEV = 1024
SEQS = 32
CAP = 256


def steps_of(stream_key, shape, split, low, top_value):
    factor_of, own = 1.0, jax.random.fold_in(stream_key, 6)
    for axis_at, parts in split:
        heights = jnp.exp(jax.random.uniform(jax.random.fold_in(own, axis_at), (parts,), jnp.float32, low / len(split), top_value / len(split)))
        factor_of = factor_of * jnp.repeat(heights, shape[axis_at] // parts).reshape([-1 if axis == axis_at else 1 for axis in range(len(shape))])
    return factor_of


def length_profile(count, total, limit, lean):
    weights = [(1 << 20) // math.isqrt(rank ** lean) + 1 for rank in range(2, count + 1)]
    rest, holding = total - limit - (count - 1), [1] * (count - 1)
    while rest > 0:
        movable = [i for i in range(count - 1) if holding[i] < limit]
        pool, left = sum([weights[i] for i in movable]), rest
        for i in movable:
            addition = min(limit - holding[i], max(1, left * weights[i] // pool), rest)
            holding[i] = holding[i] + addition
            rest = rest - addition
    return np.array([limit] + holding)


def ragged(rng, number_of, total, bound, slope):
    if number_of == 2:
        one = jax.random.randint(rng, (), max(1, total - bound), min(bound, total - 1) + 1)
        return jnp.stack([one, total - one])
    sizes = jnp.asarray(length_profile(number_of, total, bound, slope), jnp.int32)
    pairs = (number_of - 1) // 2
    giver, sink = sizes[1:1 + 2 * pairs:2], sizes[2:2 + 2 * pairs:2]
    margin = jnp.minimum(giver - 1, bound - sink)
    passed = jax.random.randint(jax.random.fold_in(rng, 1), (pairs,), 0, 1 << 20) % (margin + 1)
    sizes = sizes.at[1:1 + 2 * pairs:2].set(giver - passed).at[2:2 + 2 * pairs:2].set(sink + passed)
    return sizes[jax.random.permutation(jax.random.fold_in(rng, 2), number_of)]


def deal_out(rng, own, number, rows, amount, top, reach, skew):
    order = jax.random.permutation(rng, amount)
    packed, ordinary = portions_of(amount, rows * top, reach, skew, True), portions_of(amount, rows * top, reach, skew, False)
    places = jnp.arange(amount)

    def named(tallies, turn):
        used = int((tallies > 0).sum())
        fixed = max(1, used // 4)
        moved = fixed + (places - fixed + turn * (used - fixed)) % max(1, amount - fixed)
        return jnp.zeros((amount,), jnp.int32).at[order[jnp.where(places < fixed, places, moved)]].set(jnp.asarray(tallies, jnp.int32))

    tallies = jnp.where(number % 4 == 0, named(packed, number // 4), named(ordinary, number - number // 4 - 1))
    mixed = jax.random.permutation(jax.random.fold_in(own, 3), amount)
    giver, receiver = mixed[0:amount // 2 * 2:2], mixed[1:amount // 2 * 2:2]
    room = jnp.minimum(tallies[giver] - 1, reach - tallies[receiver]) // 2
    room = jnp.where((giver == order[0]) | (receiver == order[0]) | (tallies[receiver] == 0), 0, jnp.maximum(room, 0))
    moved = jax.random.randint(jax.random.fold_in(own, 4), (amount // 2,), 0, 1 << 20) % (room + 1)
    tallies = tallies.at[giver].add(-moved).at[receiver].add(moved)
    members = jnp.searchsorted(jnp.cumsum(tallies), jnp.arange(rows * top), side="right").astype(jnp.int32)
    listing = members.reshape(top, rows).T
    listing = listing[jax.random.permutation(jax.random.fold_in(own, 1), rows)]
    turn = jax.random.randint(jax.random.fold_in(own, 2), (rows, 1), 0, top)
    return jnp.take_along_axis(listing, (jnp.arange(top)[None, :] + turn) % top, axis=1)


def portions_of(count, total, reach, lean, full):
    loads = [(1 << 20) // math.isqrt(grade ** lean) + 1 for grade in range(1, count + 1)]
    largest = reach if full else min(reach, max(-(-total // count), total * loads[0] // sum(loads)))
    least = 1 if total - largest >= count - 1 else 0
    given, surplus = [largest] + [least] * (count - 1), total - largest - least * (count - 1)
    while surplus > 0:
        free = [i for i in range(1, count) if given[i] < largest] or [i for i in range(1, count) if given[i] < reach]
        pool, budget = sum([loads[i] for i in free]), surplus
        for i in free:
            more = min(reach - given[i], max(1, budget * loads[i] // pool), surplus)
            given[i] = given[i] + more
            surplus = surplus - more
    return np.array(given)


def normal_values(rng, shape, scale, most, cuts=(), kind=jnp.bfloat16):
    result = jax.random.normal(rng, shape, jnp.float32) * scale
    if len(cuts) > 0:
        result = steps_of(rng, shape, cuts, -0.22, 0.18) * result
    return jnp.clip(result, min=-most, max=most).astype(kind)


def setup_inputs(seed: int = 0) -> dict:
    key_of = jax.random.split(jax.random.key(seed), 15)
    tokens = normal_values(key_of[0], (SEQS, SEQ_LEN, D), 1.0, 6.0, ((0, 32),))
    resid_logits = normal_values(key_of[1], (SEQS, SEQ_LEN, CHOICES), 0.5, 3.0, ((0, 32),))
    routes_keys = jax.random.split(jax.random.fold_in(key_of[2], 1), SEQS * SEQ_LEN // TOK_DEV)
    routes_turns = jax.random.permutation(jax.random.fold_in(key_of[2], 3), SEQS * SEQ_LEN // TOK_DEV)
    routes = jax.vmap(lambda own, number: deal_out(jax.random.fold_in(key_of[2], 2), own, number, TOK_DEV, CHOICES, 2, CAP, 1))(routes_keys, routes_turns).reshape((SEQS, SEQ_LEN, 2))
    doc_ids = jax.vmap(lambda own: jnp.searchsorted(jnp.cumsum(ragged(own, DOCS, SEQ_LEN, SEQ_LEN // 2, 0)), jnp.arange(SEQ_LEN), side="right"))(jax.random.split(key_of[3], SEQS)).reshape((SEQS, SEQ_LEN)).astype(jnp.int32)
    w_qkv = normal_values(key_of[4], (D, 3 * D), D ** -0.5, 0.21875, ((0, 8),))
    w_out = normal_values(key_of[5], (D, D), (D // 64) ** -0.5, 1.75, ((0, 8),))
    gain_attn = jnp.clip(1.0 + 0.15 * jax.random.normal(key_of[6], (D,), jnp.float32), 0.25, 1.75).astype(jnp.bfloat16)
    gain_ffn = jnp.clip(1.0 + 0.15 * jax.random.normal(key_of[7], (D,), jnp.float32), 0.25, 1.75).astype(jnp.bfloat16)
    w_router = normal_values(key_of[8], (D, CHOICES), (2 * D) ** -0.5, 0.15625, ((0, 8),))
    w_const = normal_values(key_of[9], (D, 2 * NCONST), D ** -0.5, 0.21875, ((0, 8),))
    v_const = normal_values(key_of[10], (D, NCONST), 1.0, 5.0, ((0, 8),))
    w_gate_up = normal_values(key_of[11], (EXPERTS, D, 2 * FF), D ** -0.5, 0.21875, ((0, 4), (1, 8)))
    w_down = normal_values(key_of[12], (EXPERTS, FF, D), (FF // 2) ** -0.5, 0.1875, ((0, 4), (1, 8)))
    out_grad = normal_values(key_of[13], (SEQS, SEQ_LEN, D), 1.0, 6.0, ((0, 32),))
    return {"tokens": tokens, "resid_logits": resid_logits, "routes": routes, "doc_ids": doc_ids, "w_qkv": w_qkv, "w_out": w_out, "gain_attn": gain_attn, "gain_ffn": gain_ffn, "w_router": w_router, "w_const": w_const, "v_const": v_const, "w_gate_up": w_gate_up, "w_down": w_down, "out_grad": out_grad}


@jax.custom_vjp
def low(v):
    return lax.optimization_barrier(v.astype(jnp.bfloat16)).astype(jnp.float32)

@jax.custom_vjp
def low_back(v):
    return v

def low_keep(v):
    return (low(v), None)

def low_pass(kept, grad):
    return (grad,)

def back_keep(v):
    return (v, None)

def back_low(kept, grad):
    return (low(grad),)
low.defvjp(low_keep, low_pass)
low_back.defvjp(back_keep, back_low)
epsilon = 1e-06
highest = lax.Precision.HIGHEST

def normalize(values, gain_vec):
    return values * lax.rsqrt(lax.optimization_barrier(jnp.mean(values * values, -1, keepdims=True)) + epsilon) * gain_vec

def rotate(values, cosine_table, sine_table):
    half_dim = values.shape[-1] // 2
    first_half = values[..., :half_dim]
    second_half = values[..., half_dim:]
    return jnp.concatenate([first_half * cosine_table - second_half * sine_table, second_half * cosine_table + first_half * sine_table], -1)

def softmax_last(values):
    row_peak = lax.optimization_barrier(jnp.max(values, -1, keepdims=True))
    shifted = jnp.exp(values - row_peak)
    return shifted / lax.optimization_barrier(jnp.sum(shifted, -1, keepdims=True))

def sequence_forward(params, tokens_seq, logits_seq, routes_seq, docs_seq):
    w_qkv, w_out, gain_attn, gain_ffn, w_router, w_const, v_const, w_gate_up, w_down = params
    length = tokens_seq.shape[0]
    model_width = tokens_seq.shape[1]
    head_dim = model_width // HEADS
    hidden_n = w_down.shape[1]
    experts_n = w_gate_up.shape[0]
    const_n = v_const.shape[1]
    normed_one = low(normalize(tokens_seq, gain_attn))
    projected = low_back(jnp.dot(normed_one, w_qkv, precision=highest))
    half_dim = head_dim // 2
    frequency = 10000.0 ** (-jnp.arange(half_dim, dtype=jnp.float32) / half_dim)
    angles = jnp.arange(length, dtype=jnp.float32)[:, None] * frequency[None, :]
    cosine_table = jnp.cos(angles)[:, None, :]
    sine_table = jnp.sin(angles)[:, None, :]
    queries = rotate(projected[:, :model_width].reshape(length, HEADS, head_dim), cosine_table, sine_table)
    keys_all = rotate(projected[:, model_width:2 * model_width].reshape(length, HEADS, head_dim), cosine_table, sine_table)
    values_all = projected[:, 2 * model_width:].reshape(length, HEADS, head_dim)
    queries = low(queries)
    keys_all = low(keys_all)
    values_all = low(values_all)
    positions = jnp.arange(length)
    allowed = (docs_seq[:, None] == docs_seq[None, :]) & (positions[:, None] // BLOCK >= positions[None, :] // BLOCK)
    scores = low_back(jnp.einsum('qhd,khd->hqk', queries, keys_all, precision=highest) * head_dim ** (-0.5))
    scores = jnp.where(allowed[None], scores, -1e+30)
    probs_low = low(softmax_last(scores))
    attended = jnp.einsum('hqk,khd->qhd', probs_low, values_all, precision=highest).reshape(length, model_width)
    attended = low(low_back(attended))
    branch = low_back(jnp.dot(attended, w_out, precision=highest))
    middle = tokens_seq + branch
    normed_two = low(normalize(middle, gain_ffn))
    logits = jnp.dot(normed_two, w_router, precision=highest) + logits_seq
    choices_n = logits.shape[-1]
    picked = routes_seq[:, :, None] == jnp.arange(choices_n)[None, None, :]
    route_logits = lax.optimization_barrier(jnp.sum(jnp.where(picked, logits[:, None, :], 0.0), -1))
    gate_weights = softmax_last(route_logits)
    flat_routes = routes_seq.reshape(-1)
    pair_count = flat_routes.shape[0]
    one_hot = (flat_routes[:, None] == jnp.arange(choices_n)[None, :]).astype(jnp.int32)
    slot_rank = lax.optimization_barrier(jnp.sum((jnp.cumsum(one_hot, 0) - one_hot) * one_hot, 1))
    destination = jnp.where(flat_routes < experts_n, flat_routes * CAP + slot_rank, experts_n * CAP).astype(jnp.int32)
    slot_pair = jnp.full((experts_n * CAP + 1,), pair_count, jnp.int32).at[destination].set(jnp.arange(pair_count, dtype=jnp.int32))[:experts_n * CAP]
    padded_in = jnp.concatenate([normed_two, jnp.zeros((1, model_width), jnp.float32)], 0)
    expert_in = low_back(padded_in[slot_pair // 2]).reshape(experts_n, CAP, model_width)
    gate_up = low_back(jnp.einsum('ecd,edf->ecf', expert_in, w_gate_up, precision=highest))
    gate_part = gate_up[..., :hidden_n]
    activated = low(gate_part * lax.logistic(gate_part) * gate_up[..., hidden_n:])
    expert_out = jnp.einsum('ecf,efd->ecd', activated, w_down, precision=highest)
    expert_out = low(low_back(expert_out)).reshape(experts_n * CAP, model_width)
    padded_out = jnp.concatenate([expert_out, jnp.zeros((1, model_width), jnp.float32)], 0)
    pair_out = padded_out[destination].reshape(length, 2, model_width)
    mixing = softmax_last(jnp.dot(normed_two, w_const, precision=highest).reshape(length, const_n, 2))
    const_val = mixing[..., 0:1] * normed_two[:, None, :] + mixing[..., 1:2] * v_const.T[None, :, :]
    copy_weight = lax.optimization_barrier(jnp.sum(gate_weights * (routes_seq == experts_n + 1), -1))
    const_hit = routes_seq[:, :, None] == experts_n + 2 + jnp.arange(const_n)[None, None, :]
    const_weight = lax.optimization_barrier(jnp.sum(gate_weights[:, :, None] * const_hit, 1))
    expert_mix = lax.optimization_barrier(jnp.sum(gate_weights[:, :, None] * pair_out, 1)) + copy_weight[:, None] * normed_two + lax.optimization_barrier(jnp.sum(const_weight[:, :, None] * const_val, 1))
    return middle + expert_mix

def reference(tokens, resid_logits, routes, doc_ids, w_qkv, w_out, gain_attn, gain_ffn, w_router, w_const, v_const, w_gate_up, w_down, out_grad):
    params = (w_qkv.astype(jnp.float32), w_out.astype(jnp.float32), gain_attn.astype(jnp.float32), gain_ffn.astype(jnp.float32), w_router.astype(jnp.float32), w_const.astype(jnp.float32), v_const.astype(jnp.float32), w_gate_up.astype(jnp.float32), w_down.astype(jnp.float32))

    def forward(weights, inputs, logit_in):

        def one_sequence(seq_items):
            return sequence_forward(weights, seq_items[0], seq_items[1], seq_items[2], seq_items[3])
        return lax.map(jax.checkpoint(one_sequence), (inputs, logit_in, routes, doc_ids))
    output, pullback = jax.vjp(forward, params, tokens.astype(jnp.float32), resid_logits.astype(jnp.float32))
    grad_params, grad_tokens, grad_logits = pullback(out_grad.astype(jnp.float32))
    return (output.astype(jnp.bfloat16), grad_tokens.astype(jnp.bfloat16), grad_logits.astype(jnp.bfloat16), grad_params[0], grad_params[1], grad_params[2], grad_params[3], grad_params[4], grad_params[5], grad_params[6], grad_params[7], grad_params[8])
```

```python
import jax
import jax.numpy as jnp
from jax import lax
from jax.sharding import PartitionSpec as P

HEADS = 12
BLOCK = 256
CAP = 256


epsilon = 1e-06
highest = lax.Precision.HIGHEST


def normalize(values, gain_vec):
    row_scale = lax.rsqrt(jnp.mean(values * values, -1, keepdims=True) + epsilon)
    return (values * row_scale * gain_vec, row_scale)


def normalize_back(values, row_scale, gain_vec, grad_out):
    weighted = grad_out * gain_vec
    grad_gain = jnp.sum(grad_out * values * row_scale, 0)
    grad_in = row_scale * weighted - values * row_scale**3 * jnp.mean(
        weighted * values, -1, keepdims=True
    )
    return (grad_in, grad_gain)


def rotary_tables(row_count, length, head_dim):
    half_dim = head_dim // 2
    frequency = 10000.0 ** (-jnp.arange(half_dim, dtype=jnp.float32) / half_dim)
    positions = (jnp.arange(row_count) % length).astype(jnp.float32)
    angles = positions[:, None] * frequency[None, :]
    return (jnp.cos(angles)[:, None, :], jnp.sin(angles)[:, None, :])


def rotate(values, cosine_table, sine_table):
    half_dim = values.shape[-1] // 2
    first_half = values[..., :half_dim]
    second_half = values[..., half_dim:]
    return jnp.concatenate(
        [
            first_half * cosine_table - second_half * sine_table,
            second_half * cosine_table + first_half * sine_table,
        ],
        -1,
    )


def rotate_back(grad_vals, cosine_table, sine_table):
    half_dim = grad_vals.shape[-1] // 2
    first_half = grad_vals[..., :half_dim]
    second_half = grad_vals[..., half_dim:]
    return jnp.concatenate(
        [
            first_half * cosine_table + second_half * sine_table,
            second_half * cosine_table - first_half * sine_table,
        ],
        -1,
    )


def softmax_last(values):
    row_peak = jnp.max(values, -1, keepdims=True)
    shifted = jnp.exp(values - row_peak)
    return shifted / jnp.sum(shifted, -1, keepdims=True)


def block_scores(query_rows, keys_all, docs_rows, docs_all, first_row, score_scale):
    row_pos = first_row + jnp.arange(query_rows.shape[0])
    key_pos = jnp.arange(keys_all.shape[0])
    allowed = (docs_rows[:, None] == docs_all[None, :]) & (
        row_pos[:, None] // BLOCK >= key_pos[None, :] // BLOCK
    )
    scores = (
        jnp.einsum("qhd,khd->hqk", query_rows, keys_all, preferred_element_type=jnp.float32)
        * score_scale
    )
    return jnp.where(allowed[None], scores, -1e30)


def attend_forward(query_seq, key_seq, value_seq, docs_seq, score_scale):
    length = query_seq.shape[0]
    step_rows = min(512, length)
    outs_list = []
    lse_list = []
    for first_row in range(0, length, step_rows):
        last_row = first_row + step_rows
        scores = block_scores(
            query_seq[first_row:last_row],
            key_seq,
            docs_seq[first_row:last_row],
            docs_seq,
            first_row,
            score_scale,
        )
        row_peak = jnp.max(scores, -1, keepdims=True)
        shifted = jnp.exp(scores - row_peak)
        row_total = jnp.sum(shifted, -1, keepdims=True)
        prob_low = (shifted / row_total).astype(jnp.bfloat16)
        outs_list.append(
            jnp.einsum("hqk,khd->qhd", prob_low, value_seq, preferred_element_type=jnp.float32)
        )
        lse_list.append(row_peak + jnp.log(row_total))
    return (jnp.concatenate(outs_list, 0), jnp.concatenate(lse_list, 1))


def attend_backward(query_seq, key_seq, value_seq, docs_seq, lse_seq, grad_seq, score_scale):
    length = query_seq.shape[0]
    step_rows = min(512, length)
    grad_key = jnp.zeros(key_seq.shape, jnp.float32)
    grad_value = jnp.zeros(value_seq.shape, jnp.float32)
    query_grads = []
    for first_row in range(0, length, step_rows):
        last_row = first_row + step_rows
        rows_query = query_seq[first_row:last_row]
        rows_grad = grad_seq[first_row:last_row]
        scores = block_scores(
            rows_query, key_seq, docs_seq[first_row:last_row], docs_seq, first_row, score_scale
        )
        probs_full = jnp.exp(scores - lse_seq[:, first_row:last_row])
        prob_low = probs_full.astype(jnp.bfloat16)
        grad_probs = jnp.einsum(
            "qhd,khd->hqk", rows_grad, value_seq, preferred_element_type=jnp.float32
        )
        grad_value = grad_value + jnp.einsum(
            "hqk,qhd->khd", prob_low, rows_grad, preferred_element_type=jnp.float32
        )
        inner_sum = jnp.sum(probs_full * grad_probs, -1, keepdims=True)
        grad_scores = (probs_full * (grad_probs - inner_sum)).astype(jnp.bfloat16)
        query_grads.append(
            jnp.einsum("hqk,khd->qhd", grad_scores, key_seq, preferred_element_type=jnp.float32)
            * score_scale
        )
        grad_key = (
            grad_key
            + jnp.einsum(
                "hqk,qhd->khd", grad_scores, rows_query, preferred_element_type=jnp.float32
            )
            * score_scale
        )
    return (jnp.concatenate(query_grads, 0), grad_key, grad_value)


def shards(
    tokens,
    resid_logits,
    routes,
    doc_ids,
    w_qkv,
    w_out,
    gain_attn,
    gain_ffn,
    w_router,
    w_const,
    v_const,
    w_gate_up,
    w_down,
    out_grad,
):
    seq_count, length, model_width = tokens.shape
    row_count = seq_count * length
    pair_count = 2 * row_count
    head_dim = model_width // HEADS
    score_scale = head_dim ** (-0.5)
    choice_count = resid_logits.shape[-1]
    width_qkv = w_qkv.shape[1]
    width_out = w_out.shape[1]
    small_parts = [w_router, w_const, v_const, gain_attn[:, None], gain_ffn[:, None]]
    small_width = sum(part.shape[1] for part in small_parts)
    pad_width = -(width_qkv + width_out + small_width) % 128
    packed = jnp.concatenate(
        [w_qkv, w_out] + small_parts + [jnp.zeros((w_qkv.shape[0], pad_width), jnp.bfloat16)], 1
    )
    packed_full = lax.all_gather(packed, "dp", axis=0, tiled=True)
    qkv_full = packed_full[:, :width_qkv]
    out_full = packed_full[:, width_qkv : width_qkv + width_out]
    small_full = packed_full[:, width_qkv + width_out :]
    router_width, const_width = w_router.shape[1], w_const.shape[1]
    router_full = small_full[:, :router_width]
    const_full = small_full[:, router_width : router_width + const_width]
    first = router_width + const_width
    vector_full = small_full[:, first : first + v_const.shape[1]]
    first = first + v_const.shape[1]
    gain_one, gain_two = small_full[:, first], small_full[:, first + 1]
    gate_up_full, down_full = (
        lax.all_gather(w_gate_up, "dp", axis=1, tiled=True),
        lax.all_gather(w_down, "dp", axis=1, tiled=True),
    )
    local_count = gate_up_full.shape[0]
    owner_count = lax.axis_size("expert")
    expert_count = owner_count * local_count
    hidden_count = down_full.shape[1]
    const_count = vector_full.shape[1]
    gain_first = gain_one.astype(jnp.float32)
    gain_second = gain_two.astype(jnp.float32)
    inputs = tokens.reshape(row_count, model_width).astype(jnp.float32)
    normed_float, scale_one = normalize(inputs, gain_first)
    normed_one = normed_float.astype(jnp.bfloat16)
    projected = jnp.dot(normed_one, qkv_full, preferred_element_type=jnp.float32)
    cosine_table, sine_table = rotary_tables(row_count, length, head_dim)
    head_shape = (row_count, HEADS, head_dim)
    queries = rotate(
        projected[:, :model_width].reshape(head_shape), cosine_table, sine_table
    ).astype(jnp.bfloat16)
    keys_all = rotate(
        projected[:, model_width : 2 * model_width].reshape(head_shape), cosine_table, sine_table
    ).astype(jnp.bfloat16)
    values_all = projected[:, 2 * model_width :].reshape(head_shape).astype(jnp.bfloat16)
    shape_seq = (seq_count, length, HEADS, head_dim)
    attended, log_sums = lax.map(
        lambda seq_items: attend_forward(
            seq_items[0], seq_items[1], seq_items[2], seq_items[3], score_scale
        ),
        (
            queries.reshape(shape_seq),
            keys_all.reshape(shape_seq),
            values_all.reshape(shape_seq),
            doc_ids,
        ),
    )
    attended = attended.reshape(row_count, model_width).astype(jnp.bfloat16)
    branch = jnp.dot(attended, out_full, preferred_element_type=jnp.float32)
    middle = inputs + branch
    normed_two, scale_two = normalize(middle, gain_second)
    normed_low = normed_two.astype(jnp.bfloat16)
    normed_back = normed_low.astype(jnp.float32)
    logits = jnp.dot(
        normed_low, router_full, preferred_element_type=jnp.float32
    ) + resid_logits.reshape(row_count, choice_count).astype(jnp.float32)
    route_rows = routes.reshape(row_count, 2)
    picked = route_rows[:, :, None] == jnp.arange(choice_count)[None, None, :]
    route_logits = jnp.sum(jnp.where(picked, logits[:, None, :], 0.0), -1)
    gate_weights = softmax_last(route_logits)
    flat_routes = route_rows.reshape(pair_count)
    one_hot = picked.reshape(pair_count, choice_count).astype(jnp.int32)
    slot_rank = jnp.sum((jnp.cumsum(one_hot, 0) - one_hot) * one_hot, 1)
    destination = jnp.where(
        flat_routes < expert_count, flat_routes * CAP + slot_rank, expert_count * CAP
    )
    slot_pair = (
        jnp.full((expert_count * CAP + 1,), pair_count, jnp.int32)
        .at[destination]
        .set(jnp.arange(pair_count, dtype=jnp.int32))[: expert_count * CAP]
    )
    zero_row = jnp.zeros((1, model_width), jnp.bfloat16)
    padded_in = jnp.concatenate([normed_low, zero_row], 0)
    send_rows = padded_in[slot_pair // 2].reshape(owner_count, local_count * CAP, model_width)
    arrived = lax.all_to_all(send_rows, "expert", split_axis=0, concat_axis=0, tiled=True).reshape(
        owner_count, local_count, CAP, model_width
    )
    gate_up = jnp.einsum(
        "secd,edf->secf", arrived, gate_up_full, preferred_element_type=jnp.float32
    )
    gate_part = gate_up[..., :hidden_count]
    up_part = gate_up[..., hidden_count:]
    squashed = lax.logistic(gate_part)
    silu_gate = gate_part * squashed
    activated = (silu_gate * up_part).astype(jnp.bfloat16)
    expert_out = jnp.einsum(
        "secf,efd->secd", activated, down_full, preferred_element_type=jnp.float32
    ).astype(jnp.bfloat16)
    returned = lax.all_to_all(
        expert_out.reshape(owner_count, local_count * CAP, model_width),
        "expert",
        split_axis=0,
        concat_axis=0,
        tiled=True,
    ).reshape(expert_count * CAP, model_width)
    padded_out = jnp.concatenate([returned, zero_row], 0)
    pair_out = padded_out[destination].reshape(row_count, 2, model_width).astype(jnp.float32)
    mixing = softmax_last(
        jnp.dot(normed_low, const_full, preferred_element_type=jnp.float32).reshape(
            row_count, const_count, 2
        )
    )
    vectors = vector_full.astype(jnp.float32).T
    const_val = mixing[..., 0:1] * normed_back[:, None, :] + mixing[..., 1:2] * vectors[None, :, :]
    copy_hit = (route_rows == expert_count + 1).astype(jnp.float32)
    const_hit = (
        route_rows[:, :, None] == expert_count + 2 + jnp.arange(const_count)[None, None, :]
    ).astype(jnp.float32)
    copy_weight = jnp.sum(gate_weights * copy_hit, -1)
    const_weight = jnp.sum(gate_weights[:, :, None] * const_hit, 1)
    expert_mix = (
        jnp.sum(gate_weights[:, :, None] * pair_out, 1)
        + copy_weight[:, None] * normed_back
        + jnp.sum(const_weight[:, :, None] * const_val, 1)
    )
    output = (middle + expert_mix).astype(jnp.bfloat16).reshape(tokens.shape)
    grad_final = out_grad.reshape(row_count, model_width).astype(jnp.float32)
    dot_copy = jnp.sum(grad_final * normed_back, -1)
    dot_const = jnp.sum(grad_final[:, None, :] * const_val, -1)
    grad_gates = (
        jnp.sum(pair_out * grad_final[:, None, :], -1)
        + copy_hit * dot_copy[:, None]
        + jnp.sum(const_hit * dot_const[:, None, :], -1)
    )
    grad_route = gate_weights * (grad_gates - jnp.sum(gate_weights * grad_gates, -1, keepdims=True))
    grad_logits = jnp.sum(jnp.where(picked, grad_route[:, :, None], 0.0), 1)
    logit_grad = grad_logits.astype(jnp.bfloat16).reshape(resid_logits.shape)
    grad_router = jnp.dot(normed_back.T, grad_logits, precision=highest)
    grad_normed = jnp.dot(grad_logits, router_full.astype(jnp.float32).T, precision=highest)
    grad_normed = grad_normed + copy_weight[:, None] * grad_final
    grad_const_val = const_weight[:, :, None] * grad_final[:, None, :]
    grad_mix_first = jnp.sum(grad_const_val * normed_back[:, None, :], -1)
    grad_mix_second = jnp.sum(grad_const_val * vectors[None, :, :], -1)
    mix_term = mixing[..., 0] * mixing[..., 1] * (grad_mix_first - grad_mix_second)
    grad_mix_logits = jnp.stack([mix_term, -mix_term], -1).reshape(row_count, 2 * const_count)
    grad_const = jnp.dot(normed_back.T, grad_mix_logits, precision=highest)
    grad_normed = (
        grad_normed
        + jnp.dot(grad_mix_logits, const_full.astype(jnp.float32).T, precision=highest)
        + jnp.sum(grad_const_val * mixing[..., 0:1], 1)
    )
    grad_vector = jnp.dot(grad_final.T, const_weight * mixing[..., 1], precision=highest)
    pair_grads = (
        (gate_weights[:, :, None] * grad_final[:, None, :])
        .reshape(pair_count, model_width)
        .astype(jnp.bfloat16)
    )
    padded_grad = jnp.concatenate([pair_grads, zero_row], 0)
    send_grads = padded_grad[slot_pair].reshape(owner_count, local_count * CAP, model_width)
    arrived_grad = lax.all_to_all(
        send_grads, "expert", split_axis=0, concat_axis=0, tiled=True
    ).reshape(owner_count, local_count, CAP, model_width)
    grad_down = jnp.einsum(
        "secf,secd->efd", activated, arrived_grad, preferred_element_type=jnp.float32
    )
    grad_act = jnp.einsum(
        "secd,efd->secf", arrived_grad, down_full, preferred_element_type=jnp.float32
    )
    grad_gate = grad_act * up_part * squashed * (1.0 + gate_part * (1.0 - squashed))
    grad_up = grad_act * silu_gate
    grad_gate_up = jnp.concatenate([grad_gate, grad_up], -1).astype(jnp.bfloat16)
    grad_expert_gu = jnp.einsum(
        "secd,secf->edf", arrived, grad_gate_up, preferred_element_type=jnp.float32
    )
    grad_rows = jnp.einsum(
        "secf,edf->secd", grad_gate_up, gate_up_full, preferred_element_type=jnp.float32
    ).astype(jnp.bfloat16)
    back_rows = lax.all_to_all(
        grad_rows.reshape(owner_count, local_count * CAP, model_width),
        "expert",
        split_axis=0,
        concat_axis=0,
        tiled=True,
    ).reshape(expert_count * CAP, model_width)
    padded_back = jnp.concatenate([back_rows, zero_row], 0)
    grad_normed = grad_normed + jnp.sum(
        padded_back[destination].reshape(row_count, 2, model_width).astype(jnp.float32), 1
    )
    grad_expert_gu = grad_expert_gu.astype(jnp.bfloat16)
    grad_down = grad_down.astype(jnp.bfloat16)
    grad_normed, grad_expert_gu, grad_down = lax.optimization_barrier(
        (grad_normed, grad_expert_gu, grad_down)
    )
    grad_expert_down = lax.psum_scatter(
        grad_down, "dp", scatter_dimension=1, tiled=True
    ).astype(jnp.float32)
    grad_expert_gu = lax.psum_scatter(
        grad_expert_gu, "dp", scatter_dimension=1, tiled=True
    ).astype(jnp.float32)
    grad_middle, grad_gain_two = normalize_back(middle, scale_two, gain_second, grad_normed)
    grad_middle = grad_middle + grad_final
    grad_branch = grad_middle.astype(jnp.bfloat16)
    grad_out_w = lax.dot_general(
        attended, grad_branch, (((0,), (0,)), ((), ())), preferred_element_type=jnp.float32
    )
    grad_attended = lax.dot_general(
        grad_branch, out_full, (((1,), (1,)), ((), ())), preferred_element_type=jnp.float32
    ).astype(jnp.bfloat16)
    grad_query, grad_key, grad_value = lax.map(
        lambda seq_items: attend_backward(
            seq_items[0],
            seq_items[1],
            seq_items[2],
            seq_items[3],
            seq_items[4],
            seq_items[5],
            score_scale,
        ),
        (
            queries.reshape(shape_seq),
            keys_all.reshape(shape_seq),
            values_all.reshape(shape_seq),
            doc_ids,
            log_sums,
            grad_attended.reshape(shape_seq),
        ),
    )
    grad_query = rotate_back(grad_query.reshape(head_shape), cosine_table, sine_table)
    grad_key = rotate_back(grad_key.reshape(head_shape), cosine_table, sine_table)
    grad_projected = jnp.concatenate(
        [
            grad_query.reshape(row_count, model_width),
            grad_key.reshape(row_count, model_width),
            grad_value.reshape(row_count, model_width),
        ],
        -1,
    ).astype(jnp.bfloat16)
    grad_qkv = lax.dot_general(
        normed_one, grad_projected, (((0,), (0,)), ((), ())), preferred_element_type=jnp.float32
    )
    grad_normed_one = lax.dot_general(
        grad_projected, qkv_full, (((1,), (1,)), ((), ())), preferred_element_type=jnp.float32
    )
    grad_inputs, grad_gain_one = normalize_back(inputs, scale_one, gain_first, grad_normed_one)
    token_grad = (grad_inputs + grad_middle).astype(jnp.bfloat16).reshape(tokens.shape)
    small_grads = [
        grad_router,
        grad_const,
        grad_vector,
        grad_gain_one[:, None],
        grad_gain_two[:, None],
    ]
    packed_grads = jnp.concatenate(
        [part.astype(jnp.bfloat16) for part in [grad_qkv, grad_out_w] + small_grads]
        + [jnp.zeros((model_width, pad_width), jnp.bfloat16)],
        1,
    )
    packed_part = lax.psum_scatter(packed_grads, "dp", scatter_dimension=0, tiled=True)
    packed_part = lax.psum(packed_part, "expert").astype(jnp.float32)
    part_qkv = packed_part[:, :width_qkv]
    part_out = packed_part[:, width_qkv : width_qkv + width_out]
    small_part = packed_part[:, width_qkv + width_out :]
    part_router = small_part[:, :router_width]
    part_const = small_part[:, router_width : router_width + const_width]
    first = router_width + const_width
    part_vector = small_part[:, first : first + v_const.shape[1]]
    first = first + v_const.shape[1]
    part_gain_one, part_gain_two = small_part[:, first], small_part[:, first + 1]
    return (
        output,
        token_grad,
        logit_grad,
        part_qkv,
        part_out,
        part_gain_one,
        part_gain_two,
        part_router,
        part_const,
        part_vector,
        grad_expert_gu,
        grad_expert_down,
    )


def solution(mesh):
    placed = (
        P(("dp", "expert"), None, None),
        P(("dp", "expert"), None, None),
        P(("dp", "expert"), None, None),
        P(("dp", "expert"), None),
        P("dp", None),
        P("dp", None),
        P("dp"),
        P("dp"),
        P("dp", None),
        P("dp", None),
        P("dp", None),
        P("expert", "dp", None),
        P("expert", "dp", None),
        P(("dp", "expert"), None, None),
    )
    return jax.shard_map(
        shards,
        mesh=mesh,
        in_specs=placed,
        out_specs=(
            P(("dp", "expert"), None, None),
            P(("dp", "expert"), None, None),
            P(("dp", "expert"), None, None),
            P("dp", None),
            P("dp", None),
            P("dp"),
            P("dp"),
            P("dp", None),
            P("dp", None),
            P("dp", None),
            P("expert", "dp", None),
            P("expert", "dp", None),
        ),
        check_vma=False,
    )
```

```python
import functools

import jax
import jax.numpy as jnp
from jax import lax
from jax.experimental import pallas as pl
from jax.experimental.pallas import tpu as pltpu
from jax.sharding import PartitionSpec as P

HEADS = 12
BLOCK = 256
CAP = 256


epsilon = 1e-06
highest = lax.Precision.HIGHEST


def normalize(values, gain_vec):
    row_scale = lax.rsqrt(jnp.mean(values * values, -1, keepdims=True) + epsilon)
    return (values * row_scale * gain_vec, row_scale)


def normalize_back(values, row_scale, gain_vec, grad_out):
    weighted = grad_out * gain_vec
    grad_gain = jnp.sum(grad_out * values * row_scale, 0)
    grad_in = row_scale * weighted - values * row_scale**3 * jnp.mean(
        weighted * values, -1, keepdims=True
    )
    return (grad_in, grad_gain)


def rotary_tables(row_count, length, head_dim):
    half_dim = head_dim // 2
    frequency = 10000.0 ** (-jnp.arange(half_dim, dtype=jnp.float32) / half_dim)
    positions = (jnp.arange(row_count) % length).astype(jnp.float32)
    angles = positions[:, None] * frequency[None, :]
    return (jnp.cos(angles)[:, None, :], jnp.sin(angles)[:, None, :])


def rotate(values, cosine_table, sine_table):
    half_dim = values.shape[-1] // 2
    first_half = values[..., :half_dim]
    second_half = values[..., half_dim:]
    return jnp.concatenate(
        [
            first_half * cosine_table - second_half * sine_table,
            second_half * cosine_table + first_half * sine_table,
        ],
        -1,
    )


def rotate_back(grad_vals, cosine_table, sine_table):
    half_dim = grad_vals.shape[-1] // 2
    first_half = grad_vals[..., :half_dim]
    second_half = grad_vals[..., half_dim:]
    return jnp.concatenate(
        [
            first_half * cosine_table + second_half * sine_table,
            second_half * cosine_table - first_half * sine_table,
        ],
        -1,
    )


def softmax_last(values):
    row_peak = jnp.max(values, -1, keepdims=True)
    shifted = jnp.exp(values - row_peak)
    return shifted / jnp.sum(shifted, -1, keepdims=True)


def block_scores(query_rows, keys_all, docs_rows, docs_all, first_row, score_scale):
    row_pos = first_row + jnp.arange(query_rows.shape[0])
    key_pos = jnp.arange(keys_all.shape[0])
    allowed = (docs_rows[:, None] == docs_all[None, :]) & (
        row_pos[:, None] // BLOCK >= key_pos[None, :] // BLOCK
    )
    scores = (
        jnp.einsum("qhd,khd->hqk", query_rows, keys_all, preferred_element_type=jnp.float32)
        * score_scale
    )
    return jnp.where(allowed[None], scores, -1e30)


def attend_forward(query_seq, key_seq, value_seq, docs_seq, score_scale):
    length = query_seq.shape[0]
    step_rows = min(512, length)
    outs_list = []
    lse_list = []
    for first_row in range(0, length, step_rows):
        last_row = first_row + step_rows
        scores = block_scores(
            query_seq[first_row:last_row],
            key_seq,
            docs_seq[first_row:last_row],
            docs_seq,
            first_row,
            score_scale,
        )
        row_peak = jnp.max(scores, -1, keepdims=True)
        shifted = jnp.exp(scores - row_peak)
        row_total = jnp.sum(shifted, -1, keepdims=True)
        prob_low = (shifted / row_total).astype(jnp.bfloat16)
        outs_list.append(
            jnp.einsum("hqk,khd->qhd", prob_low, value_seq, preferred_element_type=jnp.float32)
        )
        lse_list.append(row_peak + jnp.log(row_total))
    return (jnp.concatenate(outs_list, 0), jnp.concatenate(lse_list, 1))


def attend_backward(query_seq, key_seq, value_seq, docs_seq, lse_seq, grad_seq, score_scale):
    length = query_seq.shape[0]
    step_rows = min(512, length)
    grad_key = jnp.zeros(key_seq.shape, jnp.float32)
    grad_value = jnp.zeros(value_seq.shape, jnp.float32)
    query_grads = []
    for first_row in range(0, length, step_rows):
        last_row = first_row + step_rows
        rows_query = query_seq[first_row:last_row]
        rows_grad = grad_seq[first_row:last_row]
        scores = block_scores(
            rows_query, key_seq, docs_seq[first_row:last_row], docs_seq, first_row, score_scale
        )
        probs_full = jnp.exp(scores - lse_seq[:, first_row:last_row])
        prob_low = probs_full.astype(jnp.bfloat16)
        grad_probs = jnp.einsum(
            "qhd,khd->hqk", rows_grad, value_seq, preferred_element_type=jnp.float32
        )
        grad_value = grad_value + jnp.einsum(
            "hqk,qhd->khd", prob_low, rows_grad, preferred_element_type=jnp.float32
        )
        inner_sum = jnp.sum(probs_full * grad_probs, -1, keepdims=True)
        grad_scores = (probs_full * (grad_probs - inner_sum)).astype(jnp.bfloat16)
        query_grads.append(
            jnp.einsum("hqk,khd->qhd", grad_scores, key_seq, preferred_element_type=jnp.float32)
            * score_scale
        )
        grad_key = (
            grad_key
            + jnp.einsum(
                "hqk,qhd->khd", grad_scores, rows_query, preferred_element_type=jnp.float32
            )
            * score_scale
        )
    return (jnp.concatenate(query_grads, 0), grad_key, grad_value)


MESH = pl.DeviceIdType.MESH


def dp_grid(dp_count):
    outer = 4 if dp_count % 4 == 0 else 1
    return outer, dp_count // outer


def place():
    me, mine = lax.axis_index("dp"), lax.axis_index("expert")
    return me, mine


def greet(peers):
    barrier = pltpu.get_barrier_semaphore()
    for peer in peers:
        pl.semaphore_signal(barrier, inc=1, device_id=peer, device_id_type=MESH)
    pl.semaphore_wait(barrier, len(peers))


def small_gather_kernel(dp_count, shard_ref, full_ref, send_sem, pass_sem, recv_sem, mate_sem, own_sem):
    outer_count, inner_count = dp_grid(dp_count)
    me, mine = place()
    outer, inner = me // inner_count, me % inner_count
    rows, columns = shard_ref.shape
    half = columns // 2
    side = pl.multiple_of((mine % 2) * half, 128)
    mate = mine + 1 - 2 * (mine % 2)
    outer_peers = [lax.rem(outer + k, outer_count) for k in range(1, outer_count)]
    inner_peers = [lax.rem(inner + k, inner_count) for k in range(1, inner_count)]
    greet(
        [(peer * inner_count + inner, mine) for peer in outer_peers]
        + [(outer * inner_count + peer, mine) for peer in inner_peers]
        + [(me, mate)]
    )

    def spot(chunk):
        return full_ref.at[pl.ds(pl.multiple_of(chunk * rows, 8), rows), pl.ds(side, half)]

    sent = []

    def send(source, chunk, device, send_at, recv_at):
        copy = pltpu.make_async_remote_copy(
            src_ref=source,
            dst_ref=spot(chunk),
            send_sem=send_at,
            recv_sem=recv_at,
            device_id=device,
            device_id_type=MESH,
        )
        copy.start()
        sent.append(copy)

    def arrived(chunk):
        pltpu.make_async_copy(spot(chunk), spot(chunk), recv_sem.at[chunk]).wait()

    own_half = shard_ref.at[:, pl.ds(side, half)]
    for k, peer in enumerate(outer_peers):
        send(own_half, me, (peer * inner_count + inner, mine), send_sem.at[0, k], recv_sem.at[me])
    for k, peer in enumerate(inner_peers):
        send(own_half, me, (outer * inner_count + peer, mine), send_sem.at[1, k], recv_sem.at[me])
    own = pltpu.make_async_copy(
        shard_ref, full_ref.at[pl.ds(pl.multiple_of(me * rows, 8), rows), :], own_sem
    )
    own.start()
    chunks = []
    for k, peer in enumerate(outer_peers):
        chunk = peer * inner_count + inner
        arrived(chunk)
        for j, other in enumerate(inner_peers):
            send(spot(chunk), chunk, (outer * inner_count + other, mine), send_sem.at[2 + k, j], recv_sem.at[chunk])
        send(spot(chunk), chunk, (me, mate), pass_sem.at[len(chunks)], mate_sem.at[chunk])
        chunks.append(chunk)
    for other in inner_peers:
        for peer in [outer] + outer_peers:
            chunk = peer * inner_count + other
            arrived(chunk)
            send(spot(chunk), chunk, (me, mate), pass_sem.at[len(chunks)], mate_sem.at[chunk])
            chunks.append(chunk)
    own.wait()
    for chunk in chunks:
        there = full_ref.at[
            pl.ds(pl.multiple_of(chunk * rows, 8), rows), pl.ds(pl.multiple_of(half - side, 128), half)
        ]
        pltpu.make_async_copy(there, there, mate_sem.at[chunk]).wait()
    for copy in sent:
        copy.wait_send()


def small_gather(shard, dp_count, collective):
    outer_count, inner_count = dp_grid(dp_count)
    rows, columns = shard.shape
    lanes = max(outer_count, inner_count)
    return pl.pallas_call(
        functools.partial(small_gather_kernel, dp_count),
        out_shape=jax.ShapeDtypeStruct((dp_count * rows, columns), shard.dtype),
        in_specs=[pl.BlockSpec(memory_space=pl.ANY)],
        out_specs=pl.BlockSpec(memory_space=pl.ANY),
        scratch_shapes=[
            pltpu.SemaphoreType.DMA((outer_count + 1, lanes)),
            pltpu.SemaphoreType.DMA((dp_count,)),
            pltpu.SemaphoreType.DMA((dp_count,)),
            pltpu.SemaphoreType.DMA((dp_count,)),
            pltpu.SemaphoreType.DMA,
        ],
        compiler_params=pltpu.CompilerParams(collective_id=collective, has_side_effects=True),
        name="small_gather",
    )(shard)


def expert_gather_kernel(dp_count, tensor_count, cuts, crossed, owner_count, trade_count, *refs):
    given = tensor_count + trade_count
    shards, outgoing = refs[:tensor_count], refs[tensor_count:given]
    fulls, incoming = refs[given : given + tensor_count], refs[given + tensor_count : 2 * given]
    send_sem, recv_sem, own_sem, trade_send, trade_recv = refs[2 * given :]
    outer_count, inner_count = dp_grid(dp_count)
    me, mine = place()
    outer, inner = me // inner_count, me % inner_count
    below, above = lax.rem(outer + outer_count - 1, outer_count), lax.rem(outer + 1, outer_count)
    inner_peers = [lax.rem(inner + k, inner_count) for k in range(1, inner_count)]
    greet(
        [(peer * inner_count + inner, mine) for peer in (below, above)]
        + [(outer * inner_count + peer, mine) for peer in inner_peers]
        + [(me, lax.rem(mine + k, owner_count)) for k in range(1, owner_count) if trade_count]
    )
    trades = []
    for t in range(trade_count):
        for k in range(1, owner_count):
            peer = lax.rem(mine + k, owner_count)
            trade = pltpu.make_async_remote_copy(
                src_ref=outgoing[t].at[peer],
                dst_ref=incoming[t].at[mine],
                send_sem=trade_send.at[t, k],
                recv_sem=trade_recv.at[t, mine],
                device_id=(me, peer),
                device_id_type=MESH,
            )
            trade.start()
            trades.append(trade)
        keep = pltpu.make_async_copy(
            outgoing[t].at[mine], incoming[t].at[mine], trade_send.at[t, 0]
        )
        keep.start()
    pieces = [
        (t, e, c) for t in range(tensor_count) for e in range(shards[t].shape[0]) for c in range(cuts[t])
    ]

    def spot(p, chunk):
        t, e, c = pieces[p]
        rows = shards[t].shape[1]
        part = rows // cuts[t]
        return fulls[t].at[e, pl.ds(pl.multiple_of(chunk * rows + c * part, 8), part), :]

    def copy_of(p, source, chunk, device, send_at):
        return pltpu.make_async_remote_copy(
            src_ref=source,
            dst_ref=spot(p, chunk),
            send_sem=send_at,
            recv_sem=recv_sem.at[p, chunk],
            device_id=device,
            device_id_type=MESH,
        )

    def source_of(p):
        t, e, c = pieces[p]
        part = shards[t].shape[1] // cuts[t]
        return shards[t].at[e, pl.ds(c * part, part), :]

    def inner_sends(p, source, chunk):
        return [
            copy_of(p, source, chunk, (outer * inner_count + peer, mine), send_sem.at[p, 0, j, chunk])
            for j, peer in enumerate(inner_peers)
        ]

    def up(p, source, chunk):
        return copy_of(p, source, chunk, (above * inner_count + inner, mine), send_sem.at[p, 1, 0, chunk])

    def down(p, source, chunk):
        return copy_of(p, source, chunk, (below * inner_count + inner, mine), send_sem.at[p, 2, 0, chunk])

    def arrived(p, chunk):
        pltpu.make_async_copy(spot(p, chunk), spot(p, chunk), recv_sem.at[p, chunk]).wait()

    can_up, can_down = outer < outer_count - 1, outer > 0
    every = range(len(pieces))
    own = []
    for p in every:
        for copy in inner_sends(p, source_of(p), me):
            copy.start()
        pl.when(can_up)(lambda p=p: up(p, source_of(p), me).start())
        pl.when(can_down)(lambda p=p: down(p, source_of(p), me).start())
        copy = pltpu.make_async_copy(source_of(p), spot(p, me), own_sem.at[p])
        copy.start()
        own.append(copy)

    def passing(p, chunk, upward):
        arrived(p, chunk)
        if upward:
            pl.when(can_up)(lambda: up(p, spot(p, chunk), chunk).start())
        else:
            pl.when(can_down)(lambda: down(p, spot(p, chunk), chunk).start())

    for p in every:
        if p in crossed:
            for peer in inner_peers:
                chunk = outer * inner_count + peer
                arrived(p, chunk)
                pl.when(can_up)(lambda p=p, chunk=chunk: up(p, spot(p, chunk), chunk).start())
                pl.when(can_down)(lambda p=p, chunk=chunk: down(p, spot(p, chunk), chunk).start())
    for step in range(1, outer_count):
        low, high = outer - step, outer + step
        for p in every:
            for upward, there, source in ((True, low >= 0, low), (False, high < outer_count, high)):

                def relay(p=p, upward=upward, source=source):
                    chunk = source * inner_count + inner
                    passing(p, chunk, upward)
                    if p in crossed:
                        for peer in inner_peers:
                            passing(p, source * inner_count + peer, upward)
                    else:
                        for copy in inner_sends(p, spot(p, chunk), chunk):
                            copy.start()

                pl.when(there)(relay)
    for t in range(trade_count):
        pltpu.make_async_copy(
            outgoing[t].at[mine], incoming[t].at[mine], trade_send.at[t, 0]
        ).wait()
        for k in range(1, owner_count):
            there = incoming[t].at[lax.rem(mine + k, owner_count)]
            pltpu.make_async_copy(
                there, there, trade_recv.at[t, lax.rem(mine + k, owner_count)]
            ).wait()
    for trade in trades:
        trade.wait_send()
    for p in every:
        own[p].wait()
        if p not in crossed:
            for peer in inner_peers:
                for plane in range(outer_count):
                    arrived(p, plane * inner_count + peer)
        for copy in inner_sends(p, source_of(p), me):
            copy.wait_send()
        if p not in crossed:
            for k in range(1, outer_count):
                chunk = lax.rem(outer + k, outer_count) * inner_count + inner
                for copy in inner_sends(p, spot(p, chunk), chunk):
                    copy.wait_send()
        columns = range(inner_count) if p in crossed else [inner]
        for plane in range(outer_count):
            for column in columns:
                chunk = plane * inner_count + column
                pl.when(can_up & (outer >= plane))(lambda p=p, chunk=chunk: up(p, spot(p, chunk), chunk).wait_send())
                pl.when(can_down & (outer <= plane))(lambda p=p, chunk=chunk: down(p, spot(p, chunk), chunk).wait_send())


def expert_gather(shards, dp_count, collective, cuts=None, crossed=(), owner_count=1, trades=()):
    outer_count, inner_count = dp_grid(dp_count)
    cuts = cuts or [1] * len(shards)
    piece_count = sum(shard.shape[0] * cut for shard, cut in zip(shards, cuts))
    anywhere = pl.BlockSpec(memory_space=pl.ANY)
    given = len(shards) + len(trades)
    return pl.pallas_call(
        functools.partial(
            expert_gather_kernel, dp_count, len(shards), cuts, crossed, owner_count, len(trades)
        ),
        out_shape=[
            jax.ShapeDtypeStruct((s.shape[0], dp_count * s.shape[1], s.shape[2]), s.dtype)
            for s in shards
        ]
        + [jax.ShapeDtypeStruct(t.shape, t.dtype) for t in trades],
        in_specs=[anywhere] * given,
        out_specs=[anywhere] * given,
        scratch_shapes=[
            pltpu.SemaphoreType.DMA((piece_count, 3, max(1, inner_count - 1), dp_count)),
            pltpu.SemaphoreType.DMA((piece_count, dp_count)),
            pltpu.SemaphoreType.DMA((piece_count,)),
            pltpu.SemaphoreType.DMA((max(1, len(trades)), owner_count)),
            pltpu.SemaphoreType.DMA((max(1, len(trades)), owner_count)),
        ],
        compiler_params=pltpu.CompilerParams(collective_id=collective, has_side_effects=True),
        name="expert_gather",
    )(*shards, *trades)


def add_into(target, source, target_at, source_at):
    rows = target.shape[-2]
    step = 16

    def body(i, carry):
        here = pl.ds(pl.multiple_of(i * step, step), step)
        target[target_at + (here, slice(None))] = (
            target[target_at + (here, slice(None))].astype(jnp.float32)
            + source(here).astype(jnp.float32)
        ).astype(target.dtype)
        return carry

    lax.fori_loop(0, rows // step, body, 0)


def final_reduce_kernel(
    part_ref, small_ref, part_out, small_out,
    swap, part_in, part_low, part_high, small_in, small_low, small_high, final_low, final_in,
    swap_send, swap_recv, in_send, in_recv, line_send, line_recv, last_send, last_recv,
):
    outer_count, inner_count = 4, 2
    me, mine = place()
    outer, inner = me // inner_count, me % inner_count
    side = mine % 2
    mate, across = mine + 1 - 2 * side, lax.rem(mine + 2, 4)
    beside = me + 1 - 2 * inner
    half_rows = small_ref.shape[1] // 2
    part_rows = part_ref.shape[1]

    def remote(source, target, device, send_at, recv_at):
        return pltpu.make_async_remote_copy(
            src_ref=source,
            dst_ref=target,
            send_sem=send_at,
            recv_sem=recv_at,
            device_id=device,
            device_id_type=MESH,
        )

    barrier = pltpu.get_barrier_semaphore()
    low_peer = lax.rem(outer + outer_count - 1, outer_count) * inner_count + inner
    high_peer = lax.rem(outer + 1, outer_count) * inner_count + inner
    for device in ((me, mate), (me, across), (beside, mine), (low_peer, mine), (high_peer, mine)):
        pl.semaphore_signal(barrier, inc=1, device_id=device, device_id_type=MESH)
    pl.semaphore_wait(barrier, 5)

    mate_rows = pl.ds(pl.multiple_of((1 - side) * half_rows, 16), half_rows)
    own_rows = pl.ds(pl.multiple_of(side * half_rows, 16), half_rows)

    def swap_copy(chunk):
        return remote(
            small_ref.at[chunk, mate_rows, :], swap.at[chunk], (me, mate), swap_send.at[chunk], swap_recv.at[chunk]
        )

    def inner_copy(p, plane):
        if p == 0:
            source = part_ref.at[plane * inner_count + 1 - inner]
            target = part_in.at[plane]
        else:
            source = swap.at[plane * inner_count + 1 - inner]
            target = small_in.at[plane]
        return remote(source, target, (beside, mine), in_send.at[p, plane], in_recv.at[p, plane])

    ins, lows, highs = (part_in, small_in), (part_low, small_low), (part_high, small_high)

    def line_copy(p, plane, upward, device_plane):
        target = (lows if upward else highs)[p].at[plane]
        way = 0 if upward else 1
        return remote(
            ins[p].at[plane],
            target,
            (device_plane * inner_count + inner, mine),
            line_send.at[p, way, plane],
            line_recv.at[p, way, plane],
        )

    def at_plane(o):
        order = sorted(range(outer_count), key=lambda t: (-abs(t - o), t))
        for plane in order:
            inner_copy(0, plane).start()
        for plane in order:
            for column in range(inner_count):
                swap_copy(plane * inner_count + column).start()
        for plane in order:
            for column in range(inner_count):
                chunk = plane * inner_count + column
                swap_copy(chunk).wait_recv()
                add_into(swap, lambda here, chunk=chunk: small_ref[chunk, pl.ds(side * half_rows + here.start, here.size), :], (chunk,), None)
            inner_copy(1, plane).start()
        for plane in order:
            for p in (0, 1):
                inner_copy(p, plane).wait_recv()
                if p == 0:
                    add_into(ins[p], lambda here, plane=plane: part_ref[plane * inner_count + inner, here, :], (plane,), None)
                else:
                    add_into(ins[p], lambda here, plane=plane: swap[plane * inner_count + inner, here, :], (plane,), None)
                if plane > o:
                    if o > 0:
                        line_copy(p, plane, True, o + 1).wait_recv()
                        add_into(ins[p], lambda here, p=p, plane=plane: lows[p][plane, here, :], (plane,), None)
                    line_copy(p, plane, True, o + 1).start()
                if plane < o:
                    if o < outer_count - 1:
                        line_copy(p, plane, False, o - 1).wait_recv()
                        add_into(ins[p], lambda here, p=p, plane=plane: highs[p][plane, here, :], (plane,), None)
                    line_copy(p, plane, False, o - 1).start()
                if plane == o:
                    if o > 0:
                        line_copy(p, plane, True, o).wait_recv()
                    if o < outer_count - 1:
                        line_copy(p, plane, False, o).wait_recv()
                    target = part_out if p == 0 else final_low
                    rows = target.shape[0]

                    def body(i, carry, p=p, target=target):
                        here = pl.ds(pl.multiple_of(i * 16, 16), 16)
                        total = ins[p][o, here, :].astype(jnp.float32)
                        if o > 0:
                            total = total + lows[p][o, here, :].astype(jnp.float32)
                        if o < outer_count - 1:
                            total = total + highs[p][o, here, :].astype(jnp.float32)
                        target[here, :] = total.astype(target.dtype)
                        return carry

                    lax.fori_loop(0, rows // 16, body, 0)
        for plane in range(outer_count):
            for p in (0, 1):
                inner_copy(p, plane).wait_send()
                if plane > o:
                    line_copy(p, plane, True, o + 1).wait_send()
                if plane < o:
                    line_copy(p, plane, False, o - 1).wait_send()
            for column in range(inner_count):
                swap_copy(plane * inner_count + column).wait_send()

    for o in range(outer_count):
        pl.when(outer == o)(functools.partial(at_plane, o))
    across_copy = remote(final_low, final_in, (me, across), last_send.at[0], last_recv.at[0])
    across_copy.start()
    across_copy.wait()

    def total_body(i, carry):
        here = pl.ds(pl.multiple_of(i * 16, 16), 16)
        there = pl.ds(pl.multiple_of(side * half_rows + i * 16, 16), 16)
        small_out[there, :] = final_low[here, :].astype(jnp.float32) + final_in[here, :].astype(jnp.float32)
        return carry

    lax.fori_loop(0, half_rows // 16, total_body, 0)
    mate_copy = remote(
        small_out.at[own_rows, :], small_out.at[own_rows, :], (me, mate), last_send.at[1], last_recv.at[1]
    )
    mate_copy.start()
    mate_copy.wait()


def final_reduce(part, small, collective):
    chunk_count, part_rows, part_columns = part.shape
    _, small_rows, small_columns = small.shape
    low = jnp.bfloat16
    in_vmem = pl.BlockSpec(memory_space=pltpu.VMEM)
    half = small_rows // 2
    return pl.pallas_call(
        final_reduce_kernel,
        out_shape=[
            jax.ShapeDtypeStruct((part_rows, part_columns), jnp.float32),
            jax.ShapeDtypeStruct((small_rows, small_columns), jnp.float32),
        ],
        in_specs=[in_vmem] * 2,
        out_specs=[in_vmem] * 2,
        scratch_shapes=[pltpu.VMEM((chunk_count, half, small_columns), low)]
        + [pltpu.VMEM((4, part_rows, part_columns), low)] * 3
        + [pltpu.VMEM((4, half, small_columns), low)] * 3
        + [pltpu.VMEM((half, small_columns), low)] * 2
        + [
            pltpu.SemaphoreType.DMA((chunk_count,)),
            pltpu.SemaphoreType.DMA((chunk_count,)),
            pltpu.SemaphoreType.DMA((2, 4)),
            pltpu.SemaphoreType.DMA((2, 4)),
            pltpu.SemaphoreType.DMA((2, 2, 4)),
            pltpu.SemaphoreType.DMA((2, 2, 4)),
            pltpu.SemaphoreType.DMA((2,)),
            pltpu.SemaphoreType.DMA((2,)),
        ],
        compiler_params=pltpu.CompilerParams(
            collective_id=collective, has_side_effects=True, vmem_limit_bytes=58 * 2**20
        ),
        name="final_reduce",
    )(part, small)


def shards(
    tokens,
    resid_logits,
    routes,
    doc_ids,
    w_qkv,
    w_out,
    gain_attn,
    gain_ffn,
    w_router,
    w_const,
    v_const,
    w_gate_up,
    w_down,
    out_grad,
):
    seq_count, length, model_width = tokens.shape
    row_count = seq_count * length
    pair_count = 2 * row_count
    head_dim = model_width // HEADS
    score_scale = head_dim ** (-0.5)
    choice_count = resid_logits.shape[-1]
    width_qkv = w_qkv.shape[1]
    width_out = w_out.shape[1]
    small_parts = [w_router, w_const, v_const, gain_attn[:, None], gain_ffn[:, None]]
    small_width = sum(part.shape[1] for part in small_parts)
    pad_width = -(width_qkv + width_out + small_width) % 256
    packed = jnp.concatenate(
        [w_qkv, w_out] + small_parts + [jnp.zeros((w_qkv.shape[0], pad_width), jnp.bfloat16)], 1
    )
    dp_count = lax.axis_size("dp")
    owner_count = lax.axis_size("expert")
    own_links = dp_count == 8 and owner_count == 4
    if own_links:
        packed_full = small_gather(packed, dp_count, 1)
    else:
        packed_full = lax.all_gather(packed, "dp", axis=0, tiled=True)
    qkv_full = packed_full[:, :width_qkv]
    out_full = packed_full[:, width_qkv : width_qkv + width_out]
    small_full = packed_full[:, width_qkv + width_out :]
    router_width, const_width = w_router.shape[1], w_const.shape[1]
    router_full = small_full[:, :router_width]
    const_full = small_full[:, router_width : router_width + const_width]
    first = router_width + const_width
    vector_full = small_full[:, first : first + v_const.shape[1]]
    first = first + v_const.shape[1]
    gain_one, gain_two = small_full[:, first], small_full[:, first + 1]
    gate_up_full = lax.all_gather(w_gate_up, "dp", axis=1, tiled=True)
    local_count = gate_up_full.shape[0]
    expert_count = owner_count * local_count
    hidden_count = w_down.shape[1] * dp_count
    const_count = vector_full.shape[1]
    gain_first = gain_one.astype(jnp.float32)
    gain_second = gain_two.astype(jnp.float32)
    inputs = tokens.reshape(row_count, model_width).astype(jnp.float32)
    normed_float, scale_one = normalize(inputs, gain_first)
    normed_one = normed_float.astype(jnp.bfloat16)
    projected = jnp.dot(normed_one, qkv_full, preferred_element_type=jnp.float32)
    cosine_table, sine_table = rotary_tables(row_count, length, head_dim)
    head_shape = (row_count, HEADS, head_dim)
    queries = rotate(
        projected[:, :model_width].reshape(head_shape), cosine_table, sine_table
    ).astype(jnp.bfloat16)
    keys_all = rotate(
        projected[:, model_width : 2 * model_width].reshape(head_shape), cosine_table, sine_table
    ).astype(jnp.bfloat16)
    values_all = projected[:, 2 * model_width :].reshape(head_shape).astype(jnp.bfloat16)
    shape_seq = (seq_count, length, HEADS, head_dim)
    attended, log_sums = lax.map(
        lambda seq_items: attend_forward(
            seq_items[0], seq_items[1], seq_items[2], seq_items[3], score_scale
        ),
        (
            queries.reshape(shape_seq),
            keys_all.reshape(shape_seq),
            values_all.reshape(shape_seq),
            doc_ids,
        ),
    )
    attended = attended.reshape(row_count, model_width).astype(jnp.bfloat16)
    branch = jnp.dot(attended, out_full, preferred_element_type=jnp.float32)
    middle = inputs + branch
    normed_two, scale_two = normalize(middle, gain_second)
    normed_low = normed_two.astype(jnp.bfloat16)
    normed_back = normed_low.astype(jnp.float32)
    logits = jnp.dot(
        normed_low, router_full, preferred_element_type=jnp.float32
    ) + resid_logits.reshape(row_count, choice_count).astype(jnp.float32)
    route_rows = routes.reshape(row_count, 2)
    picked = route_rows[:, :, None] == jnp.arange(choice_count)[None, None, :]
    route_logits = jnp.sum(jnp.where(picked, logits[:, None, :], 0.0), -1)
    gate_weights = softmax_last(route_logits)
    flat_routes = route_rows.reshape(pair_count)
    one_hot = picked.reshape(pair_count, choice_count).astype(jnp.int32)
    slot_rank = jnp.sum((jnp.cumsum(one_hot, 0) - one_hot) * one_hot, 1)
    destination = jnp.where(
        flat_routes < expert_count, flat_routes * CAP + slot_rank, expert_count * CAP
    )
    slot_pair = (
        jnp.full((expert_count * CAP + 1,), pair_count, jnp.int32)
        .at[destination]
        .set(jnp.arange(pair_count, dtype=jnp.int32))[: expert_count * CAP]
    )
    zero_row = jnp.zeros((1, model_width), jnp.bfloat16)
    padded_in = jnp.concatenate([normed_low, zero_row], 0)
    send_rows = padded_in[slot_pair // 2].reshape(owner_count, local_count * CAP, model_width)
    grad_final = out_grad.reshape(row_count, model_width).astype(jnp.float32)
    pair_grads = (
        (gate_weights[:, :, None] * grad_final[:, None, :])
        .reshape(pair_count, model_width)
        .astype(jnp.bfloat16)
    )
    padded_grad = jnp.concatenate([pair_grads, zero_row], 0)
    send_grads = padded_grad[slot_pair].reshape(owner_count, local_count * CAP, model_width)
    if own_links:
        down_full, arrived, arrived_grad = expert_gather(
            [w_down], dp_count, 2, owner_count=owner_count, trades=[send_rows, send_grads]
        )
    else:
        down_full = lax.all_gather(w_down, "dp", axis=1, tiled=True)
        arrived = lax.all_to_all(send_rows, "expert", split_axis=0, concat_axis=0, tiled=True)
        arrived_grad = lax.all_to_all(send_grads, "expert", split_axis=0, concat_axis=0, tiled=True)
    arrived = arrived.reshape(owner_count, local_count, CAP, model_width)
    arrived_grad = arrived_grad.reshape(owner_count, local_count, CAP, model_width)
    gate_up = jnp.einsum(
        "secd,edf->secf", arrived, gate_up_full, preferred_element_type=jnp.float32
    )
    gate_part = gate_up[..., :hidden_count]
    up_part = gate_up[..., hidden_count:]
    squashed = lax.logistic(gate_part)
    silu_gate = gate_part * squashed
    activated = (silu_gate * up_part).astype(jnp.bfloat16)
    expert_out = jnp.einsum(
        "secf,efd->secd", activated, down_full, preferred_element_type=jnp.float32
    ).astype(jnp.bfloat16)
    returned = lax.all_to_all(
        expert_out.reshape(owner_count, local_count * CAP, model_width),
        "expert",
        split_axis=0,
        concat_axis=0,
        tiled=True,
    ).reshape(expert_count * CAP, model_width)
    padded_out = jnp.concatenate([returned, zero_row], 0)
    pair_out = padded_out[destination].reshape(row_count, 2, model_width).astype(jnp.float32)
    mixing = softmax_last(
        jnp.dot(normed_low, const_full, preferred_element_type=jnp.float32).reshape(
            row_count, const_count, 2
        )
    )
    vectors = vector_full.astype(jnp.float32).T
    const_val = mixing[..., 0:1] * normed_back[:, None, :] + mixing[..., 1:2] * vectors[None, :, :]
    copy_hit = (route_rows == expert_count + 1).astype(jnp.float32)
    const_hit = (
        route_rows[:, :, None] == expert_count + 2 + jnp.arange(const_count)[None, None, :]
    ).astype(jnp.float32)
    copy_weight = jnp.sum(gate_weights * copy_hit, -1)
    const_weight = jnp.sum(gate_weights[:, :, None] * const_hit, 1)
    expert_mix = (
        jnp.sum(gate_weights[:, :, None] * pair_out, 1)
        + copy_weight[:, None] * normed_back
        + jnp.sum(const_weight[:, :, None] * const_val, 1)
    )
    output = (middle + expert_mix).astype(jnp.bfloat16).reshape(tokens.shape)
    dot_copy = jnp.sum(grad_final * normed_back, -1)
    dot_const = jnp.sum(grad_final[:, None, :] * const_val, -1)
    grad_gates = (
        jnp.sum(pair_out * grad_final[:, None, :], -1)
        + copy_hit * dot_copy[:, None]
        + jnp.sum(const_hit * dot_const[:, None, :], -1)
    )
    grad_route = gate_weights * (grad_gates - jnp.sum(gate_weights * grad_gates, -1, keepdims=True))
    grad_logits = jnp.sum(jnp.where(picked, grad_route[:, :, None], 0.0), 1)
    logit_grad = grad_logits.astype(jnp.bfloat16).reshape(resid_logits.shape)
    grad_router = jnp.dot(normed_back.T, grad_logits, precision=highest)
    grad_normed = jnp.dot(grad_logits, router_full.astype(jnp.float32).T, precision=highest)
    grad_normed = grad_normed + copy_weight[:, None] * grad_final
    grad_const_val = const_weight[:, :, None] * grad_final[:, None, :]
    grad_mix_first = jnp.sum(grad_const_val * normed_back[:, None, :], -1)
    grad_mix_second = jnp.sum(grad_const_val * vectors[None, :, :], -1)
    mix_term = mixing[..., 0] * mixing[..., 1] * (grad_mix_first - grad_mix_second)
    grad_mix_logits = jnp.stack([mix_term, -mix_term], -1).reshape(row_count, 2 * const_count)
    grad_const = jnp.dot(normed_back.T, grad_mix_logits, precision=highest)
    grad_normed = (
        grad_normed
        + jnp.dot(grad_mix_logits, const_full.astype(jnp.float32).T, precision=highest)
        + jnp.sum(grad_const_val * mixing[..., 0:1], 1)
    )
    grad_vector = jnp.dot(grad_final.T, const_weight * mixing[..., 1], precision=highest)
    grad_down = jnp.einsum(
        "secf,secd->efd", activated, arrived_grad, preferred_element_type=jnp.float32
    )
    grad_act = jnp.einsum(
        "secd,efd->secf", arrived_grad, down_full, preferred_element_type=jnp.float32
    )
    grad_gate = grad_act * up_part * squashed * (1.0 + gate_part * (1.0 - squashed))
    grad_up = grad_act * silu_gate
    grad_gate_up = jnp.concatenate([grad_gate, grad_up], -1).astype(jnp.bfloat16)
    grad_expert_gu = jnp.einsum(
        "secd,secf->edf", arrived, grad_gate_up, preferred_element_type=jnp.float32
    )
    grad_rows = jnp.einsum(
        "secf,edf->secd", grad_gate_up, gate_up_full, preferred_element_type=jnp.float32
    ).astype(jnp.bfloat16)
    back_rows = lax.all_to_all(
        grad_rows.reshape(owner_count, local_count * CAP, model_width),
        "expert",
        split_axis=0,
        concat_axis=0,
        tiled=True,
    ).reshape(expert_count * CAP, model_width)
    padded_back = jnp.concatenate([back_rows, zero_row], 0)
    grad_normed = grad_normed + jnp.sum(
        padded_back[destination].reshape(row_count, 2, model_width).astype(jnp.float32), 1
    )
    grad_expert_gu = grad_expert_gu.astype(jnp.bfloat16)
    grad_down = grad_down.astype(jnp.bfloat16)
    grad_normed, grad_expert_gu, grad_down = lax.optimization_barrier(
        (grad_normed, grad_expert_gu, grad_down)
    )
    grad_expert_down = lax.psum_scatter(
        grad_down, "dp", scatter_dimension=1, tiled=True
    ).astype(jnp.float32)
    linked = local_count - 1 if own_links else local_count
    gu_parts = [
        lax.psum_scatter(grad_expert_gu[e], "dp", scatter_dimension=0, tiled=True).astype(
            jnp.float32
        )
        for e in range(linked)
    ]
    grad_middle, grad_gain_two = normalize_back(middle, scale_two, gain_second, grad_normed)
    grad_middle = grad_middle + grad_final
    grad_branch = grad_middle.astype(jnp.bfloat16)
    grad_out_w = lax.dot_general(
        attended, grad_branch, (((0,), (0,)), ((), ())), preferred_element_type=jnp.float32
    )
    grad_attended = lax.dot_general(
        grad_branch, out_full, (((1,), (1,)), ((), ())), preferred_element_type=jnp.float32
    ).astype(jnp.bfloat16)
    grad_query, grad_key, grad_value = lax.map(
        lambda seq_items: attend_backward(
            seq_items[0],
            seq_items[1],
            seq_items[2],
            seq_items[3],
            seq_items[4],
            seq_items[5],
            score_scale,
        ),
        (
            queries.reshape(shape_seq),
            keys_all.reshape(shape_seq),
            values_all.reshape(shape_seq),
            doc_ids,
            log_sums,
            grad_attended.reshape(shape_seq),
        ),
    )
    grad_query = rotate_back(grad_query.reshape(head_shape), cosine_table, sine_table)
    grad_key = rotate_back(grad_key.reshape(head_shape), cosine_table, sine_table)
    grad_projected = jnp.concatenate(
        [
            grad_query.reshape(row_count, model_width),
            grad_key.reshape(row_count, model_width),
            grad_value.reshape(row_count, model_width),
        ],
        -1,
    ).astype(jnp.bfloat16)
    grad_qkv = lax.dot_general(
        normed_one, grad_projected, (((0,), (0,)), ((), ())), preferred_element_type=jnp.float32
    )
    grad_normed_one = lax.dot_general(
        grad_projected, qkv_full, (((1,), (1,)), ((), ())), preferred_element_type=jnp.float32
    )
    grad_inputs, grad_gain_one = normalize_back(inputs, scale_one, gain_first, grad_normed_one)
    token_grad = (grad_inputs + grad_middle).astype(jnp.bfloat16).reshape(tokens.shape)
    small_grads = [
        grad_router,
        grad_const,
        grad_vector,
        grad_gain_one[:, None],
        grad_gain_two[:, None],
    ]
    packed_grads = jnp.concatenate(
        [part.astype(jnp.bfloat16) for part in [grad_qkv, grad_out_w] + small_grads]
        + [jnp.zeros((model_width, pad_width), jnp.bfloat16)],
        1,
    )
    if own_links:
        gu_part, packed_part = final_reduce(
            grad_expert_gu[linked].reshape(dp_count, model_width // dp_count, 2 * hidden_count),
            packed_grads.reshape(dp_count, model_width // dp_count, packed_grads.shape[1]),
            3,
        )
        gu_parts = gu_parts + [gu_part]
    else:
        packed_part = lax.psum_scatter(packed_grads, "dp", scatter_dimension=0, tiled=True)
        packed_part = lax.psum(packed_part, "expert").astype(jnp.float32)
    grad_expert_gu = jnp.stack(gu_parts)
    part_qkv = packed_part[:, :width_qkv]
    part_out = packed_part[:, width_qkv : width_qkv + width_out]
    small_part = packed_part[:, width_qkv + width_out :]
    part_router = small_part[:, :router_width]
    part_const = small_part[:, router_width : router_width + const_width]
    first = router_width + const_width
    part_vector = small_part[:, first : first + v_const.shape[1]]
    first = first + v_const.shape[1]
    part_gain_one, part_gain_two = small_part[:, first], small_part[:, first + 1]
    return (
        output,
        token_grad,
        logit_grad,
        part_qkv,
        part_out,
        part_gain_one,
        part_gain_two,
        part_router,
        part_const,
        part_vector,
        grad_expert_gu,
        grad_expert_down,
    )


def solution(mesh):
    placed = (
        P(("dp", "expert"), None, None),
        P(("dp", "expert"), None, None),
        P(("dp", "expert"), None, None),
        P(("dp", "expert"), None),
        P("dp", None),
        P("dp", None),
        P("dp"),
        P("dp"),
        P("dp", None),
        P("dp", None),
        P("dp", None),
        P("expert", "dp", None),
        P("expert", "dp", None),
        P(("dp", "expert"), None, None),
    )
    return jax.shard_map(
        shards,
        mesh=mesh,
        in_specs=placed,
        out_specs=(
            P(("dp", "expert"), None, None),
            P(("dp", "expert"), None, None),
            P(("dp", "expert"), None, None),
            P("dp", None),
            P("dp", None),
            P("dp"),
            P("dp"),
            P("dp", None),
            P("dp", None),
            P("dp", None),
            P("expert", "dp", None),
            P("expert", "dp", None),
        ),
        check_vma=False,
    )
```

```python
import functools

import jax
import jax.numpy as jnp
import numpy as np
from jax import lax
from jax.experimental import pallas as pl
from jax.experimental.pallas import tpu as pltpu
from jax.sharding import PartitionSpec as P

HEADS = 12
BLOCK = 256
CAP = 256
GROUP = 256
MESH = pl.DeviceIdType.MESH
epsilon = 1e-06


def rotary_lanes(length, head_dim):
    half_dim = head_dim // 2
    frequency = (10000.0 ** (-np.arange(half_dim, dtype=np.float32) / half_dim)).astype(np.float32)
    angles = (np.arange(length, dtype=np.float32)[:, None] * frequency[None, :]).astype(np.float64)
    cosine = np.cos(angles).astype(np.float32)
    sine = np.sin(angles).astype(np.float32)
    return (
        np.concatenate([cosine] * 4, 1),
        np.concatenate([-sine, sine, -sine, sine], 1),
    )


def nt(left, right):
    return lax.dot_general(left, right, (((1,), (1,)), ((), ())), preferred_element_type=jnp.float32)


def tn(left, right):
    return lax.dot_general(left, right, (((0,), (0,)), ((), ())), preferred_element_type=jnp.float32)


def nn(left, right):
    return jnp.dot(left, right, preferred_element_type=jnp.float32)


def lane_ids(shape):
    return lax.broadcasted_iota(jnp.int32, shape, len(shape) - 1)


def turn(values, cosine, sine):
    lanes = lane_ids(values.shape)
    ahead, behind = pltpu.roll(values, 96, 1), pltpu.roll(values, 32, 1)
    return values * cosine + jnp.where(lanes % 64 < 32, ahead, behind) * sine


def key_span(i):
    return max(0, i - 2) * BLOCK, (i + 1) * BLOCK


def mask_of(docs_column, docs_row, i):
    low, high = key_span(i)
    return docs_column[low:high, :] == docs_row[:, i * BLOCK : (i + 1) * BLOCK]


def attention_forward_kernel(
    tokens_ref, wq_ref, wk_ref, wv_ref, wo_ref, small_ref, docs_row_ref, docs_column_ref,
    cosine_ref, sine_ref, routes_ref, resid_ref,
    normed_ref, q_ref, k_ref, v_ref, attended_ref, middle_ref, normed_two_ref, aux_ref,
    branch_ref,
):
    step = pl.program_id(0)
    rows = tokens_ref.shape[0]

    @pl.when(step == 0)
    def _():
        inputs = tokens_ref[...].astype(jnp.float32)
        gains = jnp.transpose(small_ref[:, :128].astype(jnp.float32))[18:19, :]
        scale = lax.rsqrt(jnp.mean(inputs * inputs, -1, keepdims=True) + epsilon)
        normed_ref[...] = (inputs * scale * gains).astype(jnp.bfloat16)
        branch_ref[...] = jnp.zeros_like(branch_ref)

    normed = normed_ref[...]
    cosine, sine = cosine_ref[...], sine_ref[...]
    for w_ref, out_ref, turned in ((wq_ref, q_ref, True), (wk_ref, k_ref, True), (wv_ref, v_ref, False)):
        projected = nn(normed, w_ref[...])
        for half in range(2):
            part = projected[:, half * 128 : half * 128 + 128]
            if turned:
                part = turn(part, cosine, sine)
            out_ref[:, half * 128 : half * 128 + 128] = part.astype(jnp.bfloat16)

    docs_row, docs_column = docs_row_ref[...], docs_column_ref[...]
    for i in range(rows // BLOCK):
        low, high = key_span(i)
        here = slice(i * BLOCK, (i + 1) * BLOCK)
        allowed = mask_of(docs_column, docs_row, i)
        for pair in range(2):
            lanes = slice(pair * 128, pair * 128 + 128)
            queries = q_ref[here, lanes] * jnp.asarray(0.125, jnp.bfloat16)
            keys, values = k_ref[low:high, lanes], v_ref[low:high, lanes]
            left = lane_ids(queries.shape) < 64
            outs = []
            for head in range(2):
                own = left if head == 0 else jnp.logical_not(left)
                scores = nt(keys, jnp.where(own, queries, jnp.zeros_like(queries)))
                scores = jnp.where(allowed, scores, -1e30)
                shifted = jnp.exp(scores - jnp.max(scores, 0, keepdims=True))
                probs = shifted * (1.0 / jnp.sum(shifted, 0, keepdims=True))
                outs.append(tn(probs.astype(jnp.bfloat16), values))
            attended_ref[here, lanes] = jnp.where(left, outs[0], outs[1]).astype(jnp.bfloat16)
    branch_ref[...] += nn(attended_ref[...], wo_ref[...])

    @pl.when(step == pl.num_programs(0) - 1)
    def _():
        small = small_ref[:, :128]
        gains = jnp.transpose(small.astype(jnp.float32))[19:20, :]
        middle = tokens_ref[...].astype(jnp.float32) + branch_ref[...]
        middle_ref[...] = middle
        scale = lax.rsqrt(jnp.mean(middle * middle, -1, keepdims=True) + epsilon)
        normed_two = (middle * scale * gains).astype(jnp.bfloat16)
        normed_two_ref[...] = normed_two
        logits = nn(normed_two, small) + resid_ref[...].astype(jnp.float32)
        lanes = lane_ids(logits.shape)

        def lane(at):
            return jnp.sum(jnp.where(lanes == at, logits, 0.0), -1, keepdims=True)

        def two(first, second):
            peak = jnp.maximum(first, second)
            first, second = jnp.exp(first - peak), jnp.exp(second - peak)
            return first / (first + second), second / (first + second)

        columns = list(two(lane(routes_ref[:, 0:1]), lane(routes_ref[:, 1:2])))
        columns += list(two(lane(12), lane(13))) + list(two(lane(14), lane(15)))
        columns.append(scale)
        aux = jnp.zeros_like(logits)
        for at, column in enumerate(columns):
            aux = jnp.where(lanes == at, column, aux)
        aux_ref[...] = aux


def attention_forward(tokens, packed, docs_row, docs_column, cosine, sine, routes, resid):
    rows, width = tokens.shape
    groups = width // GROUP
    low = jnp.bfloat16
    whole = lambda shape: pl.BlockSpec(shape, lambda j: (0, 0))
    column = lambda at: pl.BlockSpec((width, GROUP), lambda j: (0, at + j))
    out_column = pl.BlockSpec((rows, GROUP), lambda j: (0, j))
    full = jax.ShapeDtypeStruct((rows, width), low)
    return pl.pallas_call(
        attention_forward_kernel,
        grid=(groups,),
        out_shape=[full] * 5
        + [
            jax.ShapeDtypeStruct((rows, width), jnp.float32),
            full,
            jax.ShapeDtypeStruct((rows, 128), jnp.float32),
        ],
        in_specs=[
            whole((rows, width)),
            column(0),
            column(groups),
            column(2 * groups),
            pl.BlockSpec((GROUP, width), lambda j: (j, 3)),
            pl.BlockSpec((width, 256), lambda j: (0, 12)),
            whole((1, rows)),
            whole((rows, 1)),
            whole((rows, 128)),
            whole((rows, 128)),
            whole((rows, 2)),
            whole((rows, 128)),
        ],
        out_specs=[whole((rows, width))]
        + [out_column] * 4
        + [whole((rows, width)), whole((rows, width)), whole((rows, 128))],
        scratch_shapes=[pltpu.VMEM((rows, width), jnp.float32)],
        compiler_params=pltpu.CompilerParams(
            dimension_semantics=("arbitrary",), vmem_limit_bytes=56 * 2**20
        ),
        cost_estimate=pl.CostEstimate(
            flops=2 * rows * width * 4 * width + 8 * rows * rows * width // 2,
            bytes_accessed=24 * rows * width,
            transcendentals=rows * rows * HEADS // 2,
        ),
        name="attention_forward",
    )(tokens, packed, packed, packed, packed, packed, docs_row, docs_column, cosine, sine, routes, resid)


def attention_backward_kernel(
    grad_middle_ref, q_ref, k_ref, v_ref, attended_ref, normed_ref, tokens_ref,
    wq_ref, wk_ref, wv_ref, wo_ref, small_ref, docs_row_ref, docs_column_ref,
    cosine_ref, sine_ref, small_grad_ref,
    token_grad_ref, gq_ref, gk_ref, gv_ref, go_ref, small_out_ref,
    branch_ref, back_ref, turned_ref, key_acc, value_acc, query_acc,
):
    step = pl.program_id(0)
    rows, width = tokens_ref.shape

    @pl.when(step == 0)
    def _():
        branch_ref[...] = grad_middle_ref[...].astype(jnp.bfloat16)
        back_ref[...] = jnp.zeros_like(back_ref)

    grad_branch = branch_ref[...]
    grad_attended = nt(grad_branch, wo_ref[...]).astype(jnp.bfloat16)
    go_ref[...] = tn(attended_ref[...], grad_branch).astype(jnp.bfloat16)
    cosine, sine = cosine_ref[...], sine_ref[...]
    docs_row, docs_column = docs_row_ref[...], docs_column_ref[...]
    for pair in range(2):
        lanes = slice(pair * 128, pair * 128 + 128)
        key_acc[...] = jnp.zeros_like(key_acc)
        value_acc[...] = jnp.zeros_like(value_acc)
        for i in range(rows // BLOCK):
            low, high = key_span(i)
            here = slice(i * BLOCK, (i + 1) * BLOCK)
            allowed = mask_of(docs_column, docs_row, i)
            queries = q_ref[here, lanes] * jnp.asarray(0.125, jnp.bfloat16)
            grads = grad_attended[here, lanes]
            keys, values = k_ref[low:high, lanes], v_ref[low:high, lanes]
            left = lane_ids(queries.shape) < 64
            query_grads = []
            key_grad, value_grad = None, None
            for head in range(2):
                own = left if head == 0 else jnp.logical_not(left)
                own_queries = jnp.where(own, queries, jnp.zeros_like(queries))
                own_grads = jnp.where(own, grads, jnp.zeros_like(grads))
                scores = jnp.where(allowed, nt(keys, own_queries), -1e30)
                shifted = jnp.exp(scores - jnp.max(scores, 0, keepdims=True))
                probs = shifted * (1.0 / jnp.sum(shifted, 0, keepdims=True))
                grad_probs = nt(values, own_grads)
                inner = jnp.sum(probs * grad_probs, 0, keepdims=True)
                grad_scores = (probs * (grad_probs - inner)).astype(jnp.bfloat16)
                part_value = nn(probs.astype(jnp.bfloat16), own_grads)
                part_key = nn(grad_scores, own_queries)
                value_grad = part_value if head == 0 else value_grad + part_value
                key_grad = part_key if head == 0 else key_grad + part_key
                query_grads.append(tn(grad_scores, keys))
            value_acc[low:high, :] += value_grad
            key_acc[low:high, :] += key_grad
            query_acc[here, :] = jnp.where(left, query_grads[0], query_grads[1]) * 0.125
        turned_ref[0, :, lanes] = turn(query_acc[...], cosine, -sine).astype(jnp.bfloat16)
        turned_ref[1, :, lanes] = turn(key_acc[...], cosine, -sine).astype(jnp.bfloat16)
        turned_ref[2, :, lanes] = value_acc[...].astype(jnp.bfloat16)
    normed = normed_ref[...]
    for at, (w_ref, out_ref) in enumerate(((wq_ref, gq_ref), (wk_ref, gk_ref), (wv_ref, gv_ref))):
        turned = turned_ref[at]
        out_ref[...] = tn(normed, turned).astype(jnp.bfloat16)
        back_ref[...] += nt(turned, w_ref[...])

    @pl.when(step == pl.num_programs(0) - 1)
    def _():
        gains = jnp.transpose(small_ref[:, :128].astype(jnp.float32))[18:19, :]
        inputs = tokens_ref[...].astype(jnp.float32)
        grads = back_ref[...]
        scale = lax.rsqrt(jnp.mean(inputs * inputs, -1, keepdims=True) + epsilon)
        weighted = grads * gains
        mean = jnp.mean(weighted * inputs, -1, keepdims=True)
        grad_inputs = scale * weighted - inputs * (scale * scale * scale * mean)
        token_grad_ref[...] = (grad_inputs + grad_middle_ref[...]).astype(jnp.bfloat16)
        gain_grad = jnp.sum(grads * inputs * scale, 0, keepdims=True)
        column = jnp.transpose(jnp.broadcast_to(gain_grad, (128, width)))
        small_grad = small_grad_ref[...]
        small_grad = jnp.where(lane_ids(small_grad.shape) == 18, column, small_grad)
        small_out_ref[:, :128] = small_grad.astype(jnp.bfloat16)
        small_out_ref[:, 128:] = jnp.zeros((width, 128), jnp.bfloat16)


def attention_backward(
    grad_middle, queries, keys, values, attended, normed, tokens, packed, docs_row, docs_column,
    cosine, sine, small_grad,
):
    rows, width = tokens.shape
    groups = width // GROUP
    low = jnp.bfloat16
    whole = lambda shape: pl.BlockSpec(shape, lambda j: (0, 0))
    column = lambda at: pl.BlockSpec((width, GROUP), lambda j: (0, at + j))
    by_group = pl.BlockSpec((rows, GROUP), lambda j: (0, j))
    weight = jax.ShapeDtypeStruct((width, width), low)
    return pl.pallas_call(
        attention_backward_kernel,
        grid=(groups,),
        out_shape=[jax.ShapeDtypeStruct((rows, width), low)]
        + [weight] * 4
        + [jax.ShapeDtypeStruct((width, 256), low)],
        in_specs=[
            whole((rows, width)),
            by_group,
            by_group,
            by_group,
            by_group,
            whole((rows, width)),
            whole((rows, width)),
            column(0),
            column(groups),
            column(2 * groups),
            pl.BlockSpec((GROUP, width), lambda j: (j, 3)),
            pl.BlockSpec((width, 256), lambda j: (0, 12)),
            whole((1, rows)),
            whole((rows, 1)),
            whole((rows, 128)),
            whole((rows, 128)),
            whole((width, 128)),
        ],
        out_specs=[
            whole((rows, width)),
            column(0),
            column(0),
            column(0),
            pl.BlockSpec((GROUP, width), lambda j: (j, 0)),
            whole((width, 256)),
        ],
        scratch_shapes=[
            pltpu.VMEM((rows, width), low),
            pltpu.VMEM((rows, width), jnp.float32),
            pltpu.VMEM((3, rows, GROUP), low),
            pltpu.VMEM((rows, 128), jnp.float32),
            pltpu.VMEM((rows, 128), jnp.float32),
            pltpu.VMEM((rows, 128), jnp.float32),
        ],
        compiler_params=pltpu.CompilerParams(
            dimension_semantics=("arbitrary",), vmem_limit_bytes=56 * 2**20
        ),
        cost_estimate=pl.CostEstimate(
            flops=4 * rows * width * 4 * width + 20 * rows * rows * width // 2,
            bytes_accessed=32 * rows * width,
            transcendentals=rows * rows * HEADS // 2,
        ),
        name="attention_backward",
    )(
        grad_middle, queries, keys, values, attended, normed, tokens, packed, packed, packed,
        packed, packed, docs_row, docs_column, cosine, sine, small_grad,
    )


def routing_kernel(expert_count, routes_ref, columns_ref, rows_ref):
    rows = routes_ref.shape[0]
    lanes = lane_ids((rows, 128))
    first = (lanes == routes_ref[:, 0:1]).astype(jnp.float32)
    second = (lanes == routes_ref[:, 1:2]).astype(jnp.float32)
    down = lax.broadcasted_iota(jnp.int32, (rows, rows), 0)
    lower = (down > lane_ids((rows, rows))).astype(jnp.bfloat16)
    before_first = nn(lower, first.astype(jnp.bfloat16))
    before_second = nn(lower, second.astype(jnp.bfloat16)) + jnp.sum(first, 0, keepdims=True)
    spots = []
    for picked, before, at in ((first, before_first, 0), (second, before_second, 1)):
        rank = jnp.sum(picked * before, -1, keepdims=True)
        route = routes_ref[:, at : at + 1]
        spot = route.astype(jnp.float32) * CAP + rank
        spots.append(jnp.where(route < expert_count, spot, jnp.full_like(spot, 2.0 * expert_count * CAP)))
    both = jnp.where(lanes == 0, spots[0], jnp.where(lanes == 1, spots[1], 0.0))
    columns_ref[...] = both.astype(jnp.int32)
    rows_ref[...] = jnp.transpose(both)[0:8, :].astype(jnp.int32)


def routing(routes, expert_count):
    rows = routes.shape[0]
    return pl.pallas_call(
        functools.partial(routing_kernel, expert_count),
        out_shape=[
            jax.ShapeDtypeStruct((rows, 128), jnp.int32),
            jax.ShapeDtypeStruct((8, rows), jnp.int32),
        ],
        compiler_params=pltpu.CompilerParams(vmem_limit_bytes=40 * 2**20),
        name="routing",
    )(routes)


def dispatch_kernel(spots_ref, aux_ref, normed_ref, cot_ref, rows_ref, grads_ref, gates_ref):
    step = pl.program_id(0)

    @pl.when(step == 0)
    def _():
        gates_ref[...] = jnp.transpose(aux_ref[...])[0:8, :]

    shape = (rows_ref.shape[0], normed_ref.shape[0])
    slots = step * rows_ref.shape[0] + lax.broadcasted_iota(jnp.int32, shape, 0)
    first, second = slots == spots_ref[0:1, :], slots == spots_ref[1:2, :]
    gates = jnp.sum(
        jnp.where(first, gates_ref[0:1, :], jnp.where(second, gates_ref[1:2, :], 0.0)), -1, keepdims=True
    )
    chosen = jnp.where(first | second, 1.0, 0.0).astype(jnp.bfloat16)
    rows_ref[...] = nn(chosen, normed_ref[...]).astype(jnp.bfloat16)
    grads_ref[...] = (nn(chosen, cot_ref[...]) * gates).astype(jnp.bfloat16)


def dispatch(spots, aux, normed, cot, slot_count):
    rows, width = normed.shape
    whole = lambda shape: pl.BlockSpec(shape, lambda j: (0, 0))
    block = pl.BlockSpec((CAP, width), lambda j: (j, 0))
    return pl.pallas_call(
        dispatch_kernel,
        grid=(slot_count // CAP,),
        out_shape=[jax.ShapeDtypeStruct((slot_count, width), jnp.bfloat16)] * 2,
        in_specs=[whole((8, rows)), whole((rows, 128)), whole((rows, width)), whole((rows, width))],
        out_specs=[block, block],
        scratch_shapes=[pltpu.VMEM((8, rows), jnp.float32)],
        compiler_params=pltpu.CompilerParams(
            dimension_semantics=("arbitrary",), vmem_limit_bytes=40 * 2**20
        ),
        cost_estimate=pl.CostEstimate(
            flops=4 * slot_count * rows * width,
            bytes_accessed=4 * (rows + slot_count) * width,
            transcendentals=0,
        ),
        name="dispatch",
    )(spots, aux, normed, cot)


def halves(values):
    high = values.astype(jnp.bfloat16)
    return high, (values - high.astype(jnp.float32)).astype(jnp.bfloat16)


def combine_kernel(
    expert_count, returned_ref, spots_ref, routes_ref, aux_ref, normed_ref, middle_ref, cot_ref, small_ref,
    output_ref, logit_ref, grad_ref, small_grad_ref, vectors_ref,
):
    step = pl.program_id(0)

    @pl.when(step == 0)
    def _():
        vectors_ref[...] = jnp.transpose(small_ref[:, :128].astype(jnp.float32))[16:24, :]
        small_grad_ref[...] = jnp.zeros_like(small_grad_ref)

    rows = normed_ref.shape[0]
    slots = lane_ids((rows, returned_ref.shape[0]))
    returned = returned_ref[...]
    normed_low, cot_low = normed_ref[...], cot_ref[...]
    normed, cot = normed_low.astype(jnp.float32), cot_low.astype(jnp.float32)
    total = lambda values: jnp.sum(values, -1, keepdims=True)
    picks, inner = [], []
    for s in range(2):
        chosen = jnp.where(slots == spots_ref[:, s : s + 1], 1.0, 0.0).astype(jnp.bfloat16)
        pick = nn(chosen, returned)
        picks.append(pick)
        inner.append(total(pick * cot))
    gates = [aux_ref[:, s : s + 1] for s in range(2)]
    routes = [routes_ref[:, s : s + 1] for s in range(2)]
    dot_copy = total(cot * normed)

    def weight_of(route):
        return sum(jnp.where(routes[s] == route, gates[s], 0.0) for s in range(2))

    copy_weight = weight_of(expert_count + 1)
    mix = gates[0] * picks[0] + gates[1] * picks[1]
    pass_weight = copy_weight
    gate_grads = [
        inner[s] + jnp.where(routes[s] == expert_count + 1, dot_copy, 0.0) for s in range(2)
    ]
    lanes = lane_ids((rows, 128))
    spread = jnp.zeros((rows, 128), jnp.float32)
    for k in range(2):
        vector = vectors_ref[k : k + 1, :]
        keep, blend = aux_ref[:, 2 + 2 * k : 3 + 2 * k], aux_ref[:, 3 + 2 * k : 4 + 2 * k]
        weight = weight_of(expert_count + 2 + k)
        dot_vector = total(cot * vector)
        pass_weight = pass_weight + weight * keep
        mix = mix + (weight * blend) * vector
        value = keep * dot_copy + blend * dot_vector
        for s in range(2):
            gate_grads[s] = gate_grads[s] + jnp.where(routes[s] == expert_count + 2 + k, value, 0.0)
        term = keep * blend * (weight * dot_copy - weight * dot_vector)
        spread = jnp.where(lanes == 12 + 2 * k, term, spread)
        spread = jnp.where(lanes == 13 + 2 * k, -term, spread)
        spread = jnp.where(lanes == 16 + k, weight * blend, spread)
    mix = mix + pass_weight * normed
    output_ref[...] = (middle_ref[...] + mix).astype(jnp.bfloat16)
    mean = gates[0] * gate_grads[0] + gates[1] * gate_grads[1]
    for s in range(2):
        spread = jnp.where(lanes == routes[s], gates[s] * (gate_grads[s] - mean), spread)
    logit_ref[...] = spread[:, : logit_ref.shape[1]].astype(jnp.bfloat16)
    logits = jnp.where(lanes < 16, spread, 0.0)
    high, low = halves(logits)
    small = small_ref[:, :128]
    grad_ref[...] = pass_weight * cot + nt(high, small) + nt(low, small)
    vector_high, vector_low = halves(spread - logits)
    small_grad_ref[...] += (
        tn(normed_low, high) + tn(normed_low, low) + tn(cot_low, vector_high) + tn(cot_low, vector_low)
    )


def combine(returned, spots, routes, aux, normed, middle, cot, packed, choice_count, expert_count):
    rows, width = normed.shape
    slot_count = returned.shape[0]
    size = 256
    block = lambda columns: pl.BlockSpec((size, columns), lambda j: (j, 0))
    whole = lambda shape: pl.BlockSpec(shape, lambda j: (0, 0))
    return pl.pallas_call(
        functools.partial(combine_kernel, expert_count),
        grid=(rows // size,),
        out_shape=[
            jax.ShapeDtypeStruct((rows, width), jnp.bfloat16),
            jax.ShapeDtypeStruct((rows, choice_count), jnp.bfloat16),
            jax.ShapeDtypeStruct((rows, width), jnp.float32),
            jax.ShapeDtypeStruct((width, 128), jnp.float32),
        ],
        in_specs=[
            whole((slot_count, width)),
            block(128),
            block(2),
            block(128),
            block(width),
            block(width),
            block(width),
            pl.BlockSpec((width, 256), lambda j: (0, 12)),
        ],
        out_specs=[block(width), block(choice_count), block(width), whole((width, 128))],
        scratch_shapes=[pltpu.VMEM((8, width), jnp.float32)],
        compiler_params=pltpu.CompilerParams(
            dimension_semantics=("arbitrary",), vmem_limit_bytes=48 * 2**20
        ),
        cost_estimate=pl.CostEstimate(
            flops=4 * slot_count * rows * width,
            bytes_accessed=16 * rows * width + 2 * slot_count * width,
            transcendentals=0,
        ),
        name="combine",
    )(returned, spots, routes, aux, normed, middle, cot, packed)


def combine_back_kernel(
    back_ref, spots_ref, aux_ref, middle_ref, cot_ref, grad_ref, small_ref, small_grad_ref,
    grad_middle_ref, small_out_ref, gain_ref,
):
    step = pl.program_id(0)

    @pl.when(step == 0)
    def _():
        gain_ref[0:8, :] = jnp.transpose(small_ref[:, :128].astype(jnp.float32))[16:24, :]
        gain_ref[8:16, :] = jnp.zeros((8, gain_ref.shape[1]), jnp.float32)

    rows, width = middle_ref.shape
    slots = lane_ids((rows, back_ref.shape[0]))
    chosen = jnp.where(
        (slots == spots_ref[:, 0:1]) | (slots == spots_ref[:, 1:2]), 1.0, 0.0
    ).astype(jnp.bfloat16)
    grads = grad_ref[...] + nn(chosen, back_ref[...])
    middle, scale = middle_ref[...], aux_ref[:, 6:7]
    gain_ref[8:9, :] += jnp.sum(grads * middle * scale, 0, keepdims=True)
    weighted = grads * gain_ref[3:4, :]
    mean = jnp.mean(weighted * middle, -1, keepdims=True)
    grad_middle_ref[...] = (
        cot_ref[...].astype(jnp.float32) + scale * weighted - middle * (scale * scale * scale * mean)
    )

    @pl.when(step == pl.num_programs(0) - 1)
    def _():
        column = jnp.transpose(jnp.broadcast_to(gain_ref[8:9, :], (128, width)))
        small_grad = small_grad_ref[...]
        small_out_ref[...] = jnp.where(lane_ids(small_grad.shape) == 19, column, small_grad)


def combine_back(back, spots, aux, middle, cot, grad, packed, small_grad):
    rows, width = middle.shape
    slot_count = back.shape[0]
    size = 256
    block = lambda columns: pl.BlockSpec((size, columns), lambda j: (j, 0))
    whole = lambda shape: pl.BlockSpec(shape, lambda j: (0, 0))
    return pl.pallas_call(
        combine_back_kernel,
        grid=(rows // size,),
        out_shape=[
            jax.ShapeDtypeStruct((rows, width), jnp.float32),
            jax.ShapeDtypeStruct((width, 128), jnp.float32),
        ],
        in_specs=[
            whole((slot_count, width)),
            block(128),
            block(128),
            block(width),
            block(width),
            block(width),
            pl.BlockSpec((width, 256), lambda j: (0, 12)),
            whole((width, 128)),
        ],
        out_specs=[block(width), whole((width, 128))],
        scratch_shapes=[pltpu.VMEM((16, width), jnp.float32)],
        compiler_params=pltpu.CompilerParams(
            dimension_semantics=("arbitrary",), vmem_limit_bytes=48 * 2**20
        ),
        cost_estimate=pl.CostEstimate(
            flops=2 * slot_count * rows * width,
            bytes_accessed=14 * rows * width + 2 * slot_count * width,
            transcendentals=0,
        ),
        name="combine_back",
    )(back, spots, aux, middle, cot, grad, packed, small_grad)


def dp_grid(dp_count):
    outer = 4 if dp_count % 4 == 0 else 1
    return outer, dp_count // outer


def place():
    me, mine = lax.axis_index("dp"), lax.axis_index("expert")
    return me, mine


def greet(peers):
    barrier = pltpu.get_barrier_semaphore()
    for peer in peers:
        pl.semaphore_signal(barrier, inc=1, device_id=peer, device_id_type=MESH)
    pl.semaphore_wait(barrier, len(peers))


def small_gather_kernel(dp_count, shard_ref, full_ref, send_sem, pass_sem, recv_sem, mate_sem, own_sem):
    outer_count, inner_count = dp_grid(dp_count)
    me, mine = place()
    outer, inner = me // inner_count, me % inner_count
    rows, columns = shard_ref.shape
    half = columns // 2
    side = pl.multiple_of((mine % 2) * half, 128)
    mate = mine + 1 - 2 * (mine % 2)
    outer_peers = [lax.rem(outer + k, outer_count) for k in range(1, outer_count)]
    inner_peers = [lax.rem(inner + k, inner_count) for k in range(1, inner_count)]
    greet(
        [(peer * inner_count + inner, mine) for peer in outer_peers]
        + [(outer * inner_count + peer, mine) for peer in inner_peers]
        + [(me, mate)]
    )

    def spot(chunk):
        return full_ref.at[pl.ds(pl.multiple_of(chunk * rows, 8), rows), pl.ds(side, half)]

    sent = []

    def send(source, chunk, device, send_at, recv_at):
        copy = pltpu.make_async_remote_copy(
            src_ref=source,
            dst_ref=spot(chunk),
            send_sem=send_at,
            recv_sem=recv_at,
            device_id=device,
            device_id_type=MESH,
        )
        copy.start()
        sent.append(copy)

    def arrived(chunk):
        pltpu.make_async_copy(spot(chunk), spot(chunk), recv_sem.at[chunk]).wait()

    own_half = shard_ref.at[:, pl.ds(side, half)]
    for k, peer in enumerate(outer_peers):
        send(own_half, me, (peer * inner_count + inner, mine), send_sem.at[0, k], recv_sem.at[me])
    for k, peer in enumerate(inner_peers):
        send(own_half, me, (outer * inner_count + peer, mine), send_sem.at[1, k], recv_sem.at[me])
    own = pltpu.make_async_copy(
        shard_ref, full_ref.at[pl.ds(pl.multiple_of(me * rows, 8), rows), :], own_sem
    )
    own.start()
    chunks = []
    for k, peer in enumerate(outer_peers):
        chunk = peer * inner_count + inner
        arrived(chunk)
        for j, other in enumerate(inner_peers):
            send(spot(chunk), chunk, (outer * inner_count + other, mine), send_sem.at[2 + k, j], recv_sem.at[chunk])
        send(spot(chunk), chunk, (me, mate), pass_sem.at[len(chunks)], mate_sem.at[chunk])
        chunks.append(chunk)
    for other in inner_peers:
        for peer in [outer] + outer_peers:
            chunk = peer * inner_count + other
            arrived(chunk)
            send(spot(chunk), chunk, (me, mate), pass_sem.at[len(chunks)], mate_sem.at[chunk])
            chunks.append(chunk)
    own.wait()
    for chunk in chunks:
        there = full_ref.at[
            pl.ds(pl.multiple_of(chunk * rows, 8), rows), pl.ds(pl.multiple_of(half - side, 128), half)
        ]
        pltpu.make_async_copy(there, there, mate_sem.at[chunk]).wait()
    for copy in sent:
        copy.wait_send()


def small_gather(shard, dp_count, collective):
    outer_count, inner_count = dp_grid(dp_count)
    rows, columns = shard.shape
    lanes = max(outer_count, inner_count)
    return pl.pallas_call(
        functools.partial(small_gather_kernel, dp_count),
        out_shape=jax.ShapeDtypeStruct((dp_count * rows, columns), shard.dtype),
        in_specs=[pl.BlockSpec(memory_space=pl.ANY)],
        out_specs=pl.BlockSpec(memory_space=pl.ANY),
        scratch_shapes=[
            pltpu.SemaphoreType.DMA((outer_count + 1, lanes)),
            pltpu.SemaphoreType.DMA((dp_count,)),
            pltpu.SemaphoreType.DMA((dp_count,)),
            pltpu.SemaphoreType.DMA((dp_count,)),
            pltpu.SemaphoreType.DMA,
        ],
        compiler_params=pltpu.CompilerParams(collective_id=collective, has_side_effects=True),
        name="small_gather",
    )(shard)


def expert_gather_kernel(dp_count, tensor_count, cuts, crossed, owner_count, trade_count, *refs):
    given = tensor_count + trade_count
    shards, outgoing = refs[:tensor_count], refs[tensor_count:given]
    fulls, incoming = refs[given : given + tensor_count], refs[given + tensor_count : 2 * given]
    send_sem, recv_sem, own_sem, trade_send, trade_recv = refs[2 * given :]
    outer_count, inner_count = dp_grid(dp_count)
    me, mine = place()
    outer, inner = me // inner_count, me % inner_count
    below, above = lax.rem(outer + outer_count - 1, outer_count), lax.rem(outer + 1, outer_count)
    inner_peers = [lax.rem(inner + k, inner_count) for k in range(1, inner_count)]
    greet(
        [(peer * inner_count + inner, mine) for peer in (below, above)]
        + [(outer * inner_count + peer, mine) for peer in inner_peers]
        + [(me, lax.rem(mine + k, owner_count)) for k in range(1, owner_count) if trade_count]
    )
    trades = []
    for t in range(trade_count):
        for k in range(1, owner_count):
            peer = lax.rem(mine + k, owner_count)
            trade = pltpu.make_async_remote_copy(
                src_ref=outgoing[t].at[peer],
                dst_ref=incoming[t].at[mine],
                send_sem=trade_send.at[t, k],
                recv_sem=trade_recv.at[t, mine],
                device_id=(me, peer),
                device_id_type=MESH,
            )
            trade.start()
            trades.append(trade)
        keep = pltpu.make_async_copy(
            outgoing[t].at[mine], incoming[t].at[mine], trade_send.at[t, 0]
        )
        keep.start()
    pieces = [
        (t, e, c) for t in range(tensor_count) for e in range(shards[t].shape[0]) for c in range(cuts[t])
    ]

    def spot(p, chunk):
        t, e, c = pieces[p]
        rows = shards[t].shape[1]
        part = rows // cuts[t]
        return fulls[t].at[e, pl.ds(pl.multiple_of(chunk * rows + c * part, 8), part), :]

    def copy_of(p, source, chunk, device, send_at):
        return pltpu.make_async_remote_copy(
            src_ref=source,
            dst_ref=spot(p, chunk),
            send_sem=send_at,
            recv_sem=recv_sem.at[p, chunk],
            device_id=device,
            device_id_type=MESH,
        )

    def source_of(p):
        t, e, c = pieces[p]
        part = shards[t].shape[1] // cuts[t]
        return shards[t].at[e, pl.ds(c * part, part), :]

    def inner_sends(p, source, chunk):
        return [
            copy_of(p, source, chunk, (outer * inner_count + peer, mine), send_sem.at[p, 0, j, chunk])
            for j, peer in enumerate(inner_peers)
        ]

    def up(p, source, chunk):
        return copy_of(p, source, chunk, (above * inner_count + inner, mine), send_sem.at[p, 1, 0, chunk])

    def down(p, source, chunk):
        return copy_of(p, source, chunk, (below * inner_count + inner, mine), send_sem.at[p, 2, 0, chunk])

    def arrived(p, chunk):
        pltpu.make_async_copy(spot(p, chunk), spot(p, chunk), recv_sem.at[p, chunk]).wait()

    can_up, can_down = outer < outer_count - 1, outer > 0
    every = range(len(pieces))
    own = []
    for p in every:
        for copy in inner_sends(p, source_of(p), me):
            copy.start()
        pl.when(can_up)(lambda p=p: up(p, source_of(p), me).start())
        pl.when(can_down)(lambda p=p: down(p, source_of(p), me).start())
        copy = pltpu.make_async_copy(source_of(p), spot(p, me), own_sem.at[p])
        copy.start()
        own.append(copy)

    def passing(p, chunk, upward):
        arrived(p, chunk)
        if upward:
            pl.when(can_up)(lambda: up(p, spot(p, chunk), chunk).start())
        else:
            pl.when(can_down)(lambda: down(p, spot(p, chunk), chunk).start())

    for p in every:
        if p in crossed:
            for peer in inner_peers:
                chunk = outer * inner_count + peer
                arrived(p, chunk)
                pl.when(can_up)(lambda p=p, chunk=chunk: up(p, spot(p, chunk), chunk).start())
                pl.when(can_down)(lambda p=p, chunk=chunk: down(p, spot(p, chunk), chunk).start())
    for step in range(1, outer_count):
        low, high = outer - step, outer + step
        for p in every:
            for upward, there, source in ((True, low >= 0, low), (False, high < outer_count, high)):

                def relay(p=p, upward=upward, source=source):
                    chunk = source * inner_count + inner
                    passing(p, chunk, upward)
                    if p in crossed:
                        for peer in inner_peers:
                            passing(p, source * inner_count + peer, upward)
                    else:
                        for copy in inner_sends(p, spot(p, chunk), chunk):
                            copy.start()

                pl.when(there)(relay)
    for t in range(trade_count):
        pltpu.make_async_copy(
            outgoing[t].at[mine], incoming[t].at[mine], trade_send.at[t, 0]
        ).wait()
        for k in range(1, owner_count):
            there = incoming[t].at[lax.rem(mine + k, owner_count)]
            pltpu.make_async_copy(
                there, there, trade_recv.at[t, lax.rem(mine + k, owner_count)]
            ).wait()
    for trade in trades:
        trade.wait_send()
    for p in every:
        own[p].wait()
        if p not in crossed:
            for peer in inner_peers:
                for plane in range(outer_count):
                    arrived(p, plane * inner_count + peer)
        for copy in inner_sends(p, source_of(p), me):
            copy.wait_send()
        if p not in crossed:
            for k in range(1, outer_count):
                chunk = lax.rem(outer + k, outer_count) * inner_count + inner
                for copy in inner_sends(p, spot(p, chunk), chunk):
                    copy.wait_send()
        columns = range(inner_count) if p in crossed else [inner]
        for plane in range(outer_count):
            for column in columns:
                chunk = plane * inner_count + column
                pl.when(can_up & (outer >= plane))(lambda p=p, chunk=chunk: up(p, spot(p, chunk), chunk).wait_send())
                pl.when(can_down & (outer <= plane))(lambda p=p, chunk=chunk: down(p, spot(p, chunk), chunk).wait_send())


def expert_gather(shards, dp_count, collective, cuts=None, crossed=(), owner_count=1, trades=()):
    outer_count, inner_count = dp_grid(dp_count)
    cuts = cuts or [1] * len(shards)
    piece_count = sum(shard.shape[0] * cut for shard, cut in zip(shards, cuts))
    anywhere = pl.BlockSpec(memory_space=pl.ANY)
    given = len(shards) + len(trades)
    return pl.pallas_call(
        functools.partial(
            expert_gather_kernel, dp_count, len(shards), cuts, crossed, owner_count, len(trades)
        ),
        out_shape=[
            jax.ShapeDtypeStruct((s.shape[0], dp_count * s.shape[1], s.shape[2]), s.dtype)
            for s in shards
        ]
        + [jax.ShapeDtypeStruct(t.shape, t.dtype) for t in trades],
        in_specs=[anywhere] * given,
        out_specs=[anywhere] * given,
        scratch_shapes=[
            pltpu.SemaphoreType.DMA((piece_count, 3, max(1, inner_count - 1), dp_count)),
            pltpu.SemaphoreType.DMA((piece_count, dp_count)),
            pltpu.SemaphoreType.DMA((piece_count,)),
            pltpu.SemaphoreType.DMA((max(1, len(trades)), owner_count)),
            pltpu.SemaphoreType.DMA((max(1, len(trades)), owner_count)),
        ],
        compiler_params=pltpu.CompilerParams(collective_id=collective, has_side_effects=True),
        name="expert_gather",
    )(*shards, *trades)


def add_into(target, source, target_at):
    rows = target.shape[-2]
    step = 16

    def body(i, carry):
        here = pl.ds(pl.multiple_of(i * step, step), step)
        target[target_at + (here, slice(None))] = (
            target[target_at + (here, slice(None))].astype(jnp.float32)
            + source(here).astype(jnp.float32)
        ).astype(target.dtype)
        return carry

    lax.fori_loop(0, rows // step, body, 0)


def final_reduce_kernel(small_count, part_ref, *refs):
    small_refs, refs = refs[:small_count], refs[small_count:]
    (
    part_out, small_out, swap, part_in, part_low, part_high, small_in, small_low, small_high, final_low, final_in,
    swap_send, swap_recv, in_send, in_recv, line_send, line_recv, last_send, last_recv,
    ) = refs
    outer_count, inner_count = 4, 2
    me, mine = place()
    outer, inner = me // inner_count, me % inner_count
    side = mine % 2
    mate, across = mine + 1 - 2 * side, lax.rem(mine + 2, 4)
    beside = me + 1 - 2 * inner
    half_rows = small_refs[0].shape[1] // 2
    starts = [sum(ref.shape[2] for ref in small_refs[:n]) for n in range(small_count + 1)]

    def remote(source, target, device, send_at, recv_at):
        return pltpu.make_async_remote_copy(
            src_ref=source,
            dst_ref=target,
            send_sem=send_at,
            recv_sem=recv_at,
            device_id=device,
            device_id_type=MESH,
        )

    barrier = pltpu.get_barrier_semaphore()
    low_peer = lax.rem(outer + outer_count - 1, outer_count) * inner_count + inner
    high_peer = lax.rem(outer + 1, outer_count) * inner_count + inner
    for device in ((me, mate), (me, across), (beside, mine), (low_peer, mine), (high_peer, mine)):
        pl.semaphore_signal(barrier, inc=1, device_id=device, device_id_type=MESH)
    pl.semaphore_wait(barrier, 5)

    mate_rows = pl.ds(pl.multiple_of((1 - side) * half_rows, 16), half_rows)
    own_rows = pl.ds(pl.multiple_of(side * half_rows, 16), half_rows)

    def swap_copy(n):
        return remote(
            small_refs[n].at[:, mate_rows, :],
            swap.at[:, :, starts[n] : starts[n + 1]],
            (me, mate),
            swap_send.at[n],
            swap_recv.at[n],
        )

    def inner_copy(p, plane):
        if p == 0:
            source = part_ref.at[plane * inner_count + 1 - inner]
            target = part_in.at[plane]
        else:
            source = swap.at[plane * inner_count + 1 - inner]
            target = small_in.at[plane]
        return remote(source, target, (beside, mine), in_send.at[p, plane], in_recv.at[p, plane])

    ins, lows, highs = (part_in, small_in), (part_low, small_low), (part_high, small_high)

    def line_copy(p, plane, upward, device_plane):
        target = (lows if upward else highs)[p].at[plane]
        way = 0 if upward else 1
        return remote(
            ins[p].at[plane],
            target,
            (device_plane * inner_count + inner, mine),
            line_send.at[p, way, plane],
            line_recv.at[p, way, plane],
        )

    def add_own(chunk):
        def body(i, carry):
            here = pl.ds(pl.multiple_of(i * 16, 16), 16)
            there = pl.ds(pl.multiple_of(side * half_rows + i * 16, 16), 16)
            for n in range(small_count):
                columns = slice(starts[n], starts[n + 1])
                swap[chunk, here, columns] = (
                    swap[chunk, here, columns].astype(jnp.float32)
                    + small_refs[n][chunk, there, :].astype(jnp.float32)
                ).astype(swap.dtype)
            return carry

        lax.fori_loop(0, half_rows // 16, body, 0)

    def at_plane(o):
        order = sorted(range(outer_count), key=lambda t: (-abs(t - o), t))
        for plane in order:
            inner_copy(0, plane).start()
        for n in range(small_count):
            swap_copy(n).start()
        for n in range(small_count):
            swap_copy(n).wait_recv()
        for plane in order:
            for column in range(inner_count):
                add_own(plane * inner_count + column)
            inner_copy(1, plane).start()
        for plane in order:
            for p in (0, 1):
                inner_copy(p, plane).wait_recv()
                if p == 0:
                    add_into(ins[p], lambda here, plane=plane: part_ref[plane * inner_count + inner, here, :], (plane,))
                else:
                    add_into(ins[p], lambda here, plane=plane: swap[plane * inner_count + inner, here, :], (plane,))
                if plane > o:
                    if o > 0:
                        line_copy(p, plane, True, o + 1).wait_recv()
                        add_into(ins[p], lambda here, p=p, plane=plane: lows[p][plane, here, :], (plane,))
                    line_copy(p, plane, True, o + 1).start()
                if plane < o:
                    if o < outer_count - 1:
                        line_copy(p, plane, False, o - 1).wait_recv()
                        add_into(ins[p], lambda here, p=p, plane=plane: highs[p][plane, here, :], (plane,))
                    line_copy(p, plane, False, o - 1).start()
                if plane == o:
                    if o > 0:
                        line_copy(p, plane, True, o).wait_recv()
                    if o < outer_count - 1:
                        line_copy(p, plane, False, o).wait_recv()
                    target = part_out if p == 0 else final_low
                    rows = target.shape[0]

                    def body(i, carry, p=p, target=target):
                        here = pl.ds(pl.multiple_of(i * 16, 16), 16)
                        total = ins[p][o, here, :].astype(jnp.float32)
                        if o > 0:
                            total = total + lows[p][o, here, :].astype(jnp.float32)
                        if o < outer_count - 1:
                            total = total + highs[p][o, here, :].astype(jnp.float32)
                        target[here, :] = total.astype(target.dtype)
                        return carry

                    lax.fori_loop(0, rows // 16, body, 0)
        for plane in range(outer_count):
            for p in (0, 1):
                inner_copy(p, plane).wait_send()
                if plane > o:
                    line_copy(p, plane, True, o + 1).wait_send()
                if plane < o:
                    line_copy(p, plane, False, o - 1).wait_send()
        for n in range(small_count):
            swap_copy(n).wait_send()

    for o in range(outer_count):
        pl.when(outer == o)(functools.partial(at_plane, o))
    across_copy = remote(final_low, final_in, (me, across), last_send.at[0], last_recv.at[0])
    across_copy.start()
    across_copy.wait()

    def total_body(i, carry):
        here = pl.ds(pl.multiple_of(i * 16, 16), 16)
        there = pl.ds(pl.multiple_of(side * half_rows + i * 16, 16), 16)
        small_out[there, :] = final_low[here, :].astype(jnp.float32) + final_in[here, :].astype(jnp.float32)
        return carry

    lax.fori_loop(0, half_rows // 16, total_body, 0)
    mate_copy = remote(
        small_out.at[own_rows, :], small_out.at[own_rows, :], (me, mate), last_send.at[1], last_recv.at[1]
    )
    mate_copy.start()
    mate_copy.wait()


def final_reduce(part, smalls, collective):
    chunk_count, part_rows, part_columns = part.shape
    small_rows = smalls[0].shape[1]
    small_columns = sum(small.shape[2] for small in smalls)
    low = jnp.bfloat16
    in_vmem = pl.BlockSpec(memory_space=pltpu.VMEM)
    half = small_rows // 2
    return pl.pallas_call(
        functools.partial(final_reduce_kernel, len(smalls)),
        out_shape=[
            jax.ShapeDtypeStruct((part_rows, part_columns), jnp.float32),
            jax.ShapeDtypeStruct((small_rows, small_columns), jnp.float32),
        ],
        in_specs=[in_vmem] * (1 + len(smalls)),
        out_specs=[in_vmem] * 2,
        scratch_shapes=[pltpu.VMEM((chunk_count, half, small_columns), low)]
        + [pltpu.VMEM((4, part_rows, part_columns), low)] * 3
        + [pltpu.VMEM((4, half, small_columns), low)] * 3
        + [pltpu.VMEM((half, small_columns), low)] * 2
        + [
            pltpu.SemaphoreType.DMA((len(smalls),)),
            pltpu.SemaphoreType.DMA((len(smalls),)),
            pltpu.SemaphoreType.DMA((2, 4)),
            pltpu.SemaphoreType.DMA((2, 4)),
            pltpu.SemaphoreType.DMA((2, 2, 4)),
            pltpu.SemaphoreType.DMA((2, 2, 4)),
            pltpu.SemaphoreType.DMA((2,)),
            pltpu.SemaphoreType.DMA((2,)),
        ],
        compiler_params=pltpu.CompilerParams(
            collective_id=collective, has_side_effects=True, vmem_limit_bytes=58 * 2**20
        ),
        name="final_reduce",
    )(part, *smalls)


def shards(
    tokens,
    resid_logits,
    routes,
    doc_ids,
    w_qkv,
    w_out,
    gain_attn,
    gain_ffn,
    w_router,
    w_const,
    v_const,
    w_gate_up,
    w_down,
    out_grad,
):
    dp_count, owner_count = lax.axis_size("dp"), lax.axis_size("expert")
    own_links = dp_count == 8 and owner_count == 4
    seq_count, length, width = tokens.shape
    assert seq_count == 1
    rows = seq_count * length
    choice_count = resid_logits.shape[-1]
    local_count = w_gate_up.shape[0]
    expert_count = owner_count * local_count
    hidden_count = w_down.shape[1] * dp_count
    width_qkv, width_out = w_qkv.shape[1], w_out.shape[1]
    small_parts = [w_router, w_const, v_const, gain_attn[:, None], gain_ffn[:, None]]
    small_width = sum(part.shape[1] for part in small_parts)
    pad = jnp.zeros((w_qkv.shape[0], 256 - small_width), jnp.bfloat16)
    packed = jnp.concatenate([w_qkv, w_out] + small_parts + [pad], 1)
    inputs = tokens.reshape(rows, width)
    cot = out_grad.reshape(rows, width)
    route_rows = routes.reshape(rows, 2)
    spots, spot_rows = routing(route_rows, expert_count)
    cosine, sine = rotary_lanes(length, width // HEADS)
    docs_row, docs_column = doc_ids.reshape(1, rows), doc_ids.reshape(rows, 1)
    resid = jnp.pad(
        resid_logits.reshape(rows, choice_count).astype(jnp.float32), ((0, 0), (0, 128 - choice_count))
    )
    if own_links:
        packed_full = small_gather(packed, dp_count, 1)
    else:
        packed_full = lax.all_gather(packed, "dp", axis=0, tiled=True)
    gate_up_full = lax.all_gather(w_gate_up, "dp", axis=1, tiled=True)
    normed_one, queries, keys, values, attended, middle, normed_two, aux = attention_forward(
        inputs, packed_full, docs_row, docs_column, cosine, sine, route_rows, resid
    )
    send_rows, send_grads = dispatch(spot_rows, aux, normed_two, cot, expert_count * CAP)
    send_rows = send_rows.reshape(owner_count, local_count * CAP, width)
    send_grads = send_grads.reshape(owner_count, local_count * CAP, width)
    exchange = functools.partial(
        lax.all_to_all, axis_name="expert", split_axis=0, concat_axis=0, tiled=True
    )
    if own_links:
        down_full, arrived, arrived_grad = expert_gather(
            [w_down], dp_count, 2, owner_count=owner_count, trades=[send_rows, send_grads]
        )
    else:
        down_full = lax.all_gather(w_down, "dp", axis=1, tiled=True)
        arrived, arrived_grad = exchange(send_rows), exchange(send_grads)
    arrived = arrived.reshape(owner_count, local_count, CAP, width)
    arrived_grad = arrived_grad.reshape(owner_count, local_count, CAP, width)

    gate_up = jnp.einsum(
        "secd,edf->secf", arrived, gate_up_full, preferred_element_type=jnp.float32
    )
    gate_part = gate_up[..., :hidden_count]
    up_part = gate_up[..., hidden_count:]
    squashed = lax.logistic(gate_part)
    silu_gate = gate_part * squashed
    activated = (silu_gate * up_part).astype(jnp.bfloat16)
    grad_down = jnp.einsum(
        "secf,secd->efd", activated, arrived_grad, preferred_element_type=jnp.float32
    ).astype(jnp.bfloat16)
    activated, arrived_grad, grad_down = lax.optimization_barrier(
        (activated, arrived_grad, grad_down)
    )
    grad_expert_down = lax.psum_scatter(
        grad_down, "dp", scatter_dimension=1, tiled=True
    ).astype(jnp.float32)
    expert_out = jnp.einsum(
        "secf,efd->secd", activated, down_full, preferred_element_type=jnp.float32
    ).astype(jnp.bfloat16)
    returned = exchange(expert_out.reshape(owner_count, local_count * CAP, width))
    grad_act = jnp.einsum(
        "secd,efd->secf", arrived_grad, down_full, preferred_element_type=jnp.float32
    )
    grad_gate = grad_act * up_part * squashed * (1.0 + gate_part * (1.0 - squashed))
    grad_up = grad_act * silu_gate
    grad_gate_up = jnp.concatenate([grad_gate, grad_up], -1).astype(jnp.bfloat16)
    grad_rows = jnp.einsum(
        "secf,edf->secd", grad_gate_up, gate_up_full, preferred_element_type=jnp.float32
    ).astype(jnp.bfloat16)
    back = exchange(grad_rows.reshape(owner_count, local_count * CAP, width))
    gu_grads = [
        jnp.einsum(
            "scd,scf->df", arrived[:, e], grad_gate_up[:, e], preferred_element_type=jnp.float32
        ).astype(jnp.bfloat16)
        for e in range(local_count)
    ]
    returned, gu_grads = lax.optimization_barrier((returned, gu_grads))
    linked = local_count - 1 if own_links else local_count
    gu_parts = [
        lax.psum_scatter(gu_grads[e], "dp", scatter_dimension=0, tiled=True).astype(jnp.float32)
        for e in range(linked)
    ]

    output, logit_grad, grad_part, small_grad = combine(
        returned.reshape(expert_count * CAP, width), spots, route_rows, aux, normed_two, middle,
        cot, packed_full, choice_count, expert_count,
    )
    grad_middle, small_grad = combine_back(
        back.reshape(expert_count * CAP, width), spots, aux, middle, cot, grad_part, packed_full,
        small_grad,
    )
    token_grad, *weight_grads = attention_backward(
        grad_middle, queries, keys, values, attended, normed_one, inputs, packed_full, docs_row,
        docs_column, cosine, sine, small_grad,
    )
    if own_links:
        part_width = width // dp_count
        gu_part, packed_part = final_reduce(
            gu_grads[linked].reshape(dp_count, part_width, 2 * hidden_count),
            [grad.reshape(dp_count, part_width, grad.shape[1]) for grad in weight_grads],
            3,
        )
        gu_parts = gu_parts + [gu_part]
    else:
        packed_part = lax.psum_scatter(
            jnp.concatenate(weight_grads, 1), "dp", scatter_dimension=0, tiled=True
        )
        packed_part = lax.psum(packed_part, "expert").astype(jnp.float32)
    part_qkv = packed_part[:, :width_qkv]
    part_out = packed_part[:, width_qkv : width_qkv + width_out]
    small_part = packed_part[:, width_qkv + width_out :]
    return (
        output.reshape(tokens.shape),
        token_grad.reshape(tokens.shape),
        logit_grad.reshape(resid_logits.shape),
        part_qkv,
        part_out,
        small_part[:, 18],
        small_part[:, 19],
        small_part[:, 0:12],
        small_part[:, 12:16],
        small_part[:, 16:18],
        jnp.stack(gu_parts),
        grad_expert_down,
    )


def solution(mesh):
    placed = (
        P(("dp", "expert"), None, None),
        P(("dp", "expert"), None, None),
        P(("dp", "expert"), None, None),
        P(("dp", "expert"), None),
        P("dp", None),
        P("dp", None),
        P("dp"),
        P("dp"),
        P("dp", None),
        P("dp", None),
        P("dp", None),
        P("expert", "dp", None),
        P("expert", "dp", None),
        P(("dp", "expert"), None, None),
    )
    return jax.shard_map(
        shards,
        mesh=mesh,
        in_specs=placed,
        out_specs=(
            P(("dp", "expert"), None, None),
            P(("dp", "expert"), None, None),
            P(("dp", "expert"), None, None),
            P("dp", None),
            P("dp", None),
            P("dp"),
            P("dp"),
            P("dp", None),
            P("dp", None),
            P("dp", None),
            P("expert", "dp", None),
            P("expert", "dp", None),
        ),
        check_vma=False,
    )
```

```python
import functools

import jax
import jax.numpy as jnp
import numpy as np
from jax import lax
from jax.experimental import pallas as pl
from jax.experimental.pallas import tpu as pltpu
from jax.sharding import PartitionSpec as P

HEADS = 12
BLOCK = 256
CAP = 256
GROUP = 256
FF_BLOCK = 512
MESH = pl.DeviceIdType.MESH
epsilon = 1e-06


def rotary_lanes(length, head_dim):
    half_dim = head_dim // 2
    frequency = (10000.0 ** (-np.arange(half_dim, dtype=np.float32) / half_dim)).astype(np.float32)
    angles = (np.arange(length, dtype=np.float32)[:, None] * frequency[None, :]).astype(np.float64)
    cosine = np.cos(angles).astype(np.float32)
    sine = np.sin(angles).astype(np.float32)
    return (
        np.concatenate([cosine] * 4, 1),
        np.concatenate([-sine, sine, -sine, sine], 1),
    )


def nt(left, right):
    return lax.dot_general(left, right, (((1,), (1,)), ((), ())), preferred_element_type=jnp.float32)


def tn(left, right):
    return lax.dot_general(left, right, (((0,), (0,)), ((), ())), preferred_element_type=jnp.float32)


def nn(left, right):
    return jnp.dot(left, right, preferred_element_type=jnp.float32)


def lane_ids(shape):
    return lax.broadcasted_iota(jnp.int32, shape, len(shape) - 1)


def turn(values, cosine, sine):
    lanes = lane_ids(values.shape)
    ahead, behind = pltpu.roll(values, 96, 1), pltpu.roll(values, 32, 1)
    return values * cosine + jnp.where(lanes % 64 < 32, ahead, behind) * sine


def key_span(i):
    return max(0, i - 2) * BLOCK, (i + 1) * BLOCK


def mask_of(docs_column, docs_row, i):
    low, high = key_span(i)
    return docs_column[low:high, :] == docs_row[:, i * BLOCK : (i + 1) * BLOCK]


def attention_forward_kernel(
    tokens_ref, wq_ref, wk_ref, wv_ref, wo_ref, small_ref, docs_row_ref, docs_column_ref,
    cosine_ref, sine_ref, routes_ref, resid_ref,
    normed_ref, q_ref, k_ref, v_ref, attended_ref, middle_ref, normed_two_ref, aux_ref,
    branch_ref,
):
    step = pl.program_id(0)
    rows = tokens_ref.shape[0]

    @pl.when(step == 0)
    def _():
        inputs = tokens_ref[...].astype(jnp.float32)
        gains = jnp.transpose(small_ref[:, :128].astype(jnp.float32))[18:19, :]
        scale = lax.rsqrt(jnp.mean(inputs * inputs, -1, keepdims=True) + epsilon)
        normed_ref[...] = (inputs * scale * gains).astype(jnp.bfloat16)
        branch_ref[...] = jnp.zeros_like(branch_ref)

    normed = normed_ref[...]
    cosine, sine = cosine_ref[...], sine_ref[...]
    for w_ref, out_ref, turned in ((wq_ref, q_ref, True), (wk_ref, k_ref, True), (wv_ref, v_ref, False)):
        projected = nn(normed, w_ref[...])
        for half in range(2):
            part = projected[:, half * 128 : half * 128 + 128]
            if turned:
                part = turn(part, cosine, sine)
            out_ref[:, half * 128 : half * 128 + 128] = part.astype(jnp.bfloat16)

    docs_row, docs_column = docs_row_ref[...], docs_column_ref[...]
    for i in range(rows // BLOCK):
        low, high = key_span(i)
        here = slice(i * BLOCK, (i + 1) * BLOCK)
        allowed = mask_of(docs_column, docs_row, i)
        for pair in range(2):
            lanes = slice(pair * 128, pair * 128 + 128)
            queries = q_ref[here, lanes] * jnp.asarray(0.125, jnp.bfloat16)
            keys, values = k_ref[low:high, lanes], v_ref[low:high, lanes]
            left = lane_ids(queries.shape) < 64
            outs = []
            for head in range(2):
                own = left if head == 0 else jnp.logical_not(left)
                scores = nt(keys, jnp.where(own, queries, jnp.zeros_like(queries)))
                scores = jnp.where(allowed, scores, -1e30)
                shifted = jnp.exp(scores - jnp.max(scores, 0, keepdims=True))
                probs = shifted * (1.0 / jnp.sum(shifted, 0, keepdims=True))
                outs.append(tn(probs.astype(jnp.bfloat16), values))
            attended_ref[here, lanes] = jnp.where(left, outs[0], outs[1]).astype(jnp.bfloat16)
    branch_ref[...] += nn(attended_ref[...], wo_ref[...])

    @pl.when(step == pl.num_programs(0) - 1)
    def _():
        small = small_ref[:, :128]
        gains = jnp.transpose(small.astype(jnp.float32))[19:20, :]
        middle = tokens_ref[...].astype(jnp.float32) + branch_ref[...]
        middle_ref[...] = middle
        scale = lax.rsqrt(jnp.mean(middle * middle, -1, keepdims=True) + epsilon)
        normed_two = (middle * scale * gains).astype(jnp.bfloat16)
        normed_two_ref[...] = normed_two
        logits = nn(normed_two, small) + resid_ref[...].astype(jnp.float32)
        lanes = lane_ids(logits.shape)

        def lane(at):
            return jnp.sum(jnp.where(lanes == at, logits, 0.0), -1, keepdims=True)

        def two(first, second):
            peak = jnp.maximum(first, second)
            first, second = jnp.exp(first - peak), jnp.exp(second - peak)
            return first / (first + second), second / (first + second)

        columns = list(two(lane(routes_ref[:, 0:1]), lane(routes_ref[:, 1:2])))
        columns += list(two(lane(12), lane(13))) + list(two(lane(14), lane(15)))
        columns.append(scale)
        aux = jnp.zeros_like(logits)
        for at, column in enumerate(columns):
            aux = jnp.where(lanes == at, column, aux)
        aux_ref[...] = aux


def attention_forward(tokens, packed, docs_row, docs_column, cosine, sine, routes, resid):
    rows, width = tokens.shape
    groups = width // GROUP
    low = jnp.bfloat16
    whole = lambda shape: pl.BlockSpec(shape, lambda j: (0, 0))
    column = lambda at: pl.BlockSpec((width, GROUP), lambda j: (0, at + j))
    out_column = pl.BlockSpec((rows, GROUP), lambda j: (0, j))
    full = jax.ShapeDtypeStruct((rows, width), low)
    return pl.pallas_call(
        attention_forward_kernel,
        grid=(groups,),
        out_shape=[full] * 5
        + [
            jax.ShapeDtypeStruct((rows, width), jnp.float32),
            full,
            jax.ShapeDtypeStruct((rows, 128), jnp.float32),
        ],
        in_specs=[
            whole((rows, width)),
            column(0),
            column(groups),
            column(2 * groups),
            pl.BlockSpec((GROUP, width), lambda j: (j, 3)),
            pl.BlockSpec((width, 256), lambda j: (0, 12)),
            whole((1, rows)),
            whole((rows, 1)),
            whole((rows, 128)),
            whole((rows, 128)),
            whole((rows, 2)),
            whole((rows, 128)),
        ],
        out_specs=[whole((rows, width))]
        + [out_column] * 4
        + [whole((rows, width)), whole((rows, width)), whole((rows, 128))],
        scratch_shapes=[pltpu.VMEM((rows, width), jnp.float32)],
        compiler_params=pltpu.CompilerParams(
            dimension_semantics=("arbitrary",), vmem_limit_bytes=56 * 2**20
        ),
        cost_estimate=pl.CostEstimate(
            flops=2 * rows * width * 4 * width + 8 * rows * rows * width // 2,
            bytes_accessed=24 * rows * width,
            transcendentals=rows * rows * HEADS // 2,
        ),
        name="attention_forward",
    )(tokens, packed, packed, packed, packed, packed, docs_row, docs_column, cosine, sine, routes, resid)


def attention_backward_kernel(
    grad_middle_ref, q_ref, k_ref, v_ref, attended_ref, normed_ref, tokens_ref,
    wq_ref, wk_ref, wv_ref, wo_ref, small_ref, docs_row_ref, docs_column_ref,
    cosine_ref, sine_ref, small_grad_ref,
    token_grad_ref, gq_ref, gk_ref, gv_ref, go_ref, small_out_ref,
    branch_ref, back_ref, turned_ref, key_acc, value_acc, query_acc,
):
    step = pl.program_id(0)
    rows, width = tokens_ref.shape

    @pl.when(step == 0)
    def _():
        branch_ref[...] = grad_middle_ref[...].astype(jnp.bfloat16)
        back_ref[...] = jnp.zeros_like(back_ref)

    grad_branch = branch_ref[...]
    grad_attended = nt(grad_branch, wo_ref[...]).astype(jnp.bfloat16)
    go_ref[...] = tn(attended_ref[...], grad_branch).astype(jnp.bfloat16)
    cosine, sine = cosine_ref[...], sine_ref[...]
    docs_row, docs_column = docs_row_ref[...], docs_column_ref[...]
    for pair in range(2):
        lanes = slice(pair * 128, pair * 128 + 128)
        key_acc[...] = jnp.zeros_like(key_acc)
        value_acc[...] = jnp.zeros_like(value_acc)
        for i in range(rows // BLOCK):
            low, high = key_span(i)
            here = slice(i * BLOCK, (i + 1) * BLOCK)
            allowed = mask_of(docs_column, docs_row, i)
            queries = q_ref[here, lanes] * jnp.asarray(0.125, jnp.bfloat16)
            grads = grad_attended[here, lanes]
            keys, values = k_ref[low:high, lanes], v_ref[low:high, lanes]
            left = lane_ids(queries.shape) < 64
            query_grads = []
            key_grad, value_grad = None, None
            for head in range(2):
                own = left if head == 0 else jnp.logical_not(left)
                own_queries = jnp.where(own, queries, jnp.zeros_like(queries))
                own_grads = jnp.where(own, grads, jnp.zeros_like(grads))
                scores = jnp.where(allowed, nt(keys, own_queries), -1e30)
                shifted = jnp.exp(scores - jnp.max(scores, 0, keepdims=True))
                probs = shifted * (1.0 / jnp.sum(shifted, 0, keepdims=True))
                grad_probs = nt(values, own_grads)
                inner = jnp.sum(probs * grad_probs, 0, keepdims=True)
                grad_scores = (probs * (grad_probs - inner)).astype(jnp.bfloat16)
                part_value = nn(probs.astype(jnp.bfloat16), own_grads)
                part_key = nn(grad_scores, own_queries)
                value_grad = part_value if head == 0 else value_grad + part_value
                key_grad = part_key if head == 0 else key_grad + part_key
                query_grads.append(tn(grad_scores, keys))
            value_acc[low:high, :] += value_grad
            key_acc[low:high, :] += key_grad
            query_acc[here, :] = jnp.where(left, query_grads[0], query_grads[1]) * 0.125
        turned_ref[0, :, lanes] = turn(query_acc[...], cosine, -sine).astype(jnp.bfloat16)
        turned_ref[1, :, lanes] = turn(key_acc[...], cosine, -sine).astype(jnp.bfloat16)
        turned_ref[2, :, lanes] = value_acc[...].astype(jnp.bfloat16)
    normed = normed_ref[...]
    for at, (w_ref, out_ref) in enumerate(((wq_ref, gq_ref), (wk_ref, gk_ref), (wv_ref, gv_ref))):
        turned = turned_ref[at]
        out_ref[...] = tn(normed, turned).astype(jnp.bfloat16)
        back_ref[...] += nt(turned, w_ref[...])

    @pl.when(step == pl.num_programs(0) - 1)
    def _():
        gains = jnp.transpose(small_ref[:, :128].astype(jnp.float32))[18:19, :]
        inputs = tokens_ref[...].astype(jnp.float32)
        grads = back_ref[...]
        scale = lax.rsqrt(jnp.mean(inputs * inputs, -1, keepdims=True) + epsilon)
        weighted = grads * gains
        mean = jnp.mean(weighted * inputs, -1, keepdims=True)
        grad_inputs = scale * weighted - inputs * (scale * scale * scale * mean)
        token_grad_ref[...] = (grad_inputs + grad_middle_ref[...]).astype(jnp.bfloat16)
        gain_grad = jnp.sum(grads * inputs * scale, 0, keepdims=True)
        column = jnp.transpose(jnp.broadcast_to(gain_grad, (128, width)))
        small_grad = small_grad_ref[...]
        small_grad = jnp.where(lane_ids(small_grad.shape) == 18, column, small_grad)
        small_out_ref[:, :128] = small_grad.astype(jnp.bfloat16)
        small_out_ref[:, 128:] = jnp.zeros((width, 128), jnp.bfloat16)


def attention_backward(
    grad_middle, queries, keys, values, attended, normed, tokens, packed, docs_row, docs_column,
    cosine, sine, small_grad,
):
    rows, width = tokens.shape
    groups = width // GROUP
    low = jnp.bfloat16
    whole = lambda shape: pl.BlockSpec(shape, lambda j: (0, 0))
    column = lambda at: pl.BlockSpec((width, GROUP), lambda j: (0, at + j))
    by_group = pl.BlockSpec((rows, GROUP), lambda j: (0, j))
    weight = jax.ShapeDtypeStruct((width, width), low)
    return pl.pallas_call(
        attention_backward_kernel,
        grid=(groups,),
        out_shape=[jax.ShapeDtypeStruct((rows, width), low)]
        + [weight] * 4
        + [jax.ShapeDtypeStruct((width, 256), low)],
        in_specs=[
            whole((rows, width)),
            by_group,
            by_group,
            by_group,
            by_group,
            whole((rows, width)),
            whole((rows, width)),
            column(0),
            column(groups),
            column(2 * groups),
            pl.BlockSpec((GROUP, width), lambda j: (j, 3)),
            pl.BlockSpec((width, 256), lambda j: (0, 12)),
            whole((1, rows)),
            whole((rows, 1)),
            whole((rows, 128)),
            whole((rows, 128)),
            whole((width, 128)),
        ],
        out_specs=[
            whole((rows, width)),
            column(0),
            column(0),
            column(0),
            pl.BlockSpec((GROUP, width), lambda j: (j, 0)),
            whole((width, 256)),
        ],
        scratch_shapes=[
            pltpu.VMEM((rows, width), low),
            pltpu.VMEM((rows, width), jnp.float32),
            pltpu.VMEM((3, rows, GROUP), low),
            pltpu.VMEM((rows, 128), jnp.float32),
            pltpu.VMEM((rows, 128), jnp.float32),
            pltpu.VMEM((rows, 128), jnp.float32),
        ],
        compiler_params=pltpu.CompilerParams(
            dimension_semantics=("arbitrary",), vmem_limit_bytes=56 * 2**20
        ),
        cost_estimate=pl.CostEstimate(
            flops=4 * rows * width * 4 * width + 20 * rows * rows * width // 2,
            bytes_accessed=32 * rows * width,
            transcendentals=rows * rows * HEADS // 2,
        ),
        name="attention_backward",
    )(
        grad_middle, queries, keys, values, attended, normed, tokens, packed, packed, packed,
        packed, packed, docs_row, docs_column, cosine, sine, small_grad,
    )


def routing_kernel(expert_count, routes_ref, columns_ref, rows_ref):
    rows = routes_ref.shape[0]
    lanes = lane_ids((rows, 128))
    first = (lanes == routes_ref[:, 0:1]).astype(jnp.float32)
    second = (lanes == routes_ref[:, 1:2]).astype(jnp.float32)
    down = lax.broadcasted_iota(jnp.int32, (rows, rows), 0)
    lower = (down > lane_ids((rows, rows))).astype(jnp.bfloat16)
    before_first = nn(lower, first.astype(jnp.bfloat16))
    before_second = nn(lower, second.astype(jnp.bfloat16)) + jnp.sum(first, 0, keepdims=True)
    spots = []
    for picked, before, at in ((first, before_first, 0), (second, before_second, 1)):
        rank = jnp.sum(picked * before, -1, keepdims=True)
        route = routes_ref[:, at : at + 1]
        spot = route.astype(jnp.float32) * CAP + rank
        spots.append(jnp.where(route < expert_count, spot, jnp.full_like(spot, 2.0 * expert_count * CAP)))
    both = jnp.where(lanes == 0, spots[0], jnp.where(lanes == 1, spots[1], 0.0))
    columns_ref[...] = both.astype(jnp.int32)
    rows_ref[...] = jnp.transpose(both)[0:8, :].astype(jnp.int32)


def routing(routes, expert_count):
    rows = routes.shape[0]
    return pl.pallas_call(
        functools.partial(routing_kernel, expert_count),
        out_shape=[
            jax.ShapeDtypeStruct((rows, 128), jnp.int32),
            jax.ShapeDtypeStruct((8, rows), jnp.int32),
        ],
        compiler_params=pltpu.CompilerParams(vmem_limit_bytes=40 * 2**20),
        name="routing",
    )(routes)


def dispatch_kernel(spots_ref, aux_ref, normed_ref, cot_ref, rows_ref, grads_ref, gates_ref):
    step = pl.program_id(0)

    @pl.when(step == 0)
    def _():
        gates_ref[...] = jnp.transpose(aux_ref[...])[0:8, :]

    shape = (rows_ref.shape[0], normed_ref.shape[0])
    slots = step * rows_ref.shape[0] + lax.broadcasted_iota(jnp.int32, shape, 0)
    first, second = slots == spots_ref[0:1, :], slots == spots_ref[1:2, :]
    gates = jnp.sum(
        jnp.where(first, gates_ref[0:1, :], jnp.where(second, gates_ref[1:2, :], 0.0)), -1, keepdims=True
    )
    chosen = jnp.where(first | second, 1.0, 0.0).astype(jnp.bfloat16)
    rows_ref[...] = nn(chosen, normed_ref[...]).astype(jnp.bfloat16)
    grads_ref[...] = (nn(chosen, cot_ref[...]) * gates).astype(jnp.bfloat16)


def dispatch(spots, aux, normed, cot, slot_count):
    rows, width = normed.shape
    whole = lambda shape: pl.BlockSpec(shape, lambda j: (0, 0))
    block = pl.BlockSpec((CAP, width), lambda j: (j, 0))
    return pl.pallas_call(
        dispatch_kernel,
        grid=(slot_count // CAP,),
        out_shape=[jax.ShapeDtypeStruct((slot_count, width), jnp.bfloat16)] * 2,
        in_specs=[whole((8, rows)), whole((rows, 128)), whole((rows, width)), whole((rows, width))],
        out_specs=[block, block],
        scratch_shapes=[pltpu.VMEM((8, rows), jnp.float32)],
        compiler_params=pltpu.CompilerParams(
            dimension_semantics=("arbitrary",), vmem_limit_bytes=60 * 2**20
        ),
        cost_estimate=pl.CostEstimate(
            flops=4 * slot_count * rows * width,
            bytes_accessed=4 * (rows + slot_count) * width,
            transcendentals=0,
        ),
        name="dispatch",
    )(spots, aux, normed, cot)


def halves(values):
    high = values.astype(jnp.bfloat16)
    return high, (values - high.astype(jnp.float32)).astype(jnp.bfloat16)


def combine_kernel(
    expert_count, local_count, *refs
):
    parts, refs = refs[:local_count], refs[local_count:]
    (
        spots_ref, routes_ref, aux_ref, normed_ref, middle_ref, cot_ref, small_ref,
        output_ref, logit_ref, grad_middle_ref, small_out_ref, vectors_ref, small_grad_ref,
    ) = refs
    step = pl.program_id(0)

    @pl.when(step == 0)
    def _():
        vectors_ref[0:8, :] = jnp.transpose(small_ref[:, :128].astype(jnp.float32))[16:24, :]
        vectors_ref[8:16, :] = jnp.zeros((8, vectors_ref.shape[1]), jnp.float32)
        small_grad_ref[...] = jnp.zeros_like(small_grad_ref)

    rows, width = normed_ref.shape
    normed_low, cot_low = normed_ref[...], cot_ref[...]
    normed, cot = normed_low.astype(jnp.float32), cot_low.astype(jnp.float32)
    total = lambda values: jnp.sum(values, -1, keepdims=True)
    picks, back = [0.0, 0.0], 0.0
    for e in range(local_count):
        count = parts[e].shape[0] * CAP
        slots = lane_ids((rows, count))
        slots = slots // CAP * (local_count * CAP) + e * CAP + slots % CAP
        hits = [slots == spots_ref[:, s : s + 1] for s in range(2)]
        chosen = [jnp.where(hit, 1.0, 0.0).astype(jnp.bfloat16) for hit in hits]
        returned = parts[e][:, 0].reshape(count, width)
        for s in range(2):
            picks[s] = picks[s] + nn(chosen[s], returned)
        back = back + nn(chosen[0] + chosen[1], parts[e][:, 1].reshape(count, width))
    inner = [total(pick * cot) for pick in picks]
    gates = [aux_ref[:, s : s + 1] for s in range(2)]
    routes = [routes_ref[:, s : s + 1] for s in range(2)]
    dot_copy = total(cot * normed)

    def weight_of(route):
        return sum(jnp.where(routes[s] == route, gates[s], 0.0) for s in range(2))

    copy_weight = weight_of(expert_count + 1)
    mix = gates[0] * picks[0] + gates[1] * picks[1]
    pass_weight = copy_weight
    gate_grads = [
        inner[s] + jnp.where(routes[s] == expert_count + 1, dot_copy, 0.0) for s in range(2)
    ]
    lanes = lane_ids((rows, 128))
    spread = jnp.zeros((rows, 128), jnp.float32)
    for k in range(2):
        vector = vectors_ref[k : k + 1, :]
        keep, blend = aux_ref[:, 2 + 2 * k : 3 + 2 * k], aux_ref[:, 3 + 2 * k : 4 + 2 * k]
        weight = weight_of(expert_count + 2 + k)
        dot_vector = total(cot * vector)
        pass_weight = pass_weight + weight * keep
        mix = mix + (weight * blend) * vector
        value = keep * dot_copy + blend * dot_vector
        for s in range(2):
            gate_grads[s] = gate_grads[s] + jnp.where(routes[s] == expert_count + 2 + k, value, 0.0)
        term = keep * blend * (weight * dot_copy - weight * dot_vector)
        spread = jnp.where(lanes == 12 + 2 * k, term, spread)
        spread = jnp.where(lanes == 13 + 2 * k, -term, spread)
        spread = jnp.where(lanes == 16 + k, weight * blend, spread)
    mix = mix + pass_weight * normed
    middle, scale = middle_ref[...], aux_ref[:, 6:7]
    output_ref[...] = (middle + mix).astype(jnp.bfloat16)
    mean = gates[0] * gate_grads[0] + gates[1] * gate_grads[1]
    for s in range(2):
        spread = jnp.where(lanes == routes[s], gates[s] * (gate_grads[s] - mean), spread)
    logit_ref[...] = spread[:, : logit_ref.shape[1]].astype(jnp.bfloat16)
    logits = jnp.where(lanes < 16, spread, 0.0)
    high, low = halves(logits)
    small = small_ref[:, :128]
    vector_high, vector_low = halves(spread - logits)
    small_grad_ref[...] += (
        tn(normed_low, high) + tn(normed_low, low) + tn(cot_low, vector_high) + tn(cot_low, vector_low)
    )
    grads = back + pass_weight * cot + nt(high, small) + nt(low, small)
    vectors_ref[8:9, :] += jnp.sum(grads * middle * scale, 0, keepdims=True)
    weighted = grads * vectors_ref[3:4, :]
    mean = jnp.mean(weighted * middle, -1, keepdims=True)
    grad_middle_ref[...] = cot + scale * weighted - middle * (scale * scale * scale * mean)

    @pl.when(step == pl.num_programs(0) - 1)
    def _():
        column = jnp.transpose(jnp.broadcast_to(vectors_ref[8:9, :], (128, width)))
        small_grad = small_grad_ref[...]
        small_out_ref[...] = jnp.where(lane_ids(small_grad.shape) == 19, column, small_grad)


def combine(parts, spots, routes, aux, normed, middle, cot, packed, choice_count, expert_count):
    rows, width = normed.shape
    local_count = len(parts)
    slot_count = expert_count * CAP
    size = 256
    block = lambda columns: pl.BlockSpec((size, columns), lambda j: (j, 0))
    whole = lambda shape: pl.BlockSpec(shape, lambda j: (0,) * len(shape))
    return pl.pallas_call(
        functools.partial(combine_kernel, expert_count, local_count),
        grid=(rows // size,),
        out_shape=[
            jax.ShapeDtypeStruct((rows, width), jnp.bfloat16),
            jax.ShapeDtypeStruct((rows, choice_count), jnp.bfloat16),
            jax.ShapeDtypeStruct((rows, width), jnp.float32),
            jax.ShapeDtypeStruct((width, 128), jnp.float32),
        ],
        in_specs=[whole(part.shape) for part in parts]
        + [
            block(128),
            block(2),
            block(128),
            block(width),
            block(width),
            block(width),
            pl.BlockSpec((width, 256), lambda j: (0, 12)),
        ],
        out_specs=[block(width), block(choice_count), block(width), whole((width, 128))],
        scratch_shapes=[pltpu.VMEM((16, width), jnp.float32), pltpu.VMEM((width, 128), jnp.float32)],
        compiler_params=pltpu.CompilerParams(
            dimension_semantics=("arbitrary",), vmem_limit_bytes=56 * 2**20
        ),
        cost_estimate=pl.CostEstimate(
            flops=6 * slot_count * rows * width,
            bytes_accessed=14 * rows * width + 4 * slot_count * width,
            transcendentals=0,
        ),
        name="combine",
    )(*parts, spots, routes, aux, normed, middle, cot, packed)


def experts_kernel(linked, *refs):
    if linked:
        (
            rows_ref, grads_ref, w_gate_ref, w_up_ref, w_down_ref, before_ref,
            grad_gu_ref, grad_down_ref, first_in, second_in,
            turned_ref, out_ref, back_ref, both_ref, send_sem, recv_sem,
        ) = refs
    else:
        (
            rows_ref, grads_ref, w_gate_ref, w_up_ref, w_down_ref, grad_gu_ref, grad_down_ref,
            both_ref, turned_ref, out_ref, back_ref,
        ) = refs
    step = pl.program_id(0)
    width = rows_ref.shape[-1]
    rows = rows_ref[...].reshape(-1, width)
    grads = grads_ref[...].reshape(-1, width)

    if linked:
        me, mine = place()
        owner_count = both_ref.shape[0]
        peers = [lax.rem(mine + k, owner_count) for k in range(1, owner_count)]

        def trade(n, source, target, k, peer):
            return pltpu.make_async_remote_copy(
                src_ref=source.at[peer],
                dst_ref=target.at[mine],
                send_sem=send_sem.at[n, k],
                recv_sem=recv_sem.at[n, mine],
                device_id=(me, peer),
                device_id_type=MESH,
            )

        def keep(n, source, target):
            return pltpu.make_async_copy(source.at[mine], target.at[mine], send_sem.at[n, 0])

        def trade_start(n, source, target):
            for k, peer in enumerate(peers):
                trade(n, source, target, k + 1, peer).start()
            keep(n, source, target).start()

        def trade_finish(n, source, target):
            keep(n, source, target).wait()
            for k, peer in enumerate(peers):
                pltpu.make_async_copy(target.at[peer], target.at[peer], recv_sem.at[n, peer]).wait()
                trade(n, source, target, k + 1, peer).wait_send()

        @pl.when(step == 0)
        def _():
            greet([(me, peer) for peer in peers])
            trade_start(0, before_ref, first_in)

    @pl.when(step == 0)
    def _():
        turned_ref[...] = jnp.transpose(rows)
        out_ref[...] = jnp.zeros_like(out_ref)
        back_ref[...] = jnp.zeros_like(back_ref)

    w_gate, w_up, w_down = w_gate_ref[...], w_up_ref[...], w_down_ref[0]
    gate, up = nn(rows, w_gate), nn(rows, w_up)
    squashed = 1.0 / (1.0 + jnp.exp(-gate))
    silu = gate * squashed
    activated = (silu * up).astype(jnp.bfloat16)
    grad_act = nt(grads, w_down)
    grad_gate = (grad_act * up * (squashed * (1.0 + gate * (1.0 - squashed)))).astype(jnp.bfloat16)
    grad_up = (grad_act * silu).astype(jnp.bfloat16)
    out_ref[...] += nn(activated, w_down)
    grad_down_ref[...] = tn(activated, grads).astype(jnp.bfloat16)
    back_ref[...] += nt(grad_gate, w_gate) + nt(grad_up, w_up)
    grad_gu_ref[0] = nn(turned_ref[...], grad_gate).astype(jnp.bfloat16)
    grad_gu_ref[1] = nn(turned_ref[...], grad_up).astype(jnp.bfloat16)

    @pl.when(step == pl.num_programs(0) - 1)
    def _():
        shape = (both_ref.shape[0],) + both_ref.shape[2:]
        both_ref[:, 0] = out_ref[...].astype(jnp.bfloat16).reshape(shape)
        both_ref[:, 1] = back_ref[...].astype(jnp.bfloat16).reshape(shape)
        if linked:
            trade_start(1, both_ref, second_in)
            trade_finish(0, before_ref, first_in)
            trade_finish(1, both_ref, second_in)


def experts(arrived, arrived_grad, gate_up, down, at, before=None, collective=None):
    owners, _, cap, width = arrived.shape
    hidden = down.shape[1]
    count = owners * cap
    block = FF_BLOCK if count <= 1024 else FF_BLOCK // 4
    steps = hidden // block
    linked = before is not None
    pairs = pl.BlockSpec(
        (owners, 1, cap, width), lambda j: (0, at, 0, 0), pipeline_mode=pl.Buffered(1)
    )
    anywhere = pl.BlockSpec(memory_space=pl.ANY)
    both = jax.ShapeDtypeStruct((owners, 2, cap, width), jnp.bfloat16)
    links = {"collective_id": collective, "has_side_effects": True} if linked else {}
    return pl.pallas_call(
        functools.partial(experts_kernel, linked),
        grid=(steps,),
        out_shape=[
            jax.ShapeDtypeStruct((2, width, hidden), jnp.bfloat16),
            jax.ShapeDtypeStruct((hidden, width), jnp.bfloat16),
        ]
        + [both] * (2 if linked else 1),
        in_specs=[
            pairs,
            pairs,
            pl.BlockSpec((width, block), lambda j: (0, j)),
            pl.BlockSpec((width, block), lambda j: (0, steps + j)),
            pl.BlockSpec((1, block, width), lambda j: (at, j, 0)),
        ]
        + [anywhere] * linked,
        out_specs=[
            pl.BlockSpec((2, width, block), lambda j: (0, 0, j)),
            pl.BlockSpec((block, width), lambda j: (j, 0)),
        ]
        + ([anywhere] * 2 if linked else [pl.BlockSpec(both.shape, lambda j: (0, 0, 0, 0))]),
        scratch_shapes=[
            pltpu.VMEM((width, count), jnp.bfloat16),
            pltpu.VMEM((count, width), jnp.float32),
            pltpu.VMEM((count, width), jnp.float32),
        ]
        + (
            [
                pltpu.VMEM(both.shape, jnp.bfloat16),
                pltpu.SemaphoreType.DMA((2, owners)),
                pltpu.SemaphoreType.DMA((2, owners)),
            ]
            if linked
            else []
        ),
        compiler_params=pltpu.CompilerParams(
            dimension_semantics=("arbitrary",), vmem_limit_bytes=58 * 2**20, **links
        ),
        cost_estimate=pl.CostEstimate(
            flops=18 * count * width * hidden,
            bytes_accessed=12 * width * hidden + 8 * count * width,
            transcendentals=count * hidden,
        ),
        name="experts",
    )(arrived, arrived_grad, gate_up, gate_up, down, *([before] if linked else []))


def dp_grid(dp_count):
    outer = 4 if dp_count % 4 == 0 else 1
    return outer, dp_count // outer


def place():
    me, mine = lax.axis_index("dp"), lax.axis_index("expert")
    return me, mine


def greet(peers):
    barrier = pltpu.get_barrier_semaphore()
    for peer in peers:
        pl.semaphore_signal(barrier, inc=1, device_id=peer, device_id_type=MESH)
    pl.semaphore_wait(barrier, len(peers))


def small_gather_kernel(dp_count, shard_ref, full_ref, send_sem, pass_sem, recv_sem, mate_sem, own_sem):
    outer_count, inner_count = dp_grid(dp_count)
    me, mine = place()
    outer, inner = me // inner_count, me % inner_count
    rows, columns = shard_ref.shape
    half = columns // 2
    side = pl.multiple_of((mine % 2) * half, 128)
    mate = mine + 1 - 2 * (mine % 2)
    outer_peers = [lax.rem(outer + k, outer_count) for k in range(1, outer_count)]
    inner_peers = [lax.rem(inner + k, inner_count) for k in range(1, inner_count)]
    greet(
        [(peer * inner_count + inner, mine) for peer in outer_peers]
        + [(outer * inner_count + peer, mine) for peer in inner_peers]
        + [(me, mate)]
    )

    def spot(chunk):
        return full_ref.at[pl.ds(pl.multiple_of(chunk * rows, 8), rows), pl.ds(side, half)]

    sent = []

    def send(source, chunk, device, send_at, recv_at):
        copy = pltpu.make_async_remote_copy(
            src_ref=source,
            dst_ref=spot(chunk),
            send_sem=send_at,
            recv_sem=recv_at,
            device_id=device,
            device_id_type=MESH,
        )
        copy.start()
        sent.append(copy)

    def arrived(chunk):
        pltpu.make_async_copy(spot(chunk), spot(chunk), recv_sem.at[chunk]).wait()

    own_half = shard_ref.at[:, pl.ds(side, half)]
    for k, peer in enumerate(outer_peers):
        send(own_half, me, (peer * inner_count + inner, mine), send_sem.at[0, k], recv_sem.at[me])
    for k, peer in enumerate(inner_peers):
        send(own_half, me, (outer * inner_count + peer, mine), send_sem.at[1, k], recv_sem.at[me])
    own = pltpu.make_async_copy(
        shard_ref, full_ref.at[pl.ds(pl.multiple_of(me * rows, 8), rows), :], own_sem
    )
    own.start()
    chunks = []
    for k, peer in enumerate(outer_peers):
        chunk = peer * inner_count + inner
        arrived(chunk)
        for j, other in enumerate(inner_peers):
            send(spot(chunk), chunk, (outer * inner_count + other, mine), send_sem.at[2 + k, j], recv_sem.at[chunk])
        send(spot(chunk), chunk, (me, mate), pass_sem.at[len(chunks)], mate_sem.at[chunk])
        chunks.append(chunk)
    for other in inner_peers:
        for peer in [outer] + outer_peers:
            chunk = peer * inner_count + other
            arrived(chunk)
            send(spot(chunk), chunk, (me, mate), pass_sem.at[len(chunks)], mate_sem.at[chunk])
            chunks.append(chunk)
    own.wait()
    for chunk in chunks:
        there = full_ref.at[
            pl.ds(pl.multiple_of(chunk * rows, 8), rows), pl.ds(pl.multiple_of(half - side, 128), half)
        ]
        pltpu.make_async_copy(there, there, mate_sem.at[chunk]).wait()
    for copy in sent:
        copy.wait_send()


def small_gather(shard, dp_count, collective):
    outer_count, inner_count = dp_grid(dp_count)
    rows, columns = shard.shape
    lanes = max(outer_count, inner_count)
    return pl.pallas_call(
        functools.partial(small_gather_kernel, dp_count),
        out_shape=jax.ShapeDtypeStruct((dp_count * rows, columns), shard.dtype),
        in_specs=[pl.BlockSpec(memory_space=pl.ANY)],
        out_specs=pl.BlockSpec(memory_space=pl.ANY),
        scratch_shapes=[
            pltpu.SemaphoreType.DMA((outer_count + 1, lanes)),
            pltpu.SemaphoreType.DMA((dp_count,)),
            pltpu.SemaphoreType.DMA((dp_count,)),
            pltpu.SemaphoreType.DMA((dp_count,)),
            pltpu.SemaphoreType.DMA,
        ],
        compiler_params=pltpu.CompilerParams(collective_id=collective, has_side_effects=True),
        name="small_gather",
    )(shard)


def expert_gather_kernel(dp_count, tensor_count, cuts, crossed, owner_count, trade_count, *refs):
    given = tensor_count + trade_count
    shards, outgoing = refs[:tensor_count], refs[tensor_count:given]
    fulls, incoming = refs[given : given + tensor_count], refs[given + tensor_count : 2 * given]
    send_sem, recv_sem, own_sem, trade_send, trade_recv = refs[2 * given :]
    outer_count, inner_count = dp_grid(dp_count)
    me, mine = place()
    outer, inner = me // inner_count, me % inner_count
    below, above = lax.rem(outer + outer_count - 1, outer_count), lax.rem(outer + 1, outer_count)
    inner_peers = [lax.rem(inner + k, inner_count) for k in range(1, inner_count)]
    greet(
        [(peer * inner_count + inner, mine) for peer in (below, above)]
        + [(outer * inner_count + peer, mine) for peer in inner_peers]
        + [(me, lax.rem(mine + k, owner_count)) for k in range(1, owner_count) if trade_count]
    )
    trades = []
    for t in range(trade_count):
        for k in range(1, owner_count):
            peer = lax.rem(mine + k, owner_count)
            trade = pltpu.make_async_remote_copy(
                src_ref=outgoing[t].at[peer],
                dst_ref=incoming[t].at[mine],
                send_sem=trade_send.at[t, k],
                recv_sem=trade_recv.at[t, mine],
                device_id=(me, peer),
                device_id_type=MESH,
            )
            trade.start()
            trades.append(trade)
        keep = pltpu.make_async_copy(
            outgoing[t].at[mine], incoming[t].at[mine], trade_send.at[t, 0]
        )
        keep.start()
    pieces = [
        (t, e, c) for t in range(tensor_count) for e in range(shards[t].shape[0]) for c in range(cuts[t])
    ]

    def spot(p, chunk):
        t, e, c = pieces[p]
        rows = shards[t].shape[1]
        part = rows // cuts[t]
        return fulls[t].at[e, pl.ds(pl.multiple_of(chunk * rows + c * part, 8), part), :]

    def copy_of(p, source, chunk, device, send_at):
        return pltpu.make_async_remote_copy(
            src_ref=source,
            dst_ref=spot(p, chunk),
            send_sem=send_at,
            recv_sem=recv_sem.at[p, chunk],
            device_id=device,
            device_id_type=MESH,
        )

    def source_of(p):
        t, e, c = pieces[p]
        part = shards[t].shape[1] // cuts[t]
        return shards[t].at[e, pl.ds(c * part, part), :]

    def inner_sends(p, source, chunk):
        return [
            copy_of(p, source, chunk, (outer * inner_count + peer, mine), send_sem.at[p, 0, j, chunk])
            for j, peer in enumerate(inner_peers)
        ]

    def up(p, source, chunk):
        return copy_of(p, source, chunk, (above * inner_count + inner, mine), send_sem.at[p, 1, 0, chunk])

    def down(p, source, chunk):
        return copy_of(p, source, chunk, (below * inner_count + inner, mine), send_sem.at[p, 2, 0, chunk])

    def arrived(p, chunk):
        pltpu.make_async_copy(spot(p, chunk), spot(p, chunk), recv_sem.at[p, chunk]).wait()

    can_up, can_down = outer < outer_count - 1, outer > 0
    every = range(len(pieces))
    own = []
    for p in every:
        for copy in inner_sends(p, source_of(p), me):
            copy.start()
        pl.when(can_up)(lambda p=p: up(p, source_of(p), me).start())
        pl.when(can_down)(lambda p=p: down(p, source_of(p), me).start())
        copy = pltpu.make_async_copy(source_of(p), spot(p, me), own_sem.at[p])
        copy.start()
        own.append(copy)

    def passing(p, chunk, upward):
        arrived(p, chunk)
        if upward:
            pl.when(can_up)(lambda: up(p, spot(p, chunk), chunk).start())
        else:
            pl.when(can_down)(lambda: down(p, spot(p, chunk), chunk).start())

    for p in every:
        if p in crossed:
            for peer in inner_peers:
                chunk = outer * inner_count + peer
                arrived(p, chunk)
                pl.when(can_up)(lambda p=p, chunk=chunk: up(p, spot(p, chunk), chunk).start())
                pl.when(can_down)(lambda p=p, chunk=chunk: down(p, spot(p, chunk), chunk).start())
    for step in range(1, outer_count):
        low, high = outer - step, outer + step
        for p in every:
            for upward, there, source in ((True, low >= 0, low), (False, high < outer_count, high)):

                def relay(p=p, upward=upward, source=source):
                    chunk = source * inner_count + inner
                    passing(p, chunk, upward)
                    if p in crossed:
                        for peer in inner_peers:
                            passing(p, source * inner_count + peer, upward)
                    else:
                        for copy in inner_sends(p, spot(p, chunk), chunk):
                            copy.start()

                pl.when(there)(relay)
    for t in range(trade_count):
        pltpu.make_async_copy(
            outgoing[t].at[mine], incoming[t].at[mine], trade_send.at[t, 0]
        ).wait()
        for k in range(1, owner_count):
            there = incoming[t].at[lax.rem(mine + k, owner_count)]
            pltpu.make_async_copy(
                there, there, trade_recv.at[t, lax.rem(mine + k, owner_count)]
            ).wait()
    for trade in trades:
        trade.wait_send()
    for p in every:
        own[p].wait()
        if p not in crossed:
            for peer in inner_peers:
                for plane in range(outer_count):
                    arrived(p, plane * inner_count + peer)
        for copy in inner_sends(p, source_of(p), me):
            copy.wait_send()
        if p not in crossed:
            for k in range(1, outer_count):
                chunk = lax.rem(outer + k, outer_count) * inner_count + inner
                for copy in inner_sends(p, spot(p, chunk), chunk):
                    copy.wait_send()
        columns = range(inner_count) if p in crossed else [inner]
        for plane in range(outer_count):
            for column in columns:
                chunk = plane * inner_count + column
                pl.when(can_up & (outer >= plane))(lambda p=p, chunk=chunk: up(p, spot(p, chunk), chunk).wait_send())
                pl.when(can_down & (outer <= plane))(lambda p=p, chunk=chunk: down(p, spot(p, chunk), chunk).wait_send())


def expert_gather(shards, dp_count, collective, cuts=None, crossed=(), owner_count=1, trades=()):
    outer_count, inner_count = dp_grid(dp_count)
    cuts = cuts or [1] * len(shards)
    piece_count = sum(shard.shape[0] * cut for shard, cut in zip(shards, cuts))
    anywhere = pl.BlockSpec(memory_space=pl.ANY)
    given = len(shards) + len(trades)
    return pl.pallas_call(
        functools.partial(
            expert_gather_kernel, dp_count, len(shards), cuts, crossed, owner_count, len(trades)
        ),
        out_shape=[
            jax.ShapeDtypeStruct((s.shape[0], dp_count * s.shape[1], s.shape[2]), s.dtype)
            for s in shards
        ]
        + [jax.ShapeDtypeStruct(t.shape, t.dtype) for t in trades],
        in_specs=[anywhere] * given,
        out_specs=[anywhere] * given,
        scratch_shapes=[
            pltpu.SemaphoreType.DMA((piece_count, 3, max(1, inner_count - 1), dp_count)),
            pltpu.SemaphoreType.DMA((piece_count, dp_count)),
            pltpu.SemaphoreType.DMA((piece_count,)),
            pltpu.SemaphoreType.DMA((max(1, len(trades)), owner_count)),
            pltpu.SemaphoreType.DMA((max(1, len(trades)), owner_count)),
        ],
        compiler_params=pltpu.CompilerParams(collective_id=collective, has_side_effects=True),
        name="expert_gather",
    )(*shards, *trades)


def by_rows(count, body):
    def step(i, carry):
        body(i * 16)
        return carry

    lax.fori_loop(0, count // 16, step, 0)


def final_reduce_kernel(small_count, part_ref, *refs):
    small_refs, refs = refs[:small_count], refs[small_count:]
    (
        part_out, small_out, swap, part_in, part_low, part_high, small_in, small_low, small_high,
        final_low, final_in,
        swap_send, swap_recv, in_send, in_recv, line_send, line_recv, last_send, last_recv,
    ) = refs
    outer_count, inner_count = 4, 2
    me, mine = place()
    outer, inner = me // inner_count, me % inner_count
    side = mine % 2
    mate, across = mine + 1 - 2 * side, lax.rem(mine + 2, 4)
    beside = me + 1 - 2 * inner
    half_rows = small_refs[0].shape[1] // 2
    part_rows = part_ref.shape[2]
    starts = [sum(ref.shape[2] for ref in small_refs[:n]) for n in range(small_count + 1)]

    def remote(source, target, device, send_at, recv_at):
        return pltpu.make_async_remote_copy(
            src_ref=source,
            dst_ref=target,
            send_sem=send_at,
            recv_sem=recv_at,
            device_id=device,
            device_id_type=MESH,
        )

    barrier = pltpu.get_barrier_semaphore()
    low_peer = lax.rem(outer + outer_count - 1, outer_count) * inner_count + inner
    high_peer = lax.rem(outer + 1, outer_count) * inner_count + inner
    for device in ((me, mate), (me, across), (beside, mine), (low_peer, mine), (high_peer, mine)):
        pl.semaphore_signal(barrier, inc=1, device_id=device, device_id_type=MESH)
    pl.semaphore_wait(barrier, 5)

    mate_rows = pl.ds(pl.multiple_of((1 - side) * half_rows, 16), half_rows)
    own_rows = pl.ds(pl.multiple_of(side * half_rows, 16), half_rows)

    def swap_copy(n):
        return remote(
            small_refs[n].at[:, mate_rows, :],
            swap.at[:, :, starts[n] : starts[n + 1]],
            (me, mate),
            swap_send.at[n],
            swap_recv.at[n],
        )

    def inner_copy(plane):
        return remote(
            swap.at[plane * inner_count + 1 - inner],
            small_in.at[plane],
            (beside, mine),
            in_send.at[plane],
            in_recv.at[plane],
        )

    def line_copy(p, plane, upward, device_plane, source):
        target = ((part_low, small_low), (part_high, small_high))[0 if upward else 1][p].at[plane]
        way = 0 if upward else 1
        return remote(
            source,
            target,
            (device_plane * inner_count + inner, mine),
            line_send.at[p, way, plane],
            line_recv.at[p, way, plane],
        )

    def wide(values):
        return values.astype(jnp.float32)

    def add_own(chunk):
        def body(at):
            here = pl.ds(pl.multiple_of(at, 16), 16)
            there = pl.ds(pl.multiple_of(side * half_rows + at, 16), 16)
            for n in range(small_count):
                columns = slice(starts[n], starts[n + 1])
                swap[chunk, here, columns] = (
                    wide(swap[chunk, here, columns]) + wide(small_refs[n][chunk, there, :])
                ).astype(swap.dtype)

        by_rows(half_rows, body)

    def at_plane(o):
        order = sorted(range(outer_count), key=lambda t: (-abs(t - o), t))

        def arrive(p, plane, upward):
            line_copy(p, plane, upward, o, part_in.at[0] if p == 0 else small_in.at[0]).wait_recv()

        def held(plane):
            relayed = (plane > o > 0) or (plane < o < outer_count - 1)
            return part_in.at[plane] if relayed else part_ref.at[:, plane]

        def line_start(p, plane):
            source = held(plane) if p == 0 else small_in.at[plane]
            return line_copy(p, plane, plane > o, o + 1 if plane > o else o - 1, source)

        for n in range(small_count):
            swap_copy(n).start()
        for plane in order:
            if (plane > o and o == 0) or (plane < o and o == outer_count - 1):
                line_start(0, plane).start()
        for n in range(small_count):
            swap_copy(n).wait_recv()
        for plane in order:
            for column in range(inner_count):
                add_own(plane * inner_count + column)
            inner_copy(plane).start()
        for plane in order:
            upward = plane > o
            if plane != o and 0 < o < outer_count - 1:
                arrive(0, plane, upward)
                lines = part_low if upward else part_high

                def relay(at, plane=plane, lines=lines):
                    here = pl.ds(pl.multiple_of(at, 16), 16)
                    part_in[plane, :, here, :] = (
                        wide(part_ref[:, plane, here, :]) + wide(lines[plane, :, here, :])
                    ).astype(part_in.dtype)

                by_rows(part_rows, relay)
                line_start(0, plane).start()
            inner_copy(plane).wait_recv()
            relayed = plane != o and 0 < o < outer_count - 1
            lines = small_low if upward else small_high
            if relayed:
                arrive(1, plane, upward)

            def gather(at, plane=plane, lines=lines, relayed=relayed):
                here = pl.ds(pl.multiple_of(at, 16), 16)
                total = wide(small_in[plane, here, :]) + wide(swap[plane * inner_count + inner, here, :])
                if relayed:
                    total = total + wide(lines[plane, here, :])
                small_in[plane, here, :] = total.astype(small_in.dtype)

            by_rows(half_rows, gather)
            if plane != o:
                line_start(1, plane).start()
        for p in (1, 0):
            if o > 0:
                arrive(p, o, True)
            if o < outer_count - 1:
                arrive(p, o, False)
            if p == 1:

                def finish_small(at):
                    here = pl.ds(pl.multiple_of(at, 16), 16)
                    total = wide(small_in[o, here, :])
                    if o > 0:
                        total = total + wide(small_low[o, here, :])
                    if o < outer_count - 1:
                        total = total + wide(small_high[o, here, :])
                    final_low[here, :] = total.astype(final_low.dtype)

                by_rows(half_rows, finish_small)
                remote(final_low, final_in, (me, across), last_send.at[0], last_recv.at[0]).start()
            else:

                def finish_part(at):
                    here = pl.ds(pl.multiple_of(at, 16), 16)
                    for side_at in range(2):
                        total = wide(part_ref[side_at, o, here, :])
                        if o > 0:
                            total = total + wide(part_low[o, side_at, here, :])
                        if o < outer_count - 1:
                            total = total + wide(part_high[o, side_at, here, :])
                        size = total.shape[1]
                        part_out[here, side_at * size : (side_at + 1) * size] = total

                by_rows(part_rows, finish_part)
        for plane in range(outer_count):
            inner_copy(plane).wait_send()
            if plane != o:
                line_start(0, plane).wait_send()
                line_start(1, plane).wait_send()
        for n in range(small_count):
            swap_copy(n).wait_send()

    for o in range(outer_count):
        pl.when(outer == o)(functools.partial(at_plane, o))
    remote(final_low, final_in, (me, across), last_send.at[0], last_recv.at[0]).wait()

    def total_body(at):
        here = pl.ds(pl.multiple_of(at, 16), 16)
        there = pl.ds(pl.multiple_of(side * half_rows + at, 16), 16)
        small_out[there, :] = wide(final_low[here, :]) + wide(final_in[here, :])

    by_rows(half_rows, total_body)
    mate_copy = remote(
        small_out.at[own_rows, :], small_out.at[own_rows, :], (me, mate), last_send.at[1], last_recv.at[1]
    )
    mate_copy.start()
    mate_copy.wait()


def final_reduce(part, smalls, collective):
    sides, planes, part_rows, part_columns = part.shape
    chunk_count, small_rows, _ = smalls[0].shape
    small_columns = sum(small.shape[2] for small in smalls)
    low = jnp.bfloat16
    in_vmem = pl.BlockSpec(memory_space=pltpu.VMEM)
    half = small_rows // 2
    return pl.pallas_call(
        functools.partial(final_reduce_kernel, len(smalls)),
        out_shape=[
            jax.ShapeDtypeStruct((part_rows, sides * part_columns), jnp.float32),
            jax.ShapeDtypeStruct((small_rows, small_columns), jnp.float32),
        ],
        in_specs=[in_vmem] * (1 + len(smalls)),
        out_specs=[in_vmem] * 2,
        scratch_shapes=[pltpu.VMEM((chunk_count, half, small_columns), low)]
        + [pltpu.VMEM((planes, sides, part_rows, part_columns), low)] * 3
        + [pltpu.VMEM((planes, half, small_columns), low)] * 3
        + [pltpu.VMEM((half, small_columns), low)] * 2
        + [
            pltpu.SemaphoreType.DMA((len(smalls),)),
            pltpu.SemaphoreType.DMA((len(smalls),)),
            pltpu.SemaphoreType.DMA((planes,)),
            pltpu.SemaphoreType.DMA((planes,)),
            pltpu.SemaphoreType.DMA((2, 2, planes)),
            pltpu.SemaphoreType.DMA((2, 2, planes)),
            pltpu.SemaphoreType.DMA((2,)),
            pltpu.SemaphoreType.DMA((2,)),
        ],
        compiler_params=pltpu.CompilerParams(
            collective_id=collective, has_side_effects=True, vmem_limit_bytes=58 * 2**20
        ),
        name="final_reduce",
    )(part, *smalls)


def shards(
    tokens,
    resid_logits,
    routes,
    doc_ids,
    w_qkv,
    w_out,
    gain_attn,
    gain_ffn,
    w_router,
    w_const,
    v_const,
    w_gate_up,
    w_down,
    out_grad,
):
    dp_count, owner_count = lax.axis_size("dp"), lax.axis_size("expert")
    own_links = dp_count == 8 and owner_count == 4
    seq_count, length, width = tokens.shape
    assert seq_count == 1
    rows = seq_count * length
    choice_count = resid_logits.shape[-1]
    local_count = w_gate_up.shape[0]
    expert_count = owner_count * local_count
    hidden_count = w_down.shape[1] * dp_count
    width_qkv, width_out = w_qkv.shape[1], w_out.shape[1]
    small_parts = [w_router, w_const, v_const, gain_attn[:, None], gain_ffn[:, None]]
    small_width = sum(part.shape[1] for part in small_parts)
    pad = jnp.zeros((w_qkv.shape[0], 256 - small_width), jnp.bfloat16)
    packed = jnp.concatenate([w_qkv, w_out] + small_parts + [pad], 1)
    inputs = tokens.reshape(rows, width)
    cot = out_grad.reshape(rows, width)
    route_rows = routes.reshape(rows, 2)
    spots, spot_rows = routing(route_rows, expert_count)
    cosine, sine = rotary_lanes(length, width // HEADS)
    docs_row, docs_column = doc_ids.reshape(1, rows), doc_ids.reshape(rows, 1)
    resid = jnp.pad(
        resid_logits.reshape(rows, choice_count).astype(jnp.float32), ((0, 0), (0, 128 - choice_count))
    )
    if own_links:
        packed_full = small_gather(packed, dp_count, 1)
    else:
        packed_full = lax.all_gather(packed, "dp", axis=0, tiled=True)
    gate_up_full = [
        lax.all_gather(w_gate_up[e], "dp", axis=0, tiled=True) for e in range(local_count)
    ]
    normed_one, queries, keys, values, attended, middle, normed_two, aux = attention_forward(
        inputs, packed_full, docs_row, docs_column, cosine, sine, route_rows, resid
    )
    send_rows, send_grads = dispatch(spot_rows, aux, normed_two, cot, expert_count * CAP)
    send_rows = send_rows.reshape(owner_count, local_count * CAP, width)
    send_grads = send_grads.reshape(owner_count, local_count * CAP, width)
    exchange = functools.partial(
        lax.all_to_all, axis_name="expert", split_axis=0, concat_axis=0, tiled=True
    )
    if own_links:
        down_full, arrived, arrived_grad = expert_gather(
            [w_down], dp_count, 2, owner_count=owner_count, trades=[send_rows, send_grads]
        )
    else:
        down_full = lax.all_gather(w_down, "dp", axis=1, tiled=True)
        arrived, arrived_grad = exchange(send_rows), exchange(send_grads)
    arrived = arrived.reshape(owner_count, local_count, CAP, width)
    arrived_grad = arrived_grad.reshape(owner_count, local_count, CAP, width)

    parts, gu_parts, down_parts = [], [], []
    for e in range(local_count):
        if own_links and e == local_count - 1:
            grad_gu, grad_down, *parts = experts(
                arrived, arrived_grad, gate_up_full[e], down_full, e, both, 4
            )
        else:
            grad_gu, grad_down, both = experts(
                arrived, arrived_grad, gate_up_full[e], down_full, e
            )
            if not own_links:
                parts.append(exchange(both))
        down_parts.append(lax.psum_scatter(grad_down, "dp", scatter_dimension=0, tiled=True))
        if own_links and e == local_count - 1:
            inner = lax.axis_index("dp") % 2
            grad_gu = grad_gu.reshape(2, dp_count // 2, 2, width // dp_count, hidden_count)
            theirs = lax.ppermute(
                lax.dynamic_index_in_dim(grad_gu, 1 - inner, 2, False),
                "dp",
                [(i, i + 1 - 2 * (i % 2)) for i in range(dp_count)],
            )
        else:
            gu_part = lax.psum_scatter(grad_gu, "dp", scatter_dimension=1, tiled=True)
            gu_parts.append(
                jnp.concatenate([gu_part[0], gu_part[1]], -1).astype(jnp.float32)
            )

    if own_links:
        parts, down_parts[0] = lax.optimization_barrier((parts, down_parts[0]))
    output, logit_grad, grad_middle, small_grad = combine(
        parts, spots, route_rows, aux, normed_two, middle, cot, packed_full, choice_count, expert_count
    )
    token_grad, *weight_grads = attention_backward(
        grad_middle, queries, keys, values, attended, normed_one, inputs, packed_full, docs_row,
        docs_column, cosine, sine, small_grad,
    )
    if own_links:
        part_width = width // dp_count
        theirs, weight_grads = lax.optimization_barrier((theirs, weight_grads))
        linked = (
            lax.dynamic_index_in_dim(grad_gu, inner, 2, False).astype(jnp.float32)
            + theirs.astype(jnp.float32)
        ).astype(jnp.bfloat16)
        gu_part, packed_part = final_reduce(
            linked,
            [grad.reshape(dp_count, part_width, grad.shape[1]) for grad in weight_grads],
            3,
        )
        gu_parts = gu_parts + [gu_part]
    else:
        packed_part = lax.psum_scatter(
            jnp.concatenate(weight_grads, 1), "dp", scatter_dimension=0, tiled=True
        )
        packed_part = lax.psum(packed_part, "expert").astype(jnp.float32)
    part_qkv = packed_part[:, :width_qkv]
    part_out = packed_part[:, width_qkv : width_qkv + width_out]
    small_part = packed_part[:, width_qkv + width_out :]
    return (
        output.reshape(tokens.shape),
        token_grad.reshape(tokens.shape),
        logit_grad.reshape(resid_logits.shape),
        part_qkv,
        part_out,
        small_part[:, 18],
        small_part[:, 19],
        small_part[:, 0:12],
        small_part[:, 12:16],
        small_part[:, 16:18],
        jnp.stack(gu_parts),
        jnp.stack(down_parts).astype(jnp.float32),
    )


def solution(mesh):
    placed = (
        P(("dp", "expert"), None, None),
        P(("dp", "expert"), None, None),
        P(("dp", "expert"), None, None),
        P(("dp", "expert"), None),
        P("dp", None),
        P("dp", None),
        P("dp"),
        P("dp"),
        P("dp", None),
        P("dp", None),
        P("dp", None),
        P("expert", "dp", None),
        P("expert", "dp", None),
        P(("dp", "expert"), None, None),
    )
    return jax.shard_map(
        shards,
        mesh=mesh,
        in_specs=placed,
        out_specs=(
            P(("dp", "expert"), None, None),
            P(("dp", "expert"), None, None),
            P(("dp", "expert"), None, None),
            P("dp", None),
            P("dp", None),
            P("dp"),
            P("dp"),
            P("dp", None),
            P("dp", None),
            P("dp", None),
            P("expert", "dp", None),
            P("expert", "dp", None),
        ),
        check_vma=False,
    )
```

```python
import functools

import jax
import jax.numpy as jnp
import numpy as np
from jax import lax
from jax.experimental import pallas as pl
from jax.experimental.pallas import tpu as pltpu
from jax.sharding import PartitionSpec as P

HEADS = 12
BLOCK = 256
CAP = 256
GROUP = 256
FF_BLOCK = 512
MESH = pl.DeviceIdType.MESH
epsilon = 1e-06


def rotary_lanes(length, head_dim):
    half_dim = head_dim // 2
    frequency = (10000.0 ** (-np.arange(half_dim, dtype=np.float32) / half_dim)).astype(np.float32)
    angles = (np.arange(length, dtype=np.float32)[:, None] * frequency[None, :]).astype(np.float64)
    cosine = np.cos(angles).astype(np.float32)
    sine = np.sin(angles).astype(np.float32)
    return (
        np.concatenate([cosine] * 4, 1),
        np.concatenate([-sine, sine, -sine, sine], 1),
    )


def nt(left, right):
    return lax.dot_general(left, right, (((1,), (1,)), ((), ())), preferred_element_type=jnp.float32)


def tn(left, right):
    return lax.dot_general(left, right, (((0,), (0,)), ((), ())), preferred_element_type=jnp.float32)


def nn(left, right):
    return jnp.dot(left, right, preferred_element_type=jnp.float32)


def lane_ids(shape):
    return lax.broadcasted_iota(jnp.int32, shape, len(shape) - 1)


def turn(values, cosine, sine):
    lanes = lane_ids(values.shape)
    ahead, behind = pltpu.roll(values, 96, 1), pltpu.roll(values, 32, 1)
    return values * cosine + jnp.where(lanes % 64 < 32, ahead, behind) * sine


def key_span(i):
    return max(0, i - 2) * BLOCK, (i + 1) * BLOCK


def mask_of(docs_column, docs_row, i):
    low, high = key_span(i)
    return docs_column[low:high, :] == docs_row[:, i * BLOCK : (i + 1) * BLOCK]


def attention_forward_kernel(linked, *refs):
    (
        tokens_ref, wq_ref, wk_ref, wv_ref, wo_ref, small_ref, docs_row_ref, docs_column_ref,
        cosine_ref, sine_ref, routes_ref, resid_ref,
    ) = refs[:12]
    (
        normed_ref, q_ref, k_ref, v_ref, attended_ref, middle_ref, normed_two_ref, aux_ref,
    ) = refs[12 + bool(linked) : 20 + bool(linked)]
    step = pl.program_id(0)
    rows = tokens_ref.shape[0]
    if linked:
        branch_ref = refs[22]
        line = LineGather(refs[12].at[0], refs[21], linked, *refs[23:])

        @pl.when(step == 0)
        def _():
            greet(line.peers())
            line.start()

        @pl.when(step == 2)
        def _():
            line.relay(1)
    else:
        branch_ref = refs[20]

    @pl.when(step == 0)
    def _():
        inputs = tokens_ref[...].astype(jnp.float32)
        gains = jnp.transpose(small_ref[:, :128].astype(jnp.float32))[18:19, :]
        scale = lax.rsqrt(jnp.mean(inputs * inputs, -1, keepdims=True) + epsilon)
        normed_ref[...] = (inputs * scale * gains).astype(jnp.bfloat16)
        branch_ref[...] = jnp.zeros_like(branch_ref)

    normed = normed_ref[...]
    cosine, sine = cosine_ref[...], sine_ref[...]
    for w_ref, out_ref, turned in ((wq_ref, q_ref, True), (wk_ref, k_ref, True), (wv_ref, v_ref, False)):
        projected = nn(normed, w_ref[...])
        for half in range(2):
            part = projected[:, half * 128 : half * 128 + 128]
            if turned:
                part = turn(part, cosine, sine)
            out_ref[:, half * 128 : half * 128 + 128] = part.astype(jnp.bfloat16)

    docs_row, docs_column = docs_row_ref[...], docs_column_ref[...]
    for i in range(rows // BLOCK):
        low, high = key_span(i)
        here = slice(i * BLOCK, (i + 1) * BLOCK)
        allowed = mask_of(docs_column, docs_row, i)
        for pair in range(2):
            lanes = slice(pair * 128, pair * 128 + 128)
            queries = q_ref[here, lanes] * jnp.asarray(0.125, jnp.bfloat16)
            keys, values = k_ref[low:high, lanes], v_ref[low:high, lanes]
            left = lane_ids(queries.shape) < 64
            outs = []
            for head in range(2):
                own = left if head == 0 else jnp.logical_not(left)
                scores = nt(keys, jnp.where(own, queries, jnp.zeros_like(queries)))
                scores = jnp.where(allowed, scores, -1e30)
                shifted = jnp.exp(scores - jnp.max(scores, 0, keepdims=True))
                probs = shifted * (1.0 / jnp.sum(shifted, 0, keepdims=True))
                outs.append(tn(probs.astype(jnp.bfloat16), values))
            attended_ref[here, lanes] = jnp.where(left, outs[0], outs[1]).astype(jnp.bfloat16)
    branch_ref[...] += nn(attended_ref[...], wo_ref[...])

    @pl.when(step == pl.num_programs(0) - 1)
    def _():
        small = small_ref[:, :128]
        gains = jnp.transpose(small.astype(jnp.float32))[19:20, :]
        middle = tokens_ref[...].astype(jnp.float32) + branch_ref[...]
        middle_ref[...] = middle
        scale = lax.rsqrt(jnp.mean(middle * middle, -1, keepdims=True) + epsilon)
        normed_two = (middle * scale * gains).astype(jnp.bfloat16)
        normed_two_ref[...] = normed_two
        logits = nn(normed_two, small) + resid_ref[...].astype(jnp.float32)
        lanes = lane_ids(logits.shape)

        def lane(at):
            return jnp.sum(jnp.where(lanes == at, logits, 0.0), -1, keepdims=True)

        def two(first, second):
            peak = jnp.maximum(first, second)
            first, second = jnp.exp(first - peak), jnp.exp(second - peak)
            return first / (first + second), second / (first + second)

        columns = list(two(lane(routes_ref[:, 0:1]), lane(routes_ref[:, 1:2])))
        columns += list(two(lane(12), lane(13))) + list(two(lane(14), lane(15)))
        columns.append(scale)
        aux = jnp.zeros_like(logits)
        for at, column in enumerate(columns):
            aux = jnp.where(lanes == at, column, aux)
        aux_ref[...] = aux
        if linked:
            line.relay(2)
            line.relay(3)
            line.finish()


def attention_forward(
    tokens, packed, docs_row, docs_column, cosine, sine, routes, resid, shards=None,
    dp_count=None, collective=None,
):
    rows, width = tokens.shape
    groups = width // GROUP
    low = jnp.bfloat16
    whole = lambda shape: pl.BlockSpec(shape, lambda j: (0, 0))
    column = lambda at: pl.BlockSpec((width, GROUP), lambda j: (0, at + j))
    out_column = pl.BlockSpec((rows, GROUP), lambda j: (0, j))
    full = jax.ShapeDtypeStruct((rows, width), low)
    linked = shards is not None
    anywhere = pl.BlockSpec(memory_space=pl.ANY)
    links = {"collective_id": collective, "has_side_effects": True} if linked else {}
    gathered = []
    if linked:
        gathered = [jax.ShapeDtypeStruct((dp_count * shards.shape[1], shards.shape[2]), low)]
    return pl.pallas_call(
        functools.partial(attention_forward_kernel, dp_count if linked else 0),
        grid=(groups,),
        out_shape=[full] * 5
        + [
            jax.ShapeDtypeStruct((rows, width), jnp.float32),
            full,
            jax.ShapeDtypeStruct((rows, 128), jnp.float32),
        ]
        + gathered,
        in_specs=[
            whole((rows, width)),
            column(0),
            column(groups),
            column(2 * groups),
            pl.BlockSpec((GROUP, width), lambda j: (j, 3)),
            pl.BlockSpec((width, 256), lambda j: (0, 12)),
            whole((1, rows)),
            whole((rows, 1)),
            whole((rows, 128)),
            whole((rows, 128)),
            whole((rows, 2)),
            whole((rows, 128)),
        ]
        + [anywhere] * linked,
        out_specs=[whole((rows, width))]
        + [out_column] * 4
        + [whole((rows, width)), whole((rows, width)), whole((rows, 128))]
        + [anywhere] * linked,
        scratch_shapes=[pltpu.VMEM((rows, width), jnp.float32)]
        + (gather_semaphores(dp_count) if linked else []),
        compiler_params=pltpu.CompilerParams(
            dimension_semantics=("arbitrary",), vmem_limit_bytes=56 * 2**20, **links
        ),
        cost_estimate=pl.CostEstimate(
            flops=2 * rows * width * 4 * width + 8 * rows * rows * width // 2,
            bytes_accessed=24 * rows * width,
            transcendentals=rows * rows * HEADS // 2,
        ),
        name="attention_forward",
    )(
        tokens, packed, packed, packed, packed, packed, docs_row, docs_column, cosine, sine, routes,
        resid, *([shards] if linked else []),
    )


def attention_backward_kernel(
    grad_middle_ref, q_ref, k_ref, v_ref, attended_ref, normed_ref, tokens_ref,
    wq_ref, wk_ref, wv_ref, wo_ref, small_ref, docs_row_ref, docs_column_ref,
    cosine_ref, sine_ref, small_grad_ref,
    token_grad_ref, gq_ref, gk_ref, gv_ref, go_ref, small_out_ref,
    branch_ref, back_ref, turned_ref, key_acc, value_acc, query_acc,
):
    step = pl.program_id(0)
    rows, width = tokens_ref.shape

    @pl.when(step == 0)
    def _():
        branch_ref[...] = grad_middle_ref[...].astype(jnp.bfloat16)
        back_ref[...] = jnp.zeros_like(back_ref)

    grad_branch = branch_ref[...]
    grad_attended = nt(grad_branch, wo_ref[...]).astype(jnp.bfloat16)
    go_ref[...] = tn(attended_ref[...], grad_branch).astype(jnp.bfloat16)
    cosine, sine = cosine_ref[...], sine_ref[...]
    docs_row, docs_column = docs_row_ref[...], docs_column_ref[...]
    for pair in range(2):
        lanes = slice(pair * 128, pair * 128 + 128)
        key_acc[...] = jnp.zeros_like(key_acc)
        value_acc[...] = jnp.zeros_like(value_acc)
        for i in range(rows // BLOCK):
            low, high = key_span(i)
            here = slice(i * BLOCK, (i + 1) * BLOCK)
            allowed = mask_of(docs_column, docs_row, i)
            queries = q_ref[here, lanes] * jnp.asarray(0.125, jnp.bfloat16)
            grads = grad_attended[here, lanes]
            keys, values = k_ref[low:high, lanes], v_ref[low:high, lanes]
            left = lane_ids(queries.shape) < 64
            query_grads = []
            key_grad, value_grad = None, None
            for head in range(2):
                own = left if head == 0 else jnp.logical_not(left)
                own_queries = jnp.where(own, queries, jnp.zeros_like(queries))
                own_grads = jnp.where(own, grads, jnp.zeros_like(grads))
                scores = jnp.where(allowed, nt(keys, own_queries), -1e30)
                shifted = jnp.exp(scores - jnp.max(scores, 0, keepdims=True))
                probs = shifted * (1.0 / jnp.sum(shifted, 0, keepdims=True))
                grad_probs = nt(values, own_grads)
                inner = jnp.sum(probs * grad_probs, 0, keepdims=True)
                grad_scores = (probs * (grad_probs - inner)).astype(jnp.bfloat16)
                part_value = nn(probs.astype(jnp.bfloat16), own_grads)
                part_key = nn(grad_scores, own_queries)
                value_grad = part_value if head == 0 else value_grad + part_value
                key_grad = part_key if head == 0 else key_grad + part_key
                query_grads.append(tn(grad_scores, keys))
            value_acc[low:high, :] += value_grad
            key_acc[low:high, :] += key_grad
            query_acc[here, :] = jnp.where(left, query_grads[0], query_grads[1]) * 0.125
        turned_ref[0, :, lanes] = turn(query_acc[...], cosine, -sine).astype(jnp.bfloat16)
        turned_ref[1, :, lanes] = turn(key_acc[...], cosine, -sine).astype(jnp.bfloat16)
        turned_ref[2, :, lanes] = value_acc[...].astype(jnp.bfloat16)
    normed = normed_ref[...]
    for at, (w_ref, out_ref) in enumerate(((wq_ref, gq_ref), (wk_ref, gk_ref), (wv_ref, gv_ref))):
        turned = turned_ref[at]
        out_ref[...] = tn(normed, turned).astype(jnp.bfloat16)
        back_ref[...] += nt(turned, w_ref[...])

    @pl.when(step == pl.num_programs(0) - 1)
    def _():
        gains = jnp.transpose(small_ref[:, :128].astype(jnp.float32))[18:19, :]
        inputs = tokens_ref[...].astype(jnp.float32)
        grads = back_ref[...]
        scale = lax.rsqrt(jnp.mean(inputs * inputs, -1, keepdims=True) + epsilon)
        weighted = grads * gains
        mean = jnp.mean(weighted * inputs, -1, keepdims=True)
        grad_inputs = scale * weighted - inputs * (scale * scale * scale * mean)
        token_grad_ref[...] = (grad_inputs + grad_middle_ref[...]).astype(jnp.bfloat16)
        gain_grad = jnp.sum(grads * inputs * scale, 0, keepdims=True)
        column = jnp.transpose(jnp.broadcast_to(gain_grad, (128, width)))
        small_grad = small_grad_ref[...]
        small_grad = jnp.where(lane_ids(small_grad.shape) == 18, column, small_grad)
        small_out_ref[:, :128] = small_grad.astype(jnp.bfloat16)
        small_out_ref[:, 128:] = jnp.zeros((width, 128), jnp.bfloat16)


def attention_backward(
    grad_middle, queries, keys, values, attended, normed, tokens, packed, docs_row, docs_column,
    cosine, sine, small_grad,
):
    rows, width = tokens.shape
    groups = width // GROUP
    low = jnp.bfloat16
    whole = lambda shape: pl.BlockSpec(shape, lambda j: (0, 0))
    column = lambda at: pl.BlockSpec((width, GROUP), lambda j: (0, at + j))
    by_group = pl.BlockSpec((rows, GROUP), lambda j: (0, j))
    weight = jax.ShapeDtypeStruct((width, width), low)
    return pl.pallas_call(
        attention_backward_kernel,
        grid=(groups,),
        out_shape=[jax.ShapeDtypeStruct((rows, width), low)]
        + [weight] * 4
        + [jax.ShapeDtypeStruct((width, 256), low)],
        in_specs=[
            whole((rows, width)),
            by_group,
            by_group,
            by_group,
            by_group,
            whole((rows, width)),
            whole((rows, width)),
            column(0),
            column(groups),
            column(2 * groups),
            pl.BlockSpec((GROUP, width), lambda j: (j, 3)),
            pl.BlockSpec((width, 256), lambda j: (0, 12)),
            whole((1, rows)),
            whole((rows, 1)),
            whole((rows, 128)),
            whole((rows, 128)),
            whole((width, 128)),
        ],
        out_specs=[
            whole((rows, width)),
            column(0),
            column(0),
            column(0),
            pl.BlockSpec((GROUP, width), lambda j: (j, 0)),
            whole((width, 256)),
        ],
        scratch_shapes=[
            pltpu.VMEM((rows, width), low),
            pltpu.VMEM((rows, width), jnp.float32),
            pltpu.VMEM((3, rows, GROUP), low),
            pltpu.VMEM((rows, 128), jnp.float32),
            pltpu.VMEM((rows, 128), jnp.float32),
            pltpu.VMEM((rows, 128), jnp.float32),
        ],
        compiler_params=pltpu.CompilerParams(
            dimension_semantics=("arbitrary",), vmem_limit_bytes=56 * 2**20
        ),
        cost_estimate=pl.CostEstimate(
            flops=4 * rows * width * 4 * width + 20 * rows * rows * width // 2,
            bytes_accessed=32 * rows * width,
            transcendentals=rows * rows * HEADS // 2,
        ),
        name="attention_backward",
    )(
        grad_middle, queries, keys, values, attended, normed, tokens, packed, packed, packed,
        packed, packed, docs_row, docs_column, cosine, sine, small_grad,
    )


def routing_kernel(expert_count, routes_ref, columns_ref, rows_ref):
    rows = routes_ref.shape[0]
    lanes = lane_ids((rows, 128))
    first = (lanes == routes_ref[:, 0:1]).astype(jnp.float32)
    second = (lanes == routes_ref[:, 1:2]).astype(jnp.float32)
    down = lax.broadcasted_iota(jnp.int32, (rows, rows), 0)
    lower = (down > lane_ids((rows, rows))).astype(jnp.bfloat16)
    before_first = nn(lower, first.astype(jnp.bfloat16))
    before_second = nn(lower, second.astype(jnp.bfloat16)) + jnp.sum(first, 0, keepdims=True)
    spots = []
    for picked, before, at in ((first, before_first, 0), (second, before_second, 1)):
        rank = jnp.sum(picked * before, -1, keepdims=True)
        route = routes_ref[:, at : at + 1]
        spot = route.astype(jnp.float32) * CAP + rank
        spots.append(jnp.where(route < expert_count, spot, jnp.full_like(spot, 2.0 * expert_count * CAP)))
    both = jnp.where(lanes == 0, spots[0], jnp.where(lanes == 1, spots[1], 0.0))
    columns_ref[...] = both.astype(jnp.int32)
    rows_ref[...] = jnp.transpose(both)[0:8, :].astype(jnp.int32)


def routing(routes, expert_count):
    rows = routes.shape[0]
    return pl.pallas_call(
        functools.partial(routing_kernel, expert_count),
        out_shape=[
            jax.ShapeDtypeStruct((rows, 128), jnp.int32),
            jax.ShapeDtypeStruct((8, rows), jnp.int32),
        ],
        compiler_params=pltpu.CompilerParams(vmem_limit_bytes=40 * 2**20),
        name="routing",
    )(routes)


def dispatch_kernel(spots_ref, aux_ref, normed_ref, cot_ref, rows_ref, grads_ref, gates_ref):
    step = pl.program_id(0)

    @pl.when(step == 0)
    def _():
        gates_ref[...] = jnp.transpose(aux_ref[...])[0:8, :]

    shape = (rows_ref.shape[0], normed_ref.shape[0])
    slots = step * rows_ref.shape[0] + lax.broadcasted_iota(jnp.int32, shape, 0)
    first, second = slots == spots_ref[0:1, :], slots == spots_ref[1:2, :]
    gates = jnp.sum(
        jnp.where(first, gates_ref[0:1, :], jnp.where(second, gates_ref[1:2, :], 0.0)), -1, keepdims=True
    )
    chosen = jnp.where(first | second, 1.0, 0.0).astype(jnp.bfloat16)
    rows_ref[...] = nn(chosen, normed_ref[...]).astype(jnp.bfloat16)
    grads_ref[...] = (nn(chosen, cot_ref[...]) * gates).astype(jnp.bfloat16)


def dispatch(spots, aux, normed, cot, slot_count):
    rows, width = normed.shape
    whole = lambda shape: pl.BlockSpec(shape, lambda j: (0, 0))
    block = pl.BlockSpec((CAP, width), lambda j: (j, 0))
    return pl.pallas_call(
        dispatch_kernel,
        grid=(slot_count // CAP,),
        out_shape=[jax.ShapeDtypeStruct((slot_count, width), jnp.bfloat16)] * 2,
        in_specs=[whole((8, rows)), whole((rows, 128)), whole((rows, width)), whole((rows, width))],
        out_specs=[block, block],
        scratch_shapes=[pltpu.VMEM((8, rows), jnp.float32)],
        compiler_params=pltpu.CompilerParams(
            dimension_semantics=("arbitrary",), vmem_limit_bytes=60 * 2**20
        ),
        cost_estimate=pl.CostEstimate(
            flops=4 * slot_count * rows * width,
            bytes_accessed=4 * (rows + slot_count) * width,
            transcendentals=0,
        ),
        name="dispatch",
    )(spots, aux, normed, cot)


def halves(values):
    high = values.astype(jnp.bfloat16)
    return high, (values - high.astype(jnp.float32)).astype(jnp.bfloat16)


def combine_kernel(
    expert_count, local_count, *refs
):
    parts, refs = refs[:local_count], refs[local_count:]
    (
        spots_ref, routes_ref, aux_ref, normed_ref, middle_ref, cot_ref, small_ref,
        output_ref, logit_ref, grad_middle_ref, small_out_ref, vectors_ref, small_grad_ref,
    ) = refs
    step = pl.program_id(0)

    @pl.when(step == 0)
    def _():
        vectors_ref[0:8, :] = jnp.transpose(small_ref[:, :128].astype(jnp.float32))[16:24, :]
        vectors_ref[8:16, :] = jnp.zeros((8, vectors_ref.shape[1]), jnp.float32)
        small_grad_ref[...] = jnp.zeros_like(small_grad_ref)

    rows, width = normed_ref.shape
    normed_low, cot_low = normed_ref[...], cot_ref[...]
    normed, cot = normed_low.astype(jnp.float32), cot_low.astype(jnp.float32)
    total = lambda values: jnp.sum(values, -1, keepdims=True)
    picks, back = [0.0, 0.0], 0.0
    for e in range(local_count):
        count = parts[e].shape[0] * CAP
        slots = lane_ids((rows, count))
        slots = slots // CAP * (local_count * CAP) + e * CAP + slots % CAP
        hits = [slots == spots_ref[:, s : s + 1] for s in range(2)]
        chosen = [jnp.where(hit, 1.0, 0.0).astype(jnp.bfloat16) for hit in hits]
        returned = parts[e][:, 0].reshape(count, width)
        for s in range(2):
            picks[s] = picks[s] + nn(chosen[s], returned)
        back = back + nn(chosen[0] + chosen[1], parts[e][:, 1].reshape(count, width))
    inner = [total(pick * cot) for pick in picks]
    gates = [aux_ref[:, s : s + 1] for s in range(2)]
    routes = [routes_ref[:, s : s + 1] for s in range(2)]
    dot_copy = total(cot * normed)

    def weight_of(route):
        return sum(jnp.where(routes[s] == route, gates[s], 0.0) for s in range(2))

    copy_weight = weight_of(expert_count + 1)
    mix = gates[0] * picks[0] + gates[1] * picks[1]
    pass_weight = copy_weight
    gate_grads = [
        inner[s] + jnp.where(routes[s] == expert_count + 1, dot_copy, 0.0) for s in range(2)
    ]
    lanes = lane_ids((rows, 128))
    spread = jnp.zeros((rows, 128), jnp.float32)
    for k in range(2):
        vector = vectors_ref[k : k + 1, :]
        keep, blend = aux_ref[:, 2 + 2 * k : 3 + 2 * k], aux_ref[:, 3 + 2 * k : 4 + 2 * k]
        weight = weight_of(expert_count + 2 + k)
        dot_vector = total(cot * vector)
        pass_weight = pass_weight + weight * keep
        mix = mix + (weight * blend) * vector
        value = keep * dot_copy + blend * dot_vector
        for s in range(2):
            gate_grads[s] = gate_grads[s] + jnp.where(routes[s] == expert_count + 2 + k, value, 0.0)
        term = keep * blend * (weight * dot_copy - weight * dot_vector)
        spread = jnp.where(lanes == 12 + 2 * k, term, spread)
        spread = jnp.where(lanes == 13 + 2 * k, -term, spread)
        spread = jnp.where(lanes == 16 + k, weight * blend, spread)
    mix = mix + pass_weight * normed
    middle, scale = middle_ref[...], aux_ref[:, 6:7]
    output_ref[...] = (middle + mix).astype(jnp.bfloat16)
    mean = gates[0] * gate_grads[0] + gates[1] * gate_grads[1]
    for s in range(2):
        spread = jnp.where(lanes == routes[s], gates[s] * (gate_grads[s] - mean), spread)
    logit_ref[...] = spread[:, : logit_ref.shape[1]].astype(jnp.bfloat16)
    logits = jnp.where(lanes < 16, spread, 0.0)
    high, low = halves(logits)
    small = small_ref[:, :128]
    vector_high, vector_low = halves(spread - logits)
    small_grad_ref[...] += (
        tn(normed_low, high) + tn(normed_low, low) + tn(cot_low, vector_high) + tn(cot_low, vector_low)
    )
    grads = back + pass_weight * cot + nt(high, small) + nt(low, small)
    vectors_ref[8:9, :] += jnp.sum(grads * middle * scale, 0, keepdims=True)
    weighted = grads * vectors_ref[3:4, :]
    mean = jnp.mean(weighted * middle, -1, keepdims=True)
    grad_middle_ref[...] = cot + scale * weighted - middle * (scale * scale * scale * mean)

    @pl.when(step == pl.num_programs(0) - 1)
    def _():
        column = jnp.transpose(jnp.broadcast_to(vectors_ref[8:9, :], (128, width)))
        small_grad = small_grad_ref[...]
        small_out_ref[...] = jnp.where(lane_ids(small_grad.shape) == 19, column, small_grad)


def combine(parts, spots, routes, aux, normed, middle, cot, packed, choice_count, expert_count):
    rows, width = normed.shape
    local_count = len(parts)
    slot_count = expert_count * CAP
    size = 256
    block = lambda columns: pl.BlockSpec((size, columns), lambda j: (j, 0))
    whole = lambda shape: pl.BlockSpec(shape, lambda j: (0,) * len(shape))
    return pl.pallas_call(
        functools.partial(combine_kernel, expert_count, local_count),
        grid=(rows // size,),
        out_shape=[
            jax.ShapeDtypeStruct((rows, width), jnp.bfloat16),
            jax.ShapeDtypeStruct((rows, choice_count), jnp.bfloat16),
            jax.ShapeDtypeStruct((rows, width), jnp.float32),
            jax.ShapeDtypeStruct((width, 128), jnp.float32),
        ],
        in_specs=[whole(part.shape) for part in parts]
        + [
            block(128),
            block(2),
            block(128),
            block(width),
            block(width),
            block(width),
            pl.BlockSpec((width, 256), lambda j: (0, 12)),
        ],
        out_specs=[block(width), block(choice_count), block(width), whole((width, 128))],
        scratch_shapes=[pltpu.VMEM((16, width), jnp.float32), pltpu.VMEM((width, 128), jnp.float32)],
        compiler_params=pltpu.CompilerParams(
            dimension_semantics=("arbitrary",), vmem_limit_bytes=56 * 2**20
        ),
        cost_estimate=pl.CostEstimate(
            flops=6 * slot_count * rows * width,
            bytes_accessed=14 * rows * width + 4 * slot_count * width,
            transcendentals=0,
        ),
        name="combine",
    )(*parts, spots, routes, aux, normed, middle, cot, packed)


def experts_kernel(linked, dp_count, *refs):
    if dp_count:
        (
            rows_ref, grads_ref, w_gate_ref, w_up_ref, w_down_ref, shards_ref, grad_gu_ref,
            grad_down_ref, both_ref, full_ref, turned_ref, out_ref, back_ref, *line_sems,
        ) = refs
    elif linked:
        (
            rows_ref, grads_ref, w_gate_ref, w_up_ref, w_down_ref, before_ref,
            grad_gu_ref, grad_down_ref, first_in, second_in,
            turned_ref, out_ref, back_ref, both_ref, send_sem, recv_sem,
        ) = refs
    else:
        (
            rows_ref, grads_ref, w_gate_ref, w_up_ref, w_down_ref, grad_gu_ref, grad_down_ref,
            both_ref, turned_ref, out_ref, back_ref,
        ) = refs
    step = pl.program_id(0)
    width = rows_ref.shape[-1]
    rows = rows_ref[...].reshape(-1, width)
    grads = grads_ref[...].reshape(-1, width)

    if dp_count:
        line = LineGather(shards_ref.at[1], full_ref, dp_count, *line_sems)

        @pl.when(step == 0)
        def _():
            greet(line.peers())
            line.start()

        @pl.when(step == 2)
        def _():
            line.relay(1)

    if linked:
        me, mine = place()
        owner_count = both_ref.shape[0]
        peers = [lax.rem(mine + k, owner_count) for k in range(1, owner_count)]

        def trade(n, source, target, k, peer):
            return pltpu.make_async_remote_copy(
                src_ref=source.at[peer],
                dst_ref=target.at[mine],
                send_sem=send_sem.at[n, k],
                recv_sem=recv_sem.at[n, mine],
                device_id=(me, peer),
                device_id_type=MESH,
            )

        def keep(n, source, target):
            return pltpu.make_async_copy(source.at[mine], target.at[mine], send_sem.at[n, 0])

        def trade_start(n, source, target):
            for k, peer in enumerate(peers):
                trade(n, source, target, k + 1, peer).start()
            keep(n, source, target).start()

        def trade_finish(n, source, target):
            keep(n, source, target).wait()
            for k, peer in enumerate(peers):
                pltpu.make_async_copy(target.at[peer], target.at[peer], recv_sem.at[n, peer]).wait()
                trade(n, source, target, k + 1, peer).wait_send()

        @pl.when(step == 0)
        def _():
            greet([(me, peer) for peer in peers])
            trade_start(0, before_ref, first_in)

    @pl.when(step == 0)
    def _():
        turned_ref[...] = jnp.transpose(rows)
        out_ref[...] = jnp.zeros_like(out_ref)
        back_ref[...] = jnp.zeros_like(back_ref)

    w_gate, w_up, w_down = w_gate_ref[...], w_up_ref[...], w_down_ref[0]
    gate, up = nn(rows, w_gate), nn(rows, w_up)
    squashed = 1.0 / (1.0 + jnp.exp(-gate))
    silu = gate * squashed
    activated = (silu * up).astype(jnp.bfloat16)
    grad_act = nt(grads, w_down)
    grad_gate = (grad_act * up * (squashed * (1.0 + gate * (1.0 - squashed)))).astype(jnp.bfloat16)
    grad_up = (grad_act * silu).astype(jnp.bfloat16)
    out_ref[...] += nn(activated, w_down)
    grad_down_ref[...] = tn(activated, grads).astype(jnp.bfloat16)
    back_ref[...] += nt(grad_gate, w_gate) + nt(grad_up, w_up)
    grad_gu_ref[0] = nn(turned_ref[...], grad_gate).astype(jnp.bfloat16)
    grad_gu_ref[1] = nn(turned_ref[...], grad_up).astype(jnp.bfloat16)

    @pl.when(step == pl.num_programs(0) - 1)
    def _():
        shape = (both_ref.shape[0],) + both_ref.shape[2:]
        both_ref[:, 0] = out_ref[...].astype(jnp.bfloat16).reshape(shape)
        both_ref[:, 1] = back_ref[...].astype(jnp.bfloat16).reshape(shape)
        if dp_count:
            for hop in range(2, line.outer_count):
                line.relay(hop)
            line.finish()
        if linked:
            trade_start(1, both_ref, second_in)
            trade_finish(0, before_ref, first_in)
            trade_finish(1, both_ref, second_in)


def experts(arrived, arrived_grad, gate_up, down, at, before=None, shards=None, dp_count=0, collective=None):
    owners, _, cap, width = arrived.shape
    hidden = down.shape[1]
    count = owners * cap
    block = FF_BLOCK if count <= 1024 else FF_BLOCK // 4
    steps = hidden // block
    linked = before is not None
    pairs = pl.BlockSpec(
        (owners, 1, cap, width), lambda j: (0, at, 0, 0), pipeline_mode=pl.Buffered(1)
    )
    anywhere = pl.BlockSpec(memory_space=pl.ANY)
    both = jax.ShapeDtypeStruct((owners, 2, cap, width), jnp.bfloat16)
    gathers = shards is not None
    links = {"collective_id": collective, "has_side_effects": True} if linked or gathers else {}
    full = []
    if gathers:
        full = [jax.ShapeDtypeStruct((dp_count * shards.shape[1], shards.shape[2]), jnp.bfloat16)]
    return pl.pallas_call(
        functools.partial(experts_kernel, linked, dp_count),
        grid=(steps,),
        out_shape=[
            jax.ShapeDtypeStruct((2, width, hidden), jnp.bfloat16),
            jax.ShapeDtypeStruct((hidden, width), jnp.bfloat16),
        ]
        + [both] * (2 if linked else 1)
        + full,
        in_specs=[
            pairs,
            pairs,
            pl.BlockSpec((width, block), lambda j: (0, j)),
            pl.BlockSpec((width, block), lambda j: (0, steps + j)),
            pl.BlockSpec((1, block, width), lambda j: (at, j, 0)),
        ]
        + [anywhere] * (linked + gathers),
        out_specs=[
            pl.BlockSpec((2, width, block), lambda j: (0, 0, j)),
            pl.BlockSpec((block, width), lambda j: (j, 0)),
        ]
        + ([anywhere] * 2 if linked else [pl.BlockSpec(both.shape, lambda j: (0, 0, 0, 0))])
        + [anywhere] * gathers,
        scratch_shapes=[
            pltpu.VMEM((width, count), jnp.bfloat16),
            pltpu.VMEM((count, width), jnp.float32),
            pltpu.VMEM((count, width), jnp.float32),
        ]
        + (
            [
                pltpu.VMEM(both.shape, jnp.bfloat16),
                pltpu.SemaphoreType.DMA((2, owners)),
                pltpu.SemaphoreType.DMA((2, owners)),
            ]
            if linked
            else []
        )
        + (gather_semaphores(dp_count) if gathers else []),
        compiler_params=pltpu.CompilerParams(
            dimension_semantics=("arbitrary",), vmem_limit_bytes=58 * 2**20, **links
        ),
        cost_estimate=pl.CostEstimate(
            flops=18 * count * width * hidden,
            bytes_accessed=12 * width * hidden + 8 * count * width,
            transcendentals=count * hidden,
        ),
        name="experts",
    )(arrived, arrived_grad, gate_up, gate_up, down, *([before] if linked else []), *([shards] if gathers else []))


def dp_grid(dp_count):
    outer = 4 if dp_count % 4 == 0 else 1
    return outer, dp_count // outer


def place():
    me, mine = lax.axis_index("dp"), lax.axis_index("expert")
    return me, mine


def greet(peers):
    barrier = pltpu.get_barrier_semaphore()
    for peer in peers:
        pl.semaphore_signal(barrier, inc=1, device_id=peer, device_id_type=MESH)
    pl.semaphore_wait(barrier, len(peers))


def small_gather_kernel(dp_count, shard_ref, full_ref, send_sem, pass_sem, recv_sem, mate_sem, own_sem):
    outer_count, inner_count = dp_grid(dp_count)
    me, mine = place()
    outer, inner = me // inner_count, me % inner_count
    rows, columns = shard_ref.shape
    half = columns // 2
    side = pl.multiple_of((mine % 2) * half, 128)
    mate = mine + 1 - 2 * (mine % 2)
    outer_peers = [lax.rem(outer + k, outer_count) for k in range(1, outer_count)]
    inner_peers = [lax.rem(inner + k, inner_count) for k in range(1, inner_count)]
    greet(
        [(peer * inner_count + inner, mine) for peer in outer_peers]
        + [(outer * inner_count + peer, mine) for peer in inner_peers]
        + [(me, mate)]
    )

    def spot(chunk):
        return full_ref.at[pl.ds(pl.multiple_of(chunk * rows, 8), rows), pl.ds(side, half)]

    sent = []

    def send(source, chunk, device, send_at, recv_at):
        copy = pltpu.make_async_remote_copy(
            src_ref=source,
            dst_ref=spot(chunk),
            send_sem=send_at,
            recv_sem=recv_at,
            device_id=device,
            device_id_type=MESH,
        )
        copy.start()
        sent.append(copy)

    def arrived(chunk):
        pltpu.make_async_copy(spot(chunk), spot(chunk), recv_sem.at[chunk]).wait()

    own_half = shard_ref.at[:, pl.ds(side, half)]
    for k, peer in enumerate(outer_peers):
        send(own_half, me, (peer * inner_count + inner, mine), send_sem.at[0, k], recv_sem.at[me])
    for k, peer in enumerate(inner_peers):
        send(own_half, me, (outer * inner_count + peer, mine), send_sem.at[1, k], recv_sem.at[me])
    own = pltpu.make_async_copy(
        shard_ref, full_ref.at[pl.ds(pl.multiple_of(me * rows, 8), rows), :], own_sem
    )
    own.start()
    chunks = []
    for k, peer in enumerate(outer_peers):
        chunk = peer * inner_count + inner
        arrived(chunk)
        for j, other in enumerate(inner_peers):
            send(spot(chunk), chunk, (outer * inner_count + other, mine), send_sem.at[2 + k, j], recv_sem.at[chunk])
        send(spot(chunk), chunk, (me, mate), pass_sem.at[len(chunks)], mate_sem.at[chunk])
        chunks.append(chunk)
    for other in inner_peers:
        for peer in [outer] + outer_peers:
            chunk = peer * inner_count + other
            arrived(chunk)
            send(spot(chunk), chunk, (me, mate), pass_sem.at[len(chunks)], mate_sem.at[chunk])
            chunks.append(chunk)
    own.wait()
    for chunk in chunks:
        there = full_ref.at[
            pl.ds(pl.multiple_of(chunk * rows, 8), rows), pl.ds(pl.multiple_of(half - side, 128), half)
        ]
        pltpu.make_async_copy(there, there, mate_sem.at[chunk]).wait()
    for copy in sent:
        copy.wait_send()


def small_gather(shard, dp_count, collective):
    outer_count, inner_count = dp_grid(dp_count)
    rows, columns = shard.shape
    lanes = max(outer_count, inner_count)
    return pl.pallas_call(
        functools.partial(small_gather_kernel, dp_count),
        out_shape=jax.ShapeDtypeStruct((dp_count * rows, columns), shard.dtype),
        in_specs=[pl.BlockSpec(memory_space=pl.ANY)],
        out_specs=pl.BlockSpec(memory_space=pl.ANY),
        scratch_shapes=[
            pltpu.SemaphoreType.DMA((outer_count + 1, lanes)),
            pltpu.SemaphoreType.DMA((dp_count,)),
            pltpu.SemaphoreType.DMA((dp_count,)),
            pltpu.SemaphoreType.DMA((dp_count,)),
            pltpu.SemaphoreType.DMA,
        ],
        compiler_params=pltpu.CompilerParams(collective_id=collective, has_side_effects=True),
        name="small_gather",
    )(shard)


def expert_gather_kernel(dp_count, tensor_count, cuts, crossed, owner_count, trade_count, *refs):
    given = tensor_count + trade_count
    shards, outgoing = refs[:tensor_count], refs[tensor_count:given]
    fulls, incoming = refs[given : given + tensor_count], refs[given + tensor_count : 2 * given]
    send_sem, recv_sem, own_sem, trade_send, trade_recv = refs[2 * given :]
    outer_count, inner_count = dp_grid(dp_count)
    me, mine = place()
    outer, inner = me // inner_count, me % inner_count
    below, above = lax.rem(outer + outer_count - 1, outer_count), lax.rem(outer + 1, outer_count)
    inner_peers = [lax.rem(inner + k, inner_count) for k in range(1, inner_count)]
    greet(
        [(peer * inner_count + inner, mine) for peer in (below, above)]
        + [(outer * inner_count + peer, mine) for peer in inner_peers]
        + [(me, lax.rem(mine + k, owner_count)) for k in range(1, owner_count) if trade_count]
    )
    trades = []
    for t in range(trade_count):
        for k in range(1, owner_count):
            peer = lax.rem(mine + k, owner_count)
            trade = pltpu.make_async_remote_copy(
                src_ref=outgoing[t].at[peer],
                dst_ref=incoming[t].at[mine],
                send_sem=trade_send.at[t, k],
                recv_sem=trade_recv.at[t, mine],
                device_id=(me, peer),
                device_id_type=MESH,
            )
            trade.start()
            trades.append(trade)
        keep = pltpu.make_async_copy(
            outgoing[t].at[mine], incoming[t].at[mine], trade_send.at[t, 0]
        )
        keep.start()
    pieces = [
        (t, e, c) for t in range(tensor_count) for e in range(shards[t].shape[0]) for c in range(cuts[t])
    ]

    def spot(p, chunk):
        t, e, c = pieces[p]
        rows = shards[t].shape[1]
        part = rows // cuts[t]
        return fulls[t].at[e, pl.ds(pl.multiple_of(chunk * rows + c * part, 8), part), :]

    def copy_of(p, source, chunk, device, send_at):
        return pltpu.make_async_remote_copy(
            src_ref=source,
            dst_ref=spot(p, chunk),
            send_sem=send_at,
            recv_sem=recv_sem.at[p, chunk],
            device_id=device,
            device_id_type=MESH,
        )

    def source_of(p):
        t, e, c = pieces[p]
        part = shards[t].shape[1] // cuts[t]
        return shards[t].at[e, pl.ds(c * part, part), :]

    def inner_sends(p, source, chunk):
        return [
            copy_of(p, source, chunk, (outer * inner_count + peer, mine), send_sem.at[p, 0, j, chunk])
            for j, peer in enumerate(inner_peers)
        ]

    def up(p, source, chunk):
        return copy_of(p, source, chunk, (above * inner_count + inner, mine), send_sem.at[p, 1, 0, chunk])

    def down(p, source, chunk):
        return copy_of(p, source, chunk, (below * inner_count + inner, mine), send_sem.at[p, 2, 0, chunk])

    def arrived(p, chunk):
        pltpu.make_async_copy(spot(p, chunk), spot(p, chunk), recv_sem.at[p, chunk]).wait()

    can_up, can_down = outer < outer_count - 1, outer > 0
    every = range(len(pieces))
    own = []
    for p in every:
        for copy in inner_sends(p, source_of(p), me):
            copy.start()
        pl.when(can_up)(lambda p=p: up(p, source_of(p), me).start())
        pl.when(can_down)(lambda p=p: down(p, source_of(p), me).start())
        copy = pltpu.make_async_copy(source_of(p), spot(p, me), own_sem.at[p])
        copy.start()
        own.append(copy)

    def passing(p, chunk, upward):
        arrived(p, chunk)
        if upward:
            pl.when(can_up)(lambda: up(p, spot(p, chunk), chunk).start())
        else:
            pl.when(can_down)(lambda: down(p, spot(p, chunk), chunk).start())

    for p in every:
        if p in crossed:
            for peer in inner_peers:
                chunk = outer * inner_count + peer
                arrived(p, chunk)
                pl.when(can_up)(lambda p=p, chunk=chunk: up(p, spot(p, chunk), chunk).start())
                pl.when(can_down)(lambda p=p, chunk=chunk: down(p, spot(p, chunk), chunk).start())
    for step in range(1, outer_count):
        low, high = outer - step, outer + step
        for p in every:
            for upward, there, source in ((True, low >= 0, low), (False, high < outer_count, high)):

                def relay(p=p, upward=upward, source=source):
                    chunk = source * inner_count + inner
                    passing(p, chunk, upward)
                    if p in crossed:
                        for peer in inner_peers:
                            passing(p, source * inner_count + peer, upward)
                    else:
                        for copy in inner_sends(p, spot(p, chunk), chunk):
                            copy.start()

                pl.when(there)(relay)
    for t in range(trade_count):
        pltpu.make_async_copy(
            outgoing[t].at[mine], incoming[t].at[mine], trade_send.at[t, 0]
        ).wait()
        for k in range(1, owner_count):
            there = incoming[t].at[lax.rem(mine + k, owner_count)]
            pltpu.make_async_copy(
                there, there, trade_recv.at[t, lax.rem(mine + k, owner_count)]
            ).wait()
    for trade in trades:
        trade.wait_send()
    for p in every:
        own[p].wait()
        if p not in crossed:
            for peer in inner_peers:
                for plane in range(outer_count):
                    arrived(p, plane * inner_count + peer)
        for copy in inner_sends(p, source_of(p), me):
            copy.wait_send()
        if p not in crossed:
            for k in range(1, outer_count):
                chunk = lax.rem(outer + k, outer_count) * inner_count + inner
                for copy in inner_sends(p, spot(p, chunk), chunk):
                    copy.wait_send()
        columns = range(inner_count) if p in crossed else [inner]
        for plane in range(outer_count):
            for column in columns:
                chunk = plane * inner_count + column
                pl.when(can_up & (outer >= plane))(lambda p=p, chunk=chunk: up(p, spot(p, chunk), chunk).wait_send())
                pl.when(can_down & (outer <= plane))(lambda p=p, chunk=chunk: down(p, spot(p, chunk), chunk).wait_send())


def expert_gather(shards, dp_count, collective, cuts=None, crossed=(), owner_count=1, trades=()):
    outer_count, inner_count = dp_grid(dp_count)
    cuts = cuts or [1] * len(shards)
    piece_count = sum(shard.shape[0] * cut for shard, cut in zip(shards, cuts))
    anywhere = pl.BlockSpec(memory_space=pl.ANY)
    given = len(shards) + len(trades)
    return pl.pallas_call(
        functools.partial(
            expert_gather_kernel, dp_count, len(shards), cuts, crossed, owner_count, len(trades)
        ),
        out_shape=[
            jax.ShapeDtypeStruct((s.shape[0], dp_count * s.shape[1], s.shape[2]), s.dtype)
            for s in shards
        ]
        + [jax.ShapeDtypeStruct(t.shape, t.dtype) for t in trades],
        in_specs=[anywhere] * given,
        out_specs=[anywhere] * given,
        scratch_shapes=[
            pltpu.SemaphoreType.DMA((piece_count, 3, max(1, inner_count - 1), dp_count)),
            pltpu.SemaphoreType.DMA((piece_count, dp_count)),
            pltpu.SemaphoreType.DMA((piece_count,)),
            pltpu.SemaphoreType.DMA((max(1, len(trades)), owner_count)),
            pltpu.SemaphoreType.DMA((max(1, len(trades)), owner_count)),
        ],
        compiler_params=pltpu.CompilerParams(collective_id=collective, has_side_effects=True),
        name="expert_gather",
    )(*shards, *trades)


class LineGather:
    def __init__(self, shard, full, dp_count, send_sem, recv_sem, own_sem):
        self.shard, self.full, self.dp_count = shard, full, dp_count
        self.send_sem, self.recv_sem, self.own_sem = send_sem, recv_sem, own_sem
        self.outer_count, self.inner_count = dp_grid(dp_count)
        self.me, self.mine = place()
        self.outer, self.inner = self.me // self.inner_count, self.me % self.inner_count
        self.inner_peers = [
            lax.rem(self.inner + k, self.inner_count) for k in range(1, self.inner_count)
        ]
        self.can_up, self.can_down = self.outer < self.outer_count - 1, self.outer > 0

    def peers(self):
        below = lax.rem(self.outer + self.outer_count - 1, self.outer_count)
        above = lax.rem(self.outer + 1, self.outer_count)
        return [(peer * self.inner_count + self.inner, self.mine) for peer in (below, above)] + [
            (self.outer * self.inner_count + peer, self.mine) for peer in self.inner_peers
        ]

    def spot(self, chunk):
        rows = self.shard.shape[0]
        return self.full.at[pl.ds(pl.multiple_of(chunk * rows, 8), rows), :]

    def copy(self, source, chunk, device, way, at):
        return pltpu.make_async_remote_copy(
            src_ref=source,
            dst_ref=self.spot(chunk),
            send_sem=self.send_sem.at[way, at, chunk],
            recv_sem=self.recv_sem.at[chunk],
            device_id=(device, self.mine),
            device_id_type=MESH,
        )

    def up(self, source, chunk):
        return self.copy(source, chunk, (self.outer + 1) * self.inner_count + self.inner, 1, 0)

    def down(self, source, chunk):
        return self.copy(source, chunk, (self.outer - 1) * self.inner_count + self.inner, 2, 0)

    def across(self, source, chunk):
        return [
            self.copy(source, chunk, self.outer * self.inner_count + peer, 0, at)
            for at, peer in enumerate(self.inner_peers)
        ]

    def keep(self):
        return pltpu.make_async_copy(self.shard, self.spot(self.me), self.own_sem)

    def arrived(self, chunk):
        pltpu.make_async_copy(self.spot(chunk), self.spot(chunk), self.recv_sem.at[chunk]).wait()

    def start(self):
        for copy in self.across(self.shard, self.me):
            copy.start()
        pl.when(self.can_up)(lambda: self.up(self.shard, self.me).start())
        pl.when(self.can_down)(lambda: self.down(self.shard, self.me).start())
        self.keep().start()

    def relay(self, step):
        low, high = self.outer - step, self.outer + step

        def pass_on(source, upward):
            chunk = source * self.inner_count + self.inner
            self.arrived(chunk)
            if upward:
                pl.when(self.can_up)(lambda: self.up(self.spot(chunk), chunk).start())
            else:
                pl.when(self.can_down)(lambda: self.down(self.spot(chunk), chunk).start())
            for copy in self.across(self.spot(chunk), chunk):
                copy.start()

        pl.when(low >= 0)(lambda: pass_on(low, True))
        pl.when(high < self.outer_count)(lambda: pass_on(high, False))

    def finish(self):
        self.keep().wait()
        for peer in self.inner_peers:
            for plane in range(self.outer_count):
                self.arrived(plane * self.inner_count + peer)
        for plane in range(self.outer_count):
            chunk = plane * self.inner_count + self.inner
            for copy in self.across(self.spot(chunk), chunk):
                copy.wait_send()
            pl.when(self.can_up & (self.outer >= plane))(
                lambda chunk=chunk: self.up(self.spot(chunk), chunk).wait_send()
            )
            pl.when(self.can_down & (self.outer <= plane))(
                lambda chunk=chunk: self.down(self.spot(chunk), chunk).wait_send()
            )


def gather_semaphores(dp_count):
    inner_count = dp_grid(dp_count)[1]
    return [
        pltpu.SemaphoreType.DMA((3, max(1, inner_count - 1), dp_count)),
        pltpu.SemaphoreType.DMA((dp_count,)),
        pltpu.SemaphoreType.DMA,
    ]


def by_rows(count, body):
    def step(i, carry):
        body(i * 16)
        return carry

    lax.fori_loop(0, count // 16, step, 0)


def final_reduce_kernel(small_count, part_ref, *refs):
    small_refs, refs = refs[:small_count], refs[small_count:]
    (
        part_out, small_out, swap, part_in, part_low, part_high, small_in, small_low, small_high,
        final_low, final_in,
        swap_send, swap_recv, in_send, in_recv, line_send, line_recv, last_send, last_recv,
    ) = refs
    outer_count, inner_count = 4, 2
    me, mine = place()
    outer, inner = me // inner_count, me % inner_count
    side = mine % 2
    mate, across = mine + 1 - 2 * side, lax.rem(mine + 2, 4)
    beside = me + 1 - 2 * inner
    half_rows = small_refs[0].shape[1] // 2
    part_rows = part_ref.shape[2]
    starts = [sum(ref.shape[2] for ref in small_refs[:n]) for n in range(small_count + 1)]

    def remote(source, target, device, send_at, recv_at):
        return pltpu.make_async_remote_copy(
            src_ref=source,
            dst_ref=target,
            send_sem=send_at,
            recv_sem=recv_at,
            device_id=device,
            device_id_type=MESH,
        )

    barrier = pltpu.get_barrier_semaphore()
    low_peer = lax.rem(outer + outer_count - 1, outer_count) * inner_count + inner
    high_peer = lax.rem(outer + 1, outer_count) * inner_count + inner
    for device in ((me, mate), (me, across), (beside, mine), (low_peer, mine), (high_peer, mine)):
        pl.semaphore_signal(barrier, inc=1, device_id=device, device_id_type=MESH)
    pl.semaphore_wait(barrier, 5)

    mate_rows = pl.ds(pl.multiple_of((1 - side) * half_rows, 16), half_rows)
    own_rows = pl.ds(pl.multiple_of(side * half_rows, 16), half_rows)

    def swap_copy(n):
        return remote(
            small_refs[n].at[:, mate_rows, :],
            swap.at[:, :, starts[n] : starts[n + 1]],
            (me, mate),
            swap_send.at[n],
            swap_recv.at[n],
        )

    def inner_copy(plane):
        return remote(
            swap.at[plane * inner_count + 1 - inner],
            small_in.at[plane],
            (beside, mine),
            in_send.at[plane],
            in_recv.at[plane],
        )

    def line_copy(p, plane, upward, device_plane, source):
        target = ((part_low, small_low), (part_high, small_high))[0 if upward else 1][p].at[plane]
        way = 0 if upward else 1
        return remote(
            source,
            target,
            (device_plane * inner_count + inner, mine),
            line_send.at[p, way, plane],
            line_recv.at[p, way, plane],
        )

    def wide(values):
        return values.astype(jnp.float32)

    def add_own(chunk):
        def body(at):
            here = pl.ds(pl.multiple_of(at, 16), 16)
            there = pl.ds(pl.multiple_of(side * half_rows + at, 16), 16)
            for n in range(small_count):
                columns = slice(starts[n], starts[n + 1])
                swap[chunk, here, columns] = (
                    wide(swap[chunk, here, columns]) + wide(small_refs[n][chunk, there, :])
                ).astype(swap.dtype)

        by_rows(half_rows, body)

    def at_plane(o):
        order = sorted(range(outer_count), key=lambda t: (-abs(t - o), t))

        def arrive(p, plane, upward):
            line_copy(p, plane, upward, o, part_in.at[0] if p == 0 else small_in.at[0]).wait_recv()

        def held(plane):
            relayed = (plane > o > 0) or (plane < o < outer_count - 1)
            return part_in.at[plane] if relayed else part_ref.at[:, plane]

        def line_start(p, plane):
            source = held(plane) if p == 0 else small_in.at[plane]
            return line_copy(p, plane, plane > o, o + 1 if plane > o else o - 1, source)

        for n in range(small_count):
            swap_copy(n).start()
        for plane in order:
            if (plane > o and o == 0) or (plane < o and o == outer_count - 1):
                line_start(0, plane).start()
        for n in range(small_count):
            swap_copy(n).wait_recv()
        for plane in order:
            for column in range(inner_count):
                add_own(plane * inner_count + column)
            inner_copy(plane).start()
        for plane in order:
            upward = plane > o
            if plane != o and 0 < o < outer_count - 1:
                arrive(0, plane, upward)
                lines = part_low if upward else part_high

                def relay(at, plane=plane, lines=lines):
                    here = pl.ds(pl.multiple_of(at, 16), 16)
                    part_in[plane, :, here, :] = (
                        wide(part_ref[:, plane, here, :]) + wide(lines[plane, :, here, :])
                    ).astype(part_in.dtype)

                by_rows(part_rows, relay)
                line_start(0, plane).start()
            inner_copy(plane).wait_recv()
            relayed = plane != o and 0 < o < outer_count - 1
            lines = small_low if upward else small_high
            if relayed:
                arrive(1, plane, upward)

            def gather(at, plane=plane, lines=lines, relayed=relayed):
                here = pl.ds(pl.multiple_of(at, 16), 16)
                total = wide(small_in[plane, here, :]) + wide(swap[plane * inner_count + inner, here, :])
                if relayed:
                    total = total + wide(lines[plane, here, :])
                small_in[plane, here, :] = total.astype(small_in.dtype)

            by_rows(half_rows, gather)
            if plane != o:
                line_start(1, plane).start()
        for p in (1, 0):
            if o > 0:
                arrive(p, o, True)
            if o < outer_count - 1:
                arrive(p, o, False)
            if p == 1:

                def finish_small(at):
                    here = pl.ds(pl.multiple_of(at, 16), 16)
                    total = wide(small_in[o, here, :])
                    if o > 0:
                        total = total + wide(small_low[o, here, :])
                    if o < outer_count - 1:
                        total = total + wide(small_high[o, here, :])
                    final_low[here, :] = total.astype(final_low.dtype)

                by_rows(half_rows, finish_small)
                remote(final_low, final_in, (me, across), last_send.at[0], last_recv.at[0]).start()
            else:

                def finish_part(at):
                    here = pl.ds(pl.multiple_of(at, 16), 16)
                    for side_at in range(2):
                        total = wide(part_ref[side_at, o, here, :])
                        if o > 0:
                            total = total + wide(part_low[o, side_at, here, :])
                        if o < outer_count - 1:
                            total = total + wide(part_high[o, side_at, here, :])
                        size = total.shape[1]
                        part_out[here, side_at * size : (side_at + 1) * size] = total

                by_rows(part_rows, finish_part)
        for plane in range(outer_count):
            inner_copy(plane).wait_send()
            if plane != o:
                line_start(0, plane).wait_send()
                line_start(1, plane).wait_send()
        for n in range(small_count):
            swap_copy(n).wait_send()

    for o in range(outer_count):
        pl.when(outer == o)(functools.partial(at_plane, o))
    remote(final_low, final_in, (me, across), last_send.at[0], last_recv.at[0]).wait()

    def total_body(at):
        here = pl.ds(pl.multiple_of(at, 16), 16)
        there = pl.ds(pl.multiple_of(side * half_rows + at, 16), 16)
        small_out[there, :] = wide(final_low[here, :]) + wide(final_in[here, :])

    by_rows(half_rows, total_body)
    mate_copy = remote(
        small_out.at[own_rows, :], small_out.at[own_rows, :], (me, mate), last_send.at[1], last_recv.at[1]
    )
    mate_copy.start()
    mate_copy.wait()


def final_reduce(part, smalls, collective):
    sides, planes, part_rows, part_columns = part.shape
    chunk_count, small_rows, _ = smalls[0].shape
    small_columns = sum(small.shape[2] for small in smalls)
    low = jnp.bfloat16
    in_vmem = pl.BlockSpec(memory_space=pltpu.VMEM)
    half = small_rows // 2
    return pl.pallas_call(
        functools.partial(final_reduce_kernel, len(smalls)),
        out_shape=[
            jax.ShapeDtypeStruct((part_rows, sides * part_columns), jnp.float32),
            jax.ShapeDtypeStruct((small_rows, small_columns), jnp.float32),
        ],
        in_specs=[in_vmem] * (1 + len(smalls)),
        out_specs=[in_vmem] * 2,
        scratch_shapes=[pltpu.VMEM((chunk_count, half, small_columns), low)]
        + [pltpu.VMEM((planes, sides, part_rows, part_columns), low)] * 3
        + [pltpu.VMEM((planes, half, small_columns), low)] * 3
        + [pltpu.VMEM((half, small_columns), low)] * 2
        + [
            pltpu.SemaphoreType.DMA((len(smalls),)),
            pltpu.SemaphoreType.DMA((len(smalls),)),
            pltpu.SemaphoreType.DMA((planes,)),
            pltpu.SemaphoreType.DMA((planes,)),
            pltpu.SemaphoreType.DMA((2, 2, planes)),
            pltpu.SemaphoreType.DMA((2, 2, planes)),
            pltpu.SemaphoreType.DMA((2,)),
            pltpu.SemaphoreType.DMA((2,)),
        ],
        compiler_params=pltpu.CompilerParams(
            collective_id=collective, has_side_effects=True, vmem_limit_bytes=58 * 2**20
        ),
        name="final_reduce",
    )(part, *smalls)


def shards(
    tokens,
    resid_logits,
    routes,
    doc_ids,
    w_qkv,
    w_out,
    gain_attn,
    gain_ffn,
    w_router,
    w_const,
    v_const,
    w_gate_up,
    w_down,
    out_grad,
):
    dp_count, owner_count = lax.axis_size("dp"), lax.axis_size("expert")
    own_links = dp_count == 8 and owner_count == 4 and w_gate_up.shape[0] == 2
    seq_count, length, width = tokens.shape
    assert seq_count == 1
    rows = seq_count * length
    choice_count = resid_logits.shape[-1]
    local_count = w_gate_up.shape[0]
    expert_count = owner_count * local_count
    hidden_count = w_down.shape[1] * dp_count
    width_qkv, width_out = w_qkv.shape[1], w_out.shape[1]
    small_parts = [w_router, w_const, v_const, gain_attn[:, None], gain_ffn[:, None]]
    small_width = sum(part.shape[1] for part in small_parts)
    pad = jnp.zeros((w_qkv.shape[0], 256 - small_width), jnp.bfloat16)
    packed = jnp.concatenate([w_qkv, w_out] + small_parts + [pad], 1)
    inputs = tokens.reshape(rows, width)
    cot = out_grad.reshape(rows, width)
    route_rows = routes.reshape(rows, 2)
    spots, spot_rows = routing(route_rows, expert_count)
    cosine, sine = rotary_lanes(length, width // HEADS)
    docs_row, docs_column = doc_ids.reshape(1, rows), doc_ids.reshape(rows, 1)
    resid = jnp.pad(
        resid_logits.reshape(rows, choice_count).astype(jnp.float32), ((0, 0), (0, 128 - choice_count))
    )
    if own_links:
        packed_full = small_gather(packed, dp_count, 1)
    else:
        packed_full = lax.all_gather(packed, "dp", axis=0, tiled=True)
    attend = functools.partial(
        attention_forward, inputs, packed_full, docs_row, docs_column, cosine, sine, route_rows, resid
    )
    if own_links:
        *forward, first_gate_up = attend(w_gate_up, dp_count, 5)
        gate_up_full = [first_gate_up]
    else:
        forward = attend()
        gate_up_full = [
            lax.all_gather(w_gate_up[e], "dp", axis=0, tiled=True) for e in range(local_count)
        ]
    normed_one, queries, keys, values, attended, middle, normed_two, aux = forward
    send_rows, send_grads = dispatch(spot_rows, aux, normed_two, cot, expert_count * CAP)
    send_rows = send_rows.reshape(owner_count, local_count * CAP, width)
    send_grads = send_grads.reshape(owner_count, local_count * CAP, width)
    exchange = functools.partial(
        lax.all_to_all, axis_name="expert", split_axis=0, concat_axis=0, tiled=True
    )
    if own_links:
        down_full, arrived, arrived_grad = expert_gather(
            [w_down], dp_count, 2, owner_count=owner_count, trades=[send_rows, send_grads]
        )
    else:
        down_full = lax.all_gather(w_down, "dp", axis=1, tiled=True)
        arrived, arrived_grad = exchange(send_rows), exchange(send_grads)
    arrived = arrived.reshape(owner_count, local_count, CAP, width)
    arrived_grad = arrived_grad.reshape(owner_count, local_count, CAP, width)

    parts, gu_parts, down_parts = [], [], []
    for e in range(local_count):
        run = functools.partial(experts, arrived, arrived_grad, gate_up_full[e], down_full, e)
        if own_links and e == 0:
            grad_gu, grad_down, both, second_gate_up = run(
                shards=w_gate_up, dp_count=dp_count, collective=6
            )
            gate_up_full.append(second_gate_up)
        elif own_links:
            grad_gu, grad_down, *parts = run(before=both, collective=4)
        else:
            grad_gu, grad_down, both = run()
            parts.append(exchange(both))
        down_parts.append(lax.psum_scatter(grad_down, "dp", scatter_dimension=0, tiled=True))
        if own_links and e == local_count - 1:
            inner = lax.axis_index("dp") % 2
            grad_gu = grad_gu.reshape(2, dp_count // 2, 2, width // dp_count, hidden_count)
            theirs = lax.ppermute(
                lax.dynamic_index_in_dim(grad_gu, 1 - inner, 2, False),
                "dp",
                [(i, i + 1 - 2 * (i % 2)) for i in range(dp_count)],
            )
        else:
            gu_part = lax.psum_scatter(grad_gu, "dp", scatter_dimension=1, tiled=True)
            gu_parts.append(
                jnp.concatenate([gu_part[0], gu_part[1]], -1).astype(jnp.float32)
            )

    if own_links:
        parts, down_parts[0] = lax.optimization_barrier((parts, down_parts[0]))
    output, logit_grad, grad_middle, small_grad = combine(
        parts, spots, route_rows, aux, normed_two, middle, cot, packed_full, choice_count, expert_count
    )
    token_grad, *weight_grads = attention_backward(
        grad_middle, queries, keys, values, attended, normed_one, inputs, packed_full, docs_row,
        docs_column, cosine, sine, small_grad,
    )
    if own_links:
        part_width = width // dp_count
        theirs, weight_grads = lax.optimization_barrier((theirs, weight_grads))
        linked = (
            lax.dynamic_index_in_dim(grad_gu, inner, 2, False).astype(jnp.float32)
            + theirs.astype(jnp.float32)
        ).astype(jnp.bfloat16)
        gu_part, packed_part = final_reduce(
            linked,
            [grad.reshape(dp_count, part_width, grad.shape[1]) for grad in weight_grads],
            3,
        )
        gu_parts = gu_parts + [gu_part]
    else:
        packed_part = lax.psum_scatter(
            jnp.concatenate(weight_grads, 1), "dp", scatter_dimension=0, tiled=True
        )
        packed_part = lax.psum(packed_part, "expert").astype(jnp.float32)
    part_qkv = packed_part[:, :width_qkv]
    part_out = packed_part[:, width_qkv : width_qkv + width_out]
    small_part = packed_part[:, width_qkv + width_out :]
    return (
        output.reshape(tokens.shape),
        token_grad.reshape(tokens.shape),
        logit_grad.reshape(resid_logits.shape),
        part_qkv,
        part_out,
        small_part[:, 18],
        small_part[:, 19],
        small_part[:, 0:12],
        small_part[:, 12:16],
        small_part[:, 16:18],
        jnp.stack(gu_parts),
        jnp.stack(down_parts).astype(jnp.float32),
    )


def solution(mesh):
    placed = (
        P(("dp", "expert"), None, None),
        P(("dp", "expert"), None, None),
        P(("dp", "expert"), None, None),
        P(("dp", "expert"), None),
        P("dp", None),
        P("dp", None),
        P("dp"),
        P("dp"),
        P("dp", None),
        P("dp", None),
        P("dp", None),
        P("expert", "dp", None),
        P("expert", "dp", None),
        P(("dp", "expert"), None, None),
    )
    return jax.shard_map(
        shards,
        mesh=mesh,
        in_specs=placed,
        out_specs=(
            P(("dp", "expert"), None, None),
            P(("dp", "expert"), None, None),
            P(("dp", "expert"), None, None),
            P("dp", None),
            P("dp", None),
            P("dp"),
            P("dp"),
            P("dp", None),
            P("dp", None),
            P("dp", None),
            P("expert", "dp", None),
            P("expert", "dp", None),
        ),
        check_vma=False,
    )
```

```python
import functools

import jax
import jax.numpy as jnp
import numpy as np
from jax import lax
from jax.experimental import pallas as pl
from jax.experimental.pallas import tpu as pltpu
from jax.sharding import PartitionSpec as P

HEADS = 12
BLOCK = 256
CAP = 256
GROUP = 256
FF_BLOCK = 512
MESH = pl.DeviceIdType.MESH
epsilon = 1e-06


def rotary_lanes(length, head_dim):
    half_dim = head_dim // 2
    frequency = (10000.0 ** (-np.arange(half_dim, dtype=np.float32) / half_dim)).astype(np.float32)
    angles = (np.arange(length, dtype=np.float32)[:, None] * frequency[None, :]).astype(np.float64)
    cosine = np.cos(angles).astype(np.float32)
    sine = np.sin(angles).astype(np.float32)
    return (
        np.concatenate([cosine] * 4, 1),
        np.concatenate([-sine, sine, -sine, sine], 1),
    )


def nt(left, right):
    return lax.dot_general(left, right, (((1,), (1,)), ((), ())), preferred_element_type=jnp.float32)


def tn(left, right):
    return lax.dot_general(left, right, (((0,), (0,)), ((), ())), preferred_element_type=jnp.float32)


def nn(left, right):
    return jnp.dot(left, right, preferred_element_type=jnp.float32)


def lane_ids(shape):
    return lax.broadcasted_iota(jnp.int32, shape, len(shape) - 1)


def turn(values, cosine, sine):
    lanes = lane_ids(values.shape)
    ahead, behind = pltpu.roll(values, 96, 1), pltpu.roll(values, 32, 1)
    return values * cosine + jnp.where(lanes % 64 < 32, ahead, behind) * sine


def key_span(i):
    return max(0, i - 2) * BLOCK, (i + 1) * BLOCK


def mask_of(docs_column, docs_row, i):
    low, high = key_span(i)
    return docs_column[low:high, :] == docs_row[:, i * BLOCK : (i + 1) * BLOCK]


def attention_forward_kernel(linked, *refs):
    (
        tokens_ref, wq_ref, wk_ref, wv_ref, wo_ref, small_ref, docs_row_ref, docs_column_ref,
        cosine_ref, sine_ref, routes_ref, resid_ref,
    ) = refs[:12]
    (
        normed_ref, q_ref, k_ref, v_ref, attended_ref, middle_ref, normed_two_ref, aux_ref,
    ) = refs[12 + bool(linked) : 20 + bool(linked)]
    step = pl.program_id(0)
    rows = tokens_ref.shape[0]
    if linked:
        branch_ref = refs[22]
        line = LineGather(refs[12].at[0], refs[21], linked, *refs[23:])

        @pl.when(step == 0)
        def _():
            greet(line.peers())
            line.start()

        @pl.when(step == 2)
        def _():
            line.relay(1)
    else:
        branch_ref = refs[20]

    @pl.when(step == 0)
    def _():
        inputs = tokens_ref[...].astype(jnp.float32)
        gains = jnp.transpose(small_ref[:, :128].astype(jnp.float32))[18:19, :]
        scale = lax.rsqrt(jnp.mean(inputs * inputs, -1, keepdims=True) + epsilon)
        normed_ref[...] = (inputs * scale * gains).astype(jnp.bfloat16)
        branch_ref[...] = jnp.zeros_like(branch_ref)

    normed = normed_ref[...]
    cosine, sine = cosine_ref[...], sine_ref[...]
    for w_ref, out_ref, turned in ((wq_ref, q_ref, True), (wk_ref, k_ref, True), (wv_ref, v_ref, False)):
        projected = nn(normed, w_ref[...])
        for half in range(2):
            part = projected[:, half * 128 : half * 128 + 128]
            if turned:
                part = turn(part, cosine, sine)
            out_ref[:, half * 128 : half * 128 + 128] = part.astype(jnp.bfloat16)

    docs_row, docs_column = docs_row_ref[...], docs_column_ref[...]
    for i in range(rows // BLOCK):
        low, high = key_span(i)
        here = slice(i * BLOCK, (i + 1) * BLOCK)
        allowed = mask_of(docs_column, docs_row, i)
        for pair in range(2):
            lanes = slice(pair * 128, pair * 128 + 128)
            queries = q_ref[here, lanes] * jnp.asarray(0.125, jnp.bfloat16)
            keys, values = k_ref[low:high, lanes], v_ref[low:high, lanes]
            left = lane_ids(queries.shape) < 64
            outs = []
            for head in range(2):
                own = left if head == 0 else jnp.logical_not(left)
                scores = nt(keys, jnp.where(own, queries, jnp.zeros_like(queries)))
                scores = jnp.where(allowed, scores, -1e30)
                shifted = jnp.exp(scores - jnp.max(scores, 0, keepdims=True))
                probs = shifted * (1.0 / jnp.sum(shifted, 0, keepdims=True))
                outs.append(tn(probs.astype(jnp.bfloat16), values))
            attended_ref[here, lanes] = jnp.where(left, outs[0], outs[1]).astype(jnp.bfloat16)
    branch_ref[...] += nn(attended_ref[...], wo_ref[...])

    @pl.when(step == pl.num_programs(0) - 1)
    def _():
        small = small_ref[:, :128]
        gains = jnp.transpose(small.astype(jnp.float32))[19:20, :]
        middle = tokens_ref[...].astype(jnp.float32) + branch_ref[...]
        middle_ref[...] = middle
        scale = lax.rsqrt(jnp.mean(middle * middle, -1, keepdims=True) + epsilon)
        normed_two = (middle * scale * gains).astype(jnp.bfloat16)
        normed_two_ref[...] = normed_two
        logits = nn(normed_two, small) + resid_ref[...].astype(jnp.float32)
        lanes = lane_ids(logits.shape)

        def lane(at):
            return jnp.sum(jnp.where(lanes == at, logits, 0.0), -1, keepdims=True)

        def two(first, second):
            peak = jnp.maximum(first, second)
            first, second = jnp.exp(first - peak), jnp.exp(second - peak)
            return first / (first + second), second / (first + second)

        columns = list(two(lane(routes_ref[:, 0:1]), lane(routes_ref[:, 1:2])))
        columns += list(two(lane(12), lane(13))) + list(two(lane(14), lane(15)))
        columns.append(scale)
        aux = jnp.zeros_like(logits)
        for at, column in enumerate(columns):
            aux = jnp.where(lanes == at, column, aux)
        aux_ref[...] = aux
        if linked:
            line.relay(2)
            line.relay(3)
            line.finish()


def attention_forward(
    tokens, packed, docs_row, docs_column, cosine, sine, routes, resid, shards=None,
    dp_count=None, collective=None,
):
    rows, width = tokens.shape
    groups = width // GROUP
    low = jnp.bfloat16
    whole = lambda shape: pl.BlockSpec(shape, lambda j: (0, 0))
    column = lambda at: pl.BlockSpec((width, GROUP), lambda j: (0, at + j))
    out_column = pl.BlockSpec((rows, GROUP), lambda j: (0, j))
    full = jax.ShapeDtypeStruct((rows, width), low)
    linked = shards is not None
    anywhere = pl.BlockSpec(memory_space=pl.ANY)
    links = {"collective_id": collective, "has_side_effects": True} if linked else {}
    gathered = []
    if linked:
        gathered = [jax.ShapeDtypeStruct((dp_count * shards.shape[1], shards.shape[2]), low)]
    return pl.pallas_call(
        functools.partial(attention_forward_kernel, dp_count if linked else 0),
        grid=(groups,),
        out_shape=[full] * 5
        + [
            jax.ShapeDtypeStruct((rows, width), jnp.float32),
            full,
            jax.ShapeDtypeStruct((rows, 128), jnp.float32),
        ]
        + gathered,
        in_specs=[
            whole((rows, width)),
            column(0),
            column(groups),
            column(2 * groups),
            pl.BlockSpec((GROUP, width), lambda j: (j, 3)),
            pl.BlockSpec((width, 256), lambda j: (0, 12)),
            whole((1, rows)),
            whole((rows, 1)),
            whole((rows, 128)),
            whole((rows, 128)),
            whole((rows, 2)),
            whole((rows, 128)),
        ]
        + [anywhere] * linked,
        out_specs=[whole((rows, width))]
        + [out_column] * 4
        + [whole((rows, width)), whole((rows, width)), whole((rows, 128))]
        + [anywhere] * linked,
        scratch_shapes=[pltpu.VMEM((rows, width), jnp.float32)]
        + (gather_semaphores(dp_count) if linked else []),
        compiler_params=pltpu.CompilerParams(
            dimension_semantics=("arbitrary",), vmem_limit_bytes=56 * 2**20, **links
        ),
        cost_estimate=pl.CostEstimate(
            flops=2 * rows * width * 4 * width + 8 * rows * rows * width // 2,
            bytes_accessed=24 * rows * width,
            transcendentals=rows * rows * HEADS // 2,
        ),
        name="attention_forward",
    )(
        tokens, packed, packed, packed, packed, packed, docs_row, docs_column, cosine, sine, routes,
        resid, *([shards] if linked else []),
    )


def attention_backward_kernel(count, *refs):
    (
        grad_middle_ref, q_ref, k_ref, v_ref, attended_ref, normed_ref, tokens_ref,
        wq_ref, wk_ref, wv_ref, wo_ref, small_ref, docs_row_ref, docs_column_ref,
        cosine_ref, sine_ref, small_grad_ref,
    ) = refs[:17]
    sources, refs = refs[17 : 17 + count], refs[17 + count :]
    token_grad_ref, gq_ref, gk_ref, gv_ref, go_ref, small_out_ref = refs[:6]
    totals, refs = refs[6 : 6 + count], refs[6 + count :]
    branch_ref, back_ref, turned_ref, key_acc, value_acc, query_acc = refs[:6]
    step = pl.program_id(0)
    rows, width = tokens_ref.shape
    if count:
        line = line_reduce(sources, totals, refs[6:])

        @pl.when(step == 0)
        def _():
            greet(line.peers())
            line.each_plane(line.start)

        @pl.when(step == 2)
        def _():
            line.each_plane(lambda o: line.pass_on(o, 0))

    @pl.when(step == 0)
    def _():
        branch_ref[...] = grad_middle_ref[...].astype(jnp.bfloat16)
        back_ref[...] = jnp.zeros_like(back_ref)

    grad_branch = branch_ref[...]
    grad_attended = nt(grad_branch, wo_ref[...]).astype(jnp.bfloat16)
    go_ref[...] = tn(attended_ref[...], grad_branch).astype(jnp.bfloat16)
    cosine, sine = cosine_ref[...], sine_ref[...]
    docs_row, docs_column = docs_row_ref[...], docs_column_ref[...]
    for pair in range(2):
        lanes = slice(pair * 128, pair * 128 + 128)
        key_acc[...] = jnp.zeros_like(key_acc)
        value_acc[...] = jnp.zeros_like(value_acc)
        for i in range(rows // BLOCK):
            low, high = key_span(i)
            here = slice(i * BLOCK, (i + 1) * BLOCK)
            allowed = mask_of(docs_column, docs_row, i)
            queries = q_ref[here, lanes] * jnp.asarray(0.125, jnp.bfloat16)
            grads = grad_attended[here, lanes]
            keys, values = k_ref[low:high, lanes], v_ref[low:high, lanes]
            left = lane_ids(queries.shape) < 64
            query_grads = []
            key_grad, value_grad = None, None
            for head in range(2):
                own = left if head == 0 else jnp.logical_not(left)
                own_queries = jnp.where(own, queries, jnp.zeros_like(queries))
                own_grads = jnp.where(own, grads, jnp.zeros_like(grads))
                scores = jnp.where(allowed, nt(keys, own_queries), -1e30)
                shifted = jnp.exp(scores - jnp.max(scores, 0, keepdims=True))
                probs = shifted * (1.0 / jnp.sum(shifted, 0, keepdims=True))
                grad_probs = nt(values, own_grads)
                inner = jnp.sum(probs * grad_probs, 0, keepdims=True)
                grad_scores = (probs * (grad_probs - inner)).astype(jnp.bfloat16)
                part_value = nn(probs.astype(jnp.bfloat16), own_grads)
                part_key = nn(grad_scores, own_queries)
                value_grad = part_value if head == 0 else value_grad + part_value
                key_grad = part_key if head == 0 else key_grad + part_key
                query_grads.append(tn(grad_scores, keys))
            value_acc[low:high, :] += value_grad
            key_acc[low:high, :] += key_grad
            query_acc[here, :] = jnp.where(left, query_grads[0], query_grads[1]) * 0.125
        turned_ref[0, :, lanes] = turn(query_acc[...], cosine, -sine).astype(jnp.bfloat16)
        turned_ref[1, :, lanes] = turn(key_acc[...], cosine, -sine).astype(jnp.bfloat16)
        turned_ref[2, :, lanes] = value_acc[...].astype(jnp.bfloat16)
    normed = normed_ref[...]
    for at, (w_ref, out_ref) in enumerate(((wq_ref, gq_ref), (wk_ref, gk_ref), (wv_ref, gv_ref))):
        turned = turned_ref[at]
        out_ref[...] = tn(normed, turned).astype(jnp.bfloat16)
        back_ref[...] += nt(turned, w_ref[...])

    @pl.when(step == pl.num_programs(0) - 1)
    def _():
        gains = jnp.transpose(small_ref[:, :128].astype(jnp.float32))[18:19, :]
        inputs = tokens_ref[...].astype(jnp.float32)
        grads = back_ref[...]
        scale = lax.rsqrt(jnp.mean(inputs * inputs, -1, keepdims=True) + epsilon)
        weighted = grads * gains
        mean = jnp.mean(weighted * inputs, -1, keepdims=True)
        grad_inputs = scale * weighted - inputs * (scale * scale * scale * mean)
        token_grad_ref[...] = (grad_inputs + grad_middle_ref[...]).astype(jnp.bfloat16)
        gain_grad = jnp.sum(grads * inputs * scale, 0, keepdims=True)
        column = jnp.transpose(jnp.broadcast_to(gain_grad, (128, width)))
        small_grad = small_grad_ref[...]
        small_grad = jnp.where(lane_ids(small_grad.shape) == 18, column, small_grad)
        small_out_ref[:, :128] = small_grad.astype(jnp.bfloat16)
        small_out_ref[:, 128:] = jnp.zeros((width, 128), jnp.bfloat16)
        if count:

            def rest(o):
                for k in range(1, 4):
                    line.pass_on(o, k)
                line.finish(o)

            line.each_plane(rest)


def attention_backward(
    grad_middle, queries, keys, values, attended, normed, tokens, packed, docs_row, docs_column,
    cosine, sine, small_grad, sources=(), collective=None,
):
    rows, width = tokens.shape
    groups = width // GROUP
    low = jnp.bfloat16
    whole = lambda shape: pl.BlockSpec(shape, lambda j: (0, 0))
    column = lambda at: pl.BlockSpec((width, GROUP), lambda j: (0, at + j))
    by_group = pl.BlockSpec((rows, GROUP), lambda j: (0, j))
    weight = jax.ShapeDtypeStruct((width, width), low)
    linked = len(sources) > 0
    links = {"collective_id": collective, "has_side_effects": True} if linked else {}
    sums = []
    for source in sources:
        sides = source.shape[0] if len(source.shape) == 3 else 1
        sums.append((source.shape[-2] // 8, sides * source.shape[-1]))
    once = lambda shape: pl.BlockSpec(
        shape, lambda j: (0, 0), pipeline_mode=pl.Buffered(1)
    )
    return pl.pallas_call(
        functools.partial(attention_backward_kernel, len(sources)),
        grid=(groups,),
        out_shape=[jax.ShapeDtypeStruct((rows, width), low)]
        + [weight] * 4
        + [jax.ShapeDtypeStruct((width, 256), low)]
        + [jax.ShapeDtypeStruct(shape, jnp.float32) for shape in sums],
        in_specs=[
            once((rows, width)),
            by_group,
            by_group,
            by_group,
            by_group,
            once((rows, width)),
            once((rows, width)),
            column(0),
            column(groups),
            column(2 * groups),
            pl.BlockSpec((GROUP, width), lambda j: (j, 3)),
            pl.BlockSpec((width, 256), lambda j: (0, 12)),
            once((1, rows)),
            once((rows, 1)),
            once((rows, 128)),
            once((rows, 128)),
            once((width, 128)),
        ]
        + [pl.BlockSpec(memory_space=pl.ANY)] * len(sources),
        out_specs=[
            whole((rows, width)),
            column(0),
            column(0),
            column(0),
            pl.BlockSpec((GROUP, width), lambda j: (j, 0)),
            whole((width, 256)),
        ]
        + [whole(shape) for shape in sums],
        scratch_shapes=[
            pltpu.VMEM((rows, width), low),
            pltpu.VMEM((rows, width), jnp.float32),
            pltpu.VMEM((3, rows, GROUP), low),
            pltpu.VMEM((rows, 128), jnp.float32),
            pltpu.VMEM((rows, 128), jnp.float32),
            pltpu.VMEM((rows, 128), jnp.float32),
        ]
        + (reduce_scratch(sources) if linked else []),
        compiler_params=pltpu.CompilerParams(
            dimension_semantics=("arbitrary",), vmem_limit_bytes=61 * 2**20, **links
        ),
        cost_estimate=pl.CostEstimate(
            flops=4 * rows * width * 4 * width + 20 * rows * rows * width // 2,
            bytes_accessed=32 * rows * width,
            transcendentals=rows * rows * HEADS // 2,
        ),
        name="attention_backward",
    )(
        grad_middle, queries, keys, values, attended, normed, tokens, packed, packed, packed,
        packed, packed, docs_row, docs_column, cosine, sine, small_grad, *sources,
    )


def routing_kernel(expert_count, routes_ref, columns_ref, rows_ref):
    rows = routes_ref.shape[0]
    lanes = lane_ids((rows, 128))
    first = (lanes == routes_ref[:, 0:1]).astype(jnp.float32)
    second = (lanes == routes_ref[:, 1:2]).astype(jnp.float32)
    down = lax.broadcasted_iota(jnp.int32, (rows, rows), 0)
    lower = (down > lane_ids((rows, rows))).astype(jnp.bfloat16)
    before_first = nn(lower, first.astype(jnp.bfloat16))
    before_second = nn(lower, second.astype(jnp.bfloat16)) + jnp.sum(first, 0, keepdims=True)
    spots = []
    for picked, before, at in ((first, before_first, 0), (second, before_second, 1)):
        rank = jnp.sum(picked * before, -1, keepdims=True)
        route = routes_ref[:, at : at + 1]
        spot = route.astype(jnp.float32) * CAP + rank
        spots.append(jnp.where(route < expert_count, spot, jnp.full_like(spot, 2.0 * expert_count * CAP)))
    both = jnp.where(lanes == 0, spots[0], jnp.where(lanes == 1, spots[1], 0.0))
    columns_ref[...] = both.astype(jnp.int32)
    rows_ref[...] = jnp.transpose(both)[0:8, :].astype(jnp.int32)


def routing(routes, expert_count):
    rows = routes.shape[0]
    return pl.pallas_call(
        functools.partial(routing_kernel, expert_count),
        out_shape=[
            jax.ShapeDtypeStruct((rows, 128), jnp.int32),
            jax.ShapeDtypeStruct((8, rows), jnp.int32),
        ],
        compiler_params=pltpu.CompilerParams(vmem_limit_bytes=40 * 2**20),
        name="routing",
    )(routes)


def dispatch_kernel(spots_ref, aux_ref, normed_ref, cot_ref, rows_ref, grads_ref, gates_ref):
    step = pl.program_id(0)

    @pl.when(step == 0)
    def _():
        gates_ref[...] = jnp.transpose(aux_ref[...])[0:8, :]

    shape = (rows_ref.shape[0], normed_ref.shape[0])
    slots = step * rows_ref.shape[0] + lax.broadcasted_iota(jnp.int32, shape, 0)
    first, second = slots == spots_ref[0:1, :], slots == spots_ref[1:2, :]
    gates = jnp.sum(
        jnp.where(first, gates_ref[0:1, :], jnp.where(second, gates_ref[1:2, :], 0.0)), -1, keepdims=True
    )
    chosen = jnp.where(first | second, 1.0, 0.0).astype(jnp.bfloat16)
    rows_ref[...] = nn(chosen, normed_ref[...]).astype(jnp.bfloat16)
    grads_ref[...] = (nn(chosen, cot_ref[...]) * gates).astype(jnp.bfloat16)


def dispatch(spots, aux, normed, cot, slot_count):
    rows, width = normed.shape
    whole = lambda shape: pl.BlockSpec(shape, lambda j: (0, 0))
    block = pl.BlockSpec((CAP, width), lambda j: (j, 0))
    return pl.pallas_call(
        dispatch_kernel,
        grid=(slot_count // CAP,),
        out_shape=[jax.ShapeDtypeStruct((slot_count, width), jnp.bfloat16)] * 2,
        in_specs=[whole((8, rows)), whole((rows, 128)), whole((rows, width)), whole((rows, width))],
        out_specs=[block, block],
        scratch_shapes=[pltpu.VMEM((8, rows), jnp.float32)],
        compiler_params=pltpu.CompilerParams(
            dimension_semantics=("arbitrary",), vmem_limit_bytes=60 * 2**20
        ),
        cost_estimate=pl.CostEstimate(
            flops=4 * slot_count * rows * width,
            bytes_accessed=4 * (rows + slot_count) * width,
            transcendentals=0,
        ),
        name="dispatch",
    )(spots, aux, normed, cot)


def halves(values):
    high = values.astype(jnp.bfloat16)
    return high, (values - high.astype(jnp.float32)).astype(jnp.bfloat16)


def combine_kernel(
    expert_count, local_count, *refs
):
    parts, refs = refs[:local_count], refs[local_count:]
    (
        spots_ref, routes_ref, aux_ref, normed_ref, middle_ref, cot_ref, small_ref,
        output_ref, logit_ref, grad_middle_ref, small_out_ref, vectors_ref, small_grad_ref,
    ) = refs
    step = pl.program_id(0)

    @pl.when(step == 0)
    def _():
        vectors_ref[0:8, :] = jnp.transpose(small_ref[:, :128].astype(jnp.float32))[16:24, :]
        vectors_ref[8:16, :] = jnp.zeros((8, vectors_ref.shape[1]), jnp.float32)
        small_grad_ref[...] = jnp.zeros_like(small_grad_ref)

    rows, width = normed_ref.shape
    normed_low, cot_low = normed_ref[...], cot_ref[...]
    normed, cot = normed_low.astype(jnp.float32), cot_low.astype(jnp.float32)
    total = lambda values: jnp.sum(values, -1, keepdims=True)
    picks, back = [0.0, 0.0], 0.0
    for e in range(local_count):
        count = parts[e].shape[0] * CAP
        slots = lane_ids((rows, count))
        slots = slots // CAP * (local_count * CAP) + e * CAP + slots % CAP
        hits = [slots == spots_ref[:, s : s + 1] for s in range(2)]
        chosen = [jnp.where(hit, 1.0, 0.0).astype(jnp.bfloat16) for hit in hits]
        returned = parts[e][:, 0].reshape(count, width)
        for s in range(2):
            picks[s] = picks[s] + nn(chosen[s], returned)
        back = back + nn(chosen[0] + chosen[1], parts[e][:, 1].reshape(count, width))
    inner = [total(pick * cot) for pick in picks]
    gates = [aux_ref[:, s : s + 1] for s in range(2)]
    routes = [routes_ref[:, s : s + 1] for s in range(2)]
    dot_copy = total(cot * normed)

    def weight_of(route):
        return sum(jnp.where(routes[s] == route, gates[s], 0.0) for s in range(2))

    copy_weight = weight_of(expert_count + 1)
    mix = gates[0] * picks[0] + gates[1] * picks[1]
    pass_weight = copy_weight
    gate_grads = [
        inner[s] + jnp.where(routes[s] == expert_count + 1, dot_copy, 0.0) for s in range(2)
    ]
    lanes = lane_ids((rows, 128))
    spread = jnp.zeros((rows, 128), jnp.float32)
    for k in range(2):
        vector = vectors_ref[k : k + 1, :]
        keep, blend = aux_ref[:, 2 + 2 * k : 3 + 2 * k], aux_ref[:, 3 + 2 * k : 4 + 2 * k]
        weight = weight_of(expert_count + 2 + k)
        dot_vector = total(cot * vector)
        pass_weight = pass_weight + weight * keep
        mix = mix + (weight * blend) * vector
        value = keep * dot_copy + blend * dot_vector
        for s in range(2):
            gate_grads[s] = gate_grads[s] + jnp.where(routes[s] == expert_count + 2 + k, value, 0.0)
        term = keep * blend * (weight * dot_copy - weight * dot_vector)
        spread = jnp.where(lanes == 12 + 2 * k, term, spread)
        spread = jnp.where(lanes == 13 + 2 * k, -term, spread)
        spread = jnp.where(lanes == 16 + k, weight * blend, spread)
    mix = mix + pass_weight * normed
    middle, scale = middle_ref[...], aux_ref[:, 6:7]
    output_ref[...] = (middle + mix).astype(jnp.bfloat16)
    mean = gates[0] * gate_grads[0] + gates[1] * gate_grads[1]
    for s in range(2):
        spread = jnp.where(lanes == routes[s], gates[s] * (gate_grads[s] - mean), spread)
    logit_ref[...] = spread[:, : logit_ref.shape[1]].astype(jnp.bfloat16)
    logits = jnp.where(lanes < 16, spread, 0.0)
    high, low = halves(logits)
    small = small_ref[:, :128]
    vector_high, vector_low = halves(spread - logits)
    small_grad_ref[...] += (
        tn(normed_low, high) + tn(normed_low, low) + tn(cot_low, vector_high) + tn(cot_low, vector_low)
    )
    grads = back + pass_weight * cot + nt(high, small) + nt(low, small)
    vectors_ref[8:9, :] += jnp.sum(grads * middle * scale, 0, keepdims=True)
    weighted = grads * vectors_ref[3:4, :]
    mean = jnp.mean(weighted * middle, -1, keepdims=True)
    grad_middle_ref[...] = cot + scale * weighted - middle * (scale * scale * scale * mean)

    @pl.when(step == pl.num_programs(0) - 1)
    def _():
        column = jnp.transpose(jnp.broadcast_to(vectors_ref[8:9, :], (128, width)))
        small_grad = small_grad_ref[...]
        small_out_ref[...] = jnp.where(lane_ids(small_grad.shape) == 19, column, small_grad)


def combine(parts, spots, routes, aux, normed, middle, cot, packed, choice_count, expert_count):
    rows, width = normed.shape
    local_count = len(parts)
    slot_count = expert_count * CAP
    size = 256
    block = lambda columns: pl.BlockSpec((size, columns), lambda j: (j, 0))
    whole = lambda shape: pl.BlockSpec(shape, lambda j: (0,) * len(shape))
    return pl.pallas_call(
        functools.partial(combine_kernel, expert_count, local_count),
        grid=(rows // size,),
        out_shape=[
            jax.ShapeDtypeStruct((rows, width), jnp.bfloat16),
            jax.ShapeDtypeStruct((rows, choice_count), jnp.bfloat16),
            jax.ShapeDtypeStruct((rows, width), jnp.float32),
            jax.ShapeDtypeStruct((width, 128), jnp.float32),
        ],
        in_specs=[whole(part.shape) for part in parts]
        + [
            block(128),
            block(2),
            block(128),
            block(width),
            block(width),
            block(width),
            pl.BlockSpec((width, 256), lambda j: (0, 12)),
        ],
        out_specs=[block(width), block(choice_count), block(width), whole((width, 128))],
        scratch_shapes=[pltpu.VMEM((16, width), jnp.float32), pltpu.VMEM((width, 128), jnp.float32)],
        compiler_params=pltpu.CompilerParams(
            dimension_semantics=("arbitrary",), vmem_limit_bytes=56 * 2**20
        ),
        cost_estimate=pl.CostEstimate(
            flops=6 * slot_count * rows * width,
            bytes_accessed=14 * rows * width + 4 * slot_count * width,
            transcendentals=0,
        ),
        name="combine",
    )(*parts, spots, routes, aux, normed, middle, cot, packed)


def experts_kernel(linked, dp_count, *refs):
    if dp_count:
        (
            rows_ref, grads_ref, w_gate_ref, w_up_ref, w_down_ref, shards_ref, grad_gu_ref,
            grad_down_ref, both_ref, full_ref, turned_ref, out_ref, back_ref, *line_sems,
        ) = refs
    elif linked:
        (
            rows_ref, grads_ref, w_gate_ref, w_up_ref, w_down_ref, before_ref,
            grad_gu_ref, grad_down_ref, first_in, second_in,
            turned_ref, out_ref, back_ref, both_ref, send_sem, recv_sem,
        ) = refs
    else:
        (
            rows_ref, grads_ref, w_gate_ref, w_up_ref, w_down_ref, grad_gu_ref, grad_down_ref,
            both_ref, turned_ref, out_ref, back_ref,
        ) = refs
    step = pl.program_id(0)
    width = rows_ref.shape[-1]
    rows = rows_ref[...].reshape(-1, width)
    grads = grads_ref[...].reshape(-1, width)

    if dp_count:
        line = LineGather(
            shards_ref.at[1, :, 0 : full_ref.shape[1]], full_ref, dp_count, *line_sems
        )

        @pl.when(step == 0)
        def _():
            greet(line.peers())
            line.start()

        @pl.when(step == 2)
        def _():
            line.relay(1)

    if linked:
        me, mine = place()
        owner_count = both_ref.shape[0]
        peers = [lax.rem(mine + k, owner_count) for k in range(1, owner_count)]

        def trade(n, source, target, k, peer):
            return pltpu.make_async_remote_copy(
                src_ref=source.at[peer],
                dst_ref=target.at[mine],
                send_sem=send_sem.at[n, k],
                recv_sem=recv_sem.at[n, mine],
                device_id=(me, peer),
                device_id_type=MESH,
            )

        def keep(n, source, target):
            return pltpu.make_async_copy(source.at[mine], target.at[mine], send_sem.at[n, 0])

        def trade_start(n, source, target):
            for k, peer in enumerate(peers):
                trade(n, source, target, k + 1, peer).start()
            keep(n, source, target).start()

        def trade_finish(n, source, target):
            keep(n, source, target).wait()
            for k, peer in enumerate(peers):
                pltpu.make_async_copy(target.at[peer], target.at[peer], recv_sem.at[n, peer]).wait()
                trade(n, source, target, k + 1, peer).wait_send()

        @pl.when(step == 0)
        def _():
            greet([(me, peer) for peer in peers])
            trade_start(0, before_ref, first_in)

    @pl.when(step == 0)
    def _():
        turned_ref[...] = jnp.transpose(rows)
        out_ref[...] = jnp.zeros_like(out_ref)
        back_ref[...] = jnp.zeros_like(back_ref)

    w_gate, w_up, w_down = w_gate_ref[...], w_up_ref[...], w_down_ref[0]
    gate, up = nn(rows, w_gate), nn(rows, w_up)
    squashed = 1.0 / (1.0 + jnp.exp(-gate))
    silu = gate * squashed
    activated = (silu * up).astype(jnp.bfloat16)
    grad_act = nt(grads, w_down)
    grad_gate = (grad_act * up * (squashed * (1.0 + gate * (1.0 - squashed)))).astype(jnp.bfloat16)
    grad_up = (grad_act * silu).astype(jnp.bfloat16)
    out_ref[...] += nn(activated, w_down)
    grad_down_ref[...] = tn(activated, grads).astype(jnp.bfloat16)
    back_ref[...] += nt(grad_gate, w_gate) + nt(grad_up, w_up)
    grad_gu_ref[0] = nn(turned_ref[...], grad_gate).astype(jnp.bfloat16)
    grad_gu_ref[1] = nn(turned_ref[...], grad_up).astype(jnp.bfloat16)

    @pl.when(step == pl.num_programs(0) - 1)
    def _():
        shape = (both_ref.shape[0],) + both_ref.shape[2:]
        both_ref[:, 0] = out_ref[...].astype(jnp.bfloat16).reshape(shape)
        both_ref[:, 1] = back_ref[...].astype(jnp.bfloat16).reshape(shape)
        if dp_count:
            for hop in range(2, line.outer_count):
                line.relay(hop)
            line.finish()
        if linked:
            trade_start(1, both_ref, second_in)
            trade_finish(0, before_ref, first_in)
            trade_finish(1, both_ref, second_in)


def experts(arrived, arrived_grad, gate, up, down, at, before=None, shards=None, dp_count=0, collective=None):
    owners, _, cap, width = arrived.shape
    hidden = down.shape[1]
    count = owners * cap
    block = FF_BLOCK if count <= 1024 else FF_BLOCK // 4
    steps = hidden // block
    linked = before is not None
    pairs = pl.BlockSpec(
        (owners, 1, cap, width), lambda j: (0, at, 0, 0), pipeline_mode=pl.Buffered(1)
    )
    anywhere = pl.BlockSpec(memory_space=pl.ANY)
    both = jax.ShapeDtypeStruct((owners, 2, cap, width), jnp.bfloat16)
    gathers = shards is not None
    links = {"collective_id": collective, "has_side_effects": True} if linked or gathers else {}
    full = []
    if gathers:
        full = [jax.ShapeDtypeStruct((dp_count * shards.shape[1], hidden), jnp.bfloat16)]
    return pl.pallas_call(
        functools.partial(experts_kernel, linked, dp_count),
        grid=(steps,),
        out_shape=[
            jax.ShapeDtypeStruct((2, width, hidden), jnp.bfloat16),
            jax.ShapeDtypeStruct((hidden, width), jnp.bfloat16),
        ]
        + [both] * (2 if linked else 1)
        + full,
        in_specs=[
            pairs,
            pairs,
            pl.BlockSpec((width, block), lambda j: (0, j)),
            pl.BlockSpec((width, block), lambda j: (0, up.shape[1] // block - steps + j)),
            pl.BlockSpec((1, block, width), lambda j: (at, j, 0)),
        ]
        + [anywhere] * (linked + gathers),
        out_specs=[
            pl.BlockSpec((2, width, block), lambda j: (0, 0, j)),
            pl.BlockSpec((block, width), lambda j: (j, 0)),
        ]
        + ([anywhere] * 2 if linked else [pl.BlockSpec(both.shape, lambda j: (0, 0, 0, 0))])
        + [anywhere] * gathers,
        scratch_shapes=[
            pltpu.VMEM((width, count), jnp.bfloat16),
            pltpu.VMEM((count, width), jnp.float32),
            pltpu.VMEM((count, width), jnp.float32),
        ]
        + (
            [
                pltpu.VMEM(both.shape, jnp.bfloat16),
                pltpu.SemaphoreType.DMA((2, owners)),
                pltpu.SemaphoreType.DMA((2, owners)),
            ]
            if linked
            else []
        )
        + (gather_semaphores(dp_count) if gathers else []),
        compiler_params=pltpu.CompilerParams(
            dimension_semantics=("arbitrary",), vmem_limit_bytes=58 * 2**20, **links
        ),
        cost_estimate=pl.CostEstimate(
            flops=18 * count * width * hidden,
            bytes_accessed=12 * width * hidden + 8 * count * width,
            transcendentals=count * hidden,
        ),
        name="experts",
    )(
        arrived, arrived_grad, gate, up, down, *([before] if linked else []),
        *([shards] if gathers else []),
    )


def dp_grid(dp_count):
    outer = 4 if dp_count % 4 == 0 else 1
    return outer, dp_count // outer


def place():
    me, mine = lax.axis_index("dp"), lax.axis_index("expert")
    return me, mine


def greet(peers):
    barrier = pltpu.get_barrier_semaphore()
    for peer in peers:
        pl.semaphore_signal(barrier, inc=1, device_id=peer, device_id_type=MESH)
    pl.semaphore_wait(barrier, len(peers))


def small_gather_kernel(dp_count, shard_ref, full_ref, send_sem, pass_sem, recv_sem, mate_sem, own_sem):
    outer_count, inner_count = dp_grid(dp_count)
    me, mine = place()
    outer, inner = me // inner_count, me % inner_count
    rows, columns = shard_ref.shape
    half = columns // 2
    side = pl.multiple_of((mine % 2) * half, 128)
    mate = mine + 1 - 2 * (mine % 2)
    outer_peers = [lax.rem(outer + k, outer_count) for k in range(1, outer_count)]
    inner_peers = [lax.rem(inner + k, inner_count) for k in range(1, inner_count)]
    greet(
        [(peer * inner_count + inner, mine) for peer in outer_peers]
        + [(outer * inner_count + peer, mine) for peer in inner_peers]
        + [(me, mate)]
    )

    def spot(chunk):
        return full_ref.at[pl.ds(pl.multiple_of(chunk * rows, 8), rows), pl.ds(side, half)]

    sent = []

    def send(source, chunk, device, send_at, recv_at):
        copy = pltpu.make_async_remote_copy(
            src_ref=source,
            dst_ref=spot(chunk),
            send_sem=send_at,
            recv_sem=recv_at,
            device_id=device,
            device_id_type=MESH,
        )
        copy.start()
        sent.append(copy)

    def arrived(chunk):
        pltpu.make_async_copy(spot(chunk), spot(chunk), recv_sem.at[chunk]).wait()

    own_half = shard_ref.at[:, pl.ds(side, half)]
    for k, peer in enumerate(outer_peers):
        send(own_half, me, (peer * inner_count + inner, mine), send_sem.at[0, k], recv_sem.at[me])
    for k, peer in enumerate(inner_peers):
        send(own_half, me, (outer * inner_count + peer, mine), send_sem.at[1, k], recv_sem.at[me])
    own = pltpu.make_async_copy(
        shard_ref, full_ref.at[pl.ds(pl.multiple_of(me * rows, 8), rows), :], own_sem
    )
    own.start()
    chunks = []
    for k, peer in enumerate(outer_peers):
        chunk = peer * inner_count + inner
        arrived(chunk)
        for j, other in enumerate(inner_peers):
            send(spot(chunk), chunk, (outer * inner_count + other, mine), send_sem.at[2 + k, j], recv_sem.at[chunk])
        send(spot(chunk), chunk, (me, mate), pass_sem.at[len(chunks)], mate_sem.at[chunk])
        chunks.append(chunk)
    for other in inner_peers:
        for peer in [outer] + outer_peers:
            chunk = peer * inner_count + other
            arrived(chunk)
            send(spot(chunk), chunk, (me, mate), pass_sem.at[len(chunks)], mate_sem.at[chunk])
            chunks.append(chunk)
    own.wait()
    for chunk in chunks:
        there = full_ref.at[
            pl.ds(pl.multiple_of(chunk * rows, 8), rows), pl.ds(pl.multiple_of(half - side, 128), half)
        ]
        pltpu.make_async_copy(there, there, mate_sem.at[chunk]).wait()
    for copy in sent:
        copy.wait_send()


def small_gather(shard, dp_count, collective):
    outer_count, inner_count = dp_grid(dp_count)
    rows, columns = shard.shape
    lanes = max(outer_count, inner_count)
    return pl.pallas_call(
        functools.partial(small_gather_kernel, dp_count),
        out_shape=jax.ShapeDtypeStruct((dp_count * rows, columns), shard.dtype),
        in_specs=[pl.BlockSpec(memory_space=pl.ANY)],
        out_specs=pl.BlockSpec(memory_space=pl.ANY),
        scratch_shapes=[
            pltpu.SemaphoreType.DMA((outer_count + 1, lanes)),
            pltpu.SemaphoreType.DMA((dp_count,)),
            pltpu.SemaphoreType.DMA((dp_count,)),
            pltpu.SemaphoreType.DMA((dp_count,)),
            pltpu.SemaphoreType.DMA,
        ],
        compiler_params=pltpu.CompilerParams(collective_id=collective, has_side_effects=True),
        name="small_gather",
    )(shard)


def expert_gather_kernel(dp_count, tensor_count, cuts, crossed, owner_count, trade_count, *refs):
    given = tensor_count + trade_count
    shards, outgoing = refs[:tensor_count], refs[tensor_count:given]
    fulls, incoming = refs[given : given + tensor_count], refs[given + tensor_count : 2 * given]
    send_sem, recv_sem, own_sem, trade_send, trade_recv = refs[2 * given :]
    outer_count, inner_count = dp_grid(dp_count)
    me, mine = place()
    outer, inner = me // inner_count, me % inner_count
    below, above = lax.rem(outer + outer_count - 1, outer_count), lax.rem(outer + 1, outer_count)
    inner_peers = [lax.rem(inner + k, inner_count) for k in range(1, inner_count)]
    greet(
        [(peer * inner_count + inner, mine) for peer in (below, above)]
        + [(outer * inner_count + peer, mine) for peer in inner_peers]
        + [(me, lax.rem(mine + k, owner_count)) for k in range(1, owner_count) if trade_count]
    )
    trades = []
    for t in range(trade_count):
        for k in range(1, owner_count):
            peer = lax.rem(mine + k, owner_count)
            trade = pltpu.make_async_remote_copy(
                src_ref=outgoing[t].at[peer],
                dst_ref=incoming[t].at[mine],
                send_sem=trade_send.at[t, k],
                recv_sem=trade_recv.at[t, mine],
                device_id=(me, peer),
                device_id_type=MESH,
            )
            trade.start()
            trades.append(trade)
        keep = pltpu.make_async_copy(
            outgoing[t].at[mine], incoming[t].at[mine], trade_send.at[t, 0]
        )
        keep.start()
    pieces = [
        (t, e, c) for t in range(tensor_count) for e in range(shards[t].shape[0]) for c in range(cuts[t])
    ]

    def spot(p, chunk):
        t, e, c = pieces[p]
        rows = shards[t].shape[1]
        part = rows // cuts[t]
        return fulls[t].at[e, pl.ds(pl.multiple_of(chunk * rows + c * part, 8), part), :]

    def copy_of(p, source, chunk, device, send_at):
        return pltpu.make_async_remote_copy(
            src_ref=source,
            dst_ref=spot(p, chunk),
            send_sem=send_at,
            recv_sem=recv_sem.at[p, chunk],
            device_id=device,
            device_id_type=MESH,
        )

    def source_of(p):
        t, e, c = pieces[p]
        part = shards[t].shape[1] // cuts[t]
        return shards[t].at[e, pl.ds(c * part, part), :]

    def inner_sends(p, source, chunk):
        return [
            copy_of(p, source, chunk, (outer * inner_count + peer, mine), send_sem.at[p, 0, j, chunk])
            for j, peer in enumerate(inner_peers)
        ]

    def up(p, source, chunk):
        return copy_of(p, source, chunk, (above * inner_count + inner, mine), send_sem.at[p, 1, 0, chunk])

    def down(p, source, chunk):
        return copy_of(p, source, chunk, (below * inner_count + inner, mine), send_sem.at[p, 2, 0, chunk])

    def arrived(p, chunk):
        pltpu.make_async_copy(spot(p, chunk), spot(p, chunk), recv_sem.at[p, chunk]).wait()

    can_up, can_down = outer < outer_count - 1, outer > 0
    every = range(len(pieces))
    own = []
    for p in every:
        for copy in inner_sends(p, source_of(p), me):
            copy.start()
        pl.when(can_up)(lambda p=p: up(p, source_of(p), me).start())
        pl.when(can_down)(lambda p=p: down(p, source_of(p), me).start())
        copy = pltpu.make_async_copy(source_of(p), spot(p, me), own_sem.at[p])
        copy.start()
        own.append(copy)

    def passing(p, chunk, upward):
        arrived(p, chunk)
        if upward:
            pl.when(can_up)(lambda: up(p, spot(p, chunk), chunk).start())
        else:
            pl.when(can_down)(lambda: down(p, spot(p, chunk), chunk).start())

    for p in every:
        if p in crossed:
            for peer in inner_peers:
                chunk = outer * inner_count + peer
                arrived(p, chunk)
                pl.when(can_up)(lambda p=p, chunk=chunk: up(p, spot(p, chunk), chunk).start())
                pl.when(can_down)(lambda p=p, chunk=chunk: down(p, spot(p, chunk), chunk).start())
    for step in range(1, outer_count):
        low, high = outer - step, outer + step
        for p in every:
            for upward, there, source in ((True, low >= 0, low), (False, high < outer_count, high)):

                def relay(p=p, upward=upward, source=source):
                    chunk = source * inner_count + inner
                    passing(p, chunk, upward)
                    if p in crossed:
                        for peer in inner_peers:
                            passing(p, source * inner_count + peer, upward)
                    else:
                        for copy in inner_sends(p, spot(p, chunk), chunk):
                            copy.start()

                pl.when(there)(relay)
    for t in range(trade_count):
        pltpu.make_async_copy(
            outgoing[t].at[mine], incoming[t].at[mine], trade_send.at[t, 0]
        ).wait()
        for k in range(1, owner_count):
            there = incoming[t].at[lax.rem(mine + k, owner_count)]
            pltpu.make_async_copy(
                there, there, trade_recv.at[t, lax.rem(mine + k, owner_count)]
            ).wait()
    for trade in trades:
        trade.wait_send()
    for p in every:
        own[p].wait()
        if p not in crossed:
            for peer in inner_peers:
                for plane in range(outer_count):
                    arrived(p, plane * inner_count + peer)
        for copy in inner_sends(p, source_of(p), me):
            copy.wait_send()
        if p not in crossed:
            for k in range(1, outer_count):
                chunk = lax.rem(outer + k, outer_count) * inner_count + inner
                for copy in inner_sends(p, spot(p, chunk), chunk):
                    copy.wait_send()
        columns = range(inner_count) if p in crossed else [inner]
        for plane in range(outer_count):
            for column in columns:
                chunk = plane * inner_count + column
                pl.when(can_up & (outer >= plane))(lambda p=p, chunk=chunk: up(p, spot(p, chunk), chunk).wait_send())
                pl.when(can_down & (outer <= plane))(lambda p=p, chunk=chunk: down(p, spot(p, chunk), chunk).wait_send())


def expert_gather(shards, dp_count, collective, cuts=None, crossed=(), owner_count=1, trades=()):
    outer_count, inner_count = dp_grid(dp_count)
    cuts = cuts or [1] * len(shards)
    piece_count = sum(shard.shape[0] * cut for shard, cut in zip(shards, cuts))
    anywhere = pl.BlockSpec(memory_space=pl.ANY)
    given = len(shards) + len(trades)
    return pl.pallas_call(
        functools.partial(
            expert_gather_kernel, dp_count, len(shards), cuts, crossed, owner_count, len(trades)
        ),
        out_shape=[
            jax.ShapeDtypeStruct((s.shape[0], dp_count * s.shape[1], s.shape[2]), s.dtype)
            for s in shards
        ]
        + [jax.ShapeDtypeStruct(t.shape, t.dtype) for t in trades],
        in_specs=[anywhere] * given,
        out_specs=[anywhere] * given,
        scratch_shapes=[
            pltpu.SemaphoreType.DMA((piece_count, 3, max(1, inner_count - 1), dp_count)),
            pltpu.SemaphoreType.DMA((piece_count, dp_count)),
            pltpu.SemaphoreType.DMA((piece_count,)),
            pltpu.SemaphoreType.DMA((max(1, len(trades)), owner_count)),
            pltpu.SemaphoreType.DMA((max(1, len(trades)), owner_count)),
        ],
        compiler_params=pltpu.CompilerParams(collective_id=collective, has_side_effects=True),
        name="expert_gather",
    )(*shards, *trades)


class LineGather:
    def __init__(self, shard, full, dp_count, send_sem, recv_sem, own_sem):
        self.shard, self.full, self.dp_count = shard, full, dp_count
        self.send_sem, self.recv_sem, self.own_sem = send_sem, recv_sem, own_sem
        self.outer_count, self.inner_count = dp_grid(dp_count)
        self.me, self.mine = place()
        self.outer, self.inner = self.me // self.inner_count, self.me % self.inner_count
        self.inner_peers = [
            lax.rem(self.inner + k, self.inner_count) for k in range(1, self.inner_count)
        ]
        self.can_up, self.can_down = self.outer < self.outer_count - 1, self.outer > 0

    def peers(self):
        below = lax.rem(self.outer + self.outer_count - 1, self.outer_count)
        above = lax.rem(self.outer + 1, self.outer_count)
        return [(peer * self.inner_count + self.inner, self.mine) for peer in (below, above)] + [
            (self.outer * self.inner_count + peer, self.mine) for peer in self.inner_peers
        ]

    def spot(self, chunk):
        rows = self.shard.shape[0]
        return self.full.at[pl.ds(pl.multiple_of(chunk * rows, 8), rows), :]

    def copy(self, source, chunk, device, way, at):
        return pltpu.make_async_remote_copy(
            src_ref=source,
            dst_ref=self.spot(chunk),
            send_sem=self.send_sem.at[way, at, chunk],
            recv_sem=self.recv_sem.at[chunk],
            device_id=(device, self.mine),
            device_id_type=MESH,
        )

    def up(self, source, chunk):
        return self.copy(source, chunk, (self.outer + 1) * self.inner_count + self.inner, 1, 0)

    def down(self, source, chunk):
        return self.copy(source, chunk, (self.outer - 1) * self.inner_count + self.inner, 2, 0)

    def across(self, source, chunk):
        return [
            self.copy(source, chunk, self.outer * self.inner_count + peer, 0, at)
            for at, peer in enumerate(self.inner_peers)
        ]

    def keep(self):
        return pltpu.make_async_copy(self.shard, self.spot(self.me), self.own_sem)

    def arrived(self, chunk):
        pltpu.make_async_copy(self.spot(chunk), self.spot(chunk), self.recv_sem.at[chunk]).wait()

    def start(self):
        for copy in self.across(self.shard, self.me):
            copy.start()
        pl.when(self.can_up)(lambda: self.up(self.shard, self.me).start())
        pl.when(self.can_down)(lambda: self.down(self.shard, self.me).start())
        self.keep().start()

    def relay(self, step):
        low, high = self.outer - step, self.outer + step

        def pass_on(source, upward):
            chunk = source * self.inner_count + self.inner
            self.arrived(chunk)
            if upward:
                pl.when(self.can_up)(lambda: self.up(self.spot(chunk), chunk).start())
            else:
                pl.when(self.can_down)(lambda: self.down(self.spot(chunk), chunk).start())
            for copy in self.across(self.spot(chunk), chunk):
                copy.start()

        pl.when(low >= 0)(lambda: pass_on(low, True))
        pl.when(high < self.outer_count)(lambda: pass_on(high, False))

    def finish(self):
        self.keep().wait()
        for peer in self.inner_peers:
            for plane in range(self.outer_count):
                self.arrived(plane * self.inner_count + peer)
        for plane in range(self.outer_count):
            chunk = plane * self.inner_count + self.inner
            for copy in self.across(self.spot(chunk), chunk):
                copy.wait_send()
            pl.when(self.can_up & (self.outer >= plane))(
                lambda chunk=chunk: self.up(self.spot(chunk), chunk).wait_send()
            )
            pl.when(self.can_down & (self.outer <= plane))(
                lambda chunk=chunk: self.down(self.spot(chunk), chunk).wait_send()
            )


def gather_semaphores(dp_count):
    inner_count = dp_grid(dp_count)[1]
    return [
        pltpu.SemaphoreType.DMA((3, max(1, inner_count - 1), dp_count)),
        pltpu.SemaphoreType.DMA((dp_count,)),
        pltpu.SemaphoreType.DMA,
    ]


def by_rows(count, body):
    def step(i, carry):
        body(i * 16)
        return carry

    lax.fori_loop(0, count // 16, step, 0)


class LineReduce:
    def __init__(self, sources, totals, owns, ins, lows, highs, own_sem, in_send, in_recv, line_send, line_recv):
        self.sources, self.totals = sources, totals
        self.owns, self.ins, self.lows, self.highs = owns, ins, lows, highs
        self.own_sem, self.in_send, self.in_recv = own_sem, in_send, in_recv
        self.line_send, self.line_recv = line_send, line_recv
        self.me, self.mine = place()
        self.outer, self.inner = self.me // 2, self.me % 2
        self.every = range(len(sources))

    def peers(self):
        low, high = lax.rem(self.outer + 3, 4), lax.rem(self.outer + 1, 4)
        return [
            (self.me + 1 - 2 * self.inner, self.mine),
            (low * 2 + self.inner, self.mine),
            (high * 2 + self.inner, self.mine),
        ]

    def order(self, o):
        return sorted(range(4), key=lambda plane: (-abs(plane - o), plane))

    def chunk(self, p, at):
        source = self.sources[p]
        rows = self.owns[p].shape[-2]
        here = pl.ds(pl.multiple_of(at * rows, 16), rows)
        return source.at[:, here, :] if len(source.shape) == 3 else source.at[here, :]

    def own_copy(self, p, plane):
        return pltpu.make_async_copy(
            self.chunk(p, plane * 2 + self.inner), self.owns[p].at[plane], self.own_sem.at[p, plane]
        )

    def in_copy(self, p, plane):
        return pltpu.make_async_remote_copy(
            src_ref=self.chunk(p, plane * 2 + 1 - self.inner),
            dst_ref=self.ins[p].at[plane],
            send_sem=self.in_send.at[p, plane],
            recv_sem=self.in_recv.at[p, plane],
            device_id=(self.me + 1 - 2 * self.inner, self.mine),
            device_id_type=MESH,
        )

    def line_copy(self, p, plane, upward, device_plane):
        target = self.lows[p].at[plane - 1] if upward else self.highs[p].at[plane]
        return pltpu.make_async_remote_copy(
            src_ref=self.ins[p].at[plane],
            dst_ref=target,
            send_sem=self.line_send.at[p, 0 if upward else 1, plane],
            recv_sem=self.line_recv.at[p, 0 if upward else 1, plane],
            device_id=(device_plane * 2 + self.inner, self.mine),
            device_id_type=MESH,
        )

    def start(self, o):
        for plane in self.order(o):
            for p in self.every:
                self.in_copy(p, plane).start()
        for plane in self.order(o):
            for p in self.every:
                self.own_copy(p, plane).start()

    def line_start(self, o, p, plane):
        return self.line_copy(p, plane, plane > o, o + 1 if plane > o else o - 1)

    def pass_on(self, o, k):
        plane = self.order(o)[k]
        for p in self.every:
            self.own_copy(p, plane).wait()
            self.in_copy(p, plane).wait_recv()
            terms = [self.owns[p].at[plane]]
            if o > 0 and plane >= o:
                self.line_copy(p, plane, True, o).wait_recv()
                terms.append(self.lows[p].at[plane - 1])
            if o < 3 and plane <= o:
                self.line_copy(p, plane, False, o).wait_recv()
                terms.append(self.highs[p].at[plane])
            held = self.ins[p].at[plane]
            last = plane == o
            sides = held.shape[0] if len(held.shape) == 3 else 0

            def body(at, p=p, terms=terms, held=held, last=last, sides=sides):
                here = pl.ds(pl.multiple_of(at, 16), 16)
                for side in range(max(1, sides)):
                    spot = (side, here) if sides else (here,)
                    total = held[spot].astype(jnp.float32)
                    for term in terms:
                        total = total + term[spot].astype(jnp.float32)
                    if last:
                        size = total.shape[-1]
                        self.totals[p][here, side * size : (side + 1) * size] = total
                    else:
                        held[spot] = total.astype(held.dtype)

            by_rows(held.shape[-2], body)
            if not last:
                self.line_start(o, p, plane).start()

    def finish(self, o):
        for plane in range(4):
            for p in self.every:
                self.in_copy(p, plane).wait_send()
                if plane != o:
                    self.line_start(o, p, plane).wait_send()

    def each_plane(self, body):
        for o in range(4):
            pl.when(self.outer == o)(functools.partial(body, o))


def reduce_scratch(sources):
    shapes = []
    for planes in (4, 4, 3, 3):
        for source in sources:
            rows = source.shape[-2] // 8
            shapes.append(pltpu.VMEM((planes,) + source.shape[:-2] + (rows, source.shape[-1]), jnp.bfloat16))
    count = len(sources)
    return shapes + [
        pltpu.SemaphoreType.DMA((count, 4)),
        pltpu.SemaphoreType.DMA((count, 4)),
        pltpu.SemaphoreType.DMA((count, 4)),
        pltpu.SemaphoreType.DMA((count, 2, 4)),
        pltpu.SemaphoreType.DMA((count, 2, 4)),
    ]


def line_reduce(sources, totals, scratch):
    count = len(sources)
    buffers = [scratch[n * count : (n + 1) * count] for n in range(4)]
    return LineReduce(sources, totals, *buffers, *scratch[4 * count :])


def final_reduce_kernel(small_count, *refs):
    small_refs, refs = refs[:small_count], refs[small_count:]
    (
        small_out, swap, small_in, small_low, small_high, final_low, final_in,
        swap_send, swap_recv, in_send, in_recv, line_send, line_recv, last_send, last_recv,
    ) = refs
    outer_count, inner_count = 4, 2
    me, mine = place()
    outer, inner = me // inner_count, me % inner_count
    side = mine % 2
    mate, across = mine + 1 - 2 * side, lax.rem(mine + 2, 4)
    beside = me + 1 - 2 * inner
    half_rows = small_refs[0].shape[1] // 2
    starts = [sum(ref.shape[2] for ref in small_refs[:n]) for n in range(small_count + 1)]

    def remote(source, target, device, send_at, recv_at):
        return pltpu.make_async_remote_copy(
            src_ref=source,
            dst_ref=target,
            send_sem=send_at,
            recv_sem=recv_at,
            device_id=device,
            device_id_type=MESH,
        )

    low_peer = lax.rem(outer + outer_count - 1, outer_count) * inner_count + inner
    high_peer = lax.rem(outer + 1, outer_count) * inner_count + inner
    greet([(me, mate), (me, across), (beside, mine), (low_peer, mine), (high_peer, mine)])

    mate_rows = pl.ds(pl.multiple_of((1 - side) * half_rows, 16), half_rows)
    own_rows = pl.ds(pl.multiple_of(side * half_rows, 16), half_rows)

    def swap_copy(n):
        return remote(
            small_refs[n].at[:, mate_rows, :],
            swap.at[:, :, starts[n] : starts[n + 1]],
            (me, mate),
            swap_send.at[n],
            swap_recv.at[n],
        )

    def inner_copy(plane):
        return remote(
            swap.at[plane * inner_count + 1 - inner],
            small_in.at[plane],
            (beside, mine),
            in_send.at[plane],
            in_recv.at[plane],
        )

    def line_copy(plane, upward, device_plane):
        way = 0 if upward else 1
        return remote(
            small_in.at[plane],
            (small_low if upward else small_high).at[plane],
            (device_plane * inner_count + inner, mine),
            line_send.at[way, plane],
            line_recv.at[way, plane],
        )

    def wide(values):
        return values.astype(jnp.float32)

    def add_own(chunk):
        def body(at):
            here = pl.ds(pl.multiple_of(at, 16), 16)
            there = pl.ds(pl.multiple_of(side * half_rows + at, 16), 16)
            for n in range(small_count):
                columns = slice(starts[n], starts[n + 1])
                swap[chunk, here, columns] = (
                    wide(swap[chunk, here, columns]) + wide(small_refs[n][chunk, there, :])
                ).astype(swap.dtype)

        by_rows(half_rows, body)

    def at_plane(o):
        order = sorted(range(outer_count), key=lambda t: (-abs(t - o), t))

        def line_start(plane):
            return line_copy(plane, plane > o, o + 1 if plane > o else o - 1)

        for n in range(small_count):
            swap_copy(n).start()
        for n in range(small_count):
            swap_copy(n).wait_recv()
        for plane in order:
            add_own(plane * inner_count + 1 - inner)
            inner_copy(plane).start()
        for plane in order:
            add_own(plane * inner_count + inner)
            inner_copy(plane).wait_recv()
            terms = [swap.at[plane * inner_count + inner]]
            if o > 0 and plane >= o:
                line_copy(plane, True, o).wait_recv()
                terms.append(small_low.at[plane])
            if o < outer_count - 1 and plane <= o:
                line_copy(plane, False, o).wait_recv()
                terms.append(small_high.at[plane])
            target = final_low if plane == o else small_in.at[plane]

            def gather(at, plane=plane, terms=terms, target=target):
                here = pl.ds(pl.multiple_of(at, 16), 16)
                total = wide(small_in[plane, here, :])
                for term in terms:
                    total = total + wide(term[here, :])
                target[here, :] = total.astype(target.dtype)

            by_rows(half_rows, gather)
            if plane != o:
                line_start(plane).start()
        remote(final_low, final_in, (me, across), last_send.at[0], last_recv.at[0]).start()
        for plane in range(outer_count):
            inner_copy(plane).wait_send()
            if plane != o:
                line_start(plane).wait_send()
        for n in range(small_count):
            swap_copy(n).wait_send()

    for o in range(outer_count):
        pl.when(outer == o)(functools.partial(at_plane, o))
    remote(final_low, final_in, (me, across), last_send.at[0], last_recv.at[0]).wait()

    def total_body(at):
        here = pl.ds(pl.multiple_of(at, 16), 16)
        there = pl.ds(pl.multiple_of(side * half_rows + at, 16), 16)
        small_out[there, :] = wide(final_low[here, :]) + wide(final_in[here, :])

    by_rows(half_rows, total_body)
    mate_copy = remote(
        small_out.at[own_rows, :], small_out.at[own_rows, :], (me, mate), last_send.at[1], last_recv.at[1]
    )
    mate_copy.start()
    mate_copy.wait()


def final_reduce(smalls, collective):
    chunk_count, small_rows, _ = smalls[0].shape
    small_columns = sum(small.shape[2] for small in smalls)
    low = jnp.bfloat16
    planes = 4
    in_vmem = pl.BlockSpec(memory_space=pltpu.VMEM)
    half = small_rows // 2
    return pl.pallas_call(
        functools.partial(final_reduce_kernel, len(smalls)),
        out_shape=jax.ShapeDtypeStruct((small_rows, small_columns), jnp.float32),
        in_specs=[in_vmem] * len(smalls),
        out_specs=in_vmem,
        scratch_shapes=[pltpu.VMEM((chunk_count, half, small_columns), low)]
        + [pltpu.VMEM((planes, half, small_columns), low)] * 3
        + [pltpu.VMEM((half, small_columns), low)] * 2
        + [
            pltpu.SemaphoreType.DMA((len(smalls),)),
            pltpu.SemaphoreType.DMA((len(smalls),)),
            pltpu.SemaphoreType.DMA((planes,)),
            pltpu.SemaphoreType.DMA((planes,)),
            pltpu.SemaphoreType.DMA((2, planes)),
            pltpu.SemaphoreType.DMA((2, planes)),
            pltpu.SemaphoreType.DMA((2,)),
            pltpu.SemaphoreType.DMA((2,)),
        ],
        compiler_params=pltpu.CompilerParams(
            collective_id=collective, has_side_effects=True, vmem_limit_bytes=40 * 2**20
        ),
        name="final_reduce",
    )(*smalls)


def shards(
    tokens,
    resid_logits,
    routes,
    doc_ids,
    w_qkv,
    w_out,
    gain_attn,
    gain_ffn,
    w_router,
    w_const,
    v_const,
    w_gate_up,
    w_down,
    out_grad,
):
    dp_count, owner_count = lax.axis_size("dp"), lax.axis_size("expert")
    own_links = dp_count == 8 and owner_count == 4 and w_gate_up.shape[0] == 2
    seq_count, length, width = tokens.shape
    assert seq_count == 1
    rows = seq_count * length
    choice_count = resid_logits.shape[-1]
    local_count = w_gate_up.shape[0]
    expert_count = owner_count * local_count
    hidden_count = w_down.shape[1] * dp_count
    width_qkv, width_out = w_qkv.shape[1], w_out.shape[1]
    small_parts = [w_router, w_const, v_const, gain_attn[:, None], gain_ffn[:, None]]
    small_width = sum(part.shape[1] for part in small_parts)
    pad = jnp.zeros((w_qkv.shape[0], 256 - small_width), jnp.bfloat16)
    packed = jnp.concatenate([w_qkv, w_out] + small_parts + [pad], 1)
    inputs = tokens.reshape(rows, width)
    cot = out_grad.reshape(rows, width)
    route_rows = routes.reshape(rows, 2)
    spots, spot_rows = routing(route_rows, expert_count)
    cosine, sine = rotary_lanes(length, width // HEADS)
    docs_row, docs_column = doc_ids.reshape(1, rows), doc_ids.reshape(rows, 1)
    resid = jnp.pad(
        resid_logits.reshape(rows, choice_count).astype(jnp.float32), ((0, 0), (0, 128 - choice_count))
    )
    if own_links:
        packed_full = small_gather(packed, dp_count, 1)
    else:
        packed_full = lax.all_gather(packed, "dp", axis=0, tiled=True)
    attend = functools.partial(
        attention_forward, inputs, packed_full, docs_row, docs_column, cosine, sine, route_rows, resid
    )
    gather = functools.partial(lax.all_gather, axis_name="dp", axis=0, tiled=True)
    gates = [gather(w_gate_up[e]) for e in range(1 if own_links else local_count)]
    ups = list(gates)
    if own_links:
        ups.append(gather(w_gate_up[1, :, hidden_count:]))
    forward = attend()
    normed_one, queries, keys, values, attended, middle, normed_two, aux = forward
    send_rows, send_grads = dispatch(spot_rows, aux, normed_two, cot, expert_count * CAP)
    send_rows = send_rows.reshape(owner_count, local_count * CAP, width)
    send_grads = send_grads.reshape(owner_count, local_count * CAP, width)
    exchange = functools.partial(
        lax.all_to_all, axis_name="expert", split_axis=0, concat_axis=0, tiled=True
    )
    if own_links:
        down_full, arrived, arrived_grad = expert_gather(
            [w_down], dp_count, 2, owner_count=owner_count, trades=[send_rows, send_grads]
        )
    else:
        down_full = lax.all_gather(w_down, "dp", axis=1, tiled=True)
        arrived, arrived_grad = exchange(send_rows), exchange(send_grads)
    arrived = arrived.reshape(owner_count, local_count, CAP, width)
    arrived_grad = arrived_grad.reshape(owner_count, local_count, CAP, width)

    parts, gu_parts, down_parts, sources = [], [], [], []
    for e in range(local_count):
        run = functools.partial(experts, arrived, arrived_grad, gates[e], ups[e], down_full, e)
        if own_links and e == 0:
            grad_gu, grad_down, both, next_gate = run(
                shards=w_gate_up, dp_count=dp_count, collective=6
            )
            gates.append(next_gate)
        elif own_links:
            grad_gu, grad_down, *parts = run(before=both, collective=4)
        else:
            grad_gu, grad_down, both = run()
            parts.append(exchange(both))
        if own_links and e == local_count - 1:
            sources = [grad_gu, grad_down]
        else:
            down_parts.append(
                lax.psum_scatter(grad_down, "dp", scatter_dimension=0, tiled=True)
            )
            gu_part = lax.psum_scatter(grad_gu, "dp", scatter_dimension=1, tiled=True)
            gu_parts.append(jnp.concatenate([gu_part[0], gu_part[1]], -1).astype(jnp.float32))
    if own_links:
        parts, down_parts[0] = lax.optimization_barrier((parts, down_parts[0]))
    down_parts = [part.astype(jnp.float32) for part in down_parts]
    output, logit_grad, grad_middle, small_grad = combine(
        parts, spots, route_rows, aux, normed_two, middle, cot, packed_full, choice_count, expert_count
    )
    backward = functools.partial(
        attention_backward, grad_middle, queries, keys, values, attended, normed_one, inputs,
        packed_full, docs_row, docs_column, cosine, sine, small_grad,
    )
    if own_links:
        token_grad, *weight_grads, gu_part, down_part = backward(sources, 7)
        gu_parts.append(gu_part)
        down_parts.append(down_part)
        packed_part = final_reduce(
            [grad.reshape(dp_count, width // dp_count, grad.shape[1]) for grad in weight_grads], 3
        )
    else:
        token_grad, *weight_grads = backward()
        packed_part = lax.psum_scatter(
            jnp.concatenate(weight_grads, 1), "dp", scatter_dimension=0, tiled=True
        )
        packed_part = lax.psum(packed_part, "expert").astype(jnp.float32)
    part_qkv = packed_part[:, :width_qkv]
    part_out = packed_part[:, width_qkv : width_qkv + width_out]
    small_part = packed_part[:, width_qkv + width_out :]
    return (
        output.reshape(tokens.shape),
        token_grad.reshape(tokens.shape),
        logit_grad.reshape(resid_logits.shape),
        part_qkv,
        part_out,
        small_part[:, 18],
        small_part[:, 19],
        small_part[:, 0:12],
        small_part[:, 12:16],
        small_part[:, 16:18],
        jnp.stack(gu_parts),
        jnp.stack(down_parts),
    )


def solution(mesh):
    placed = (
        P(("dp", "expert"), None, None),
        P(("dp", "expert"), None, None),
        P(("dp", "expert"), None, None),
        P(("dp", "expert"), None),
        P("dp", None),
        P("dp", None),
        P("dp"),
        P("dp"),
        P("dp", None),
        P("dp", None),
        P("dp", None),
        P("expert", "dp", None),
        P("expert", "dp", None),
        P(("dp", "expert"), None, None),
    )
    return jax.shard_map(
        shards,
        mesh=mesh,
        in_specs=placed,
        out_specs=(
            P(("dp", "expert"), None, None),
            P(("dp", "expert"), None, None),
            P(("dp", "expert"), None, None),
            P("dp", None),
            P("dp", None),
            P("dp"),
            P("dp"),
            P("dp", None),
            P("dp", None),
            P("dp", None),
            P("expert", "dp", None),
            P("expert", "dp", None),
        ),
        check_vma=False,
    )
```

```python
import functools

import jax
import jax.numpy as jnp
import numpy as np
from jax import lax
from jax.experimental import pallas as pl
from jax.experimental.pallas import tpu as pltpu
from jax.sharding import PartitionSpec as P

HEADS = 12
BLOCK = 256
CAP = 256
GROUP = 256
FF_BLOCK = 512
MESH = pl.DeviceIdType.MESH
epsilon = 1e-06


def rotary_lanes(length, head_dim):
    half_dim = head_dim // 2
    frequency = (10000.0 ** (-np.arange(half_dim, dtype=np.float32) / half_dim)).astype(np.float32)
    angles = (np.arange(length, dtype=np.float32)[:, None] * frequency[None, :]).astype(np.float64)
    cosine = np.cos(angles).astype(np.float32)
    sine = np.sin(angles).astype(np.float32)
    return (
        np.concatenate([cosine] * 4, 1),
        np.concatenate([-sine, sine, -sine, sine], 1),
    )


def nt(left, right):
    return lax.dot_general(left, right, (((1,), (1,)), ((), ())), preferred_element_type=jnp.float32)


def tn(left, right):
    return lax.dot_general(left, right, (((0,), (0,)), ((), ())), preferred_element_type=jnp.float32)


def nn(left, right):
    return jnp.dot(left, right, preferred_element_type=jnp.float32)


def lane_ids(shape):
    return lax.broadcasted_iota(jnp.int32, shape, len(shape) - 1)


def turn(values, cosine, sine):
    lanes = lane_ids(values.shape)
    ahead, behind = pltpu.roll(values, 96, 1), pltpu.roll(values, 32, 1)
    return values * cosine + jnp.where(lanes % 64 < 32, ahead, behind) * sine


def key_span(i):
    return max(0, i - 2) * BLOCK, (i + 1) * BLOCK


def mask_of(docs_column, docs_row, i):
    low, high = key_span(i)
    return docs_column[low:high, :] == docs_row[:, i * BLOCK : (i + 1) * BLOCK]


def attention_forward_kernel(linked, *refs):
    (
        tokens_ref, wq_ref, wk_ref, wv_ref, wo_ref, small_ref, docs_row_ref, docs_column_ref,
        cosine_ref, sine_ref, routes_ref, resid_ref,
    ) = refs[:12]
    (
        normed_ref, q_ref, k_ref, v_ref, attended_ref, middle_ref, normed_two_ref, aux_ref,
    ) = refs[12 + bool(linked) : 20 + bool(linked)]
    step = pl.program_id(0)
    rows = tokens_ref.shape[0]
    if linked:
        branch_ref = refs[22]
        line = LineGather(refs[12].at[0], refs[21], linked, *refs[23:])

        @pl.when(step == 0)
        def _():
            greet(line.peers())
            line.start()

        @pl.when(step == 2)
        def _():
            line.relay(1)
    else:
        branch_ref = refs[20]

    @pl.when(step == 0)
    def _():
        inputs = tokens_ref[...].astype(jnp.float32)
        gains = jnp.transpose(small_ref[:, :128].astype(jnp.float32))[18:19, :]
        scale = lax.rsqrt(jnp.mean(inputs * inputs, -1, keepdims=True) + epsilon)
        normed_ref[...] = (inputs * scale * gains).astype(jnp.bfloat16)
        branch_ref[...] = jnp.zeros_like(branch_ref)

    normed = normed_ref[...]
    cosine, sine = cosine_ref[...], sine_ref[...]
    for w_ref, out_ref, turned in ((wq_ref, q_ref, True), (wk_ref, k_ref, True), (wv_ref, v_ref, False)):
        projected = nn(normed, w_ref[...])
        for half in range(2):
            part = projected[:, half * 128 : half * 128 + 128]
            if turned:
                part = turn(part, cosine, sine)
            out_ref[:, half * 128 : half * 128 + 128] = part.astype(jnp.bfloat16)

    docs_row, docs_column = docs_row_ref[...], docs_column_ref[...]
    for i in range(rows // BLOCK):
        low, high = key_span(i)
        here = slice(i * BLOCK, (i + 1) * BLOCK)
        allowed = mask_of(docs_column, docs_row, i)
        for pair in range(2):
            lanes = slice(pair * 128, pair * 128 + 128)
            queries = q_ref[here, lanes] * jnp.asarray(0.125, jnp.bfloat16)
            keys, values = k_ref[low:high, lanes], v_ref[low:high, lanes]
            left = lane_ids(queries.shape) < 64
            outs = []
            for head in range(2):
                own = left if head == 0 else jnp.logical_not(left)
                scores = nt(keys, jnp.where(own, queries, jnp.zeros_like(queries)))
                scores = jnp.where(allowed, scores, -1e30)
                shifted = jnp.exp(scores - jnp.max(scores, 0, keepdims=True))
                probs = shifted * (1.0 / jnp.sum(shifted, 0, keepdims=True))
                outs.append(tn(probs.astype(jnp.bfloat16), values))
            attended_ref[here, lanes] = jnp.where(left, outs[0], outs[1]).astype(jnp.bfloat16)
    branch_ref[...] += nn(attended_ref[...], wo_ref[...])

    @pl.when(step == pl.num_programs(0) - 1)
    def _():
        small = small_ref[:, :128]
        gains = jnp.transpose(small.astype(jnp.float32))[19:20, :]
        middle = tokens_ref[...].astype(jnp.float32) + branch_ref[...]
        middle_ref[...] = middle
        scale = lax.rsqrt(jnp.mean(middle * middle, -1, keepdims=True) + epsilon)
        normed_two = (middle * scale * gains).astype(jnp.bfloat16)
        normed_two_ref[...] = normed_two
        logits = nn(normed_two, small) + resid_ref[...].astype(jnp.float32)
        lanes = lane_ids(logits.shape)

        def lane(at):
            return jnp.sum(jnp.where(lanes == at, logits, 0.0), -1, keepdims=True)

        def two(first, second):
            peak = jnp.maximum(first, second)
            first, second = jnp.exp(first - peak), jnp.exp(second - peak)
            return first / (first + second), second / (first + second)

        columns = list(two(lane(routes_ref[:, 0:1]), lane(routes_ref[:, 1:2])))
        columns += list(two(lane(12), lane(13))) + list(two(lane(14), lane(15)))
        columns.append(scale)
        aux = jnp.zeros_like(logits)
        for at, column in enumerate(columns):
            aux = jnp.where(lanes == at, column, aux)
        aux_ref[...] = aux
        if linked:
            line.relay(2)
            line.relay(3)
            line.finish()


def attention_forward(
    tokens, packed, docs_row, docs_column, cosine, sine, routes, resid, shards=None,
    dp_count=None, collective=None,
):
    rows, width = tokens.shape
    groups = width // GROUP
    low = jnp.bfloat16
    whole = lambda shape: pl.BlockSpec(shape, lambda j: (0, 0))
    column = lambda at: pl.BlockSpec((width, GROUP), lambda j: (0, at + j))
    out_column = pl.BlockSpec((rows, GROUP), lambda j: (0, j))
    full = jax.ShapeDtypeStruct((rows, width), low)
    linked = shards is not None
    anywhere = pl.BlockSpec(memory_space=pl.ANY)
    links = {"collective_id": collective, "has_side_effects": True} if linked else {}
    gathered = []
    if linked:
        gathered = [jax.ShapeDtypeStruct((dp_count * shards.shape[1], shards.shape[2]), low)]
    return pl.pallas_call(
        functools.partial(attention_forward_kernel, dp_count if linked else 0),
        grid=(groups,),
        out_shape=[full] * 5
        + [
            jax.ShapeDtypeStruct((rows, width), jnp.float32),
            full,
            jax.ShapeDtypeStruct((rows, 128), jnp.float32),
        ]
        + gathered,
        in_specs=[
            whole((rows, width)),
            column(0),
            column(groups),
            column(2 * groups),
            pl.BlockSpec((GROUP, width), lambda j: (j, 3)),
            pl.BlockSpec((width, 256), lambda j: (0, 12)),
            whole((1, rows)),
            whole((rows, 1)),
            whole((rows, 128)),
            whole((rows, 128)),
            whole((rows, 2)),
            whole((rows, 128)),
        ]
        + [anywhere] * linked,
        out_specs=[whole((rows, width))]
        + [out_column] * 4
        + [whole((rows, width)), whole((rows, width)), whole((rows, 128))]
        + [anywhere] * linked,
        scratch_shapes=[pltpu.VMEM((rows, width), jnp.float32)]
        + (gather_semaphores(dp_count) if linked else []),
        compiler_params=pltpu.CompilerParams(
            dimension_semantics=("arbitrary",), vmem_limit_bytes=56 * 2**20, **links
        ),
        cost_estimate=pl.CostEstimate(
            flops=2 * rows * width * 4 * width + 8 * rows * rows * width // 2,
            bytes_accessed=24 * rows * width,
            transcendentals=rows * rows * HEADS // 2,
        ),
        name="attention_forward",
    )(
        tokens, packed, packed, packed, packed, packed, docs_row, docs_column, cosine, sine, routes,
        resid, *([shards] if linked else []),
    )


def attention_backward_kernel(count, *refs):
    (
        grad_middle_ref, q_ref, k_ref, v_ref, attended_ref, normed_ref, tokens_ref,
        wq_ref, wk_ref, wv_ref, wo_ref, small_ref, docs_row_ref, docs_column_ref,
        cosine_ref, sine_ref, small_grad_ref,
    ) = refs[:17]
    sources, refs = refs[17 : 17 + count], refs[17 + count :]
    token_grad_ref, gq_ref, gk_ref, gv_ref, go_ref, small_out_ref = refs[:6]
    totals, refs = refs[6 : 6 + count], refs[6 + count :]
    branch_ref, back_ref, turned_ref, key_acc, value_acc, query_acc = refs[:6]
    step = pl.program_id(0)
    rows, width = tokens_ref.shape
    if count:
        line = line_reduce(sources, totals, refs[6:])

        @pl.when(step == 0)
        def _():
            greet(line.peers())
            line.each_plane(line.start)

        @pl.when(step == 2)
        def _():
            line.each_plane(lambda o: line.pass_on(o, 0))

    @pl.when(step == 0)
    def _():
        branch_ref[...] = grad_middle_ref[...].astype(jnp.bfloat16)
        back_ref[...] = jnp.zeros_like(back_ref)

    grad_branch = branch_ref[...]
    grad_attended = nt(grad_branch, wo_ref[...]).astype(jnp.bfloat16)
    go_ref[...] = tn(attended_ref[...], grad_branch).astype(jnp.bfloat16)
    cosine, sine = cosine_ref[...], sine_ref[...]
    docs_row, docs_column = docs_row_ref[...], docs_column_ref[...]
    for pair in range(2):
        lanes = slice(pair * 128, pair * 128 + 128)
        key_acc[...] = jnp.zeros_like(key_acc)
        value_acc[...] = jnp.zeros_like(value_acc)
        for i in range(rows // BLOCK):
            low, high = key_span(i)
            here = slice(i * BLOCK, (i + 1) * BLOCK)
            allowed = mask_of(docs_column, docs_row, i)
            queries = q_ref[here, lanes] * jnp.asarray(0.125, jnp.bfloat16)
            grads = grad_attended[here, lanes]
            keys, values = k_ref[low:high, lanes], v_ref[low:high, lanes]
            left = lane_ids(queries.shape) < 64
            query_grads = []
            key_grad, value_grad = None, None
            for head in range(2):
                own = left if head == 0 else jnp.logical_not(left)
                own_queries = jnp.where(own, queries, jnp.zeros_like(queries))
                own_grads = jnp.where(own, grads, jnp.zeros_like(grads))
                scores = jnp.where(allowed, nt(keys, own_queries), -1e30)
                shifted = jnp.exp(scores - jnp.max(scores, 0, keepdims=True))
                probs = shifted * (1.0 / jnp.sum(shifted, 0, keepdims=True))
                grad_probs = nt(values, own_grads)
                inner = jnp.sum(probs * grad_probs, 0, keepdims=True)
                grad_scores = (probs * (grad_probs - inner)).astype(jnp.bfloat16)
                part_value = nn(probs.astype(jnp.bfloat16), own_grads)
                part_key = nn(grad_scores, own_queries)
                value_grad = part_value if head == 0 else value_grad + part_value
                key_grad = part_key if head == 0 else key_grad + part_key
                query_grads.append(tn(grad_scores, keys))
            value_acc[low:high, :] += value_grad
            key_acc[low:high, :] += key_grad
            query_acc[here, :] = jnp.where(left, query_grads[0], query_grads[1]) * 0.125
        turned_ref[0, :, lanes] = turn(query_acc[...], cosine, -sine).astype(jnp.bfloat16)
        turned_ref[1, :, lanes] = turn(key_acc[...], cosine, -sine).astype(jnp.bfloat16)
        turned_ref[2, :, lanes] = value_acc[...].astype(jnp.bfloat16)
    normed = normed_ref[...]
    for at, (w_ref, out_ref) in enumerate(((wq_ref, gq_ref), (wk_ref, gk_ref), (wv_ref, gv_ref))):
        turned = turned_ref[at]
        out_ref[...] = tn(normed, turned).astype(jnp.bfloat16)
        back_ref[...] += nt(turned, w_ref[...])

    @pl.when(step == pl.num_programs(0) - 1)
    def _():
        gains = jnp.transpose(small_ref[:, :128].astype(jnp.float32))[18:19, :]
        inputs = tokens_ref[...].astype(jnp.float32)
        grads = back_ref[...]
        scale = lax.rsqrt(jnp.mean(inputs * inputs, -1, keepdims=True) + epsilon)
        weighted = grads * gains
        mean = jnp.mean(weighted * inputs, -1, keepdims=True)
        grad_inputs = scale * weighted - inputs * (scale * scale * scale * mean)
        token_grad_ref[...] = (grad_inputs + grad_middle_ref[...]).astype(jnp.bfloat16)
        gain_grad = jnp.sum(grads * inputs * scale, 0, keepdims=True)
        column = jnp.transpose(jnp.broadcast_to(gain_grad, (128, width)))
        small_grad = small_grad_ref[...]
        small_grad = jnp.where(lane_ids(small_grad.shape) == 18, column, small_grad)
        small_out_ref[:, :128] = small_grad.astype(jnp.bfloat16)
        small_out_ref[:, 128:] = jnp.zeros((width, 128), jnp.bfloat16)
        if count:

            def rest(o):
                for k in range(1, 4):
                    line.pass_on(o, k)
                line.finish(o)

            line.each_plane(rest)


def attention_backward(
    grad_middle, queries, keys, values, attended, normed, tokens, packed, docs_row, docs_column,
    cosine, sine, small_grad, sources=(), collective=None,
):
    rows, width = tokens.shape
    groups = width // GROUP
    low = jnp.bfloat16
    whole = lambda shape: pl.BlockSpec(shape, lambda j: (0, 0))
    column = lambda at: pl.BlockSpec((width, GROUP), lambda j: (0, at + j))
    by_group = pl.BlockSpec((rows, GROUP), lambda j: (0, j))
    weight = jax.ShapeDtypeStruct((width, width), low)
    linked = len(sources) > 0
    links = {"collective_id": collective, "has_side_effects": True} if linked else {}
    sums = []
    for source in sources:
        sides = source.shape[0] if len(source.shape) == 3 else 1
        sums.append((source.shape[-2] // 8, sides * source.shape[-1]))
    once = lambda shape: pl.BlockSpec(
        shape, lambda j: (0, 0), pipeline_mode=pl.Buffered(1)
    )
    return pl.pallas_call(
        functools.partial(attention_backward_kernel, len(sources)),
        grid=(groups,),
        out_shape=[jax.ShapeDtypeStruct((rows, width), low)]
        + [weight] * 4
        + [jax.ShapeDtypeStruct((width, 256), low)]
        + [jax.ShapeDtypeStruct(shape, jnp.float32) for shape in sums],
        in_specs=[
            once((rows, width)),
            by_group,
            by_group,
            by_group,
            by_group,
            once((rows, width)),
            once((rows, width)),
            column(0),
            column(groups),
            column(2 * groups),
            pl.BlockSpec((GROUP, width), lambda j: (j, 3)),
            pl.BlockSpec((width, 256), lambda j: (0, 12)),
            once((1, rows)),
            once((rows, 1)),
            once((rows, 128)),
            once((rows, 128)),
            once((width, 128)),
        ]
        + [pl.BlockSpec(memory_space=pl.ANY)] * len(sources),
        out_specs=[
            whole((rows, width)),
            column(0),
            column(0),
            column(0),
            pl.BlockSpec((GROUP, width), lambda j: (j, 0)),
            whole((width, 256)),
        ]
        + [whole(shape) for shape in sums],
        scratch_shapes=[
            pltpu.VMEM((rows, width), low),
            pltpu.VMEM((rows, width), jnp.float32),
            pltpu.VMEM((3, rows, GROUP), low),
            pltpu.VMEM((rows, 128), jnp.float32),
            pltpu.VMEM((rows, 128), jnp.float32),
            pltpu.VMEM((rows, 128), jnp.float32),
        ]
        + (reduce_scratch(sources) if linked else []),
        compiler_params=pltpu.CompilerParams(
            dimension_semantics=("arbitrary",), vmem_limit_bytes=61 * 2**20, **links
        ),
        cost_estimate=pl.CostEstimate(
            flops=4 * rows * width * 4 * width + 20 * rows * rows * width // 2,
            bytes_accessed=32 * rows * width,
            transcendentals=rows * rows * HEADS // 2,
        ),
        name="attention_backward",
    )(
        grad_middle, queries, keys, values, attended, normed, tokens, packed, packed, packed,
        packed, packed, docs_row, docs_column, cosine, sine, small_grad, *sources,
    )


def routing_kernel(expert_count, routes_ref, columns_ref, rows_ref):
    rows = routes_ref.shape[0]
    lanes = lane_ids((rows, 128))
    first = (lanes == routes_ref[:, 0:1]).astype(jnp.float32)
    second = (lanes == routes_ref[:, 1:2]).astype(jnp.float32)
    down = lax.broadcasted_iota(jnp.int32, (rows, rows), 0)
    lower = (down > lane_ids((rows, rows))).astype(jnp.bfloat16)
    before_first = nn(lower, first.astype(jnp.bfloat16))
    before_second = nn(lower, second.astype(jnp.bfloat16)) + jnp.sum(first, 0, keepdims=True)
    spots = []
    for picked, before, at in ((first, before_first, 0), (second, before_second, 1)):
        rank = jnp.sum(picked * before, -1, keepdims=True)
        route = routes_ref[:, at : at + 1]
        spot = route.astype(jnp.float32) * CAP + rank
        spots.append(jnp.where(route < expert_count, spot, jnp.full_like(spot, 2.0 * expert_count * CAP)))
    both = jnp.where(lanes == 0, spots[0], jnp.where(lanes == 1, spots[1], 0.0))
    columns_ref[...] = both.astype(jnp.int32)
    rows_ref[...] = jnp.transpose(both)[0:8, :].astype(jnp.int32)


def routing(routes, expert_count):
    rows = routes.shape[0]
    return pl.pallas_call(
        functools.partial(routing_kernel, expert_count),
        out_shape=[
            jax.ShapeDtypeStruct((rows, 128), jnp.int32),
            jax.ShapeDtypeStruct((8, rows), jnp.int32),
        ],
        compiler_params=pltpu.CompilerParams(vmem_limit_bytes=40 * 2**20),
        name="routing",
    )(routes)


def dispatch_kernel(spots_ref, aux_ref, normed_ref, cot_ref, rows_ref, grads_ref, gates_ref):
    step = pl.program_id(0)

    @pl.when(step == 0)
    def _():
        gates_ref[...] = jnp.transpose(aux_ref[...])[0:8, :]

    shape = (rows_ref.shape[0], normed_ref.shape[0])
    slots = step * rows_ref.shape[0] + lax.broadcasted_iota(jnp.int32, shape, 0)
    first, second = slots == spots_ref[0:1, :], slots == spots_ref[1:2, :]
    gates = jnp.sum(
        jnp.where(first, gates_ref[0:1, :], jnp.where(second, gates_ref[1:2, :], 0.0)), -1, keepdims=True
    )
    chosen = jnp.where(first | second, 1.0, 0.0).astype(jnp.bfloat16)
    rows_ref[...] = nn(chosen, normed_ref[...]).astype(jnp.bfloat16)
    grads_ref[...] = (nn(chosen, cot_ref[...]) * gates).astype(jnp.bfloat16)


def dispatch(spots, aux, normed, cot, owner_count, local_count):
    rows, width = normed.shape
    slot_count = owner_count * local_count * CAP
    whole = lambda shape: pl.BlockSpec(shape, lambda j: (0, 0))
    block = pl.BlockSpec(
        (None, None, CAP, width), lambda j: (j % local_count, j // local_count, 0, 0)
    )
    return pl.pallas_call(
        dispatch_kernel,
        grid=(slot_count // CAP,),
        out_shape=[jax.ShapeDtypeStruct((local_count, owner_count, CAP, width), jnp.bfloat16)] * 2,
        in_specs=[whole((8, rows)), whole((rows, 128)), whole((rows, width)), whole((rows, width))],
        out_specs=[block, block],
        scratch_shapes=[pltpu.VMEM((8, rows), jnp.float32)],
        compiler_params=pltpu.CompilerParams(
            dimension_semantics=("arbitrary",), vmem_limit_bytes=60 * 2**20
        ),
        cost_estimate=pl.CostEstimate(
            flops=4 * slot_count * rows * width,
            bytes_accessed=4 * (rows + slot_count) * width,
            transcendentals=0,
        ),
        name="dispatch",
    )(spots, aux, normed, cot)


def halves(values):
    high = values.astype(jnp.bfloat16)
    return high, (values - high.astype(jnp.float32)).astype(jnp.bfloat16)


def combine_kernel(
    expert_count, local_count, *refs
):
    parts, refs = refs[:local_count], refs[local_count:]
    (
        spots_ref, routes_ref, aux_ref, normed_ref, middle_ref, cot_ref, small_ref,
        output_ref, logit_ref, grad_middle_ref, small_out_ref, vectors_ref, small_grad_ref,
    ) = refs
    step = pl.program_id(0)

    @pl.when(step == 0)
    def _():
        vectors_ref[0:8, :] = jnp.transpose(small_ref[:, :128].astype(jnp.float32))[16:24, :]
        vectors_ref[8:16, :] = jnp.zeros((8, vectors_ref.shape[1]), jnp.float32)
        small_grad_ref[...] = jnp.zeros_like(small_grad_ref)

    rows, width = normed_ref.shape
    normed_low, cot_low = normed_ref[...], cot_ref[...]
    normed, cot = normed_low.astype(jnp.float32), cot_low.astype(jnp.float32)
    total = lambda values: jnp.sum(values, -1, keepdims=True)
    picks, back = [0.0, 0.0], 0.0
    for e in range(local_count):
        count = parts[e].shape[0] * CAP
        slots = lane_ids((rows, count))
        slots = slots // CAP * (local_count * CAP) + e * CAP + slots % CAP
        hits = [slots == spots_ref[:, s : s + 1] for s in range(2)]
        chosen = [jnp.where(hit, 1.0, 0.0).astype(jnp.bfloat16) for hit in hits]
        returned = parts[e][:, 0].reshape(count, width)
        for s in range(2):
            picks[s] = picks[s] + nn(chosen[s], returned)
        back = back + nn(chosen[0] + chosen[1], parts[e][:, 1].reshape(count, width))
    inner = [total(pick * cot) for pick in picks]
    gates = [aux_ref[:, s : s + 1] for s in range(2)]
    routes = [routes_ref[:, s : s + 1] for s in range(2)]
    dot_copy = total(cot * normed)

    def weight_of(route):
        return sum(jnp.where(routes[s] == route, gates[s], 0.0) for s in range(2))

    copy_weight = weight_of(expert_count + 1)
    mix = gates[0] * picks[0] + gates[1] * picks[1]
    pass_weight = copy_weight
    gate_grads = [
        inner[s] + jnp.where(routes[s] == expert_count + 1, dot_copy, 0.0) for s in range(2)
    ]
    lanes = lane_ids((rows, 128))
    spread = jnp.zeros((rows, 128), jnp.float32)
    for k in range(2):
        vector = vectors_ref[k : k + 1, :]
        keep, blend = aux_ref[:, 2 + 2 * k : 3 + 2 * k], aux_ref[:, 3 + 2 * k : 4 + 2 * k]
        weight = weight_of(expert_count + 2 + k)
        dot_vector = total(cot * vector)
        pass_weight = pass_weight + weight * keep
        mix = mix + (weight * blend) * vector
        value = keep * dot_copy + blend * dot_vector
        for s in range(2):
            gate_grads[s] = gate_grads[s] + jnp.where(routes[s] == expert_count + 2 + k, value, 0.0)
        term = keep * blend * (weight * dot_copy - weight * dot_vector)
        spread = jnp.where(lanes == 12 + 2 * k, term, spread)
        spread = jnp.where(lanes == 13 + 2 * k, -term, spread)
        spread = jnp.where(lanes == 16 + k, weight * blend, spread)
    mix = mix + pass_weight * normed
    middle, scale = middle_ref[...], aux_ref[:, 6:7]
    output_ref[...] = (middle + mix).astype(jnp.bfloat16)
    mean = gates[0] * gate_grads[0] + gates[1] * gate_grads[1]
    for s in range(2):
        spread = jnp.where(lanes == routes[s], gates[s] * (gate_grads[s] - mean), spread)
    logit_ref[...] = spread[:, : logit_ref.shape[1]].astype(jnp.bfloat16)
    logits = jnp.where(lanes < 16, spread, 0.0)
    high, low = halves(logits)
    small = small_ref[:, :128]
    vector_high, vector_low = halves(spread - logits)
    small_grad_ref[...] += (
        tn(normed_low, high) + tn(normed_low, low) + tn(cot_low, vector_high) + tn(cot_low, vector_low)
    )
    grads = back + pass_weight * cot + nt(high, small) + nt(low, small)
    vectors_ref[8:9, :] += jnp.sum(grads * middle * scale, 0, keepdims=True)
    weighted = grads * vectors_ref[3:4, :]
    mean = jnp.mean(weighted * middle, -1, keepdims=True)
    grad_middle_ref[...] = cot + scale * weighted - middle * (scale * scale * scale * mean)

    @pl.when(step == pl.num_programs(0) - 1)
    def _():
        column = jnp.transpose(jnp.broadcast_to(vectors_ref[8:9, :], (128, width)))
        small_grad = small_grad_ref[...]
        small_out_ref[...] = jnp.where(lane_ids(small_grad.shape) == 19, column, small_grad)


def combine(parts, spots, routes, aux, normed, middle, cot, packed, choice_count, expert_count):
    rows, width = normed.shape
    local_count = len(parts)
    slot_count = expert_count * CAP
    size = 256
    block = lambda columns: pl.BlockSpec((size, columns), lambda j: (j, 0))
    whole = lambda shape: pl.BlockSpec(shape, lambda j: (0,) * len(shape))
    return pl.pallas_call(
        functools.partial(combine_kernel, expert_count, local_count),
        grid=(rows // size,),
        out_shape=[
            jax.ShapeDtypeStruct((rows, width), jnp.bfloat16),
            jax.ShapeDtypeStruct((rows, choice_count), jnp.bfloat16),
            jax.ShapeDtypeStruct((rows, width), jnp.float32),
            jax.ShapeDtypeStruct((width, 128), jnp.float32),
        ],
        in_specs=[whole(part.shape) for part in parts]
        + [
            block(128),
            block(2),
            block(128),
            block(width),
            block(width),
            block(width),
            pl.BlockSpec((width, 256), lambda j: (0, 12)),
        ],
        out_specs=[block(width), block(choice_count), block(width), whole((width, 128))],
        scratch_shapes=[pltpu.VMEM((16, width), jnp.float32), pltpu.VMEM((width, 128), jnp.float32)],
        compiler_params=pltpu.CompilerParams(
            dimension_semantics=("arbitrary",), vmem_limit_bytes=56 * 2**20
        ),
        cost_estimate=pl.CostEstimate(
            flops=6 * slot_count * rows * width,
            bytes_accessed=14 * rows * width + 4 * slot_count * width,
            transcendentals=0,
        ),
        name="combine",
    )(*parts, spots, routes, aux, normed, middle, cot, packed)


def experts_kernel(mode, dp_count, *refs):
    rows_ref, grads_ref, w_gate_ref, w_up_ref, w_down_ref = refs[:5]
    if mode == 0:
        grad_gu_ref, grad_down_ref, both_ref, turned_ref, out_ref, back_ref = refs[5:]
    if mode == 1:
        next_rows, next_grads, shards_ref, grad_gu_ref, grad_down_ref, both_ref = refs[5:11]
        rows_out, grads_out, full_ref, turned_ref, out_ref, back_ref = refs[11:17]
        sems = refs[17:]
    if mode == 2:
        before_ref, source_ref, grad_gu_ref, grad_down_ref, first_in, second_in, total_ref = refs[5:12]
        turned_ref, out_ref, back_ref, both_ref = refs[12:16]
        sems = refs[16:]
    step = pl.program_id(0)
    width = rows_ref.shape[-1]
    rows = rows_ref[...].reshape(-1, width)
    grads = grads_ref[...].reshape(-1, width)
    if mode == 1:
        line = LineGather(shards_ref.at[1], full_ref, dp_count, *sems[:3])
        trades = [
            Trade(next_rows.at[1], rows_out, *sems[3:5]),
            Trade(next_grads.at[1], grads_out, *sems[5:7]),
        ]

        @pl.when(step == 0)
        def _():
            greet(line.peers() + trades[0].peers())
            line.start()
            for trade in trades:
                trade.start()

        for hop in range(1, line.outer_count):
            pl.when(step == hop)(functools.partial(line.relay, hop))

    if mode == 2:
        trades = [Trade(before_ref, first_in, *sems[:2]), Trade(both_ref, second_in, *sems[2:4])]
        line = line_reduce([source_ref], [total_ref], sems[4:])

        @pl.when(step == 0)
        def _():
            greet(line.peers() + trades[0].peers())
            line.each_plane(line.start)
            trades[0].start()

        for hop in range(3):
            pl.when(step == hop + 1)(
                functools.partial(line.each_plane, functools.partial(line.pass_on, k=hop))
            )

    @pl.when(step == 0)
    def _():
        turned_ref[...] = jnp.transpose(rows)
        out_ref[...] = jnp.zeros_like(out_ref)
        back_ref[...] = jnp.zeros_like(back_ref)

    w_gate, w_up, w_down = w_gate_ref[...], w_up_ref[...], w_down_ref[...]
    gate, up = nn(rows, w_gate), nn(rows, w_up)
    squashed = 1.0 / (1.0 + jnp.exp(-gate))
    silu = gate * squashed
    activated = (silu * up).astype(jnp.bfloat16)
    grad_act = nt(grads, w_down)
    grad_gate = (grad_act * up * (squashed * (1.0 + gate * (1.0 - squashed)))).astype(jnp.bfloat16)
    grad_up = (grad_act * silu).astype(jnp.bfloat16)
    out_ref[...] += nn(activated, w_down)
    grad_down_ref[...] = tn(activated, grads).astype(jnp.bfloat16)
    back_ref[...] += nt(grad_gate, w_gate) + nt(grad_up, w_up)
    grad_gu_ref[0] = nn(turned_ref[...], grad_gate).astype(jnp.bfloat16)
    grad_gu_ref[1] = nn(turned_ref[...], grad_up).astype(jnp.bfloat16)

    @pl.when(step == pl.num_programs(0) - 1)
    def _():
        shape = (both_ref.shape[0],) + both_ref.shape[2:]
        both_ref[:, 0] = out_ref[...].astype(jnp.bfloat16).reshape(shape)
        both_ref[:, 1] = back_ref[...].astype(jnp.bfloat16).reshape(shape)
        if mode == 1:
            line.finish()
            for trade in trades:
                trade.finish()
        if mode == 2:
            trades[1].start()

            def rest(o):
                line.pass_on(o, 3)
                line.finish(o)

            line.each_plane(rest)
            for trade in trades:
                trade.finish()


def experts(rows, grads, gate, up, down, mode=0, dp_count=0, extras=(), collective=None):
    owners, cap, width = rows.shape
    hidden = down.shape[0]
    count = owners * cap
    block = FF_BLOCK if count <= 1024 else FF_BLOCK // 4
    steps = hidden // block
    low = jnp.bfloat16
    pairs = pl.BlockSpec((owners, cap, width), lambda j: (0, 0, 0), pipeline_mode=pl.Buffered(1))
    anywhere = pl.BlockSpec(memory_space=pl.ANY)
    both = jax.ShapeDtypeStruct((owners, 2, cap, width), low)
    links = {"collective_id": collective, "has_side_effects": True} if mode else {}
    out_shape = [
        jax.ShapeDtypeStruct((2, width, hidden), low),
        jax.ShapeDtypeStruct((hidden, width), low),
    ]
    out_specs = [
        pl.BlockSpec((2, width, block), lambda j: (0, 0, j)),
        pl.BlockSpec((block, width), lambda j: (j, 0)),
    ]
    scratch = [
        pltpu.VMEM((width, count), low),
        pltpu.VMEM((count, width), jnp.float32),
        pltpu.VMEM((count, width), jnp.float32),
    ]
    if mode < 2:
        out_shape.append(both)
        out_specs.append(pl.BlockSpec(both.shape, lambda j: (0, 0, 0, 0)))
    if mode == 1:
        shards = extras[2]
        out_shape += [jax.ShapeDtypeStruct(rows.shape, low)] * 2
        out_shape.append(jax.ShapeDtypeStruct((dp_count * shards.shape[1], shards.shape[2]), low))
        out_specs += [anywhere] * 3
        scratch += gather_semaphores(dp_count) + trade_semaphores(owners) + trade_semaphores(owners)
    if mode == 2:
        total = (hidden // 8, width)
        out_shape += [both, both, jax.ShapeDtypeStruct(total, jnp.float32)]
        out_specs += [anywhere] * 2 + [pl.BlockSpec(total, lambda j: (0, 0))]
        scratch.append(pltpu.VMEM(both.shape, low))
        scratch += trade_semaphores(owners) + trade_semaphores(owners) + reduce_scratch([extras[1]])
    return pl.pallas_call(
        functools.partial(experts_kernel, mode, dp_count),
        grid=(steps,),
        out_shape=out_shape,
        in_specs=[
            pairs,
            pairs,
            pl.BlockSpec((width, block), lambda j: (0, j)),
            pl.BlockSpec((width, block), lambda j: (0, up.shape[1] // block - steps + j)),
            pl.BlockSpec((block, width), lambda j: (j, 0)),
        ]
        + [anywhere] * len(extras),
        out_specs=out_specs,
        scratch_shapes=scratch,
        compiler_params=pltpu.CompilerParams(
            dimension_semantics=("arbitrary",), vmem_limit_bytes=60 * 2**20, **links
        ),
        cost_estimate=pl.CostEstimate(
            flops=18 * count * width * hidden,
            bytes_accessed=12 * width * hidden + 8 * count * width,
            transcendentals=count * hidden,
        ),
        name="experts",
    )(rows, grads, gate, up, down, *extras)


def dp_grid(dp_count):
    outer = 4 if dp_count % 4 == 0 else 1
    return outer, dp_count // outer


def place():
    me, mine = lax.axis_index("dp"), lax.axis_index("expert")
    return me, mine


def greet(peers):
    barrier = pltpu.get_barrier_semaphore()
    for peer in peers:
        pl.semaphore_signal(barrier, inc=1, device_id=peer, device_id_type=MESH)
    pl.semaphore_wait(barrier, len(peers))


def small_gather_kernel(dp_count, shard_ref, full_ref, send_sem, pass_sem, recv_sem, mate_sem, own_sem):
    outer_count, inner_count = dp_grid(dp_count)
    me, mine = place()
    outer, inner = me // inner_count, me % inner_count
    rows, columns = shard_ref.shape
    half = columns // 2
    side = pl.multiple_of((mine % 2) * half, 128)
    mate = mine + 1 - 2 * (mine % 2)
    outer_peers = [lax.rem(outer + k, outer_count) for k in range(1, outer_count)]
    inner_peers = [lax.rem(inner + k, inner_count) for k in range(1, inner_count)]
    greet(
        [(peer * inner_count + inner, mine) for peer in outer_peers]
        + [(outer * inner_count + peer, mine) for peer in inner_peers]
        + [(me, mate)]
    )

    def spot(chunk):
        return full_ref.at[pl.ds(pl.multiple_of(chunk * rows, 8), rows), pl.ds(side, half)]

    sent = []

    def send(source, chunk, device, send_at, recv_at):
        copy = pltpu.make_async_remote_copy(
            src_ref=source,
            dst_ref=spot(chunk),
            send_sem=send_at,
            recv_sem=recv_at,
            device_id=device,
            device_id_type=MESH,
        )
        copy.start()
        sent.append(copy)

    def arrived(chunk):
        pltpu.make_async_copy(spot(chunk), spot(chunk), recv_sem.at[chunk]).wait()

    own_half = shard_ref.at[:, pl.ds(side, half)]
    for k, peer in enumerate(outer_peers):
        send(own_half, me, (peer * inner_count + inner, mine), send_sem.at[0, k], recv_sem.at[me])
    for k, peer in enumerate(inner_peers):
        send(own_half, me, (outer * inner_count + peer, mine), send_sem.at[1, k], recv_sem.at[me])
    own = pltpu.make_async_copy(
        shard_ref, full_ref.at[pl.ds(pl.multiple_of(me * rows, 8), rows), :], own_sem
    )
    own.start()
    chunks = []
    for k, peer in enumerate(outer_peers):
        chunk = peer * inner_count + inner
        arrived(chunk)
        for j, other in enumerate(inner_peers):
            send(spot(chunk), chunk, (outer * inner_count + other, mine), send_sem.at[2 + k, j], recv_sem.at[chunk])
        send(spot(chunk), chunk, (me, mate), pass_sem.at[len(chunks)], mate_sem.at[chunk])
        chunks.append(chunk)
    for other in inner_peers:
        for peer in [outer] + outer_peers:
            chunk = peer * inner_count + other
            arrived(chunk)
            send(spot(chunk), chunk, (me, mate), pass_sem.at[len(chunks)], mate_sem.at[chunk])
            chunks.append(chunk)
    own.wait()
    for chunk in chunks:
        there = full_ref.at[
            pl.ds(pl.multiple_of(chunk * rows, 8), rows), pl.ds(pl.multiple_of(half - side, 128), half)
        ]
        pltpu.make_async_copy(there, there, mate_sem.at[chunk]).wait()
    for copy in sent:
        copy.wait_send()


def small_gather(shard, dp_count, collective):
    outer_count, inner_count = dp_grid(dp_count)
    rows, columns = shard.shape
    lanes = max(outer_count, inner_count)
    return pl.pallas_call(
        functools.partial(small_gather_kernel, dp_count),
        out_shape=jax.ShapeDtypeStruct((dp_count * rows, columns), shard.dtype),
        in_specs=[pl.BlockSpec(memory_space=pl.ANY)],
        out_specs=pl.BlockSpec(memory_space=pl.ANY),
        scratch_shapes=[
            pltpu.SemaphoreType.DMA((outer_count + 1, lanes)),
            pltpu.SemaphoreType.DMA((dp_count,)),
            pltpu.SemaphoreType.DMA((dp_count,)),
            pltpu.SemaphoreType.DMA((dp_count,)),
            pltpu.SemaphoreType.DMA,
        ],
        compiler_params=pltpu.CompilerParams(collective_id=collective, has_side_effects=True),
        name="small_gather",
    )(shard)


class LineGather:
    def __init__(self, shard, full, dp_count, send_sem, recv_sem, own_sem):
        self.shard, self.full, self.dp_count = shard, full, dp_count
        self.send_sem, self.recv_sem, self.own_sem = send_sem, recv_sem, own_sem
        self.outer_count, self.inner_count = dp_grid(dp_count)
        self.me, self.mine = place()
        self.outer, self.inner = self.me // self.inner_count, self.me % self.inner_count
        self.inner_peers = [
            lax.rem(self.inner + k, self.inner_count) for k in range(1, self.inner_count)
        ]
        self.can_up, self.can_down = self.outer < self.outer_count - 1, self.outer > 0

    def peers(self):
        below = lax.rem(self.outer + self.outer_count - 1, self.outer_count)
        above = lax.rem(self.outer + 1, self.outer_count)
        return [(peer * self.inner_count + self.inner, self.mine) for peer in (below, above)] + [
            (self.outer * self.inner_count + peer, self.mine) for peer in self.inner_peers
        ]

    def spot(self, chunk):
        rows = self.shard.shape[0]
        return self.full.at[pl.ds(pl.multiple_of(chunk * rows, 8), rows), :]

    def copy(self, source, chunk, device, way, at):
        return pltpu.make_async_remote_copy(
            src_ref=source,
            dst_ref=self.spot(chunk),
            send_sem=self.send_sem.at[way, at, chunk],
            recv_sem=self.recv_sem.at[chunk],
            device_id=(device, self.mine),
            device_id_type=MESH,
        )

    def up(self, source, chunk):
        return self.copy(source, chunk, (self.outer + 1) * self.inner_count + self.inner, 1, 0)

    def down(self, source, chunk):
        return self.copy(source, chunk, (self.outer - 1) * self.inner_count + self.inner, 2, 0)

    def across(self, source, chunk):
        return [
            self.copy(source, chunk, self.outer * self.inner_count + peer, 0, at)
            for at, peer in enumerate(self.inner_peers)
        ]

    def keep(self):
        return pltpu.make_async_copy(self.shard, self.spot(self.me), self.own_sem)

    def arrived(self, chunk):
        pltpu.make_async_copy(self.spot(chunk), self.spot(chunk), self.recv_sem.at[chunk]).wait()

    def start(self):
        for copy in self.across(self.shard, self.me):
            copy.start()
        pl.when(self.can_up)(lambda: self.up(self.shard, self.me).start())
        pl.when(self.can_down)(lambda: self.down(self.shard, self.me).start())
        self.keep().start()

    def relay(self, step):
        low, high = self.outer - step, self.outer + step

        def pass_on(source, upward):
            chunk = source * self.inner_count + self.inner
            self.arrived(chunk)
            if upward:
                pl.when(self.can_up)(lambda: self.up(self.spot(chunk), chunk).start())
            else:
                pl.when(self.can_down)(lambda: self.down(self.spot(chunk), chunk).start())
            for copy in self.across(self.spot(chunk), chunk):
                copy.start()

        pl.when(low >= 0)(lambda: pass_on(low, True))
        pl.when(high < self.outer_count)(lambda: pass_on(high, False))

    def finish(self):
        self.keep().wait()
        for peer in self.inner_peers:
            for plane in range(self.outer_count):
                self.arrived(plane * self.inner_count + peer)
        for plane in range(self.outer_count):
            chunk = plane * self.inner_count + self.inner
            for copy in self.across(self.spot(chunk), chunk):
                copy.wait_send()
            pl.when(self.can_up & (self.outer >= plane))(
                lambda chunk=chunk: self.up(self.spot(chunk), chunk).wait_send()
            )
            pl.when(self.can_down & (self.outer <= plane))(
                lambda chunk=chunk: self.down(self.spot(chunk), chunk).wait_send()
            )


def gather_semaphores(dp_count):
    inner_count = dp_grid(dp_count)[1]
    return [
        pltpu.SemaphoreType.DMA((3, max(1, inner_count - 1), dp_count)),
        pltpu.SemaphoreType.DMA((dp_count,)),
        pltpu.SemaphoreType.DMA,
    ]


def by_rows(count, body):
    def step(i, carry):
        body(i * 16)
        return carry

    lax.fori_loop(0, count // 16, step, 0)


class Trade:
    def __init__(self, source, target, send_sem, recv_sem):
        self.source, self.target, self.send_sem, self.recv_sem = source, target, send_sem, recv_sem
        self.me, self.mine = place()
        count = target.shape[0]
        self.partners = [lax.rem(self.mine + k, count) for k in range(1, count)]

    def peers(self):
        return [(self.me, peer) for peer in self.partners]

    def copy(self, k):
        peer = self.partners[k]
        return pltpu.make_async_remote_copy(
            src_ref=self.source.at[peer],
            dst_ref=self.target.at[self.mine],
            send_sem=self.send_sem.at[k + 1],
            recv_sem=self.recv_sem.at[self.mine],
            device_id=(self.me, peer),
            device_id_type=MESH,
        )

    def keep(self):
        return pltpu.make_async_copy(
            self.source.at[self.mine], self.target.at[self.mine], self.send_sem.at[0]
        )

    def start(self):
        for k in range(len(self.partners)):
            self.copy(k).start()
        self.keep().start()

    def finish(self):
        self.keep().wait()
        for k, peer in enumerate(self.partners):
            there = self.target.at[peer]
            pltpu.make_async_copy(there, there, self.recv_sem.at[peer]).wait()
            self.copy(k).wait_send()


def trade_semaphores(owner_count):
    return [pltpu.SemaphoreType.DMA((owner_count,)), pltpu.SemaphoreType.DMA((owner_count,))]


def expert_gather_kernel(dp_count, rows_ref, grads_ref, shards_ref, rows_out, grads_out, full_ref, *sems):
    line = LineGather(shards_ref.at[0], full_ref, dp_count, *sems[:3])
    trades = [Trade(rows_ref.at[0], rows_out, *sems[3:5]), Trade(grads_ref.at[0], grads_out, *sems[5:7])]
    greet(line.peers() + trades[0].peers())
    line.start()
    for trade in trades:
        trade.start()
    for hop in range(1, line.outer_count):
        line.relay(hop)
    line.finish()
    for trade in trades:
        trade.finish()


def expert_gather(rows, grads, shards, dp_count, collective):
    anywhere = pl.BlockSpec(memory_space=pl.ANY)
    return pl.pallas_call(
        functools.partial(expert_gather_kernel, dp_count),
        out_shape=[
            jax.ShapeDtypeStruct(rows.shape[1:], rows.dtype),
            jax.ShapeDtypeStruct(grads.shape[1:], grads.dtype),
            jax.ShapeDtypeStruct((dp_count * shards.shape[1], shards.shape[2]), shards.dtype),
        ],
        in_specs=[anywhere] * 3,
        out_specs=[anywhere] * 3,
        scratch_shapes=gather_semaphores(dp_count)
        + trade_semaphores(rows.shape[1])
        + trade_semaphores(rows.shape[1]),
        compiler_params=pltpu.CompilerParams(collective_id=collective, has_side_effects=True),
        name="expert_gather",
    )(rows, grads, shards)


class LineReduce:
    def __init__(self, sources, totals, owns, ins, lows, highs, own_sem, in_send, in_recv, line_send, line_recv):
        self.sources, self.totals = sources, totals
        self.owns, self.ins, self.lows, self.highs = owns, ins, lows, highs
        self.own_sem, self.in_send, self.in_recv = own_sem, in_send, in_recv
        self.line_send, self.line_recv = line_send, line_recv
        self.me, self.mine = place()
        self.outer, self.inner = self.me // 2, self.me % 2
        self.every = range(len(sources))

    def peers(self):
        low, high = lax.rem(self.outer + 3, 4), lax.rem(self.outer + 1, 4)
        return [
            (self.me + 1 - 2 * self.inner, self.mine),
            (low * 2 + self.inner, self.mine),
            (high * 2 + self.inner, self.mine),
        ]

    def order(self, o):
        return sorted(range(4), key=lambda plane: (-abs(plane - o), plane))

    def chunk(self, p, at):
        source = self.sources[p]
        rows = self.owns[p].shape[-2]
        here = pl.ds(pl.multiple_of(at * rows, 16), rows)
        return source.at[:, here, :] if len(source.shape) == 3 else source.at[here, :]

    def own_copy(self, p, plane):
        return pltpu.make_async_copy(
            self.chunk(p, plane * 2 + self.inner), self.owns[p].at[plane], self.own_sem.at[p, plane]
        )

    def in_copy(self, p, plane):
        return pltpu.make_async_remote_copy(
            src_ref=self.chunk(p, plane * 2 + 1 - self.inner),
            dst_ref=self.ins[p].at[plane],
            send_sem=self.in_send.at[p, plane],
            recv_sem=self.in_recv.at[p, plane],
            device_id=(self.me + 1 - 2 * self.inner, self.mine),
            device_id_type=MESH,
        )

    def line_copy(self, p, plane, upward, device_plane):
        target = self.lows[p].at[plane - 1] if upward else self.highs[p].at[plane]
        return pltpu.make_async_remote_copy(
            src_ref=self.ins[p].at[plane],
            dst_ref=target,
            send_sem=self.line_send.at[p, 0 if upward else 1, plane],
            recv_sem=self.line_recv.at[p, 0 if upward else 1, plane],
            device_id=(device_plane * 2 + self.inner, self.mine),
            device_id_type=MESH,
        )

    def start(self, o):
        for plane in self.order(o):
            for p in self.every:
                self.in_copy(p, plane).start()
        for plane in self.order(o):
            for p in self.every:
                self.own_copy(p, plane).start()

    def line_start(self, o, p, plane):
        return self.line_copy(p, plane, plane > o, o + 1 if plane > o else o - 1)

    def pass_on(self, o, k):
        plane = self.order(o)[k]
        for p in self.every:
            self.own_copy(p, plane).wait()
            self.in_copy(p, plane).wait_recv()
            terms = [self.owns[p].at[plane]]
            if o > 0 and plane >= o:
                self.line_copy(p, plane, True, o).wait_recv()
                terms.append(self.lows[p].at[plane - 1])
            if o < 3 and plane <= o:
                self.line_copy(p, plane, False, o).wait_recv()
                terms.append(self.highs[p].at[plane])
            held = self.ins[p].at[plane]
            last = plane == o
            sides = held.shape[0] if len(held.shape) == 3 else 0

            def body(at, p=p, terms=terms, held=held, last=last, sides=sides):
                here = pl.ds(pl.multiple_of(at, 16), 16)
                for side in range(max(1, sides)):
                    spot = (side, here) if sides else (here,)
                    total = held[spot].astype(jnp.float32)
                    for term in terms:
                        total = total + term[spot].astype(jnp.float32)
                    if last:
                        size = total.shape[-1]
                        self.totals[p][here, side * size : (side + 1) * size] = total
                    else:
                        held[spot] = total.astype(held.dtype)

            by_rows(held.shape[-2], body)
            if not last:
                self.line_start(o, p, plane).start()

    def finish(self, o):
        for plane in range(4):
            for p in self.every:
                self.in_copy(p, plane).wait_send()
                if plane != o:
                    self.line_start(o, p, plane).wait_send()

    def each_plane(self, body):
        for o in range(4):
            pl.when(self.outer == o)(functools.partial(body, o))


def reduce_scratch(sources):
    shapes = []
    for planes in (4, 4, 3, 3):
        for source in sources:
            rows = source.shape[-2] // 8
            shapes.append(pltpu.VMEM((planes,) + source.shape[:-2] + (rows, source.shape[-1]), jnp.bfloat16))
    count = len(sources)
    return shapes + [
        pltpu.SemaphoreType.DMA((count, 4)),
        pltpu.SemaphoreType.DMA((count, 4)),
        pltpu.SemaphoreType.DMA((count, 4)),
        pltpu.SemaphoreType.DMA((count, 2, 4)),
        pltpu.SemaphoreType.DMA((count, 2, 4)),
    ]


def line_reduce(sources, totals, scratch):
    count = len(sources)
    buffers = [scratch[n * count : (n + 1) * count] for n in range(4)]
    return LineReduce(sources, totals, *buffers, *scratch[4 * count :])


def final_reduce_kernel(small_count, *refs):
    small_refs, refs = refs[:small_count], refs[small_count:]
    (
        small_out, swap, small_in, small_low, small_high, final_low, final_in,
        swap_send, swap_recv, in_send, in_recv, line_send, line_recv, last_send, last_recv,
    ) = refs
    outer_count, inner_count = 4, 2
    me, mine = place()
    outer, inner = me // inner_count, me % inner_count
    side = mine % 2
    mate, across = mine + 1 - 2 * side, lax.rem(mine + 2, 4)
    beside = me + 1 - 2 * inner
    half_rows = small_refs[0].shape[1] // 2
    starts = [sum(ref.shape[2] for ref in small_refs[:n]) for n in range(small_count + 1)]

    def remote(source, target, device, send_at, recv_at):
        return pltpu.make_async_remote_copy(
            src_ref=source,
            dst_ref=target,
            send_sem=send_at,
            recv_sem=recv_at,
            device_id=device,
            device_id_type=MESH,
        )

    low_peer = lax.rem(outer + outer_count - 1, outer_count) * inner_count + inner
    high_peer = lax.rem(outer + 1, outer_count) * inner_count + inner
    greet([(me, mate), (me, across), (beside, mine), (low_peer, mine), (high_peer, mine)])

    mate_rows = pl.ds(pl.multiple_of((1 - side) * half_rows, 16), half_rows)
    own_rows = pl.ds(pl.multiple_of(side * half_rows, 16), half_rows)

    def swap_copy(n):
        return remote(
            small_refs[n].at[:, mate_rows, :],
            swap.at[:, :, starts[n] : starts[n + 1]],
            (me, mate),
            swap_send.at[n],
            swap_recv.at[n],
        )

    def inner_copy(plane):
        return remote(
            swap.at[plane * inner_count + 1 - inner],
            small_in.at[plane],
            (beside, mine),
            in_send.at[plane],
            in_recv.at[plane],
        )

    def line_copy(plane, upward, device_plane):
        way = 0 if upward else 1
        return remote(
            small_in.at[plane],
            (small_low if upward else small_high).at[plane],
            (device_plane * inner_count + inner, mine),
            line_send.at[way, plane],
            line_recv.at[way, plane],
        )

    def wide(values):
        return values.astype(jnp.float32)

    def add_own(chunk):
        def body(at):
            here = pl.ds(pl.multiple_of(at, 16), 16)
            there = pl.ds(pl.multiple_of(side * half_rows + at, 16), 16)
            for n in range(small_count):
                columns = slice(starts[n], starts[n + 1])
                swap[chunk, here, columns] = (
                    wide(swap[chunk, here, columns]) + wide(small_refs[n][chunk, there, :])
                ).astype(swap.dtype)

        by_rows(half_rows, body)

    def at_plane(o):
        order = sorted(range(outer_count), key=lambda t: (-abs(t - o), t))

        def line_start(plane):
            return line_copy(plane, plane > o, o + 1 if plane > o else o - 1)

        for n in range(small_count):
            swap_copy(n).start()
        for n in range(small_count):
            swap_copy(n).wait_recv()
        for plane in order:
            add_own(plane * inner_count + 1 - inner)
            inner_copy(plane).start()
        for plane in order:
            add_own(plane * inner_count + inner)
            inner_copy(plane).wait_recv()
            terms = [swap.at[plane * inner_count + inner]]
            if o > 0 and plane >= o:
                line_copy(plane, True, o).wait_recv()
                terms.append(small_low.at[plane])
            if o < outer_count - 1 and plane <= o:
                line_copy(plane, False, o).wait_recv()
                terms.append(small_high.at[plane])
            target = final_low if plane == o else small_in.at[plane]

            def gather(at, plane=plane, terms=terms, target=target):
                here = pl.ds(pl.multiple_of(at, 16), 16)
                total = wide(small_in[plane, here, :])
                for term in terms:
                    total = total + wide(term[here, :])
                target[here, :] = total.astype(target.dtype)

            by_rows(half_rows, gather)
            if plane != o:
                line_start(plane).start()
        remote(final_low, final_in, (me, across), last_send.at[0], last_recv.at[0]).start()
        for plane in range(outer_count):
            inner_copy(plane).wait_send()
            if plane != o:
                line_start(plane).wait_send()
        for n in range(small_count):
            swap_copy(n).wait_send()

    for o in range(outer_count):
        pl.when(outer == o)(functools.partial(at_plane, o))
    remote(final_low, final_in, (me, across), last_send.at[0], last_recv.at[0]).wait()

    def total_body(at):
        here = pl.ds(pl.multiple_of(at, 16), 16)
        there = pl.ds(pl.multiple_of(side * half_rows + at, 16), 16)
        small_out[there, :] = wide(final_low[here, :]) + wide(final_in[here, :])

    by_rows(half_rows, total_body)
    mate_copy = remote(
        small_out.at[own_rows, :], small_out.at[own_rows, :], (me, mate), last_send.at[1], last_recv.at[1]
    )
    mate_copy.start()
    mate_copy.wait()


def final_reduce(smalls, collective):
    chunk_count, small_rows, _ = smalls[0].shape
    small_columns = sum(small.shape[2] for small in smalls)
    low = jnp.bfloat16
    planes = 4
    in_vmem = pl.BlockSpec(memory_space=pltpu.VMEM)
    half = small_rows // 2
    return pl.pallas_call(
        functools.partial(final_reduce_kernel, len(smalls)),
        out_shape=jax.ShapeDtypeStruct((small_rows, small_columns), jnp.float32),
        in_specs=[in_vmem] * len(smalls),
        out_specs=in_vmem,
        scratch_shapes=[pltpu.VMEM((chunk_count, half, small_columns), low)]
        + [pltpu.VMEM((planes, half, small_columns), low)] * 3
        + [pltpu.VMEM((half, small_columns), low)] * 2
        + [
            pltpu.SemaphoreType.DMA((len(smalls),)),
            pltpu.SemaphoreType.DMA((len(smalls),)),
            pltpu.SemaphoreType.DMA((planes,)),
            pltpu.SemaphoreType.DMA((planes,)),
            pltpu.SemaphoreType.DMA((2, planes)),
            pltpu.SemaphoreType.DMA((2, planes)),
            pltpu.SemaphoreType.DMA((2,)),
            pltpu.SemaphoreType.DMA((2,)),
        ],
        compiler_params=pltpu.CompilerParams(
            collective_id=collective, has_side_effects=True, vmem_limit_bytes=40 * 2**20
        ),
        name="final_reduce",
    )(*smalls)


def shards(
    tokens,
    resid_logits,
    routes,
    doc_ids,
    w_qkv,
    w_out,
    gain_attn,
    gain_ffn,
    w_router,
    w_const,
    v_const,
    w_gate_up,
    w_down,
    out_grad,
):
    dp_count, owner_count = lax.axis_size("dp"), lax.axis_size("expert")
    own_links = dp_count == 8 and owner_count == 4 and w_gate_up.shape[0] == 2
    seq_count, length, width = tokens.shape
    assert seq_count == 1
    rows = seq_count * length
    choice_count = resid_logits.shape[-1]
    local_count = w_gate_up.shape[0]
    expert_count = owner_count * local_count
    hidden_count = w_down.shape[1] * dp_count
    width_qkv, width_out = w_qkv.shape[1], w_out.shape[1]
    small_parts = [w_router, w_const, v_const, gain_attn[:, None], gain_ffn[:, None]]
    small_width = sum(part.shape[1] for part in small_parts)
    pad = jnp.zeros((w_qkv.shape[0], 256 - small_width), jnp.bfloat16)
    packed = jnp.concatenate([w_qkv, w_out] + small_parts + [pad], 1)
    inputs = tokens.reshape(rows, width)
    cot = out_grad.reshape(rows, width)
    route_rows = routes.reshape(rows, 2)
    spots, spot_rows = routing(route_rows, expert_count)
    cosine, sine = rotary_lanes(length, width // HEADS)
    docs_row, docs_column = doc_ids.reshape(1, rows), doc_ids.reshape(rows, 1)
    resid = jnp.pad(
        resid_logits.reshape(rows, choice_count).astype(jnp.float32), ((0, 0), (0, 128 - choice_count))
    )
    if own_links:
        packed_full = small_gather(packed, dp_count, 1)
    else:
        packed_full = lax.all_gather(packed, "dp", axis=0, tiled=True)
    gather = functools.partial(lax.all_gather, axis_name="dp", axis=0, tiled=True)
    first_gate_up = gather(w_gate_up[0])
    if own_links:
        second_down = gather(w_down[1])
    normed_one, queries, keys, values, attended, middle, normed_two, aux = attention_forward(
        inputs, packed_full, docs_row, docs_column, cosine, sine, route_rows, resid
    )
    send_rows, send_grads = dispatch(spot_rows, aux, normed_two, cot, owner_count, local_count)
    if own_links:
        rows_in, grads_in, first_down = expert_gather(send_rows, send_grads, w_down, dp_count, 2)
        grad_gu, grad_down, both, next_rows, next_grads, second_gate_up = experts(
            rows_in, grads_in, first_gate_up, first_gate_up, first_down, 1, dp_count,
            [send_rows, send_grads, w_gate_up], 6,
        )
        gu_parts = [lax.psum_scatter(grad_gu, "dp", scatter_dimension=1, tiled=True)]
        second_gu, second_grad_down, *parts, down_part = experts(
            next_rows, next_grads, second_gate_up, second_gate_up, second_down, 2, dp_count,
            [both, grad_down], 4,
        )
        down_parts = [down_part]
    else:
        exchange = functools.partial(
            lax.all_to_all, axis_name="expert", split_axis=0, concat_axis=0, tiled=True
        )
        parts, gu_parts, down_parts = [], [], []
        for e in range(local_count):
            gate_up = first_gate_up if e == 0 else gather(w_gate_up[e])
            grad_gu, grad_down, both = experts(
                exchange(send_rows[e]), exchange(send_grads[e]), gate_up, gate_up, gather(w_down[e])
            )
            parts.append(exchange(both))
            gu_parts.append(lax.psum_scatter(grad_gu, "dp", scatter_dimension=1, tiled=True))
            down_parts.append(lax.psum_scatter(grad_down, "dp", scatter_dimension=0, tiled=True))
    gu_parts = [jnp.concatenate([part[0], part[1]], -1).astype(jnp.float32) for part in gu_parts]
    down_parts = [part.astype(jnp.float32) for part in down_parts]
    output, logit_grad, grad_middle, small_grad = combine(
        parts, spots, route_rows, aux, normed_two, middle, cot, packed_full, choice_count, expert_count
    )
    backward = functools.partial(
        attention_backward, grad_middle, queries, keys, values, attended, normed_one, inputs,
        packed_full, docs_row, docs_column, cosine, sine, small_grad,
    )
    if own_links:
        token_grad, *weight_grads, gu_part, down_part = backward([second_gu, second_grad_down], 7)
        gu_parts.append(gu_part)
        down_parts.append(down_part)
        packed_part = final_reduce(
            [grad.reshape(dp_count, width // dp_count, grad.shape[1]) for grad in weight_grads], 3
        )
    else:
        token_grad, *weight_grads = backward()
        packed_part = lax.psum_scatter(
            jnp.concatenate(weight_grads, 1), "dp", scatter_dimension=0, tiled=True
        )
        packed_part = lax.psum(packed_part, "expert").astype(jnp.float32)
    part_qkv = packed_part[:, :width_qkv]
    part_out = packed_part[:, width_qkv : width_qkv + width_out]
    small_part = packed_part[:, width_qkv + width_out :]
    return (
        output.reshape(tokens.shape),
        token_grad.reshape(tokens.shape),
        logit_grad.reshape(resid_logits.shape),
        part_qkv,
        part_out,
        small_part[:, 18],
        small_part[:, 19],
        small_part[:, 0:12],
        small_part[:, 12:16],
        small_part[:, 16:18],
        jnp.stack(gu_parts),
        jnp.stack(down_parts),
    )


def solution(mesh):
    placed = (
        P(("dp", "expert"), None, None),
        P(("dp", "expert"), None, None),
        P(("dp", "expert"), None, None),
        P(("dp", "expert"), None),
        P("dp", None),
        P("dp", None),
        P("dp"),
        P("dp"),
        P("dp", None),
        P("dp", None),
        P("dp", None),
        P("expert", "dp", None),
        P("expert", "dp", None),
        P(("dp", "expert"), None, None),
    )
    return jax.shard_map(
        shards,
        mesh=mesh,
        in_specs=placed,
        out_specs=(
            P(("dp", "expert"), None, None),
            P(("dp", "expert"), None, None),
            P(("dp", "expert"), None, None),
            P("dp", None),
            P("dp", None),
            P("dp"),
            P("dp"),
            P("dp", None),
            P("dp", None),
            P("dp", None),
            P("expert", "dp", None),
            P("expert", "dp", None),
        ),
        check_vma=False,
    )
```

```python
import functools

import jax
import jax.numpy as jnp
import numpy as np
from jax import lax
from jax.experimental import pallas as pl
from jax.experimental.pallas import tpu as pltpu
from jax.sharding import PartitionSpec as P

HEADS = 12
BLOCK = 256
CAP = 256
GROUP = 256
FF_BLOCK = 512
MESH = pl.DeviceIdType.MESH
epsilon = 1e-06


def rotary_lanes(length, head_dim):
    half_dim = head_dim // 2
    frequency = (10000.0 ** (-np.arange(half_dim, dtype=np.float32) / half_dim)).astype(np.float32)
    angles = (np.arange(length, dtype=np.float32)[:, None] * frequency[None, :]).astype(np.float64)
    cosine = np.cos(angles).astype(np.float32)
    sine = np.sin(angles).astype(np.float32)
    return (
        np.concatenate([cosine] * 4, 1),
        np.concatenate([-sine, sine, -sine, sine], 1),
    )


def nt(left, right):
    return lax.dot_general(left, right, (((1,), (1,)), ((), ())), preferred_element_type=jnp.float32)


def tn(left, right):
    return lax.dot_general(left, right, (((0,), (0,)), ((), ())), preferred_element_type=jnp.float32)


def nn(left, right):
    return jnp.dot(left, right, preferred_element_type=jnp.float32)


def lane_ids(shape):
    return lax.broadcasted_iota(jnp.int32, shape, len(shape) - 1)


def turn(values, cosine, sine):
    lanes = lane_ids(values.shape)
    ahead, behind = pltpu.roll(values, 96, 1), pltpu.roll(values, 32, 1)
    return values * cosine + jnp.where(lanes % 64 < 32, ahead, behind) * sine


def key_span(i):
    return max(0, i - 2) * BLOCK, (i + 1) * BLOCK


def mask_of(docs_column, docs_row, i):
    low, high = key_span(i)
    return docs_column[low:high, :] == docs_row[:, i * BLOCK : (i + 1) * BLOCK]


def attention_forward_kernel(linked, *refs):
    (
        tokens_ref, wq_ref, wk_ref, wv_ref, wo_ref, small_ref, docs_row_ref, docs_column_ref,
        cosine_ref, sine_ref, routes_ref, resid_ref,
    ) = refs[:12]
    (
        normed_ref, q_ref, k_ref, v_ref, attended_ref, middle_ref, normed_two_ref, aux_ref,
    ) = refs[12 + bool(linked) : 20 + bool(linked)]
    step = pl.program_id(0)
    rows = tokens_ref.shape[0]
    if linked:
        branch_ref = refs[22]
        line = LineGather(refs[12].at[0], refs[21], linked, *refs[23:])

        @pl.when(step == 0)
        def _():
            greet(line.peers())
            line.start()

        @pl.when(step == 2)
        def _():
            line.relay(1)
    else:
        branch_ref = refs[20]

    @pl.when(step == 0)
    def _():
        inputs = tokens_ref[...].astype(jnp.float32)
        gains = jnp.transpose(small_ref[:, :128].astype(jnp.float32))[18:19, :]
        scale = lax.rsqrt(jnp.mean(inputs * inputs, -1, keepdims=True) + epsilon)
        normed_ref[...] = (inputs * scale * gains).astype(jnp.bfloat16)
        branch_ref[...] = jnp.zeros_like(branch_ref)

    normed = normed_ref[...]
    cosine, sine = cosine_ref[...], sine_ref[...]
    for w_ref, out_ref, turned in ((wq_ref, q_ref, True), (wk_ref, k_ref, True), (wv_ref, v_ref, False)):
        projected = nn(normed, w_ref[...])
        for half in range(2):
            part = projected[:, half * 128 : half * 128 + 128]
            if turned:
                part = turn(part, cosine, sine)
            out_ref[:, half * 128 : half * 128 + 128] = part.astype(jnp.bfloat16)

    docs_row, docs_column = docs_row_ref[...], docs_column_ref[...]
    for i in range(rows // BLOCK):
        low, high = key_span(i)
        here = slice(i * BLOCK, (i + 1) * BLOCK)
        allowed = mask_of(docs_column, docs_row, i)
        for pair in range(2):
            lanes = slice(pair * 128, pair * 128 + 128)
            queries = q_ref[here, lanes] * jnp.asarray(0.125, jnp.bfloat16)
            keys, values = k_ref[low:high, lanes], v_ref[low:high, lanes]
            left = lane_ids(queries.shape) < 64
            outs = []
            for head in range(2):
                own = left if head == 0 else jnp.logical_not(left)
                scores = nt(keys, jnp.where(own, queries, jnp.zeros_like(queries)))
                scores = jnp.where(allowed, scores, -1e30)
                shifted = jnp.exp(scores - jnp.max(scores, 0, keepdims=True))
                probs = shifted * (1.0 / jnp.sum(shifted, 0, keepdims=True))
                outs.append(tn(probs.astype(jnp.bfloat16), values))
            attended_ref[here, lanes] = jnp.where(left, outs[0], outs[1]).astype(jnp.bfloat16)
    branch_ref[...] += nn(attended_ref[...], wo_ref[...])

    @pl.when(step == pl.num_programs(0) - 1)
    def _():
        small = small_ref[:, :128]
        gains = jnp.transpose(small.astype(jnp.float32))[19:20, :]
        middle = tokens_ref[...].astype(jnp.float32) + branch_ref[...]
        middle_ref[...] = middle
        scale = lax.rsqrt(jnp.mean(middle * middle, -1, keepdims=True) + epsilon)
        normed_two = (middle * scale * gains).astype(jnp.bfloat16)
        normed_two_ref[...] = normed_two
        logits = nn(normed_two, small) + resid_ref[...].astype(jnp.float32)
        lanes = lane_ids(logits.shape)

        def lane(at):
            return jnp.sum(jnp.where(lanes == at, logits, 0.0), -1, keepdims=True)

        def two(first, second):
            peak = jnp.maximum(first, second)
            first, second = jnp.exp(first - peak), jnp.exp(second - peak)
            return first / (first + second), second / (first + second)

        columns = list(two(lane(routes_ref[:, 0:1]), lane(routes_ref[:, 1:2])))
        columns += list(two(lane(12), lane(13))) + list(two(lane(14), lane(15)))
        columns.append(scale)
        aux = jnp.zeros_like(logits)
        for at, column in enumerate(columns):
            aux = jnp.where(lanes == at, column, aux)
        aux_ref[...] = aux
        if linked:
            line.relay(2)
            line.relay(3)
            line.finish()


def attention_forward(
    tokens, packed, docs_row, docs_column, cosine, sine, routes, resid, shards=None,
    dp_count=None, collective=None,
):
    rows, width = tokens.shape
    groups = width // GROUP
    low = jnp.bfloat16
    whole = lambda shape: pl.BlockSpec(shape, lambda j: (0, 0))
    column = lambda at: pl.BlockSpec((width, GROUP), lambda j: (0, at + j))
    out_column = pl.BlockSpec((rows, GROUP), lambda j: (0, j))
    full = jax.ShapeDtypeStruct((rows, width), low)
    linked = shards is not None
    anywhere = pl.BlockSpec(memory_space=pl.ANY)
    links = {"collective_id": collective, "has_side_effects": True} if linked else {}
    gathered = []
    if linked:
        gathered = [jax.ShapeDtypeStruct((dp_count * shards.shape[1], shards.shape[2]), low)]
    return pl.pallas_call(
        functools.partial(attention_forward_kernel, dp_count if linked else 0),
        grid=(groups,),
        out_shape=[full] * 5
        + [
            jax.ShapeDtypeStruct((rows, width), jnp.float32),
            full,
            jax.ShapeDtypeStruct((rows, 128), jnp.float32),
        ]
        + gathered,
        in_specs=[
            whole((rows, width)),
            column(0),
            column(groups),
            column(2 * groups),
            pl.BlockSpec((GROUP, width), lambda j: (j, 3)),
            pl.BlockSpec((width, 256), lambda j: (0, 12)),
            whole((1, rows)),
            whole((rows, 1)),
            whole((rows, 128)),
            whole((rows, 128)),
            whole((rows, 2)),
            whole((rows, 128)),
        ]
        + [anywhere] * linked,
        out_specs=[whole((rows, width))]
        + [out_column] * 4
        + [whole((rows, width)), whole((rows, width)), whole((rows, 128))]
        + [anywhere] * linked,
        scratch_shapes=[pltpu.VMEM((rows, width), jnp.float32)]
        + (gather_semaphores(dp_count) if linked else []),
        compiler_params=pltpu.CompilerParams(
            dimension_semantics=("arbitrary",), vmem_limit_bytes=56 * 2**20, **links
        ),
        cost_estimate=pl.CostEstimate(
            flops=2 * rows * width * 4 * width + 8 * rows * rows * width // 2,
            bytes_accessed=24 * rows * width,
            transcendentals=rows * rows * HEADS // 2,
        ),
        name="attention_forward",
    )(
        tokens, packed, packed, packed, packed, packed, docs_row, docs_column, cosine, sine, routes,
        resid, *([shards] if linked else []),
    )


def attention_backward_kernel(count, *refs):
    (
        grad_middle_ref, q_ref, k_ref, v_ref, attended_ref, normed_ref, tokens_ref,
        wq_ref, wk_ref, wv_ref, wo_ref, small_ref, docs_row_ref, docs_column_ref,
        cosine_ref, sine_ref, small_grad_ref,
    ) = refs[:17]
    sources, refs = refs[17 : 17 + count], refs[17 + count :]
    token_grad_ref, gq_ref, gk_ref, gv_ref, go_ref, small_out_ref = refs[:6]
    totals, refs = refs[6 : 6 + count], refs[6 + count :]
    branch_ref, back_ref, turned_ref, key_acc, value_acc, query_acc = refs[:6]
    step = pl.program_id(0)
    rows, width = tokens_ref.shape
    if count:
        line = line_reduce(sources, totals, refs[6:])

        @pl.when(step == 0)
        def _():
            greet(line.peers())
            line.each_plane(line.start)

        @pl.when(step == 2)
        def _():
            line.each_plane(lambda o: line.pass_on(o, 0))

    @pl.when(step == 0)
    def _():
        branch_ref[...] = grad_middle_ref[...].astype(jnp.bfloat16)
        back_ref[...] = jnp.zeros_like(back_ref)

    grad_branch = branch_ref[...]
    grad_attended = nt(grad_branch, wo_ref[...]).astype(jnp.bfloat16)
    go_ref[...] = tn(attended_ref[...], grad_branch).astype(jnp.bfloat16)
    cosine, sine = cosine_ref[...], sine_ref[...]
    docs_row, docs_column = docs_row_ref[...], docs_column_ref[...]
    for pair in range(2):
        lanes = slice(pair * 128, pair * 128 + 128)
        key_acc[...] = jnp.zeros_like(key_acc)
        value_acc[...] = jnp.zeros_like(value_acc)
        for i in range(rows // BLOCK):
            low, high = key_span(i)
            here = slice(i * BLOCK, (i + 1) * BLOCK)
            allowed = mask_of(docs_column, docs_row, i)
            queries = q_ref[here, lanes] * jnp.asarray(0.125, jnp.bfloat16)
            grads = grad_attended[here, lanes]
            keys, values = k_ref[low:high, lanes], v_ref[low:high, lanes]
            left = lane_ids(queries.shape) < 64
            query_grads = []
            key_grad, value_grad = None, None
            for head in range(2):
                own = left if head == 0 else jnp.logical_not(left)
                own_queries = jnp.where(own, queries, jnp.zeros_like(queries))
                own_grads = jnp.where(own, grads, jnp.zeros_like(grads))
                scores = jnp.where(allowed, nt(keys, own_queries), -1e30)
                shifted = jnp.exp(scores - jnp.max(scores, 0, keepdims=True))
                probs = shifted * (1.0 / jnp.sum(shifted, 0, keepdims=True))
                grad_probs = nt(values, own_grads)
                inner = jnp.sum(probs * grad_probs, 0, keepdims=True)
                grad_scores = (probs * (grad_probs - inner)).astype(jnp.bfloat16)
                part_value = nn(probs.astype(jnp.bfloat16), own_grads)
                part_key = nn(grad_scores, own_queries)
                value_grad = part_value if head == 0 else value_grad + part_value
                key_grad = part_key if head == 0 else key_grad + part_key
                query_grads.append(tn(grad_scores, keys))
            value_acc[low:high, :] += value_grad
            key_acc[low:high, :] += key_grad
            query_acc[here, :] = jnp.where(left, query_grads[0], query_grads[1]) * 0.125
        turned_ref[0, :, lanes] = turn(query_acc[...], cosine, -sine).astype(jnp.bfloat16)
        turned_ref[1, :, lanes] = turn(key_acc[...], cosine, -sine).astype(jnp.bfloat16)
        turned_ref[2, :, lanes] = value_acc[...].astype(jnp.bfloat16)
    normed = normed_ref[...]
    for at, (w_ref, out_ref) in enumerate(((wq_ref, gq_ref), (wk_ref, gk_ref), (wv_ref, gv_ref))):
        turned = turned_ref[at]
        out_ref[...] = tn(normed, turned).astype(jnp.bfloat16)
        back_ref[...] += nt(turned, w_ref[...])

    @pl.when(step == pl.num_programs(0) - 1)
    def _():
        gains = jnp.transpose(small_ref[:, :128].astype(jnp.float32))[18:19, :]
        inputs = tokens_ref[...].astype(jnp.float32)
        grads = back_ref[...]
        scale = lax.rsqrt(jnp.mean(inputs * inputs, -1, keepdims=True) + epsilon)
        weighted = grads * gains
        mean = jnp.mean(weighted * inputs, -1, keepdims=True)
        grad_inputs = scale * weighted - inputs * (scale * scale * scale * mean)
        token_grad_ref[...] = (grad_inputs + grad_middle_ref[...]).astype(jnp.bfloat16)
        gain_grad = jnp.sum(grads * inputs * scale, 0, keepdims=True)
        column = jnp.transpose(jnp.broadcast_to(gain_grad, (128, width)))
        small_grad = small_grad_ref[...]
        small_grad = jnp.where(lane_ids(small_grad.shape) == 18, column, small_grad)
        small_out_ref[:, :128] = small_grad.astype(jnp.bfloat16)
        small_out_ref[:, 128:] = jnp.zeros((width, 128), jnp.bfloat16)
        if count:

            def rest(o):
                for k in range(1, 4):
                    line.pass_on(o, k)
                line.finish(o)

            line.each_plane(rest)


def attention_backward(
    grad_middle, queries, keys, values, attended, normed, tokens, packed, docs_row, docs_column,
    cosine, sine, small_grad, sources=(), collective=None,
):
    rows, width = tokens.shape
    groups = width // GROUP
    low = jnp.bfloat16
    whole = lambda shape: pl.BlockSpec(shape, lambda j: (0, 0))
    column = lambda at: pl.BlockSpec((width, GROUP), lambda j: (0, at + j))
    by_group = pl.BlockSpec((rows, GROUP), lambda j: (0, j))
    weight = jax.ShapeDtypeStruct((width, width), low)
    linked = len(sources) > 0
    links = {"collective_id": collective, "has_side_effects": True} if linked else {}
    sums = []
    for source in sources:
        sides = source.shape[0] if len(source.shape) == 3 else 1
        sums.append((source.shape[-2] // 8, sides * source.shape[-1]))
    once = lambda shape: pl.BlockSpec(
        shape, lambda j: (0, 0), pipeline_mode=pl.Buffered(1)
    )
    return pl.pallas_call(
        functools.partial(attention_backward_kernel, len(sources)),
        grid=(groups,),
        out_shape=[jax.ShapeDtypeStruct((rows, width), low)]
        + [weight] * 4
        + [jax.ShapeDtypeStruct((width, 256), low)]
        + [jax.ShapeDtypeStruct(shape, jnp.float32) for shape in sums],
        in_specs=[
            once((rows, width)),
            by_group,
            by_group,
            by_group,
            by_group,
            once((rows, width)),
            once((rows, width)),
            column(0),
            column(groups),
            column(2 * groups),
            pl.BlockSpec((GROUP, width), lambda j: (j, 3)),
            pl.BlockSpec((width, 256), lambda j: (0, 12)),
            once((1, rows)),
            once((rows, 1)),
            once((rows, 128)),
            once((rows, 128)),
            once((width, 128)),
        ]
        + [pl.BlockSpec(memory_space=pl.ANY)] * len(sources),
        out_specs=[
            whole((rows, width)),
            column(0),
            column(0),
            column(0),
            pl.BlockSpec((GROUP, width), lambda j: (j, 0)),
            whole((width, 256)),
        ]
        + [whole(shape) for shape in sums],
        scratch_shapes=[
            pltpu.VMEM((rows, width), low),
            pltpu.VMEM((rows, width), jnp.float32),
            pltpu.VMEM((3, rows, GROUP), low),
            pltpu.VMEM((rows, 128), jnp.float32),
            pltpu.VMEM((rows, 128), jnp.float32),
            pltpu.VMEM((rows, 128), jnp.float32),
        ]
        + (reduce_scratch(sources) if linked else []),
        compiler_params=pltpu.CompilerParams(
            dimension_semantics=("arbitrary",), vmem_limit_bytes=61 * 2**20, **links
        ),
        cost_estimate=pl.CostEstimate(
            flops=4 * rows * width * 4 * width + 20 * rows * rows * width // 2,
            bytes_accessed=32 * rows * width,
            transcendentals=rows * rows * HEADS // 2,
        ),
        name="attention_backward",
    )(
        grad_middle, queries, keys, values, attended, normed, tokens, packed, packed, packed,
        packed, packed, docs_row, docs_column, cosine, sine, small_grad, *sources,
    )


def routing_kernel(expert_count, routes_ref, columns_ref, rows_ref):
    rows = routes_ref.shape[0]
    lanes = lane_ids((rows, 128))
    first = (lanes == routes_ref[:, 0:1]).astype(jnp.float32)
    second = (lanes == routes_ref[:, 1:2]).astype(jnp.float32)
    down = lax.broadcasted_iota(jnp.int32, (rows, rows), 0)
    lower = (down > lane_ids((rows, rows))).astype(jnp.bfloat16)
    before_first = nn(lower, first.astype(jnp.bfloat16))
    before_second = nn(lower, second.astype(jnp.bfloat16)) + jnp.sum(first, 0, keepdims=True)
    spots = []
    for picked, before, at in ((first, before_first, 0), (second, before_second, 1)):
        rank = jnp.sum(picked * before, -1, keepdims=True)
        route = routes_ref[:, at : at + 1]
        spot = route.astype(jnp.float32) * CAP + rank
        spots.append(jnp.where(route < expert_count, spot, jnp.full_like(spot, 2.0 * expert_count * CAP)))
    both = jnp.where(lanes == 0, spots[0], jnp.where(lanes == 1, spots[1], 0.0))
    columns_ref[...] = both.astype(jnp.int32)
    rows_ref[...] = jnp.transpose(both)[0:8, :].astype(jnp.int32)


def routing(routes, expert_count):
    rows = routes.shape[0]
    return pl.pallas_call(
        functools.partial(routing_kernel, expert_count),
        out_shape=[
            jax.ShapeDtypeStruct((rows, 128), jnp.int32),
            jax.ShapeDtypeStruct((8, rows), jnp.int32),
        ],
        compiler_params=pltpu.CompilerParams(vmem_limit_bytes=40 * 2**20),
        name="routing",
    )(routes)


def dispatch_kernel(spots_ref, aux_ref, normed_ref, cot_ref, rows_ref, grads_ref, gates_ref):
    step = pl.program_id(0)

    @pl.when(step == 0)
    def _():
        gates_ref[...] = jnp.transpose(aux_ref[...])[0:8, :]

    shape = (rows_ref.shape[0], normed_ref.shape[0])
    slots = step * rows_ref.shape[0] + lax.broadcasted_iota(jnp.int32, shape, 0)
    first, second = slots == spots_ref[0:1, :], slots == spots_ref[1:2, :]
    gates = jnp.sum(
        jnp.where(first, gates_ref[0:1, :], jnp.where(second, gates_ref[1:2, :], 0.0)), -1, keepdims=True
    )
    chosen = jnp.where(first | second, 1.0, 0.0).astype(jnp.bfloat16)
    rows_ref[...] = nn(chosen, normed_ref[...]).astype(jnp.bfloat16)
    grads_ref[...] = (nn(chosen, cot_ref[...]) * gates).astype(jnp.bfloat16)


def dispatch(spots, aux, normed, cot, owner_count, local_count):
    rows, width = normed.shape
    slot_count = owner_count * local_count * CAP
    whole = lambda shape: pl.BlockSpec(shape, lambda j: (0, 0))
    block = pl.BlockSpec(
        (None, None, CAP, width), lambda j: (j % local_count, j // local_count, 0, 0)
    )
    return pl.pallas_call(
        dispatch_kernel,
        grid=(slot_count // CAP,),
        out_shape=[jax.ShapeDtypeStruct((local_count, owner_count, CAP, width), jnp.bfloat16)] * 2,
        in_specs=[whole((8, rows)), whole((rows, 128)), whole((rows, width)), whole((rows, width))],
        out_specs=[block, block],
        scratch_shapes=[pltpu.VMEM((8, rows), jnp.float32)],
        compiler_params=pltpu.CompilerParams(
            dimension_semantics=("arbitrary",), vmem_limit_bytes=60 * 2**20
        ),
        cost_estimate=pl.CostEstimate(
            flops=4 * slot_count * rows * width,
            bytes_accessed=4 * (rows + slot_count) * width,
            transcendentals=0,
        ),
        name="dispatch",
    )(spots, aux, normed, cot)


def halves(values):
    high = values.astype(jnp.bfloat16)
    return high, (values - high.astype(jnp.float32)).astype(jnp.bfloat16)


def combine_kernel(
    expert_count, local_count, *refs
):
    parts, refs = refs[:local_count], refs[local_count:]
    (
        spots_ref, routes_ref, aux_ref, normed_ref, middle_ref, cot_ref, small_ref,
        output_ref, logit_ref, grad_middle_ref, small_out_ref, vectors_ref, small_grad_ref,
    ) = refs
    step = pl.program_id(0)

    @pl.when(step == 0)
    def _():
        vectors_ref[0:8, :] = jnp.transpose(small_ref[:, :128].astype(jnp.float32))[16:24, :]
        vectors_ref[8:16, :] = jnp.zeros((8, vectors_ref.shape[1]), jnp.float32)
        small_grad_ref[...] = jnp.zeros_like(small_grad_ref)

    rows, width = normed_ref.shape
    normed_low, cot_low = normed_ref[...], cot_ref[...]
    normed, cot = normed_low.astype(jnp.float32), cot_low.astype(jnp.float32)
    total = lambda values: jnp.sum(values, -1, keepdims=True)
    picks, back = [0.0, 0.0], 0.0
    for e in range(local_count):
        count = parts[e].shape[0] * CAP
        slots = lane_ids((rows, count))
        slots = slots // CAP * (local_count * CAP) + e * CAP + slots % CAP
        hits = [slots == spots_ref[:, s : s + 1] for s in range(2)]
        chosen = [jnp.where(hit, 1.0, 0.0).astype(jnp.bfloat16) for hit in hits]
        returned = parts[e][:, 0].reshape(count, width)
        for s in range(2):
            picks[s] = picks[s] + nn(chosen[s], returned)
        back = back + nn(chosen[0] + chosen[1], parts[e][:, 1].reshape(count, width))
    inner = [total(pick * cot) for pick in picks]
    gates = [aux_ref[:, s : s + 1] for s in range(2)]
    routes = [routes_ref[:, s : s + 1] for s in range(2)]
    dot_copy = total(cot * normed)

    def weight_of(route):
        return sum(jnp.where(routes[s] == route, gates[s], 0.0) for s in range(2))

    copy_weight = weight_of(expert_count + 1)
    mix = gates[0] * picks[0] + gates[1] * picks[1]
    pass_weight = copy_weight
    gate_grads = [
        inner[s] + jnp.where(routes[s] == expert_count + 1, dot_copy, 0.0) for s in range(2)
    ]
    lanes = lane_ids((rows, 128))
    spread = jnp.zeros((rows, 128), jnp.float32)
    for k in range(2):
        vector = vectors_ref[k : k + 1, :]
        keep, blend = aux_ref[:, 2 + 2 * k : 3 + 2 * k], aux_ref[:, 3 + 2 * k : 4 + 2 * k]
        weight = weight_of(expert_count + 2 + k)
        dot_vector = total(cot * vector)
        pass_weight = pass_weight + weight * keep
        mix = mix + (weight * blend) * vector
        value = keep * dot_copy + blend * dot_vector
        for s in range(2):
            gate_grads[s] = gate_grads[s] + jnp.where(routes[s] == expert_count + 2 + k, value, 0.0)
        term = keep * blend * (weight * dot_copy - weight * dot_vector)
        spread = jnp.where(lanes == 12 + 2 * k, term, spread)
        spread = jnp.where(lanes == 13 + 2 * k, -term, spread)
        spread = jnp.where(lanes == 16 + k, weight * blend, spread)
    mix = mix + pass_weight * normed
    middle, scale = middle_ref[...], aux_ref[:, 6:7]
    output_ref[...] = (middle + mix).astype(jnp.bfloat16)
    mean = gates[0] * gate_grads[0] + gates[1] * gate_grads[1]
    for s in range(2):
        spread = jnp.where(lanes == routes[s], gates[s] * (gate_grads[s] - mean), spread)
    logit_ref[...] = spread[:, : logit_ref.shape[1]].astype(jnp.bfloat16)
    logits = jnp.where(lanes < 16, spread, 0.0)
    high, low = halves(logits)
    small = small_ref[:, :128]
    vector_high, vector_low = halves(spread - logits)
    small_grad_ref[...] += (
        tn(normed_low, high) + tn(normed_low, low) + tn(cot_low, vector_high) + tn(cot_low, vector_low)
    )
    grads = back + pass_weight * cot + nt(high, small) + nt(low, small)
    vectors_ref[8:9, :] += jnp.sum(grads * middle * scale, 0, keepdims=True)
    weighted = grads * vectors_ref[3:4, :]
    mean = jnp.mean(weighted * middle, -1, keepdims=True)
    grad_middle_ref[...] = cot + scale * weighted - middle * (scale * scale * scale * mean)

    @pl.when(step == pl.num_programs(0) - 1)
    def _():
        column = jnp.transpose(jnp.broadcast_to(vectors_ref[8:9, :], (128, width)))
        small_grad = small_grad_ref[...]
        small_out_ref[...] = jnp.where(lane_ids(small_grad.shape) == 19, column, small_grad)


def combine(parts, spots, routes, aux, normed, middle, cot, packed, choice_count, expert_count):
    rows, width = normed.shape
    local_count = len(parts)
    slot_count = expert_count * CAP
    size = 256
    block = lambda columns: pl.BlockSpec((size, columns), lambda j: (j, 0))
    whole = lambda shape: pl.BlockSpec(shape, lambda j: (0,) * len(shape))
    return pl.pallas_call(
        functools.partial(combine_kernel, expert_count, local_count),
        grid=(rows // size,),
        out_shape=[
            jax.ShapeDtypeStruct((rows, width), jnp.bfloat16),
            jax.ShapeDtypeStruct((rows, choice_count), jnp.bfloat16),
            jax.ShapeDtypeStruct((rows, width), jnp.float32),
            jax.ShapeDtypeStruct((width, 128), jnp.float32),
        ],
        in_specs=[whole(part.shape) for part in parts]
        + [
            block(128),
            block(2),
            block(128),
            block(width),
            block(width),
            block(width),
            pl.BlockSpec((width, 256), lambda j: (0, 12)),
        ],
        out_specs=[block(width), block(choice_count), block(width), whole((width, 128))],
        scratch_shapes=[pltpu.VMEM((16, width), jnp.float32), pltpu.VMEM((width, 128), jnp.float32)],
        compiler_params=pltpu.CompilerParams(
            dimension_semantics=("arbitrary",), vmem_limit_bytes=56 * 2**20
        ),
        cost_estimate=pl.CostEstimate(
            flops=6 * slot_count * rows * width,
            bytes_accessed=14 * rows * width + 4 * slot_count * width,
            transcendentals=0,
        ),
        name="combine",
    )(*parts, spots, routes, aux, normed, middle, cot, packed)


def experts_kernel(mode, dp_count, *refs):
    rows_ref, grads_ref, w_gate_ref, w_up_ref, w_down_ref = refs[:5]
    if mode == 0:
        grad_gu_ref, grad_down_ref, both_ref, turned_ref, out_ref, back_ref = refs[5:]
    if mode == 1:
        next_rows, next_grads, shards_ref, grad_gu_ref, grad_down_ref, both_ref = refs[5:11]
        rows_out, grads_out, full_ref, turned_ref, out_ref, back_ref = refs[11:17]
        sems = refs[17:]
    if mode == 2:
        before_ref, source_ref, grad_gu_ref, grad_down_ref, first_in, second_in, total_ref = refs[5:12]
        turned_ref, out_ref, back_ref, both_ref = refs[12:16]
        sems = refs[16:]
    step = pl.program_id(0)
    width = rows_ref.shape[-1]
    rows = rows_ref[...].reshape(-1, width)
    grads = grads_ref[...].reshape(-1, width)
    if mode == 1:
        line = LineGather(shards_ref.at[1], full_ref, dp_count, *sems[:3])
        trades = [
            Trade(next_rows.at[1], rows_out, *sems[3:5]),
            Trade(next_grads.at[1], grads_out, *sems[5:7]),
        ]

        @pl.when(step == 0)
        def _():
            greet(line.peers() + trades[0].peers())
            line.start()
            for trade in trades:
                trade.start()

        for hop in range(1, line.outer_count):
            pl.when(step == hop)(functools.partial(line.relay, hop))

    if mode == 2:
        trades = [Trade(before_ref, first_in, *sems[:2]), Trade(both_ref, second_in, *sems[2:4])]
        line = line_reduce([source_ref], [total_ref], sems[4:])

        @pl.when(step == 0)
        def _():
            greet(line.peers() + trades[0].peers())
            line.each_plane(line.start)
            trades[0].start()

        for hop in range(3):
            pl.when(step == hop + 1)(
                functools.partial(line.each_plane, functools.partial(line.pass_on, k=hop))
            )

    @pl.when(step == 0)
    def _():
        turned_ref[...] = jnp.transpose(rows)
        out_ref[...] = jnp.zeros_like(out_ref)
        back_ref[...] = jnp.zeros_like(back_ref)

    w_gate, w_up, w_down = w_gate_ref[...], w_up_ref[...], w_down_ref[...]
    gate, up = nn(rows, w_gate), nn(rows, w_up)
    squashed = 1.0 / (1.0 + jnp.exp(-gate))
    silu = gate * squashed
    activated = (silu * up).astype(jnp.bfloat16)
    grad_act = nt(grads, w_down)
    grad_gate = (grad_act * up * (squashed * (1.0 + gate * (1.0 - squashed)))).astype(jnp.bfloat16)
    grad_up = (grad_act * silu).astype(jnp.bfloat16)
    out_ref[...] += nn(activated, w_down)
    grad_down_ref[...] = tn(activated, grads).astype(jnp.bfloat16)
    back_ref[...] += nt(grad_gate, w_gate) + nt(grad_up, w_up)
    grad_gu_ref[0] = nn(turned_ref[...], grad_gate).astype(jnp.bfloat16)
    grad_gu_ref[1] = nn(turned_ref[...], grad_up).astype(jnp.bfloat16)

    @pl.when(step == pl.num_programs(0) - 1)
    def _():
        shape = (both_ref.shape[0],) + both_ref.shape[2:]
        both_ref[:, 0] = out_ref[...].astype(jnp.bfloat16).reshape(shape)
        both_ref[:, 1] = back_ref[...].astype(jnp.bfloat16).reshape(shape)
        if mode == 1:
            line.finish()
            for trade in trades:
                trade.finish()
        if mode == 2:
            trades[1].start()

            def rest(o):
                line.pass_on(o, 3)
                line.finish(o)

            line.each_plane(rest)
            for trade in trades:
                trade.finish()


def experts(rows, grads, gate, up, down, mode=0, dp_count=0, extras=(), collective=None):
    owners, cap, width = rows.shape
    hidden = down.shape[0]
    count = owners * cap
    block = FF_BLOCK if count <= 1024 else FF_BLOCK // 4
    steps = hidden // block
    low = jnp.bfloat16
    pairs = pl.BlockSpec((owners, cap, width), lambda j: (0, 0, 0), pipeline_mode=pl.Buffered(1))
    anywhere = pl.BlockSpec(memory_space=pl.ANY)
    both = jax.ShapeDtypeStruct((owners, 2, cap, width), low)
    links = {"collective_id": collective, "has_side_effects": True} if mode else {}
    out_shape = [
        jax.ShapeDtypeStruct((2, width, hidden), low),
        jax.ShapeDtypeStruct((hidden, width), low),
    ]
    out_specs = [
        pl.BlockSpec((2, width, block), lambda j: (0, 0, j)),
        pl.BlockSpec((block, width), lambda j: (j, 0)),
    ]
    scratch = [
        pltpu.VMEM((width, count), low),
        pltpu.VMEM((count, width), jnp.float32),
        pltpu.VMEM((count, width), jnp.float32),
    ]
    if mode < 2:
        out_shape.append(both)
        out_specs.append(pl.BlockSpec(both.shape, lambda j: (0, 0, 0, 0)))
    if mode == 1:
        shards = extras[2]
        out_shape += [jax.ShapeDtypeStruct(rows.shape, low)] * 2
        out_shape.append(jax.ShapeDtypeStruct((dp_count * shards.shape[1], shards.shape[2]), low))
        out_specs += [anywhere] * 3
        scratch += gather_semaphores(dp_count) + trade_semaphores(owners) + trade_semaphores(owners)
    if mode == 2:
        total = (hidden // 8, width)
        out_shape += [both, both, jax.ShapeDtypeStruct(total, jnp.float32)]
        out_specs += [anywhere] * 2 + [pl.BlockSpec(total, lambda j: (0, 0))]
        scratch.append(pltpu.VMEM(both.shape, low))
        scratch += trade_semaphores(owners) + trade_semaphores(owners) + reduce_scratch([extras[1]])
    return pl.pallas_call(
        functools.partial(experts_kernel, mode, dp_count),
        grid=(steps,),
        out_shape=out_shape,
        in_specs=[
            pairs,
            pairs,
            pl.BlockSpec((width, block), lambda j: (0, j)),
            pl.BlockSpec((width, block), lambda j: (0, up.shape[1] // block - steps + j)),
            pl.BlockSpec((block, width), lambda j: (j, 0)),
        ]
        + [anywhere] * len(extras),
        out_specs=out_specs,
        scratch_shapes=scratch,
        compiler_params=pltpu.CompilerParams(
            dimension_semantics=("arbitrary",), vmem_limit_bytes=60 * 2**20, **links
        ),
        cost_estimate=pl.CostEstimate(
            flops=18 * count * width * hidden,
            bytes_accessed=12 * width * hidden + 8 * count * width,
            transcendentals=count * hidden,
        ),
        name="experts",
    )(rows, grads, gate, up, down, *extras)


def dp_grid(dp_count):
    outer = 4 if dp_count % 4 == 0 else 1
    return outer, dp_count // outer


def place():
    me, mine = lax.axis_index("dp"), lax.axis_index("expert")
    return me, mine


def greet(peers):
    barrier = pltpu.get_barrier_semaphore()
    for peer in peers:
        pl.semaphore_signal(barrier, inc=1, device_id=peer, device_id_type=MESH)
    pl.semaphore_wait(barrier, len(peers))


class LineGather:
    def __init__(self, shard, full, dp_count, send_sem, recv_sem, own_sem, columns=None, also=None):
        self.columns = slice(None) if columns is None else columns
        self.also = also or (lambda chunk: None)
        self.shard, self.full, self.dp_count = shard, full, dp_count
        self.send_sem, self.recv_sem, self.own_sem = send_sem, recv_sem, own_sem
        self.outer_count, self.inner_count = dp_grid(dp_count)
        self.me, self.mine = place()
        self.outer, self.inner = self.me // self.inner_count, self.me % self.inner_count
        self.inner_peers = [
            lax.rem(self.inner + k, self.inner_count) for k in range(1, self.inner_count)
        ]
        self.can_up, self.can_down = self.outer < self.outer_count - 1, self.outer > 0

    def peers(self):
        below = lax.rem(self.outer + self.outer_count - 1, self.outer_count)
        above = lax.rem(self.outer + 1, self.outer_count)
        return [(peer * self.inner_count + self.inner, self.mine) for peer in (below, above)] + [
            (self.outer * self.inner_count + peer, self.mine) for peer in self.inner_peers
        ]

    def spot(self, chunk):
        rows = self.shard.shape[0]
        return self.full.at[pl.ds(pl.multiple_of(chunk * rows, 8), rows), self.columns]

    def copy(self, source, chunk, device, way, at):
        return pltpu.make_async_remote_copy(
            src_ref=source,
            dst_ref=self.spot(chunk),
            send_sem=self.send_sem.at[way, at, chunk],
            recv_sem=self.recv_sem.at[chunk],
            device_id=(device, self.mine),
            device_id_type=MESH,
        )

    def up(self, source, chunk):
        return self.copy(source, chunk, (self.outer + 1) * self.inner_count + self.inner, 1, 0)

    def down(self, source, chunk):
        return self.copy(source, chunk, (self.outer - 1) * self.inner_count + self.inner, 2, 0)

    def across(self, source, chunk):
        return [
            self.copy(source, chunk, self.outer * self.inner_count + peer, 0, at)
            for at, peer in enumerate(self.inner_peers)
        ]

    def keep(self):
        return pltpu.make_async_copy(self.shard, self.spot(self.me), self.own_sem)

    def arrived(self, chunk):
        pltpu.make_async_copy(self.spot(chunk), self.spot(chunk), self.recv_sem.at[chunk]).wait()

    def start(self):
        for copy in self.across(self.shard, self.me):
            copy.start()
        pl.when(self.can_up)(lambda: self.up(self.shard, self.me).start())
        pl.when(self.can_down)(lambda: self.down(self.shard, self.me).start())
        self.keep().start()

    def relay(self, step):
        low, high = self.outer - step, self.outer + step

        def pass_on(source, upward):
            chunk = source * self.inner_count + self.inner
            self.arrived(chunk)
            if upward:
                pl.when(self.can_up)(lambda: self.up(self.spot(chunk), chunk).start())
            else:
                pl.when(self.can_down)(lambda: self.down(self.spot(chunk), chunk).start())
            for copy in self.across(self.spot(chunk), chunk):
                copy.start()
            self.also(chunk)

        pl.when(low >= 0)(lambda: pass_on(low, True))
        pl.when(high < self.outer_count)(lambda: pass_on(high, False))

    def finish(self):
        self.keep().wait()
        for peer in self.inner_peers:
            for k in range(self.outer_count):
                chunk = lax.rem(self.outer + k, self.outer_count) * self.inner_count + peer
                self.arrived(chunk)
                self.also(chunk)
        for plane in range(self.outer_count):
            chunk = plane * self.inner_count + self.inner
            for copy in self.across(self.spot(chunk), chunk):
                copy.wait_send()
            pl.when(self.can_up & (self.outer >= plane))(
                lambda chunk=chunk: self.up(self.spot(chunk), chunk).wait_send()
            )
            pl.when(self.can_down & (self.outer <= plane))(
                lambda chunk=chunk: self.down(self.spot(chunk), chunk).wait_send()
            )


def gather_semaphores(dp_count):
    inner_count = dp_grid(dp_count)[1]
    return [
        pltpu.SemaphoreType.DMA((3, max(1, inner_count - 1), dp_count)),
        pltpu.SemaphoreType.DMA((dp_count,)),
        pltpu.SemaphoreType.DMA,
    ]


def by_rows(count, body):
    def step(i, carry):
        body(i * 16)
        return carry

    lax.fori_loop(0, count // 16, step, 0)


class Trade:
    def __init__(self, source, target, send_sem, recv_sem):
        self.source, self.target, self.send_sem, self.recv_sem = source, target, send_sem, recv_sem
        self.me, self.mine = place()
        count = target.shape[0]
        self.partners = [lax.rem(self.mine + k, count) for k in range(1, count)]

    def peers(self):
        return [(self.me, peer) for peer in self.partners]

    def copy(self, k):
        peer = self.partners[k]
        return pltpu.make_async_remote_copy(
            src_ref=self.source.at[peer],
            dst_ref=self.target.at[self.mine],
            send_sem=self.send_sem.at[k + 1],
            recv_sem=self.recv_sem.at[self.mine],
            device_id=(self.me, peer),
            device_id_type=MESH,
        )

    def keep(self):
        return pltpu.make_async_copy(
            self.source.at[self.mine], self.target.at[self.mine], self.send_sem.at[0]
        )

    def start(self):
        for k in range(len(self.partners)):
            self.copy(k).start()
        self.keep().start()

    def finish(self):
        self.keep().wait()
        for k, peer in enumerate(self.partners):
            there = self.target.at[peer]
            pltpu.make_async_copy(there, there, self.recv_sem.at[peer]).wait()
            self.copy(k).wait_send()


def trade_semaphores(owner_count):
    return [pltpu.SemaphoreType.DMA((owner_count,)), pltpu.SemaphoreType.DMA((owner_count,))]


def expert_gather_kernel(dp_count, rows_ref, grads_ref, shards_ref, rows_out, grads_out, full_ref, *sems):
    line = LineGather(shards_ref.at[0], full_ref, dp_count, *sems[:3])
    trades = [Trade(rows_ref.at[0], rows_out, *sems[3:5]), Trade(grads_ref.at[0], grads_out, *sems[5:7])]
    greet(line.peers() + trades[0].peers())
    line.start()
    for trade in trades:
        trade.start()
    for hop in range(1, line.outer_count):
        line.relay(hop)
    line.finish()
    for trade in trades:
        trade.finish()


def expert_gather(rows, grads, shards, dp_count, collective):
    anywhere = pl.BlockSpec(memory_space=pl.ANY)
    return pl.pallas_call(
        functools.partial(expert_gather_kernel, dp_count),
        out_shape=[
            jax.ShapeDtypeStruct(rows.shape[1:], rows.dtype),
            jax.ShapeDtypeStruct(grads.shape[1:], grads.dtype),
            jax.ShapeDtypeStruct((dp_count * shards.shape[1], shards.shape[2]), shards.dtype),
        ],
        in_specs=[anywhere] * 3,
        out_specs=[anywhere] * 3,
        scratch_shapes=gather_semaphores(dp_count)
        + trade_semaphores(rows.shape[1])
        + trade_semaphores(rows.shape[1]),
        compiler_params=pltpu.CompilerParams(collective_id=collective, has_side_effects=True),
        name="expert_gather",
    )(rows, grads, shards)


def small_gather_kernel(
    dp_count, expert_count, shard_ref, routes_ref, full_ref, columns_ref, rows_ref,
    send_sem, recv_sem, own_sem, pass_sem, mate_sem, all_sem,
):
    me, mine = place()
    rows, columns = shard_ref.shape
    half = columns // 2
    side = mine % 2
    mate = mine + 1 - 2 * side
    own_columns = pl.ds(pl.multiple_of(side * half, 128), half)
    mate_columns = pl.ds(pl.multiple_of((1 - side) * half, 128), half)

    def there(chunk, lanes):
        return full_ref.at[pl.ds(pl.multiple_of(chunk * rows, 8), rows), lanes]

    def pass_copy(chunk):
        return pltpu.make_async_remote_copy(
            src_ref=there(chunk, own_columns),
            dst_ref=there(chunk, own_columns),
            send_sem=pass_sem.at[chunk],
            recv_sem=mate_sem.at[chunk],
            device_id=(me, mate),
            device_id_type=MESH,
        )

    line = LineGather(
        shard_ref.at[:, own_columns], full_ref, dp_count, send_sem, recv_sem, own_sem,
        own_columns, lambda chunk: pass_copy(chunk).start(),
    )
    greet(line.peers() + [(me, mate)])
    line.start()
    other = pltpu.make_async_copy(shard_ref.at[:, mate_columns], there(me, mate_columns), all_sem)
    other.start()
    routing_kernel(expert_count, routes_ref, columns_ref, rows_ref)
    for hop in range(1, line.outer_count):
        line.relay(hop)
    line.finish()
    other.wait()
    for k in range(1, dp_count):
        chunk = lax.rem(me + k, dp_count)
        target = there(chunk, mate_columns)
        pltpu.make_async_copy(target, target, mate_sem.at[chunk]).wait()
        pass_copy(chunk).wait_send()


def small_gather(shard, routes, expert_count, dp_count, collective):
    rows, columns = shard.shape
    tokens = routes.shape[0]
    anywhere, in_vmem = pl.BlockSpec(memory_space=pl.ANY), pl.BlockSpec(memory_space=pltpu.VMEM)
    return pl.pallas_call(
        functools.partial(small_gather_kernel, dp_count, expert_count),
        out_shape=[
            jax.ShapeDtypeStruct((dp_count * rows, columns), shard.dtype),
            jax.ShapeDtypeStruct((tokens, 128), jnp.int32),
            jax.ShapeDtypeStruct((8, tokens), jnp.int32),
        ],
        in_specs=[anywhere, in_vmem],
        out_specs=[anywhere, in_vmem, in_vmem],
        scratch_shapes=gather_semaphores(dp_count)
        + [
            pltpu.SemaphoreType.DMA((dp_count,)),
            pltpu.SemaphoreType.DMA((dp_count,)),
            pltpu.SemaphoreType.DMA,
        ],
        compiler_params=pltpu.CompilerParams(
            collective_id=collective, has_side_effects=True, vmem_limit_bytes=60 * 2**20
        ),
        name="small_gather",
    )(shard, routes)


class LineReduce:
    def __init__(self, sources, totals, owns, ins, lows, highs, own_sem, in_send, in_recv, line_send, line_recv):
        self.sources, self.totals = sources, totals
        self.owns, self.ins, self.lows, self.highs = owns, ins, lows, highs
        self.own_sem, self.in_send, self.in_recv = own_sem, in_send, in_recv
        self.line_send, self.line_recv = line_send, line_recv
        self.me, self.mine = place()
        self.outer, self.inner = self.me // 2, self.me % 2
        self.every = range(len(sources))

    def peers(self):
        low, high = lax.rem(self.outer + 3, 4), lax.rem(self.outer + 1, 4)
        return [
            (self.me + 1 - 2 * self.inner, self.mine),
            (low * 2 + self.inner, self.mine),
            (high * 2 + self.inner, self.mine),
        ]

    def order(self, o):
        return sorted(range(4), key=lambda plane: (-abs(plane - o), plane))

    def chunk(self, p, at):
        source = self.sources[p]
        rows = self.owns[p].shape[-2]
        here = pl.ds(pl.multiple_of(at * rows, 16), rows)
        return source.at[:, here, :] if len(source.shape) == 3 else source.at[here, :]

    def own_copy(self, p, plane):
        return pltpu.make_async_copy(
            self.chunk(p, plane * 2 + self.inner), self.owns[p].at[plane], self.own_sem.at[p, plane]
        )

    def in_copy(self, p, plane):
        return pltpu.make_async_remote_copy(
            src_ref=self.chunk(p, plane * 2 + 1 - self.inner),
            dst_ref=self.ins[p].at[plane],
            send_sem=self.in_send.at[p, plane],
            recv_sem=self.in_recv.at[p, plane],
            device_id=(self.me + 1 - 2 * self.inner, self.mine),
            device_id_type=MESH,
        )

    def line_copy(self, p, plane, upward, device_plane):
        target = self.lows[p].at[plane - 1] if upward else self.highs[p].at[plane]
        return pltpu.make_async_remote_copy(
            src_ref=self.ins[p].at[plane],
            dst_ref=target,
            send_sem=self.line_send.at[p, 0 if upward else 1, plane],
            recv_sem=self.line_recv.at[p, 0 if upward else 1, plane],
            device_id=(device_plane * 2 + self.inner, self.mine),
            device_id_type=MESH,
        )

    def start(self, o):
        for plane in self.order(o):
            for p in self.every:
                self.in_copy(p, plane).start()
        for plane in self.order(o):
            for p in self.every:
                self.own_copy(p, plane).start()

    def line_start(self, o, p, plane):
        return self.line_copy(p, plane, plane > o, o + 1 if plane > o else o - 1)

    def pass_on(self, o, k):
        plane = self.order(o)[k]
        for p in self.every:
            self.own_copy(p, plane).wait()
            self.in_copy(p, plane).wait_recv()
            terms = [self.owns[p].at[plane]]
            if o > 0 and plane >= o:
                self.line_copy(p, plane, True, o).wait_recv()
                terms.append(self.lows[p].at[plane - 1])
            if o < 3 and plane <= o:
                self.line_copy(p, plane, False, o).wait_recv()
                terms.append(self.highs[p].at[plane])
            held = self.ins[p].at[plane]
            last = plane == o
            sides = held.shape[0] if len(held.shape) == 3 else 0

            def body(at, p=p, terms=terms, held=held, last=last, sides=sides):
                here = pl.ds(pl.multiple_of(at, 16), 16)
                for side in range(max(1, sides)):
                    spot = (side, here) if sides else (here,)
                    total = held[spot].astype(jnp.float32)
                    for term in terms:
                        total = total + term[spot].astype(jnp.float32)
                    if last:
                        size = total.shape[-1]
                        self.totals[p][here, side * size : (side + 1) * size] = total
                    else:
                        held[spot] = total.astype(held.dtype)

            by_rows(held.shape[-2], body)
            if not last:
                self.line_start(o, p, plane).start()

    def finish(self, o):
        for plane in range(4):
            for p in self.every:
                self.in_copy(p, plane).wait_send()
                if plane != o:
                    self.line_start(o, p, plane).wait_send()

    def each_plane(self, body):
        for o in range(4):
            pl.when(self.outer == o)(functools.partial(body, o))


def reduce_scratch(sources):
    shapes = []
    for planes in (4, 4, 3, 3):
        for source in sources:
            rows = source.shape[-2] // 8
            shapes.append(pltpu.VMEM((planes,) + source.shape[:-2] + (rows, source.shape[-1]), jnp.bfloat16))
    count = len(sources)
    return shapes + [
        pltpu.SemaphoreType.DMA((count, 4)),
        pltpu.SemaphoreType.DMA((count, 4)),
        pltpu.SemaphoreType.DMA((count, 4)),
        pltpu.SemaphoreType.DMA((count, 2, 4)),
        pltpu.SemaphoreType.DMA((count, 2, 4)),
    ]


def line_reduce(sources, totals, scratch):
    count = len(sources)
    buffers = [scratch[n * count : (n + 1) * count] for n in range(4)]
    return LineReduce(sources, totals, *buffers, *scratch[4 * count :])


def final_reduce_kernel(small_count, *refs):
    small_refs, refs = refs[:small_count], refs[small_count:]
    (
        small_out, swap, small_in, small_low, small_high, final_low, final_in,
        swap_send, swap_recv, in_send, in_recv, line_send, line_recv, last_send, last_recv,
    ) = refs
    outer_count, inner_count = 4, 2
    me, mine = place()
    outer, inner = me // inner_count, me % inner_count
    side = mine % 2
    mate, across = mine + 1 - 2 * side, lax.rem(mine + 2, 4)
    beside = me + 1 - 2 * inner
    half_rows = small_refs[0].shape[1] // 2
    starts = [sum(ref.shape[2] for ref in small_refs[:n]) for n in range(small_count + 1)]

    def remote(source, target, device, send_at, recv_at):
        return pltpu.make_async_remote_copy(
            src_ref=source,
            dst_ref=target,
            send_sem=send_at,
            recv_sem=recv_at,
            device_id=device,
            device_id_type=MESH,
        )

    low_peer = lax.rem(outer + outer_count - 1, outer_count) * inner_count + inner
    high_peer = lax.rem(outer + 1, outer_count) * inner_count + inner
    greet([(me, mate), (me, across), (beside, mine), (low_peer, mine), (high_peer, mine)])

    mate_rows = pl.ds(pl.multiple_of((1 - side) * half_rows, 16), half_rows)
    own_rows = pl.ds(pl.multiple_of(side * half_rows, 16), half_rows)

    def swap_copy(n):
        return remote(
            small_refs[n].at[:, mate_rows, :],
            swap.at[:, :, starts[n] : starts[n + 1]],
            (me, mate),
            swap_send.at[n],
            swap_recv.at[n],
        )

    def inner_copy(plane):
        return remote(
            swap.at[plane * inner_count + 1 - inner],
            small_in.at[plane],
            (beside, mine),
            in_send.at[plane],
            in_recv.at[plane],
        )

    def line_copy(plane, upward, device_plane):
        way = 0 if upward else 1
        return remote(
            small_in.at[plane],
            (small_low if upward else small_high).at[plane],
            (device_plane * inner_count + inner, mine),
            line_send.at[way, plane],
            line_recv.at[way, plane],
        )

    def wide(values):
        return values.astype(jnp.float32)

    def add_own(chunk):
        def body(at):
            here = pl.ds(pl.multiple_of(at, 16), 16)
            there = pl.ds(pl.multiple_of(side * half_rows + at, 16), 16)
            for n in range(small_count):
                columns = slice(starts[n], starts[n + 1])
                swap[chunk, here, columns] = (
                    wide(swap[chunk, here, columns]) + wide(small_refs[n][chunk, there, :])
                ).astype(swap.dtype)

        by_rows(half_rows, body)

    def at_plane(o):
        order = sorted(range(outer_count), key=lambda t: (-abs(t - o), t))

        def line_start(plane):
            return line_copy(plane, plane > o, o + 1 if plane > o else o - 1)

        for n in range(small_count):
            swap_copy(n).start()
        for n in range(small_count):
            swap_copy(n).wait_recv()
        for plane in order:
            add_own(plane * inner_count + 1 - inner)
            inner_copy(plane).start()
        for plane in order:
            add_own(plane * inner_count + inner)
            inner_copy(plane).wait_recv()
            terms = [swap.at[plane * inner_count + inner]]
            if o > 0 and plane >= o:
                line_copy(plane, True, o).wait_recv()
                terms.append(small_low.at[plane])
            if o < outer_count - 1 and plane <= o:
                line_copy(plane, False, o).wait_recv()
                terms.append(small_high.at[plane])
            target = final_low if plane == o else small_in.at[plane]

            def gather(at, plane=plane, terms=terms, target=target):
                here = pl.ds(pl.multiple_of(at, 16), 16)
                total = wide(small_in[plane, here, :])
                for term in terms:
                    total = total + wide(term[here, :])
                target[here, :] = total.astype(target.dtype)

            by_rows(half_rows, gather)
            if plane != o:
                line_start(plane).start()
        remote(final_low, final_in, (me, across), last_send.at[0], last_recv.at[0]).start()
        for plane in range(outer_count):
            inner_copy(plane).wait_send()
            if plane != o:
                line_start(plane).wait_send()
        for n in range(small_count):
            swap_copy(n).wait_send()

    for o in range(outer_count):
        pl.when(outer == o)(functools.partial(at_plane, o))
    remote(final_low, final_in, (me, across), last_send.at[0], last_recv.at[0]).wait()

    def total_body(at):
        here = pl.ds(pl.multiple_of(at, 16), 16)
        there = pl.ds(pl.multiple_of(side * half_rows + at, 16), 16)
        small_out[there, :] = wide(final_low[here, :]) + wide(final_in[here, :])

    by_rows(half_rows, total_body)
    mate_copy = remote(
        small_out.at[own_rows, :], small_out.at[own_rows, :], (me, mate), last_send.at[1], last_recv.at[1]
    )
    mate_copy.start()
    mate_copy.wait()


def final_reduce(smalls, collective):
    chunk_count, small_rows, _ = smalls[0].shape
    small_columns = sum(small.shape[2] for small in smalls)
    low = jnp.bfloat16
    planes = 4
    in_vmem = pl.BlockSpec(memory_space=pltpu.VMEM)
    half = small_rows // 2
    return pl.pallas_call(
        functools.partial(final_reduce_kernel, len(smalls)),
        out_shape=jax.ShapeDtypeStruct((small_rows, small_columns), jnp.float32),
        in_specs=[in_vmem] * len(smalls),
        out_specs=in_vmem,
        scratch_shapes=[pltpu.VMEM((chunk_count, half, small_columns), low)]
        + [pltpu.VMEM((planes, half, small_columns), low)] * 3
        + [pltpu.VMEM((half, small_columns), low)] * 2
        + [
            pltpu.SemaphoreType.DMA((len(smalls),)),
            pltpu.SemaphoreType.DMA((len(smalls),)),
            pltpu.SemaphoreType.DMA((planes,)),
            pltpu.SemaphoreType.DMA((planes,)),
            pltpu.SemaphoreType.DMA((2, planes)),
            pltpu.SemaphoreType.DMA((2, planes)),
            pltpu.SemaphoreType.DMA((2,)),
            pltpu.SemaphoreType.DMA((2,)),
        ],
        compiler_params=pltpu.CompilerParams(
            collective_id=collective, has_side_effects=True, vmem_limit_bytes=40 * 2**20
        ),
        name="final_reduce",
    )(*smalls)


def shards(
    tokens,
    resid_logits,
    routes,
    doc_ids,
    w_qkv,
    w_out,
    gain_attn,
    gain_ffn,
    w_router,
    w_const,
    v_const,
    w_gate_up,
    w_down,
    out_grad,
):
    dp_count, owner_count = lax.axis_size("dp"), lax.axis_size("expert")
    own_links = dp_count == 8 and owner_count == 4 and w_gate_up.shape[0] == 2
    seq_count, length, width = tokens.shape
    assert seq_count == 1
    rows = seq_count * length
    choice_count = resid_logits.shape[-1]
    local_count = w_gate_up.shape[0]
    expert_count = owner_count * local_count
    hidden_count = w_down.shape[1] * dp_count
    width_qkv, width_out = w_qkv.shape[1], w_out.shape[1]
    small_parts = [w_router, w_const, v_const, gain_attn[:, None], gain_ffn[:, None]]
    small_width = sum(part.shape[1] for part in small_parts)
    pad = jnp.zeros((w_qkv.shape[0], 256 - small_width), jnp.bfloat16)
    packed = jnp.concatenate([w_qkv, w_out] + small_parts + [pad], 1)
    inputs = tokens.reshape(rows, width)
    cot = out_grad.reshape(rows, width)
    route_rows = routes.reshape(rows, 2)
    cosine, sine = rotary_lanes(length, width // HEADS)
    docs_row, docs_column = doc_ids.reshape(1, rows), doc_ids.reshape(rows, 1)
    resid = jnp.pad(
        resid_logits.reshape(rows, choice_count).astype(jnp.float32), ((0, 0), (0, 128 - choice_count))
    )
    if own_links:
        packed_full, spots, spot_rows = small_gather(packed, route_rows, expert_count, dp_count, 1)
    else:
        spots, spot_rows = routing(route_rows, expert_count)
        packed_full = lax.all_gather(packed, "dp", axis=0, tiled=True)
    gather = functools.partial(lax.all_gather, axis_name="dp", axis=0, tiled=True)
    if own_links:
        first_gate_up, second_down, packed_full = lax.optimization_barrier(
            (w_gate_up[0], w_down[1], packed_full)
        )
        first_gate_up, second_down = gather(first_gate_up), gather(second_down)
    else:
        first_gate_up = gather(w_gate_up[0])
    normed_one, queries, keys, values, attended, middle, normed_two, aux = attention_forward(
        inputs, packed_full, docs_row, docs_column, cosine, sine, route_rows, resid
    )
    send_rows, send_grads = dispatch(spot_rows, aux, normed_two, cot, owner_count, local_count)
    if own_links:
        rows_in, grads_in, first_down = expert_gather(send_rows, send_grads, w_down, dp_count, 2)
        grad_gu, grad_down, both, next_rows, next_grads, second_gate_up = experts(
            rows_in, grads_in, first_gate_up, first_gate_up, first_down, 1, dp_count,
            [send_rows, send_grads, w_gate_up], 6,
        )
        gu_parts = [lax.psum_scatter(grad_gu, "dp", scatter_dimension=1, tiled=True)]
        second_gu, second_grad_down, *parts, down_part = experts(
            next_rows, next_grads, second_gate_up, second_gate_up, second_down, 2, dp_count,
            [both, grad_down], 4,
        )
        down_parts = [down_part]
    else:
        exchange = functools.partial(
            lax.all_to_all, axis_name="expert", split_axis=0, concat_axis=0, tiled=True
        )
        parts, gu_parts, down_parts = [], [], []
        for e in range(local_count):
            gate_up = first_gate_up if e == 0 else gather(w_gate_up[e])
            grad_gu, grad_down, both = experts(
                exchange(send_rows[e]), exchange(send_grads[e]), gate_up, gate_up, gather(w_down[e])
            )
            parts.append(exchange(both))
            gu_parts.append(lax.psum_scatter(grad_gu, "dp", scatter_dimension=1, tiled=True))
            down_parts.append(lax.psum_scatter(grad_down, "dp", scatter_dimension=0, tiled=True))
    gu_parts = [jnp.concatenate([part[0], part[1]], -1).astype(jnp.float32) for part in gu_parts]
    down_parts = [part.astype(jnp.float32) for part in down_parts]
    output, logit_grad, grad_middle, small_grad = combine(
        parts, spots, route_rows, aux, normed_two, middle, cot, packed_full, choice_count, expert_count
    )
    backward = functools.partial(
        attention_backward, grad_middle, queries, keys, values, attended, normed_one, inputs,
        packed_full, docs_row, docs_column, cosine, sine, small_grad,
    )
    if own_links:
        token_grad, *weight_grads, gu_part, down_part = backward([second_gu, second_grad_down], 7)
        gu_parts.append(gu_part)
        down_parts.append(down_part)
        packed_part = final_reduce(
            [grad.reshape(dp_count, width // dp_count, grad.shape[1]) for grad in weight_grads], 3
        )
    else:
        token_grad, *weight_grads = backward()
        packed_part = lax.psum_scatter(
            jnp.concatenate(weight_grads, 1), "dp", scatter_dimension=0, tiled=True
        )
        packed_part = lax.psum(packed_part, "expert").astype(jnp.float32)
    part_qkv = packed_part[:, :width_qkv]
    part_out = packed_part[:, width_qkv : width_qkv + width_out]
    small_part = packed_part[:, width_qkv + width_out :]
    return (
        output.reshape(tokens.shape),
        token_grad.reshape(tokens.shape),
        logit_grad.reshape(resid_logits.shape),
        part_qkv,
        part_out,
        small_part[:, 18],
        small_part[:, 19],
        small_part[:, 0:12],
        small_part[:, 12:16],
        small_part[:, 16:18],
        jnp.stack(gu_parts),
        jnp.stack(down_parts),
    )


def solution(mesh):
    placed = (
        P(("dp", "expert"), None, None),
        P(("dp", "expert"), None, None),
        P(("dp", "expert"), None, None),
        P(("dp", "expert"), None),
        P("dp", None),
        P("dp", None),
        P("dp"),
        P("dp"),
        P("dp", None),
        P("dp", None),
        P("dp", None),
        P("expert", "dp", None),
        P("expert", "dp", None),
        P(("dp", "expert"), None, None),
    )
    return jax.shard_map(
        shards,
        mesh=mesh,
        in_specs=placed,
        out_specs=(
            P(("dp", "expert"), None, None),
            P(("dp", "expert"), None, None),
            P(("dp", "expert"), None, None),
            P("dp", None),
            P("dp", None),
            P("dp"),
            P("dp"),
            P("dp", None),
            P("dp", None),
            P("dp", None),
            P("expert", "dp", None),
            P("expert", "dp", None),
        ),
        check_vma=False,
    )
```

```python
import functools

import jax
import jax.numpy as jnp
import numpy as np
from jax import lax
from jax.experimental import pallas as pl
from jax.experimental.pallas import tpu as pltpu
from jax.sharding import PartitionSpec as P

HEADS = 12
BLOCK = 256
CAP = 256
GROUP = 256
FF_BLOCK = 512
MESH = pl.DeviceIdType.MESH
epsilon = 1e-06


def rotary_lanes(length, head_dim):
    half_dim = head_dim // 2
    frequency = (10000.0 ** (-np.arange(half_dim, dtype=np.float32) / half_dim)).astype(np.float32)
    angles = (np.arange(length, dtype=np.float32)[:, None] * frequency[None, :]).astype(np.float64)
    cosine = np.cos(angles).astype(np.float32)
    sine = np.sin(angles).astype(np.float32)
    return (
        np.concatenate([cosine] * 4, 1),
        np.concatenate([-sine, sine, -sine, sine], 1),
    )


def nt(left, right):
    return lax.dot_general(left, right, (((1,), (1,)), ((), ())), preferred_element_type=jnp.float32)


def tn(left, right):
    return lax.dot_general(left, right, (((0,), (0,)), ((), ())), preferred_element_type=jnp.float32)


def nn(left, right):
    return jnp.dot(left, right, preferred_element_type=jnp.float32)


def lane_ids(shape):
    return lax.broadcasted_iota(jnp.int32, shape, len(shape) - 1)


def turn(values, cosine, sine):
    lanes = lane_ids(values.shape)
    ahead, behind = pltpu.roll(values, 96, 1), pltpu.roll(values, 32, 1)
    return values * cosine + jnp.where(lanes % 64 < 32, ahead, behind) * sine


def key_span(i):
    return max(0, i - 2) * BLOCK, (i + 1) * BLOCK


def mask_of(docs_column, docs_row, i):
    low, high = key_span(i)
    return docs_column[low:high, :] == docs_row[:, i * BLOCK : (i + 1) * BLOCK]


def attention_forward_kernel(linked, *refs):
    (
        tokens_ref, wq_ref, wk_ref, wv_ref, wo_ref, small_ref, docs_row_ref, docs_column_ref,
        cosine_ref, sine_ref, routes_ref, resid_ref,
    ) = refs[:12]
    (
        normed_ref, q_ref, k_ref, v_ref, attended_ref, middle_ref, normed_two_ref, aux_ref,
    ) = refs[12 + bool(linked) : 20 + bool(linked)]
    step = pl.program_id(0)
    rows = tokens_ref.shape[0]
    if linked:
        branch_ref = refs[22]
        line = LineGather(refs[12].at[1], refs[21], linked, *refs[23:])

        @pl.when(step == 0)
        def _():
            greet(line.peers())
            line.start()

        for hop in range(1, 3):
            pl.when(step == hop)(functools.partial(line.relay, hop))
    else:
        branch_ref = refs[20]

    @pl.when(step == 0)
    def _():
        inputs = tokens_ref[...].astype(jnp.float32)
        gains = jnp.transpose(small_ref[:, :128].astype(jnp.float32))[18:19, :]
        scale = lax.rsqrt(jnp.mean(inputs * inputs, -1, keepdims=True) + epsilon)
        normed_ref[...] = (inputs * scale * gains).astype(jnp.bfloat16)
        branch_ref[...] = jnp.zeros_like(branch_ref)

    normed = normed_ref[...]
    cosine, sine = cosine_ref[...], sine_ref[...]
    for w_ref, out_ref, turned in ((wq_ref, q_ref, True), (wk_ref, k_ref, True), (wv_ref, v_ref, False)):
        projected = nn(normed, w_ref[...])
        for half in range(2):
            part = projected[:, half * 128 : half * 128 + 128]
            if turned:
                part = turn(part, cosine, sine)
            out_ref[:, half * 128 : half * 128 + 128] = part.astype(jnp.bfloat16)

    docs_row, docs_column = docs_row_ref[...], docs_column_ref[...]
    for i in range(rows // BLOCK):
        low, high = key_span(i)
        here = slice(i * BLOCK, (i + 1) * BLOCK)
        allowed = mask_of(docs_column, docs_row, i)
        for pair in range(2):
            lanes = slice(pair * 128, pair * 128 + 128)
            queries = q_ref[here, lanes] * jnp.asarray(0.125, jnp.bfloat16)
            keys, values = k_ref[low:high, lanes], v_ref[low:high, lanes]
            left = lane_ids(queries.shape) < 64
            outs = []
            for head in range(2):
                own = left if head == 0 else jnp.logical_not(left)
                scores = nt(keys, jnp.where(own, queries, jnp.zeros_like(queries)))
                scores = jnp.where(allowed, scores, -1e30)
                shifted = jnp.exp(scores - jnp.max(scores, 0, keepdims=True))
                probs = shifted * (1.0 / jnp.sum(shifted, 0, keepdims=True))
                outs.append(tn(probs.astype(jnp.bfloat16), values))
            attended_ref[here, lanes] = jnp.where(left, outs[0], outs[1]).astype(jnp.bfloat16)
    branch_ref[...] += nn(attended_ref[...], wo_ref[...])

    @pl.when(step == pl.num_programs(0) - 1)
    def _():
        small = small_ref[:, :128]
        gains = jnp.transpose(small.astype(jnp.float32))[19:20, :]
        middle = tokens_ref[...].astype(jnp.float32) + branch_ref[...]
        middle_ref[...] = middle
        scale = lax.rsqrt(jnp.mean(middle * middle, -1, keepdims=True) + epsilon)
        normed_two = (middle * scale * gains).astype(jnp.bfloat16)
        normed_two_ref[...] = normed_two
        logits = nn(normed_two, small) + resid_ref[...].astype(jnp.float32)
        lanes = lane_ids(logits.shape)

        def lane(at):
            return jnp.sum(jnp.where(lanes == at, logits, 0.0), -1, keepdims=True)

        def two(first, second):
            peak = jnp.maximum(first, second)
            first, second = jnp.exp(first - peak), jnp.exp(second - peak)
            return first / (first + second), second / (first + second)

        columns = list(two(lane(routes_ref[:, 0:1]), lane(routes_ref[:, 1:2])))
        columns += list(two(lane(12), lane(13))) + list(two(lane(14), lane(15)))
        columns.append(scale)
        aux = jnp.zeros_like(logits)
        for at, column in enumerate(columns):
            aux = jnp.where(lanes == at, column, aux)
        aux_ref[...] = aux
        if linked:
            line.relay(3)
            line.finish()


def attention_forward(
    tokens, packed, docs_row, docs_column, cosine, sine, routes, resid, shards=None,
    dp_count=None, collective=None,
):
    rows, width = tokens.shape
    groups = width // GROUP
    low = jnp.bfloat16
    whole = lambda shape: pl.BlockSpec(shape, lambda j: (0, 0))
    column = lambda at: pl.BlockSpec((width, GROUP), lambda j: (0, at + j))
    out_column = pl.BlockSpec((rows, GROUP), lambda j: (0, j))
    full = jax.ShapeDtypeStruct((rows, width), low)
    linked = shards is not None
    anywhere = pl.BlockSpec(memory_space=pl.ANY)
    links = {"collective_id": collective, "has_side_effects": True} if linked else {}
    gathered = []
    if linked:
        gathered = [jax.ShapeDtypeStruct((dp_count * shards.shape[1], shards.shape[2]), low)]
    return pl.pallas_call(
        functools.partial(attention_forward_kernel, dp_count if linked else 0),
        grid=(groups,),
        out_shape=[full] * 5
        + [
            jax.ShapeDtypeStruct((rows, width), jnp.float32),
            full,
            jax.ShapeDtypeStruct((rows, 128), jnp.float32),
        ]
        + gathered,
        in_specs=[
            whole((rows, width)),
            column(0),
            column(groups),
            column(2 * groups),
            pl.BlockSpec((GROUP, width), lambda j: (j, 3)),
            pl.BlockSpec((width, 256), lambda j: (0, 12)),
            whole((1, rows)),
            whole((rows, 1)),
            whole((rows, 128)),
            whole((rows, 128)),
            whole((rows, 2)),
            whole((rows, 128)),
        ]
        + [anywhere] * linked,
        out_specs=[whole((rows, width))]
        + [out_column] * 4
        + [whole((rows, width)), whole((rows, width)), whole((rows, 128))]
        + [anywhere] * linked,
        scratch_shapes=[pltpu.VMEM((rows, width), jnp.float32)]
        + (gather_semaphores(dp_count) if linked else []),
        compiler_params=pltpu.CompilerParams(
            dimension_semantics=("arbitrary",), vmem_limit_bytes=56 * 2**20, **links
        ),
        cost_estimate=pl.CostEstimate(
            flops=2 * rows * width * 4 * width + 8 * rows * rows * width // 2,
            bytes_accessed=24 * rows * width,
            transcendentals=rows * rows * HEADS // 2,
        ),
        name="attention_forward",
    )(
        tokens, packed, packed, packed, packed, packed, docs_row, docs_column, cosine, sine, routes,
        resid, *([shards] if linked else []),
    )


def attention_backward_kernel(count, *refs):
    (
        grad_middle_ref, q_ref, k_ref, v_ref, attended_ref, normed_ref, tokens_ref,
        wq_ref, wk_ref, wv_ref, wo_ref, small_ref, docs_row_ref, docs_column_ref,
        cosine_ref, sine_ref, small_grad_ref,
    ) = refs[:17]
    sources, refs = refs[17 : 17 + count], refs[17 + count :]
    token_grad_ref, gq_ref, gk_ref, gv_ref, go_ref, small_out_ref = refs[:6]
    totals, refs = refs[6 : 6 + count], refs[6 + count :]
    branch_ref, back_ref, turned_ref, key_acc, value_acc, query_acc = refs[:6]
    step = pl.program_id(0)
    rows, width = tokens_ref.shape
    if count:
        line = line_reduce(sources, totals, refs[6:])

        @pl.when(step == 0)
        def _():
            greet(line.peers())
            line.each_plane(line.start)

        @pl.when(step == 2)
        def _():
            line.each_plane(lambda o: line.pass_on(o, 0))

    @pl.when(step == 0)
    def _():
        branch_ref[...] = grad_middle_ref[...].astype(jnp.bfloat16)
        back_ref[...] = jnp.zeros_like(back_ref)

    grad_branch = branch_ref[...]
    grad_attended = nt(grad_branch, wo_ref[...]).astype(jnp.bfloat16)
    go_ref[...] = tn(attended_ref[...], grad_branch).astype(jnp.bfloat16)
    cosine, sine = cosine_ref[...], sine_ref[...]
    docs_row, docs_column = docs_row_ref[...], docs_column_ref[...]
    for pair in range(2):
        lanes = slice(pair * 128, pair * 128 + 128)
        key_acc[...] = jnp.zeros_like(key_acc)
        value_acc[...] = jnp.zeros_like(value_acc)
        for i in range(rows // BLOCK):
            low, high = key_span(i)
            here = slice(i * BLOCK, (i + 1) * BLOCK)
            allowed = mask_of(docs_column, docs_row, i)
            queries = q_ref[here, lanes] * jnp.asarray(0.125, jnp.bfloat16)
            grads = grad_attended[here, lanes]
            keys, values = k_ref[low:high, lanes], v_ref[low:high, lanes]
            left = lane_ids(queries.shape) < 64
            query_grads = []
            key_grad, value_grad = None, None
            for head in range(2):
                own = left if head == 0 else jnp.logical_not(left)
                own_queries = jnp.where(own, queries, jnp.zeros_like(queries))
                own_grads = jnp.where(own, grads, jnp.zeros_like(grads))
                scores = jnp.where(allowed, nt(keys, own_queries), -1e30)
                shifted = jnp.exp(scores - jnp.max(scores, 0, keepdims=True))
                probs = shifted * (1.0 / jnp.sum(shifted, 0, keepdims=True))
                grad_probs = nt(values, own_grads)
                inner = jnp.sum(probs * grad_probs, 0, keepdims=True)
                grad_scores = (probs * (grad_probs - inner)).astype(jnp.bfloat16)
                part_value = nn(probs.astype(jnp.bfloat16), own_grads)
                part_key = nn(grad_scores, own_queries)
                value_grad = part_value if head == 0 else value_grad + part_value
                key_grad = part_key if head == 0 else key_grad + part_key
                query_grads.append(tn(grad_scores, keys))
            value_acc[low:high, :] += value_grad
            key_acc[low:high, :] += key_grad
            query_acc[here, :] = jnp.where(left, query_grads[0], query_grads[1]) * 0.125
        turned_ref[0, :, lanes] = turn(query_acc[...], cosine, -sine).astype(jnp.bfloat16)
        turned_ref[1, :, lanes] = turn(key_acc[...], cosine, -sine).astype(jnp.bfloat16)
        turned_ref[2, :, lanes] = value_acc[...].astype(jnp.bfloat16)
    normed = normed_ref[...]
    for at, (w_ref, out_ref) in enumerate(((wq_ref, gq_ref), (wk_ref, gk_ref), (wv_ref, gv_ref))):
        turned = turned_ref[at]
        out_ref[...] = tn(normed, turned).astype(jnp.bfloat16)
        back_ref[...] += nt(turned, w_ref[...])

    @pl.when(step == pl.num_programs(0) - 1)
    def _():
        gains = jnp.transpose(small_ref[:, :128].astype(jnp.float32))[18:19, :]
        inputs = tokens_ref[...].astype(jnp.float32)
        grads = back_ref[...]
        scale = lax.rsqrt(jnp.mean(inputs * inputs, -1, keepdims=True) + epsilon)
        weighted = grads * gains
        mean = jnp.mean(weighted * inputs, -1, keepdims=True)
        grad_inputs = scale * weighted - inputs * (scale * scale * scale * mean)
        token_grad_ref[...] = (grad_inputs + grad_middle_ref[...]).astype(jnp.bfloat16)
        gain_grad = jnp.sum(grads * inputs * scale, 0, keepdims=True)
        column = jnp.transpose(jnp.broadcast_to(gain_grad, (128, width)))
        small_grad = small_grad_ref[...]
        small_grad = jnp.where(lane_ids(small_grad.shape) == 18, column, small_grad)
        small_out_ref[:, :128] = small_grad.astype(jnp.bfloat16)
        small_out_ref[:, 128:] = jnp.zeros((width, 128), jnp.bfloat16)
        if count:

            def rest(o):
                for k in range(1, 4):
                    line.pass_on(o, k)
                line.finish(o)

            line.each_plane(rest)


def attention_backward(
    grad_middle, queries, keys, values, attended, normed, tokens, packed, docs_row, docs_column,
    cosine, sine, small_grad, sources=(), collective=None,
):
    rows, width = tokens.shape
    groups = width // GROUP
    low = jnp.bfloat16
    whole = lambda shape: pl.BlockSpec(shape, lambda j: (0, 0))
    column = lambda at: pl.BlockSpec((width, GROUP), lambda j: (0, at + j))
    by_group = pl.BlockSpec((rows, GROUP), lambda j: (0, j))
    weight = jax.ShapeDtypeStruct((width, width), low)
    linked = len(sources) > 0
    links = {"collective_id": collective, "has_side_effects": True} if linked else {}
    sums = []
    for source in sources:
        sides = source.shape[0] if len(source.shape) == 3 else 1
        sums.append((source.shape[-2] // 8, sides * source.shape[-1]))
    once = lambda shape: pl.BlockSpec(
        shape, lambda j: (0, 0), pipeline_mode=pl.Buffered(1)
    )
    return pl.pallas_call(
        functools.partial(attention_backward_kernel, len(sources)),
        grid=(groups,),
        out_shape=[jax.ShapeDtypeStruct((rows, width), low)]
        + [weight] * 4
        + [jax.ShapeDtypeStruct((width, 256), low)]
        + [jax.ShapeDtypeStruct(shape, jnp.float32) for shape in sums],
        in_specs=[
            once((rows, width)),
            by_group,
            by_group,
            by_group,
            by_group,
            once((rows, width)),
            once((rows, width)),
            column(0),
            column(groups),
            column(2 * groups),
            pl.BlockSpec((GROUP, width), lambda j: (j, 3)),
            pl.BlockSpec((width, 256), lambda j: (0, 12)),
            once((1, rows)),
            once((rows, 1)),
            once((rows, 128)),
            once((rows, 128)),
            once((width, 128)),
        ]
        + [pl.BlockSpec(memory_space=pl.ANY)] * len(sources),
        out_specs=[
            whole((rows, width)),
            column(0),
            column(0),
            column(0),
            pl.BlockSpec((GROUP, width), lambda j: (j, 0)),
            whole((width, 256)),
        ]
        + [whole(shape) for shape in sums],
        scratch_shapes=[
            pltpu.VMEM((rows, width), low),
            pltpu.VMEM((rows, width), jnp.float32),
            pltpu.VMEM((3, rows, GROUP), low),
            pltpu.VMEM((rows, 128), jnp.float32),
            pltpu.VMEM((rows, 128), jnp.float32),
            pltpu.VMEM((rows, 128), jnp.float32),
        ]
        + (reduce_scratch(sources) if linked else []),
        compiler_params=pltpu.CompilerParams(
            dimension_semantics=("arbitrary",), vmem_limit_bytes=61 * 2**20, **links
        ),
        cost_estimate=pl.CostEstimate(
            flops=4 * rows * width * 4 * width + 20 * rows * rows * width // 2,
            bytes_accessed=32 * rows * width,
            transcendentals=rows * rows * HEADS // 2,
        ),
        name="attention_backward",
    )(
        grad_middle, queries, keys, values, attended, normed, tokens, packed, packed, packed,
        packed, packed, docs_row, docs_column, cosine, sine, small_grad, *sources,
    )


def routing_kernel(expert_count, routes_ref, columns_ref, rows_ref):
    rows = routes_ref.shape[0]
    lanes = lane_ids((rows, 128))
    first = (lanes == routes_ref[:, 0:1]).astype(jnp.float32)
    second = (lanes == routes_ref[:, 1:2]).astype(jnp.float32)
    down = lax.broadcasted_iota(jnp.int32, (rows, rows), 0)
    lower = (down > lane_ids((rows, rows))).astype(jnp.bfloat16)
    before_first = nn(lower, first.astype(jnp.bfloat16))
    before_second = nn(lower, second.astype(jnp.bfloat16)) + jnp.sum(first, 0, keepdims=True)
    spots = []
    for picked, before, at in ((first, before_first, 0), (second, before_second, 1)):
        rank = jnp.sum(picked * before, -1, keepdims=True)
        route = routes_ref[:, at : at + 1]
        spot = route.astype(jnp.float32) * CAP + rank
        spots.append(jnp.where(route < expert_count, spot, jnp.full_like(spot, 2.0 * expert_count * CAP)))
    both = jnp.where(lanes == 0, spots[0], jnp.where(lanes == 1, spots[1], 0.0))
    columns_ref[...] = both.astype(jnp.int32)
    rows_ref[...] = jnp.transpose(both)[0:8, :].astype(jnp.int32)


def routing(routes, expert_count):
    rows = routes.shape[0]
    return pl.pallas_call(
        functools.partial(routing_kernel, expert_count),
        out_shape=[
            jax.ShapeDtypeStruct((rows, 128), jnp.int32),
            jax.ShapeDtypeStruct((8, rows), jnp.int32),
        ],
        compiler_params=pltpu.CompilerParams(vmem_limit_bytes=40 * 2**20),
        name="routing",
    )(routes)


def dispatch_kernel(spots_ref, aux_ref, normed_ref, cot_ref, rows_ref, grads_ref, gates_ref):
    step = pl.program_id(0)

    @pl.when(step == 0)
    def _():
        gates_ref[...] = jnp.transpose(aux_ref[...])[0:8, :]

    shape = (rows_ref.shape[0], normed_ref.shape[0])
    slots = step * rows_ref.shape[0] + lax.broadcasted_iota(jnp.int32, shape, 0)
    first, second = slots == spots_ref[0:1, :], slots == spots_ref[1:2, :]
    gates = jnp.sum(
        jnp.where(first, gates_ref[0:1, :], jnp.where(second, gates_ref[1:2, :], 0.0)), -1, keepdims=True
    )
    chosen = jnp.where(first | second, 1.0, 0.0).astype(jnp.bfloat16)
    rows_ref[...] = nn(chosen, normed_ref[...]).astype(jnp.bfloat16)
    grads_ref[...] = (nn(chosen, cot_ref[...]) * gates).astype(jnp.bfloat16)


def dispatch(spots, aux, normed, cot, owner_count, local_count):
    rows, width = normed.shape
    slot_count = owner_count * local_count * CAP
    whole = lambda shape: pl.BlockSpec(shape, lambda j: (0, 0))
    block = pl.BlockSpec(
        (None, None, CAP, width), lambda j: (j % local_count, j // local_count, 0, 0)
    )
    return pl.pallas_call(
        dispatch_kernel,
        grid=(slot_count // CAP,),
        out_shape=[jax.ShapeDtypeStruct((local_count, owner_count, CAP, width), jnp.bfloat16)] * 2,
        in_specs=[whole((8, rows)), whole((rows, 128)), whole((rows, width)), whole((rows, width))],
        out_specs=[block, block],
        scratch_shapes=[pltpu.VMEM((8, rows), jnp.float32)],
        compiler_params=pltpu.CompilerParams(
            dimension_semantics=("arbitrary",), vmem_limit_bytes=60 * 2**20
        ),
        cost_estimate=pl.CostEstimate(
            flops=4 * slot_count * rows * width,
            bytes_accessed=4 * (rows + slot_count) * width,
            transcendentals=0,
        ),
        name="dispatch",
    )(spots, aux, normed, cot)


def halves(values):
    high = values.astype(jnp.bfloat16)
    return high, (values - high.astype(jnp.float32)).astype(jnp.bfloat16)


def combine_kernel(
    expert_count, local_count, *refs
):
    parts, refs = refs[:local_count], refs[local_count:]
    (
        spots_ref, routes_ref, aux_ref, normed_ref, middle_ref, cot_ref, small_ref,
        output_ref, logit_ref, grad_middle_ref, small_out_ref, vectors_ref, small_grad_ref,
    ) = refs
    step = pl.program_id(0)

    @pl.when(step == 0)
    def _():
        vectors_ref[0:8, :] = jnp.transpose(small_ref[:, :128].astype(jnp.float32))[16:24, :]
        vectors_ref[8:16, :] = jnp.zeros((8, vectors_ref.shape[1]), jnp.float32)
        small_grad_ref[...] = jnp.zeros_like(small_grad_ref)

    rows, width = normed_ref.shape
    normed_low, cot_low = normed_ref[...], cot_ref[...]
    normed, cot = normed_low.astype(jnp.float32), cot_low.astype(jnp.float32)
    total = lambda values: jnp.sum(values, -1, keepdims=True)
    picks, back = [0.0, 0.0], 0.0
    for e in range(local_count):
        count = parts[e].shape[0] * CAP
        slots = lane_ids((rows, count))
        slots = slots // CAP * (local_count * CAP) + e * CAP + slots % CAP
        hits = [slots == spots_ref[:, s : s + 1] for s in range(2)]
        chosen = [jnp.where(hit, 1.0, 0.0).astype(jnp.bfloat16) for hit in hits]
        returned = parts[e][:, 0].reshape(count, width)
        for s in range(2):
            picks[s] = picks[s] + nn(chosen[s], returned)
        back = back + nn(chosen[0] + chosen[1], parts[e][:, 1].reshape(count, width))
    inner = [total(pick * cot) for pick in picks]
    gates = [aux_ref[:, s : s + 1] for s in range(2)]
    routes = [routes_ref[:, s : s + 1] for s in range(2)]
    dot_copy = total(cot * normed)

    def weight_of(route):
        return sum(jnp.where(routes[s] == route, gates[s], 0.0) for s in range(2))

    copy_weight = weight_of(expert_count + 1)
    mix = gates[0] * picks[0] + gates[1] * picks[1]
    pass_weight = copy_weight
    gate_grads = [
        inner[s] + jnp.where(routes[s] == expert_count + 1, dot_copy, 0.0) for s in range(2)
    ]
    lanes = lane_ids((rows, 128))
    spread = jnp.zeros((rows, 128), jnp.float32)
    for k in range(2):
        vector = vectors_ref[k : k + 1, :]
        keep, blend = aux_ref[:, 2 + 2 * k : 3 + 2 * k], aux_ref[:, 3 + 2 * k : 4 + 2 * k]
        weight = weight_of(expert_count + 2 + k)
        dot_vector = total(cot * vector)
        pass_weight = pass_weight + weight * keep
        mix = mix + (weight * blend) * vector
        value = keep * dot_copy + blend * dot_vector
        for s in range(2):
            gate_grads[s] = gate_grads[s] + jnp.where(routes[s] == expert_count + 2 + k, value, 0.0)
        term = keep * blend * (weight * dot_copy - weight * dot_vector)
        spread = jnp.where(lanes == 12 + 2 * k, term, spread)
        spread = jnp.where(lanes == 13 + 2 * k, -term, spread)
        spread = jnp.where(lanes == 16 + k, weight * blend, spread)
    mix = mix + pass_weight * normed
    middle, scale = middle_ref[...], aux_ref[:, 6:7]
    output_ref[...] = (middle + mix).astype(jnp.bfloat16)
    mean = gates[0] * gate_grads[0] + gates[1] * gate_grads[1]
    for s in range(2):
        spread = jnp.where(lanes == routes[s], gates[s] * (gate_grads[s] - mean), spread)
    logit_ref[...] = spread[:, : logit_ref.shape[1]].astype(jnp.bfloat16)
    logits = jnp.where(lanes < 16, spread, 0.0)
    high, low = halves(logits)
    small = small_ref[:, :128]
    vector_high, vector_low = halves(spread - logits)
    small_grad_ref[...] += (
        tn(normed_low, high) + tn(normed_low, low) + tn(cot_low, vector_high) + tn(cot_low, vector_low)
    )
    grads = back + pass_weight * cot + nt(high, small) + nt(low, small)
    vectors_ref[8:9, :] += jnp.sum(grads * middle * scale, 0, keepdims=True)
    weighted = grads * vectors_ref[3:4, :]
    mean = jnp.mean(weighted * middle, -1, keepdims=True)
    grad_middle_ref[...] = cot + scale * weighted - middle * (scale * scale * scale * mean)

    @pl.when(step == pl.num_programs(0) - 1)
    def _():
        column = jnp.transpose(jnp.broadcast_to(vectors_ref[8:9, :], (128, width)))
        small_grad = small_grad_ref[...]
        small_out_ref[...] = jnp.where(lane_ids(small_grad.shape) == 19, column, small_grad)


def combine(parts, spots, routes, aux, normed, middle, cot, packed, choice_count, expert_count):
    rows, width = normed.shape
    local_count = len(parts)
    slot_count = expert_count * CAP
    size = 256
    block = lambda columns: pl.BlockSpec((size, columns), lambda j: (j, 0))
    whole = lambda shape: pl.BlockSpec(shape, lambda j: (0,) * len(shape))
    return pl.pallas_call(
        functools.partial(combine_kernel, expert_count, local_count),
        grid=(rows // size,),
        out_shape=[
            jax.ShapeDtypeStruct((rows, width), jnp.bfloat16),
            jax.ShapeDtypeStruct((rows, choice_count), jnp.bfloat16),
            jax.ShapeDtypeStruct((rows, width), jnp.float32),
            jax.ShapeDtypeStruct((width, 128), jnp.float32),
        ],
        in_specs=[whole(part.shape) for part in parts]
        + [
            block(128),
            block(2),
            block(128),
            block(width),
            block(width),
            block(width),
            pl.BlockSpec((width, 256), lambda j: (0, 12)),
        ],
        out_specs=[block(width), block(choice_count), block(width), whole((width, 128))],
        scratch_shapes=[pltpu.VMEM((16, width), jnp.float32), pltpu.VMEM((width, 128), jnp.float32)],
        compiler_params=pltpu.CompilerParams(
            dimension_semantics=("arbitrary",), vmem_limit_bytes=56 * 2**20
        ),
        cost_estimate=pl.CostEstimate(
            flops=6 * slot_count * rows * width,
            bytes_accessed=14 * rows * width + 4 * slot_count * width,
            transcendentals=0,
        ),
        name="combine",
    )(*parts, spots, routes, aux, normed, middle, cot, packed)


def experts_kernel(mode, dp_count, *refs):
    rows_ref, grads_ref, w_gate_ref, w_up_ref, w_down_ref = refs[:5]
    if mode == 0:
        grad_gu_ref, grad_down_ref, both_ref, turned_ref, out_ref, back_ref = refs[5:]
    if mode == 1:
        next_rows, next_grads, shards_ref, grad_gu_ref, grad_down_ref, both_ref = refs[5:11]
        rows_out, grads_out, full_ref, turned_ref, out_ref, back_ref = refs[11:17]
        sems = refs[17:]
    if mode == 2:
        before_ref, source_ref, grad_gu_ref, grad_down_ref, first_in, second_in, total_ref = refs[5:12]
        turned_ref, out_ref, back_ref, both_ref = refs[12:16]
        sems = refs[16:]
    step = pl.program_id(0)
    width = rows_ref.shape[-1]
    rows = rows_ref[...].reshape(-1, width)
    grads = grads_ref[...].reshape(-1, width)
    if mode == 1:
        line = LineGather(shards_ref.at[1], full_ref, dp_count, *sems[:3])
        trades = [
            Trade(next_rows.at[1], rows_out, *sems[3:5]),
            Trade(next_grads.at[1], grads_out, *sems[5:7]),
        ]

        @pl.when(step == 0)
        def _():
            greet(line.peers() + trades[0].peers())
            line.start()
            for trade in trades:
                trade.start()

        for hop in range(1, line.outer_count):
            pl.when(step == hop)(functools.partial(line.relay, hop))

    if mode == 2:
        trades = [Trade(before_ref, first_in, *sems[:2]), Trade(both_ref, second_in, *sems[2:4])]
        line = line_reduce([source_ref], [total_ref], sems[4:])

        @pl.when(step == 0)
        def _():
            greet(line.peers() + trades[0].peers())
            line.each_plane(line.start)
            trades[0].start()

        for hop in range(3):
            pl.when(step == hop + 1)(
                functools.partial(line.each_plane, functools.partial(line.pass_on, k=hop))
            )

    @pl.when(step == 0)
    def _():
        turned_ref[...] = jnp.transpose(rows)
        out_ref[...] = jnp.zeros_like(out_ref)
        back_ref[...] = jnp.zeros_like(back_ref)

    w_gate, w_up, w_down = w_gate_ref[...], w_up_ref[...], w_down_ref[...]
    gate, up = nn(rows, w_gate), nn(rows, w_up)
    squashed = 1.0 / (1.0 + jnp.exp(-gate))
    silu = gate * squashed
    activated = (silu * up).astype(jnp.bfloat16)
    grad_act = nt(grads, w_down)
    grad_gate = (grad_act * up * (squashed * (1.0 + gate * (1.0 - squashed)))).astype(jnp.bfloat16)
    grad_up = (grad_act * silu).astype(jnp.bfloat16)
    out_ref[...] += nn(activated, w_down)
    grad_down_ref[...] = tn(activated, grads).astype(jnp.bfloat16)
    back_ref[...] += nt(grad_gate, w_gate) + nt(grad_up, w_up)
    grad_gu_ref[0] = nn(turned_ref[...], grad_gate).astype(jnp.bfloat16)
    grad_gu_ref[1] = nn(turned_ref[...], grad_up).astype(jnp.bfloat16)

    @pl.when(step == pl.num_programs(0) - 1)
    def _():
        shape = (both_ref.shape[0],) + both_ref.shape[2:]
        both_ref[:, 0] = out_ref[...].astype(jnp.bfloat16).reshape(shape)
        both_ref[:, 1] = back_ref[...].astype(jnp.bfloat16).reshape(shape)
        if mode == 1:
            line.finish()
            for trade in trades:
                trade.finish()
        if mode == 2:
            trades[1].start()

            def rest(o):
                line.pass_on(o, 3)
                line.finish(o)

            line.each_plane(rest)
            for trade in trades:
                trade.finish()


def experts(rows, grads, gate, up, down, mode=0, dp_count=0, extras=(), collective=None):
    owners, cap, width = rows.shape
    hidden = down.shape[0]
    count = owners * cap
    block = FF_BLOCK if count <= 1024 else FF_BLOCK // 4
    steps = hidden // block
    low = jnp.bfloat16
    pairs = pl.BlockSpec((owners, cap, width), lambda j: (0, 0, 0), pipeline_mode=pl.Buffered(1))
    anywhere = pl.BlockSpec(memory_space=pl.ANY)
    both = jax.ShapeDtypeStruct((owners, 2, cap, width), low)
    links = {"collective_id": collective, "has_side_effects": True} if mode else {}
    out_shape = [
        jax.ShapeDtypeStruct((2, width, hidden), low),
        jax.ShapeDtypeStruct((hidden, width), low),
    ]
    out_specs = [
        pl.BlockSpec((2, width, block), lambda j: (0, 0, j)),
        pl.BlockSpec((block, width), lambda j: (j, 0)),
    ]
    scratch = [
        pltpu.VMEM((width, count), low),
        pltpu.VMEM((count, width), jnp.float32),
        pltpu.VMEM((count, width), jnp.float32),
    ]
    if mode < 2:
        out_shape.append(both)
        out_specs.append(pl.BlockSpec(both.shape, lambda j: (0, 0, 0, 0)))
    if mode == 1:
        shards = extras[2]
        out_shape += [jax.ShapeDtypeStruct(rows.shape, low)] * 2
        out_shape.append(jax.ShapeDtypeStruct((dp_count * shards.shape[1], shards.shape[2]), low))
        out_specs += [anywhere] * 3
        scratch += gather_semaphores(dp_count) + trade_semaphores(owners) + trade_semaphores(owners)
    if mode == 2:
        total = (width // 8, 2 * hidden)
        out_shape += [both, both, jax.ShapeDtypeStruct(total, jnp.float32)]
        out_specs += [anywhere] * 2 + [pl.BlockSpec(total, lambda j: (0, 0))]
        scratch.append(pltpu.VMEM(both.shape, low))
        scratch += trade_semaphores(owners) + trade_semaphores(owners) + reduce_scratch([extras[1]])
    return pl.pallas_call(
        functools.partial(experts_kernel, mode, dp_count),
        grid=(steps,),
        out_shape=out_shape,
        in_specs=[
            pairs,
            pairs,
            pl.BlockSpec((width, block), lambda j: (0, j)),
            pl.BlockSpec((width, block), lambda j: (0, up.shape[1] // block - steps + j)),
            pl.BlockSpec((block, width), lambda j: (j, 0)),
        ]
        + [anywhere] * len(extras),
        out_specs=out_specs,
        scratch_shapes=scratch,
        compiler_params=pltpu.CompilerParams(
            dimension_semantics=("arbitrary",), vmem_limit_bytes=60 * 2**20, **links
        ),
        cost_estimate=pl.CostEstimate(
            flops=18 * count * width * hidden,
            bytes_accessed=12 * width * hidden + 8 * count * width,
            transcendentals=count * hidden,
        ),
        name="experts",
    )(rows, grads, gate, up, down, *extras)


def dp_grid(dp_count):
    outer = 4 if dp_count % 4 == 0 else 1
    return outer, dp_count // outer


def place():
    me, mine = lax.axis_index("dp"), lax.axis_index("expert")
    return me, mine


def greet(peers):
    barrier = pltpu.get_barrier_semaphore()
    for peer in peers:
        pl.semaphore_signal(barrier, inc=1, device_id=peer, device_id_type=MESH)
    pl.semaphore_wait(barrier, len(peers))


class LineGather:
    def __init__(self, shard, full, dp_count, send_sem, recv_sem, own_sem, columns=None, also=None):
        self.columns = slice(None) if columns is None else columns
        self.also = also or (lambda chunk: None)
        self.shard, self.full, self.dp_count = shard, full, dp_count
        self.send_sem, self.recv_sem, self.own_sem = send_sem, recv_sem, own_sem
        self.outer_count, self.inner_count = dp_grid(dp_count)
        self.me, self.mine = place()
        self.outer, self.inner = self.me // self.inner_count, self.me % self.inner_count
        self.inner_peers = [
            lax.rem(self.inner + k, self.inner_count) for k in range(1, self.inner_count)
        ]
        self.can_up, self.can_down = self.outer < self.outer_count - 1, self.outer > 0

    def peers(self):
        below = lax.rem(self.outer + self.outer_count - 1, self.outer_count)
        above = lax.rem(self.outer + 1, self.outer_count)
        return [(peer * self.inner_count + self.inner, self.mine) for peer in (below, above)] + [
            (self.outer * self.inner_count + peer, self.mine) for peer in self.inner_peers
        ]

    def spot(self, chunk):
        rows = self.shard.shape[0]
        return self.full.at[pl.ds(pl.multiple_of(chunk * rows, 8), rows), self.columns]

    def copy(self, source, chunk, device, way, at):
        return pltpu.make_async_remote_copy(
            src_ref=source,
            dst_ref=self.spot(chunk),
            send_sem=self.send_sem.at[way, at, chunk],
            recv_sem=self.recv_sem.at[chunk],
            device_id=(device, self.mine),
            device_id_type=MESH,
        )

    def up(self, source, chunk):
        return self.copy(source, chunk, (self.outer + 1) * self.inner_count + self.inner, 1, 0)

    def down(self, source, chunk):
        return self.copy(source, chunk, (self.outer - 1) * self.inner_count + self.inner, 2, 0)

    def across(self, source, chunk):
        return [
            self.copy(source, chunk, self.outer * self.inner_count + peer, 0, at)
            for at, peer in enumerate(self.inner_peers)
        ]

    def keep(self):
        return pltpu.make_async_copy(self.shard, self.spot(self.me), self.own_sem)

    def arrived(self, chunk):
        pltpu.make_async_copy(self.spot(chunk), self.spot(chunk), self.recv_sem.at[chunk]).wait()

    def start(self):
        for copy in self.across(self.shard, self.me):
            copy.start()
        pl.when(self.can_up)(lambda: self.up(self.shard, self.me).start())
        pl.when(self.can_down)(lambda: self.down(self.shard, self.me).start())
        self.keep().start()

    def relay(self, step):
        low, high = self.outer - step, self.outer + step

        def pass_on(source, upward):
            chunk = source * self.inner_count + self.inner
            self.arrived(chunk)
            if upward:
                pl.when(self.can_up)(lambda: self.up(self.spot(chunk), chunk).start())
            else:
                pl.when(self.can_down)(lambda: self.down(self.spot(chunk), chunk).start())
            for copy in self.across(self.spot(chunk), chunk):
                copy.start()
            self.also(chunk)

        pl.when(low >= 0)(lambda: pass_on(low, True))
        pl.when(high < self.outer_count)(lambda: pass_on(high, False))

    def finish(self):
        self.keep().wait()
        for peer in self.inner_peers:
            for k in range(self.outer_count):
                chunk = lax.rem(self.outer + k, self.outer_count) * self.inner_count + peer
                self.arrived(chunk)
                self.also(chunk)
        for plane in range(self.outer_count):
            chunk = plane * self.inner_count + self.inner
            for copy in self.across(self.spot(chunk), chunk):
                copy.wait_send()
            pl.when(self.can_up & (self.outer >= plane))(
                lambda chunk=chunk: self.up(self.spot(chunk), chunk).wait_send()
            )
            pl.when(self.can_down & (self.outer <= plane))(
                lambda chunk=chunk: self.down(self.spot(chunk), chunk).wait_send()
            )


def gather_semaphores(dp_count):
    inner_count = dp_grid(dp_count)[1]
    return [
        pltpu.SemaphoreType.DMA((3, max(1, inner_count - 1), dp_count)),
        pltpu.SemaphoreType.DMA((dp_count,)),
        pltpu.SemaphoreType.DMA,
    ]


def by_rows(count, body):
    def step(i, carry):
        body(i * 16)
        return carry

    lax.fori_loop(0, count // 16, step, 0)


class Trade:
    def __init__(self, source, target, send_sem, recv_sem):
        self.source, self.target, self.send_sem, self.recv_sem = source, target, send_sem, recv_sem
        self.me, self.mine = place()
        count = target.shape[0]
        self.partners = [lax.rem(self.mine + k, count) for k in range(1, count)]

    def peers(self):
        return [(self.me, peer) for peer in self.partners]

    def copy(self, k):
        peer = self.partners[k]
        return pltpu.make_async_remote_copy(
            src_ref=self.source.at[peer],
            dst_ref=self.target.at[self.mine],
            send_sem=self.send_sem.at[k + 1],
            recv_sem=self.recv_sem.at[self.mine],
            device_id=(self.me, peer),
            device_id_type=MESH,
        )

    def keep(self):
        return pltpu.make_async_copy(
            self.source.at[self.mine], self.target.at[self.mine], self.send_sem.at[0]
        )

    def start(self):
        for k in range(len(self.partners)):
            self.copy(k).start()
        self.keep().start()

    def finish(self):
        self.keep().wait()
        for k, peer in enumerate(self.partners):
            there = self.target.at[peer]
            pltpu.make_async_copy(there, there, self.recv_sem.at[peer]).wait()
            self.copy(k).wait_send()


def trade_semaphores(owner_count):
    return [pltpu.SemaphoreType.DMA((owner_count,)), pltpu.SemaphoreType.DMA((owner_count,))]


def expert_gather_kernel(dp_count, rows_ref, grads_ref, shards_ref, rows_out, grads_out, full_ref, *sems):
    line = LineGather(shards_ref.at[0], full_ref, dp_count, *sems[:3])
    trades = [Trade(rows_ref.at[0], rows_out, *sems[3:5]), Trade(grads_ref.at[0], grads_out, *sems[5:7])]
    greet(line.peers() + trades[0].peers())
    line.start()
    for trade in trades:
        trade.start()
    for hop in range(1, line.outer_count):
        line.relay(hop)
    line.finish()
    for trade in trades:
        trade.finish()


def expert_gather(rows, grads, shards, dp_count, collective):
    anywhere = pl.BlockSpec(memory_space=pl.ANY)
    return pl.pallas_call(
        functools.partial(expert_gather_kernel, dp_count),
        out_shape=[
            jax.ShapeDtypeStruct(rows.shape[1:], rows.dtype),
            jax.ShapeDtypeStruct(grads.shape[1:], grads.dtype),
            jax.ShapeDtypeStruct((dp_count * shards.shape[1], shards.shape[2]), shards.dtype),
        ],
        in_specs=[anywhere] * 3,
        out_specs=[anywhere] * 3,
        scratch_shapes=gather_semaphores(dp_count)
        + trade_semaphores(rows.shape[1])
        + trade_semaphores(rows.shape[1]),
        compiler_params=pltpu.CompilerParams(collective_id=collective, has_side_effects=True),
        name="expert_gather",
    )(rows, grads, shards)


def small_gather_kernel(
    dp_count, expert_count, shard_ref, routes_ref, full_ref, columns_ref, rows_ref,
    send_sem, recv_sem, own_sem, pass_sem, mate_sem, all_sem,
):
    me, mine = place()
    rows, columns = shard_ref.shape
    half = columns // 2
    side = mine % 2
    mate = mine + 1 - 2 * side
    own_columns = pl.ds(pl.multiple_of(side * half, 128), half)
    mate_columns = pl.ds(pl.multiple_of((1 - side) * half, 128), half)

    def there(chunk, lanes):
        return full_ref.at[pl.ds(pl.multiple_of(chunk * rows, 8), rows), lanes]

    def pass_copy(chunk):
        return pltpu.make_async_remote_copy(
            src_ref=there(chunk, own_columns),
            dst_ref=there(chunk, own_columns),
            send_sem=pass_sem.at[chunk],
            recv_sem=mate_sem.at[chunk],
            device_id=(me, mate),
            device_id_type=MESH,
        )

    line = LineGather(
        shard_ref.at[:, own_columns], full_ref, dp_count, send_sem, recv_sem, own_sem,
        own_columns, lambda chunk: pass_copy(chunk).start(),
    )
    greet(line.peers() + [(me, mate)])
    line.start()
    other = pltpu.make_async_copy(shard_ref.at[:, mate_columns], there(me, mate_columns), all_sem)
    other.start()
    routing_kernel(expert_count, routes_ref, columns_ref, rows_ref)
    for hop in range(1, line.outer_count):
        line.relay(hop)
    line.finish()
    other.wait()
    for k in range(1, dp_count):
        chunk = lax.rem(me + k, dp_count)
        target = there(chunk, mate_columns)
        pltpu.make_async_copy(target, target, mate_sem.at[chunk]).wait()
        pass_copy(chunk).wait_send()


def small_gather(shard, routes, expert_count, dp_count, collective):
    rows, columns = shard.shape
    tokens = routes.shape[0]
    anywhere, in_vmem = pl.BlockSpec(memory_space=pl.ANY), pl.BlockSpec(memory_space=pltpu.VMEM)
    return pl.pallas_call(
        functools.partial(small_gather_kernel, dp_count, expert_count),
        out_shape=[
            jax.ShapeDtypeStruct((dp_count * rows, columns), shard.dtype),
            jax.ShapeDtypeStruct((tokens, 128), jnp.int32),
            jax.ShapeDtypeStruct((8, tokens), jnp.int32),
        ],
        in_specs=[anywhere, in_vmem],
        out_specs=[anywhere, in_vmem, in_vmem],
        scratch_shapes=gather_semaphores(dp_count)
        + [
            pltpu.SemaphoreType.DMA((dp_count,)),
            pltpu.SemaphoreType.DMA((dp_count,)),
            pltpu.SemaphoreType.DMA,
        ],
        compiler_params=pltpu.CompilerParams(
            collective_id=collective, has_side_effects=True, vmem_limit_bytes=60 * 2**20
        ),
        name="small_gather",
    )(shard, routes)


class LineReduce:
    def __init__(self, sources, totals, owns, ins, lows, highs, own_sem, in_send, in_recv, line_send, line_recv):
        self.sources, self.totals = sources, totals
        self.owns, self.ins, self.lows, self.highs = owns, ins, lows, highs
        self.own_sem, self.in_send, self.in_recv = own_sem, in_send, in_recv
        self.line_send, self.line_recv = line_send, line_recv
        self.me, self.mine = place()
        self.outer, self.inner = self.me // 2, self.me % 2
        self.every = range(len(sources))

    def peers(self):
        low, high = lax.rem(self.outer + 3, 4), lax.rem(self.outer + 1, 4)
        return [
            (self.me + 1 - 2 * self.inner, self.mine),
            (low * 2 + self.inner, self.mine),
            (high * 2 + self.inner, self.mine),
        ]

    def order(self, o):
        return sorted(range(4), key=lambda plane: (-abs(plane - o), plane))

    def chunk(self, p, at):
        source = self.sources[p]
        rows = self.owns[p].shape[-2]
        here = pl.ds(pl.multiple_of(at * rows, 16), rows)
        return source.at[:, here, :] if len(source.shape) == 3 else source.at[here, :]

    def own_copy(self, p, plane):
        return pltpu.make_async_copy(
            self.chunk(p, plane * 2 + self.inner), self.owns[p].at[plane], self.own_sem.at[p, plane]
        )

    def in_copy(self, p, plane):
        return pltpu.make_async_remote_copy(
            src_ref=self.chunk(p, plane * 2 + 1 - self.inner),
            dst_ref=self.ins[p].at[plane],
            send_sem=self.in_send.at[p, plane],
            recv_sem=self.in_recv.at[p, plane],
            device_id=(self.me + 1 - 2 * self.inner, self.mine),
            device_id_type=MESH,
        )

    def line_copy(self, p, plane, upward, device_plane):
        target = self.lows[p].at[plane - 1] if upward else self.highs[p].at[plane]
        return pltpu.make_async_remote_copy(
            src_ref=self.ins[p].at[plane],
            dst_ref=target,
            send_sem=self.line_send.at[p, 0 if upward else 1, plane],
            recv_sem=self.line_recv.at[p, 0 if upward else 1, plane],
            device_id=(device_plane * 2 + self.inner, self.mine),
            device_id_type=MESH,
        )

    def start(self, o):
        for plane in self.order(o):
            for p in self.every:
                self.in_copy(p, plane).start()
        for plane in self.order(o):
            for p in self.every:
                self.own_copy(p, plane).start()

    def line_start(self, o, p, plane):
        return self.line_copy(p, plane, plane > o, o + 1 if plane > o else o - 1)

    def pass_on(self, o, k):
        plane = self.order(o)[k]
        for p in self.every:
            self.own_copy(p, plane).wait()
            self.in_copy(p, plane).wait_recv()
            terms = [self.owns[p].at[plane]]
            if o > 0 and plane >= o:
                self.line_copy(p, plane, True, o).wait_recv()
                terms.append(self.lows[p].at[plane - 1])
            if o < 3 and plane <= o:
                self.line_copy(p, plane, False, o).wait_recv()
                terms.append(self.highs[p].at[plane])
            held = self.ins[p].at[plane]
            last = plane == o
            sides = held.shape[0] if len(held.shape) == 3 else 0

            def body(at, p=p, terms=terms, held=held, last=last, sides=sides):
                here = pl.ds(pl.multiple_of(at, 16), 16)
                for side in range(max(1, sides)):
                    spot = (side, here) if sides else (here,)
                    total = held[spot].astype(jnp.float32)
                    for term in terms:
                        total = total + term[spot].astype(jnp.float32)
                    if last:
                        size = total.shape[-1]
                        self.totals[p][here, side * size : (side + 1) * size] = total
                    else:
                        held[spot] = total.astype(held.dtype)

            by_rows(held.shape[-2], body)
            if not last:
                self.line_start(o, p, plane).start()

    def finish(self, o):
        for plane in range(4):
            for p in self.every:
                self.in_copy(p, plane).wait_send()
                if plane != o:
                    self.line_start(o, p, plane).wait_send()

    def each_plane(self, body):
        for o in range(4):
            pl.when(self.outer == o)(functools.partial(body, o))


def reduce_scratch(sources):
    shapes = []
    for planes in (4, 4, 3, 3):
        for source in sources:
            rows = source.shape[-2] // 8
            shapes.append(pltpu.VMEM((planes,) + source.shape[:-2] + (rows, source.shape[-1]), jnp.bfloat16))
    count = len(sources)
    return shapes + [
        pltpu.SemaphoreType.DMA((count, 4)),
        pltpu.SemaphoreType.DMA((count, 4)),
        pltpu.SemaphoreType.DMA((count, 4)),
        pltpu.SemaphoreType.DMA((count, 2, 4)),
        pltpu.SemaphoreType.DMA((count, 2, 4)),
    ]


def line_reduce(sources, totals, scratch):
    count = len(sources)
    buffers = [scratch[n * count : (n + 1) * count] for n in range(4)]
    return LineReduce(sources, totals, *buffers, *scratch[4 * count :])


def final_reduce_kernel(small_count, *refs):
    small_refs, refs = refs[:small_count], refs[small_count:]
    (
        small_out, swap, small_in, small_low, small_high, final_low, final_in,
        swap_send, swap_recv, in_send, in_recv, line_send, line_recv, last_send, last_recv,
    ) = refs
    outer_count, inner_count = 4, 2
    me, mine = place()
    outer, inner = me // inner_count, me % inner_count
    side = mine % 2
    mate, across = mine + 1 - 2 * side, lax.rem(mine + 2, 4)
    beside = me + 1 - 2 * inner
    half_rows = small_refs[0].shape[1] // 2
    starts = [sum(ref.shape[2] for ref in small_refs[:n]) for n in range(small_count + 1)]

    def remote(source, target, device, send_at, recv_at):
        return pltpu.make_async_remote_copy(
            src_ref=source,
            dst_ref=target,
            send_sem=send_at,
            recv_sem=recv_at,
            device_id=device,
            device_id_type=MESH,
        )

    low_peer = lax.rem(outer + outer_count - 1, outer_count) * inner_count + inner
    high_peer = lax.rem(outer + 1, outer_count) * inner_count + inner
    greet([(me, mate), (me, across), (beside, mine), (low_peer, mine), (high_peer, mine)])

    mate_rows = pl.ds(pl.multiple_of((1 - side) * half_rows, 16), half_rows)
    own_rows = pl.ds(pl.multiple_of(side * half_rows, 16), half_rows)

    def swap_copy(n):
        return remote(
            small_refs[n].at[:, mate_rows, :],
            swap.at[:, :, starts[n] : starts[n + 1]],
            (me, mate),
            swap_send.at[n],
            swap_recv.at[n],
        )

    def inner_copy(plane):
        return remote(
            swap.at[plane * inner_count + 1 - inner],
            small_in.at[plane],
            (beside, mine),
            in_send.at[plane],
            in_recv.at[plane],
        )

    def line_copy(plane, upward, device_plane):
        way = 0 if upward else 1
        return remote(
            small_in.at[plane],
            (small_low if upward else small_high).at[plane],
            (device_plane * inner_count + inner, mine),
            line_send.at[way, plane],
            line_recv.at[way, plane],
        )

    def wide(values):
        return values.astype(jnp.float32)

    def add_own(chunk):
        def body(at):
            here = pl.ds(pl.multiple_of(at, 16), 16)
            there = pl.ds(pl.multiple_of(side * half_rows + at, 16), 16)
            for n in range(small_count):
                columns = slice(starts[n], starts[n + 1])
                swap[chunk, here, columns] = (
                    wide(swap[chunk, here, columns]) + wide(small_refs[n][chunk, there, :])
                ).astype(swap.dtype)

        by_rows(half_rows, body)

    def at_plane(o):
        order = sorted(range(outer_count), key=lambda t: (-abs(t - o), t))

        def line_start(plane):
            return line_copy(plane, plane > o, o + 1 if plane > o else o - 1)

        for n in range(small_count):
            swap_copy(n).start()
        for n in range(small_count):
            swap_copy(n).wait_recv()
        for plane in order:
            add_own(plane * inner_count + 1 - inner)
            inner_copy(plane).start()
        for plane in order:
            add_own(plane * inner_count + inner)
            inner_copy(plane).wait_recv()
            terms = [swap.at[plane * inner_count + inner]]
            if o > 0 and plane >= o:
                line_copy(plane, True, o).wait_recv()
                terms.append(small_low.at[plane])
            if o < outer_count - 1 and plane <= o:
                line_copy(plane, False, o).wait_recv()
                terms.append(small_high.at[plane])
            target = final_low if plane == o else small_in.at[plane]

            def gather(at, plane=plane, terms=terms, target=target):
                here = pl.ds(pl.multiple_of(at, 16), 16)
                total = wide(small_in[plane, here, :])
                for term in terms:
                    total = total + wide(term[here, :])
                target[here, :] = total.astype(target.dtype)

            by_rows(half_rows, gather)
            if plane != o:
                line_start(plane).start()
        remote(final_low, final_in, (me, across), last_send.at[0], last_recv.at[0]).start()
        for plane in range(outer_count):
            inner_copy(plane).wait_send()
            if plane != o:
                line_start(plane).wait_send()
        for n in range(small_count):
            swap_copy(n).wait_send()

    for o in range(outer_count):
        pl.when(outer == o)(functools.partial(at_plane, o))
    remote(final_low, final_in, (me, across), last_send.at[0], last_recv.at[0]).wait()

    def total_body(at):
        here = pl.ds(pl.multiple_of(at, 16), 16)
        there = pl.ds(pl.multiple_of(side * half_rows + at, 16), 16)
        small_out[there, :] = wide(final_low[here, :]) + wide(final_in[here, :])

    by_rows(half_rows, total_body)
    mate_copy = remote(
        small_out.at[own_rows, :], small_out.at[own_rows, :], (me, mate), last_send.at[1], last_recv.at[1]
    )
    mate_copy.start()
    mate_copy.wait()


def final_reduce(smalls, collective):
    chunk_count, small_rows, _ = smalls[0].shape
    small_columns = sum(small.shape[2] for small in smalls)
    low = jnp.bfloat16
    planes = 4
    in_vmem = pl.BlockSpec(memory_space=pltpu.VMEM)
    half = small_rows // 2
    return pl.pallas_call(
        functools.partial(final_reduce_kernel, len(smalls)),
        out_shape=jax.ShapeDtypeStruct((small_rows, small_columns), jnp.float32),
        in_specs=[in_vmem] * len(smalls),
        out_specs=in_vmem,
        scratch_shapes=[pltpu.VMEM((chunk_count, half, small_columns), low)]
        + [pltpu.VMEM((planes, half, small_columns), low)] * 3
        + [pltpu.VMEM((half, small_columns), low)] * 2
        + [
            pltpu.SemaphoreType.DMA((len(smalls),)),
            pltpu.SemaphoreType.DMA((len(smalls),)),
            pltpu.SemaphoreType.DMA((planes,)),
            pltpu.SemaphoreType.DMA((planes,)),
            pltpu.SemaphoreType.DMA((2, planes)),
            pltpu.SemaphoreType.DMA((2, planes)),
            pltpu.SemaphoreType.DMA((2,)),
            pltpu.SemaphoreType.DMA((2,)),
        ],
        compiler_params=pltpu.CompilerParams(
            collective_id=collective, has_side_effects=True, vmem_limit_bytes=40 * 2**20
        ),
        name="final_reduce",
    )(*smalls)


def shards(
    tokens,
    resid_logits,
    routes,
    doc_ids,
    w_qkv,
    w_out,
    gain_attn,
    gain_ffn,
    w_router,
    w_const,
    v_const,
    w_gate_up,
    w_down,
    out_grad,
):
    dp_count, owner_count = lax.axis_size("dp"), lax.axis_size("expert")
    own_links = dp_count == 8 and owner_count == 4 and w_gate_up.shape[0] == 2
    seq_count, length, width = tokens.shape
    assert seq_count == 1
    rows = seq_count * length
    choice_count = resid_logits.shape[-1]
    local_count = w_gate_up.shape[0]
    expert_count = owner_count * local_count
    hidden_count = w_down.shape[1] * dp_count
    width_qkv, width_out = w_qkv.shape[1], w_out.shape[1]
    small_parts = [w_router, w_const, v_const, gain_attn[:, None], gain_ffn[:, None]]
    small_width = sum(part.shape[1] for part in small_parts)
    pad = jnp.zeros((w_qkv.shape[0], 256 - small_width), jnp.bfloat16)
    packed = jnp.concatenate([w_qkv, w_out] + small_parts + [pad], 1)
    inputs = tokens.reshape(rows, width)
    cot = out_grad.reshape(rows, width)
    route_rows = routes.reshape(rows, 2)
    cosine, sine = rotary_lanes(length, width // HEADS)
    docs_row, docs_column = doc_ids.reshape(1, rows), doc_ids.reshape(rows, 1)
    resid = jnp.pad(
        resid_logits.reshape(rows, choice_count).astype(jnp.float32), ((0, 0), (0, 128 - choice_count))
    )
    if own_links:
        packed_full, spots, spot_rows = small_gather(packed, route_rows, expert_count, dp_count, 1)
    else:
        spots, spot_rows = routing(route_rows, expert_count)
        packed_full = lax.all_gather(packed, "dp", axis=0, tiled=True)
    gather = functools.partial(lax.all_gather, axis_name="dp", axis=0, tiled=True)
    if own_links:
        first_gate_up, packed_full = lax.optimization_barrier((w_gate_up[0], packed_full))
        first_gate_up = gather(first_gate_up)
    else:
        first_gate_up = gather(w_gate_up[0])
    attend = functools.partial(
        attention_forward, inputs, packed_full, docs_row, docs_column, cosine, sine, route_rows, resid
    )
    if own_links:
        *forward, second_down = attend(w_down, dp_count, 5)
    else:
        forward = attend()
    normed_one, queries, keys, values, attended, middle, normed_two, aux = forward
    send_rows, send_grads = dispatch(spot_rows, aux, normed_two, cot, owner_count, local_count)
    if own_links:
        rows_in, grads_in, first_down = expert_gather(send_rows, send_grads, w_down, dp_count, 2)
        grad_gu, grad_down, both, next_rows, next_grads, second_gate_up = experts(
            rows_in, grads_in, first_gate_up, first_gate_up, first_down, 1, dp_count,
            [send_rows, send_grads, w_gate_up], 6,
        )
        down_parts = [lax.psum_scatter(grad_down, "dp", scatter_dimension=0, tiled=True)]
        second_gu, grad_down, *parts, gu_part = experts(
            next_rows, next_grads, second_gate_up, second_gate_up, second_down, 2, dp_count,
            [both, grad_gu], 4,
        )
        parts, down_parts[0] = lax.optimization_barrier((parts, down_parts[0]))
        down_parts.append(lax.psum_scatter(grad_down, "dp", scatter_dimension=0, tiled=True))
        gu_parts = [gu_part]
    else:
        exchange = functools.partial(
            lax.all_to_all, axis_name="expert", split_axis=0, concat_axis=0, tiled=True
        )
        parts, gu_parts, down_parts = [], [], []
        for e in range(local_count):
            gate_up = first_gate_up if e == 0 else gather(w_gate_up[e])
            grad_gu, grad_down, both = experts(
                exchange(send_rows[e]), exchange(send_grads[e]), gate_up, gate_up, gather(w_down[e])
            )
            parts.append(exchange(both))
            gu_part = lax.psum_scatter(grad_gu, "dp", scatter_dimension=1, tiled=True)
            gu_parts.append(jnp.concatenate([gu_part[0], gu_part[1]], -1).astype(jnp.float32))
            down_parts.append(lax.psum_scatter(grad_down, "dp", scatter_dimension=0, tiled=True))
    down_parts = [part.astype(jnp.float32) for part in down_parts]
    output, logit_grad, grad_middle, small_grad = combine(
        parts, spots, route_rows, aux, normed_two, middle, cot, packed_full, choice_count, expert_count
    )
    backward = functools.partial(
        attention_backward, grad_middle, queries, keys, values, attended, normed_one, inputs,
        packed_full, docs_row, docs_column, cosine, sine, small_grad,
    )
    if own_links:
        token_grad, *weight_grads, gu_part = backward([second_gu], 7)
        gu_parts.append(gu_part)
        packed_part = final_reduce(
            [grad.reshape(dp_count, width // dp_count, grad.shape[1]) for grad in weight_grads], 3
        )
    else:
        token_grad, *weight_grads = backward()
        packed_part = lax.psum_scatter(
            jnp.concatenate(weight_grads, 1), "dp", scatter_dimension=0, tiled=True
        )
        packed_part = lax.psum(packed_part, "expert").astype(jnp.float32)
    part_qkv = packed_part[:, :width_qkv]
    part_out = packed_part[:, width_qkv : width_qkv + width_out]
    small_part = packed_part[:, width_qkv + width_out :]
    return (
        output.reshape(tokens.shape),
        token_grad.reshape(tokens.shape),
        logit_grad.reshape(resid_logits.shape),
        part_qkv,
        part_out,
        small_part[:, 18],
        small_part[:, 19],
        small_part[:, 0:12],
        small_part[:, 12:16],
        small_part[:, 16:18],
        jnp.stack(gu_parts),
        jnp.stack(down_parts),
    )


def solution(mesh):
    placed = (
        P(("dp", "expert"), None, None),
        P(("dp", "expert"), None, None),
        P(("dp", "expert"), None, None),
        P(("dp", "expert"), None),
        P("dp", None),
        P("dp", None),
        P("dp"),
        P("dp"),
        P("dp", None),
        P("dp", None),
        P("dp", None),
        P("expert", "dp", None),
        P("expert", "dp", None),
        P(("dp", "expert"), None, None),
    )
    return jax.shard_map(
        shards,
        mesh=mesh,
        in_specs=placed,
        out_specs=(
            P(("dp", "expert"), None, None),
            P(("dp", "expert"), None, None),
            P(("dp", "expert"), None, None),
            P("dp", None),
            P("dp", None),
            P("dp"),
            P("dp"),
            P("dp", None),
            P("dp", None),
            P("dp", None),
            P("expert", "dp", None),
            P("expert", "dp", None),
        ),
        check_vma=False,
    )
```

```python
import functools

import jax
import jax.numpy as jnp
import numpy as np
from jax import lax
from jax.experimental import pallas as pl
from jax.experimental.pallas import tpu as pltpu
from jax.sharding import PartitionSpec as P

HEADS = 12
BLOCK = 256
CAP = 256
GROUP = 256
FF_BLOCK = 256
MESH = pl.DeviceIdType.MESH
epsilon = 1e-06


def rotary_lanes(length, head_dim):
    half_dim = head_dim // 2
    frequency = (10000.0 ** (-np.arange(half_dim, dtype=np.float32) / half_dim)).astype(np.float32)
    angles = (np.arange(length, dtype=np.float32)[:, None] * frequency[None, :]).astype(np.float64)
    cosine = np.cos(angles).astype(np.float32)
    sine = np.sin(angles).astype(np.float32)
    return (
        np.concatenate([cosine] * 4, 1),
        np.concatenate([-sine, sine, -sine, sine], 1),
    )


def nt(left, right):
    return lax.dot_general(left, right, (((1,), (1,)), ((), ())), preferred_element_type=jnp.float32)


def tn(left, right):
    return lax.dot_general(left, right, (((0,), (0,)), ((), ())), preferred_element_type=jnp.float32)


def nn(left, right):
    return jnp.dot(left, right, preferred_element_type=jnp.float32)


def lane_ids(shape):
    return lax.broadcasted_iota(jnp.int32, shape, len(shape) - 1)


def turn(values, cosine, sine):
    lanes = lane_ids(values.shape)
    ahead, behind = pltpu.roll(values, 96, 1), pltpu.roll(values, 32, 1)
    return values * cosine + jnp.where(lanes % 64 < 32, ahead, behind) * sine


def key_span(i):
    return max(0, i - 2) * BLOCK, (i + 1) * BLOCK


def mask_of(docs_column, docs_row, i):
    low, high = key_span(i)
    return docs_column[low:high, :] == docs_row[:, i * BLOCK : (i + 1) * BLOCK]


def attention_forward_kernel(linked, *refs):
    (
        tokens_ref, wq_ref, wk_ref, wv_ref, wo_ref, small_ref, docs_row_ref, docs_column_ref,
        cosine_ref, sine_ref, routes_ref, resid_ref,
    ) = refs[:12]
    (
        normed_ref, q_ref, k_ref, v_ref, attended_ref, middle_ref, normed_two_ref, aux_ref,
    ) = refs[12 + bool(linked) : 20 + bool(linked)]
    step = pl.program_id(0)
    rows = tokens_ref.shape[0]
    if linked:
        branch_ref = refs[22]
        line = PairGather(refs[12].at[0], refs[21], linked, refs[23:])

        @pl.when(step == 0)
        def _():
            greet(line.peers())
            line.start()

        for hop in range(1, 3):
            pl.when(step == hop)(functools.partial(line.relay, hop))
    else:
        branch_ref = refs[20]

    @pl.when(step == 0)
    def _():
        inputs = tokens_ref[...].astype(jnp.float32)
        gains = jnp.transpose(small_ref[:, :128].astype(jnp.float32))[18:19, :]
        scale = lax.rsqrt(jnp.mean(inputs * inputs, -1, keepdims=True) + epsilon)
        normed_ref[...] = (inputs * scale * gains).astype(jnp.bfloat16)
        branch_ref[...] = jnp.zeros_like(branch_ref)

    normed = normed_ref[...]
    cosine, sine = cosine_ref[...], sine_ref[...]
    for w_ref, out_ref, turned in ((wq_ref, q_ref, True), (wk_ref, k_ref, True), (wv_ref, v_ref, False)):
        projected = nn(normed, w_ref[...])
        for half in range(2):
            part = projected[:, half * 128 : half * 128 + 128]
            if turned:
                part = turn(part, cosine, sine)
            out_ref[:, half * 128 : half * 128 + 128] = part.astype(jnp.bfloat16)

    docs_row, docs_column = docs_row_ref[...], docs_column_ref[...]
    for i in range(rows // BLOCK):
        low, high = key_span(i)
        here = slice(i * BLOCK, (i + 1) * BLOCK)
        allowed = mask_of(docs_column, docs_row, i)
        for pair in range(2):
            lanes = slice(pair * 128, pair * 128 + 128)
            queries = q_ref[here, lanes] * jnp.asarray(0.125, jnp.bfloat16)
            keys, values = k_ref[low:high, lanes], v_ref[low:high, lanes]
            left = lane_ids(queries.shape) < 64
            outs = []
            for head in range(2):
                own = left if head == 0 else jnp.logical_not(left)
                scores = nt(keys, jnp.where(own, queries, jnp.zeros_like(queries)))
                scores = jnp.where(allowed, scores, -1e30)
                shifted = jnp.exp(scores - jnp.max(scores, 0, keepdims=True))
                probs = shifted * (1.0 / jnp.sum(shifted, 0, keepdims=True))
                outs.append(tn(probs.astype(jnp.bfloat16), values))
            attended_ref[here, lanes] = jnp.where(left, outs[0], outs[1]).astype(jnp.bfloat16)
    branch_ref[...] += nn(attended_ref[...], wo_ref[...])

    @pl.when(step == pl.num_programs(0) - 1)
    def _():
        small = small_ref[:, :128]
        gains = jnp.transpose(small.astype(jnp.float32))[19:20, :]
        middle = tokens_ref[...].astype(jnp.float32) + branch_ref[...]
        middle_ref[...] = middle
        scale = lax.rsqrt(jnp.mean(middle * middle, -1, keepdims=True) + epsilon)
        normed_two = (middle * scale * gains).astype(jnp.bfloat16)
        normed_two_ref[...] = normed_two
        logits = nn(normed_two, small) + resid_ref[...].astype(jnp.float32)
        lanes = lane_ids(logits.shape)

        def lane(at):
            return jnp.sum(jnp.where(lanes == at, logits, 0.0), -1, keepdims=True)

        def two(first, second):
            peak = jnp.maximum(first, second)
            first, second = jnp.exp(first - peak), jnp.exp(second - peak)
            return first / (first + second), second / (first + second)

        columns = list(two(lane(routes_ref[:, 0:1]), lane(routes_ref[:, 1:2])))
        columns += list(two(lane(12), lane(13))) + list(two(lane(14), lane(15)))
        columns.append(scale)
        aux = jnp.zeros_like(logits)
        for at, column in enumerate(columns):
            aux = jnp.where(lanes == at, column, aux)
        aux_ref[...] = aux
        if linked:
            line.relay(3)
            line.finish()


def attention_forward(
    tokens, packed, docs_row, docs_column, cosine, sine, routes, resid, shards=None,
    dp_count=None, collective=None,
):
    rows, width = tokens.shape
    groups = width // GROUP
    low = jnp.bfloat16
    whole = lambda shape: pl.BlockSpec(shape, lambda j: (0, 0))
    column = lambda at: pl.BlockSpec((width, GROUP), lambda j: (0, at + j))
    out_column = pl.BlockSpec((rows, GROUP), lambda j: (0, j))
    full = jax.ShapeDtypeStruct((rows, width), low)
    linked = shards is not None
    anywhere = pl.BlockSpec(memory_space=pl.ANY)
    links = {"collective_id": collective, "has_side_effects": True} if linked else {}
    gathered = []
    if linked:
        gathered = [jax.ShapeDtypeStruct((dp_count * shards.shape[1], shards.shape[2]), low)]
    return pl.pallas_call(
        functools.partial(attention_forward_kernel, dp_count if linked else 0),
        grid=(groups,),
        out_shape=[full] * 5
        + [
            jax.ShapeDtypeStruct((rows, width), jnp.float32),
            full,
            jax.ShapeDtypeStruct((rows, 128), jnp.float32),
        ]
        + gathered,
        in_specs=[
            whole((rows, width)),
            column(0),
            column(groups),
            column(2 * groups),
            pl.BlockSpec((GROUP, width), lambda j: (j, 3)),
            pl.BlockSpec((width, 256), lambda j: (0, 12)),
            whole((1, rows)),
            whole((rows, 1)),
            whole((rows, 128)),
            whole((rows, 128)),
            whole((rows, 2)),
            whole((rows, 128)),
        ]
        + [anywhere] * linked,
        out_specs=[whole((rows, width))]
        + [out_column] * 4
        + [whole((rows, width)), whole((rows, width)), whole((rows, 128))]
        + [anywhere] * linked,
        scratch_shapes=[pltpu.VMEM((rows, width), jnp.float32)]
        + (pair_semaphores(dp_count) if linked else []),
        compiler_params=pltpu.CompilerParams(
            dimension_semantics=("arbitrary",), vmem_limit_bytes=56 * 2**20, **links
        ),
        cost_estimate=pl.CostEstimate(
            flops=2 * rows * width * 4 * width + 8 * rows * rows * width // 2,
            bytes_accessed=24 * rows * width,
            transcendentals=rows * rows * HEADS // 2,
        ),
        name="attention_forward",
    )(
        tokens, packed, packed, packed, packed, packed, docs_row, docs_column, cosine, sine, routes,
        resid, *([shards] if linked else []),
    )


def attention_backward_kernel(count, *refs):
    (
        grad_middle_ref, q_ref, k_ref, v_ref, attended_ref, normed_ref, tokens_ref,
        wq_ref, wk_ref, wv_ref, wo_ref, small_ref, docs_row_ref, docs_column_ref,
        cosine_ref, sine_ref, small_grad_ref,
    ) = refs[:17]
    sources, refs = refs[17 : 17 + count], refs[17 + count :]
    token_grad_ref, gq_ref, gk_ref, gv_ref, go_ref, small_out_ref = refs[:6]
    totals, refs = refs[6 : 6 + count], refs[6 + count :]
    branch_ref, back_ref, turned_ref, key_acc, value_acc, query_acc = refs[:6]
    step = pl.program_id(0)
    rows, width = tokens_ref.shape
    if count:
        line = GroupReduce(sources, totals, refs[6:])

        @pl.when(step == 0)
        def _():
            greet(line.peers())
            line.start()

        pl.when(step == 2)(lambda: line.pass_on(0))

    @pl.when(step == 0)
    def _():
        branch_ref[...] = grad_middle_ref[...].astype(jnp.bfloat16)
        back_ref[...] = jnp.zeros_like(back_ref)

    grad_branch = branch_ref[...]
    grad_attended = nt(grad_branch, wo_ref[...]).astype(jnp.bfloat16)
    go_ref[...] = tn(attended_ref[...], grad_branch).astype(jnp.bfloat16)
    cosine, sine = cosine_ref[...], sine_ref[...]
    docs_row, docs_column = docs_row_ref[...], docs_column_ref[...]
    for pair in range(2):
        lanes = slice(pair * 128, pair * 128 + 128)
        key_acc[...] = jnp.zeros_like(key_acc)
        value_acc[...] = jnp.zeros_like(value_acc)
        for i in range(rows // BLOCK):
            low, high = key_span(i)
            here = slice(i * BLOCK, (i + 1) * BLOCK)
            allowed = mask_of(docs_column, docs_row, i)
            queries = q_ref[here, lanes] * jnp.asarray(0.125, jnp.bfloat16)
            grads = grad_attended[here, lanes]
            keys, values = k_ref[low:high, lanes], v_ref[low:high, lanes]
            left = lane_ids(queries.shape) < 64
            query_grads = []
            key_grad, value_grad = None, None
            for head in range(2):
                own = left if head == 0 else jnp.logical_not(left)
                own_queries = jnp.where(own, queries, jnp.zeros_like(queries))
                own_grads = jnp.where(own, grads, jnp.zeros_like(grads))
                scores = jnp.where(allowed, nt(keys, own_queries), -1e30)
                shifted = jnp.exp(scores - jnp.max(scores, 0, keepdims=True))
                probs = shifted * (1.0 / jnp.sum(shifted, 0, keepdims=True))
                grad_probs = nt(values, own_grads)
                inner = jnp.sum(probs * grad_probs, 0, keepdims=True)
                grad_scores = (probs * (grad_probs - inner)).astype(jnp.bfloat16)
                part_value = nn(probs.astype(jnp.bfloat16), own_grads)
                part_key = nn(grad_scores, own_queries)
                value_grad = part_value if head == 0 else value_grad + part_value
                key_grad = part_key if head == 0 else key_grad + part_key
                query_grads.append(tn(grad_scores, keys))
            value_acc[low:high, :] += value_grad
            key_acc[low:high, :] += key_grad
            query_acc[here, :] = jnp.where(left, query_grads[0], query_grads[1]) * 0.125
        turned_ref[0, :, lanes] = turn(query_acc[...], cosine, -sine).astype(jnp.bfloat16)
        turned_ref[1, :, lanes] = turn(key_acc[...], cosine, -sine).astype(jnp.bfloat16)
        turned_ref[2, :, lanes] = value_acc[...].astype(jnp.bfloat16)
    normed = normed_ref[...]
    for at, (w_ref, out_ref) in enumerate(((wq_ref, gq_ref), (wk_ref, gk_ref), (wv_ref, gv_ref))):
        turned = turned_ref[at]
        out_ref[...] = tn(normed, turned).astype(jnp.bfloat16)
        back_ref[...] += nt(turned, w_ref[...])

    @pl.when(step == pl.num_programs(0) - 1)
    def _():
        gains = jnp.transpose(small_ref[:, :128].astype(jnp.float32))[18:19, :]
        inputs = tokens_ref[...].astype(jnp.float32)
        grads = back_ref[...]
        scale = lax.rsqrt(jnp.mean(inputs * inputs, -1, keepdims=True) + epsilon)
        weighted = grads * gains
        mean = jnp.mean(weighted * inputs, -1, keepdims=True)
        grad_inputs = scale * weighted - inputs * (scale * scale * scale * mean)
        token_grad_ref[...] = (grad_inputs + grad_middle_ref[...]).astype(jnp.bfloat16)
        gain_grad = jnp.sum(grads * inputs * scale, 0, keepdims=True)
        column = jnp.transpose(jnp.broadcast_to(gain_grad, (128, width)))
        small_grad = small_grad_ref[...]
        small_grad = jnp.where(lane_ids(small_grad.shape) == 18, column, small_grad)
        small_out_ref[:, :128] = small_grad.astype(jnp.bfloat16)
        small_out_ref[:, 128:] = jnp.zeros((width, 128), jnp.bfloat16)
        if count:
            for k in range(1, 4):
                line.pass_on(k)
            line.finish()


def attention_backward(
    grad_middle, queries, keys, values, attended, normed, tokens, packed, docs_row, docs_column,
    cosine, sine, small_grad, sources=(), collective=None,
):
    rows, width = tokens.shape
    groups = width // GROUP
    low = jnp.bfloat16
    whole = lambda shape: pl.BlockSpec(shape, lambda j: (0, 0))
    column = lambda at: pl.BlockSpec((width, GROUP), lambda j: (0, at + j))
    by_group = pl.BlockSpec((rows, GROUP), lambda j: (0, j))
    weight = jax.ShapeDtypeStruct((width, width), low)
    linked = len(sources) > 0
    links = {"collective_id": collective, "has_side_effects": True} if linked else {}
    sums = []
    for source in sources:
        sides = source.shape[0] if len(source.shape) == 3 else 1
        sums.append((source.shape[-2] // 8, sides * source.shape[-1]))
    once = lambda shape: pl.BlockSpec(
        shape, lambda j: (0, 0), pipeline_mode=pl.Buffered(1)
    )
    return pl.pallas_call(
        functools.partial(attention_backward_kernel, len(sources)),
        grid=(groups,),
        out_shape=[jax.ShapeDtypeStruct((rows, width), low)]
        + [weight] * 4
        + [jax.ShapeDtypeStruct((width, 256), low)]
        + [jax.ShapeDtypeStruct(shape, jnp.float32) for shape in sums],
        in_specs=[
            once((rows, width)),
            by_group,
            by_group,
            by_group,
            by_group,
            once((rows, width)),
            once((rows, width)),
            column(0),
            column(groups),
            column(2 * groups),
            pl.BlockSpec((GROUP, width), lambda j: (j, 3)),
            pl.BlockSpec((width, 256), lambda j: (0, 12)),
            once((1, rows)),
            once((rows, 1)),
            once((rows, 128)),
            once((rows, 128)),
            once((width, 128)),
        ]
        + [pl.BlockSpec(memory_space=pl.ANY)] * len(sources),
        out_specs=[
            whole((rows, width)),
            column(0),
            column(0),
            column(0),
            pl.BlockSpec((GROUP, width), lambda j: (j, 0)),
            whole((width, 256)),
        ]
        + [whole(shape) for shape in sums],
        scratch_shapes=[
            pltpu.VMEM((rows, width), low),
            pltpu.VMEM((rows, width), jnp.float32),
            pltpu.VMEM((3, rows, GROUP), low),
            pltpu.VMEM((rows, 128), jnp.float32),
            pltpu.VMEM((rows, 128), jnp.float32),
            pltpu.VMEM((rows, 128), jnp.float32),
        ]
        + [shape for source in sources for shape in reduce_scratch(source)],
        compiler_params=pltpu.CompilerParams(
            dimension_semantics=("arbitrary",), vmem_limit_bytes=61 * 2**20, **links
        ),
        cost_estimate=pl.CostEstimate(
            flops=4 * rows * width * 4 * width + 20 * rows * rows * width // 2,
            bytes_accessed=32 * rows * width,
            transcendentals=rows * rows * HEADS // 2,
        ),
        name="attention_backward",
    )(
        grad_middle, queries, keys, values, attended, normed, tokens, packed, packed, packed,
        packed, packed, docs_row, docs_column, cosine, sine, small_grad, *sources,
    )


def routing_kernel(expert_count, routes_ref, columns_ref, rows_ref):
    rows = routes_ref.shape[0]
    lanes = lane_ids((rows, 128))
    first = (lanes == routes_ref[:, 0:1]).astype(jnp.float32)
    second = (lanes == routes_ref[:, 1:2]).astype(jnp.float32)
    down = lax.broadcasted_iota(jnp.int32, (rows, rows), 0)
    lower = (down > lane_ids((rows, rows))).astype(jnp.bfloat16)
    before_first = nn(lower, first.astype(jnp.bfloat16))
    before_second = nn(lower, second.astype(jnp.bfloat16)) + jnp.sum(first, 0, keepdims=True)
    spots = []
    for picked, before, at in ((first, before_first, 0), (second, before_second, 1)):
        rank = jnp.sum(picked * before, -1, keepdims=True)
        route = routes_ref[:, at : at + 1]
        spot = route.astype(jnp.float32) * CAP + rank
        spots.append(jnp.where(route < expert_count, spot, jnp.full_like(spot, 2.0 * expert_count * CAP)))
    both = jnp.where(lanes == 0, spots[0], jnp.where(lanes == 1, spots[1], 0.0))
    columns_ref[...] = both.astype(jnp.int32)
    rows_ref[...] = jnp.transpose(both)[0:8, :].astype(jnp.int32)


def routing(routes, expert_count):
    rows = routes.shape[0]
    return pl.pallas_call(
        functools.partial(routing_kernel, expert_count),
        out_shape=[
            jax.ShapeDtypeStruct((rows, 128), jnp.int32),
            jax.ShapeDtypeStruct((8, rows), jnp.int32),
        ],
        compiler_params=pltpu.CompilerParams(vmem_limit_bytes=40 * 2**20),
        name="routing",
    )(routes)


def dispatch_kernel(spots_ref, aux_ref, normed_ref, cot_ref, rows_ref, grads_ref, gates_ref):
    step = pl.program_id(0)

    @pl.when(step == 0)
    def _():
        gates_ref[...] = jnp.transpose(aux_ref[...])[0:8, :]

    shape = (rows_ref.shape[0], normed_ref.shape[0])
    slots = step * rows_ref.shape[0] + lax.broadcasted_iota(jnp.int32, shape, 0)
    first, second = slots == spots_ref[0:1, :], slots == spots_ref[1:2, :]
    gates = jnp.sum(
        jnp.where(first, gates_ref[0:1, :], jnp.where(second, gates_ref[1:2, :], 0.0)), -1, keepdims=True
    )
    chosen = jnp.where(first | second, 1.0, 0.0).astype(jnp.bfloat16)
    rows_ref[...] = nn(chosen, normed_ref[...]).astype(jnp.bfloat16)
    grads_ref[...] = (nn(chosen, cot_ref[...]) * gates).astype(jnp.bfloat16)


def dispatch(spots, aux, normed, cot, owner_count, local_count):
    rows, width = normed.shape
    slot_count = owner_count * local_count * CAP
    whole = lambda shape: pl.BlockSpec(shape, lambda j: (0, 0))
    block = pl.BlockSpec(
        (None, None, CAP, width), lambda j: (j % local_count, j // local_count, 0, 0)
    )
    return pl.pallas_call(
        dispatch_kernel,
        grid=(slot_count // CAP,),
        out_shape=[jax.ShapeDtypeStruct((local_count, owner_count, CAP, width), jnp.bfloat16)] * 2,
        in_specs=[whole((8, rows)), whole((rows, 128)), whole((rows, width)), whole((rows, width))],
        out_specs=[block, block],
        scratch_shapes=[pltpu.VMEM((8, rows), jnp.float32)],
        compiler_params=pltpu.CompilerParams(
            dimension_semantics=("arbitrary",), vmem_limit_bytes=60 * 2**20
        ),
        cost_estimate=pl.CostEstimate(
            flops=4 * slot_count * rows * width,
            bytes_accessed=4 * (rows + slot_count) * width,
            transcendentals=0,
        ),
        name="dispatch",
    )(spots, aux, normed, cot)


def halves(values):
    high = values.astype(jnp.bfloat16)
    return high, (values - high.astype(jnp.float32)).astype(jnp.bfloat16)


def combine_kernel(
    expert_count, local_count, *refs
):
    parts, refs = refs[:local_count], refs[local_count:]
    (
        spots_ref, routes_ref, aux_ref, normed_ref, middle_ref, cot_ref, small_ref,
        output_ref, logit_ref, grad_middle_ref, small_out_ref, vectors_ref, small_grad_ref,
    ) = refs
    step = pl.program_id(0)

    @pl.when(step == 0)
    def _():
        vectors_ref[0:8, :] = jnp.transpose(small_ref[:, :128].astype(jnp.float32))[16:24, :]
        vectors_ref[8:16, :] = jnp.zeros((8, vectors_ref.shape[1]), jnp.float32)
        small_grad_ref[...] = jnp.zeros_like(small_grad_ref)

    rows, width = normed_ref.shape
    normed_low, cot_low = normed_ref[...], cot_ref[...]
    normed, cot = normed_low.astype(jnp.float32), cot_low.astype(jnp.float32)
    total = lambda values: jnp.sum(values, -1, keepdims=True)
    picks, back = [0.0, 0.0], 0.0
    for e in range(local_count):
        count = parts[e].shape[0] * CAP
        slots = lane_ids((rows, count))
        slots = slots // CAP * (local_count * CAP) + e * CAP + slots % CAP
        hits = [slots == spots_ref[:, s : s + 1] for s in range(2)]
        chosen = [jnp.where(hit, 1.0, 0.0).astype(jnp.bfloat16) for hit in hits]
        returned = parts[e][:, 0].reshape(count, width)
        for s in range(2):
            picks[s] = picks[s] + nn(chosen[s], returned)
        back = back + nn(chosen[0] + chosen[1], parts[e][:, 1].reshape(count, width))
    inner = [total(pick * cot) for pick in picks]
    gates = [aux_ref[:, s : s + 1] for s in range(2)]
    routes = [routes_ref[:, s : s + 1] for s in range(2)]
    dot_copy = total(cot * normed)

    def weight_of(route):
        return sum(jnp.where(routes[s] == route, gates[s], 0.0) for s in range(2))

    copy_weight = weight_of(expert_count + 1)
    mix = gates[0] * picks[0] + gates[1] * picks[1]
    pass_weight = copy_weight
    gate_grads = [
        inner[s] + jnp.where(routes[s] == expert_count + 1, dot_copy, 0.0) for s in range(2)
    ]
    lanes = lane_ids((rows, 128))
    spread = jnp.zeros((rows, 128), jnp.float32)
    for k in range(2):
        vector = vectors_ref[k : k + 1, :]
        keep, blend = aux_ref[:, 2 + 2 * k : 3 + 2 * k], aux_ref[:, 3 + 2 * k : 4 + 2 * k]
        weight = weight_of(expert_count + 2 + k)
        dot_vector = total(cot * vector)
        pass_weight = pass_weight + weight * keep
        mix = mix + (weight * blend) * vector
        value = keep * dot_copy + blend * dot_vector
        for s in range(2):
            gate_grads[s] = gate_grads[s] + jnp.where(routes[s] == expert_count + 2 + k, value, 0.0)
        term = keep * blend * (weight * dot_copy - weight * dot_vector)
        spread = jnp.where(lanes == 12 + 2 * k, term, spread)
        spread = jnp.where(lanes == 13 + 2 * k, -term, spread)
        spread = jnp.where(lanes == 16 + k, weight * blend, spread)
    mix = mix + pass_weight * normed
    middle, scale = middle_ref[...], aux_ref[:, 6:7]
    output_ref[...] = (middle + mix).astype(jnp.bfloat16)
    mean = gates[0] * gate_grads[0] + gates[1] * gate_grads[1]
    for s in range(2):
        spread = jnp.where(lanes == routes[s], gates[s] * (gate_grads[s] - mean), spread)
    logit_ref[...] = spread[:, : logit_ref.shape[1]].astype(jnp.bfloat16)
    logits = jnp.where(lanes < 16, spread, 0.0)
    high, low = halves(logits)
    small = small_ref[:, :128]
    vector_high, vector_low = halves(spread - logits)
    small_grad_ref[...] += (
        tn(normed_low, high) + tn(normed_low, low) + tn(cot_low, vector_high) + tn(cot_low, vector_low)
    )
    grads = back + pass_weight * cot + nt(high, small) + nt(low, small)
    vectors_ref[8:9, :] += jnp.sum(grads * middle * scale, 0, keepdims=True)
    weighted = grads * vectors_ref[3:4, :]
    mean = jnp.mean(weighted * middle, -1, keepdims=True)
    grad_middle_ref[...] = cot + scale * weighted - middle * (scale * scale * scale * mean)

    @pl.when(step == pl.num_programs(0) - 1)
    def _():
        column = jnp.transpose(jnp.broadcast_to(vectors_ref[8:9, :], (128, width)))
        small_grad = small_grad_ref[...]
        small_out_ref[...] = jnp.where(lane_ids(small_grad.shape) == 19, column, small_grad)


def combine(parts, spots, routes, aux, normed, middle, cot, packed, choice_count, expert_count):
    rows, width = normed.shape
    local_count = len(parts)
    slot_count = expert_count * CAP
    size = 256
    block = lambda columns: pl.BlockSpec((size, columns), lambda j: (j, 0))
    whole = lambda shape: pl.BlockSpec(shape, lambda j: (0,) * len(shape))
    return pl.pallas_call(
        functools.partial(combine_kernel, expert_count, local_count),
        grid=(rows // size,),
        out_shape=[
            jax.ShapeDtypeStruct((rows, width), jnp.bfloat16),
            jax.ShapeDtypeStruct((rows, choice_count), jnp.bfloat16),
            jax.ShapeDtypeStruct((rows, width), jnp.float32),
            jax.ShapeDtypeStruct((width, 128), jnp.float32),
        ],
        in_specs=[whole(part.shape) for part in parts]
        + [
            block(128),
            block(2),
            block(128),
            block(width),
            block(width),
            block(width),
            pl.BlockSpec((width, 256), lambda j: (0, 12)),
        ],
        out_specs=[block(width), block(choice_count), block(width), whole((width, 128))],
        scratch_shapes=[pltpu.VMEM((16, width), jnp.float32), pltpu.VMEM((width, 128), jnp.float32)],
        compiler_params=pltpu.CompilerParams(
            dimension_semantics=("arbitrary",), vmem_limit_bytes=56 * 2**20
        ),
        cost_estimate=pl.CostEstimate(
            flops=6 * slot_count * rows * width,
            bytes_accessed=14 * rows * width + 4 * slot_count * width,
            transcendentals=0,
        ),
        name="combine",
    )(*parts, spots, routes, aux, normed, middle, cot, packed)


def experts_kernel(mode, dp_count, *refs):
    rows_ref, grads_ref, w_gate_ref, w_up_ref, w_down_ref = refs[:5]
    if mode == 0:
        grad_gu_ref, grad_down_ref, both_ref, turned_ref, out_ref, back_ref = refs[5:]
    if mode == 1:
        next_rows, next_grads, *shard_refs = refs[5:9]
        grad_gu_ref, grad_down_ref, both_ref, rows_out, grads_out, *full_refs = refs[9:16]
        turned_ref, out_ref, back_ref = refs[16:19]
        sems = refs[19:]
    if mode == 2:
        before_ref, *sources = refs[5:8]
        grad_gu_ref, grad_down_ref, first_in, second_in, *totals = refs[8:14]
        turned_ref, out_ref, back_ref, both_ref = refs[14:18]
        sems = refs[18:]
    step = pl.program_id(0)
    width = rows_ref.shape[-1]
    rows = rows_ref[...].reshape(-1, width)
    grads = grads_ref[...].reshape(-1, width)
    if mode == 1:
        lines = [
            PairGather(shard.at[1], full, dp_count, sems[6 * n : 6 * n + 6])
            for n, (shard, full) in enumerate(zip(shard_refs, full_refs))
        ]
        trades = [
            Trade(next_rows.at[1], rows_out, *sems[12:14]),
            Trade(next_grads.at[1], grads_out, *sems[14:16]),
        ]

        @pl.when(step == 0)
        def _():
            greet(lines[0].peers() + trades[0].peers())
            for line in lines + trades:
                line.start()

        for hop in range(1, 4):

            @pl.when(step == 2 * hop)
            def _(hop=hop):
                for line in lines:
                    line.relay(hop)

    if mode == 2:
        trades = [Trade(before_ref, first_in, *sems[:2]), Trade(both_ref, second_in, *sems[2:4])]
        line = GroupReduce(sources, totals, sems[4:])

        @pl.when(step == 0)
        def _():
            greet(line.peers() + trades[0].peers())
            line.start()
            trades[0].start()

        pl.when(step == 4)(lambda: line.pass_on(0))

    @pl.when(step == 0)
    def _():
        turned_ref[...] = jnp.transpose(rows)
        out_ref[...] = jnp.zeros_like(out_ref)
        back_ref[...] = jnp.zeros_like(back_ref)

    w_gate, w_up, w_down = w_gate_ref[...], w_up_ref[...], w_down_ref[...]
    gate, up = nn(rows, w_gate), nn(rows, w_up)
    squashed = 1.0 / (1.0 + jnp.exp(-gate))
    silu = gate * squashed
    activated = (silu * up).astype(jnp.bfloat16)
    grad_act = nt(grads, w_down)
    grad_gate = (grad_act * up * (squashed * (1.0 + gate * (1.0 - squashed)))).astype(jnp.bfloat16)
    grad_up = (grad_act * silu).astype(jnp.bfloat16)
    out_ref[...] += nn(activated, w_down)
    grad_down_ref[...] = tn(activated, grads).astype(jnp.bfloat16)
    back_ref[...] += nt(grad_gate, w_gate) + nt(grad_up, w_up)
    grad_gu_ref[0] = nn(turned_ref[...], grad_gate).astype(jnp.bfloat16)
    grad_gu_ref[1] = nn(turned_ref[...], grad_up).astype(jnp.bfloat16)

    @pl.when(step == pl.num_programs(0) - 1)
    def _():
        shape = (both_ref.shape[0],) + both_ref.shape[2:]
        both_ref[:, 0] = out_ref[...].astype(jnp.bfloat16).reshape(shape)
        both_ref[:, 1] = back_ref[...].astype(jnp.bfloat16).reshape(shape)
        if mode == 1:
            for part in lines + trades:
                part.finish()
        if mode == 2:
            trades[1].start()
            for k in range(1, 4):
                line.pass_on(k)
            line.finish()
            for trade in trades:
                trade.finish()


def experts(rows, grads, gate, up, down, mode=0, dp_count=0, extras=(), collective=None):
    owners, cap, width = rows.shape
    hidden = down.shape[0]
    count = owners * cap
    block = FF_BLOCK if count <= 1024 else FF_BLOCK // 2
    steps = hidden // block
    low = jnp.bfloat16
    pairs = pl.BlockSpec((owners, cap, width), lambda j: (0, 0, 0), pipeline_mode=pl.Buffered(1))
    anywhere = pl.BlockSpec(memory_space=pl.ANY)
    both = jax.ShapeDtypeStruct((owners, 2, cap, width), low)
    links = {"collective_id": collective, "has_side_effects": True} if mode else {}
    out_shape = [
        jax.ShapeDtypeStruct((2, width, hidden), low),
        jax.ShapeDtypeStruct((hidden, width), low),
    ]
    out_specs = [
        pl.BlockSpec((2, width, block), lambda j: (0, 0, j)),
        pl.BlockSpec((block, width), lambda j: (j, 0)),
    ]
    scratch = [
        pltpu.VMEM((width, count), low),
        pltpu.VMEM((count, width), jnp.float32),
        pltpu.VMEM((count, width), jnp.float32),
    ]
    if mode < 2:
        out_shape.append(both)
        out_specs.append(pl.BlockSpec(both.shape, lambda j: (0, 0, 0, 0)))
    if mode == 1:
        out_shape += [jax.ShapeDtypeStruct(rows.shape, low)] * 2
        for shards in extras[2:]:
            out_shape.append(jax.ShapeDtypeStruct((dp_count * shards.shape[1], shards.shape[2]), low))
        out_specs += [anywhere] * 4
        scratch += pair_semaphores(dp_count) * 2 + trade_semaphores(owners) * 2
    if mode == 2:
        out_shape += [both, both]
        out_specs += [anywhere] * 2
        for shape in ((width // 8, 2 * hidden), (hidden // 8, width)):
            out_shape.append(jax.ShapeDtypeStruct(shape, jnp.float32))
            out_specs.append(pl.BlockSpec(shape, lambda j: (0, 0)))
        scratch.append(pltpu.VMEM(both.shape, low))
        scratch += trade_semaphores(owners) * 2
        for source in extras[1:]:
            scratch += reduce_scratch(source)
    return pl.pallas_call(
        functools.partial(experts_kernel, mode, dp_count),
        grid=(steps,),
        out_shape=out_shape,
        in_specs=[
            pairs,
            pairs,
            pl.BlockSpec((width, block), lambda j: (0, j)),
            pl.BlockSpec((width, block), lambda j: (0, up.shape[1] // block - steps + j)),
            pl.BlockSpec((block, width), lambda j: (j, 0)),
        ]
        + [anywhere] * len(extras),
        out_specs=out_specs,
        scratch_shapes=scratch,
        compiler_params=pltpu.CompilerParams(
            dimension_semantics=("arbitrary",), vmem_limit_bytes=60 * 2**20, **links
        ),
        cost_estimate=pl.CostEstimate(
            flops=18 * count * width * hidden,
            bytes_accessed=12 * width * hidden + 8 * count * width,
            transcendentals=count * hidden,
        ),
        name="experts",
    )(rows, grads, gate, up, down, *extras)


def dp_grid(dp_count):
    outer = 4 if dp_count % 4 == 0 else 1
    return outer, dp_count // outer


def place():
    me, mine = lax.axis_index("dp"), lax.axis_index("expert")
    return me, mine


def greet(peers):
    barrier = pltpu.get_barrier_semaphore()
    for peer in peers:
        pl.semaphore_signal(barrier, inc=1, device_id=peer, device_id_type=MESH)
    pl.semaphore_wait(barrier, len(peers))


class LineGather:
    def __init__(
        self, shard, full, dp_count, send_sem, recv_sem, own_sem, columns=None, also=None, span=None, crossed=False
    ):
        self.columns = slice(None) if columns is None else columns
        self.also = also or (lambda chunk: None)
        self.stride = shard.shape[0]
        self.first, self.count = span or (0, self.stride)
        self.crossed = crossed
        self.shard = shard.at[self.first : self.first + self.count, :] if span else shard
        self.full, self.dp_count = full, dp_count
        self.send_sem, self.recv_sem, self.own_sem = send_sem, recv_sem, own_sem
        self.outer_count, self.inner_count = dp_grid(dp_count)
        self.me, self.mine = place()
        self.outer, self.inner = self.me // self.inner_count, self.me % self.inner_count
        self.inner_peers = [
            lax.rem(self.inner + k, self.inner_count) for k in range(1, self.inner_count)
        ]
        self.lanes = [self.inner] + (self.inner_peers if crossed else [])
        self.can_up, self.can_down = self.outer < self.outer_count - 1, self.outer > 0

    def peers(self):
        below = lax.rem(self.outer + self.outer_count - 1, self.outer_count)
        above = lax.rem(self.outer + 1, self.outer_count)
        return [(peer * self.inner_count + self.inner, self.mine) for peer in (below, above)] + [
            (self.outer * self.inner_count + peer, self.mine) for peer in self.inner_peers
        ]

    def spot(self, chunk):
        start = pl.multiple_of(chunk * self.stride + self.first, 8)
        return self.full.at[pl.ds(start, self.count), self.columns]

    def copy(self, source, chunk, device, way, at):
        return pltpu.make_async_remote_copy(
            src_ref=source,
            dst_ref=self.spot(chunk),
            send_sem=self.send_sem.at[way, at, chunk],
            recv_sem=self.recv_sem.at[chunk],
            device_id=(device, self.mine),
            device_id_type=MESH,
        )

    def up(self, source, chunk):
        return self.copy(source, chunk, (self.outer + 1) * self.inner_count + self.inner, 1, 0)

    def down(self, source, chunk):
        return self.copy(source, chunk, (self.outer - 1) * self.inner_count + self.inner, 2, 0)

    def across(self, source, chunk):
        return [
            self.copy(source, chunk, self.outer * self.inner_count + peer, 0, at)
            for at, peer in enumerate(self.inner_peers)
        ]

    def keep(self):
        return pltpu.make_async_copy(self.shard, self.spot(self.me), self.own_sem)

    def arrived(self, chunk):
        pltpu.make_async_copy(self.spot(chunk), self.spot(chunk), self.recv_sem.at[chunk]).wait()

    def start(self):
        for copy in self.across(self.shard, self.me):
            copy.start()
        pl.when(self.can_up)(lambda: self.up(self.shard, self.me).start())
        pl.when(self.can_down)(lambda: self.down(self.shard, self.me).start())
        self.keep().start()

    def turn_in(self):
        if self.crossed:
            for peer in self.inner_peers:
                chunk = self.outer * self.inner_count + peer
                self.arrived(chunk)
                pl.when(self.can_up)(lambda: self.up(self.spot(chunk), chunk).start())
                pl.when(self.can_down)(lambda: self.down(self.spot(chunk), chunk).start())

    def relay(self, step):
        low, high = self.outer - step, self.outer + step

        def pass_on(source, upward):
            for lane in self.lanes:
                chunk = source * self.inner_count + lane
                self.arrived(chunk)
                if upward:
                    pl.when(self.can_up)(lambda: self.up(self.spot(chunk), chunk).start())
                else:
                    pl.when(self.can_down)(lambda: self.down(self.spot(chunk), chunk).start())
                if not self.crossed:
                    for copy in self.across(self.spot(chunk), chunk):
                        copy.start()
                    self.also(chunk)

        pl.when(low >= 0)(lambda: pass_on(low, True))
        pl.when(high < self.outer_count)(lambda: pass_on(high, False))

    def finish(self):
        self.keep().wait()
        if self.crossed:
            for copy in self.across(self.shard, self.me):
                copy.wait_send()
        else:
            for peer in self.inner_peers:
                for k in range(self.outer_count):
                    chunk = lax.rem(self.outer + k, self.outer_count) * self.inner_count + peer
                    self.arrived(chunk)
                    self.also(chunk)
        for plane in range(self.outer_count):
            for lane in self.lanes:
                chunk = plane * self.inner_count + lane
                if not self.crossed:
                    for copy in self.across(self.spot(chunk), chunk):
                        copy.wait_send()
                pl.when(self.can_up & (self.outer >= plane))(
                    lambda chunk=chunk: self.up(self.spot(chunk), chunk).wait_send()
                )
                pl.when(self.can_down & (self.outer <= plane))(
                    lambda chunk=chunk: self.down(self.spot(chunk), chunk).wait_send()
                )


def crossed_rows(rows):
    return max(1, (rows + 48) // 96) * 16


class PairGather:
    def __init__(self, shard, full, dp_count, sems):
        rows = shard.shape[0]
        rest = crossed_rows(rows)
        self.parts = [
            LineGather(shard, full, dp_count, *sems[:3], span=(rows - rest, rest), crossed=True),
            LineGather(shard, full, dp_count, *sems[3:6], span=(0, rows - rest)),
        ]
        self.peers = self.parts[0].peers

    def start(self):
        for part in self.parts:
            part.start()

    def relay(self, step):
        if step == 1:
            self.parts[0].turn_in()
        for part in self.parts:
            part.relay(step)

    def finish(self):
        for part in self.parts:
            part.finish()


def pair_semaphores(dp_count):
    return gather_semaphores(dp_count) + gather_semaphores(dp_count)


def gather_semaphores(dp_count):
    inner_count = dp_grid(dp_count)[1]
    return [
        pltpu.SemaphoreType.DMA((3, max(1, inner_count - 1), dp_count)),
        pltpu.SemaphoreType.DMA((dp_count,)),
        pltpu.SemaphoreType.DMA,
    ]


def by_rows(count, body):
    def step(i, carry):
        body(i * 16)
        return carry

    lax.fori_loop(0, count // 16, step, 0)


class Trade:
    def __init__(self, source, target, send_sem, recv_sem):
        self.source, self.target, self.send_sem, self.recv_sem = source, target, send_sem, recv_sem
        self.me, self.mine = place()
        count = target.shape[0]
        self.partners = [lax.rem(self.mine + k, count) for k in range(1, count)]

    def peers(self):
        return [(self.me, peer) for peer in self.partners]

    def copy(self, k):
        peer = self.partners[k]
        return pltpu.make_async_remote_copy(
            src_ref=self.source.at[peer],
            dst_ref=self.target.at[self.mine],
            send_sem=self.send_sem.at[k + 1],
            recv_sem=self.recv_sem.at[self.mine],
            device_id=(self.me, peer),
            device_id_type=MESH,
        )

    def keep(self):
        return pltpu.make_async_copy(
            self.source.at[self.mine], self.target.at[self.mine], self.send_sem.at[0]
        )

    def start(self):
        for k in range(len(self.partners)):
            self.copy(k).start()
        self.keep().start()

    def finish(self):
        self.keep().wait()
        for k, peer in enumerate(self.partners):
            there = self.target.at[peer]
            pltpu.make_async_copy(there, there, self.recv_sem.at[peer]).wait()
            self.copy(k).wait_send()


def trade_semaphores(owner_count):
    return [pltpu.SemaphoreType.DMA((owner_count,)), pltpu.SemaphoreType.DMA((owner_count,))]


def expert_gather_kernel(dp_count, rows_ref, grads_ref, shards_ref, rows_out, grads_out, full_ref, *sems):
    line = PairGather(shards_ref.at[0], full_ref, dp_count, sems[:6])
    trades = [Trade(rows_ref.at[0], rows_out, *sems[6:8]), Trade(grads_ref.at[0], grads_out, *sems[8:10])]
    greet(line.peers() + trades[0].peers())
    line.start()
    for trade in trades:
        trade.start()
    for hop in range(1, 4):
        line.relay(hop)
    line.finish()
    for trade in trades:
        trade.finish()


def expert_gather(rows, grads, shards, dp_count, collective):
    anywhere = pl.BlockSpec(memory_space=pl.ANY)
    return pl.pallas_call(
        functools.partial(expert_gather_kernel, dp_count),
        out_shape=[
            jax.ShapeDtypeStruct(rows.shape[1:], rows.dtype),
            jax.ShapeDtypeStruct(grads.shape[1:], grads.dtype),
            jax.ShapeDtypeStruct((dp_count * shards.shape[1], shards.shape[2]), shards.dtype),
        ],
        in_specs=[anywhere] * 3,
        out_specs=[anywhere] * 3,
        scratch_shapes=pair_semaphores(dp_count)
        + trade_semaphores(rows.shape[1])
        + trade_semaphores(rows.shape[1]),
        compiler_params=pltpu.CompilerParams(collective_id=collective, has_side_effects=True),
        name="expert_gather",
    )(rows, grads, shards)


def small_gather_kernel(
    dp_count, expert_count, shard_ref, routes_ref, full_ref, columns_ref, rows_ref,
    send_sem, recv_sem, own_sem, pass_sem, mate_sem, all_sem,
):
    me, mine = place()
    rows, columns = shard_ref.shape
    half = columns // 2
    side = mine % 2
    mate = mine + 1 - 2 * side
    own_columns = pl.ds(pl.multiple_of(side * half, 128), half)
    mate_columns = pl.ds(pl.multiple_of((1 - side) * half, 128), half)

    def there(chunk, lanes):
        return full_ref.at[pl.ds(pl.multiple_of(chunk * rows, 8), rows), lanes]

    def pass_copy(chunk):
        return pltpu.make_async_remote_copy(
            src_ref=there(chunk, own_columns),
            dst_ref=there(chunk, own_columns),
            send_sem=pass_sem.at[chunk],
            recv_sem=mate_sem.at[chunk],
            device_id=(me, mate),
            device_id_type=MESH,
        )

    line = LineGather(
        shard_ref.at[:, own_columns], full_ref, dp_count, send_sem, recv_sem, own_sem,
        own_columns, lambda chunk: pass_copy(chunk).start(),
    )
    greet(line.peers() + [(me, mate)])
    line.start()
    other = pltpu.make_async_copy(shard_ref.at[:, mate_columns], there(me, mate_columns), all_sem)
    other.start()
    routing_kernel(expert_count, routes_ref, columns_ref, rows_ref)
    for hop in range(1, line.outer_count):
        line.relay(hop)
    line.finish()
    other.wait()
    for k in range(1, dp_count):
        chunk = lax.rem(me + k, dp_count)
        target = there(chunk, mate_columns)
        pltpu.make_async_copy(target, target, mate_sem.at[chunk]).wait()
        pass_copy(chunk).wait_send()


def small_gather(shard, routes, expert_count, dp_count, collective):
    rows, columns = shard.shape
    tokens = routes.shape[0]
    anywhere, in_vmem = pl.BlockSpec(memory_space=pl.ANY), pl.BlockSpec(memory_space=pltpu.VMEM)
    return pl.pallas_call(
        functools.partial(small_gather_kernel, dp_count, expert_count),
        out_shape=[
            jax.ShapeDtypeStruct((dp_count * rows, columns), shard.dtype),
            jax.ShapeDtypeStruct((tokens, 128), jnp.int32),
            jax.ShapeDtypeStruct((8, tokens), jnp.int32),
        ],
        in_specs=[anywhere, in_vmem],
        out_specs=[anywhere, in_vmem, in_vmem],
        scratch_shapes=gather_semaphores(dp_count)
        + [
            pltpu.SemaphoreType.DMA((dp_count,)),
            pltpu.SemaphoreType.DMA((dp_count,)),
            pltpu.SemaphoreType.DMA,
        ],
        compiler_params=pltpu.CompilerParams(
            collective_id=collective, has_side_effects=True, vmem_limit_bytes=60 * 2**20
        ),
        name="small_gather",
    )(shard, routes)


class LineReduce:
    def __init__(self, source, total, scratch):
        self.source, self.total = source, total
        self.owns, self.ins, self.lows, self.highs = scratch[:4]
        self.held, self.cross_lows, self.cross_highs, self.cross_in = scratch[4:8]
        self.own_sem, self.in_send, self.in_recv, self.line_send, self.line_recv = scratch[8:13]
        self.held_sem, self.cross_send, self.cross_recv, self.turn_sem = scratch[13:17]
        self.me, self.mine = place()
        self.outer, self.inner = self.me // 2, self.me % 2
        self.main, self.rest = self.owns.shape[-2], self.held.shape[-2]

    def peers(self):
        low, high = lax.rem(self.outer + 3, 4), lax.rem(self.outer + 1, 4)
        return [
            (self.me + 1 - 2 * self.inner, self.mine),
            (low * 2 + self.inner, self.mine),
            (high * 2 + self.inner, self.mine),
        ]

    def order(self, o):
        return sorted(range(4), key=lambda plane: (-abs(plane - o), plane))

    def chunk(self, at, rest):
        start = at * (self.main + self.rest) + (self.main if rest else 0)
        here = pl.ds(pl.multiple_of(start, 16), self.rest if rest else self.main)
        return self.source.at[:, here, :] if len(self.source.shape) == 3 else self.source.at[here, :]

    def lane(self, j):
        return self.inner if j == 0 else 1 - self.inner

    def own_copy(self, plane):
        return pltpu.make_async_copy(
            self.chunk(plane * 2 + self.inner, False), self.owns.at[plane], self.own_sem.at[plane]
        )

    def held_copy(self, j, plane):
        return pltpu.make_async_copy(
            self.chunk(plane * 2 + self.lane(j), True), self.held.at[j, plane], self.held_sem.at[j, plane]
        )

    def remote(self, source, target, device, send_sem, recv_sem):
        return pltpu.make_async_remote_copy(
            src_ref=source,
            dst_ref=target,
            send_sem=send_sem,
            recv_sem=recv_sem,
            device_id=(device, self.mine),
            device_id_type=MESH,
        )

    def in_copy(self, plane):
        return self.remote(
            self.chunk(plane * 2 + 1 - self.inner, False),
            self.ins.at[plane],
            self.me + 1 - 2 * self.inner,
            self.in_send.at[plane],
            self.in_recv.at[plane],
        )

    def line_copy(self, plane, upward, device_plane):
        way = 0 if upward else 1
        return self.remote(
            self.ins.at[plane],
            self.lows.at[plane - 1] if upward else self.highs.at[plane],
            device_plane * 2 + self.inner,
            self.line_send.at[way, plane],
            self.line_recv.at[way, plane],
        )

    def cross_copy(self, j, plane, upward, device_plane):
        way = 0 if upward else 1
        return self.remote(
            self.held.at[j, plane],
            self.cross_lows.at[j, plane - 1] if upward else self.cross_highs.at[j, plane],
            device_plane * 2 + self.inner,
            self.cross_send.at[j, way, plane],
            self.cross_recv.at[j, way, plane],
        )

    def turn_copy(self, o):
        return self.remote(
            self.held.at[1, o],
            self.cross_in,
            self.me + 1 - 2 * self.inner,
            self.turn_sem.at[0],
            self.turn_sem.at[1],
        )

    def start(self, o):
        for plane in self.order(o):
            for j in range(2):
                self.held_copy(j, plane).start()
        for plane in self.order(o):
            self.in_copy(plane).start()
        for plane in self.order(o):
            self.own_copy(plane).start()

    def next_plane(self, o, plane):
        return (plane > o, o + 1 if plane > o else o - 1)

    def incoming(self, o, plane):
        ways = []
        if o > 0 and plane >= o:
            ways.append(True)
        if o < 3 and plane <= o:
            ways.append(False)
        return ways

    def add(self, target, terms, total_row=None):
        sides = target.shape[0] if len(target.shape) == 3 else 0

        def body(at):
            here = pl.ds(pl.multiple_of(at, 16), 16)
            for side in range(max(1, sides)):
                spot = (side, here) if sides else (here,)
                total = target[spot].astype(jnp.float32)
                for term in terms:
                    total = total + term[spot].astype(jnp.float32)
                if total_row is None:
                    target[spot] = total.astype(target.dtype)
                else:
                    there = pl.ds(pl.multiple_of(total_row + at, 16), 16)
                    size = total.shape[-1]
                    self.total[there, side * size : (side + 1) * size] = total

        by_rows(target.shape[-2], body)

    def pass_on(self, o, k):
        plane = self.order(o)[k]
        ways = self.incoming(o, plane)
        for j in (1, 0):
            self.held_copy(j, plane).wait()
            terms = []
            for upward in ways:
                self.cross_copy(j, plane, upward, o).wait_recv()
                terms.append(
                    self.cross_lows.at[j, plane - 1] if upward else self.cross_highs.at[j, plane]
                )
            if plane != o:
                if terms:
                    self.add(self.held.at[j, plane], terms)
                self.cross_copy(j, plane, *self.next_plane(o, plane)).start()
            elif j == 1:
                self.add(self.held.at[1, o], terms)
                self.turn_copy(o).start()
            else:
                last_terms = terms + [self.cross_in]
        self.own_copy(plane).wait()
        self.in_copy(plane).wait_recv()
        terms = [self.owns.at[plane]]
        for upward in ways:
            self.line_copy(plane, upward, o).wait_recv()
            terms.append(self.lows.at[plane - 1] if upward else self.highs.at[plane])
        if plane != o:
            self.add(self.ins.at[plane], terms)
            self.line_copy(plane, *self.next_plane(o, plane)).start()
        else:
            self.add(self.ins.at[plane], terms, 0)
            self.turn_copy(o).wait_recv()
            self.add(self.held.at[0, o], last_terms, self.main)

    def finish(self, o):
        self.turn_copy(o).wait_send()
        for plane in range(4):
            self.in_copy(plane).wait_send()
            if plane != o:
                self.line_copy(plane, *self.next_plane(o, plane)).wait_send()
                for j in range(2):
                    self.cross_copy(j, plane, *self.next_plane(o, plane)).wait_send()


def reduce_scratch(source):
    rows = source.shape[-2] // 8
    rest = crossed_rows(rows)
    lead, columns = source.shape[:-2], source.shape[-1]
    low = jnp.bfloat16

    def buffer(front, count):
        return pltpu.VMEM(front + lead + (count, columns), low)

    return [
        buffer((4,), rows - rest),
        buffer((4,), rows - rest),
        buffer((3,), rows - rest),
        buffer((3,), rows - rest),
        buffer((2, 4), rest),
        buffer((2, 3), rest),
        buffer((2, 3), rest),
        buffer((), rest),
        pltpu.SemaphoreType.DMA((4,)),
        pltpu.SemaphoreType.DMA((4,)),
        pltpu.SemaphoreType.DMA((4,)),
        pltpu.SemaphoreType.DMA((2, 4)),
        pltpu.SemaphoreType.DMA((2, 4)),
        pltpu.SemaphoreType.DMA((2, 4)),
        pltpu.SemaphoreType.DMA((2, 2, 4)),
        pltpu.SemaphoreType.DMA((2, 2, 4)),
        pltpu.SemaphoreType.DMA((2,)),
    ]


class GroupReduce:
    def __init__(self, sources, totals, scratch):
        self.lines = [
            LineReduce(source, total, scratch[17 * n : 17 * n + 17])
            for n, (source, total) in enumerate(zip(sources, totals))
        ]
        self.outer = self.lines[0].outer
        self.peers = self.lines[0].peers

    def each_plane(self, body):
        for o in range(4):
            pl.when(self.outer == o)(functools.partial(body, o))

    def start(self):
        self.each_plane(lambda o: [line.start(o) and None for line in self.lines] and None)

    def pass_on(self, k):
        self.each_plane(lambda o: [line.pass_on(o, k) for line in self.lines] and None)

    def finish(self):
        self.each_plane(lambda o: [line.finish(o) for line in self.lines] and None)


def final_reduce_kernel(small_count, *refs):
    small_refs, refs = refs[:small_count], refs[small_count:]
    (
        small_out, swap, small_in, small_low, small_high, final_low, final_in,
        swap_send, swap_recv, in_send, in_recv, line_send, line_recv, last_send, last_recv,
    ) = refs
    outer_count, inner_count = 4, 2
    me, mine = place()
    outer, inner = me // inner_count, me % inner_count
    side = mine % 2
    mate, across = mine + 1 - 2 * side, lax.rem(mine + 2, 4)
    beside = me + 1 - 2 * inner
    half_rows = small_refs[0].shape[1] // 2
    starts = [sum(ref.shape[2] for ref in small_refs[:n]) for n in range(small_count + 1)]

    def remote(source, target, device, send_at, recv_at):
        return pltpu.make_async_remote_copy(
            src_ref=source,
            dst_ref=target,
            send_sem=send_at,
            recv_sem=recv_at,
            device_id=device,
            device_id_type=MESH,
        )

    low_peer = lax.rem(outer + outer_count - 1, outer_count) * inner_count + inner
    high_peer = lax.rem(outer + 1, outer_count) * inner_count + inner
    greet([(me, mate), (me, across), (beside, mine), (low_peer, mine), (high_peer, mine)])

    mate_rows = pl.ds(pl.multiple_of((1 - side) * half_rows, 16), half_rows)
    own_rows = pl.ds(pl.multiple_of(side * half_rows, 16), half_rows)

    def swap_copy(n):
        return remote(
            small_refs[n].at[:, mate_rows, :],
            swap.at[:, :, starts[n] : starts[n + 1]],
            (me, mate),
            swap_send.at[n],
            swap_recv.at[n],
        )

    def inner_copy(plane):
        return remote(
            swap.at[plane * inner_count + 1 - inner],
            small_in.at[plane],
            (beside, mine),
            in_send.at[plane],
            in_recv.at[plane],
        )

    def line_copy(plane, upward, device_plane):
        way = 0 if upward else 1
        return remote(
            small_in.at[plane],
            (small_low if upward else small_high).at[plane],
            (device_plane * inner_count + inner, mine),
            line_send.at[way, plane],
            line_recv.at[way, plane],
        )

    def wide(values):
        return values.astype(jnp.float32)

    def add_own(chunk):
        def body(at):
            here = pl.ds(pl.multiple_of(at, 16), 16)
            there = pl.ds(pl.multiple_of(side * half_rows + at, 16), 16)
            for n in range(small_count):
                columns = slice(starts[n], starts[n + 1])
                swap[chunk, here, columns] = (
                    wide(swap[chunk, here, columns]) + wide(small_refs[n][chunk, there, :])
                ).astype(swap.dtype)

        by_rows(half_rows, body)

    def at_plane(o):
        order = sorted(range(outer_count), key=lambda t: (-abs(t - o), t))

        def line_start(plane):
            return line_copy(plane, plane > o, o + 1 if plane > o else o - 1)

        for n in range(small_count):
            swap_copy(n).start()
        for n in range(small_count):
            swap_copy(n).wait_recv()
        for plane in order:
            add_own(plane * inner_count + 1 - inner)
            inner_copy(plane).start()
        for plane in order:
            add_own(plane * inner_count + inner)
            inner_copy(plane).wait_recv()
            terms = [swap.at[plane * inner_count + inner]]
            if o > 0 and plane >= o:
                line_copy(plane, True, o).wait_recv()
                terms.append(small_low.at[plane])
            if o < outer_count - 1 and plane <= o:
                line_copy(plane, False, o).wait_recv()
                terms.append(small_high.at[plane])
            target = final_low if plane == o else small_in.at[plane]

            def gather(at, plane=plane, terms=terms, target=target):
                here = pl.ds(pl.multiple_of(at, 16), 16)
                total = wide(small_in[plane, here, :])
                for term in terms:
                    total = total + wide(term[here, :])
                target[here, :] = total.astype(target.dtype)

            by_rows(half_rows, gather)
            if plane != o:
                line_start(plane).start()
        remote(final_low, final_in, (me, across), last_send.at[0], last_recv.at[0]).start()
        for plane in range(outer_count):
            inner_copy(plane).wait_send()
            if plane != o:
                line_start(plane).wait_send()
        for n in range(small_count):
            swap_copy(n).wait_send()

    for o in range(outer_count):
        pl.when(outer == o)(functools.partial(at_plane, o))
    remote(final_low, final_in, (me, across), last_send.at[0], last_recv.at[0]).wait()

    def total_body(at):
        here = pl.ds(pl.multiple_of(at, 16), 16)
        there = pl.ds(pl.multiple_of(side * half_rows + at, 16), 16)
        small_out[there, :] = wide(final_low[here, :]) + wide(final_in[here, :])

    by_rows(half_rows, total_body)
    mate_copy = remote(
        small_out.at[own_rows, :], small_out.at[own_rows, :], (me, mate), last_send.at[1], last_recv.at[1]
    )
    mate_copy.start()
    mate_copy.wait()


def final_reduce(smalls, collective):
    chunk_count, small_rows, _ = smalls[0].shape
    small_columns = sum(small.shape[2] for small in smalls)
    low = jnp.bfloat16
    planes = 4
    in_vmem = pl.BlockSpec(memory_space=pltpu.VMEM)
    half = small_rows // 2
    return pl.pallas_call(
        functools.partial(final_reduce_kernel, len(smalls)),
        out_shape=jax.ShapeDtypeStruct((small_rows, small_columns), jnp.float32),
        in_specs=[in_vmem] * len(smalls),
        out_specs=in_vmem,
        scratch_shapes=[pltpu.VMEM((chunk_count, half, small_columns), low)]
        + [pltpu.VMEM((planes, half, small_columns), low)] * 3
        + [pltpu.VMEM((half, small_columns), low)] * 2
        + [
            pltpu.SemaphoreType.DMA((len(smalls),)),
            pltpu.SemaphoreType.DMA((len(smalls),)),
            pltpu.SemaphoreType.DMA((planes,)),
            pltpu.SemaphoreType.DMA((planes,)),
            pltpu.SemaphoreType.DMA((2, planes)),
            pltpu.SemaphoreType.DMA((2, planes)),
            pltpu.SemaphoreType.DMA((2,)),
            pltpu.SemaphoreType.DMA((2,)),
        ],
        compiler_params=pltpu.CompilerParams(
            collective_id=collective, has_side_effects=True, vmem_limit_bytes=40 * 2**20
        ),
        name="final_reduce",
    )(*smalls)


def shards(
    tokens,
    resid_logits,
    routes,
    doc_ids,
    w_qkv,
    w_out,
    gain_attn,
    gain_ffn,
    w_router,
    w_const,
    v_const,
    w_gate_up,
    w_down,
    out_grad,
):
    dp_count, owner_count = lax.axis_size("dp"), lax.axis_size("expert")
    own_links = dp_count == 8 and owner_count == 4 and w_gate_up.shape[0] == 2
    seq_count, length, width = tokens.shape
    assert seq_count == 1
    rows = seq_count * length
    choice_count = resid_logits.shape[-1]
    local_count = w_gate_up.shape[0]
    expert_count = owner_count * local_count
    hidden_count = w_down.shape[1] * dp_count
    width_qkv, width_out = w_qkv.shape[1], w_out.shape[1]
    small_parts = [w_router, w_const, v_const, gain_attn[:, None], gain_ffn[:, None]]
    small_width = sum(part.shape[1] for part in small_parts)
    pad = jnp.zeros((w_qkv.shape[0], 256 - small_width), jnp.bfloat16)
    packed = jnp.concatenate([w_qkv, w_out] + small_parts + [pad], 1)
    inputs = tokens.reshape(rows, width)
    cot = out_grad.reshape(rows, width)
    route_rows = routes.reshape(rows, 2)
    cosine, sine = rotary_lanes(length, width // HEADS)
    docs_row, docs_column = doc_ids.reshape(1, rows), doc_ids.reshape(rows, 1)
    resid = jnp.pad(
        resid_logits.reshape(rows, choice_count).astype(jnp.float32), ((0, 0), (0, 128 - choice_count))
    )
    if own_links:
        packed_full, spots, spot_rows = small_gather(packed, route_rows, expert_count, dp_count, 1)
    else:
        spots, spot_rows = routing(route_rows, expert_count)
        packed_full = lax.all_gather(packed, "dp", axis=0, tiled=True)
    gather = functools.partial(lax.all_gather, axis_name="dp", axis=0, tiled=True)
    attend = functools.partial(
        attention_forward, inputs, packed_full, docs_row, docs_column, cosine, sine, route_rows, resid
    )
    if own_links:
        *forward, first_gate_up = attend(w_gate_up, dp_count, 5)
    else:
        forward = attend()
    normed_one, queries, keys, values, attended, middle, normed_two, aux = forward
    send_rows, send_grads = dispatch(spot_rows, aux, normed_two, cot, owner_count, local_count)
    if own_links:
        rows_in, grads_in, first_down = expert_gather(send_rows, send_grads, w_down, dp_count, 2)
        grad_gu, grad_down, both, next_rows, next_grads, second_gate_up, second_down = experts(
            rows_in, grads_in, first_gate_up, first_gate_up, first_down, 1, dp_count,
            [send_rows, send_grads, w_gate_up, w_down], 6,
        )
        second_gu, second_grad_down, *parts, gu_part, down_part = experts(
            next_rows, next_grads, second_gate_up, second_gate_up, second_down, 2, dp_count,
            [both, grad_gu, grad_down], 4,
        )
        gu_parts, down_parts = [gu_part], [down_part]
    else:
        exchange = functools.partial(
            lax.all_to_all, axis_name="expert", split_axis=0, concat_axis=0, tiled=True
        )
        parts, gu_parts, down_parts = [], [], []
        for e in range(local_count):
            gate_up = gather(w_gate_up[e])
            grad_gu, grad_down, both = experts(
                exchange(send_rows[e]), exchange(send_grads[e]), gate_up, gate_up, gather(w_down[e])
            )
            parts.append(exchange(both))
            gu_part = lax.psum_scatter(grad_gu, "dp", scatter_dimension=1, tiled=True)
            gu_parts.append(jnp.concatenate([gu_part[0], gu_part[1]], -1).astype(jnp.float32))
            down_parts.append(lax.psum_scatter(grad_down, "dp", scatter_dimension=0, tiled=True))
    down_parts = [part.astype(jnp.float32) for part in down_parts]
    output, logit_grad, grad_middle, small_grad = combine(
        parts, spots, route_rows, aux, normed_two, middle, cot, packed_full, choice_count, expert_count
    )
    backward = functools.partial(
        attention_backward, grad_middle, queries, keys, values, attended, normed_one, inputs,
        packed_full, docs_row, docs_column, cosine, sine, small_grad,
    )
    if own_links:
        token_grad, *weight_grads, gu_part, down_part = backward([second_gu, second_grad_down], 7)
        gu_parts.append(gu_part)
        down_parts.append(down_part)
        packed_part = final_reduce(
            [grad.reshape(dp_count, width // dp_count, grad.shape[1]) for grad in weight_grads], 3
        )
    else:
        token_grad, *weight_grads = backward()
        packed_part = lax.psum_scatter(
            jnp.concatenate(weight_grads, 1), "dp", scatter_dimension=0, tiled=True
        )
        packed_part = lax.psum(packed_part, "expert").astype(jnp.float32)
    part_qkv = packed_part[:, :width_qkv]
    part_out = packed_part[:, width_qkv : width_qkv + width_out]
    small_part = packed_part[:, width_qkv + width_out :]
    return (
        output.reshape(tokens.shape),
        token_grad.reshape(tokens.shape),
        logit_grad.reshape(resid_logits.shape),
        part_qkv,
        part_out,
        small_part[:, 18],
        small_part[:, 19],
        small_part[:, 0:12],
        small_part[:, 12:16],
        small_part[:, 16:18],
        jnp.stack(gu_parts),
        jnp.stack(down_parts),
    )


def solution(mesh):
    placed = (
        P(("dp", "expert"), None, None),
        P(("dp", "expert"), None, None),
        P(("dp", "expert"), None, None),
        P(("dp", "expert"), None),
        P("dp", None),
        P("dp", None),
        P("dp"),
        P("dp"),
        P("dp", None),
        P("dp", None),
        P("dp", None),
        P("expert", "dp", None),
        P("expert", "dp", None),
        P(("dp", "expert"), None, None),
    )
    return jax.shard_map(
        shards,
        mesh=mesh,
        in_specs=placed,
        out_specs=(
            P(("dp", "expert"), None, None),
            P(("dp", "expert"), None, None),
            P(("dp", "expert"), None, None),
            P("dp", None),
            P("dp", None),
            P("dp"),
            P("dp"),
            P("dp", None),
            P("dp", None),
            P("dp", None),
            P("expert", "dp", None),
            P("expert", "dp", None),
        ),
        check_vma=False,
    )
```

```python
import functools

import jax
import jax.numpy as jnp
import numpy as np
from jax import lax
from jax.experimental import pallas as pl
from jax.experimental.pallas import tpu as pltpu
from jax.sharding import PartitionSpec as P

HEADS = 12
BLOCK = 256
CAP = 256
GROUP = 256
FF_BLOCK = 512
MESH = pl.DeviceIdType.MESH
epsilon = 1e-06


def rotary_lanes(length, head_dim):
    half_dim = head_dim // 2
    frequency = (10000.0 ** (-np.arange(half_dim, dtype=np.float32) / half_dim)).astype(np.float32)
    angles = (np.arange(length, dtype=np.float32)[:, None] * frequency[None, :]).astype(np.float64)
    cosine = np.cos(angles).astype(np.float32)
    sine = np.sin(angles).astype(np.float32)
    return (
        np.concatenate([cosine] * 4, 1),
        np.concatenate([-sine, sine, -sine, sine], 1),
    )


def nt(left, right):
    return lax.dot_general(left, right, (((1,), (1,)), ((), ())), preferred_element_type=jnp.float32)


def tn(left, right):
    return lax.dot_general(left, right, (((0,), (0,)), ((), ())), preferred_element_type=jnp.float32)


def nn(left, right):
    return jnp.dot(left, right, preferred_element_type=jnp.float32)


def lane_ids(shape):
    return lax.broadcasted_iota(jnp.int32, shape, len(shape) - 1)


def turn(values, cosine, sine):
    lanes = lane_ids(values.shape)
    ahead, behind = pltpu.roll(values, 96, 1), pltpu.roll(values, 32, 1)
    return values * cosine + jnp.where(lanes % 64 < 32, ahead, behind) * sine


def key_span(i):
    return max(0, i - 2) * BLOCK, (i + 1) * BLOCK


def mask_of(docs_column, docs_row, i):
    low, high = key_span(i)
    return docs_column[low:high, :] == docs_row[:, i * BLOCK : (i + 1) * BLOCK]


def attention_forward_kernel(linked, *refs):
    (
        tokens_ref, wq_ref, wk_ref, wv_ref, wo_ref, small_ref, docs_row_ref, docs_column_ref,
        cosine_ref, sine_ref, routes_ref, resid_ref,
    ) = refs[:12]
    (
        normed_ref, q_ref, k_ref, v_ref, attended_ref, middle_ref, normed_two_ref, aux_ref,
    ) = refs[12 + bool(linked) : 20 + bool(linked)]
    step = pl.program_id(0)
    rows = tokens_ref.shape[0]
    if linked:
        branch_ref = refs[22]
        line = LineGather(refs[12].at[0], refs[21], linked, *refs[23:])

        @pl.when(step == 0)
        def _():
            greet(line.peers())
            line.start()

        @pl.when(step == 2)
        def _():
            line.relay(1)
    else:
        branch_ref = refs[20]

    @pl.when(step == 0)
    def _():
        inputs = tokens_ref[...].astype(jnp.float32)
        gains = jnp.transpose(small_ref[:, :128].astype(jnp.float32))[18:19, :]
        scale = lax.rsqrt(jnp.mean(inputs * inputs, -1, keepdims=True) + epsilon)
        normed_ref[...] = (inputs * scale * gains).astype(jnp.bfloat16)
        branch_ref[...] = jnp.zeros_like(branch_ref)

    normed = normed_ref[...]
    cosine, sine = cosine_ref[...], sine_ref[...]
    for w_ref, out_ref, turned in ((wq_ref, q_ref, True), (wk_ref, k_ref, True), (wv_ref, v_ref, False)):
        projected = nn(normed, w_ref[...])
        for half in range(2):
            part = projected[:, half * 128 : half * 128 + 128]
            if turned:
                part = turn(part, cosine, sine)
            out_ref[:, half * 128 : half * 128 + 128] = part.astype(jnp.bfloat16)

    docs_row, docs_column = docs_row_ref[...], docs_column_ref[...]
    for i in range(rows // BLOCK):
        low, high = key_span(i)
        here = slice(i * BLOCK, (i + 1) * BLOCK)
        allowed = mask_of(docs_column, docs_row, i)
        for pair in range(2):
            lanes = slice(pair * 128, pair * 128 + 128)
            queries = q_ref[here, lanes] * jnp.asarray(0.125, jnp.bfloat16)
            keys, values = k_ref[low:high, lanes], v_ref[low:high, lanes]
            left = lane_ids(queries.shape) < 64
            outs = []
            for head in range(2):
                own = left if head == 0 else jnp.logical_not(left)
                scores = nt(keys, jnp.where(own, queries, jnp.zeros_like(queries)))
                scores = jnp.where(allowed, scores, -1e30)
                shifted = jnp.exp(scores - jnp.max(scores, 0, keepdims=True))
                probs = shifted * (1.0 / jnp.sum(shifted, 0, keepdims=True))
                outs.append(tn(probs.astype(jnp.bfloat16), values))
            attended_ref[here, lanes] = jnp.where(left, outs[0], outs[1]).astype(jnp.bfloat16)
    branch_ref[...] += nn(attended_ref[...], wo_ref[...])

    @pl.when(step == pl.num_programs(0) - 1)
    def _():
        small = small_ref[:, :128]
        gains = jnp.transpose(small.astype(jnp.float32))[19:20, :]
        middle = tokens_ref[...].astype(jnp.float32) + branch_ref[...]
        middle_ref[...] = middle
        scale = lax.rsqrt(jnp.mean(middle * middle, -1, keepdims=True) + epsilon)
        normed_two = (middle * scale * gains).astype(jnp.bfloat16)
        normed_two_ref[...] = normed_two
        logits = nn(normed_two, small) + resid_ref[...].astype(jnp.float32)
        lanes = lane_ids(logits.shape)

        def lane(at):
            return jnp.sum(jnp.where(lanes == at, logits, 0.0), -1, keepdims=True)

        def two(first, second):
            peak = jnp.maximum(first, second)
            first, second = jnp.exp(first - peak), jnp.exp(second - peak)
            return first / (first + second), second / (first + second)

        columns = list(two(lane(routes_ref[:, 0:1]), lane(routes_ref[:, 1:2])))
        columns += list(two(lane(12), lane(13))) + list(two(lane(14), lane(15)))
        columns.append(scale)
        aux = jnp.zeros_like(logits)
        for at, column in enumerate(columns):
            aux = jnp.where(lanes == at, column, aux)
        aux_ref[...] = aux
        if linked:
            line.relay(2)
            line.relay(3)
            line.finish()


def attention_forward(
    tokens, packed, docs_row, docs_column, cosine, sine, routes, resid, shards=None,
    dp_count=None, collective=None,
):
    rows, width = tokens.shape
    groups = width // GROUP
    low = jnp.bfloat16
    whole = lambda shape: pl.BlockSpec(shape, lambda j: (0, 0))
    column = lambda at: pl.BlockSpec((width, GROUP), lambda j: (0, at + j))
    out_column = pl.BlockSpec((rows, GROUP), lambda j: (0, j))
    full = jax.ShapeDtypeStruct((rows, width), low)
    linked = shards is not None
    anywhere = pl.BlockSpec(memory_space=pl.ANY)
    links = {"collective_id": collective, "has_side_effects": True} if linked else {}
    gathered = []
    if linked:
        gathered = [jax.ShapeDtypeStruct((dp_count * shards.shape[1], shards.shape[2]), low)]
    return pl.pallas_call(
        functools.partial(attention_forward_kernel, dp_count if linked else 0),
        grid=(groups,),
        out_shape=[full] * 5
        + [
            jax.ShapeDtypeStruct((rows, width), jnp.float32),
            full,
            jax.ShapeDtypeStruct((rows, 128), jnp.float32),
        ]
        + gathered,
        in_specs=[
            whole((rows, width)),
            column(0),
            column(groups),
            column(2 * groups),
            pl.BlockSpec((GROUP, width), lambda j: (j, 3)),
            pl.BlockSpec((width, 256), lambda j: (0, 12)),
            whole((1, rows)),
            whole((rows, 1)),
            whole((rows, 128)),
            whole((rows, 128)),
            whole((rows, 2)),
            whole((rows, 128)),
        ]
        + [anywhere] * linked,
        out_specs=[whole((rows, width))]
        + [out_column] * 4
        + [whole((rows, width)), whole((rows, width)), whole((rows, 128))]
        + [anywhere] * linked,
        scratch_shapes=[pltpu.VMEM((rows, width), jnp.float32)]
        + (gather_semaphores(dp_count) if linked else []),
        compiler_params=pltpu.CompilerParams(
            dimension_semantics=("arbitrary",), vmem_limit_bytes=56 * 2**20, **links
        ),
        cost_estimate=pl.CostEstimate(
            flops=2 * rows * width * 4 * width + 8 * rows * rows * width // 2,
            bytes_accessed=24 * rows * width,
            transcendentals=rows * rows * HEADS // 2,
        ),
        name="attention_forward",
    )(
        tokens, packed, packed, packed, packed, packed, docs_row, docs_column, cosine, sine, routes,
        resid, *([shards] if linked else []),
    )


def attention_backward_kernel(count, *refs):
    (
        grad_middle_ref, q_ref, k_ref, v_ref, attended_ref, normed_ref, tokens_ref,
        wq_ref, wk_ref, wv_ref, wo_ref, small_ref, docs_row_ref, docs_column_ref,
        cosine_ref, sine_ref, small_grad_ref,
    ) = refs[:17]
    sources, refs = refs[17 : 17 + count], refs[17 + count :]
    token_grad_ref, gq_ref, gk_ref, gv_ref, go_ref, small_out_ref = refs[:6]
    totals, refs = refs[6 : 6 + count], refs[6 + count :]
    branch_ref, back_ref, turned_ref, key_acc, value_acc, query_acc = refs[:6]
    step = pl.program_id(0)
    rows, width = tokens_ref.shape
    if count:
        line = line_reduce(sources[0], totals[0], refs[6:], 2)

        @pl.when(step == 0)
        def _():
            greet(line.peers())
            line.each_plane(line.start)

        pl.when(step == 1)(lambda: line.turns([0], []))
        pl.when(step == 2)(lambda: line.turns([1], [0]))

    @pl.when(step == 0)
    def _():
        branch_ref[...] = grad_middle_ref[...].astype(jnp.bfloat16)
        back_ref[...] = jnp.zeros_like(back_ref)

    grad_branch = branch_ref[...]
    grad_attended = nt(grad_branch, wo_ref[...]).astype(jnp.bfloat16)
    go_ref[...] = tn(attended_ref[...], grad_branch).astype(jnp.bfloat16)
    cosine, sine = cosine_ref[...], sine_ref[...]
    docs_row, docs_column = docs_row_ref[...], docs_column_ref[...]
    for pair in range(2):
        lanes = slice(pair * 128, pair * 128 + 128)
        key_acc[...] = jnp.zeros_like(key_acc)
        value_acc[...] = jnp.zeros_like(value_acc)
        for i in range(rows // BLOCK):
            low, high = key_span(i)
            here = slice(i * BLOCK, (i + 1) * BLOCK)
            allowed = mask_of(docs_column, docs_row, i)
            queries = q_ref[here, lanes] * jnp.asarray(0.125, jnp.bfloat16)
            grads = grad_attended[here, lanes]
            keys, values = k_ref[low:high, lanes], v_ref[low:high, lanes]
            left = lane_ids(queries.shape) < 64
            query_grads = []
            key_grad, value_grad = None, None
            for head in range(2):
                own = left if head == 0 else jnp.logical_not(left)
                own_queries = jnp.where(own, queries, jnp.zeros_like(queries))
                own_grads = jnp.where(own, grads, jnp.zeros_like(grads))
                scores = jnp.where(allowed, nt(keys, own_queries), -1e30)
                shifted = jnp.exp(scores - jnp.max(scores, 0, keepdims=True))
                probs = shifted * (1.0 / jnp.sum(shifted, 0, keepdims=True))
                grad_probs = nt(values, own_grads)
                inner = jnp.sum(probs * grad_probs, 0, keepdims=True)
                grad_scores = (probs * (grad_probs - inner)).astype(jnp.bfloat16)
                part_value = nn(probs.astype(jnp.bfloat16), own_grads)
                part_key = nn(grad_scores, own_queries)
                value_grad = part_value if head == 0 else value_grad + part_value
                key_grad = part_key if head == 0 else key_grad + part_key
                query_grads.append(tn(grad_scores, keys))
            value_acc[low:high, :] += value_grad
            key_acc[low:high, :] += key_grad
            query_acc[here, :] = jnp.where(left, query_grads[0], query_grads[1]) * 0.125
        turned_ref[0, :, lanes] = turn(query_acc[...], cosine, -sine).astype(jnp.bfloat16)
        turned_ref[1, :, lanes] = turn(key_acc[...], cosine, -sine).astype(jnp.bfloat16)
        turned_ref[2, :, lanes] = value_acc[...].astype(jnp.bfloat16)
    normed = normed_ref[...]
    for at, (w_ref, out_ref) in enumerate(((wq_ref, gq_ref), (wk_ref, gk_ref), (wv_ref, gv_ref))):
        turned = turned_ref[at]
        out_ref[...] = tn(normed, turned).astype(jnp.bfloat16)
        back_ref[...] += nt(turned, w_ref[...])

    @pl.when(step == pl.num_programs(0) - 1)
    def _():
        gains = jnp.transpose(small_ref[:, :128].astype(jnp.float32))[18:19, :]
        inputs = tokens_ref[...].astype(jnp.float32)
        grads = back_ref[...]
        scale = lax.rsqrt(jnp.mean(inputs * inputs, -1, keepdims=True) + epsilon)
        weighted = grads * gains
        mean = jnp.mean(weighted * inputs, -1, keepdims=True)
        grad_inputs = scale * weighted - inputs * (scale * scale * scale * mean)
        token_grad_ref[...] = (grad_inputs + grad_middle_ref[...]).astype(jnp.bfloat16)
        gain_grad = jnp.sum(grads * inputs * scale, 0, keepdims=True)
        column = jnp.transpose(jnp.broadcast_to(gain_grad, (128, width)))
        small_grad = small_grad_ref[...]
        small_grad = jnp.where(lane_ids(small_grad.shape) == 18, column, small_grad)
        small_out_ref[:, :128] = small_grad.astype(jnp.bfloat16)
        small_out_ref[:, 128:] = jnp.zeros((width, 128), jnp.bfloat16)
        if count:
            line.turns([2, 3], [1, 2, 3])
            line.each_plane(line.finish)


def attention_backward(
    grad_middle, queries, keys, values, attended, normed, tokens, packed, docs_row, docs_column,
    cosine, sine, small_grad, sources=(), collective=None,
):
    rows, width = tokens.shape
    groups = width // GROUP
    low = jnp.bfloat16
    whole = lambda shape: pl.BlockSpec(shape, lambda j: (0, 0))
    column = lambda at: pl.BlockSpec((width, GROUP), lambda j: (0, at + j))
    by_group = pl.BlockSpec((rows, GROUP), lambda j: (0, j))
    weight = jax.ShapeDtypeStruct((width, width), low)
    linked = len(sources) > 0
    links = {"collective_id": collective, "has_side_effects": True} if linked else {}
    sums = []
    for source in sources:
        sides = source.shape[0] if len(source.shape) == 3 else 1
        sums.append((source.shape[-2] // 8, sides * source.shape[-1]))
    once = lambda shape: pl.BlockSpec(
        shape, lambda j: (0, 0), pipeline_mode=pl.Buffered(1)
    )
    return pl.pallas_call(
        functools.partial(attention_backward_kernel, len(sources)),
        grid=(groups,),
        out_shape=[jax.ShapeDtypeStruct((rows, width), low)]
        + [weight] * 4
        + [jax.ShapeDtypeStruct((width, 256), low)]
        + [jax.ShapeDtypeStruct(shape, jnp.float32) for shape in sums],
        in_specs=[
            once((rows, width)),
            by_group,
            by_group,
            by_group,
            by_group,
            once((rows, width)),
            once((rows, width)),
            column(0),
            column(groups),
            column(2 * groups),
            pl.BlockSpec((GROUP, width), lambda j: (j, 3)),
            pl.BlockSpec((width, 256), lambda j: (0, 12)),
            once((1, rows)),
            once((rows, 1)),
            once((rows, 128)),
            once((rows, 128)),
            once((width, 128)),
        ]
        + [pl.BlockSpec(memory_space=pl.ANY)] * len(sources),
        out_specs=[
            whole((rows, width)),
            column(0),
            column(0),
            column(0),
            pl.BlockSpec((GROUP, width), lambda j: (j, 0)),
            whole((width, 256)),
        ]
        + [whole(shape) for shape in sums],
        scratch_shapes=[
            pltpu.VMEM((rows, width), low),
            pltpu.VMEM((rows, width), jnp.float32),
            pltpu.VMEM((3, rows, GROUP), low),
            pltpu.VMEM((rows, 128), jnp.float32),
            pltpu.VMEM((rows, 128), jnp.float32),
            pltpu.VMEM((rows, 128), jnp.float32),
        ]
        + (reduce_scratch(sources[0], 2) if linked else []),
        compiler_params=pltpu.CompilerParams(
            dimension_semantics=("arbitrary",), vmem_limit_bytes=61 * 2**20, **links
        ),
        cost_estimate=pl.CostEstimate(
            flops=4 * rows * width * 4 * width + 20 * rows * rows * width // 2,
            bytes_accessed=32 * rows * width,
            transcendentals=rows * rows * HEADS // 2,
        ),
        name="attention_backward",
    )(
        grad_middle, queries, keys, values, attended, normed, tokens, packed, packed, packed,
        packed, packed, docs_row, docs_column, cosine, sine, small_grad, *sources,
    )


def routing_kernel(expert_count, routes_ref, columns_ref, rows_ref):
    rows = routes_ref.shape[0]
    lanes = lane_ids((rows, 128))
    first = (lanes == routes_ref[:, 0:1]).astype(jnp.float32)
    second = (lanes == routes_ref[:, 1:2]).astype(jnp.float32)
    down = lax.broadcasted_iota(jnp.int32, (rows, rows), 0)
    lower = (down > lane_ids((rows, rows))).astype(jnp.bfloat16)
    before_first = nn(lower, first.astype(jnp.bfloat16))
    before_second = nn(lower, second.astype(jnp.bfloat16)) + jnp.sum(first, 0, keepdims=True)
    spots = []
    for picked, before, at in ((first, before_first, 0), (second, before_second, 1)):
        rank = jnp.sum(picked * before, -1, keepdims=True)
        route = routes_ref[:, at : at + 1]
        spot = route.astype(jnp.float32) * CAP + rank
        spots.append(jnp.where(route < expert_count, spot, jnp.full_like(spot, 2.0 * expert_count * CAP)))
    both = jnp.where(lanes == 0, spots[0], jnp.where(lanes == 1, spots[1], 0.0))
    columns_ref[...] = both.astype(jnp.int32)
    rows_ref[...] = jnp.transpose(both)[0:8, :].astype(jnp.int32)


def routing(routes, expert_count):
    rows = routes.shape[0]
    return pl.pallas_call(
        functools.partial(routing_kernel, expert_count),
        out_shape=[
            jax.ShapeDtypeStruct((rows, 128), jnp.int32),
            jax.ShapeDtypeStruct((8, rows), jnp.int32),
        ],
        compiler_params=pltpu.CompilerParams(vmem_limit_bytes=40 * 2**20),
        name="routing",
    )(routes)


def dispatch_kernel(spots_ref, aux_ref, normed_ref, cot_ref, rows_ref, grads_ref, gates_ref):
    step = pl.program_id(0)

    @pl.when(step == 0)
    def _():
        gates_ref[...] = jnp.transpose(aux_ref[...])[0:8, :]

    shape = (rows_ref.shape[0], normed_ref.shape[0])
    slots = step * rows_ref.shape[0] + lax.broadcasted_iota(jnp.int32, shape, 0)
    first, second = slots == spots_ref[0:1, :], slots == spots_ref[1:2, :]
    gates = jnp.sum(
        jnp.where(first, gates_ref[0:1, :], jnp.where(second, gates_ref[1:2, :], 0.0)), -1, keepdims=True
    )
    chosen = jnp.where(first | second, 1.0, 0.0).astype(jnp.bfloat16)
    rows_ref[...] = nn(chosen, normed_ref[...]).astype(jnp.bfloat16)
    grads_ref[...] = (nn(chosen, cot_ref[...]) * gates).astype(jnp.bfloat16)


def dispatch(spots, aux, normed, cot, owner_count, local_count):
    rows, width = normed.shape
    slot_count = owner_count * local_count * CAP
    whole = lambda shape: pl.BlockSpec(shape, lambda j: (0, 0))
    block = pl.BlockSpec(
        (None, None, CAP, width), lambda j: (j % local_count, j // local_count, 0, 0)
    )
    return pl.pallas_call(
        dispatch_kernel,
        grid=(slot_count // CAP,),
        out_shape=[jax.ShapeDtypeStruct((local_count, owner_count, CAP, width), jnp.bfloat16)] * 2,
        in_specs=[whole((8, rows)), whole((rows, 128)), whole((rows, width)), whole((rows, width))],
        out_specs=[block, block],
        scratch_shapes=[pltpu.VMEM((8, rows), jnp.float32)],
        compiler_params=pltpu.CompilerParams(
            dimension_semantics=("arbitrary",), vmem_limit_bytes=60 * 2**20
        ),
        cost_estimate=pl.CostEstimate(
            flops=4 * slot_count * rows * width,
            bytes_accessed=4 * (rows + slot_count) * width,
            transcendentals=0,
        ),
        name="dispatch",
    )(spots, aux, normed, cot)


def halves(values):
    high = values.astype(jnp.bfloat16)
    return high, (values - high.astype(jnp.float32)).astype(jnp.bfloat16)


def combine_kernel(
    expert_count, local_count, *refs
):
    parts, refs = refs[:local_count], refs[local_count:]
    (
        spots_ref, routes_ref, aux_ref, normed_ref, middle_ref, cot_ref, small_ref,
        output_ref, logit_ref, grad_middle_ref, small_out_ref, vectors_ref, small_grad_ref,
    ) = refs
    step = pl.program_id(0)

    @pl.when(step == 0)
    def _():
        vectors_ref[0:8, :] = jnp.transpose(small_ref[:, :128].astype(jnp.float32))[16:24, :]
        vectors_ref[8:16, :] = jnp.zeros((8, vectors_ref.shape[1]), jnp.float32)
        small_grad_ref[...] = jnp.zeros_like(small_grad_ref)

    rows, width = normed_ref.shape
    normed_low, cot_low = normed_ref[...], cot_ref[...]
    normed, cot = normed_low.astype(jnp.float32), cot_low.astype(jnp.float32)
    total = lambda values: jnp.sum(values, -1, keepdims=True)
    picks, back = [0.0, 0.0], 0.0
    for e in range(local_count):
        count = parts[e].shape[0] * CAP
        slots = lane_ids((rows, count))
        slots = slots // CAP * (local_count * CAP) + e * CAP + slots % CAP
        hits = [slots == spots_ref[:, s : s + 1] for s in range(2)]
        chosen = [jnp.where(hit, 1.0, 0.0).astype(jnp.bfloat16) for hit in hits]
        returned = parts[e][:, 0].reshape(count, width)
        for s in range(2):
            picks[s] = picks[s] + nn(chosen[s], returned)
        back = back + nn(chosen[0] + chosen[1], parts[e][:, 1].reshape(count, width))
    inner = [total(pick * cot) for pick in picks]
    gates = [aux_ref[:, s : s + 1] for s in range(2)]
    routes = [routes_ref[:, s : s + 1] for s in range(2)]
    dot_copy = total(cot * normed)

    def weight_of(route):
        return sum(jnp.where(routes[s] == route, gates[s], 0.0) for s in range(2))

    copy_weight = weight_of(expert_count + 1)
    mix = gates[0] * picks[0] + gates[1] * picks[1]
    pass_weight = copy_weight
    gate_grads = [
        inner[s] + jnp.where(routes[s] == expert_count + 1, dot_copy, 0.0) for s in range(2)
    ]
    lanes = lane_ids((rows, 128))
    spread = jnp.zeros((rows, 128), jnp.float32)
    for k in range(2):
        vector = vectors_ref[k : k + 1, :]
        keep, blend = aux_ref[:, 2 + 2 * k : 3 + 2 * k], aux_ref[:, 3 + 2 * k : 4 + 2 * k]
        weight = weight_of(expert_count + 2 + k)
        dot_vector = total(cot * vector)
        pass_weight = pass_weight + weight * keep
        mix = mix + (weight * blend) * vector
        value = keep * dot_copy + blend * dot_vector
        for s in range(2):
            gate_grads[s] = gate_grads[s] + jnp.where(routes[s] == expert_count + 2 + k, value, 0.0)
        term = keep * blend * (weight * dot_copy - weight * dot_vector)
        spread = jnp.where(lanes == 12 + 2 * k, term, spread)
        spread = jnp.where(lanes == 13 + 2 * k, -term, spread)
        spread = jnp.where(lanes == 16 + k, weight * blend, spread)
    mix = mix + pass_weight * normed
    middle, scale = middle_ref[...], aux_ref[:, 6:7]
    output_ref[...] = (middle + mix).astype(jnp.bfloat16)
    mean = gates[0] * gate_grads[0] + gates[1] * gate_grads[1]
    for s in range(2):
        spread = jnp.where(lanes == routes[s], gates[s] * (gate_grads[s] - mean), spread)
    logit_ref[...] = spread[:, : logit_ref.shape[1]].astype(jnp.bfloat16)
    logits = jnp.where(lanes < 16, spread, 0.0)
    high, low = halves(logits)
    small = small_ref[:, :128]
    vector_high, vector_low = halves(spread - logits)
    small_grad_ref[...] += (
        tn(normed_low, high) + tn(normed_low, low) + tn(cot_low, vector_high) + tn(cot_low, vector_low)
    )
    grads = back + pass_weight * cot + nt(high, small) + nt(low, small)
    vectors_ref[8:9, :] += jnp.sum(grads * middle * scale, 0, keepdims=True)
    weighted = grads * vectors_ref[3:4, :]
    mean = jnp.mean(weighted * middle, -1, keepdims=True)
    grad_middle_ref[...] = cot + scale * weighted - middle * (scale * scale * scale * mean)

    @pl.when(step == pl.num_programs(0) - 1)
    def _():
        column = jnp.transpose(jnp.broadcast_to(vectors_ref[8:9, :], (128, width)))
        small_grad = small_grad_ref[...]
        small_out_ref[...] = jnp.where(lane_ids(small_grad.shape) == 19, column, small_grad)


def combine(parts, spots, routes, aux, normed, middle, cot, packed, choice_count, expert_count):
    rows, width = normed.shape
    local_count = len(parts)
    slot_count = expert_count * CAP
    size = 256
    block = lambda columns: pl.BlockSpec((size, columns), lambda j: (j, 0))
    whole = lambda shape: pl.BlockSpec(shape, lambda j: (0,) * len(shape))
    return pl.pallas_call(
        functools.partial(combine_kernel, expert_count, local_count),
        grid=(rows // size,),
        out_shape=[
            jax.ShapeDtypeStruct((rows, width), jnp.bfloat16),
            jax.ShapeDtypeStruct((rows, choice_count), jnp.bfloat16),
            jax.ShapeDtypeStruct((rows, width), jnp.float32),
            jax.ShapeDtypeStruct((width, 128), jnp.float32),
        ],
        in_specs=[whole(part.shape) for part in parts]
        + [
            block(128),
            block(2),
            block(128),
            block(width),
            block(width),
            block(width),
            pl.BlockSpec((width, 256), lambda j: (0, 12)),
        ],
        out_specs=[block(width), block(choice_count), block(width), whole((width, 128))],
        scratch_shapes=[pltpu.VMEM((16, width), jnp.float32), pltpu.VMEM((width, 128), jnp.float32)],
        compiler_params=pltpu.CompilerParams(
            dimension_semantics=("arbitrary",), vmem_limit_bytes=56 * 2**20
        ),
        cost_estimate=pl.CostEstimate(
            flops=6 * slot_count * rows * width,
            bytes_accessed=14 * rows * width + 4 * slot_count * width,
            transcendentals=0,
        ),
        name="combine",
    )(*parts, spots, routes, aux, normed, middle, cot, packed)


def experts_kernel(mode, dp_count, *refs):
    rows_ref, grads_ref, w_gate_ref, w_up_ref, w_down_ref = refs[:5]
    if mode == 0:
        grad_gu_ref, grad_down_ref, both_ref, turned_ref, out_ref, back_ref = refs[5:]
    if mode == 1:
        next_rows, next_grads, shards_ref, grad_gu_ref, grad_down_ref, both_ref = refs[5:11]
        rows_out, grads_out, full_ref, turned_ref, out_ref, back_ref = refs[11:17]
        sems = refs[17:]
    if mode == 2:
        before_ref, source_ref, grad_gu_ref, grad_down_ref, first_in, second_in, total_ref = refs[5:12]
        turned_ref, out_ref, back_ref, both_ref = refs[12:16]
        sems = refs[16:]
    step = pl.program_id(0)
    width = rows_ref.shape[-1]
    rows = rows_ref[...].reshape(-1, width)
    grads = grads_ref[...].reshape(-1, width)
    if mode == 1:
        half = full_ref.shape[1] // 2
        lines = []
        for n in range(2):
            columns = slice(n * half, n * half + half)
            lines.append(
                LineGather(
                    shards_ref.at[1, :, columns], full_ref, dp_count, *sems[3 * n : 3 * n + 3], columns
                )
            )
        trades = [
            Trade(next_rows.at[1], rows_out, *sems[6:8]),
            Trade(next_grads.at[1], grads_out, *sems[8:10]),
        ]

        @pl.when(step == 0)
        def _():
            greet(lines[0].peers() + trades[0].peers())
            for part in lines + trades:
                part.start()

        for hop in range(1, 4):

            @pl.when(step == hop)
            def _(hop=hop):
                for part in lines:
                    part.relay(hop)

    if mode == 2:
        trades = [Trade(before_ref, first_in, *sems[:2]), Trade(both_ref, second_in, *sems[2:4])]
        line = line_reduce(source_ref, total_ref, sems[4:], 2)

        @pl.when(step == 0)
        def _():
            greet(line.peers() + trades[0].peers())
            line.each_plane(line.start)
            trades[0].start()

        pl.when(step == 2)(lambda: line.turns([0], []))

    @pl.when(step == 0)
    def _():
        turned_ref[...] = jnp.transpose(rows)
        out_ref[...] = jnp.zeros_like(out_ref)
        back_ref[...] = jnp.zeros_like(back_ref)

    w_gate, w_up, w_down = w_gate_ref[...], w_up_ref[...], w_down_ref[...]
    gate, up = nn(rows, w_gate), nn(rows, w_up)
    squashed = 1.0 / (1.0 + jnp.exp(-gate))
    silu = gate * squashed
    activated = (silu * up).astype(jnp.bfloat16)
    grad_act = nt(grads, w_down)
    grad_gate = (grad_act * up * (squashed * (1.0 + gate * (1.0 - squashed)))).astype(jnp.bfloat16)
    grad_up = (grad_act * silu).astype(jnp.bfloat16)
    out_ref[...] += nn(activated, w_down)
    grad_down_ref[...] = tn(activated, grads).astype(jnp.bfloat16)
    back_ref[...] += nt(grad_gate, w_gate) + nt(grad_up, w_up)
    grad_gu_ref[0] = nn(turned_ref[...], grad_gate).astype(jnp.bfloat16)
    grad_gu_ref[1] = nn(turned_ref[...], grad_up).astype(jnp.bfloat16)

    @pl.when(step == pl.num_programs(0) - 1)
    def _():
        shape = (both_ref.shape[0],) + both_ref.shape[2:]
        both_ref[:, 0] = out_ref[...].astype(jnp.bfloat16).reshape(shape)
        both_ref[:, 1] = back_ref[...].astype(jnp.bfloat16).reshape(shape)
        if mode == 1:
            for part in lines + trades:
                part.finish()
        if mode == 2:
            trades[1].start()
            line.turns([1, 2, 3], [0, 1, 2, 3])
            line.each_plane(line.finish)
            for trade in trades:
                trade.finish()


def experts(rows, grads, gate, up, down, mode=0, dp_count=0, extras=(), collective=None):
    owners, cap, width = rows.shape
    hidden = down.shape[0]
    count = owners * cap
    block = FF_BLOCK if count <= 1024 else FF_BLOCK // 4
    steps = hidden // block
    low = jnp.bfloat16
    pairs = pl.BlockSpec((owners, cap, width), lambda j: (0, 0, 0), pipeline_mode=pl.Buffered(1))
    anywhere = pl.BlockSpec(memory_space=pl.ANY)
    both = jax.ShapeDtypeStruct((owners, 2, cap, width), low)
    links = {"collective_id": collective, "has_side_effects": True} if mode else {}
    out_shape = [
        jax.ShapeDtypeStruct((2, width, hidden), low),
        jax.ShapeDtypeStruct((hidden, width), low),
    ]
    out_specs = [
        pl.BlockSpec((2, width, block), lambda j: (0, 0, j)),
        pl.BlockSpec((block, width), lambda j: (j, 0)),
    ]
    scratch = [
        pltpu.VMEM((width, count), low),
        pltpu.VMEM((count, width), jnp.float32),
        pltpu.VMEM((count, width), jnp.float32),
    ]
    if mode < 2:
        out_shape.append(both)
        out_specs.append(pl.BlockSpec(both.shape, lambda j: (0, 0, 0, 0)))
    if mode == 1:
        shards = extras[2]
        out_shape += [jax.ShapeDtypeStruct(rows.shape, low)] * 2
        out_shape.append(jax.ShapeDtypeStruct((dp_count * shards.shape[1], shards.shape[2]), low))
        out_specs += [anywhere] * 3
        scratch += gather_semaphores(dp_count) * 2 + trade_semaphores(owners) + trade_semaphores(owners)
    if mode == 2:
        total = (width // 8, 2 * hidden)
        out_shape += [both, both, jax.ShapeDtypeStruct(total, jnp.float32)]
        out_specs += [anywhere] * 2 + [pl.BlockSpec(total, lambda j: (0, 0))]
        scratch.append(pltpu.VMEM(both.shape, low))
        scratch += trade_semaphores(owners) + trade_semaphores(owners) + reduce_scratch(extras[1], 2)
    return pl.pallas_call(
        functools.partial(experts_kernel, mode, dp_count),
        grid=(steps,),
        out_shape=out_shape,
        in_specs=[
            pairs,
            pairs,
            pl.BlockSpec((width, block), lambda j: (0, j)),
            pl.BlockSpec((width, block), lambda j: (0, up.shape[1] // block - steps + j)),
            pl.BlockSpec((block, width), lambda j: (j, 0)),
        ]
        + [anywhere] * len(extras),
        out_specs=out_specs,
        scratch_shapes=scratch,
        compiler_params=pltpu.CompilerParams(
            dimension_semantics=("arbitrary",), vmem_limit_bytes=60 * 2**20, **links
        ),
        cost_estimate=pl.CostEstimate(
            flops=18 * count * width * hidden,
            bytes_accessed=12 * width * hidden + 8 * count * width,
            transcendentals=count * hidden,
        ),
        name="experts",
    )(rows, grads, gate, up, down, *extras)


def dp_grid(dp_count):
    outer = 4 if dp_count % 4 == 0 else 1
    return outer, dp_count // outer


def place():
    me, mine = lax.axis_index("dp"), lax.axis_index("expert")
    return me, mine


def greet(peers):
    barrier = pltpu.get_barrier_semaphore()
    for peer in peers:
        pl.semaphore_signal(barrier, inc=1, device_id=peer, device_id_type=MESH)
    pl.semaphore_wait(barrier, len(peers))


class LineGather:
    def __init__(self, shard, full, dp_count, send_sem, recv_sem, own_sem, columns=None, also=None):
        self.columns = slice(None) if columns is None else columns
        self.also = also or (lambda chunk: None)
        self.shard, self.full, self.dp_count = shard, full, dp_count
        self.send_sem, self.recv_sem, self.own_sem = send_sem, recv_sem, own_sem
        self.outer_count, self.inner_count = dp_grid(dp_count)
        self.me, self.mine = place()
        self.outer, self.inner = self.me // self.inner_count, self.me % self.inner_count
        self.inner_peers = [
            lax.rem(self.inner + k, self.inner_count) for k in range(1, self.inner_count)
        ]
        self.can_up, self.can_down = self.outer < self.outer_count - 1, self.outer > 0

    def peers(self):
        below = lax.rem(self.outer + self.outer_count - 1, self.outer_count)
        above = lax.rem(self.outer + 1, self.outer_count)
        return [(peer * self.inner_count + self.inner, self.mine) for peer in (below, above)] + [
            (self.outer * self.inner_count + peer, self.mine) for peer in self.inner_peers
        ]

    def spot(self, chunk):
        rows = self.shard.shape[0]
        return self.full.at[pl.ds(pl.multiple_of(chunk * rows, 8), rows), self.columns]

    def copy(self, source, chunk, device, way, at):
        return pltpu.make_async_remote_copy(
            src_ref=source,
            dst_ref=self.spot(chunk),
            send_sem=self.send_sem.at[way, at, chunk],
            recv_sem=self.recv_sem.at[chunk],
            device_id=(device, self.mine),
            device_id_type=MESH,
        )

    def up(self, source, chunk):
        return self.copy(source, chunk, (self.outer + 1) * self.inner_count + self.inner, 1, 0)

    def down(self, source, chunk):
        return self.copy(source, chunk, (self.outer - 1) * self.inner_count + self.inner, 2, 0)

    def across(self, source, chunk):
        return [
            self.copy(source, chunk, self.outer * self.inner_count + peer, 0, at)
            for at, peer in enumerate(self.inner_peers)
        ]

    def keep(self):
        return pltpu.make_async_copy(self.shard, self.spot(self.me), self.own_sem)

    def arrived(self, chunk):
        pltpu.make_async_copy(self.spot(chunk), self.spot(chunk), self.recv_sem.at[chunk]).wait()

    def start(self):
        for copy in self.across(self.shard, self.me):
            copy.start()
        pl.when(self.can_up)(lambda: self.up(self.shard, self.me).start())
        pl.when(self.can_down)(lambda: self.down(self.shard, self.me).start())
        self.keep().start()

    def relay(self, step):
        low, high = self.outer - step, self.outer + step

        def pass_on(source, upward):
            chunk = source * self.inner_count + self.inner
            self.arrived(chunk)
            if upward:
                pl.when(self.can_up)(lambda: self.up(self.spot(chunk), chunk).start())
            else:
                pl.when(self.can_down)(lambda: self.down(self.spot(chunk), chunk).start())
            for copy in self.across(self.spot(chunk), chunk):
                copy.start()
            self.also(chunk)

        pl.when(low >= 0)(lambda: pass_on(low, True))
        pl.when(high < self.outer_count)(lambda: pass_on(high, False))

    def finish(self):
        self.keep().wait()
        for peer in self.inner_peers:
            for k in range(self.outer_count):
                chunk = lax.rem(self.outer + k, self.outer_count) * self.inner_count + peer
                self.arrived(chunk)
                self.also(chunk)
        for plane in range(self.outer_count):
            chunk = plane * self.inner_count + self.inner
            for copy in self.across(self.spot(chunk), chunk):
                copy.wait_send()
            pl.when(self.can_up & (self.outer >= plane))(
                lambda chunk=chunk: self.up(self.spot(chunk), chunk).wait_send()
            )
            pl.when(self.can_down & (self.outer <= plane))(
                lambda chunk=chunk: self.down(self.spot(chunk), chunk).wait_send()
            )


def gather_semaphores(dp_count):
    inner_count = dp_grid(dp_count)[1]
    return [
        pltpu.SemaphoreType.DMA((3, max(1, inner_count - 1), dp_count)),
        pltpu.SemaphoreType.DMA((dp_count,)),
        pltpu.SemaphoreType.DMA,
    ]


def by_rows(count, body):
    def step(i, carry):
        body(i * 16)
        return carry

    lax.fori_loop(0, count // 16, step, 0)


class Trade:
    def __init__(self, source, target, send_sem, recv_sem):
        self.source, self.target, self.send_sem, self.recv_sem = source, target, send_sem, recv_sem
        self.me, self.mine = place()
        count = target.shape[0]
        self.partners = [lax.rem(self.mine + k, count) for k in range(1, count)]

    def peers(self):
        return [(self.me, peer) for peer in self.partners]

    def copy(self, k):
        peer = self.partners[k]
        return pltpu.make_async_remote_copy(
            src_ref=self.source.at[peer],
            dst_ref=self.target.at[self.mine],
            send_sem=self.send_sem.at[k + 1],
            recv_sem=self.recv_sem.at[self.mine],
            device_id=(self.me, peer),
            device_id_type=MESH,
        )

    def keep(self):
        return pltpu.make_async_copy(
            self.source.at[self.mine], self.target.at[self.mine], self.send_sem.at[0]
        )

    def start(self):
        for k in range(len(self.partners)):
            self.copy(k).start()
        self.keep().start()

    def finish(self):
        self.keep().wait()
        for k, peer in enumerate(self.partners):
            there = self.target.at[peer]
            pltpu.make_async_copy(there, there, self.recv_sem.at[peer]).wait()
            self.copy(k).wait_send()


def trade_semaphores(owner_count):
    return [pltpu.SemaphoreType.DMA((owner_count,)), pltpu.SemaphoreType.DMA((owner_count,))]


def expert_gather_kernel(dp_count, rows_ref, grads_ref, shards_ref, rows_out, grads_out, full_ref, *sems):
    line = LineGather(shards_ref.at[0], full_ref, dp_count, *sems[:3])
    trades = [Trade(rows_ref.at[0], rows_out, *sems[3:5]), Trade(grads_ref.at[0], grads_out, *sems[5:7])]
    greet(line.peers() + trades[0].peers())
    line.start()
    for trade in trades:
        trade.start()
    for hop in range(1, line.outer_count):
        line.relay(hop)
    line.finish()
    for trade in trades:
        trade.finish()


def expert_gather(rows, grads, shards, dp_count, collective):
    anywhere = pl.BlockSpec(memory_space=pl.ANY)
    return pl.pallas_call(
        functools.partial(expert_gather_kernel, dp_count),
        out_shape=[
            jax.ShapeDtypeStruct(rows.shape[1:], rows.dtype),
            jax.ShapeDtypeStruct(grads.shape[1:], grads.dtype),
            jax.ShapeDtypeStruct((dp_count * shards.shape[1], shards.shape[2]), shards.dtype),
        ],
        in_specs=[anywhere] * 3,
        out_specs=[anywhere] * 3,
        scratch_shapes=gather_semaphores(dp_count)
        + trade_semaphores(rows.shape[1])
        + trade_semaphores(rows.shape[1]),
        compiler_params=pltpu.CompilerParams(collective_id=collective, has_side_effects=True),
        name="expert_gather",
    )(rows, grads, shards)


def small_gather_kernel(
    dp_count, expert_count, shard_ref, routes_ref, full_ref, columns_ref, rows_ref,
    send_sem, recv_sem, own_sem, pass_sem, mate_sem, all_sem,
):
    me, mine = place()
    rows, columns = shard_ref.shape
    half = columns // 2
    side = mine % 2
    mate = mine + 1 - 2 * side
    own_columns = pl.ds(pl.multiple_of(side * half, 128), half)
    mate_columns = pl.ds(pl.multiple_of((1 - side) * half, 128), half)

    def there(chunk, lanes):
        return full_ref.at[pl.ds(pl.multiple_of(chunk * rows, 8), rows), lanes]

    def pass_copy(chunk):
        return pltpu.make_async_remote_copy(
            src_ref=there(chunk, own_columns),
            dst_ref=there(chunk, own_columns),
            send_sem=pass_sem.at[chunk],
            recv_sem=mate_sem.at[chunk],
            device_id=(me, mate),
            device_id_type=MESH,
        )

    line = LineGather(
        shard_ref.at[:, own_columns], full_ref, dp_count, send_sem, recv_sem, own_sem,
        own_columns, lambda chunk: pass_copy(chunk).start(),
    )
    greet(line.peers() + [(me, mate)])
    line.start()
    other = pltpu.make_async_copy(shard_ref.at[:, mate_columns], there(me, mate_columns), all_sem)
    other.start()
    routing_kernel(expert_count, routes_ref, columns_ref, rows_ref)
    for hop in range(1, line.outer_count):
        line.relay(hop)
    line.finish()
    other.wait()
    for k in range(1, dp_count):
        chunk = lax.rem(me + k, dp_count)
        target = there(chunk, mate_columns)
        pltpu.make_async_copy(target, target, mate_sem.at[chunk]).wait()
        pass_copy(chunk).wait_send()


def small_gather(shard, routes, expert_count, dp_count, collective):
    rows, columns = shard.shape
    tokens = routes.shape[0]
    anywhere, in_vmem = pl.BlockSpec(memory_space=pl.ANY), pl.BlockSpec(memory_space=pltpu.VMEM)
    return pl.pallas_call(
        functools.partial(small_gather_kernel, dp_count, expert_count),
        out_shape=[
            jax.ShapeDtypeStruct((dp_count * rows, columns), shard.dtype),
            jax.ShapeDtypeStruct((tokens, 128), jnp.int32),
            jax.ShapeDtypeStruct((8, tokens), jnp.int32),
        ],
        in_specs=[anywhere, in_vmem],
        out_specs=[anywhere, in_vmem, in_vmem],
        scratch_shapes=gather_semaphores(dp_count)
        + [
            pltpu.SemaphoreType.DMA((dp_count,)),
            pltpu.SemaphoreType.DMA((dp_count,)),
            pltpu.SemaphoreType.DMA,
        ],
        compiler_params=pltpu.CompilerParams(
            collective_id=collective, has_side_effects=True, vmem_limit_bytes=60 * 2**20
        ),
        name="small_gather",
    )(shard, routes)


class LineReduce:
    def __init__(self, sources, totals, owns, ins, lows, highs, own_sem, in_send, in_recv, line_send, line_recv):
        self.sources, self.totals = sources, totals
        self.owns, self.ins, self.lows, self.highs = owns, ins, lows, highs
        self.own_sem, self.in_send, self.in_recv = own_sem, in_send, in_recv
        self.line_send, self.line_recv = line_send, line_recv
        self.me, self.mine = place()
        self.outer, self.inner = self.me // 2, self.me % 2
        self.every = range(len(sources))

    def peers(self):
        low, high = lax.rem(self.outer + 3, 4), lax.rem(self.outer + 1, 4)
        return [
            (self.me + 1 - 2 * self.inner, self.mine),
            (low * 2 + self.inner, self.mine),
            (high * 2 + self.inner, self.mine),
        ]

    def order(self, o):
        return sorted(range(4), key=lambda plane: (-abs(plane - o), plane))

    def chunk(self, p, at):
        source = self.sources[p]
        rows = self.owns[p].shape[-2]
        here = pl.ds(pl.multiple_of(at * rows, 16), rows)
        return source.at[:, here, :] if len(source.shape) == 3 else source.at[here, :]

    def own_copy(self, p, plane):
        return pltpu.make_async_copy(
            self.chunk(p, plane * 2 + self.inner), self.owns[p].at[plane], self.own_sem.at[p, plane]
        )

    def in_copy(self, p, plane):
        return pltpu.make_async_remote_copy(
            src_ref=self.chunk(p, plane * 2 + 1 - self.inner),
            dst_ref=self.ins[p].at[plane],
            send_sem=self.in_send.at[p, plane],
            recv_sem=self.in_recv.at[p, plane],
            device_id=(self.me + 1 - 2 * self.inner, self.mine),
            device_id_type=MESH,
        )

    def line_copy(self, p, plane, upward, device_plane):
        target = self.lows[p].at[plane - 1] if upward else self.highs[p].at[plane]
        return pltpu.make_async_remote_copy(
            src_ref=self.ins[p].at[plane],
            dst_ref=target,
            send_sem=self.line_send.at[p, 0 if upward else 1, plane],
            recv_sem=self.line_recv.at[p, 0 if upward else 1, plane],
            device_id=(device_plane * 2 + self.inner, self.mine),
            device_id_type=MESH,
        )

    def start(self, o):
        for plane in self.order(o):
            for p in self.every:
                self.in_copy(p, plane).start()
        for plane in self.order(o):
            for p in self.every:
                self.own_copy(p, plane).start()

    def line_start(self, o, p, plane):
        return self.line_copy(p, plane, plane > o, o + 1 if plane > o else o - 1)

    def pass_on(self, o, k):
        plane = self.order(o)[k]
        for p in self.every:
            self.own_copy(p, plane).wait()
            self.in_copy(p, plane).wait_recv()
            terms = [self.owns[p].at[plane]]
            if o > 0 and plane >= o:
                self.line_copy(p, plane, True, o).wait_recv()
                terms.append(self.lows[p].at[plane - 1])
            if o < 3 and plane <= o:
                self.line_copy(p, plane, False, o).wait_recv()
                terms.append(self.highs[p].at[plane])
            held = self.ins[p].at[plane]
            last = plane == o
            sides = held.shape[0] if len(held.shape) == 3 else 0

            def body(at, p=p, terms=terms, held=held, last=last, sides=sides):
                here = pl.ds(pl.multiple_of(at, 16), 16)
                for side in range(max(1, sides)):
                    spot = (side, here) if sides else (here,)
                    total = held[spot].astype(jnp.float32)
                    for term in terms:
                        total = total + term[spot].astype(jnp.float32)
                    if last:
                        size = total.shape[-1]
                        self.totals[p][here, side * size : (side + 1) * size] = total
                    else:
                        held[spot] = total.astype(held.dtype)

            by_rows(held.shape[-2], body)
            if not last:
                self.line_start(o, p, plane).start()

    def finish(self, o):
        for plane in range(4):
            for p in self.every:
                self.in_copy(p, plane).wait_send()
                if plane != o:
                    self.line_start(o, p, plane).wait_send()

    def each_plane(self, body):
        for o in range(4):
            pl.when(self.outer == o)(functools.partial(body, o))

    def turns(self, ends, middles):
        def body(o):
            for k in ends if o in (0, 3) else middles:
                self.pass_on(o, k)

        self.each_plane(body)


def pieces_of(source, cut):
    columns = source.shape[-1]
    size = columns // cut
    fronts = [(side,) for side in range(source.shape[0])] if len(source.shape) == 3 else [()]
    return [
        (front, slice(c * size, c * size + size), slice(n * columns + c * size, n * columns + c * size + size))
        for n, front in enumerate(fronts)
        for c in range(cut)
    ]


def reduce_scratch(source, cut):
    rows = source.shape[-2] // 8
    size = source.shape[-1] // cut
    count = len(pieces_of(source, cut))
    shapes = []
    for planes in (4, 4, 3, 3):
        shapes += [pltpu.VMEM((planes, rows, size), jnp.bfloat16)] * count
    return shapes + [
        pltpu.SemaphoreType.DMA((count, 4)),
        pltpu.SemaphoreType.DMA((count, 4)),
        pltpu.SemaphoreType.DMA((count, 4)),
        pltpu.SemaphoreType.DMA((count, 2, 4)),
        pltpu.SemaphoreType.DMA((count, 2, 4)),
    ]


def line_reduce(source, total, scratch, cut):
    pieces = pieces_of(source, cut)
    count = len(pieces)
    buffers = [scratch[n * count : (n + 1) * count] for n in range(4)]
    sources = [source.at[front + (slice(None), columns)] for front, columns, _ in pieces]
    totals = [total.at[:, columns] for _, _, columns in pieces]
    return LineReduce(sources, totals, *buffers, *scratch[4 * count :])


def final_reduce_kernel(small_count, *refs):
    small_refs, refs = refs[:small_count], refs[small_count:]
    (
        small_out, swap, small_own, small_in, small_low, small_high, final_low, final_in, own_sem,
        swap_send, swap_recv, in_send, in_recv, line_send, line_recv, last_send, last_recv,
    ) = refs
    outer_count, inner_count = 4, 2
    me, mine = place()
    outer, inner = me // inner_count, me % inner_count
    side = mine % 2
    mate, across = mine + 1 - 2 * side, lax.rem(mine + 2, 4)
    beside = me + 1 - 2 * inner
    half_rows = small_refs[0].shape[1] // 2
    starts = [sum(ref.shape[2] for ref in small_refs[:n]) for n in range(small_count + 1)]

    def remote(source, target, device, send_at, recv_at):
        return pltpu.make_async_remote_copy(
            src_ref=source,
            dst_ref=target,
            send_sem=send_at,
            recv_sem=recv_at,
            device_id=device,
            device_id_type=MESH,
        )

    low_peer = lax.rem(outer + outer_count - 1, outer_count) * inner_count + inner
    high_peer = lax.rem(outer + 1, outer_count) * inner_count + inner
    greet([(me, mate), (me, across), (beside, mine), (low_peer, mine), (high_peer, mine)])

    mate_rows = pl.ds(pl.multiple_of((1 - side) * half_rows, 16), half_rows)
    own_rows = pl.ds(pl.multiple_of(side * half_rows, 16), half_rows)

    def swap_copy(n):
        return remote(
            small_refs[n].at[:, mate_rows, :],
            swap.at[:, :, starts[n] : starts[n + 1]],
            (me, mate),
            swap_send.at[n],
            swap_recv.at[n],
        )

    def own_copy(n):
        return pltpu.make_async_copy(
            small_refs[n].at[:, own_rows, :], small_own.at[:, :, starts[n] : starts[n + 1]], own_sem.at[n]
        )

    def inner_copy(plane):
        return remote(
            swap.at[plane * inner_count + 1 - inner],
            small_in.at[plane],
            (beside, mine),
            in_send.at[plane],
            in_recv.at[plane],
        )

    def line_copy(plane, upward, device_plane):
        way = 0 if upward else 1
        return remote(
            small_in.at[plane],
            (small_low if upward else small_high).at[plane],
            (device_plane * inner_count + inner, mine),
            line_send.at[way, plane],
            line_recv.at[way, plane],
        )

    def wide(values):
        return values.astype(jnp.float32)

    def add_own(chunk):
        def body(at):
            here = pl.ds(pl.multiple_of(at, 16), 16)
            swap[chunk, here, :] = (
                wide(swap[chunk, here, :]) + wide(small_own[chunk, here, :])
            ).astype(swap.dtype)

        by_rows(half_rows, body)

    def at_plane(o):
        order = sorted(range(outer_count), key=lambda t: (-abs(t - o), t))

        def line_start(plane):
            return line_copy(plane, plane > o, o + 1 if plane > o else o - 1)

        for n in range(small_count):
            swap_copy(n).start()
            own_copy(n).start()
        for n in range(small_count):
            swap_copy(n).wait_recv()
            own_copy(n).wait()
        for plane in order:
            add_own(plane * inner_count + 1 - inner)
            inner_copy(plane).start()
        for plane in order:
            add_own(plane * inner_count + inner)
            inner_copy(plane).wait_recv()
            terms = [swap.at[plane * inner_count + inner]]
            if o > 0 and plane >= o:
                line_copy(plane, True, o).wait_recv()
                terms.append(small_low.at[plane])
            if o < outer_count - 1 and plane <= o:
                line_copy(plane, False, o).wait_recv()
                terms.append(small_high.at[plane])
            target = final_low if plane == o else small_in.at[plane]

            def gather(at, plane=plane, terms=terms, target=target):
                here = pl.ds(pl.multiple_of(at, 16), 16)
                total = wide(small_in[plane, here, :])
                for term in terms:
                    total = total + wide(term[here, :])
                target[here, :] = total.astype(target.dtype)

            by_rows(half_rows, gather)
            if plane != o:
                line_start(plane).start()
        remote(final_low, final_in, (me, across), last_send.at[0], last_recv.at[0]).start()
        for plane in range(outer_count):
            inner_copy(plane).wait_send()
            if plane != o:
                line_start(plane).wait_send()
        for n in range(small_count):
            swap_copy(n).wait_send()

    for o in range(outer_count):
        pl.when(outer == o)(functools.partial(at_plane, o))
    remote(final_low, final_in, (me, across), last_send.at[0], last_recv.at[0]).wait()

    def total_body(at):
        here = pl.ds(pl.multiple_of(at, 16), 16)
        there = pl.ds(pl.multiple_of(side * half_rows + at, 16), 16)
        small_out[there, :] = wide(final_low[here, :]) + wide(final_in[here, :])

    by_rows(half_rows, total_body)
    mate_copy = remote(
        small_out.at[own_rows, :], small_out.at[own_rows, :], (me, mate), last_send.at[1], last_recv.at[1]
    )
    mate_copy.start()
    mate_copy.wait()


def final_reduce(smalls, collective):
    chunk_count, small_rows, _ = smalls[0].shape
    small_columns = sum(small.shape[2] for small in smalls)
    low = jnp.bfloat16
    planes = 4
    in_vmem = pl.BlockSpec(memory_space=pltpu.VMEM)
    half = small_rows // 2
    return pl.pallas_call(
        functools.partial(final_reduce_kernel, len(smalls)),
        out_shape=jax.ShapeDtypeStruct((small_rows, small_columns), jnp.float32),
        in_specs=[pl.BlockSpec(memory_space=pl.ANY)] * len(smalls),
        out_specs=in_vmem,
        scratch_shapes=[pltpu.VMEM((chunk_count, half, small_columns), low)] * 2
        + [pltpu.VMEM((planes, half, small_columns), low)] * 3
        + [pltpu.VMEM((half, small_columns), low)] * 2
        + [
            pltpu.SemaphoreType.DMA((len(smalls),)),
            pltpu.SemaphoreType.DMA((len(smalls),)),
            pltpu.SemaphoreType.DMA((len(smalls),)),
            pltpu.SemaphoreType.DMA((planes,)),
            pltpu.SemaphoreType.DMA((planes,)),
            pltpu.SemaphoreType.DMA((2, planes)),
            pltpu.SemaphoreType.DMA((2, planes)),
            pltpu.SemaphoreType.DMA((2,)),
            pltpu.SemaphoreType.DMA((2,)),
        ],
        compiler_params=pltpu.CompilerParams(
            collective_id=collective, has_side_effects=True, vmem_limit_bytes=60 * 2**20
        ),
        name="final_reduce",
    )(*smalls)


def shards(
    tokens,
    resid_logits,
    routes,
    doc_ids,
    w_qkv,
    w_out,
    gain_attn,
    gain_ffn,
    w_router,
    w_const,
    v_const,
    w_gate_up,
    w_down,
    out_grad,
):
    dp_count, owner_count = lax.axis_size("dp"), lax.axis_size("expert")
    own_links = dp_count == 8 and owner_count == 4 and w_gate_up.shape[0] == 2
    seq_count, length, width = tokens.shape
    assert seq_count == 1
    rows = seq_count * length
    choice_count = resid_logits.shape[-1]
    local_count = w_gate_up.shape[0]
    expert_count = owner_count * local_count
    hidden_count = w_down.shape[1] * dp_count
    width_qkv, width_out = w_qkv.shape[1], w_out.shape[1]
    small_parts = [w_router, w_const, v_const, gain_attn[:, None], gain_ffn[:, None]]
    small_width = sum(part.shape[1] for part in small_parts)
    pad = jnp.zeros((w_qkv.shape[0], 256 - small_width), jnp.bfloat16)
    packed = jnp.concatenate([w_qkv, w_out] + small_parts + [pad], 1)
    inputs = tokens.reshape(rows, width)
    cot = out_grad.reshape(rows, width)
    route_rows = routes.reshape(rows, 2)
    cosine, sine = rotary_lanes(length, width // HEADS)
    docs_row, docs_column = doc_ids.reshape(1, rows), doc_ids.reshape(rows, 1)
    resid = jnp.pad(
        resid_logits.reshape(rows, choice_count).astype(jnp.float32), ((0, 0), (0, 128 - choice_count))
    )
    if own_links:
        packed_full, spots, spot_rows = small_gather(packed, route_rows, expert_count, dp_count, 1)
    else:
        spots, spot_rows = routing(route_rows, expert_count)
        packed_full = lax.all_gather(packed, "dp", axis=0, tiled=True)
    gather = functools.partial(lax.all_gather, axis_name="dp", axis=0, tiled=True)
    if own_links:
        first_gate_up, second_down, packed_full = lax.optimization_barrier(
            (w_gate_up[0], w_down[1], packed_full)
        )
        first_gate_up, second_down = gather(first_gate_up), gather(second_down)
    else:
        first_gate_up = gather(w_gate_up[0])
    normed_one, queries, keys, values, attended, middle, normed_two, aux = attention_forward(
        inputs, packed_full, docs_row, docs_column, cosine, sine, route_rows, resid
    )
    send_rows, send_grads = dispatch(spot_rows, aux, normed_two, cot, owner_count, local_count)
    if own_links:
        rows_in, grads_in, first_down = expert_gather(send_rows, send_grads, w_down, dp_count, 2)
        grad_gu, grad_down, both, next_rows, next_grads, second_gate_up = experts(
            rows_in, grads_in, first_gate_up, first_gate_up, first_down, 1, dp_count,
            [send_rows, send_grads, w_gate_up], 6,
        )
        down_parts = [lax.psum_scatter(grad_down, "dp", scatter_dimension=0, tiled=True)]
        second_gu, grad_down, *parts, gu_part = experts(
            next_rows, next_grads, second_gate_up, second_gate_up, second_down, 2, dp_count,
            [both, grad_gu], 4,
        )
        parts, down_parts[0] = lax.optimization_barrier((parts, down_parts[0]))
        down_parts.append(lax.psum_scatter(grad_down, "dp", scatter_dimension=0, tiled=True))
        gu_parts = [gu_part]
    else:
        exchange = functools.partial(
            lax.all_to_all, axis_name="expert", split_axis=0, concat_axis=0, tiled=True
        )
        parts, gu_parts, down_parts = [], [], []
        for e in range(local_count):
            gate_up = first_gate_up if e == 0 else gather(w_gate_up[e])
            grad_gu, grad_down, both = experts(
                exchange(send_rows[e]), exchange(send_grads[e]), gate_up, gate_up, gather(w_down[e])
            )
            parts.append(exchange(both))
            gu_part = lax.psum_scatter(grad_gu, "dp", scatter_dimension=1, tiled=True)
            gu_parts.append(jnp.concatenate([gu_part[0], gu_part[1]], -1).astype(jnp.float32))
            down_parts.append(lax.psum_scatter(grad_down, "dp", scatter_dimension=0, tiled=True))
    down_parts = [part.astype(jnp.float32) for part in down_parts]
    output, logit_grad, grad_middle, small_grad = combine(
        parts, spots, route_rows, aux, normed_two, middle, cot, packed_full, choice_count, expert_count
    )
    backward = functools.partial(
        attention_backward, grad_middle, queries, keys, values, attended, normed_one, inputs,
        packed_full, docs_row, docs_column, cosine, sine, small_grad,
    )
    if own_links:
        token_grad, *weight_grads, gu_part = backward([second_gu], 7)
        gu_parts.append(gu_part)
        packed_part = final_reduce(
            [grad.reshape(dp_count, width // dp_count, grad.shape[1]) for grad in weight_grads], 3
        )
    else:
        token_grad, *weight_grads = backward()
        packed_part = lax.psum_scatter(
            jnp.concatenate(weight_grads, 1), "dp", scatter_dimension=0, tiled=True
        )
        packed_part = lax.psum(packed_part, "expert").astype(jnp.float32)
    part_qkv = packed_part[:, :width_qkv]
    part_out = packed_part[:, width_qkv : width_qkv + width_out]
    small_part = packed_part[:, width_qkv + width_out :]
    return (
        output.reshape(tokens.shape),
        token_grad.reshape(tokens.shape),
        logit_grad.reshape(resid_logits.shape),
        part_qkv,
        part_out,
        small_part[:, 18],
        small_part[:, 19],
        small_part[:, 0:12],
        small_part[:, 12:16],
        small_part[:, 16:18],
        jnp.stack(gu_parts),
        jnp.stack(down_parts),
    )


def solution(mesh):
    placed = (
        P(("dp", "expert"), None, None),
        P(("dp", "expert"), None, None),
        P(("dp", "expert"), None, None),
        P(("dp", "expert"), None),
        P("dp", None),
        P("dp", None),
        P("dp"),
        P("dp"),
        P("dp", None),
        P("dp", None),
        P("dp", None),
        P("expert", "dp", None),
        P("expert", "dp", None),
        P(("dp", "expert"), None, None),
    )
    return jax.shard_map(
        shards,
        mesh=mesh,
        in_specs=placed,
        out_specs=(
            P(("dp", "expert"), None, None),
            P(("dp", "expert"), None, None),
            P(("dp", "expert"), None, None),
            P("dp", None),
            P("dp", None),
            P("dp"),
            P("dp"),
            P("dp", None),
            P("dp", None),
            P("dp", None),
            P("expert", "dp", None),
            P("expert", "dp", None),
        ),
        check_vma=False,
    )
```

```python
import functools

import jax
import jax.numpy as jnp
import numpy as np
from jax import lax
from jax.experimental import pallas as pl
from jax.experimental.pallas import tpu as pltpu
from jax.sharding import PartitionSpec as P

HEADS = 12
BLOCK = 256
CAP = 256
GROUP = 256
FF_BLOCK = 512
MESH = pl.DeviceIdType.MESH
epsilon = 1e-06


def rotary_lanes(length, head_dim):
    half_dim = head_dim // 2
    frequency = (10000.0 ** (-np.arange(half_dim, dtype=np.float32) / half_dim)).astype(np.float32)
    angles = (np.arange(length, dtype=np.float32)[:, None] * frequency[None, :]).astype(np.float64)
    cosine = np.cos(angles).astype(np.float32)
    sine = np.sin(angles).astype(np.float32)
    return (
        np.concatenate([cosine] * 4, 1),
        np.concatenate([-sine, sine, -sine, sine], 1),
    )


def nt(left, right):
    return lax.dot_general(left, right, (((1,), (1,)), ((), ())), preferred_element_type=jnp.float32)


def tn(left, right):
    return lax.dot_general(left, right, (((0,), (0,)), ((), ())), preferred_element_type=jnp.float32)


def nn(left, right):
    return jnp.dot(left, right, preferred_element_type=jnp.float32)


def lane_ids(shape):
    return lax.broadcasted_iota(jnp.int32, shape, len(shape) - 1)


def turn(values, cosine, sine):
    lanes = lane_ids(values.shape)
    ahead, behind = pltpu.roll(values, 96, 1), pltpu.roll(values, 32, 1)
    return values * cosine + jnp.where(lanes % 64 < 32, ahead, behind) * sine


def key_span(i):
    return max(0, i - 2) * BLOCK, (i + 1) * BLOCK


def mask_of(docs_column, docs_row, i):
    low, high = key_span(i)
    return docs_column[low:high, :] == docs_row[:, i * BLOCK : (i + 1) * BLOCK]


def attention_forward_kernel(linked, *refs):
    (
        tokens_ref, wq_ref, wk_ref, wv_ref, wo_ref, small_ref, docs_row_ref,
        cosine_ref, sine_ref, table_ref,
    ) = refs[:10]
    (
        normed_ref, q_ref, k_ref, v_ref, attended_ref, middle_ref, normed_two_ref, aux_ref,
    ) = refs[10 + bool(linked) : 18 + bool(linked)]
    step = pl.program_id(0)
    rows = tokens_ref.shape[0]
    if linked:
        branch_ref = refs[20]
        line = LineGather(refs[10].at[0], refs[19], linked, *refs[21:])

        @pl.when(step == 0)
        def _():
            greet(line.peers())
            line.start()

        @pl.when(step == 2)
        def _():
            line.relay(1)
    else:
        branch_ref = refs[18]

    @pl.when(step == 0)
    def _():
        inputs = tokens_ref[...].astype(jnp.float32)
        gains = jnp.transpose(small_ref[:, :128].astype(jnp.float32))[18:19, :]
        scale = lax.rsqrt(jnp.mean(inputs * inputs, -1, keepdims=True) + epsilon)
        normed_ref[...] = (inputs * scale * gains).astype(jnp.bfloat16)
        branch_ref[...] = jnp.zeros_like(branch_ref)

    normed = normed_ref[...]
    cosine, sine = cosine_ref[...], sine_ref[...]
    for w_ref, out_ref, turned in ((wq_ref, q_ref, True), (wk_ref, k_ref, True), (wv_ref, v_ref, False)):
        projected = nn(normed, w_ref[...])
        for half in range(2):
            part = projected[:, half * 128 : half * 128 + 128]
            if turned:
                part = turn(part, cosine, sine)
            out_ref[:, half * 128 : half * 128 + 128] = part.astype(jnp.bfloat16)

    docs_row, docs_column = docs_row_ref[...], table_ref[:, 18:19].astype(jnp.int32)
    for i in range(rows // BLOCK):
        low, high = key_span(i)
        here = slice(i * BLOCK, (i + 1) * BLOCK)
        allowed = mask_of(docs_column, docs_row, i)
        for pair in range(2):
            lanes = slice(pair * 128, pair * 128 + 128)
            queries = q_ref[here, lanes] * jnp.asarray(0.125, jnp.bfloat16)
            keys, values = k_ref[low:high, lanes], v_ref[low:high, lanes]
            left = lane_ids(queries.shape) < 64
            outs = []
            for head in range(2):
                own = left if head == 0 else jnp.logical_not(left)
                scores = nt(keys, jnp.where(own, queries, jnp.zeros_like(queries)))
                scores = jnp.where(allowed, scores, -1e30)
                shifted = jnp.exp(scores - jnp.max(scores, 0, keepdims=True))
                probs = shifted * (1.0 / jnp.sum(shifted, 0, keepdims=True))
                outs.append(tn(probs.astype(jnp.bfloat16), values))
            attended_ref[here, lanes] = jnp.where(left, outs[0], outs[1]).astype(jnp.bfloat16)
    branch_ref[...] += nn(attended_ref[...], wo_ref[...])

    @pl.when(step == pl.num_programs(0) - 1)
    def _():
        small = small_ref[:, :128]
        gains = jnp.transpose(small.astype(jnp.float32))[19:20, :]
        middle = tokens_ref[...].astype(jnp.float32) + branch_ref[...]
        middle_ref[...] = middle
        scale = lax.rsqrt(jnp.mean(middle * middle, -1, keepdims=True) + epsilon)
        normed_two = (middle * scale * gains).astype(jnp.bfloat16)
        normed_two_ref[...] = normed_two
        logits = nn(normed_two, small) + table_ref[...]
        lanes = lane_ids(logits.shape)

        def lane(at):
            return jnp.sum(jnp.where(lanes == at, logits, 0.0), -1, keepdims=True)

        def two(first, second):
            peak = jnp.maximum(first, second)
            first, second = jnp.exp(first - peak), jnp.exp(second - peak)
            return first / (first + second), second / (first + second)

        columns = list(two(*[lane(table_ref[:, 16 + s : 17 + s].astype(jnp.int32)) for s in range(2)]))
        columns += list(two(lane(12), lane(13))) + list(two(lane(14), lane(15)))
        columns.append(scale)
        aux = jnp.zeros_like(logits)
        for at, column in enumerate(columns):
            aux = jnp.where(lanes == at, column, aux)
        aux_ref[...] = aux
        if linked:
            line.relay(2)
            line.relay(3)
            line.finish()


def attention_forward(
    tokens, packed, docs_row, cosine, sine, table, shards=None,
    dp_count=None, collective=None,
):
    rows, width = tokens.shape
    groups = width // GROUP
    low = jnp.bfloat16
    whole = lambda shape: pl.BlockSpec(shape, lambda j: (0, 0))
    column = lambda at: pl.BlockSpec((width, GROUP), lambda j: (0, at + j))
    out_column = pl.BlockSpec((rows, GROUP), lambda j: (0, j))
    full = jax.ShapeDtypeStruct((rows, width), low)
    linked = shards is not None
    anywhere = pl.BlockSpec(memory_space=pl.ANY)
    links = {"collective_id": collective, "has_side_effects": True} if linked else {}
    gathered = []
    if linked:
        gathered = [jax.ShapeDtypeStruct((dp_count * shards.shape[1], shards.shape[2]), low)]
    return pl.pallas_call(
        functools.partial(attention_forward_kernel, dp_count if linked else 0),
        grid=(groups,),
        out_shape=[full] * 5
        + [
            jax.ShapeDtypeStruct((rows, width), jnp.float32),
            full,
            jax.ShapeDtypeStruct((rows, 128), jnp.float32),
        ]
        + gathered,
        in_specs=[
            whole((rows, width)),
            column(0),
            column(groups),
            column(2 * groups),
            pl.BlockSpec((GROUP, width), lambda j: (j, 3)),
            pl.BlockSpec((width, 256), lambda j: (0, 12)),
            whole((1, rows)),
            whole((rows, 128)),
            whole((rows, 128)),
            whole((rows, 128)),
        ]
        + [anywhere] * linked,
        out_specs=[whole((rows, width))]
        + [out_column] * 4
        + [whole((rows, width)), whole((rows, width)), whole((rows, 128))]
        + [anywhere] * linked,
        scratch_shapes=[pltpu.VMEM((rows, width), jnp.float32)]
        + (gather_semaphores(dp_count) if linked else []),
        compiler_params=pltpu.CompilerParams(
            dimension_semantics=("arbitrary",), vmem_limit_bytes=56 * 2**20, **links
        ),
        cost_estimate=pl.CostEstimate(
            flops=2 * rows * width * 4 * width + 8 * rows * rows * width // 2,
            bytes_accessed=24 * rows * width,
            transcendentals=rows * rows * HEADS // 2,
        ),
        name="attention_forward",
    )(
        tokens, packed, packed, packed, packed, packed, docs_row, cosine, sine, table,
        *([shards] if linked else []),
    )


def attention_backward_kernel(count, *refs):
    (
        grad_middle_ref, q_ref, k_ref, v_ref, attended_ref, normed_ref, tokens_ref,
        wq_ref, wk_ref, wv_ref, wo_ref, small_ref, docs_row_ref, table_ref,
        cosine_ref, sine_ref, small_grad_ref,
    ) = refs[:17]
    sources, refs = refs[17 : 17 + count], refs[17 + count :]
    token_grad_ref, gq_ref, gk_ref, gv_ref, go_ref, small_out_ref = refs[:6]
    totals, refs = refs[6 : 6 + count], refs[6 + count :]
    branch_ref, back_ref, turned_ref, key_acc, value_acc, query_acc = refs[:6]
    step = pl.program_id(0)
    rows, width = tokens_ref.shape
    if count:
        line = line_reduce(sources[0], totals[0], refs[6:], 2, (1,))

        @pl.when(step == 0)
        def _():
            greet(line.peers())
            line.each_plane(line.start)

        pl.when(step == 1)(lambda: line.turns([0], []))
        pl.when(step == 2)(lambda: line.turns([1], [0]))

    @pl.when(step == 0)
    def _():
        branch_ref[...] = grad_middle_ref[...].astype(jnp.bfloat16)
        back_ref[...] = jnp.zeros_like(back_ref)

    grad_branch = branch_ref[...]
    grad_attended = nt(grad_branch, wo_ref[...]).astype(jnp.bfloat16)
    go_ref[...] = tn(attended_ref[...], grad_branch).astype(jnp.bfloat16)
    cosine, sine = cosine_ref[...], sine_ref[...]
    docs_row, docs_column = docs_row_ref[...], table_ref[:, 18:19].astype(jnp.int32)
    for pair in range(2):
        lanes = slice(pair * 128, pair * 128 + 128)
        key_acc[...] = jnp.zeros_like(key_acc)
        value_acc[...] = jnp.zeros_like(value_acc)
        for i in range(rows // BLOCK):
            low, high = key_span(i)
            here = slice(i * BLOCK, (i + 1) * BLOCK)
            allowed = mask_of(docs_column, docs_row, i)
            queries = q_ref[here, lanes] * jnp.asarray(0.125, jnp.bfloat16)
            grads = grad_attended[here, lanes]
            keys, values = k_ref[low:high, lanes], v_ref[low:high, lanes]
            left = lane_ids(queries.shape) < 64
            query_grads = []
            key_grad, value_grad = None, None
            for head in range(2):
                own = left if head == 0 else jnp.logical_not(left)
                own_queries = jnp.where(own, queries, jnp.zeros_like(queries))
                own_grads = jnp.where(own, grads, jnp.zeros_like(grads))
                scores = jnp.where(allowed, nt(keys, own_queries), -1e30)
                shifted = jnp.exp(scores - jnp.max(scores, 0, keepdims=True))
                probs = shifted * (1.0 / jnp.sum(shifted, 0, keepdims=True))
                grad_probs = nt(values, own_grads)
                inner = jnp.sum(probs * grad_probs, 0, keepdims=True)
                grad_scores = (probs * (grad_probs - inner)).astype(jnp.bfloat16)
                part_value = nn(probs.astype(jnp.bfloat16), own_grads)
                part_key = nn(grad_scores, own_queries)
                value_grad = part_value if head == 0 else value_grad + part_value
                key_grad = part_key if head == 0 else key_grad + part_key
                query_grads.append(tn(grad_scores, keys))
            value_acc[low:high, :] += value_grad
            key_acc[low:high, :] += key_grad
            query_acc[here, :] = jnp.where(left, query_grads[0], query_grads[1]) * 0.125
        turned_ref[0, :, lanes] = turn(query_acc[...], cosine, -sine).astype(jnp.bfloat16)
        turned_ref[1, :, lanes] = turn(key_acc[...], cosine, -sine).astype(jnp.bfloat16)
        turned_ref[2, :, lanes] = value_acc[...].astype(jnp.bfloat16)
    normed = normed_ref[...]
    for at, (w_ref, out_ref) in enumerate(((wq_ref, gq_ref), (wk_ref, gk_ref), (wv_ref, gv_ref))):
        turned = turned_ref[at]
        out_ref[...] = tn(normed, turned).astype(jnp.bfloat16)
        back_ref[...] += nt(turned, w_ref[...])

    @pl.when(step == pl.num_programs(0) - 1)
    def _():
        gains = jnp.transpose(small_ref[:, :128].astype(jnp.float32))[18:19, :]
        inputs = tokens_ref[...].astype(jnp.float32)
        grads = back_ref[...]
        scale = lax.rsqrt(jnp.mean(inputs * inputs, -1, keepdims=True) + epsilon)
        weighted = grads * gains
        mean = jnp.mean(weighted * inputs, -1, keepdims=True)
        grad_inputs = scale * weighted - inputs * (scale * scale * scale * mean)
        token_grad_ref[...] = (grad_inputs + grad_middle_ref[...]).astype(jnp.bfloat16)
        gain_grad = jnp.sum(grads * inputs * scale, 0, keepdims=True)
        column = jnp.transpose(jnp.broadcast_to(gain_grad, (128, width)))
        small_grad = small_grad_ref[...]
        small_grad = jnp.where(lane_ids(small_grad.shape) == 18, column, small_grad)
        small_out_ref[:, :128] = small_grad.astype(jnp.bfloat16)
        small_out_ref[:, 128:] = jnp.zeros((width, 128), jnp.bfloat16)
        if count:
            line.turns([2, 3], [1, 2, 3])
            line.each_plane(line.finish)


def attention_backward(
    grad_middle, queries, keys, values, attended, normed, tokens, packed, docs_row, table,
    cosine, sine, small_grad, sources=(), collective=None,
):
    rows, width = tokens.shape
    groups = width // GROUP
    low = jnp.bfloat16
    whole = lambda shape: pl.BlockSpec(shape, lambda j: (0, 0))
    column = lambda at: pl.BlockSpec((width, GROUP), lambda j: (0, at + j))
    by_group = pl.BlockSpec((rows, GROUP), lambda j: (0, j))
    weight = jax.ShapeDtypeStruct((width, width), low)
    linked = len(sources) > 0
    links = {"collective_id": collective, "has_side_effects": True} if linked else {}
    sums = []
    for source in sources:
        sums.append((source.shape[-2] // 8, source.shape[-1]))
    once = lambda shape: pl.BlockSpec(
        shape, lambda j: (0, 0), pipeline_mode=pl.Buffered(1)
    )
    return pl.pallas_call(
        functools.partial(attention_backward_kernel, len(sources)),
        grid=(groups,),
        out_shape=[jax.ShapeDtypeStruct((rows, width), low)]
        + [weight] * 4
        + [jax.ShapeDtypeStruct((width, 256), low)]
        + [jax.ShapeDtypeStruct(shape, jnp.float32) for shape in sums],
        in_specs=[
            once((rows, width)),
            by_group,
            by_group,
            by_group,
            by_group,
            once((rows, width)),
            once((rows, width)),
            column(0),
            column(groups),
            column(2 * groups),
            pl.BlockSpec((GROUP, width), lambda j: (j, 3)),
            pl.BlockSpec((width, 256), lambda j: (0, 12)),
            once((1, rows)),
            once((rows, 128)),
            once((rows, 128)),
            once((rows, 128)),
            once((width, 128)),
        ]
        + [pl.BlockSpec(memory_space=pl.ANY)] * len(sources),
        out_specs=[
            whole((rows, width)),
            column(0),
            column(0),
            column(0),
            pl.BlockSpec((GROUP, width), lambda j: (j, 0)),
            whole((width, 256)),
        ]
        + [whole(shape) for shape in sums],
        scratch_shapes=[
            pltpu.VMEM((rows, width), low),
            pltpu.VMEM((rows, width), jnp.float32),
            pltpu.VMEM((3, rows, GROUP), low),
            pltpu.VMEM((rows, 128), jnp.float32),
            pltpu.VMEM((rows, 128), jnp.float32),
            pltpu.VMEM((rows, 128), jnp.float32),
        ]
        + (reduce_scratch(sources[0], 2, (1,)) if linked else []),
        compiler_params=pltpu.CompilerParams(
            dimension_semantics=("arbitrary",), vmem_limit_bytes=61 * 2**20, **links
        ),
        cost_estimate=pl.CostEstimate(
            flops=4 * rows * width * 4 * width + 20 * rows * rows * width // 2,
            bytes_accessed=32 * rows * width,
            transcendentals=rows * rows * HEADS // 2,
        ),
        name="attention_backward",
    )(
        grad_middle, queries, keys, values, attended, normed, tokens, packed, packed, packed,
        packed, packed, docs_row, table, cosine, sine, small_grad, *sources,
    )


def routing_kernel(expert_count, table_ref, columns_ref, rows_ref):
    rows = table_ref.shape[0]
    lanes = lane_ids((rows, 128))
    routes = [table_ref[:, 16 + s : 17 + s].astype(jnp.int32) for s in range(2)]
    first = (lanes == routes[0]).astype(jnp.float32)
    second = (lanes == routes[1]).astype(jnp.float32)
    down = lax.broadcasted_iota(jnp.int32, (rows, rows), 0)
    lower = (down > lane_ids((rows, rows))).astype(jnp.bfloat16)
    before_first = nn(lower, first.astype(jnp.bfloat16))
    before_second = nn(lower, second.astype(jnp.bfloat16)) + jnp.sum(first, 0, keepdims=True)
    spots = []
    for picked, before, at in ((first, before_first, 0), (second, before_second, 1)):
        rank = jnp.sum(picked * before, -1, keepdims=True)
        route = routes[at]
        spot = route.astype(jnp.float32) * CAP + rank
        spots.append(jnp.where(route < expert_count, spot, jnp.full_like(spot, 2.0 * expert_count * CAP)))
    both = jnp.where(lanes == 0, spots[0], jnp.where(lanes == 1, spots[1], 0.0))
    columns_ref[...] = both.astype(jnp.int32)
    rows_ref[...] = jnp.transpose(both)[0:8, :].astype(jnp.int32)


def routing(table, expert_count):
    rows = table.shape[0]
    return pl.pallas_call(
        functools.partial(routing_kernel, expert_count),
        out_shape=[
            jax.ShapeDtypeStruct((rows, 128), jnp.int32),
            jax.ShapeDtypeStruct((8, rows), jnp.int32),
        ],
        compiler_params=pltpu.CompilerParams(vmem_limit_bytes=40 * 2**20),
        name="routing",
    )(table)


def dispatch_kernel(local_count, spots_ref, aux_ref, normed_ref, cot_ref, rows_ref, grads_ref, gates_ref):
    step = pl.program_id(0)

    @pl.when(step == 0)
    def _():
        gates_ref[...] = jnp.transpose(aux_ref[...])[0:8, :]

    owners, width = rows_ref.shape[0], rows_ref.shape[2]
    shape = (owners * CAP, normed_ref.shape[0])
    place_in = lax.broadcasted_iota(jnp.int32, shape, 0)
    first_owner = step // local_count * owners
    slots = (first_owner + place_in // CAP) * (local_count * CAP)
    slots = slots + step % local_count * CAP + place_in % CAP
    first, second = slots == spots_ref[0:1, :], slots == spots_ref[1:2, :]
    gates = jnp.sum(
        jnp.where(first, gates_ref[0:1, :], jnp.where(second, gates_ref[1:2, :], 0.0)), -1, keepdims=True
    )
    chosen = jnp.where(first | second, 1.0, 0.0).astype(jnp.bfloat16)
    rows_ref[...] = nn(chosen, normed_ref[...]).astype(jnp.bfloat16).reshape(owners, CAP, width)
    grads_ref[...] = (
        (nn(chosen, cot_ref[...]) * gates).astype(jnp.bfloat16).reshape(owners, CAP, width)
    )


def dispatch(spots, aux, normed, cot, owner_count, local_count):
    rows, width = normed.shape
    slot_count = owner_count * local_count * CAP
    whole = lambda shape: pl.BlockSpec(shape, lambda j: (0, 0))
    block = pl.BlockSpec(
        (None, 2, CAP, width), lambda j: (j % local_count, j // local_count, 0, 0)
    )
    return pl.pallas_call(
        functools.partial(dispatch_kernel, local_count),
        grid=(slot_count // CAP // 2,),
        out_shape=[jax.ShapeDtypeStruct((local_count, owner_count, CAP, width), jnp.bfloat16)] * 2,
        in_specs=[whole((8, rows)), whole((rows, 128)), whole((rows, width)), whole((rows, width))],
        out_specs=[block, block],
        scratch_shapes=[pltpu.VMEM((8, rows), jnp.float32)],
        compiler_params=pltpu.CompilerParams(
            dimension_semantics=("arbitrary",), vmem_limit_bytes=60 * 2**20
        ),
        cost_estimate=pl.CostEstimate(
            flops=4 * slot_count * rows * width,
            bytes_accessed=4 * (rows + slot_count) * width,
            transcendentals=0,
        ),
        name="dispatch",
    )(spots, aux, normed, cot)


def halves(values):
    high = values.astype(jnp.bfloat16)
    return high, (values - high.astype(jnp.float32)).astype(jnp.bfloat16)


def combine_kernel(
    expert_count, local_count, linked, *refs
):
    parts, refs = refs[:local_count], refs[local_count:]
    spots_ref, table_ref, aux_ref, normed_ref, middle_ref, cot_ref, small_ref = refs[:7]
    refs = refs[7:]
    if linked:
        source_ref, refs = refs[0], refs[1:]
    output_ref, logit_ref, grad_middle_ref, small_out_ref = refs[:4]
    refs = refs[4:]
    if linked:
        total_ref, refs = refs[0], refs[1:]
    vectors_ref, small_grad_ref = refs[:2]
    step = pl.program_id(0)
    if linked:
        line = line_reduce(source_ref, total_ref, refs[2:], 2, (0,))

        @pl.when(step == 0)
        def _():
            greet(line.peers())
            line.each_plane(line.start)

        pl.when(step == 1)(lambda: line.turns([0], []))

    @pl.when(step == 0)
    def _():
        vectors_ref[0:8, :] = jnp.transpose(small_ref[:, :128].astype(jnp.float32))[16:24, :]
        vectors_ref[8:16, :] = jnp.zeros((8, vectors_ref.shape[1]), jnp.float32)
        small_grad_ref[...] = jnp.zeros_like(small_grad_ref)

    rows, width = normed_ref.shape
    normed_low, cot_low = normed_ref[...], cot_ref[...]
    normed, cot = normed_low.astype(jnp.float32), cot_low.astype(jnp.float32)
    total = lambda values: jnp.sum(values, -1, keepdims=True)
    picks, back = [0.0, 0.0], 0.0
    for e in range(local_count):
        count = parts[e].shape[0] * CAP
        slots = lane_ids((rows, count))
        slots = slots // CAP * (local_count * CAP) + e * CAP + slots % CAP
        hits = [slots == spots_ref[:, s : s + 1] for s in range(2)]
        chosen = [jnp.where(hit, 1.0, 0.0).astype(jnp.bfloat16) for hit in hits]
        returned = parts[e][:, 0].reshape(count, width)
        both = nn(jnp.concatenate(chosen, 0), returned)
        for s in range(2):
            picks[s] = picks[s] + both[s * rows : (s + 1) * rows, :]
        back = back + nn(chosen[0] + chosen[1], parts[e][:, 1].reshape(count, width))
    inner = [total(pick * cot) for pick in picks]
    gates = [aux_ref[:, s : s + 1] for s in range(2)]
    routes = [table_ref[:, 16 + s : 17 + s].astype(jnp.int32) for s in range(2)]
    dot_copy = total(cot * normed)

    def weight_of(route):
        return sum(jnp.where(routes[s] == route, gates[s], 0.0) for s in range(2))

    copy_weight = weight_of(expert_count + 1)
    mix = gates[0] * picks[0] + gates[1] * picks[1]
    pass_weight = copy_weight
    gate_grads = [
        inner[s] + jnp.where(routes[s] == expert_count + 1, dot_copy, 0.0) for s in range(2)
    ]
    lanes = lane_ids((rows, 128))
    spread = jnp.zeros((rows, 128), jnp.float32)
    for k in range(2):
        vector = vectors_ref[k : k + 1, :]
        keep, blend = aux_ref[:, 2 + 2 * k : 3 + 2 * k], aux_ref[:, 3 + 2 * k : 4 + 2 * k]
        weight = weight_of(expert_count + 2 + k)
        dot_vector = total(cot * vector)
        pass_weight = pass_weight + weight * keep
        mix = mix + (weight * blend) * vector
        value = keep * dot_copy + blend * dot_vector
        for s in range(2):
            gate_grads[s] = gate_grads[s] + jnp.where(routes[s] == expert_count + 2 + k, value, 0.0)
        term = keep * blend * (weight * dot_copy - weight * dot_vector)
        spread = jnp.where(lanes == 12 + 2 * k, term, spread)
        spread = jnp.where(lanes == 13 + 2 * k, -term, spread)
        spread = jnp.where(lanes == 16 + k, weight * blend, spread)
    mix = mix + pass_weight * normed
    middle, scale = middle_ref[...], aux_ref[:, 6:7]
    output_ref[...] = (middle + mix).astype(jnp.bfloat16)
    mean = gates[0] * gate_grads[0] + gates[1] * gate_grads[1]
    for s in range(2):
        spread = jnp.where(lanes == routes[s], gates[s] * (gate_grads[s] - mean), spread)
    logit_ref[...] = spread[:, : logit_ref.shape[1]].astype(jnp.bfloat16)
    logits = jnp.where(lanes < 16, spread, 0.0)
    high, low = halves(logits)
    small = small_ref[:, :128]
    vector_high, vector_low = halves(spread - logits)
    small_grad_ref[...] += (
        tn(normed_low, high) + tn(normed_low, low) + tn(cot_low, vector_high) + tn(cot_low, vector_low)
    )
    grads = back + pass_weight * cot + nt(high, small) + nt(low, small)
    vectors_ref[8:9, :] += jnp.sum(grads * middle * scale, 0, keepdims=True)
    weighted = grads * vectors_ref[3:4, :]
    mean = jnp.mean(weighted * middle, -1, keepdims=True)
    grad_middle_ref[...] = cot + scale * weighted - middle * (scale * scale * scale * mean)

    @pl.when(step == pl.num_programs(0) - 1)
    def _():
        column = jnp.transpose(jnp.broadcast_to(vectors_ref[8:9, :], (128, width)))
        small_grad = small_grad_ref[...]
        small_out_ref[...] = jnp.where(lane_ids(small_grad.shape) == 19, column, small_grad)
        if linked:
            line.turns([1, 2, 3], [0, 1, 2, 3])
            line.each_plane(line.finish)


def combine(
    parts, spots, table, aux, normed, middle, cot, packed, choice_count, expert_count, source=None,
    collective=None,
):
    rows, width = normed.shape
    local_count = len(parts)
    slot_count = expert_count * CAP
    size = 512
    linked = source is not None
    links = {"collective_id": collective, "has_side_effects": True} if linked else {}
    block = lambda columns: pl.BlockSpec((size, columns), lambda j: (j, 0))
    whole = lambda shape: pl.BlockSpec(shape, lambda j: (0,) * len(shape))
    once = lambda shape: pl.BlockSpec(
        shape, lambda j: (0,) * len(shape), pipeline_mode=pl.Buffered(1)
    )
    return pl.pallas_call(
        functools.partial(combine_kernel, expert_count, local_count, linked),
        grid=(rows // size,),
        out_shape=[
            jax.ShapeDtypeStruct((rows, width), jnp.bfloat16),
            jax.ShapeDtypeStruct((rows, choice_count), jnp.bfloat16),
            jax.ShapeDtypeStruct((rows, width), jnp.float32),
            jax.ShapeDtypeStruct((width, 128), jnp.float32),
        ]
        + ([jax.ShapeDtypeStruct((width // 8, source.shape[2]), jnp.float32)] if linked else []),
        in_specs=[once(part.shape) for part in parts]
        + [
            block(128),
            block(128),
            block(128),
            block(width),
            block(width),
            block(width),
            pl.BlockSpec((width, 256), lambda j: (0, 12)),
        ]
        + [pl.BlockSpec(memory_space=pl.ANY)] * linked,
        out_specs=[block(width), block(choice_count), block(width), whole((width, 128))]
        + ([whole((width // 8, source.shape[2]))] if linked else []),
        scratch_shapes=[pltpu.VMEM((16, width), jnp.float32), pltpu.VMEM((width, 128), jnp.float32)]
        + (reduce_scratch(source, 2, (0,)) if linked else []),
        compiler_params=pltpu.CompilerParams(
            dimension_semantics=("arbitrary",), vmem_limit_bytes=58 * 2**20, **links
        ),
        cost_estimate=pl.CostEstimate(
            flops=6 * slot_count * rows * width,
            bytes_accessed=14 * rows * width + 4 * slot_count * width,
            transcendentals=0,
        ),
        name="combine",
    )(*parts, spots, table, aux, normed, middle, cot, packed, *([source] if linked else []))


def experts_kernel(mode, dp_count, *refs):
    rows_ref, grads_ref, w_gate_ref, w_up_ref, w_down_ref = refs[:5]
    if mode == 0:
        grad_gu_ref, grad_down_ref, both_ref, turned_ref, out_ref, back_ref = refs[5:]
    if mode == 1:
        next_rows, next_grads, shards_ref, grad_gu_ref, grad_down_ref, both_ref = refs[5:11]
        rows_out, grads_out, full_ref, turned_ref, out_ref, back_ref = refs[11:17]
        sems = refs[17:]
    if mode == 2:
        before_ref, source_ref, grad_gu_ref, grad_down_ref, first_in, second_in, total_ref = refs[5:12]
        turned_ref, out_ref, back_ref, both_ref = refs[12:16]
        sems = refs[16:]
    step = pl.program_id(0)
    width = rows_ref.shape[-1]
    rows = rows_ref[...].reshape(-1, width)
    grads = grads_ref[...].reshape(-1, width)
    if mode == 1:
        half = full_ref.shape[1] // 2
        lines = []
        for n in range(2):
            columns = slice(n * half, n * half + half)
            lines.append(
                LineGather(
                    shards_ref.at[1, :, columns], full_ref, dp_count, *sems[3 * n : 3 * n + 3], columns
                )
            )
        trades = [
            Trade(next_rows.at[1], rows_out, *sems[6:8]),
            Trade(next_grads.at[1], grads_out, *sems[8:10]),
        ]

        @pl.when(step == 0)
        def _():
            greet(lines[0].peers() + trades[0].peers())
            for part in lines + trades:
                part.start()

        for hop in range(1, 4):

            @pl.when(step == hop)
            def _(hop=hop):
                for part in lines:
                    part.relay(hop)

    if mode == 2:
        trades = [Trade(before_ref, first_in, *sems[:2]), Trade(both_ref, second_in, *sems[2:4])]
        line = line_reduce(source_ref, total_ref, sems[4:], 2)

        @pl.when(step == 0)
        def _():
            greet(line.peers() + trades[0].peers())
            line.each_plane(line.start)
            trades[0].start()

        pl.when(step == 2)(lambda: line.turns([0], []))

    @pl.when(step == 0)
    def _():
        turned_ref[...] = jnp.transpose(rows)
        out_ref[...] = jnp.zeros_like(out_ref)
        back_ref[...] = jnp.zeros_like(back_ref)

    w_gate, w_up, w_down = w_gate_ref[...], w_up_ref[...], w_down_ref[...]
    gate, up = nn(rows, w_gate), nn(rows, w_up)
    squashed = 1.0 / (1.0 + jnp.exp(-gate))
    silu = gate * squashed
    activated = (silu * up).astype(jnp.bfloat16)
    grad_act = nt(grads, w_down)
    grad_gate = (grad_act * up * (squashed * (1.0 + gate * (1.0 - squashed)))).astype(jnp.bfloat16)
    grad_up = (grad_act * silu).astype(jnp.bfloat16)
    out_ref[...] += nn(activated, w_down)
    grad_down_ref[...] = tn(activated, grads).astype(jnp.bfloat16)
    back_ref[...] += nt(grad_gate, w_gate) + nt(grad_up, w_up)
    grad_gu_ref[0] = nn(turned_ref[...], grad_gate).astype(jnp.bfloat16)
    grad_gu_ref[1] = nn(turned_ref[...], grad_up).astype(jnp.bfloat16)

    @pl.when(step == pl.num_programs(0) - 1)
    def _():
        shape = (both_ref.shape[0],) + both_ref.shape[2:]
        both_ref[:, 0] = out_ref[...].astype(jnp.bfloat16).reshape(shape)
        both_ref[:, 1] = back_ref[...].astype(jnp.bfloat16).reshape(shape)
        if mode == 1:
            for part in lines + trades:
                part.finish()
        if mode == 2:
            trades[1].start()
            line.turns([1, 2, 3], [0, 1, 2, 3])
            line.each_plane(line.finish)
            for trade in trades:
                trade.finish()


def experts(rows, grads, gate, up, down, mode=0, dp_count=0, extras=(), collective=None):
    owners, cap, width = rows.shape
    hidden = down.shape[0]
    count = owners * cap
    block = FF_BLOCK if count <= 1024 else FF_BLOCK // 4
    steps = hidden // block
    low = jnp.bfloat16
    pairs = pl.BlockSpec((owners, cap, width), lambda j: (0, 0, 0), pipeline_mode=pl.Buffered(1))
    anywhere = pl.BlockSpec(memory_space=pl.ANY)
    both = jax.ShapeDtypeStruct((owners, 2, cap, width), low)
    links = {"collective_id": collective, "has_side_effects": True} if mode else {}
    out_shape = [
        jax.ShapeDtypeStruct((2, width, hidden), low),
        jax.ShapeDtypeStruct((hidden, width), low),
    ]
    out_specs = [
        pl.BlockSpec((2, width, block), lambda j: (0, 0, j)),
        pl.BlockSpec((block, width), lambda j: (j, 0)),
    ]
    scratch = [
        pltpu.VMEM((width, count), low),
        pltpu.VMEM((count, width), jnp.float32),
        pltpu.VMEM((count, width), jnp.float32),
    ]
    if mode < 2:
        out_shape.append(both)
        out_specs.append(pl.BlockSpec(both.shape, lambda j: (0, 0, 0, 0)))
    if mode == 1:
        shards = extras[2]
        out_shape += [jax.ShapeDtypeStruct(rows.shape, low)] * 2
        out_shape.append(jax.ShapeDtypeStruct((dp_count * shards.shape[1], shards.shape[2]), low))
        out_specs += [anywhere] * 3
        scratch += gather_semaphores(dp_count) * 2 + trade_semaphores(owners) + trade_semaphores(owners)
    if mode == 2:
        total = (width // 8, 2 * hidden)
        out_shape += [both, both, jax.ShapeDtypeStruct(total, jnp.float32)]
        out_specs += [anywhere] * 2 + [pl.BlockSpec(total, lambda j: (0, 0))]
        scratch.append(pltpu.VMEM(both.shape, low))
        scratch += trade_semaphores(owners) + trade_semaphores(owners) + reduce_scratch(extras[1], 2)
    return pl.pallas_call(
        functools.partial(experts_kernel, mode, dp_count),
        grid=(steps,),
        out_shape=out_shape,
        in_specs=[
            pairs,
            pairs,
            pl.BlockSpec((width, block), lambda j: (0, j)),
            pl.BlockSpec((width, block), lambda j: (0, up.shape[1] // block - steps + j)),
            pl.BlockSpec((block, width), lambda j: (j, 0)),
        ]
        + [anywhere] * len(extras),
        out_specs=out_specs,
        scratch_shapes=scratch,
        compiler_params=pltpu.CompilerParams(
            dimension_semantics=("arbitrary",), vmem_limit_bytes=60 * 2**20, **links
        ),
        cost_estimate=pl.CostEstimate(
            flops=18 * count * width * hidden,
            bytes_accessed=12 * width * hidden + 8 * count * width,
            transcendentals=count * hidden,
        ),
        name="experts",
    )(rows, grads, gate, up, down, *extras)


def dp_grid(dp_count):
    outer = 4 if dp_count % 4 == 0 else 1
    return outer, dp_count // outer


def place():
    me, mine = lax.axis_index("dp"), lax.axis_index("expert")
    return me, mine


def greet(peers):
    barrier = pltpu.get_barrier_semaphore()
    for peer in peers:
        pl.semaphore_signal(barrier, inc=1, device_id=peer, device_id_type=MESH)
    pl.semaphore_wait(barrier, len(peers))


class LineGather:
    def __init__(self, shard, full, dp_count, send_sem, recv_sem, own_sem, columns=None, also=None):
        self.columns = slice(None) if columns is None else columns
        self.also = also or (lambda chunk: None)
        self.shard, self.full, self.dp_count = shard, full, dp_count
        self.send_sem, self.recv_sem, self.own_sem = send_sem, recv_sem, own_sem
        self.outer_count, self.inner_count = dp_grid(dp_count)
        self.me, self.mine = place()
        self.outer, self.inner = self.me // self.inner_count, self.me % self.inner_count
        self.inner_peers = [
            lax.rem(self.inner + k, self.inner_count) for k in range(1, self.inner_count)
        ]
        self.can_up, self.can_down = self.outer < self.outer_count - 1, self.outer > 0

    def peers(self):
        below = lax.rem(self.outer + self.outer_count - 1, self.outer_count)
        above = lax.rem(self.outer + 1, self.outer_count)
        return [(peer * self.inner_count + self.inner, self.mine) for peer in (below, above)] + [
            (self.outer * self.inner_count + peer, self.mine) for peer in self.inner_peers
        ]

    def spot(self, chunk):
        rows = self.shard.shape[0]
        return self.full.at[pl.ds(pl.multiple_of(chunk * rows, 8), rows), self.columns]

    def copy(self, source, chunk, device, way, at):
        return pltpu.make_async_remote_copy(
            src_ref=source,
            dst_ref=self.spot(chunk),
            send_sem=self.send_sem.at[way, at, chunk],
            recv_sem=self.recv_sem.at[chunk],
            device_id=(device, self.mine),
            device_id_type=MESH,
        )

    def up(self, source, chunk):
        return self.copy(source, chunk, (self.outer + 1) * self.inner_count + self.inner, 1, 0)

    def down(self, source, chunk):
        return self.copy(source, chunk, (self.outer - 1) * self.inner_count + self.inner, 2, 0)

    def across(self, source, chunk):
        return [
            self.copy(source, chunk, self.outer * self.inner_count + peer, 0, at)
            for at, peer in enumerate(self.inner_peers)
        ]

    def keep(self):
        return pltpu.make_async_copy(self.shard, self.spot(self.me), self.own_sem)

    def arrived(self, chunk):
        pltpu.make_async_copy(self.spot(chunk), self.spot(chunk), self.recv_sem.at[chunk]).wait()

    def start(self):
        for copy in self.across(self.shard, self.me):
            copy.start()
        pl.when(self.can_up)(lambda: self.up(self.shard, self.me).start())
        pl.when(self.can_down)(lambda: self.down(self.shard, self.me).start())
        self.keep().start()

    def relay(self, step):
        low, high = self.outer - step, self.outer + step

        def pass_on(source, upward):
            chunk = source * self.inner_count + self.inner
            self.arrived(chunk)
            if upward:
                pl.when(self.can_up)(lambda: self.up(self.spot(chunk), chunk).start())
            else:
                pl.when(self.can_down)(lambda: self.down(self.spot(chunk), chunk).start())
            for copy in self.across(self.spot(chunk), chunk):
                copy.start()
            self.also(chunk)

        pl.when(low >= 0)(lambda: pass_on(low, True))
        pl.when(high < self.outer_count)(lambda: pass_on(high, False))

    def finish(self):
        self.keep().wait()
        for peer in self.inner_peers:
            for k in range(self.outer_count):
                chunk = lax.rem(self.outer + k, self.outer_count) * self.inner_count + peer
                self.arrived(chunk)
                self.also(chunk)
        for plane in range(self.outer_count):
            chunk = plane * self.inner_count + self.inner
            for copy in self.across(self.spot(chunk), chunk):
                copy.wait_send()
            pl.when(self.can_up & (self.outer >= plane))(
                lambda chunk=chunk: self.up(self.spot(chunk), chunk).wait_send()
            )
            pl.when(self.can_down & (self.outer <= plane))(
                lambda chunk=chunk: self.down(self.spot(chunk), chunk).wait_send()
            )


def gather_semaphores(dp_count):
    inner_count = dp_grid(dp_count)[1]
    return [
        pltpu.SemaphoreType.DMA((3, max(1, inner_count - 1), dp_count)),
        pltpu.SemaphoreType.DMA((dp_count,)),
        pltpu.SemaphoreType.DMA,
    ]


def by_rows(count, body):
    def step(i, carry):
        body(i * 16)
        return carry

    lax.fori_loop(0, count // 16, step, 0)


class Trade:
    def __init__(self, source, target, send_sem, recv_sem):
        self.source, self.target, self.send_sem, self.recv_sem = source, target, send_sem, recv_sem
        self.me, self.mine = place()
        count = target.shape[0]
        self.partners = [lax.rem(self.mine + k, count) for k in range(1, count)]

    def peers(self):
        return [(self.me, peer) for peer in self.partners]

    def copy(self, k):
        peer = self.partners[k]
        return pltpu.make_async_remote_copy(
            src_ref=self.source.at[peer],
            dst_ref=self.target.at[self.mine],
            send_sem=self.send_sem.at[k + 1],
            recv_sem=self.recv_sem.at[self.mine],
            device_id=(self.me, peer),
            device_id_type=MESH,
        )

    def keep(self):
        return pltpu.make_async_copy(
            self.source.at[self.mine], self.target.at[self.mine], self.send_sem.at[0]
        )

    def start(self):
        for k in range(len(self.partners)):
            self.copy(k).start()
        self.keep().start()

    def finish(self):
        self.keep().wait()
        for k, peer in enumerate(self.partners):
            there = self.target.at[peer]
            pltpu.make_async_copy(there, there, self.recv_sem.at[peer]).wait()
            self.copy(k).wait_send()


def trade_semaphores(owner_count):
    return [pltpu.SemaphoreType.DMA((owner_count,)), pltpu.SemaphoreType.DMA((owner_count,))]


def expert_gather_kernel(dp_count, rows_ref, grads_ref, shards_ref, rows_out, grads_out, full_ref, *sems):
    line = LineGather(shards_ref.at[0], full_ref, dp_count, *sems[:3])
    trades = [Trade(rows_ref.at[0], rows_out, *sems[3:5]), Trade(grads_ref.at[0], grads_out, *sems[5:7])]
    greet(line.peers() + trades[0].peers())
    line.start()
    for trade in trades:
        trade.start()
    for hop in range(1, line.outer_count):
        line.relay(hop)
    line.finish()
    for trade in trades:
        trade.finish()


def expert_gather(rows, grads, shards, dp_count, collective):
    anywhere = pl.BlockSpec(memory_space=pl.ANY)
    return pl.pallas_call(
        functools.partial(expert_gather_kernel, dp_count),
        out_shape=[
            jax.ShapeDtypeStruct(rows.shape[1:], rows.dtype),
            jax.ShapeDtypeStruct(grads.shape[1:], grads.dtype),
            jax.ShapeDtypeStruct((dp_count * shards.shape[1], shards.shape[2]), shards.dtype),
        ],
        in_specs=[anywhere] * 3,
        out_specs=[anywhere] * 3,
        scratch_shapes=gather_semaphores(dp_count)
        + trade_semaphores(rows.shape[1])
        + trade_semaphores(rows.shape[1]),
        compiler_params=pltpu.CompilerParams(collective_id=collective, has_side_effects=True),
        name="expert_gather",
    )(rows, grads, shards)


def small_gather_kernel(
    dp_count, expert_count, shard_ref, routes_ref, docs_ref, resid_ref, gate_up_ref, down_ref,
    full_ref, columns_ref, rows_ref, table_ref, gate_up_out, down_out,
    send_sem, recv_sem, own_sem, pass_sem, mate_sem, all_sem, slice_sem, stack_ref,
):
    me, mine = place()
    rows, columns = shard_ref.shape
    half = columns // 2
    side = mine % 2
    mate = mine + 1 - 2 * side
    own_columns = pl.ds(pl.multiple_of(side * half, 128), half)
    mate_columns = pl.ds(pl.multiple_of((1 - side) * half, 128), half)

    def there(chunk, lanes):
        return full_ref.at[pl.ds(pl.multiple_of(chunk * rows, 8), rows), lanes]

    def pass_copy(chunk):
        return pltpu.make_async_remote_copy(
            src_ref=there(chunk, own_columns),
            dst_ref=there(chunk, own_columns),
            send_sem=pass_sem.at[chunk],
            recv_sem=mate_sem.at[chunk],
            device_id=(me, mate),
            device_id_type=MESH,
        )

    line = LineGather(
        shard_ref.at[:, own_columns], full_ref, dp_count, send_sem, recv_sem, own_sem,
        own_columns, lambda chunk: pass_copy(chunk).start(),
    )
    greet(line.peers() + [(me, mate)])
    line.start()
    other = pltpu.make_async_copy(shard_ref.at[:, mate_columns], there(me, mate_columns), all_sem)
    other.start()
    slices = [
        pltpu.make_async_copy(gate_up_ref.at[0], gate_up_out, slice_sem.at[0]),
        pltpu.make_async_copy(down_ref.at[1], down_out, slice_sem.at[1]),
    ]
    for part in slices:
        part.start()
    stack_ref[...] = jnp.zeros_like(stack_ref)
    stack_ref[0 : resid_ref.shape[0], :] = resid_ref[...].astype(jnp.float32)
    stack_ref[16:18, :] = routes_ref[...].astype(jnp.float32)
    stack_ref[18:19, :] = docs_ref[...].astype(jnp.float32)
    table_ref[...] = jnp.transpose(stack_ref[...])
    routing_kernel(expert_count, table_ref, columns_ref, rows_ref)
    for hop in range(1, line.outer_count):
        line.relay(hop)
    line.finish()
    other.wait()
    for part in slices:
        part.wait()
    for k in range(1, dp_count):
        chunk = lax.rem(me + k, dp_count)
        target = there(chunk, mate_columns)
        pltpu.make_async_copy(target, target, mate_sem.at[chunk]).wait()
        pass_copy(chunk).wait_send()


def small_gather(shard, routes, docs, resid, gate_up, down, expert_count, dp_count, collective):
    rows, columns = shard.shape
    tokens = routes.shape[1]
    anywhere, in_vmem = pl.BlockSpec(memory_space=pl.ANY), pl.BlockSpec(memory_space=pltpu.VMEM)
    return pl.pallas_call(
        functools.partial(small_gather_kernel, dp_count, expert_count),
        out_shape=[
            jax.ShapeDtypeStruct((dp_count * rows, columns), shard.dtype),
            jax.ShapeDtypeStruct((tokens, 128), jnp.int32),
            jax.ShapeDtypeStruct((8, tokens), jnp.int32),
            jax.ShapeDtypeStruct((tokens, 128), jnp.float32),
            jax.ShapeDtypeStruct(gate_up.shape[1:], gate_up.dtype),
            jax.ShapeDtypeStruct(down.shape[1:], down.dtype),
        ],
        in_specs=[anywhere] + [in_vmem] * 3 + [anywhere] * 2,
        out_specs=[anywhere] + [in_vmem] * 3 + [anywhere] * 2,
        scratch_shapes=gather_semaphores(dp_count)
        + [
            pltpu.SemaphoreType.DMA((dp_count,)),
            pltpu.SemaphoreType.DMA((dp_count,)),
            pltpu.SemaphoreType.DMA,
            pltpu.SemaphoreType.DMA((2,)),
            pltpu.VMEM((128, tokens), jnp.float32),
        ],
        compiler_params=pltpu.CompilerParams(
            collective_id=collective, has_side_effects=True, vmem_limit_bytes=60 * 2**20
        ),
        name="small_gather",
    )(shard, routes, docs, resid, gate_up, down)


class LineReduce:
    def __init__(self, sources, totals, owns, ins, lows, highs, own_sem, in_send, in_recv, line_send, line_recv):
        self.sources, self.totals = sources, totals
        self.owns, self.ins, self.lows, self.highs = owns, ins, lows, highs
        self.own_sem, self.in_send, self.in_recv = own_sem, in_send, in_recv
        self.line_send, self.line_recv = line_send, line_recv
        self.me, self.mine = place()
        self.outer, self.inner = self.me // 2, self.me % 2
        self.every = range(len(sources))

    def peers(self):
        low, high = lax.rem(self.outer + 3, 4), lax.rem(self.outer + 1, 4)
        return [
            (self.me + 1 - 2 * self.inner, self.mine),
            (low * 2 + self.inner, self.mine),
            (high * 2 + self.inner, self.mine),
        ]

    def order(self, o):
        return sorted(range(4), key=lambda plane: (-abs(plane - o), plane))

    def chunk(self, p, at):
        source = self.sources[p]
        rows = self.owns[p].shape[-2]
        here = pl.ds(pl.multiple_of(at * rows, 16), rows)
        return source.at[:, here, :] if len(source.shape) == 3 else source.at[here, :]

    def own_copy(self, p, plane):
        return pltpu.make_async_copy(
            self.chunk(p, plane * 2 + self.inner), self.owns[p].at[plane], self.own_sem.at[p, plane]
        )

    def in_copy(self, p, plane):
        return pltpu.make_async_remote_copy(
            src_ref=self.chunk(p, plane * 2 + 1 - self.inner),
            dst_ref=self.ins[p].at[plane],
            send_sem=self.in_send.at[p, plane],
            recv_sem=self.in_recv.at[p, plane],
            device_id=(self.me + 1 - 2 * self.inner, self.mine),
            device_id_type=MESH,
        )

    def line_copy(self, p, plane, upward, device_plane):
        target = self.lows[p].at[plane - 1] if upward else self.highs[p].at[plane]
        return pltpu.make_async_remote_copy(
            src_ref=self.ins[p].at[plane],
            dst_ref=target,
            send_sem=self.line_send.at[p, 0 if upward else 1, plane],
            recv_sem=self.line_recv.at[p, 0 if upward else 1, plane],
            device_id=(device_plane * 2 + self.inner, self.mine),
            device_id_type=MESH,
        )

    def start(self, o):
        for plane in self.order(o):
            for p in self.every:
                self.in_copy(p, plane).start()
        for plane in self.order(o):
            for p in self.every:
                self.own_copy(p, plane).start()

    def line_start(self, o, p, plane):
        return self.line_copy(p, plane, plane > o, o + 1 if plane > o else o - 1)

    def pass_on(self, o, k):
        plane = self.order(o)[k]
        for p in self.every:
            self.own_copy(p, plane).wait()
            self.in_copy(p, plane).wait_recv()
            terms = [self.owns[p].at[plane]]
            if o > 0 and plane >= o:
                self.line_copy(p, plane, True, o).wait_recv()
                terms.append(self.lows[p].at[plane - 1])
            if o < 3 and plane <= o:
                self.line_copy(p, plane, False, o).wait_recv()
                terms.append(self.highs[p].at[plane])
            held = self.ins[p].at[plane]
            last = plane == o
            sides = held.shape[0] if len(held.shape) == 3 else 0

            def body(at, p=p, terms=terms, held=held, last=last, sides=sides):
                here = pl.ds(pl.multiple_of(at, 16), 16)
                for side in range(max(1, sides)):
                    spot = (side, here) if sides else (here,)
                    total = held[spot].astype(jnp.float32)
                    for term in terms:
                        total = total + term[spot].astype(jnp.float32)
                    if last:
                        size = total.shape[-1]
                        self.totals[p][here, side * size : (side + 1) * size] = total
                    else:
                        held[spot] = total.astype(held.dtype)

            by_rows(held.shape[-2], body)
            if not last:
                self.line_start(o, p, plane).start()

    def finish(self, o):
        for plane in range(4):
            for p in self.every:
                self.in_copy(p, plane).wait_send()
                if plane != o:
                    self.line_start(o, p, plane).wait_send()

    def each_plane(self, body):
        for o in range(4):
            pl.when(self.outer == o)(functools.partial(body, o))

    def turns(self, ends, middles):
        def body(o):
            for k in ends if o in (0, 3) else middles:
                self.pass_on(o, k)

        self.each_plane(body)


def pieces_of(source, cut, sides=None):
    columns = source.shape[-1]
    size = columns // cut
    fronts = [()]
    if len(source.shape) == 3:
        fronts = [(side,) for side in (range(source.shape[0]) if sides is None else sides)]
    return [
        (front, slice(c * size, c * size + size), slice(n * columns + c * size, n * columns + c * size + size))
        for n, front in enumerate(fronts)
        for c in range(cut)
    ]


def reduce_scratch(source, cut, sides=None):
    rows = source.shape[-2] // 8
    size = source.shape[-1] // cut
    count = len(pieces_of(source, cut, sides))
    shapes = []
    for planes in (4, 4, 3, 3):
        shapes += [pltpu.VMEM((planes, rows, size), jnp.bfloat16)] * count
    return shapes + [
        pltpu.SemaphoreType.DMA((count, 4)),
        pltpu.SemaphoreType.DMA((count, 4)),
        pltpu.SemaphoreType.DMA((count, 4)),
        pltpu.SemaphoreType.DMA((count, 2, 4)),
        pltpu.SemaphoreType.DMA((count, 2, 4)),
    ]


def line_reduce(source, total, scratch, cut, sides=None):
    pieces = pieces_of(source, cut, sides)
    count = len(pieces)
    buffers = [scratch[n * count : (n + 1) * count] for n in range(4)]
    sources = [source.at[front + (slice(None), columns)] for front, columns, _ in pieces]
    totals = [total.at[:, columns] for _, _, columns in pieces]
    return LineReduce(sources, totals, *buffers, *scratch[4 * count :])


def final_reduce_kernel(small_count, *refs):
    small_refs, refs = refs[:small_count], refs[small_count:]
    (
        small_out, swap, small_own, small_in, small_low, small_high, final_low, final_in, own_sem,
        swap_send, swap_recv, in_send, in_recv, line_send, line_recv, last_send, last_recv,
    ) = refs
    outer_count, inner_count = 4, 2
    me, mine = place()
    outer, inner = me // inner_count, me % inner_count
    side = mine % 2
    mate, across = mine + 1 - 2 * side, lax.rem(mine + 2, 4)
    beside = me + 1 - 2 * inner
    half_rows = small_refs[0].shape[1] // 2
    starts = [sum(ref.shape[2] for ref in small_refs[:n]) for n in range(small_count + 1)]

    def remote(source, target, device, send_at, recv_at):
        return pltpu.make_async_remote_copy(
            src_ref=source,
            dst_ref=target,
            send_sem=send_at,
            recv_sem=recv_at,
            device_id=device,
            device_id_type=MESH,
        )

    low_peer = lax.rem(outer + outer_count - 1, outer_count) * inner_count + inner
    high_peer = lax.rem(outer + 1, outer_count) * inner_count + inner
    greet([(me, mate), (me, across), (beside, mine), (low_peer, mine), (high_peer, mine)])

    mate_rows = pl.ds(pl.multiple_of((1 - side) * half_rows, 16), half_rows)
    own_rows = pl.ds(pl.multiple_of(side * half_rows, 16), half_rows)

    def swap_copy(n):
        return remote(
            small_refs[n].at[:, mate_rows, :],
            swap.at[:, :, starts[n] : starts[n + 1]],
            (me, mate),
            swap_send.at[n],
            swap_recv.at[n],
        )

    def own_copy(n):
        return pltpu.make_async_copy(
            small_refs[n].at[:, own_rows, :], small_own.at[:, :, starts[n] : starts[n + 1]], own_sem.at[n]
        )

    def inner_copy(plane):
        return remote(
            swap.at[plane * inner_count + 1 - inner],
            small_in.at[plane],
            (beside, mine),
            in_send.at[plane],
            in_recv.at[plane],
        )

    def line_copy(plane, upward, device_plane):
        way = 0 if upward else 1
        return remote(
            small_in.at[plane],
            (small_low if upward else small_high).at[plane],
            (device_plane * inner_count + inner, mine),
            line_send.at[way, plane],
            line_recv.at[way, plane],
        )

    def wide(values):
        return values.astype(jnp.float32)

    def add_own(chunk):
        def body(at):
            here = pl.ds(pl.multiple_of(at, 16), 16)
            swap[chunk, here, :] = (
                wide(swap[chunk, here, :]) + wide(small_own[chunk, here, :])
            ).astype(swap.dtype)

        by_rows(half_rows, body)

    def at_plane(o):
        order = sorted(range(outer_count), key=lambda t: (-abs(t - o), t))

        def line_start(plane):
            return line_copy(plane, plane > o, o + 1 if plane > o else o - 1)

        for n in range(small_count):
            swap_copy(n).start()
            own_copy(n).start()
        for n in range(small_count):
            swap_copy(n).wait_recv()
            own_copy(n).wait()
        for plane in order:
            add_own(plane * inner_count + 1 - inner)
            inner_copy(plane).start()
        for plane in order:
            add_own(plane * inner_count + inner)
            inner_copy(plane).wait_recv()
            terms = [swap.at[plane * inner_count + inner]]
            if o > 0 and plane >= o:
                line_copy(plane, True, o).wait_recv()
                terms.append(small_low.at[plane])
            if o < outer_count - 1 and plane <= o:
                line_copy(plane, False, o).wait_recv()
                terms.append(small_high.at[plane])
            target = final_low if plane == o else small_in.at[plane]

            def gather(at, plane=plane, terms=terms, target=target):
                here = pl.ds(pl.multiple_of(at, 16), 16)
                total = wide(small_in[plane, here, :])
                for term in terms:
                    total = total + wide(term[here, :])
                target[here, :] = total.astype(target.dtype)

            by_rows(half_rows, gather)
            if plane != o:
                line_start(plane).start()
        remote(final_low, final_in, (me, across), last_send.at[0], last_recv.at[0]).start()
        for plane in range(outer_count):
            inner_copy(plane).wait_send()
            if plane != o:
                line_start(plane).wait_send()
        for n in range(small_count):
            swap_copy(n).wait_send()

    for o in range(outer_count):
        pl.when(outer == o)(functools.partial(at_plane, o))
    remote(final_low, final_in, (me, across), last_send.at[0], last_recv.at[0]).wait()

    def total_body(at):
        here = pl.ds(pl.multiple_of(at, 16), 16)
        there = pl.ds(pl.multiple_of(side * half_rows + at, 16), 16)
        small_out[there, :] = wide(final_low[here, :]) + wide(final_in[here, :])

    by_rows(half_rows, total_body)
    mate_copy = remote(
        small_out.at[own_rows, :], small_out.at[own_rows, :], (me, mate), last_send.at[1], last_recv.at[1]
    )
    mate_copy.start()
    mate_copy.wait()


def final_reduce(smalls, collective):
    chunk_count, small_rows, _ = smalls[0].shape
    small_columns = sum(small.shape[2] for small in smalls)
    low = jnp.bfloat16
    planes = 4
    in_vmem = pl.BlockSpec(memory_space=pltpu.VMEM)
    half = small_rows // 2
    return pl.pallas_call(
        functools.partial(final_reduce_kernel, len(smalls)),
        out_shape=jax.ShapeDtypeStruct((small_rows, small_columns), jnp.float32),
        in_specs=[pl.BlockSpec(memory_space=pl.ANY)] * len(smalls),
        out_specs=in_vmem,
        scratch_shapes=[pltpu.VMEM((chunk_count, half, small_columns), low)] * 2
        + [pltpu.VMEM((planes, half, small_columns), low)] * 3
        + [pltpu.VMEM((half, small_columns), low)] * 2
        + [
            pltpu.SemaphoreType.DMA((len(smalls),)),
            pltpu.SemaphoreType.DMA((len(smalls),)),
            pltpu.SemaphoreType.DMA((len(smalls),)),
            pltpu.SemaphoreType.DMA((planes,)),
            pltpu.SemaphoreType.DMA((planes,)),
            pltpu.SemaphoreType.DMA((2, planes)),
            pltpu.SemaphoreType.DMA((2, planes)),
            pltpu.SemaphoreType.DMA((2,)),
            pltpu.SemaphoreType.DMA((2,)),
        ],
        compiler_params=pltpu.CompilerParams(
            collective_id=collective, has_side_effects=True, vmem_limit_bytes=60 * 2**20
        ),
        name="final_reduce",
    )(*smalls)


def shards(
    tokens,
    resid_logits,
    routes,
    doc_ids,
    w_qkv,
    w_out,
    gain_attn,
    gain_ffn,
    w_router,
    w_const,
    v_const,
    w_gate_up,
    w_down,
    out_grad,
):
    dp_count, owner_count = lax.axis_size("dp"), lax.axis_size("expert")
    own_links = dp_count == 8 and owner_count == 4 and w_gate_up.shape[0] == 2
    seq_count, length, width = tokens.shape
    assert seq_count == 1
    rows = seq_count * length
    choice_count = resid_logits.shape[-1]
    local_count = w_gate_up.shape[0]
    expert_count = owner_count * local_count
    hidden_count = w_down.shape[1] * dp_count
    width_qkv, width_out = w_qkv.shape[1], w_out.shape[1]
    small_parts = [w_router, w_const, v_const, gain_attn[:, None], gain_ffn[:, None]]
    small_width = sum(part.shape[1] for part in small_parts)
    pad = jnp.zeros((w_qkv.shape[0], 256 - small_width), jnp.bfloat16)
    packed = jnp.concatenate([w_qkv, w_out] + small_parts + [pad], 1)
    inputs = tokens.reshape(rows, width)
    cot = out_grad.reshape(rows, width)
    route_rows = routes.reshape(rows, 2)
    cosine, sine = rotary_lanes(length, width // HEADS)
    docs_row = doc_ids.reshape(1, rows)
    resid_rows = resid_logits.reshape(rows, choice_count)
    if own_links:
        packed_full, spots, spot_rows, table, gate_up_shard, down_shard = small_gather(
            packed, route_rows.T, docs_row, resid_rows.T, w_gate_up, w_down, expert_count, dp_count, 1
        )
    else:
        columns = [
            resid_rows, jnp.zeros((rows, 16 - choice_count)), route_rows, docs_row.T, jnp.zeros((rows, 109))
        ]
        table = jnp.concatenate([column.astype(jnp.float32) for column in columns], 1)
        spots, spot_rows = routing(table, expert_count)
        packed_full = lax.all_gather(packed, "dp", axis=0, tiled=True)
    gather = functools.partial(lax.all_gather, axis_name="dp", axis=0, tiled=True)
    if own_links:
        first_gate_up, second_down = gather(gate_up_shard), gather(down_shard)
    else:
        first_gate_up = gather(w_gate_up[0])
    normed_one, queries, keys, values, attended, middle, normed_two, aux = attention_forward(
        inputs, packed_full, docs_row, cosine, sine, table
    )
    send_rows, send_grads = dispatch(spot_rows, aux, normed_two, cot, owner_count, local_count)
    if own_links:
        rows_in, grads_in, first_down = expert_gather(send_rows, send_grads, w_down, dp_count, 2)
        grad_gu, grad_down, both, next_rows, next_grads, second_gate_up = experts(
            rows_in, grads_in, first_gate_up, first_gate_up, first_down, 1, dp_count,
            [send_rows, send_grads, w_gate_up], 6,
        )
        down_parts = [lax.psum_scatter(grad_down, "dp", scatter_dimension=0, tiled=True)]
        second_gu, grad_down, *parts, gu_part = experts(
            next_rows, next_grads, second_gate_up, second_gate_up, second_down, 2, dp_count,
            [both, grad_gu], 4,
        )
        parts, down_parts[0] = lax.optimization_barrier((parts, down_parts[0]))
        down_parts.append(lax.psum_scatter(grad_down, "dp", scatter_dimension=0, tiled=True))
        gu_parts = [gu_part]
    else:
        exchange = functools.partial(
            lax.all_to_all, axis_name="expert", split_axis=0, concat_axis=0, tiled=True
        )
        parts, gu_parts, down_parts = [], [], []
        for e in range(local_count):
            gate_up = first_gate_up if e == 0 else gather(w_gate_up[e])
            grad_gu, grad_down, both = experts(
                exchange(send_rows[e]), exchange(send_grads[e]), gate_up, gate_up, gather(w_down[e])
            )
            parts.append(exchange(both))
            gu_part = lax.psum_scatter(grad_gu, "dp", scatter_dimension=1, tiled=True)
            gu_parts.append(jnp.concatenate([gu_part[0], gu_part[1]], -1).astype(jnp.float32))
            down_parts.append(lax.psum_scatter(grad_down, "dp", scatter_dimension=0, tiled=True))
    down_parts = [part.astype(jnp.float32) for part in down_parts]
    mix = functools.partial(
        combine, parts, spots, table, aux, normed_two, middle, cot, packed_full, choice_count, expert_count
    )
    if own_links:
        output, logit_grad, grad_middle, small_grad, gate_part = mix(second_gu, 5)
    else:
        output, logit_grad, grad_middle, small_grad = mix()
    backward = functools.partial(
        attention_backward, grad_middle, queries, keys, values, attended, normed_one, inputs,
        packed_full, docs_row, table, cosine, sine, small_grad,
    )
    if own_links:
        token_grad, *weight_grads, up_part = backward([second_gu], 7)
        gu_parts.append(jnp.concatenate([gate_part, up_part], 1))
        packed_part = final_reduce(
            [grad.reshape(dp_count, width // dp_count, grad.shape[1]) for grad in weight_grads], 3
        )
    else:
        token_grad, *weight_grads = backward()
        packed_part = lax.psum_scatter(
            jnp.concatenate(weight_grads, 1), "dp", scatter_dimension=0, tiled=True
        )
        packed_part = lax.psum(packed_part, "expert").astype(jnp.float32)
    part_qkv = packed_part[:, :width_qkv]
    part_out = packed_part[:, width_qkv : width_qkv + width_out]
    small_part = packed_part[:, width_qkv + width_out :]
    return (
        output.reshape(tokens.shape),
        token_grad.reshape(tokens.shape),
        logit_grad.reshape(resid_logits.shape),
        part_qkv,
        part_out,
        small_part[:, 18],
        small_part[:, 19],
        small_part[:, 0:12],
        small_part[:, 12:16],
        small_part[:, 16:18],
        jnp.stack(gu_parts),
        jnp.stack(down_parts),
    )


def solution(mesh):
    placed = (
        P(("dp", "expert"), None, None),
        P(("dp", "expert"), None, None),
        P(("dp", "expert"), None, None),
        P(("dp", "expert"), None),
        P("dp", None),
        P("dp", None),
        P("dp"),
        P("dp"),
        P("dp", None),
        P("dp", None),
        P("dp", None),
        P("expert", "dp", None),
        P("expert", "dp", None),
        P(("dp", "expert"), None, None),
    )
    return jax.shard_map(
        shards,
        mesh=mesh,
        in_specs=placed,
        out_specs=(
            P(("dp", "expert"), None, None),
            P(("dp", "expert"), None, None),
            P(("dp", "expert"), None, None),
            P("dp", None),
            P("dp", None),
            P("dp"),
            P("dp"),
            P("dp", None),
            P("dp", None),
            P("dp", None),
            P("expert", "dp", None),
            P("expert", "dp", None),
        ),
        check_vma=False,
    )
```

```python
import functools

import jax
import jax.numpy as jnp
import numpy as np
from jax import lax
from jax.experimental import pallas as pl
from jax.experimental.pallas import tpu as pltpu
from jax.sharding import PartitionSpec as P

HEADS = 12
BLOCK = 256
CAP = 256
GROUP = 256
FF_BLOCK = 512
MESH = pl.DeviceIdType.MESH
epsilon = 1e-06


def rotary_lanes(length, head_dim):
    half_dim = head_dim // 2
    frequency = (10000.0 ** (-np.arange(half_dim, dtype=np.float32) / half_dim)).astype(np.float32)
    angles = (np.arange(length, dtype=np.float32)[:, None] * frequency[None, :]).astype(np.float64)
    cosine = np.cos(angles).astype(np.float32)
    sine = np.sin(angles).astype(np.float32)
    return (
        np.concatenate([cosine] * 4, 1),
        np.concatenate([-sine, sine, -sine, sine], 1),
    )


def nt(left, right):
    return lax.dot_general(left, right, (((1,), (1,)), ((), ())), preferred_element_type=jnp.float32)


def tn(left, right):
    return lax.dot_general(left, right, (((0,), (0,)), ((), ())), preferred_element_type=jnp.float32)


def nn(left, right):
    return jnp.dot(left, right, preferred_element_type=jnp.float32)


def lane_ids(shape):
    return lax.broadcasted_iota(jnp.int32, shape, len(shape) - 1)


def turn(values, cosine, sine):
    lanes = lane_ids(values.shape)
    ahead, behind = pltpu.roll(values, 96, 1), pltpu.roll(values, 32, 1)
    return values * cosine + jnp.where(lanes % 64 < 32, ahead, behind) * sine


def key_span(i):
    return max(0, i - 2) * BLOCK, (i + 1) * BLOCK


def mask_of(docs_column, docs_row, i):
    low, high = key_span(i)
    return docs_column[low:high, :] == docs_row[:, i * BLOCK : (i + 1) * BLOCK]


def attention_forward_kernel(linked, *refs):
    (
        tokens_ref, wq_ref, wk_ref, wv_ref, wo_ref, small_ref, docs_row_ref,
        cosine_ref, sine_ref, table_ref,
    ) = refs[:10]
    (
        normed_ref, q_ref, k_ref, v_ref, attended_ref, middle_ref, normed_two_ref, aux_ref,
    ) = refs[10 + bool(linked) : 18 + bool(linked)]
    step = pl.program_id(0)
    rows = tokens_ref.shape[0]
    if linked:
        branch_ref = refs[20]
        line = LineGather(refs[10].at[0], refs[19], linked, *refs[21:])

        @pl.when(step == 0)
        def _():
            greet(line.peers())
            line.start()

        @pl.when(step == 2)
        def _():
            line.relay(1)
    else:
        branch_ref = refs[18]

    @pl.when(step == 0)
    def _():
        inputs = tokens_ref[...].astype(jnp.float32)
        gains = jnp.transpose(small_ref[:, :128].astype(jnp.float32))[18:19, :]
        scale = lax.rsqrt(jnp.mean(inputs * inputs, -1, keepdims=True) + epsilon)
        normed_ref[...] = (inputs * scale * gains).astype(jnp.bfloat16)
        branch_ref[...] = jnp.zeros_like(branch_ref)

    normed = normed_ref[...]
    cosine, sine = cosine_ref[...], sine_ref[...]
    for w_ref, out_ref, turned in ((wq_ref, q_ref, True), (wk_ref, k_ref, True), (wv_ref, v_ref, False)):
        projected = nn(normed, w_ref[...])
        for half in range(2):
            part = projected[:, half * 128 : half * 128 + 128]
            if turned:
                part = turn(part, cosine, sine)
            out_ref[:, half * 128 : half * 128 + 128] = part.astype(jnp.bfloat16)

    docs_row, docs_column = docs_row_ref[...], table_ref[:, 18:19].astype(jnp.int32)
    for i in range(rows // BLOCK):
        low, high = key_span(i)
        here = slice(i * BLOCK, (i + 1) * BLOCK)
        allowed = mask_of(docs_column, docs_row, i)
        for pair in range(2):
            lanes = slice(pair * 128, pair * 128 + 128)
            queries = q_ref[here, lanes] * jnp.asarray(0.125, jnp.bfloat16)
            keys, values = k_ref[low:high, lanes], v_ref[low:high, lanes]
            left = lane_ids(queries.shape) < 64
            outs = []
            for head in range(2):
                own = left if head == 0 else jnp.logical_not(left)
                scores = nt(keys, jnp.where(own, queries, jnp.zeros_like(queries)))
                scores = jnp.where(allowed, scores, -1e30)
                shifted = jnp.exp(scores - jnp.max(scores, 0, keepdims=True))
                probs = shifted * (1.0 / jnp.sum(shifted, 0, keepdims=True))
                outs.append(tn(probs.astype(jnp.bfloat16), values))
            attended_ref[here, lanes] = jnp.where(left, outs[0], outs[1]).astype(jnp.bfloat16)
    branch_ref[...] += nn(attended_ref[...], wo_ref[...])

    @pl.when(step == pl.num_programs(0) - 1)
    def _():
        small = small_ref[:, :128]
        gains = jnp.transpose(small.astype(jnp.float32))[19:20, :]
        middle = tokens_ref[...].astype(jnp.float32) + branch_ref[...]
        middle_ref[...] = middle
        scale = lax.rsqrt(jnp.mean(middle * middle, -1, keepdims=True) + epsilon)
        normed_two = (middle * scale * gains).astype(jnp.bfloat16)
        normed_two_ref[...] = normed_two
        logits = nn(normed_two, small) + table_ref[...]
        lanes = lane_ids(logits.shape)

        def lane(at):
            return jnp.sum(jnp.where(lanes == at, logits, 0.0), -1, keepdims=True)

        def two(first, second):
            peak = jnp.maximum(first, second)
            first, second = jnp.exp(first - peak), jnp.exp(second - peak)
            return first / (first + second), second / (first + second)

        columns = list(two(*[lane(table_ref[:, 16 + s : 17 + s].astype(jnp.int32)) for s in range(2)]))
        columns += list(two(lane(12), lane(13))) + list(two(lane(14), lane(15)))
        columns.append(scale)
        aux = jnp.zeros_like(logits)
        for at, column in enumerate(columns):
            aux = jnp.where(lanes == at, column, aux)
        aux_ref[...] = aux
        if linked:
            line.relay(2)
            line.relay(3)
            line.finish()


def attention_forward(
    tokens, packed, docs_row, cosine, sine, table, shards=None,
    dp_count=None, collective=None,
):
    rows, width = tokens.shape
    groups = width // GROUP
    low = jnp.bfloat16
    whole = lambda shape: pl.BlockSpec(shape, lambda j: (0, 0))
    column = lambda at: pl.BlockSpec((width, GROUP), lambda j: (0, at + j))
    out_column = pl.BlockSpec((rows, GROUP), lambda j: (0, j))
    full = jax.ShapeDtypeStruct((rows, width), low)
    linked = shards is not None
    anywhere = pl.BlockSpec(memory_space=pl.ANY)
    links = {"collective_id": collective, "has_side_effects": True} if linked else {}
    gathered = []
    if linked:
        gathered = [jax.ShapeDtypeStruct((dp_count * shards.shape[1], shards.shape[2]), low)]
    return pl.pallas_call(
        functools.partial(attention_forward_kernel, dp_count if linked else 0),
        grid=(groups,),
        out_shape=[full] * 5
        + [
            jax.ShapeDtypeStruct((rows, width), jnp.float32),
            full,
            jax.ShapeDtypeStruct((rows, 128), jnp.float32),
        ]
        + gathered,
        in_specs=[
            whole((rows, width)),
            column(0),
            column(groups),
            column(2 * groups),
            pl.BlockSpec((GROUP, width), lambda j: (j, 3)),
            pl.BlockSpec((width, 256), lambda j: (0, 12)),
            whole((1, rows)),
            whole((rows, 128)),
            whole((rows, 128)),
            whole((rows, 128)),
        ]
        + [anywhere] * linked,
        out_specs=[whole((rows, width))]
        + [out_column] * 4
        + [whole((rows, width)), whole((rows, width)), whole((rows, 128))]
        + [anywhere] * linked,
        scratch_shapes=[pltpu.VMEM((rows, width), jnp.float32)]
        + (gather_semaphores(dp_count) if linked else []),
        compiler_params=pltpu.CompilerParams(
            dimension_semantics=("arbitrary",), vmem_limit_bytes=56 * 2**20, **links
        ),
        cost_estimate=pl.CostEstimate(
            flops=2 * rows * width * 4 * width + 8 * rows * rows * width // 2,
            bytes_accessed=24 * rows * width,
            transcendentals=rows * rows * HEADS // 2,
        ),
        name="attention_forward",
    )(
        tokens, packed, packed, packed, packed, packed, docs_row, cosine, sine, table,
        *([shards] if linked else []),
    )


def attention_backward_kernel(count, *refs):
    (
        grad_middle_ref, q_ref, k_ref, v_ref, attended_ref, normed_ref, tokens_ref,
        wq_ref, wk_ref, wv_ref, wo_ref, small_ref, docs_row_ref, table_ref,
        cosine_ref, sine_ref, small_grad_ref,
    ) = refs[:17]
    sources, refs = refs[17 : 17 + count], refs[17 + count :]
    token_grad_ref, gq_ref, gk_ref, gv_ref, go_ref, small_out_ref = refs[:6]
    totals, refs = refs[6 : 6 + count], refs[6 + count :]
    branch_ref, back_ref, turned_ref, key_acc, value_acc, query_acc = refs[:6]
    step = pl.program_id(0)
    rows, width = tokens_ref.shape
    if count:
        line = line_reduce(sources[0], totals[0], refs[6:], 2)

        @pl.when(step == 0)
        def _():
            greet(line.peers())
            line.each_plane(line.start)

        pl.when(step == 1)(lambda: line.turns([0], []))
        pl.when(step == 2)(lambda: line.turns([1], [0]))

    @pl.when(step == 0)
    def _():
        branch_ref[...] = grad_middle_ref[...].astype(jnp.bfloat16)
        back_ref[...] = jnp.zeros_like(back_ref)

    grad_branch = branch_ref[...]
    grad_attended = nt(grad_branch, wo_ref[...]).astype(jnp.bfloat16)
    go_ref[...] = tn(attended_ref[...], grad_branch).astype(jnp.bfloat16)
    cosine, sine = cosine_ref[...], sine_ref[...]
    docs_row, docs_column = docs_row_ref[...], table_ref[:, 18:19].astype(jnp.int32)
    for pair in range(2):
        lanes = slice(pair * 128, pair * 128 + 128)
        key_acc[...] = jnp.zeros_like(key_acc)
        value_acc[...] = jnp.zeros_like(value_acc)
        for i in range(rows // BLOCK):
            low, high = key_span(i)
            here = slice(i * BLOCK, (i + 1) * BLOCK)
            allowed = mask_of(docs_column, docs_row, i)
            queries = q_ref[here, lanes] * jnp.asarray(0.125, jnp.bfloat16)
            grads = grad_attended[here, lanes]
            keys, values = k_ref[low:high, lanes], v_ref[low:high, lanes]
            left = lane_ids(queries.shape) < 64
            query_grads = []
            key_grad, value_grad = None, None
            for head in range(2):
                own = left if head == 0 else jnp.logical_not(left)
                own_queries = jnp.where(own, queries, jnp.zeros_like(queries))
                own_grads = jnp.where(own, grads, jnp.zeros_like(grads))
                scores = jnp.where(allowed, nt(keys, own_queries), -1e30)
                shifted = jnp.exp(scores - jnp.max(scores, 0, keepdims=True))
                probs = shifted * (1.0 / jnp.sum(shifted, 0, keepdims=True))
                grad_probs = nt(values, own_grads)
                inner = jnp.sum(probs * grad_probs, 0, keepdims=True)
                grad_scores = (probs * (grad_probs - inner)).astype(jnp.bfloat16)
                part_value = nn(probs.astype(jnp.bfloat16), own_grads)
                part_key = nn(grad_scores, own_queries)
                value_grad = part_value if head == 0 else value_grad + part_value
                key_grad = part_key if head == 0 else key_grad + part_key
                query_grads.append(tn(grad_scores, keys))
            value_acc[low:high, :] += value_grad
            key_acc[low:high, :] += key_grad
            query_acc[here, :] = jnp.where(left, query_grads[0], query_grads[1]) * 0.125
        turned_ref[0, :, lanes] = turn(query_acc[...], cosine, -sine).astype(jnp.bfloat16)
        turned_ref[1, :, lanes] = turn(key_acc[...], cosine, -sine).astype(jnp.bfloat16)
        turned_ref[2, :, lanes] = value_acc[...].astype(jnp.bfloat16)
    normed = normed_ref[...]
    for at, (w_ref, out_ref) in enumerate(((wq_ref, gq_ref), (wk_ref, gk_ref), (wv_ref, gv_ref))):
        turned = turned_ref[at]
        out_ref[...] = tn(normed, turned).astype(jnp.bfloat16)
        back_ref[...] += nt(turned, w_ref[...])

    @pl.when(step == pl.num_programs(0) - 1)
    def _():
        gains = jnp.transpose(small_ref[:, :128].astype(jnp.float32))[18:19, :]
        inputs = tokens_ref[...].astype(jnp.float32)
        grads = back_ref[...]
        scale = lax.rsqrt(jnp.mean(inputs * inputs, -1, keepdims=True) + epsilon)
        weighted = grads * gains
        mean = jnp.mean(weighted * inputs, -1, keepdims=True)
        grad_inputs = scale * weighted - inputs * (scale * scale * scale * mean)
        token_grad_ref[...] = (grad_inputs + grad_middle_ref[...]).astype(jnp.bfloat16)
        gain_grad = jnp.sum(grads * inputs * scale, 0, keepdims=True)
        column = jnp.transpose(jnp.broadcast_to(gain_grad, (128, width)))
        small_grad = small_grad_ref[...]
        small_grad = jnp.where(lane_ids(small_grad.shape) == 18, column, small_grad)
        small_out_ref[...] = small_grad.astype(jnp.bfloat16)
        if count:
            line.turns([2, 3], [1, 2, 3])
            line.each_plane(line.finish)


def attention_backward(
    grad_middle, queries, keys, values, attended, normed, tokens, packed, docs_row, table,
    cosine, sine, small_grad, sources=(), collective=None,
):
    rows, width = tokens.shape
    groups = width // GROUP
    low = jnp.bfloat16
    whole = lambda shape: pl.BlockSpec(shape, lambda j: (0, 0))
    column = lambda at: pl.BlockSpec((width, GROUP), lambda j: (0, at + j))
    by_group = pl.BlockSpec((rows, GROUP), lambda j: (0, j))
    weight = jax.ShapeDtypeStruct((width, width), low)
    linked = len(sources) > 0
    links = {"collective_id": collective, "has_side_effects": True} if linked else {}
    sums = []
    for source in sources:
        sums.append((source.shape[-2] // 8, source.shape[0] * source.shape[-1]))
    once = lambda shape: pl.BlockSpec(
        shape, lambda j: (0, 0), pipeline_mode=pl.Buffered(1)
    )
    return pl.pallas_call(
        functools.partial(attention_backward_kernel, len(sources)),
        grid=(groups,),
        out_shape=[jax.ShapeDtypeStruct((rows, width), low)]
        + [weight] * 4
        + [jax.ShapeDtypeStruct((width, 128), low)]
        + [jax.ShapeDtypeStruct(shape, jnp.float32) for shape in sums],
        in_specs=[
            once((rows, width)),
            by_group,
            by_group,
            by_group,
            by_group,
            once((rows, width)),
            once((rows, width)),
            column(0),
            column(groups),
            column(2 * groups),
            pl.BlockSpec((GROUP, width), lambda j: (j, 3)),
            pl.BlockSpec((width, 256), lambda j: (0, 12)),
            once((1, rows)),
            once((rows, 128)),
            once((rows, 128)),
            once((rows, 128)),
            once((width, 128)),
        ]
        + [pl.BlockSpec(memory_space=pl.ANY)] * len(sources),
        out_specs=[
            whole((rows, width)),
            column(0),
            column(0),
            column(0),
            pl.BlockSpec((GROUP, width), lambda j: (j, 0)),
            whole((width, 128)),
        ]
        + [whole(shape) for shape in sums],
        scratch_shapes=[
            pltpu.VMEM((rows, width), low),
            pltpu.VMEM((rows, width), jnp.float32),
            pltpu.VMEM((3, rows, GROUP), low),
            pltpu.VMEM((rows, 128), jnp.float32),
            pltpu.VMEM((rows, 128), jnp.float32),
            pltpu.VMEM((rows, 128), jnp.float32),
        ]
        + (reduce_scratch(sources[0], 2) if linked else []),
        compiler_params=pltpu.CompilerParams(
            dimension_semantics=("arbitrary",), vmem_limit_bytes=61 * 2**20, **links
        ),
        cost_estimate=pl.CostEstimate(
            flops=4 * rows * width * 4 * width + 20 * rows * rows * width // 2,
            bytes_accessed=32 * rows * width,
            transcendentals=rows * rows * HEADS // 2,
        ),
        name="attention_backward",
    )(
        grad_middle, queries, keys, values, attended, normed, tokens, packed, packed, packed,
        packed, packed, docs_row, table, cosine, sine, small_grad, *sources,
    )


def routing_kernel(expert_count, table_ref, columns_ref, rows_ref):
    rows = table_ref.shape[0]
    lanes = lane_ids((rows, 128))
    routes = [table_ref[:, 16 + s : 17 + s].astype(jnp.int32) for s in range(2)]
    first = (lanes == routes[0]).astype(jnp.float32)
    second = (lanes == routes[1]).astype(jnp.float32)
    down = lax.broadcasted_iota(jnp.int32, (rows, rows), 0)
    lower = (down > lane_ids((rows, rows))).astype(jnp.bfloat16)
    before_first = nn(lower, first.astype(jnp.bfloat16))
    before_second = nn(lower, second.astype(jnp.bfloat16)) + jnp.sum(first, 0, keepdims=True)
    spots = []
    for picked, before, at in ((first, before_first, 0), (second, before_second, 1)):
        rank = jnp.sum(picked * before, -1, keepdims=True)
        route = routes[at]
        spot = route.astype(jnp.float32) * CAP + rank
        spots.append(jnp.where(route < expert_count, spot, jnp.full_like(spot, 2.0 * expert_count * CAP)))
    both = jnp.where(lanes == 0, spots[0], jnp.where(lanes == 1, spots[1], 0.0))
    columns_ref[...] = both.astype(jnp.int32)
    rows_ref[...] = jnp.transpose(both)[0:8, :].astype(jnp.int32)


def routing(table, expert_count):
    rows = table.shape[0]
    return pl.pallas_call(
        functools.partial(routing_kernel, expert_count),
        out_shape=[
            jax.ShapeDtypeStruct((rows, 128), jnp.int32),
            jax.ShapeDtypeStruct((8, rows), jnp.int32),
        ],
        compiler_params=pltpu.CompilerParams(vmem_limit_bytes=40 * 2**20),
        name="routing",
    )(table)


def dispatch_kernel(local_count, spots_ref, aux_ref, normed_ref, cot_ref, rows_ref, grads_ref, gates_ref):
    step = pl.program_id(0)

    @pl.when(step == 0)
    def _():
        gates_ref[...] = jnp.transpose(aux_ref[...])[0:8, :]

    owners, width = rows_ref.shape[0], rows_ref.shape[2]
    shape = (owners * CAP, normed_ref.shape[0])
    place_in = lax.broadcasted_iota(jnp.int32, shape, 0)
    first_owner = step // local_count * owners
    slots = (first_owner + place_in // CAP) * (local_count * CAP)
    slots = slots + step % local_count * CAP + place_in % CAP
    first, second = slots == spots_ref[0:1, :], slots == spots_ref[1:2, :]
    gates = jnp.sum(
        jnp.where(first, gates_ref[0:1, :], jnp.where(second, gates_ref[1:2, :], 0.0)), -1, keepdims=True
    )
    chosen = jnp.where(first | second, 1.0, 0.0).astype(jnp.bfloat16)
    rows_ref[...] = nn(chosen, normed_ref[...]).astype(jnp.bfloat16).reshape(owners, CAP, width)
    grads_ref[...] = (
        (nn(chosen, cot_ref[...]) * gates).astype(jnp.bfloat16).reshape(owners, CAP, width)
    )


def dispatch(spots, aux, normed, cot, owner_count, local_count):
    rows, width = normed.shape
    slot_count = owner_count * local_count * CAP
    whole = lambda shape: pl.BlockSpec(shape, lambda j: (0, 0))
    block = pl.BlockSpec(
        (None, 2, CAP, width), lambda j: (j % local_count, j // local_count, 0, 0)
    )
    return pl.pallas_call(
        functools.partial(dispatch_kernel, local_count),
        grid=(slot_count // CAP // 2,),
        out_shape=[jax.ShapeDtypeStruct((local_count, owner_count, CAP, width), jnp.bfloat16)] * 2,
        in_specs=[whole((8, rows)), whole((rows, 128)), whole((rows, width)), whole((rows, width))],
        out_specs=[block, block],
        scratch_shapes=[pltpu.VMEM((8, rows), jnp.float32)],
        compiler_params=pltpu.CompilerParams(
            dimension_semantics=("arbitrary",), vmem_limit_bytes=60 * 2**20
        ),
        cost_estimate=pl.CostEstimate(
            flops=4 * slot_count * rows * width,
            bytes_accessed=4 * (rows + slot_count) * width,
            transcendentals=0,
        ),
        name="dispatch",
    )(spots, aux, normed, cot)


def halves(values):
    high = values.astype(jnp.bfloat16)
    return high, (values - high.astype(jnp.float32)).astype(jnp.bfloat16)


def combine_kernel(
    expert_count, local_count, linked, *refs
):
    parts, refs = refs[:local_count], refs[local_count:]
    spots_ref, table_ref, aux_ref, normed_ref, middle_ref, cot_ref, small_ref = refs[:7]
    refs = refs[7:]
    if linked:
        source_ref, refs = refs[0], refs[1:]
    output_ref, logit_ref, grad_middle_ref, small_out_ref = refs[:4]
    refs = refs[4:]
    if linked:
        total_ref, refs = refs[0], refs[1:]
    vectors_ref, small_grad_ref = refs[:2]
    step = pl.program_id(0)
    if linked:
        line = line_reduce(source_ref, total_ref, refs[2:], 2, (0,))

        @pl.when(step == 0)
        def _():
            greet(line.peers())
            line.each_plane(line.start)

        pl.when(step == 1)(lambda: line.turns([0], []))

    @pl.when(step == 0)
    def _():
        vectors_ref[0:8, :] = jnp.transpose(small_ref[:, :128].astype(jnp.float32))[16:24, :]
        vectors_ref[8:16, :] = jnp.zeros((8, vectors_ref.shape[1]), jnp.float32)
        small_grad_ref[...] = jnp.zeros_like(small_grad_ref)

    rows, width = normed_ref.shape
    normed_low, cot_low = normed_ref[...], cot_ref[...]
    normed, cot = normed_low.astype(jnp.float32), cot_low.astype(jnp.float32)
    total = lambda values: jnp.sum(values, -1, keepdims=True)
    picks, back = [0.0, 0.0], 0.0
    for e in range(local_count):
        count = parts[e].shape[0] * CAP
        slots = lane_ids((rows, count))
        slots = slots // CAP * (local_count * CAP) + e * CAP + slots % CAP
        hits = [slots == spots_ref[:, s : s + 1] for s in range(2)]
        chosen = [jnp.where(hit, 1.0, 0.0).astype(jnp.bfloat16) for hit in hits]
        returned = parts[e][:, 0].reshape(count, width)
        both = nn(jnp.concatenate(chosen, 0), returned)
        for s in range(2):
            picks[s] = picks[s] + both[s * rows : (s + 1) * rows, :]
        back = back + nn(chosen[0] + chosen[1], parts[e][:, 1].reshape(count, width))
    inner = [total(pick * cot) for pick in picks]
    gates = [aux_ref[:, s : s + 1] for s in range(2)]
    routes = [table_ref[:, 16 + s : 17 + s].astype(jnp.int32) for s in range(2)]
    dot_copy = total(cot * normed)

    def weight_of(route):
        return sum(jnp.where(routes[s] == route, gates[s], 0.0) for s in range(2))

    copy_weight = weight_of(expert_count + 1)
    mix = gates[0] * picks[0] + gates[1] * picks[1]
    pass_weight = copy_weight
    gate_grads = [
        inner[s] + jnp.where(routes[s] == expert_count + 1, dot_copy, 0.0) for s in range(2)
    ]
    lanes = lane_ids((rows, 128))
    spread = jnp.zeros((rows, 128), jnp.float32)
    for k in range(2):
        vector = vectors_ref[k : k + 1, :]
        keep, blend = aux_ref[:, 2 + 2 * k : 3 + 2 * k], aux_ref[:, 3 + 2 * k : 4 + 2 * k]
        weight = weight_of(expert_count + 2 + k)
        dot_vector = total(cot * vector)
        pass_weight = pass_weight + weight * keep
        mix = mix + (weight * blend) * vector
        value = keep * dot_copy + blend * dot_vector
        for s in range(2):
            gate_grads[s] = gate_grads[s] + jnp.where(routes[s] == expert_count + 2 + k, value, 0.0)
        term = keep * blend * (weight * dot_copy - weight * dot_vector)
        spread = jnp.where(lanes == 12 + 2 * k, term, spread)
        spread = jnp.where(lanes == 13 + 2 * k, -term, spread)
        spread = jnp.where(lanes == 16 + k, weight * blend, spread)
    mix = mix + pass_weight * normed
    middle, scale = middle_ref[...], aux_ref[:, 6:7]
    output_ref[...] = (middle + mix).astype(jnp.bfloat16)
    mean = gates[0] * gate_grads[0] + gates[1] * gate_grads[1]
    for s in range(2):
        spread = jnp.where(lanes == routes[s], gates[s] * (gate_grads[s] - mean), spread)
    logit_ref[...] = spread[:, : logit_ref.shape[1]].astype(jnp.bfloat16)
    logits = jnp.where(lanes < 16, spread, 0.0)
    high, low = halves(logits)
    small = small_ref[:, :128]
    vector_high, vector_low = halves(spread - logits)
    small_grad_ref[...] += (
        tn(normed_low, high) + tn(normed_low, low) + tn(cot_low, vector_high) + tn(cot_low, vector_low)
    )
    grads = back + pass_weight * cot + nt(high, small) + nt(low, small)
    vectors_ref[8:9, :] += jnp.sum(grads * middle * scale, 0, keepdims=True)
    weighted = grads * vectors_ref[3:4, :]
    mean = jnp.mean(weighted * middle, -1, keepdims=True)
    grad_middle_ref[...] = cot + scale * weighted - middle * (scale * scale * scale * mean)

    @pl.when(step == pl.num_programs(0) - 1)
    def _():
        column = jnp.transpose(jnp.broadcast_to(vectors_ref[8:9, :], (128, width)))
        small_grad = small_grad_ref[...]
        small_out_ref[...] = jnp.where(lane_ids(small_grad.shape) == 19, column, small_grad)
        if linked:
            line.turns([1, 2, 3], [0, 1, 2, 3])
            line.each_plane(line.finish)


def combine(
    parts, spots, table, aux, normed, middle, cot, packed, choice_count, expert_count, source=None,
    collective=None,
):
    rows, width = normed.shape
    local_count = len(parts)
    slot_count = expert_count * CAP
    size = 512
    linked = source is not None
    links = {"collective_id": collective, "has_side_effects": True} if linked else {}
    block = lambda columns: pl.BlockSpec((size, columns), lambda j: (j, 0))
    whole = lambda shape: pl.BlockSpec(shape, lambda j: (0,) * len(shape))
    once = lambda shape: pl.BlockSpec(
        shape, lambda j: (0,) * len(shape), pipeline_mode=pl.Buffered(1)
    )
    return pl.pallas_call(
        functools.partial(combine_kernel, expert_count, local_count, linked),
        grid=(rows // size,),
        out_shape=[
            jax.ShapeDtypeStruct((rows, width), jnp.bfloat16),
            jax.ShapeDtypeStruct((rows, choice_count), jnp.bfloat16),
            jax.ShapeDtypeStruct((rows, width), jnp.float32),
            jax.ShapeDtypeStruct((width, 128), jnp.float32),
        ]
        + ([jax.ShapeDtypeStruct((width // 8, source.shape[2]), jnp.float32)] if linked else []),
        in_specs=[once(part.shape) for part in parts]
        + [
            block(128),
            block(128),
            block(128),
            block(width),
            block(width),
            block(width),
            pl.BlockSpec((width, 256), lambda j: (0, 12)),
        ]
        + [pl.BlockSpec(memory_space=pl.ANY)] * linked,
        out_specs=[block(width), block(choice_count), block(width), whole((width, 128))]
        + ([whole((width // 8, source.shape[2]))] if linked else []),
        scratch_shapes=[pltpu.VMEM((16, width), jnp.float32), pltpu.VMEM((width, 128), jnp.float32)]
        + (reduce_scratch(source, 2, (0,)) if linked else []),
        compiler_params=pltpu.CompilerParams(
            dimension_semantics=("arbitrary",), vmem_limit_bytes=58 * 2**20, **links
        ),
        cost_estimate=pl.CostEstimate(
            flops=6 * slot_count * rows * width,
            bytes_accessed=14 * rows * width + 4 * slot_count * width,
            transcendentals=0,
        ),
        name="combine",
    )(*parts, spots, table, aux, normed, middle, cot, packed, *([source] if linked else []))


def experts_kernel(mode, dp_count, *refs):
    rows_ref, grads_ref, w_gate_ref, w_up_ref, w_down_ref = refs[:5]
    if mode == 0:
        grad_gu_ref, grad_down_ref, both_ref, turned_ref, out_ref, back_ref = refs[5:]
    if mode == 1:
        next_rows, next_grads, shards_ref, grad_gu_ref, grad_down_ref, both_ref = refs[5:11]
        rows_out, grads_out, full_ref, turned_ref, out_ref, back_ref = refs[11:17]
        sems = refs[17:]
    if mode == 2:
        before_ref, source_ref, grad_gu_ref, grad_down_ref, first_in, second_in, total_ref = refs[5:12]
        turned_ref, out_ref, back_ref, both_ref = refs[12:16]
        sems = refs[16:]
    step = pl.program_id(0)
    width = rows_ref.shape[-1]
    rows = rows_ref[...].reshape(-1, width)
    grads = grads_ref[...].reshape(-1, width)
    if mode == 1:
        half = full_ref.shape[1] // 2
        lines = []
        for n in range(2):
            columns = slice(n * half, n * half + half)
            lines.append(
                LineGather(
                    shards_ref.at[1, :, columns], full_ref, dp_count, *sems[3 * n : 3 * n + 3], columns
                )
            )
        trades = [
            Trade(next_rows.at[1], rows_out, *sems[6:8]),
            Trade(next_grads.at[1], grads_out, *sems[8:10]),
        ]

        @pl.when(step == 0)
        def _():
            greet(lines[0].peers() + trades[0].peers())
            for part in lines + trades:
                part.start()

        for hop in range(1, 4):

            @pl.when(step == hop)
            def _(hop=hop):
                for part in lines:
                    part.relay(hop)

    if mode == 2:
        trades = [Trade(before_ref, first_in, *sems[:2]), Trade(both_ref, second_in, *sems[2:4])]
        line = line_reduce(source_ref, total_ref, sems[4:], 2)

        @pl.when(step == 0)
        def _():
            greet(line.peers() + trades[0].peers())
            line.each_plane(line.start)
            trades[0].start()

        pl.when(step == 2)(lambda: line.turns([0], []))

    @pl.when(step == 0)
    def _():
        turned_ref[...] = jnp.transpose(rows)
        out_ref[...] = jnp.zeros_like(out_ref)
        back_ref[...] = jnp.zeros_like(back_ref)

    w_gate, w_up, w_down = w_gate_ref[...], w_up_ref[...], w_down_ref[...]
    gate, up = nn(rows, w_gate), nn(rows, w_up)
    squashed = 1.0 / (1.0 + jnp.exp(-gate))
    silu = gate * squashed
    activated = (silu * up).astype(jnp.bfloat16)
    grad_act = nt(grads, w_down)
    grad_gate = (grad_act * up * (squashed * (1.0 + gate * (1.0 - squashed)))).astype(jnp.bfloat16)
    grad_up = (grad_act * silu).astype(jnp.bfloat16)
    out_ref[...] += nn(activated, w_down)
    grad_down_ref[...] = tn(activated, grads).astype(jnp.bfloat16)
    back_ref[...] += nt(grad_gate, w_gate) + nt(grad_up, w_up)
    grad_gu_ref[0] = nn(turned_ref[...], grad_gate).astype(jnp.bfloat16)
    grad_gu_ref[1] = nn(turned_ref[...], grad_up).astype(jnp.bfloat16)

    @pl.when(step == pl.num_programs(0) - 1)
    def _():
        shape = (both_ref.shape[0],) + both_ref.shape[2:]
        both_ref[:, 0] = out_ref[...].astype(jnp.bfloat16).reshape(shape)
        both_ref[:, 1] = back_ref[...].astype(jnp.bfloat16).reshape(shape)
        if mode == 1:
            for part in lines + trades:
                part.finish()
        if mode == 2:
            trades[1].start()
            line.turns([1, 2, 3], [0, 1, 2, 3])
            line.each_plane(line.finish)
            for trade in trades:
                trade.finish()


def experts(rows, grads, gate, up, down, mode=0, dp_count=0, extras=(), collective=None):
    owners, cap, width = rows.shape
    hidden = down.shape[0]
    count = owners * cap
    block = FF_BLOCK if count <= 1024 else FF_BLOCK // 4
    steps = hidden // block
    low = jnp.bfloat16
    pairs = pl.BlockSpec((owners, cap, width), lambda j: (0, 0, 0), pipeline_mode=pl.Buffered(1))
    anywhere = pl.BlockSpec(memory_space=pl.ANY)
    both = jax.ShapeDtypeStruct((owners, 2, cap, width), low)
    links = {"collective_id": collective, "has_side_effects": True} if mode else {}
    out_shape = [
        jax.ShapeDtypeStruct((2, width, hidden), low),
        jax.ShapeDtypeStruct((hidden, width), low),
    ]
    out_specs = [
        pl.BlockSpec((2, width, block), lambda j: (0, 0, j)),
        pl.BlockSpec((block, width), lambda j: (j, 0)),
    ]
    scratch = [
        pltpu.VMEM((width, count), low),
        pltpu.VMEM((count, width), jnp.float32),
        pltpu.VMEM((count, width), jnp.float32),
    ]
    if mode < 2:
        out_shape.append(both)
        out_specs.append(pl.BlockSpec(both.shape, lambda j: (0, 0, 0, 0)))
    if mode == 1:
        shards = extras[2]
        out_shape += [jax.ShapeDtypeStruct(rows.shape, low)] * 2
        out_shape.append(jax.ShapeDtypeStruct((dp_count * shards.shape[1], shards.shape[2]), low))
        out_specs += [anywhere] * 3
        scratch += gather_semaphores(dp_count) * 2 + trade_semaphores(owners) + trade_semaphores(owners)
    if mode == 2:
        total = (width // 8, 2 * hidden)
        out_shape += [both, both, jax.ShapeDtypeStruct(total, jnp.float32)]
        out_specs += [anywhere] * 2 + [pl.BlockSpec(total, lambda j: (0, 0))]
        scratch.append(pltpu.VMEM(both.shape, low))
        scratch += trade_semaphores(owners) + trade_semaphores(owners) + reduce_scratch(extras[1], 2)
    return pl.pallas_call(
        functools.partial(experts_kernel, mode, dp_count),
        grid=(steps,),
        out_shape=out_shape,
        in_specs=[
            pairs,
            pairs,
            pl.BlockSpec((width, block), lambda j: (0, j)),
            pl.BlockSpec((width, block), lambda j: (0, up.shape[1] // block - steps + j)),
            pl.BlockSpec((block, width), lambda j: (j, 0)),
        ]
        + [anywhere] * len(extras),
        out_specs=out_specs,
        scratch_shapes=scratch,
        compiler_params=pltpu.CompilerParams(
            dimension_semantics=("arbitrary",), vmem_limit_bytes=60 * 2**20, **links
        ),
        cost_estimate=pl.CostEstimate(
            flops=18 * count * width * hidden,
            bytes_accessed=12 * width * hidden + 8 * count * width,
            transcendentals=count * hidden,
        ),
        name="experts",
    )(rows, grads, gate, up, down, *extras)


def dp_grid(dp_count):
    outer = 4 if dp_count % 4 == 0 else 1
    return outer, dp_count // outer


def place():
    me, mine = lax.axis_index("dp"), lax.axis_index("expert")
    return me, mine


def greet(peers):
    barrier = pltpu.get_barrier_semaphore()
    for peer in peers:
        pl.semaphore_signal(barrier, inc=1, device_id=peer, device_id_type=MESH)
    pl.semaphore_wait(barrier, len(peers))


class LineGather:
    def __init__(self, shard, full, dp_count, send_sem, recv_sem, own_sem, columns=None, also=None):
        self.columns = slice(None) if columns is None else columns
        self.also = also or (lambda chunk: None)
        self.shard, self.full, self.dp_count = shard, full, dp_count
        self.send_sem, self.recv_sem, self.own_sem = send_sem, recv_sem, own_sem
        self.outer_count, self.inner_count = dp_grid(dp_count)
        self.me, self.mine = place()
        self.outer, self.inner = self.me // self.inner_count, self.me % self.inner_count
        self.inner_peers = [
            lax.rem(self.inner + k, self.inner_count) for k in range(1, self.inner_count)
        ]
        self.can_up, self.can_down = self.outer < self.outer_count - 1, self.outer > 0

    def peers(self):
        below = lax.rem(self.outer + self.outer_count - 1, self.outer_count)
        above = lax.rem(self.outer + 1, self.outer_count)
        return [(peer * self.inner_count + self.inner, self.mine) for peer in (below, above)] + [
            (self.outer * self.inner_count + peer, self.mine) for peer in self.inner_peers
        ]

    def spot(self, chunk):
        rows = self.shard.shape[0]
        return self.full.at[pl.ds(pl.multiple_of(chunk * rows, 8), rows), self.columns]

    def copy(self, source, chunk, device, way, at):
        return pltpu.make_async_remote_copy(
            src_ref=source,
            dst_ref=self.spot(chunk),
            send_sem=self.send_sem.at[way, at, chunk],
            recv_sem=self.recv_sem.at[chunk],
            device_id=(device, self.mine),
            device_id_type=MESH,
        )

    def up(self, source, chunk):
        return self.copy(source, chunk, (self.outer + 1) * self.inner_count + self.inner, 1, 0)

    def down(self, source, chunk):
        return self.copy(source, chunk, (self.outer - 1) * self.inner_count + self.inner, 2, 0)

    def across(self, source, chunk):
        return [
            self.copy(source, chunk, self.outer * self.inner_count + peer, 0, at)
            for at, peer in enumerate(self.inner_peers)
        ]

    def keep(self):
        return pltpu.make_async_copy(self.shard, self.spot(self.me), self.own_sem)

    def arrived(self, chunk):
        pltpu.make_async_copy(self.spot(chunk), self.spot(chunk), self.recv_sem.at[chunk]).wait()

    def start(self):
        for copy in self.across(self.shard, self.me):
            copy.start()
        pl.when(self.can_up)(lambda: self.up(self.shard, self.me).start())
        pl.when(self.can_down)(lambda: self.down(self.shard, self.me).start())
        self.keep().start()

    def relay(self, step):
        low, high = self.outer - step, self.outer + step

        def pass_on(source, upward):
            chunk = source * self.inner_count + self.inner
            self.arrived(chunk)
            if upward:
                pl.when(self.can_up)(lambda: self.up(self.spot(chunk), chunk).start())
            else:
                pl.when(self.can_down)(lambda: self.down(self.spot(chunk), chunk).start())
            for copy in self.across(self.spot(chunk), chunk):
                copy.start()
            self.also(chunk)

        pl.when(low >= 0)(lambda: pass_on(low, True))
        pl.when(high < self.outer_count)(lambda: pass_on(high, False))

    def finish(self):
        self.keep().wait()
        for peer in self.inner_peers:
            for k in range(self.outer_count):
                chunk = lax.rem(self.outer + k, self.outer_count) * self.inner_count + peer
                self.arrived(chunk)
                self.also(chunk)
        for plane in range(self.outer_count):
            chunk = plane * self.inner_count + self.inner
            for copy in self.across(self.spot(chunk), chunk):
                copy.wait_send()
            pl.when(self.can_up & (self.outer >= plane))(
                lambda chunk=chunk: self.up(self.spot(chunk), chunk).wait_send()
            )
            pl.when(self.can_down & (self.outer <= plane))(
                lambda chunk=chunk: self.down(self.spot(chunk), chunk).wait_send()
            )


def gather_semaphores(dp_count):
    inner_count = dp_grid(dp_count)[1]
    return [
        pltpu.SemaphoreType.DMA((3, max(1, inner_count - 1), dp_count)),
        pltpu.SemaphoreType.DMA((dp_count,)),
        pltpu.SemaphoreType.DMA,
    ]


def by_rows(count, body):
    def step(i, carry):
        body(i * 16)
        return carry

    lax.fori_loop(0, count // 16, step, 0)


class Trade:
    def __init__(self, source, target, send_sem, recv_sem):
        self.source, self.target, self.send_sem, self.recv_sem = source, target, send_sem, recv_sem
        self.me, self.mine = place()
        count = target.shape[0]
        self.partners = [lax.rem(self.mine + k, count) for k in range(1, count)]

    def peers(self):
        return [(self.me, peer) for peer in self.partners]

    def copy(self, k):
        peer = self.partners[k]
        return pltpu.make_async_remote_copy(
            src_ref=self.source.at[peer],
            dst_ref=self.target.at[self.mine],
            send_sem=self.send_sem.at[k + 1],
            recv_sem=self.recv_sem.at[self.mine],
            device_id=(self.me, peer),
            device_id_type=MESH,
        )

    def keep(self):
        return pltpu.make_async_copy(
            self.source.at[self.mine], self.target.at[self.mine], self.send_sem.at[0]
        )

    def start(self):
        for k in range(len(self.partners)):
            self.copy(k).start()
        self.keep().start()

    def finish(self):
        self.keep().wait()
        for k, peer in enumerate(self.partners):
            there = self.target.at[peer]
            pltpu.make_async_copy(there, there, self.recv_sem.at[peer]).wait()
            self.copy(k).wait_send()


def trade_semaphores(owner_count):
    return [pltpu.SemaphoreType.DMA((owner_count,)), pltpu.SemaphoreType.DMA((owner_count,))]


def expert_gather_kernel(dp_count, rows_ref, grads_ref, shards_ref, rows_out, grads_out, full_ref, *sems):
    line = LineGather(shards_ref.at[0], full_ref, dp_count, *sems[:3])
    trades = [Trade(rows_ref.at[0], rows_out, *sems[3:5]), Trade(grads_ref.at[0], grads_out, *sems[5:7])]
    greet(line.peers() + trades[0].peers())
    line.start()
    for trade in trades:
        trade.start()
    for hop in range(1, line.outer_count):
        line.relay(hop)
    line.finish()
    for trade in trades:
        trade.finish()


def expert_gather(rows, grads, shards, dp_count, collective):
    anywhere = pl.BlockSpec(memory_space=pl.ANY)
    return pl.pallas_call(
        functools.partial(expert_gather_kernel, dp_count),
        out_shape=[
            jax.ShapeDtypeStruct(rows.shape[1:], rows.dtype),
            jax.ShapeDtypeStruct(grads.shape[1:], grads.dtype),
            jax.ShapeDtypeStruct((dp_count * shards.shape[1], shards.shape[2]), shards.dtype),
        ],
        in_specs=[anywhere] * 3,
        out_specs=[anywhere] * 3,
        scratch_shapes=gather_semaphores(dp_count)
        + trade_semaphores(rows.shape[1])
        + trade_semaphores(rows.shape[1]),
        compiler_params=pltpu.CompilerParams(collective_id=collective, has_side_effects=True),
        name="expert_gather",
    )(rows, grads, shards)


def small_gather_kernel(
    dp_count, expert_count, shard_ref, routes_ref, docs_ref, resid_ref,
    full_ref, columns_ref, rows_ref, table_ref, pass_sem, mate_sem, all_sem, stack_ref, *sems,
):
    me, mine = place()
    rows, columns = shard_ref.shape
    half = columns // 2
    side = mine % 2
    mate = mine + 1 - 2 * side
    mate_columns = pl.ds(pl.multiple_of((1 - side) * half, 128), half)
    first = half // 256 * 128
    spans = [(0, first), (first, half - first)]

    def there(chunk, lanes):
        return full_ref.at[pl.ds(pl.multiple_of(chunk * rows, 8), rows), lanes]

    def columns_at(n, of):
        start, size = spans[n]
        return pl.ds(pl.multiple_of(of * half + start, 128), size)

    def pass_copy(n, chunk):
        here = there(chunk, columns_at(n, side))
        return pltpu.make_async_remote_copy(
            src_ref=here,
            dst_ref=here,
            send_sem=pass_sem.at[n, chunk],
            recv_sem=mate_sem.at[n, chunk],
            device_id=(me, mate),
            device_id_type=MESH,
        )

    lines = []
    for n in range(2):
        lines.append(
            LineGather(
                shard_ref.at[:, columns_at(n, side)], full_ref, dp_count, *sems[3 * n : 3 * n + 3],
                columns_at(n, side), lambda chunk, n=n: pass_copy(n, chunk).start(),
            )
        )
    greet(lines[0].peers() + [(me, mate)])
    for line in lines:
        line.start()
    other = pltpu.make_async_copy(shard_ref.at[:, mate_columns], there(me, mate_columns), all_sem)
    other.start()
    stack_ref[...] = jnp.zeros_like(stack_ref)
    stack_ref[0 : resid_ref.shape[0], :] = resid_ref[...].astype(jnp.float32)
    stack_ref[16:18, :] = routes_ref[...].astype(jnp.float32)
    stack_ref[18:19, :] = docs_ref[...].astype(jnp.float32)
    table_ref[...] = jnp.transpose(stack_ref[...])
    routing_kernel(expert_count, table_ref, columns_ref, rows_ref)
    for hop in range(1, lines[0].outer_count):
        for line in lines:
            line.relay(hop)
    for line in lines:
        line.finish()
    other.wait()
    for k in range(1, dp_count):
        chunk = lax.rem(me + k, dp_count)
        for n in range(2):
            target = there(chunk, columns_at(n, 1 - side))
            pltpu.make_async_copy(target, target, mate_sem.at[n, chunk]).wait()
            pass_copy(n, chunk).wait_send()


def small_gather(shard, routes, docs, resid, expert_count, dp_count, collective):
    rows, columns = shard.shape
    tokens = routes.shape[1]
    anywhere, in_vmem = pl.BlockSpec(memory_space=pl.ANY), pl.BlockSpec(memory_space=pltpu.VMEM)
    return pl.pallas_call(
        functools.partial(small_gather_kernel, dp_count, expert_count),
        out_shape=[
            jax.ShapeDtypeStruct((dp_count * rows, columns), shard.dtype),
            jax.ShapeDtypeStruct((tokens, 128), jnp.int32),
            jax.ShapeDtypeStruct((8, tokens), jnp.int32),
            jax.ShapeDtypeStruct((tokens, 128), jnp.float32),
        ],
        in_specs=[anywhere] + [in_vmem] * 3,
        out_specs=[anywhere] + [in_vmem] * 3,
        scratch_shapes=[
            pltpu.SemaphoreType.DMA((2, dp_count)),
            pltpu.SemaphoreType.DMA((2, dp_count)),
            pltpu.SemaphoreType.DMA,
            pltpu.VMEM((128, tokens), jnp.float32),
        ]
        + gather_semaphores(dp_count) * 2,
        compiler_params=pltpu.CompilerParams(
            collective_id=collective, has_side_effects=True, vmem_limit_bytes=60 * 2**20
        ),
        name="small_gather",
    )(shard, routes, docs, resid)


class LineReduce:
    def __init__(self, sources, totals, owns, ins, lows, highs, own_sem, in_send, in_recv, line_send, line_recv):
        self.sources, self.totals = sources, totals
        self.owns, self.ins, self.lows, self.highs = owns, ins, lows, highs
        self.own_sem, self.in_send, self.in_recv = own_sem, in_send, in_recv
        self.line_send, self.line_recv = line_send, line_recv
        self.me, self.mine = place()
        self.outer, self.inner = self.me // 2, self.me % 2
        self.every = range(len(sources))

    def peers(self):
        low, high = lax.rem(self.outer + 3, 4), lax.rem(self.outer + 1, 4)
        return [
            (self.me + 1 - 2 * self.inner, self.mine),
            (low * 2 + self.inner, self.mine),
            (high * 2 + self.inner, self.mine),
        ]

    def order(self, o):
        return sorted(range(4), key=lambda plane: (-abs(plane - o), plane))

    def chunk(self, p, at):
        source = self.sources[p]
        rows = self.owns[p].shape[-2]
        here = pl.ds(pl.multiple_of(at * rows, 16), rows)
        return source.at[:, here, :] if len(source.shape) == 3 else source.at[here, :]

    def own_copy(self, p, plane):
        return pltpu.make_async_copy(
            self.chunk(p, plane * 2 + self.inner), self.owns[p].at[plane], self.own_sem.at[p, plane]
        )

    def in_copy(self, p, plane):
        return pltpu.make_async_remote_copy(
            src_ref=self.chunk(p, plane * 2 + 1 - self.inner),
            dst_ref=self.ins[p].at[plane],
            send_sem=self.in_send.at[p, plane],
            recv_sem=self.in_recv.at[p, plane],
            device_id=(self.me + 1 - 2 * self.inner, self.mine),
            device_id_type=MESH,
        )

    def line_copy(self, p, plane, upward, device_plane):
        target = self.lows[p].at[plane - 1] if upward else self.highs[p].at[plane]
        return pltpu.make_async_remote_copy(
            src_ref=self.ins[p].at[plane],
            dst_ref=target,
            send_sem=self.line_send.at[p, 0 if upward else 1, plane],
            recv_sem=self.line_recv.at[p, 0 if upward else 1, plane],
            device_id=(device_plane * 2 + self.inner, self.mine),
            device_id_type=MESH,
        )

    def start(self, o):
        for plane in self.order(o):
            for p in self.every:
                self.in_copy(p, plane).start()
        for plane in self.order(o):
            for p in self.every:
                self.own_copy(p, plane).start()

    def line_start(self, o, p, plane):
        return self.line_copy(p, plane, plane > o, o + 1 if plane > o else o - 1)

    def pass_on(self, o, k):
        plane = self.order(o)[k]
        for p in self.every:
            self.own_copy(p, plane).wait()
            self.in_copy(p, plane).wait_recv()
            terms = [self.owns[p].at[plane]]
            if o > 0 and plane >= o:
                self.line_copy(p, plane, True, o).wait_recv()
                terms.append(self.lows[p].at[plane - 1])
            if o < 3 and plane <= o:
                self.line_copy(p, plane, False, o).wait_recv()
                terms.append(self.highs[p].at[plane])
            held = self.ins[p].at[plane]
            last = plane == o
            sides = held.shape[0] if len(held.shape) == 3 else 0

            def body(at, p=p, terms=terms, held=held, last=last, sides=sides):
                here = pl.ds(pl.multiple_of(at, 16), 16)
                for side in range(max(1, sides)):
                    spot = (side, here) if sides else (here,)
                    total = held[spot].astype(jnp.float32)
                    for term in terms:
                        total = total + term[spot].astype(jnp.float32)
                    if last:
                        size = total.shape[-1]
                        self.totals[p][here, side * size : (side + 1) * size] = total
                    else:
                        held[spot] = total.astype(held.dtype)

            by_rows(held.shape[-2], body)
            if not last:
                self.line_start(o, p, plane).start()

    def finish(self, o):
        for plane in range(4):
            for p in self.every:
                self.in_copy(p, plane).wait_send()
                if plane != o:
                    self.line_start(o, p, plane).wait_send()

    def each_plane(self, body):
        for o in range(4):
            pl.when(self.outer == o)(functools.partial(body, o))

    def turns(self, ends, middles):
        def body(o):
            for k in ends if o in (0, 3) else middles:
                self.pass_on(o, k)

        self.each_plane(body)


def pieces_of(source, cut, sides=None):
    columns = source.shape[-1]
    size = columns // cut
    fronts = [()]
    if len(source.shape) == 3:
        fronts = [(side,) for side in (range(source.shape[0]) if sides is None else sides)]
    return [
        (front, slice(c * size, c * size + size), slice(n * columns + c * size, n * columns + c * size + size))
        for n, front in enumerate(fronts)
        for c in range(cut)
    ]


def reduce_scratch(source, cut, sides=None):
    rows = source.shape[-2] // 8
    size = source.shape[-1] // cut
    count = len(pieces_of(source, cut, sides))
    shapes = []
    for planes in (4, 4, 3, 3):
        shapes += [pltpu.VMEM((planes, rows, size), jnp.bfloat16)] * count
    return shapes + [
        pltpu.SemaphoreType.DMA((count, 4)),
        pltpu.SemaphoreType.DMA((count, 4)),
        pltpu.SemaphoreType.DMA((count, 4)),
        pltpu.SemaphoreType.DMA((count, 2, 4)),
        pltpu.SemaphoreType.DMA((count, 2, 4)),
    ]


def line_reduce(source, total, scratch, cut, sides=None):
    pieces = pieces_of(source, cut, sides)
    count = len(pieces)
    buffers = [scratch[n * count : (n + 1) * count] for n in range(4)]
    sources = [source.at[front + (slice(None), columns)] for front, columns, _ in pieces]
    totals = [total.at[:, columns] for _, _, columns in pieces]
    return LineReduce(sources, totals, *buffers, *scratch[4 * count :])


def final_reduce_kernel(small_count, *refs):
    small_refs, refs = refs[:small_count], refs[small_count:]
    (
        small_out, swap, small_own, small_in, small_low, small_high, final_low, final_in, own_sem,
        swap_send, swap_recv, in_send, in_recv, line_send, line_recv, last_send, last_recv,
    ) = refs
    outer_count, inner_count = 4, 2
    me, mine = place()
    outer, inner = me // inner_count, me % inner_count
    side = mine % 2
    mate, across = mine + 1 - 2 * side, lax.rem(mine + 2, 4)
    beside = me + 1 - 2 * inner
    half_rows = small_refs[0].shape[1] // 2
    starts = [sum(ref.shape[2] for ref in small_refs[:n]) for n in range(small_count + 1)]

    def remote(source, target, device, send_at, recv_at):
        return pltpu.make_async_remote_copy(
            src_ref=source,
            dst_ref=target,
            send_sem=send_at,
            recv_sem=recv_at,
            device_id=device,
            device_id_type=MESH,
        )

    low_peer = lax.rem(outer + outer_count - 1, outer_count) * inner_count + inner
    high_peer = lax.rem(outer + 1, outer_count) * inner_count + inner
    greet([(me, mate), (me, across), (beside, mine), (low_peer, mine), (high_peer, mine)])

    mate_rows = pl.ds(pl.multiple_of((1 - side) * half_rows, 16), half_rows)
    own_rows = pl.ds(pl.multiple_of(side * half_rows, 16), half_rows)

    middle = starts[-1] // 256 * 128
    spans = [slice(0, middle), slice(middle, starts[-1])]

    def swap_copy(n):
        return remote(
            small_refs[n].at[:, mate_rows, :],
            swap.at[:, :, starts[n] : starts[n + 1]],
            (me, mate),
            swap_send.at[n],
            swap_recv.at[n],
        )

    def own_copy(n):
        return pltpu.make_async_copy(
            small_refs[n].at[:, own_rows, :], small_own.at[:, :, starts[n] : starts[n + 1]], own_sem.at[n]
        )

    def inner_copy(p, plane):
        return remote(
            swap.at[plane * inner_count + 1 - inner, :, spans[p]],
            small_in.at[plane, :, spans[p]],
            (beside, mine),
            in_send.at[p, plane],
            in_recv.at[p, plane],
        )

    def line_copy(p, plane, upward, device_plane):
        way = 0 if upward else 1
        return remote(
            small_in.at[plane, :, spans[p]],
            (small_low if upward else small_high).at[plane, :, spans[p]],
            (device_plane * inner_count + inner, mine),
            line_send.at[p, way, plane],
            line_recv.at[p, way, plane],
        )

    def last_copy(p):
        return remote(
            final_low.at[:, spans[p]], final_in.at[:, spans[p]], (me, across), last_send.at[p], last_recv.at[p]
        )

    def wide(values):
        return values.astype(jnp.float32)

    def add_own(chunk, lanes):
        def body(at):
            here = pl.ds(pl.multiple_of(at, 16), 16)
            swap[chunk, here, lanes] = (
                wide(swap[chunk, here, lanes]) + wide(small_own[chunk, here, lanes])
            ).astype(swap.dtype)

        by_rows(half_rows, body)

    def at_plane(o):
        order = sorted(range(outer_count), key=lambda t: (-abs(t - o), t))

        def line_start(p, plane):
            return line_copy(p, plane, plane > o, o + 1 if plane > o else o - 1)

        for n in range(small_count):
            swap_copy(n).start()
            own_copy(n).start()
        for n in range(small_count):
            swap_copy(n).wait_recv()
            own_copy(n).wait()
        for plane in order:
            for p in range(2):
                add_own(plane * inner_count + 1 - inner, spans[p])
                inner_copy(p, plane).start()
        for plane in order:
            for p in range(2):
                add_own(plane * inner_count + inner, spans[p])
                inner_copy(p, plane).wait_recv()
                terms = [swap.at[plane * inner_count + inner]]
                if o > 0 and plane >= o:
                    line_copy(p, plane, True, o).wait_recv()
                    terms.append(small_low.at[plane])
                if o < outer_count - 1 and plane <= o:
                    line_copy(p, plane, False, o).wait_recv()
                    terms.append(small_high.at[plane])
                target = final_low if plane == o else small_in.at[plane]

                def gather(at, plane=plane, terms=terms, target=target, lanes=spans[p]):
                    here = pl.ds(pl.multiple_of(at, 16), 16)
                    total = wide(small_in[plane, here, lanes])
                    for term in terms:
                        total = total + wide(term[here, lanes])
                    target[here, lanes] = total.astype(target.dtype)

                by_rows(half_rows, gather)
                if plane != o:
                    line_start(p, plane).start()
                else:
                    last_copy(p).start()
        for plane in range(outer_count):
            for p in range(2):
                inner_copy(p, plane).wait_send()
                if plane != o:
                    line_start(p, plane).wait_send()
        for n in range(small_count):
            swap_copy(n).wait_send()

    for o in range(outer_count):
        pl.when(outer == o)(functools.partial(at_plane, o))
    for p in range(2):
        last_copy(p).wait()

    def total_body(at):
        here = pl.ds(pl.multiple_of(at, 16), 16)
        there = pl.ds(pl.multiple_of(side * half_rows + at, 16), 16)
        small_out[there, :] = wide(final_low[here, :]) + wide(final_in[here, :])

    by_rows(half_rows, total_body)
    mate_copy = remote(
        small_out.at[own_rows, :], small_out.at[own_rows, :], (me, mate), last_send.at[2], last_recv.at[2]
    )
    mate_copy.start()
    mate_copy.wait()


def final_reduce(smalls, collective):
    chunk_count, small_rows, _ = smalls[0].shape
    small_columns = sum(small.shape[2] for small in smalls)
    low = jnp.bfloat16
    planes = 4
    in_vmem = pl.BlockSpec(memory_space=pltpu.VMEM)
    half = small_rows // 2
    return pl.pallas_call(
        functools.partial(final_reduce_kernel, len(smalls)),
        out_shape=jax.ShapeDtypeStruct((small_rows, small_columns), jnp.float32),
        in_specs=[pl.BlockSpec(memory_space=pl.ANY)] * len(smalls),
        out_specs=in_vmem,
        scratch_shapes=[pltpu.VMEM((chunk_count, half, small_columns), low)] * 2
        + [pltpu.VMEM((planes, half, small_columns), low)] * 3
        + [pltpu.VMEM((half, small_columns), low)] * 2
        + [
            pltpu.SemaphoreType.DMA((len(smalls),)),
            pltpu.SemaphoreType.DMA((len(smalls),)),
            pltpu.SemaphoreType.DMA((len(smalls),)),
            pltpu.SemaphoreType.DMA((2, planes)),
            pltpu.SemaphoreType.DMA((2, planes)),
            pltpu.SemaphoreType.DMA((2, 2, planes)),
            pltpu.SemaphoreType.DMA((2, 2, planes)),
            pltpu.SemaphoreType.DMA((3,)),
            pltpu.SemaphoreType.DMA((3,)),
        ],
        compiler_params=pltpu.CompilerParams(
            collective_id=collective, has_side_effects=True, vmem_limit_bytes=60 * 2**20
        ),
        name="final_reduce",
    )(*smalls)


def shards(
    tokens,
    resid_logits,
    routes,
    doc_ids,
    w_qkv,
    w_out,
    gain_attn,
    gain_ffn,
    w_router,
    w_const,
    v_const,
    w_gate_up,
    w_down,
    out_grad,
):
    dp_count, owner_count = lax.axis_size("dp"), lax.axis_size("expert")
    own_links = dp_count == 8 and owner_count == 4 and w_gate_up.shape[0] == 2
    seq_count, length, width = tokens.shape
    assert seq_count == 1
    rows = seq_count * length
    choice_count = resid_logits.shape[-1]
    local_count = w_gate_up.shape[0]
    expert_count = owner_count * local_count
    hidden_count = w_down.shape[1] * dp_count
    width_qkv, width_out = w_qkv.shape[1], w_out.shape[1]
    small_parts = [w_router, w_const, v_const, gain_attn[:, None], gain_ffn[:, None]]
    small_width = sum(part.shape[1] for part in small_parts)
    pad = jnp.zeros((w_qkv.shape[0], 256 - small_width), jnp.bfloat16)
    packed = jnp.concatenate([w_qkv, w_out] + small_parts + [pad], 1)
    inputs = tokens.reshape(rows, width)
    cot = out_grad.reshape(rows, width)
    route_rows = routes.reshape(rows, 2)
    cosine, sine = rotary_lanes(length, width // HEADS)
    docs_row = doc_ids.reshape(1, rows)
    resid_rows = resid_logits.reshape(rows, choice_count)
    if own_links:
        packed_full, spots, spot_rows, table = small_gather(
            packed, route_rows.T, docs_row, resid_rows.T, expert_count, dp_count, 1
        )
    else:
        columns = [
            resid_rows, jnp.zeros((rows, 16 - choice_count)), route_rows, docs_row.T, jnp.zeros((rows, 109))
        ]
        table = jnp.concatenate([column.astype(jnp.float32) for column in columns], 1)
        spots, spot_rows = routing(table, expert_count)
        packed_full = lax.all_gather(packed, "dp", axis=0, tiled=True)
    gather = functools.partial(lax.all_gather, axis_name="dp", axis=0, tiled=True)
    if own_links:
        first_gate_up, second_down, packed_full = lax.optimization_barrier(
            (w_gate_up[0], w_down[1], packed_full)
        )
        first_gate_up, second_down = gather(first_gate_up), gather(second_down)
    else:
        first_gate_up = gather(w_gate_up[0])
    normed_one, queries, keys, values, attended, middle, normed_two, aux = attention_forward(
        inputs, packed_full, docs_row, cosine, sine, table
    )
    send_rows, send_grads = dispatch(spot_rows, aux, normed_two, cot, owner_count, local_count)
    if own_links:
        rows_in, grads_in, first_down = expert_gather(send_rows, send_grads, w_down, dp_count, 2)
        grad_gu, grad_down, both, next_rows, next_grads, second_gate_up = experts(
            rows_in, grads_in, first_gate_up, first_gate_up, first_down, 1, dp_count,
            [send_rows, send_grads, w_gate_up], 6,
        )
        down_parts = [lax.psum_scatter(grad_down, "dp", scatter_dimension=0, tiled=True)]
        second_gu, grad_down, *parts, gu_part = experts(
            next_rows, next_grads, second_gate_up, second_gate_up, second_down, 2, dp_count,
            [both, grad_gu], 4,
        )
        parts, down_parts[0] = lax.optimization_barrier((parts, down_parts[0]))
        down_parts.append(lax.psum_scatter(grad_down, "dp", scatter_dimension=0, tiled=True))
        gu_parts = [gu_part]
    else:
        exchange = functools.partial(
            lax.all_to_all, axis_name="expert", split_axis=0, concat_axis=0, tiled=True
        )
        parts, gu_parts, down_parts = [], [], []
        for e in range(local_count):
            gate_up = first_gate_up if e == 0 else gather(w_gate_up[e])
            grad_gu, grad_down, both = experts(
                exchange(send_rows[e]), exchange(send_grads[e]), gate_up, gate_up, gather(w_down[e])
            )
            parts.append(exchange(both))
            gu_part = lax.psum_scatter(grad_gu, "dp", scatter_dimension=1, tiled=True)
            gu_parts.append(jnp.concatenate([gu_part[0], gu_part[1]], -1).astype(jnp.float32))
            down_parts.append(lax.psum_scatter(grad_down, "dp", scatter_dimension=0, tiled=True))
    down_parts = [part.astype(jnp.float32) for part in down_parts]
    output, logit_grad, grad_middle, small_grad = combine(
        parts, spots, table, aux, normed_two, middle, cot, packed_full, choice_count, expert_count
    )
    backward = functools.partial(
        attention_backward, grad_middle, queries, keys, values, attended, normed_one, inputs,
        packed_full, docs_row, table, cosine, sine, small_grad,
    )
    if own_links:
        token_grad, *weight_grads, gu_part = backward([second_gu], 7)
        gu_parts.append(gu_part)
        packed_part = final_reduce(
            [grad.reshape(dp_count, width // dp_count, grad.shape[1]) for grad in weight_grads], 3
        )
    else:
        token_grad, *weight_grads = backward()
        packed_part = lax.psum_scatter(
            jnp.concatenate(weight_grads, 1), "dp", scatter_dimension=0, tiled=True
        )
        packed_part = lax.psum(packed_part, "expert").astype(jnp.float32)
    part_qkv = packed_part[:, :width_qkv]
    part_out = packed_part[:, width_qkv : width_qkv + width_out]
    small_part = packed_part[:, width_qkv + width_out :]
    return (
        output.reshape(tokens.shape),
        token_grad.reshape(tokens.shape),
        logit_grad.reshape(resid_logits.shape),
        part_qkv,
        part_out,
        small_part[:, 18],
        small_part[:, 19],
        small_part[:, 0:12],
        small_part[:, 12:16],
        small_part[:, 16:18],
        jnp.stack(gu_parts),
        jnp.stack(down_parts),
    )


def solution(mesh):
    placed = (
        P(("dp", "expert"), None, None),
        P(("dp", "expert"), None, None),
        P(("dp", "expert"), None, None),
        P(("dp", "expert"), None),
        P("dp", None),
        P("dp", None),
        P("dp"),
        P("dp"),
        P("dp", None),
        P("dp", None),
        P("dp", None),
        P("expert", "dp", None),
        P("expert", "dp", None),
        P(("dp", "expert"), None, None),
    )
    return jax.shard_map(
        shards,
        mesh=mesh,
        in_specs=placed,
        out_specs=(
            P(("dp", "expert"), None, None),
            P(("dp", "expert"), None, None),
            P(("dp", "expert"), None, None),
            P("dp", None),
            P("dp", None),
            P("dp"),
            P("dp"),
            P("dp", None),
            P("dp", None),
            P("dp", None),
            P("expert", "dp", None),
            P("expert", "dp", None),
        ),
        check_vma=False,
    )
```

```python
import functools

import jax
import jax.numpy as jnp
import numpy as np
from jax import lax
from jax.experimental import pallas as pl
from jax.experimental.pallas import tpu as pltpu
from jax.sharding import PartitionSpec as P

HEADS = 12
BLOCK = 256
CAP = 256
GROUP = 256
FF_BLOCK = 512
MESH = pl.DeviceIdType.MESH
epsilon = 1e-06


def rotary_lanes(length, head_dim):
    half_dim = head_dim // 2
    frequency = (10000.0 ** (-np.arange(half_dim, dtype=np.float32) / half_dim)).astype(np.float32)
    angles = (np.arange(length, dtype=np.float32)[:, None] * frequency[None, :]).astype(np.float64)
    cosine = np.cos(angles).astype(np.float32)
    sine = np.sin(angles).astype(np.float32)
    return (
        np.concatenate([cosine] * 4, 1),
        np.concatenate([-sine, sine, -sine, sine], 1),
    )


def nt(left, right):
    return lax.dot_general(left, right, (((1,), (1,)), ((), ())), preferred_element_type=jnp.float32)


def tn(left, right):
    return lax.dot_general(left, right, (((0,), (0,)), ((), ())), preferred_element_type=jnp.float32)


def nn(left, right):
    return jnp.dot(left, right, preferred_element_type=jnp.float32)


def lane_ids(shape):
    return lax.broadcasted_iota(jnp.int32, shape, len(shape) - 1)


def turn(values, cosine, sine):
    lanes = lane_ids(values.shape)
    ahead, behind = pltpu.roll(values, 96, 1), pltpu.roll(values, 32, 1)
    return values * cosine + jnp.where(lanes % 64 < 32, ahead, behind) * sine


def key_span(i):
    return max(0, i - 2) * BLOCK, (i + 1) * BLOCK


def mask_of(docs_column, docs_row, i):
    low, high = key_span(i)
    return docs_column[low:high, :] == docs_row[:, i * BLOCK : (i + 1) * BLOCK]


def attention_forward_kernel(linked, *refs):
    (
        tokens_ref, wq_ref, wk_ref, wv_ref, wo_ref, small_ref, docs_row_ref,
        cosine_ref, sine_ref, table_ref,
    ) = refs[:10]
    (
        normed_ref, q_ref, k_ref, v_ref, attended_ref, middle_ref, normed_two_ref, aux_ref,
    ) = refs[10 + bool(linked) : 18 + bool(linked)]
    step = pl.program_id(0)
    rows = tokens_ref.shape[0]
    if linked:
        branch_ref = refs[20]
        line = LineGather(refs[10].at[0], refs[19], linked, *refs[21:])

        @pl.when(step == 0)
        def _():
            greet(line.peers())
            line.start()

        @pl.when(step == 2)
        def _():
            line.relay(1)
    else:
        branch_ref = refs[18]

    @pl.when(step == 0)
    def _():
        inputs = tokens_ref[...].astype(jnp.float32)
        gains = jnp.transpose(small_ref[:, :128].astype(jnp.float32))[18:19, :]
        scale = lax.rsqrt(jnp.mean(inputs * inputs, -1, keepdims=True) + epsilon)
        normed_ref[...] = (inputs * scale * gains).astype(jnp.bfloat16)
        branch_ref[...] = jnp.zeros_like(branch_ref)

    normed = normed_ref[...]
    cosine, sine = cosine_ref[...], sine_ref[...]
    for w_ref, out_ref, turned in ((wq_ref, q_ref, True), (wk_ref, k_ref, True), (wv_ref, v_ref, False)):
        projected = nn(normed, w_ref[...])
        for half in range(2):
            part = projected[:, half * 128 : half * 128 + 128]
            if turned:
                part = turn(part, cosine, sine)
            out_ref[:, half * 128 : half * 128 + 128] = part.astype(jnp.bfloat16)

    docs_row, docs_column = docs_row_ref[...], table_ref[:, 18:19].astype(jnp.int32)
    for i in range(rows // BLOCK):
        low, high = key_span(i)
        here = slice(i * BLOCK, (i + 1) * BLOCK)
        allowed = mask_of(docs_column, docs_row, i)
        for pair in range(2):
            lanes = slice(pair * 128, pair * 128 + 128)
            queries = q_ref[here, lanes] * jnp.asarray(0.125, jnp.bfloat16)
            keys, values = k_ref[low:high, lanes], v_ref[low:high, lanes]
            left = lane_ids(queries.shape) < 64
            outs = []
            for head in range(2):
                own = left if head == 0 else jnp.logical_not(left)
                scores = nt(keys, jnp.where(own, queries, jnp.zeros_like(queries)))
                scores = jnp.where(allowed, scores, -1e30)
                shifted = jnp.exp(scores - jnp.max(scores, 0, keepdims=True))
                probs = shifted * (1.0 / jnp.sum(shifted, 0, keepdims=True))
                outs.append(tn(probs.astype(jnp.bfloat16), values))
            attended_ref[here, lanes] = jnp.where(left, outs[0], outs[1]).astype(jnp.bfloat16)
    branch_ref[...] += nn(attended_ref[...], wo_ref[...])

    @pl.when(step == pl.num_programs(0) - 1)
    def _():
        small = small_ref[:, :128]
        gains = jnp.transpose(small.astype(jnp.float32))[19:20, :]
        middle = tokens_ref[...].astype(jnp.float32) + branch_ref[...]
        middle_ref[...] = middle
        scale = lax.rsqrt(jnp.mean(middle * middle, -1, keepdims=True) + epsilon)
        normed_two = (middle * scale * gains).astype(jnp.bfloat16)
        normed_two_ref[...] = normed_two
        logits = nn(normed_two, small) + table_ref[...]
        lanes = lane_ids(logits.shape)

        def lane(at):
            return jnp.sum(jnp.where(lanes == at, logits, 0.0), -1, keepdims=True)

        def two(first, second):
            peak = jnp.maximum(first, second)
            first, second = jnp.exp(first - peak), jnp.exp(second - peak)
            return first / (first + second), second / (first + second)

        columns = list(two(*[lane(table_ref[:, 16 + s : 17 + s].astype(jnp.int32)) for s in range(2)]))
        columns += list(two(lane(12), lane(13))) + list(two(lane(14), lane(15)))
        columns.append(scale)
        aux = jnp.zeros_like(logits)
        for at, column in enumerate(columns):
            aux = jnp.where(lanes == at, column, aux)
        aux_ref[...] = aux
        if linked:
            line.relay(2)
            line.relay(3)
            line.finish()


def attention_forward(
    tokens, packed, docs_row, cosine, sine, table, shards=None,
    dp_count=None, collective=None,
):
    rows, width = tokens.shape
    groups = width // GROUP
    low = jnp.bfloat16
    whole = lambda shape: pl.BlockSpec(shape, lambda j: (0, 0))
    column = lambda at: pl.BlockSpec((width, GROUP), lambda j: (0, at + j))
    out_column = pl.BlockSpec((rows, GROUP), lambda j: (0, j))
    full = jax.ShapeDtypeStruct((rows, width), low)
    linked = shards is not None
    anywhere = pl.BlockSpec(memory_space=pl.ANY)
    links = {"collective_id": collective, "has_side_effects": True} if linked else {}
    gathered = []
    if linked:
        gathered = [jax.ShapeDtypeStruct((dp_count * shards.shape[1], shards.shape[2]), low)]
    return pl.pallas_call(
        functools.partial(attention_forward_kernel, dp_count if linked else 0),
        grid=(groups,),
        out_shape=[full] * 5
        + [
            jax.ShapeDtypeStruct((rows, width), jnp.float32),
            full,
            jax.ShapeDtypeStruct((rows, 128), jnp.float32),
        ]
        + gathered,
        in_specs=[
            whole((rows, width)),
            column(0),
            column(groups),
            column(2 * groups),
            pl.BlockSpec((GROUP, width), lambda j: (j, 3)),
            pl.BlockSpec((width, 256), lambda j: (0, 12)),
            whole((1, rows)),
            whole((rows, 128)),
            whole((rows, 128)),
            whole((rows, 128)),
        ]
        + [anywhere] * linked,
        out_specs=[whole((rows, width))]
        + [out_column] * 4
        + [whole((rows, width)), whole((rows, width)), whole((rows, 128))]
        + [anywhere] * linked,
        scratch_shapes=[pltpu.VMEM((rows, width), jnp.float32)]
        + (gather_semaphores(dp_count) if linked else []),
        compiler_params=pltpu.CompilerParams(
            dimension_semantics=("arbitrary",), vmem_limit_bytes=56 * 2**20, **links
        ),
        cost_estimate=pl.CostEstimate(
            flops=2 * rows * width * 4 * width + 8 * rows * rows * width // 2,
            bytes_accessed=24 * rows * width,
            transcendentals=rows * rows * HEADS // 2,
        ),
        name="attention_forward",
    )(
        tokens, packed, packed, packed, packed, packed, docs_row, cosine, sine, table,
        *([shards] if linked else []),
    )


def attention_backward_kernel(count, *refs):
    (
        grad_middle_ref, q_ref, k_ref, v_ref, attended_ref, normed_ref, tokens_ref,
        wq_ref, wk_ref, wv_ref, wo_ref, small_ref, docs_row_ref, table_ref,
        cosine_ref, sine_ref, small_grad_ref,
    ) = refs[:17]
    sources, refs = refs[17 : 17 + count], refs[17 + count :]
    token_grad_ref, gq_ref, gk_ref, gv_ref, go_ref, small_out_ref = refs[:6]
    totals, refs = refs[6 : 6 + count], refs[6 + count :]
    branch_ref, back_ref, turned_ref, key_acc, value_acc, query_acc = refs[:6]
    step = pl.program_id(0)
    rows, width = tokens_ref.shape
    if count:
        line = line_reduce(sources[0], totals[0], refs[6:], 2)

        @pl.when(step == 0)
        def _():
            greet(line.peers())
            line.each_plane(line.start)

        pl.when(step == 1)(lambda: line.turns([0], []))
        pl.when(step == 2)(lambda: line.turns([1], [0]))

    @pl.when(step == 0)
    def _():
        branch_ref[...] = grad_middle_ref[...].astype(jnp.bfloat16)
        back_ref[...] = jnp.zeros_like(back_ref)

    grad_branch = branch_ref[...]
    grad_attended = nt(grad_branch, wo_ref[...]).astype(jnp.bfloat16)
    go_ref[...] = tn(attended_ref[...], grad_branch).astype(jnp.bfloat16)
    cosine, sine = cosine_ref[...], sine_ref[...]
    docs_row, docs_column = docs_row_ref[...], table_ref[:, 18:19].astype(jnp.int32)
    for pair in range(2):
        lanes = slice(pair * 128, pair * 128 + 128)
        key_acc[...] = jnp.zeros_like(key_acc)
        value_acc[...] = jnp.zeros_like(value_acc)
        for i in range(rows // BLOCK):
            low, high = key_span(i)
            here = slice(i * BLOCK, (i + 1) * BLOCK)
            allowed = mask_of(docs_column, docs_row, i)
            queries = q_ref[here, lanes] * jnp.asarray(0.125, jnp.bfloat16)
            grads = grad_attended[here, lanes]
            keys, values = k_ref[low:high, lanes], v_ref[low:high, lanes]
            left = lane_ids(queries.shape) < 64
            query_grads = []
            key_grad, value_grad = None, None
            for head in range(2):
                own = left if head == 0 else jnp.logical_not(left)
                own_queries = jnp.where(own, queries, jnp.zeros_like(queries))
                own_grads = jnp.where(own, grads, jnp.zeros_like(grads))
                scores = jnp.where(allowed, nt(keys, own_queries), -1e30)
                shifted = jnp.exp(scores - jnp.max(scores, 0, keepdims=True))
                probs = shifted * (1.0 / jnp.sum(shifted, 0, keepdims=True))
                grad_probs = nt(values, own_grads)
                inner = jnp.sum(probs * grad_probs, 0, keepdims=True)
                grad_scores = (probs * (grad_probs - inner)).astype(jnp.bfloat16)
                part_value = nn(probs.astype(jnp.bfloat16), own_grads)
                part_key = nn(grad_scores, own_queries)
                value_grad = part_value if head == 0 else value_grad + part_value
                key_grad = part_key if head == 0 else key_grad + part_key
                query_grads.append(tn(grad_scores, keys))
            value_acc[low:high, :] += value_grad
            key_acc[low:high, :] += key_grad
            query_acc[here, :] = jnp.where(left, query_grads[0], query_grads[1]) * 0.125
        turned_ref[0, :, lanes] = turn(query_acc[...], cosine, -sine).astype(jnp.bfloat16)
        turned_ref[1, :, lanes] = turn(key_acc[...], cosine, -sine).astype(jnp.bfloat16)
        turned_ref[2, :, lanes] = value_acc[...].astype(jnp.bfloat16)
    normed = normed_ref[...]
    for at, (w_ref, out_ref) in enumerate(((wq_ref, gq_ref), (wk_ref, gk_ref), (wv_ref, gv_ref))):
        turned = turned_ref[at]
        out_ref[...] = tn(normed, turned).astype(jnp.bfloat16)
        back_ref[...] += nt(turned, w_ref[...])

    @pl.when(step == pl.num_programs(0) - 1)
    def _():
        gains = jnp.transpose(small_ref[:, :128].astype(jnp.float32))[18:19, :]
        inputs = tokens_ref[...].astype(jnp.float32)
        grads = back_ref[...]
        scale = lax.rsqrt(jnp.mean(inputs * inputs, -1, keepdims=True) + epsilon)
        weighted = grads * gains
        mean = jnp.mean(weighted * inputs, -1, keepdims=True)
        grad_inputs = scale * weighted - inputs * (scale * scale * scale * mean)
        token_grad_ref[...] = (grad_inputs + grad_middle_ref[...]).astype(jnp.bfloat16)
        gain_grad = jnp.sum(grads * inputs * scale, 0, keepdims=True)
        column = jnp.transpose(jnp.broadcast_to(gain_grad, (128, width)))
        small_grad = small_grad_ref[...]
        small_grad = jnp.where(lane_ids(small_grad.shape) == 18, column, small_grad)
        small_out_ref[...] = small_grad.astype(jnp.bfloat16)
        if count:
            line.turns([2, 3], [1, 2, 3])
            line.each_plane(line.finish)


def attention_backward(
    grad_middle, queries, keys, values, attended, normed, tokens, packed, docs_row, table,
    cosine, sine, small_grad, sources=(), collective=None,
):
    rows, width = tokens.shape
    groups = width // GROUP
    low = jnp.bfloat16
    whole = lambda shape: pl.BlockSpec(shape, lambda j: (0, 0))
    column = lambda at: pl.BlockSpec((width, GROUP), lambda j: (0, at + j))
    by_group = pl.BlockSpec((rows, GROUP), lambda j: (0, j))
    weight = jax.ShapeDtypeStruct((width, width), low)
    linked = len(sources) > 0
    links = {"collective_id": collective, "has_side_effects": True} if linked else {}
    sums = []
    for source in sources:
        sums.append((source.shape[-2] // 8, source.shape[0] * source.shape[-1]))
    once = lambda shape: pl.BlockSpec(
        shape, lambda j: (0, 0), pipeline_mode=pl.Buffered(1)
    )
    return pl.pallas_call(
        functools.partial(attention_backward_kernel, len(sources)),
        grid=(groups,),
        out_shape=[jax.ShapeDtypeStruct((rows, width), low)]
        + [weight] * 4
        + [jax.ShapeDtypeStruct((width, 128), low)]
        + [jax.ShapeDtypeStruct(shape, jnp.float32) for shape in sums],
        in_specs=[
            once((rows, width)),
            by_group,
            by_group,
            by_group,
            by_group,
            once((rows, width)),
            once((rows, width)),
            column(0),
            column(groups),
            column(2 * groups),
            pl.BlockSpec((GROUP, width), lambda j: (j, 3)),
            pl.BlockSpec((width, 256), lambda j: (0, 12)),
            once((1, rows)),
            once((rows, 128)),
            once((rows, 128)),
            once((rows, 128)),
            once((width, 128)),
        ]
        + [pl.BlockSpec(memory_space=pl.ANY)] * len(sources),
        out_specs=[
            whole((rows, width)),
            column(0),
            column(0),
            column(0),
            pl.BlockSpec((GROUP, width), lambda j: (j, 0)),
            whole((width, 128)),
        ]
        + [whole(shape) for shape in sums],
        scratch_shapes=[
            pltpu.VMEM((rows, width), low),
            pltpu.VMEM((rows, width), jnp.float32),
            pltpu.VMEM((3, rows, GROUP), low),
            pltpu.VMEM((rows, 128), jnp.float32),
            pltpu.VMEM((rows, 128), jnp.float32),
            pltpu.VMEM((rows, 128), jnp.float32),
        ]
        + (reduce_scratch(sources[0], 2) if linked else []),
        compiler_params=pltpu.CompilerParams(
            dimension_semantics=("arbitrary",), vmem_limit_bytes=61 * 2**20, **links
        ),
        cost_estimate=pl.CostEstimate(
            flops=4 * rows * width * 4 * width + 20 * rows * rows * width // 2,
            bytes_accessed=32 * rows * width,
            transcendentals=rows * rows * HEADS // 2,
        ),
        name="attention_backward",
    )(
        grad_middle, queries, keys, values, attended, normed, tokens, packed, packed, packed,
        packed, packed, docs_row, table, cosine, sine, small_grad, *sources,
    )


def routing_kernel(expert_count, table_ref, columns_ref, rows_ref):
    rows = table_ref.shape[0]
    lanes = lane_ids((rows, 128))
    routes = [table_ref[:, 16 + s : 17 + s].astype(jnp.int32) for s in range(2)]
    first = (lanes == routes[0]).astype(jnp.float32)
    second = (lanes == routes[1]).astype(jnp.float32)
    down = lax.broadcasted_iota(jnp.int32, (rows, rows), 0)
    lower = (down > lane_ids((rows, rows))).astype(jnp.bfloat16)
    before_first = nn(lower, first.astype(jnp.bfloat16))
    before_second = nn(lower, second.astype(jnp.bfloat16)) + jnp.sum(first, 0, keepdims=True)
    spots = []
    for picked, before, at in ((first, before_first, 0), (second, before_second, 1)):
        rank = jnp.sum(picked * before, -1, keepdims=True)
        route = routes[at]
        spot = route.astype(jnp.float32) * CAP + rank
        spots.append(jnp.where(route < expert_count, spot, jnp.full_like(spot, 2.0 * expert_count * CAP)))
    both = jnp.where(lanes == 0, spots[0], jnp.where(lanes == 1, spots[1], 0.0))
    columns_ref[...] = both.astype(jnp.int32)
    rows_ref[...] = jnp.transpose(both)[0:8, :].astype(jnp.int32)


def routing(table, expert_count):
    rows = table.shape[0]
    return pl.pallas_call(
        functools.partial(routing_kernel, expert_count),
        out_shape=[
            jax.ShapeDtypeStruct((rows, 128), jnp.int32),
            jax.ShapeDtypeStruct((8, rows), jnp.int32),
        ],
        compiler_params=pltpu.CompilerParams(vmem_limit_bytes=40 * 2**20),
        name="routing",
    )(table)


def dispatch_kernel(local_count, spots_ref, aux_ref, normed_ref, cot_ref, rows_ref, grads_ref, gates_ref):
    step = pl.program_id(0)

    @pl.when(step == 0)
    def _():
        gates_ref[...] = jnp.transpose(aux_ref[...])[0:8, :]

    owners, width = rows_ref.shape[0], rows_ref.shape[2]
    shape = (owners * CAP, normed_ref.shape[0])
    place_in = lax.broadcasted_iota(jnp.int32, shape, 0)
    first_owner = step // local_count * owners
    slots = (first_owner + place_in // CAP) * (local_count * CAP)
    slots = slots + step % local_count * CAP + place_in % CAP
    first, second = slots == spots_ref[0:1, :], slots == spots_ref[1:2, :]
    gates = jnp.sum(
        jnp.where(first, gates_ref[0:1, :], jnp.where(second, gates_ref[1:2, :], 0.0)), -1, keepdims=True
    )
    chosen = jnp.where(first | second, 1.0, 0.0).astype(jnp.bfloat16)
    rows_ref[...] = nn(chosen, normed_ref[...]).astype(jnp.bfloat16).reshape(owners, CAP, width)
    grads_ref[...] = (
        (nn(chosen, cot_ref[...]) * gates).astype(jnp.bfloat16).reshape(owners, CAP, width)
    )


def dispatch(spots, aux, normed, cot, owner_count, local_count):
    rows, width = normed.shape
    slot_count = owner_count * local_count * CAP
    whole = lambda shape: pl.BlockSpec(shape, lambda j: (0, 0))
    block = pl.BlockSpec(
        (None, 2, CAP, width), lambda j: (j % local_count, j // local_count, 0, 0)
    )
    return pl.pallas_call(
        functools.partial(dispatch_kernel, local_count),
        grid=(slot_count // CAP // 2,),
        out_shape=[jax.ShapeDtypeStruct((local_count, owner_count, CAP, width), jnp.bfloat16)] * 2,
        in_specs=[whole((8, rows)), whole((rows, 128)), whole((rows, width)), whole((rows, width))],
        out_specs=[block, block],
        scratch_shapes=[pltpu.VMEM((8, rows), jnp.float32)],
        compiler_params=pltpu.CompilerParams(
            dimension_semantics=("arbitrary",), vmem_limit_bytes=60 * 2**20
        ),
        cost_estimate=pl.CostEstimate(
            flops=4 * slot_count * rows * width,
            bytes_accessed=4 * (rows + slot_count) * width,
            transcendentals=0,
        ),
        name="dispatch",
    )(spots, aux, normed, cot)


def halves(values):
    high = values.astype(jnp.bfloat16)
    return high, (values - high.astype(jnp.float32)).astype(jnp.bfloat16)


def combine_kernel(
    expert_count, local_count, linked, *refs
):
    parts, refs = refs[:local_count], refs[local_count:]
    spots_ref, table_ref, aux_ref, normed_ref, middle_ref, cot_ref, small_ref = refs[:7]
    refs = refs[7:]
    if linked:
        source_ref, refs = refs[0], refs[1:]
    output_ref, logit_ref, grad_middle_ref, small_out_ref = refs[:4]
    refs = refs[4:]
    if linked:
        total_ref, refs = refs[0], refs[1:]
    vectors_ref, small_grad_ref = refs[:2]
    step = pl.program_id(0)
    if linked:
        line = line_reduce(source_ref, total_ref, refs[2:], 2, (0,))

        @pl.when(step == 0)
        def _():
            greet(line.peers())
            line.each_plane(line.start)

        pl.when(step == 1)(lambda: line.turns([0], []))

    @pl.when(step == 0)
    def _():
        vectors_ref[0:8, :] = jnp.transpose(small_ref[:, :128].astype(jnp.float32))[16:24, :]
        vectors_ref[8:16, :] = jnp.zeros((8, vectors_ref.shape[1]), jnp.float32)
        small_grad_ref[...] = jnp.zeros_like(small_grad_ref)

    rows, width = normed_ref.shape
    normed_low, cot_low = normed_ref[...], cot_ref[...]
    normed, cot = normed_low.astype(jnp.float32), cot_low.astype(jnp.float32)
    total = lambda values: jnp.sum(values, -1, keepdims=True)
    picks, back = [0.0, 0.0], 0.0
    for e in range(local_count):
        count = parts[e].shape[0] * CAP
        slots = lane_ids((rows, count))
        slots = slots // CAP * (local_count * CAP) + e * CAP + slots % CAP
        hits = [slots == spots_ref[:, s : s + 1] for s in range(2)]
        chosen = [jnp.where(hit, 1.0, 0.0).astype(jnp.bfloat16) for hit in hits]
        returned = parts[e][:, 0].reshape(count, width)
        both = nn(jnp.concatenate(chosen, 0), returned)
        for s in range(2):
            picks[s] = picks[s] + both[s * rows : (s + 1) * rows, :]
        back = back + nn(chosen[0] + chosen[1], parts[e][:, 1].reshape(count, width))
    inner = [total(pick * cot) for pick in picks]
    gates = [aux_ref[:, s : s + 1] for s in range(2)]
    routes = [table_ref[:, 16 + s : 17 + s].astype(jnp.int32) for s in range(2)]
    dot_copy = total(cot * normed)

    def weight_of(route):
        return sum(jnp.where(routes[s] == route, gates[s], 0.0) for s in range(2))

    copy_weight = weight_of(expert_count + 1)
    mix = gates[0] * picks[0] + gates[1] * picks[1]
    pass_weight = copy_weight
    gate_grads = [
        inner[s] + jnp.where(routes[s] == expert_count + 1, dot_copy, 0.0) for s in range(2)
    ]
    lanes = lane_ids((rows, 128))
    spread = jnp.zeros((rows, 128), jnp.float32)
    for k in range(2):
        vector = vectors_ref[k : k + 1, :]
        keep, blend = aux_ref[:, 2 + 2 * k : 3 + 2 * k], aux_ref[:, 3 + 2 * k : 4 + 2 * k]
        weight = weight_of(expert_count + 2 + k)
        dot_vector = total(cot * vector)
        pass_weight = pass_weight + weight * keep
        mix = mix + (weight * blend) * vector
        value = keep * dot_copy + blend * dot_vector
        for s in range(2):
            gate_grads[s] = gate_grads[s] + jnp.where(routes[s] == expert_count + 2 + k, value, 0.0)
        term = keep * blend * (weight * dot_copy - weight * dot_vector)
        spread = jnp.where(lanes == 12 + 2 * k, term, spread)
        spread = jnp.where(lanes == 13 + 2 * k, -term, spread)
        spread = jnp.where(lanes == 16 + k, weight * blend, spread)
    mix = mix + pass_weight * normed
    middle, scale = middle_ref[...], aux_ref[:, 6:7]
    output_ref[...] = (middle + mix).astype(jnp.bfloat16)
    mean = gates[0] * gate_grads[0] + gates[1] * gate_grads[1]
    for s in range(2):
        spread = jnp.where(lanes == routes[s], gates[s] * (gate_grads[s] - mean), spread)
    logit_ref[...] = spread[:, : logit_ref.shape[1]].astype(jnp.bfloat16)
    logits = jnp.where(lanes < 16, spread, 0.0)
    high, low = halves(logits)
    small = small_ref[:, :128]
    vector_high, vector_low = halves(spread - logits)
    small_grad_ref[...] += (
        tn(normed_low, high) + tn(normed_low, low) + tn(cot_low, vector_high) + tn(cot_low, vector_low)
    )
    grads = back + pass_weight * cot + nt(high, small) + nt(low, small)
    vectors_ref[8:9, :] += jnp.sum(grads * middle * scale, 0, keepdims=True)
    weighted = grads * vectors_ref[3:4, :]
    mean = jnp.mean(weighted * middle, -1, keepdims=True)
    grad_middle_ref[...] = cot + scale * weighted - middle * (scale * scale * scale * mean)

    @pl.when(step == pl.num_programs(0) - 1)
    def _():
        column = jnp.transpose(jnp.broadcast_to(vectors_ref[8:9, :], (128, width)))
        small_grad = small_grad_ref[...]
        small_out_ref[...] = jnp.where(lane_ids(small_grad.shape) == 19, column, small_grad)
        if linked:
            line.turns([1, 2, 3], [0, 1, 2, 3])
            line.each_plane(line.finish)


def combine(
    parts, spots, table, aux, normed, middle, cot, packed, choice_count, expert_count, source=None,
    collective=None,
):
    rows, width = normed.shape
    local_count = len(parts)
    slot_count = expert_count * CAP
    size = 256
    linked = source is not None
    links = {"collective_id": collective, "has_side_effects": True} if linked else {}
    block = lambda columns: pl.BlockSpec((size, columns), lambda j: (j, 0))
    whole = lambda shape: pl.BlockSpec(shape, lambda j: (0,) * len(shape))
    return pl.pallas_call(
        functools.partial(combine_kernel, expert_count, local_count, linked),
        grid=(rows // size,),
        out_shape=[
            jax.ShapeDtypeStruct((rows, width), jnp.bfloat16),
            jax.ShapeDtypeStruct((rows, choice_count), jnp.bfloat16),
            jax.ShapeDtypeStruct((rows, width), jnp.float32),
            jax.ShapeDtypeStruct((width, 128), jnp.float32),
        ]
        + ([jax.ShapeDtypeStruct((width // 8, source.shape[2]), jnp.float32)] if linked else []),
        in_specs=[whole(part.shape) for part in parts]
        + [
            block(128),
            block(128),
            block(128),
            block(width),
            block(width),
            block(width),
            pl.BlockSpec((width, 256), lambda j: (0, 12)),
        ]
        + [pl.BlockSpec(memory_space=pl.ANY)] * linked,
        out_specs=[block(width), block(choice_count), block(width), whole((width, 128))]
        + ([whole((width // 8, source.shape[2]))] if linked else []),
        scratch_shapes=[pltpu.VMEM((16, width), jnp.float32), pltpu.VMEM((width, 128), jnp.float32)]
        + (reduce_scratch(source, 2, (0,)) if linked else []),
        compiler_params=pltpu.CompilerParams(
            dimension_semantics=("arbitrary",), vmem_limit_bytes=58 * 2**20, **links
        ),
        cost_estimate=pl.CostEstimate(
            flops=6 * slot_count * rows * width,
            bytes_accessed=14 * rows * width + 4 * slot_count * width,
            transcendentals=0,
        ),
        name="combine",
    )(*parts, spots, table, aux, normed, middle, cot, packed, *([source] if linked else []))


def experts_kernel(mode, dp_count, *refs):
    rows_ref, grads_ref, w_gate_ref, w_up_ref, w_down_ref = refs[:5]
    if mode == 0:
        grad_gu_ref, grad_down_ref, both_ref, turned_ref, out_ref, back_ref = refs[5:]
    if mode == 1:
        next_rows, next_grads, shards_ref, grad_gu_ref, grad_down_ref, both_ref = refs[5:11]
        rows_out, grads_out, full_ref, turned_ref, out_ref, back_ref = refs[11:17]
        sems = refs[17:]
    if mode == 2:
        before_ref, source_ref, grad_gu_ref, grad_down_ref, first_in, second_in, total_ref = refs[5:12]
        turned_ref, out_ref, back_ref, both_ref = refs[12:16]
        sems = refs[16:]
    step = pl.program_id(0)
    width = rows_ref.shape[-1]
    rows = rows_ref[...].reshape(-1, width)
    grads = grads_ref[...].reshape(-1, width)
    if mode == 1:
        half = full_ref.shape[1] // 2
        lines = []
        for n in range(2):
            columns = slice(n * half, n * half + half)
            lines.append(
                LineGather(
                    shards_ref.at[1, :, columns], full_ref, dp_count, *sems[3 * n : 3 * n + 3], columns
                )
            )
        trades = [
            Trade(next_rows.at[1], rows_out, *sems[6:8]),
            Trade(next_grads.at[1], grads_out, *sems[8:10]),
        ]

        @pl.when(step == 0)
        def _():
            greet(lines[0].peers() + trades[0].peers())
            for part in lines + trades:
                part.start()

        for hop in range(1, 4):

            @pl.when(step == hop)
            def _(hop=hop):
                for part in lines:
                    part.relay(hop)

    if mode == 2:
        trades = [Trade(before_ref, first_in, *sems[:2]), Trade(both_ref, second_in, *sems[2:4])]
        line = line_reduce(source_ref, total_ref, sems[4:], 2)

        @pl.when(step == 0)
        def _():
            greet(line.peers() + trades[0].peers())
            line.each_plane(line.start)
            trades[0].start()

        pl.when(step == 2)(lambda: line.turns([0], []))

    @pl.when(step == 0)
    def _():
        turned_ref[...] = jnp.transpose(rows)
        out_ref[...] = jnp.zeros_like(out_ref)
        back_ref[...] = jnp.zeros_like(back_ref)

    w_gate, w_up, w_down = w_gate_ref[...], w_up_ref[...], w_down_ref[...]
    gate, up = nn(rows, w_gate), nn(rows, w_up)
    squashed = 1.0 / (1.0 + jnp.exp(-gate))
    silu = gate * squashed
    activated = (silu * up).astype(jnp.bfloat16)
    grad_act = nt(grads, w_down)
    grad_gate = (grad_act * up * (squashed * (1.0 + gate * (1.0 - squashed)))).astype(jnp.bfloat16)
    grad_up = (grad_act * silu).astype(jnp.bfloat16)
    out_ref[...] += nn(activated, w_down)
    grad_down_ref[...] = tn(activated, grads).astype(jnp.bfloat16)
    back_ref[...] += nt(grad_gate, w_gate) + nt(grad_up, w_up)
    grad_gu_ref[0] = nn(turned_ref[...], grad_gate).astype(jnp.bfloat16)
    grad_gu_ref[1] = nn(turned_ref[...], grad_up).astype(jnp.bfloat16)

    @pl.when(step == pl.num_programs(0) - 1)
    def _():
        shape = (both_ref.shape[0],) + both_ref.shape[2:]
        both_ref[:, 0] = out_ref[...].astype(jnp.bfloat16).reshape(shape)
        both_ref[:, 1] = back_ref[...].astype(jnp.bfloat16).reshape(shape)
        if mode == 1:
            for part in lines + trades:
                part.finish()
        if mode == 2:
            trades[1].start()
            line.turns([1, 2, 3], [0, 1, 2, 3])
            line.each_plane(line.finish)
            for trade in trades:
                trade.finish()


def experts(rows, grads, gate, up, down, mode=0, dp_count=0, extras=(), collective=None):
    owners, cap, width = rows.shape
    hidden = down.shape[0]
    count = owners * cap
    block = FF_BLOCK if count <= 1024 else FF_BLOCK // 4
    steps = hidden // block
    low = jnp.bfloat16
    pairs = pl.BlockSpec((owners, cap, width), lambda j: (0, 0, 0), pipeline_mode=pl.Buffered(1))
    anywhere = pl.BlockSpec(memory_space=pl.ANY)
    both = jax.ShapeDtypeStruct((owners, 2, cap, width), low)
    links = {"collective_id": collective, "has_side_effects": True} if mode else {}
    out_shape = [
        jax.ShapeDtypeStruct((2, width, hidden), low),
        jax.ShapeDtypeStruct((hidden, width), low),
    ]
    out_specs = [
        pl.BlockSpec((2, width, block), lambda j: (0, 0, j)),
        pl.BlockSpec((block, width), lambda j: (j, 0)),
    ]
    scratch = [
        pltpu.VMEM((width, count), low),
        pltpu.VMEM((count, width), jnp.float32),
        pltpu.VMEM((count, width), jnp.float32),
    ]
    if mode < 2:
        out_shape.append(both)
        out_specs.append(pl.BlockSpec(both.shape, lambda j: (0, 0, 0, 0)))
    if mode == 1:
        shards = extras[2]
        out_shape += [jax.ShapeDtypeStruct(rows.shape, low)] * 2
        out_shape.append(jax.ShapeDtypeStruct((dp_count * shards.shape[1], shards.shape[2]), low))
        out_specs += [anywhere] * 3
        scratch += gather_semaphores(dp_count) * 2 + trade_semaphores(owners) + trade_semaphores(owners)
    if mode == 2:
        total = (width // 8, 2 * hidden)
        out_shape += [both, both, jax.ShapeDtypeStruct(total, jnp.float32)]
        out_specs += [anywhere] * 2 + [pl.BlockSpec(total, lambda j: (0, 0))]
        scratch.append(pltpu.VMEM(both.shape, low))
        scratch += trade_semaphores(owners) + trade_semaphores(owners) + reduce_scratch(extras[1], 2)
    return pl.pallas_call(
        functools.partial(experts_kernel, mode, dp_count),
        grid=(steps,),
        out_shape=out_shape,
        in_specs=[
            pairs,
            pairs,
            pl.BlockSpec((width, block), lambda j: (0, j)),
            pl.BlockSpec((width, block), lambda j: (0, up.shape[1] // block - steps + j)),
            pl.BlockSpec((block, width), lambda j: (j, 0)),
        ]
        + [anywhere] * len(extras),
        out_specs=out_specs,
        scratch_shapes=scratch,
        compiler_params=pltpu.CompilerParams(
            dimension_semantics=("arbitrary",), vmem_limit_bytes=60 * 2**20, **links
        ),
        cost_estimate=pl.CostEstimate(
            flops=18 * count * width * hidden,
            bytes_accessed=12 * width * hidden + 8 * count * width,
            transcendentals=count * hidden,
        ),
        name="experts",
    )(rows, grads, gate, up, down, *extras)


def dp_grid(dp_count):
    outer = 4 if dp_count % 4 == 0 else 1
    return outer, dp_count // outer


def place():
    me, mine = lax.axis_index("dp"), lax.axis_index("expert")
    return me, mine


def greet(peers):
    barrier = pltpu.get_barrier_semaphore()
    for peer in peers:
        pl.semaphore_signal(barrier, inc=1, device_id=peer, device_id_type=MESH)
    pl.semaphore_wait(barrier, len(peers))


class LineGather:
    def __init__(self, shard, full, dp_count, send_sem, recv_sem, own_sem, columns=None, also=None):
        self.columns = slice(None) if columns is None else columns
        self.also = also or (lambda chunk: None)
        self.shard, self.full, self.dp_count = shard, full, dp_count
        self.send_sem, self.recv_sem, self.own_sem = send_sem, recv_sem, own_sem
        self.outer_count, self.inner_count = dp_grid(dp_count)
        self.me, self.mine = place()
        self.outer, self.inner = self.me // self.inner_count, self.me % self.inner_count
        self.inner_peers = [
            lax.rem(self.inner + k, self.inner_count) for k in range(1, self.inner_count)
        ]
        self.can_up, self.can_down = self.outer < self.outer_count - 1, self.outer > 0

    def peers(self):
        below = lax.rem(self.outer + self.outer_count - 1, self.outer_count)
        above = lax.rem(self.outer + 1, self.outer_count)
        return [(peer * self.inner_count + self.inner, self.mine) for peer in (below, above)] + [
            (self.outer * self.inner_count + peer, self.mine) for peer in self.inner_peers
        ]

    def spot(self, chunk):
        rows = self.shard.shape[0]
        return self.full.at[pl.ds(pl.multiple_of(chunk * rows, 8), rows), self.columns]

    def copy(self, source, chunk, device, way, at):
        return pltpu.make_async_remote_copy(
            src_ref=source,
            dst_ref=self.spot(chunk),
            send_sem=self.send_sem.at[way, at, chunk],
            recv_sem=self.recv_sem.at[chunk],
            device_id=(device, self.mine),
            device_id_type=MESH,
        )

    def up(self, source, chunk):
        return self.copy(source, chunk, (self.outer + 1) * self.inner_count + self.inner, 1, 0)

    def down(self, source, chunk):
        return self.copy(source, chunk, (self.outer - 1) * self.inner_count + self.inner, 2, 0)

    def across(self, source, chunk):
        return [
            self.copy(source, chunk, self.outer * self.inner_count + peer, 0, at)
            for at, peer in enumerate(self.inner_peers)
        ]

    def keep(self):
        return pltpu.make_async_copy(self.shard, self.spot(self.me), self.own_sem)

    def arrived(self, chunk):
        pltpu.make_async_copy(self.spot(chunk), self.spot(chunk), self.recv_sem.at[chunk]).wait()

    def start(self):
        for copy in self.across(self.shard, self.me):
            copy.start()
        pl.when(self.can_up)(lambda: self.up(self.shard, self.me).start())
        pl.when(self.can_down)(lambda: self.down(self.shard, self.me).start())
        self.keep().start()

    def relay(self, step):
        low, high = self.outer - step, self.outer + step

        def pass_on(source, upward):
            chunk = source * self.inner_count + self.inner
            self.arrived(chunk)
            if upward:
                pl.when(self.can_up)(lambda: self.up(self.spot(chunk), chunk).start())
            else:
                pl.when(self.can_down)(lambda: self.down(self.spot(chunk), chunk).start())
            for copy in self.across(self.spot(chunk), chunk):
                copy.start()
            self.also(chunk)

        pl.when(low >= 0)(lambda: pass_on(low, True))
        pl.when(high < self.outer_count)(lambda: pass_on(high, False))

    def finish(self):
        self.keep().wait()
        for peer in self.inner_peers:
            for k in range(self.outer_count):
                chunk = lax.rem(self.outer + k, self.outer_count) * self.inner_count + peer
                self.arrived(chunk)
                self.also(chunk)
        for plane in range(self.outer_count):
            chunk = plane * self.inner_count + self.inner
            for copy in self.across(self.spot(chunk), chunk):
                copy.wait_send()
            pl.when(self.can_up & (self.outer >= plane))(
                lambda chunk=chunk: self.up(self.spot(chunk), chunk).wait_send()
            )
            pl.when(self.can_down & (self.outer <= plane))(
                lambda chunk=chunk: self.down(self.spot(chunk), chunk).wait_send()
            )


def gather_semaphores(dp_count):
    inner_count = dp_grid(dp_count)[1]
    return [
        pltpu.SemaphoreType.DMA((3, max(1, inner_count - 1), dp_count)),
        pltpu.SemaphoreType.DMA((dp_count,)),
        pltpu.SemaphoreType.DMA,
    ]


def by_rows(count, body):
    def step(i, carry):
        body(i * 16)
        return carry

    lax.fori_loop(0, count // 16, step, 0)


class Trade:
    def __init__(self, source, target, send_sem, recv_sem):
        self.source, self.target, self.send_sem, self.recv_sem = source, target, send_sem, recv_sem
        self.me, self.mine = place()
        count = target.shape[0]
        self.partners = [lax.rem(self.mine + k, count) for k in range(1, count)]

    def peers(self):
        return [(self.me, peer) for peer in self.partners]

    def copy(self, k):
        peer = self.partners[k]
        return pltpu.make_async_remote_copy(
            src_ref=self.source.at[peer],
            dst_ref=self.target.at[self.mine],
            send_sem=self.send_sem.at[k + 1],
            recv_sem=self.recv_sem.at[self.mine],
            device_id=(self.me, peer),
            device_id_type=MESH,
        )

    def keep(self):
        return pltpu.make_async_copy(
            self.source.at[self.mine], self.target.at[self.mine], self.send_sem.at[0]
        )

    def start(self):
        for k in range(len(self.partners)):
            self.copy(k).start()
        self.keep().start()

    def finish(self):
        self.keep().wait()
        for k, peer in enumerate(self.partners):
            there = self.target.at[peer]
            pltpu.make_async_copy(there, there, self.recv_sem.at[peer]).wait()
            self.copy(k).wait_send()


def trade_semaphores(owner_count):
    return [pltpu.SemaphoreType.DMA((owner_count,)), pltpu.SemaphoreType.DMA((owner_count,))]


def expert_gather_kernel(
    dp_count, rows_ref, grads_ref, down_ref, gate_up_ref, rows_out, grads_out, full_ref, up_ref, *sems
):
    half = up_ref.shape[1] // 2
    lines = [LineGather(down_ref.at[0], full_ref, dp_count, *sems[:3])]
    for n in range(2):
        columns = slice(n * half, n * half + half)
        shard = gate_up_ref.at[0, :, (2 + n) * half : (3 + n) * half]
        lines.append(LineGather(shard, up_ref, dp_count, *sems[3 * n + 3 : 3 * n + 6], columns))
    trades = [Trade(rows_ref.at[0], rows_out, *sems[9:11]), Trade(grads_ref.at[0], grads_out, *sems[11:13])]
    greet(lines[0].peers() + trades[0].peers())
    for part in lines + trades:
        part.start()
    for hop in range(1, lines[0].outer_count):
        for line in lines:
            line.relay(hop)
    for part in lines + trades:
        part.finish()


def expert_gather(rows, grads, down, gate_up, dp_count, collective):
    anywhere = pl.BlockSpec(memory_space=pl.ANY)
    return pl.pallas_call(
        functools.partial(expert_gather_kernel, dp_count),
        out_shape=[
            jax.ShapeDtypeStruct(rows.shape[1:], rows.dtype),
            jax.ShapeDtypeStruct(grads.shape[1:], grads.dtype),
            jax.ShapeDtypeStruct((dp_count * down.shape[1], down.shape[2]), down.dtype),
            jax.ShapeDtypeStruct((dp_count * gate_up.shape[1], gate_up.shape[2] // 2), gate_up.dtype),
        ],
        in_specs=[anywhere] * 4,
        out_specs=[anywhere] * 4,
        scratch_shapes=gather_semaphores(dp_count) * 3 + trade_semaphores(rows.shape[1]) * 2,
        compiler_params=pltpu.CompilerParams(collective_id=collective, has_side_effects=True),
        name="expert_gather",
    )(rows, grads, down, gate_up)


def small_gather_kernel(
    dp_count, expert_count, shard_ref, routes_ref, docs_ref, resid_ref,
    full_ref, columns_ref, rows_ref, table_ref, pass_sem, mate_sem, all_sem, stack_ref, *sems,
):
    me, mine = place()
    rows, columns = shard_ref.shape
    half = columns // 2
    side = mine % 2
    mate = mine + 1 - 2 * side
    mate_columns = pl.ds(pl.multiple_of((1 - side) * half, 128), half)
    first = half // 256 * 128
    spans = [(0, first), (first, half - first)]

    def there(chunk, lanes):
        return full_ref.at[pl.ds(pl.multiple_of(chunk * rows, 8), rows), lanes]

    def columns_at(n, of):
        start, size = spans[n]
        return pl.ds(pl.multiple_of(of * half + start, 128), size)

    def pass_copy(n, chunk):
        here = there(chunk, columns_at(n, side))
        return pltpu.make_async_remote_copy(
            src_ref=here,
            dst_ref=here,
            send_sem=pass_sem.at[n, chunk],
            recv_sem=mate_sem.at[n, chunk],
            device_id=(me, mate),
            device_id_type=MESH,
        )

    lines = []
    for n in range(2):
        lines.append(
            LineGather(
                shard_ref.at[:, columns_at(n, side)], full_ref, dp_count, *sems[3 * n : 3 * n + 3],
                columns_at(n, side), lambda chunk, n=n: pass_copy(n, chunk).start(),
            )
        )
    greet(lines[0].peers() + [(me, mate)])
    for line in lines:
        line.start()
    other = pltpu.make_async_copy(shard_ref.at[:, mate_columns], there(me, mate_columns), all_sem)
    other.start()
    stack_ref[...] = jnp.zeros_like(stack_ref)
    stack_ref[0 : resid_ref.shape[0], :] = resid_ref[...].astype(jnp.float32)
    stack_ref[16:18, :] = routes_ref[...].astype(jnp.float32)
    stack_ref[18:19, :] = docs_ref[...].astype(jnp.float32)
    table_ref[...] = jnp.transpose(stack_ref[...])
    routing_kernel(expert_count, table_ref, columns_ref, rows_ref)
    for hop in range(1, lines[0].outer_count):
        for line in lines:
            line.relay(hop)
    for line in lines:
        line.finish()
    other.wait()
    for k in range(1, dp_count):
        chunk = lax.rem(me + k, dp_count)
        for n in range(2):
            target = there(chunk, columns_at(n, 1 - side))
            pltpu.make_async_copy(target, target, mate_sem.at[n, chunk]).wait()
            pass_copy(n, chunk).wait_send()


def small_gather(shard, routes, docs, resid, expert_count, dp_count, collective):
    rows, columns = shard.shape
    tokens = routes.shape[1]
    anywhere, in_vmem = pl.BlockSpec(memory_space=pl.ANY), pl.BlockSpec(memory_space=pltpu.VMEM)
    return pl.pallas_call(
        functools.partial(small_gather_kernel, dp_count, expert_count),
        out_shape=[
            jax.ShapeDtypeStruct((dp_count * rows, columns), shard.dtype),
            jax.ShapeDtypeStruct((tokens, 128), jnp.int32),
            jax.ShapeDtypeStruct((8, tokens), jnp.int32),
            jax.ShapeDtypeStruct((tokens, 128), jnp.float32),
        ],
        in_specs=[anywhere] + [in_vmem] * 3,
        out_specs=[anywhere] + [in_vmem] * 3,
        scratch_shapes=[
            pltpu.SemaphoreType.DMA((2, dp_count)),
            pltpu.SemaphoreType.DMA((2, dp_count)),
            pltpu.SemaphoreType.DMA,
            pltpu.VMEM((128, tokens), jnp.float32),
        ]
        + gather_semaphores(dp_count) * 2,
        compiler_params=pltpu.CompilerParams(
            collective_id=collective, has_side_effects=True, vmem_limit_bytes=60 * 2**20
        ),
        name="small_gather",
    )(shard, routes, docs, resid)


class LineReduce:
    def __init__(self, sources, totals, owns, ins, lows, highs, own_sem, in_send, in_recv, line_send, line_recv):
        self.sources, self.totals = sources, totals
        self.owns, self.ins, self.lows, self.highs = owns, ins, lows, highs
        self.own_sem, self.in_send, self.in_recv = own_sem, in_send, in_recv
        self.line_send, self.line_recv = line_send, line_recv
        self.me, self.mine = place()
        self.outer, self.inner = self.me // 2, self.me % 2
        self.every = range(len(sources))

    def peers(self):
        low, high = lax.rem(self.outer + 3, 4), lax.rem(self.outer + 1, 4)
        return [
            (self.me + 1 - 2 * self.inner, self.mine),
            (low * 2 + self.inner, self.mine),
            (high * 2 + self.inner, self.mine),
        ]

    def order(self, o):
        return sorted(range(4), key=lambda plane: (-abs(plane - o), plane))

    def chunk(self, p, at):
        source = self.sources[p]
        rows = self.owns[p].shape[-2]
        here = pl.ds(pl.multiple_of(at * rows, 16), rows)
        return source.at[:, here, :] if len(source.shape) == 3 else source.at[here, :]

    def own_copy(self, p, plane):
        return pltpu.make_async_copy(
            self.chunk(p, plane * 2 + self.inner), self.owns[p].at[plane], self.own_sem.at[p, plane]
        )

    def in_copy(self, p, plane):
        return pltpu.make_async_remote_copy(
            src_ref=self.chunk(p, plane * 2 + 1 - self.inner),
            dst_ref=self.ins[p].at[plane],
            send_sem=self.in_send.at[p, plane],
            recv_sem=self.in_recv.at[p, plane],
            device_id=(self.me + 1 - 2 * self.inner, self.mine),
            device_id_type=MESH,
        )

    def line_copy(self, p, plane, upward, device_plane):
        target = self.lows[p].at[plane - 1] if upward else self.highs[p].at[plane]
        return pltpu.make_async_remote_copy(
            src_ref=self.ins[p].at[plane],
            dst_ref=target,
            send_sem=self.line_send.at[p, 0 if upward else 1, plane],
            recv_sem=self.line_recv.at[p, 0 if upward else 1, plane],
            device_id=(device_plane * 2 + self.inner, self.mine),
            device_id_type=MESH,
        )

    def start(self, o):
        for plane in self.order(o):
            for p in self.every:
                self.in_copy(p, plane).start()
        for plane in self.order(o):
            for p in self.every:
                self.own_copy(p, plane).start()

    def line_start(self, o, p, plane):
        return self.line_copy(p, plane, plane > o, o + 1 if plane > o else o - 1)

    def pass_on(self, o, k):
        plane = self.order(o)[k]
        for p in self.every:
            self.own_copy(p, plane).wait()
            self.in_copy(p, plane).wait_recv()
            terms = [self.owns[p].at[plane]]
            if o > 0 and plane >= o:
                self.line_copy(p, plane, True, o).wait_recv()
                terms.append(self.lows[p].at[plane - 1])
            if o < 3 and plane <= o:
                self.line_copy(p, plane, False, o).wait_recv()
                terms.append(self.highs[p].at[plane])
            held = self.ins[p].at[plane]
            last = plane == o
            sides = held.shape[0] if len(held.shape) == 3 else 0

            def body(at, p=p, terms=terms, held=held, last=last, sides=sides):
                here = pl.ds(pl.multiple_of(at, 16), 16)
                for side in range(max(1, sides)):
                    spot = (side, here) if sides else (here,)
                    total = held[spot].astype(jnp.float32)
                    for term in terms:
                        total = total + term[spot].astype(jnp.float32)
                    if last:
                        size = total.shape[-1]
                        self.totals[p][here, side * size : (side + 1) * size] = total
                    else:
                        held[spot] = total.astype(held.dtype)

            by_rows(held.shape[-2], body)
            if not last:
                self.line_start(o, p, plane).start()

    def finish(self, o):
        for plane in range(4):
            for p in self.every:
                self.in_copy(p, plane).wait_send()
                if plane != o:
                    self.line_start(o, p, plane).wait_send()

    def each_plane(self, body):
        for o in range(4):
            pl.when(self.outer == o)(functools.partial(body, o))

    def turns(self, ends, middles):
        def body(o):
            for k in ends if o in (0, 3) else middles:
                self.pass_on(o, k)

        self.each_plane(body)


def pieces_of(source, cut, sides=None):
    columns = source.shape[-1]
    size = columns // cut
    fronts = [()]
    if len(source.shape) == 3:
        fronts = [(side,) for side in (range(source.shape[0]) if sides is None else sides)]
    return [
        (front, slice(c * size, c * size + size), slice(n * columns + c * size, n * columns + c * size + size))
        for n, front in enumerate(fronts)
        for c in range(cut)
    ]


def reduce_scratch(source, cut, sides=None):
    rows = source.shape[-2] // 8
    size = source.shape[-1] // cut
    count = len(pieces_of(source, cut, sides))
    shapes = []
    for planes in (4, 4, 3, 3):
        shapes += [pltpu.VMEM((planes, rows, size), jnp.bfloat16)] * count
    return shapes + [
        pltpu.SemaphoreType.DMA((count, 4)),
        pltpu.SemaphoreType.DMA((count, 4)),
        pltpu.SemaphoreType.DMA((count, 4)),
        pltpu.SemaphoreType.DMA((count, 2, 4)),
        pltpu.SemaphoreType.DMA((count, 2, 4)),
    ]


def line_reduce(source, total, scratch, cut, sides=None):
    pieces = pieces_of(source, cut, sides)
    count = len(pieces)
    buffers = [scratch[n * count : (n + 1) * count] for n in range(4)]
    sources = [source.at[front + (slice(None), columns)] for front, columns, _ in pieces]
    totals = [total.at[:, columns] for _, _, columns in pieces]
    return LineReduce(sources, totals, *buffers, *scratch[4 * count :])


def final_reduce_kernel(small_count, *refs):
    small_refs, refs = refs[:small_count], refs[small_count:]
    (
        small_out, swap, small_own, small_in, small_low, small_high, final_low, final_in, own_sem,
        swap_send, swap_recv, in_send, in_recv, line_send, line_recv, last_send, last_recv,
    ) = refs
    outer_count, inner_count = 4, 2
    me, mine = place()
    outer, inner = me // inner_count, me % inner_count
    side = mine % 2
    mate, across = mine + 1 - 2 * side, lax.rem(mine + 2, 4)
    beside = me + 1 - 2 * inner
    half_rows = small_refs[0].shape[1] // 2
    starts = [sum(ref.shape[2] for ref in small_refs[:n]) for n in range(small_count + 1)]

    def remote(source, target, device, send_at, recv_at):
        return pltpu.make_async_remote_copy(
            src_ref=source,
            dst_ref=target,
            send_sem=send_at,
            recv_sem=recv_at,
            device_id=device,
            device_id_type=MESH,
        )

    low_peer = lax.rem(outer + outer_count - 1, outer_count) * inner_count + inner
    high_peer = lax.rem(outer + 1, outer_count) * inner_count + inner
    greet([(me, mate), (me, across), (beside, mine), (low_peer, mine), (high_peer, mine)])

    mate_rows = pl.ds(pl.multiple_of((1 - side) * half_rows, 16), half_rows)
    own_rows = pl.ds(pl.multiple_of(side * half_rows, 16), half_rows)

    middle = starts[-1] // 256 * 128
    spans = [slice(0, middle), slice(middle, starts[-1])]

    def swap_copy(n):
        return remote(
            small_refs[n].at[:, mate_rows, :],
            swap.at[:, :, starts[n] : starts[n + 1]],
            (me, mate),
            swap_send.at[n],
            swap_recv.at[n],
        )

    def own_copy(n):
        return pltpu.make_async_copy(
            small_refs[n].at[:, own_rows, :], small_own.at[:, :, starts[n] : starts[n + 1]], own_sem.at[n]
        )

    def inner_copy(p, plane):
        return remote(
            swap.at[plane * inner_count + 1 - inner, :, spans[p]],
            small_in.at[plane, :, spans[p]],
            (beside, mine),
            in_send.at[p, plane],
            in_recv.at[p, plane],
        )

    def line_copy(p, plane, upward, device_plane):
        way = 0 if upward else 1
        return remote(
            small_in.at[plane, :, spans[p]],
            (small_low if upward else small_high).at[plane, :, spans[p]],
            (device_plane * inner_count + inner, mine),
            line_send.at[p, way, plane],
            line_recv.at[p, way, plane],
        )

    def last_copy(p):
        return remote(
            final_low.at[:, spans[p]], final_in.at[:, spans[p]], (me, across), last_send.at[p], last_recv.at[p]
        )

    def wide(values):
        return values.astype(jnp.float32)

    def add_own(chunk, lanes):
        def body(at):
            here = pl.ds(pl.multiple_of(at, 16), 16)
            swap[chunk, here, lanes] = (
                wide(swap[chunk, here, lanes]) + wide(small_own[chunk, here, lanes])
            ).astype(swap.dtype)

        by_rows(half_rows, body)

    def at_plane(o):
        order = sorted(range(outer_count), key=lambda t: (-abs(t - o), t))

        def line_start(p, plane):
            return line_copy(p, plane, plane > o, o + 1 if plane > o else o - 1)

        for n in range(small_count):
            swap_copy(n).start()
            own_copy(n).start()
        for n in range(small_count):
            swap_copy(n).wait_recv()
            own_copy(n).wait()
        for plane in order:
            for p in range(2):
                add_own(plane * inner_count + 1 - inner, spans[p])
                inner_copy(p, plane).start()
        for plane in order:
            for p in range(2):
                add_own(plane * inner_count + inner, spans[p])
                inner_copy(p, plane).wait_recv()
                terms = [swap.at[plane * inner_count + inner]]
                if o > 0 and plane >= o:
                    line_copy(p, plane, True, o).wait_recv()
                    terms.append(small_low.at[plane])
                if o < outer_count - 1 and plane <= o:
                    line_copy(p, plane, False, o).wait_recv()
                    terms.append(small_high.at[plane])
                target = final_low if plane == o else small_in.at[plane]

                def gather(at, plane=plane, terms=terms, target=target, lanes=spans[p]):
                    here = pl.ds(pl.multiple_of(at, 16), 16)
                    total = wide(small_in[plane, here, lanes])
                    for term in terms:
                        total = total + wide(term[here, lanes])
                    target[here, lanes] = total.astype(target.dtype)

                by_rows(half_rows, gather)
                if plane != o:
                    line_start(p, plane).start()
                else:
                    last_copy(p).start()
        for plane in range(outer_count):
            for p in range(2):
                inner_copy(p, plane).wait_send()
                if plane != o:
                    line_start(p, plane).wait_send()
        for n in range(small_count):
            swap_copy(n).wait_send()

    for o in range(outer_count):
        pl.when(outer == o)(functools.partial(at_plane, o))
    for p in range(2):
        last_copy(p).wait()

    def total_body(at):
        here = pl.ds(pl.multiple_of(at, 16), 16)
        there = pl.ds(pl.multiple_of(side * half_rows + at, 16), 16)
        small_out[there, :] = wide(final_low[here, :]) + wide(final_in[here, :])

    by_rows(half_rows, total_body)
    mate_copy = remote(
        small_out.at[own_rows, :], small_out.at[own_rows, :], (me, mate), last_send.at[2], last_recv.at[2]
    )
    mate_copy.start()
    mate_copy.wait()


def final_reduce(smalls, collective):
    chunk_count, small_rows, _ = smalls[0].shape
    small_columns = sum(small.shape[2] for small in smalls)
    low = jnp.bfloat16
    planes = 4
    in_vmem = pl.BlockSpec(memory_space=pltpu.VMEM)
    half = small_rows // 2
    return pl.pallas_call(
        functools.partial(final_reduce_kernel, len(smalls)),
        out_shape=jax.ShapeDtypeStruct((small_rows, small_columns), jnp.float32),
        in_specs=[pl.BlockSpec(memory_space=pl.ANY)] * len(smalls),
        out_specs=in_vmem,
        scratch_shapes=[pltpu.VMEM((chunk_count, half, small_columns), low)] * 2
        + [pltpu.VMEM((planes, half, small_columns), low)] * 3
        + [pltpu.VMEM((half, small_columns), low)] * 2
        + [
            pltpu.SemaphoreType.DMA((len(smalls),)),
            pltpu.SemaphoreType.DMA((len(smalls),)),
            pltpu.SemaphoreType.DMA((len(smalls),)),
            pltpu.SemaphoreType.DMA((2, planes)),
            pltpu.SemaphoreType.DMA((2, planes)),
            pltpu.SemaphoreType.DMA((2, 2, planes)),
            pltpu.SemaphoreType.DMA((2, 2, planes)),
            pltpu.SemaphoreType.DMA((3,)),
            pltpu.SemaphoreType.DMA((3,)),
        ],
        compiler_params=pltpu.CompilerParams(
            collective_id=collective, has_side_effects=True, vmem_limit_bytes=60 * 2**20
        ),
        name="final_reduce",
    )(*smalls)


def shards(
    tokens,
    resid_logits,
    routes,
    doc_ids,
    w_qkv,
    w_out,
    gain_attn,
    gain_ffn,
    w_router,
    w_const,
    v_const,
    w_gate_up,
    w_down,
    out_grad,
):
    dp_count, owner_count = lax.axis_size("dp"), lax.axis_size("expert")
    own_links = dp_count == 8 and owner_count == 4 and w_gate_up.shape[0] == 2
    seq_count, length, width = tokens.shape
    assert seq_count == 1
    rows = seq_count * length
    choice_count = resid_logits.shape[-1]
    local_count = w_gate_up.shape[0]
    expert_count = owner_count * local_count
    hidden_count = w_down.shape[1] * dp_count
    width_qkv, width_out = w_qkv.shape[1], w_out.shape[1]
    small_parts = [w_router, w_const, v_const, gain_attn[:, None], gain_ffn[:, None]]
    small_width = sum(part.shape[1] for part in small_parts)
    pad = jnp.zeros((w_qkv.shape[0], 256 - small_width), jnp.bfloat16)
    packed = jnp.concatenate([w_qkv, w_out] + small_parts + [pad], 1)
    inputs = tokens.reshape(rows, width)
    cot = out_grad.reshape(rows, width)
    route_rows = routes.reshape(rows, 2)
    cosine, sine = rotary_lanes(length, width // HEADS)
    docs_row = doc_ids.reshape(1, rows)
    resid_rows = resid_logits.reshape(rows, choice_count)
    if own_links:
        packed_full, spots, spot_rows, table = small_gather(
            packed, route_rows.T, docs_row, resid_rows.T, expert_count, dp_count, 1
        )
    else:
        columns = [
            resid_rows, jnp.zeros((rows, 16 - choice_count)), route_rows, docs_row.T, jnp.zeros((rows, 109))
        ]
        table = jnp.concatenate([column.astype(jnp.float32) for column in columns], 1)
        spots, spot_rows = routing(table, expert_count)
        packed_full = lax.all_gather(packed, "dp", axis=0, tiled=True)
    gather = functools.partial(lax.all_gather, axis_name="dp", axis=0, tiled=True)
    if own_links:
        first_gate, second_down, packed_full = lax.optimization_barrier(
            (w_gate_up[0, :, :hidden_count], w_down[1], packed_full)
        )
        first_gate, second_down = gather(first_gate), gather(second_down)
    else:
        first_gate_up = gather(w_gate_up[0])
    normed_one, queries, keys, values, attended, middle, normed_two, aux = attention_forward(
        inputs, packed_full, docs_row, cosine, sine, table
    )
    send_rows, send_grads = dispatch(spot_rows, aux, normed_two, cot, owner_count, local_count)
    if own_links:
        rows_in, grads_in, first_down, first_up = expert_gather(
            send_rows, send_grads, w_down, w_gate_up, dp_count, 2
        )
        grad_gu, grad_down, both, next_rows, next_grads, second_gate_up = experts(
            rows_in, grads_in, first_gate, first_up, first_down, 1, dp_count,
            [send_rows, send_grads, w_gate_up], 6,
        )
        down_parts = [lax.psum_scatter(grad_down, "dp", scatter_dimension=0, tiled=True)]
        second_gu, grad_down, *parts, gu_part = experts(
            next_rows, next_grads, second_gate_up, second_gate_up, second_down, 2, dp_count,
            [both, grad_gu], 4,
        )
        down_parts.append(lax.psum_scatter(grad_down, "dp", scatter_dimension=0, tiled=True))
        gu_parts = [gu_part]
    else:
        exchange = functools.partial(
            lax.all_to_all, axis_name="expert", split_axis=0, concat_axis=0, tiled=True
        )
        parts, gu_parts, down_parts = [], [], []
        for e in range(local_count):
            gate_up = first_gate_up if e == 0 else gather(w_gate_up[e])
            grad_gu, grad_down, both = experts(
                exchange(send_rows[e]), exchange(send_grads[e]), gate_up, gate_up, gather(w_down[e])
            )
            parts.append(exchange(both))
            gu_part = lax.psum_scatter(grad_gu, "dp", scatter_dimension=1, tiled=True)
            gu_parts.append(jnp.concatenate([gu_part[0], gu_part[1]], -1).astype(jnp.float32))
            down_parts.append(lax.psum_scatter(grad_down, "dp", scatter_dimension=0, tiled=True))
    down_parts = [part.astype(jnp.float32) for part in down_parts]
    output, logit_grad, grad_middle, small_grad = combine(
        parts, spots, table, aux, normed_two, middle, cot, packed_full, choice_count, expert_count
    )
    if own_links:
        grad_middle, down_parts[0] = lax.optimization_barrier((grad_middle, down_parts[0]))
    backward = functools.partial(
        attention_backward, grad_middle, queries, keys, values, attended, normed_one, inputs,
        packed_full, docs_row, table, cosine, sine, small_grad,
    )
    if own_links:
        token_grad, *weight_grads, gu_part = backward([second_gu], 7)
        gu_parts.append(gu_part)
        packed_part = final_reduce(
            [grad.reshape(dp_count, width // dp_count, grad.shape[1]) for grad in weight_grads], 3
        )
    else:
        token_grad, *weight_grads = backward()
        packed_part = lax.psum_scatter(
            jnp.concatenate(weight_grads, 1), "dp", scatter_dimension=0, tiled=True
        )
        packed_part = lax.psum(packed_part, "expert").astype(jnp.float32)
    part_qkv = packed_part[:, :width_qkv]
    part_out = packed_part[:, width_qkv : width_qkv + width_out]
    small_part = packed_part[:, width_qkv + width_out :]
    return (
        output.reshape(tokens.shape),
        token_grad.reshape(tokens.shape),
        logit_grad.reshape(resid_logits.shape),
        part_qkv,
        part_out,
        small_part[:, 18],
        small_part[:, 19],
        small_part[:, 0:12],
        small_part[:, 12:16],
        small_part[:, 16:18],
        jnp.stack(gu_parts),
        jnp.stack(down_parts),
    )


def solution(mesh):
    placed = (
        P(("dp", "expert"), None, None),
        P(("dp", "expert"), None, None),
        P(("dp", "expert"), None, None),
        P(("dp", "expert"), None),
        P("dp", None),
        P("dp", None),
        P("dp"),
        P("dp"),
        P("dp", None),
        P("dp", None),
        P("dp", None),
        P("expert", "dp", None),
        P("expert", "dp", None),
        P(("dp", "expert"), None, None),
    )
    return jax.shard_map(
        shards,
        mesh=mesh,
        in_specs=placed,
        out_specs=(
            P(("dp", "expert"), None, None),
            P(("dp", "expert"), None, None),
            P(("dp", "expert"), None, None),
            P("dp", None),
            P("dp", None),
            P("dp"),
            P("dp"),
            P("dp", None),
            P("dp", None),
            P("dp", None),
            P("expert", "dp", None),
            P("expert", "dp", None),
        ),
        check_vma=False,
    )
```

```python
import functools

import jax
import jax.numpy as jnp
import numpy as np
from jax import lax
from jax.experimental import pallas as pl
from jax.experimental.pallas import tpu as pltpu
from jax.sharding import PartitionSpec as P

HEADS = 12
BLOCK = 256
CAP = 256
GROUP = 256
FF_BLOCK = 512
MESH = pl.DeviceIdType.MESH
epsilon = 1e-06


def rotary_lanes(length, head_dim):
    half_dim = head_dim // 2
    frequency = (10000.0 ** (-np.arange(half_dim, dtype=np.float32) / half_dim)).astype(np.float32)
    angles = (np.arange(length, dtype=np.float32)[:, None] * frequency[None, :]).astype(np.float64)
    cosine = np.cos(angles).astype(np.float32)
    sine = np.sin(angles).astype(np.float32)
    return (
        np.concatenate([cosine] * 4, 1),
        np.concatenate([-sine, sine, -sine, sine], 1),
    )


def nt(left, right):
    return lax.dot_general(left, right, (((1,), (1,)), ((), ())), preferred_element_type=jnp.float32)


def tn(left, right):
    return lax.dot_general(left, right, (((0,), (0,)), ((), ())), preferred_element_type=jnp.float32)


def nn(left, right):
    return jnp.dot(left, right, preferred_element_type=jnp.float32)


def lane_ids(shape):
    return lax.broadcasted_iota(jnp.int32, shape, len(shape) - 1)


def turn(values, cosine, sine):
    lanes = lane_ids(values.shape)
    ahead, behind = pltpu.roll(values, 96, 1), pltpu.roll(values, 32, 1)
    return values * cosine + jnp.where(lanes % 64 < 32, ahead, behind) * sine


def key_span(i):
    return max(0, i - 2) * BLOCK, (i + 1) * BLOCK


def mask_of(docs_column, docs_row, i):
    low, high = key_span(i)
    return docs_column[low:high, :] == docs_row[:, i * BLOCK : (i + 1) * BLOCK]


def attention_forward_kernel(linked, *refs):
    (
        tokens_ref, wq_ref, wk_ref, wv_ref, wo_ref, small_ref, docs_row_ref,
        cosine_ref, sine_ref, table_ref,
    ) = refs[:10]
    (
        normed_ref, q_ref, k_ref, v_ref, attended_ref, middle_ref, normed_two_ref, aux_ref,
    ) = refs[10 + bool(linked) : 18 + bool(linked)]
    step = pl.program_id(0)
    rows = tokens_ref.shape[0]
    if linked:
        branch_ref = refs[20]
        line = LineGather(refs[10].at[0], refs[19], linked, *refs[21:])

        @pl.when(step == 0)
        def _():
            greet(line.peers())
            line.start()

        @pl.when(step == 2)
        def _():
            line.relay(1)
    else:
        branch_ref = refs[18]

    @pl.when(step == 0)
    def _():
        inputs = tokens_ref[...].astype(jnp.float32)
        gains = jnp.transpose(small_ref[:, :128].astype(jnp.float32))[18:19, :]
        scale = lax.rsqrt(jnp.mean(inputs * inputs, -1, keepdims=True) + epsilon)
        normed_ref[...] = (inputs * scale * gains).astype(jnp.bfloat16)
        branch_ref[...] = jnp.zeros_like(branch_ref)

    normed = normed_ref[...]
    cosine, sine = cosine_ref[...], sine_ref[...]
    for w_ref, out_ref, turned in ((wq_ref, q_ref, True), (wk_ref, k_ref, True), (wv_ref, v_ref, False)):
        projected = nn(normed, w_ref[...])
        for half in range(2):
            part = projected[:, half * 128 : half * 128 + 128]
            if turned:
                part = turn(part, cosine, sine)
            out_ref[:, half * 128 : half * 128 + 128] = part.astype(jnp.bfloat16)

    docs_row, docs_column = docs_row_ref[...], table_ref[:, 18:19].astype(jnp.int32)
    for i in range(rows // BLOCK):
        low, high = key_span(i)
        here = slice(i * BLOCK, (i + 1) * BLOCK)
        allowed = mask_of(docs_column, docs_row, i)
        for pair in range(2):
            lanes = slice(pair * 128, pair * 128 + 128)
            queries = q_ref[here, lanes] * jnp.asarray(0.125, jnp.bfloat16)
            keys, values = k_ref[low:high, lanes], v_ref[low:high, lanes]
            left = lane_ids(queries.shape) < 64
            outs = []
            for head in range(2):
                own = left if head == 0 else jnp.logical_not(left)
                scores = nt(keys, jnp.where(own, queries, jnp.zeros_like(queries)))
                scores = jnp.where(allowed, scores, -1e30)
                shifted = jnp.exp(scores - jnp.max(scores, 0, keepdims=True))
                probs = shifted * (1.0 / jnp.sum(shifted, 0, keepdims=True))
                outs.append(tn(probs.astype(jnp.bfloat16), values))
            attended_ref[here, lanes] = jnp.where(left, outs[0], outs[1]).astype(jnp.bfloat16)
    branch_ref[...] += nn(attended_ref[...], wo_ref[...])

    @pl.when(step == pl.num_programs(0) - 1)
    def _():
        small = small_ref[:, :128]
        gains = jnp.transpose(small.astype(jnp.float32))[19:20, :]
        middle = tokens_ref[...].astype(jnp.float32) + branch_ref[...]
        middle_ref[...] = middle
        scale = lax.rsqrt(jnp.mean(middle * middle, -1, keepdims=True) + epsilon)
        normed_two = (middle * scale * gains).astype(jnp.bfloat16)
        normed_two_ref[...] = normed_two
        logits = nn(normed_two, small) + table_ref[...]
        lanes = lane_ids(logits.shape)

        def lane(at):
            return jnp.sum(jnp.where(lanes == at, logits, 0.0), -1, keepdims=True)

        def two(first, second):
            peak = jnp.maximum(first, second)
            first, second = jnp.exp(first - peak), jnp.exp(second - peak)
            return first / (first + second), second / (first + second)

        columns = list(two(*[lane(table_ref[:, 16 + s : 17 + s].astype(jnp.int32)) for s in range(2)]))
        columns += list(two(lane(12), lane(13))) + list(two(lane(14), lane(15)))
        columns.append(scale)
        aux = jnp.zeros_like(logits)
        for at, column in enumerate(columns):
            aux = jnp.where(lanes == at, column, aux)
        aux_ref[...] = aux
        if linked:
            line.relay(2)
            line.relay(3)
            line.finish()


def attention_forward(
    tokens, packed, docs_row, cosine, sine, table, shards=None,
    dp_count=None, collective=None,
):
    rows, width = tokens.shape
    groups = width // GROUP
    low = jnp.bfloat16
    whole = lambda shape: pl.BlockSpec(shape, lambda j: (0, 0))
    column = lambda at: pl.BlockSpec((width, GROUP), lambda j: (0, at + j))
    out_column = pl.BlockSpec((rows, GROUP), lambda j: (0, j))
    full = jax.ShapeDtypeStruct((rows, width), low)
    linked = shards is not None
    anywhere = pl.BlockSpec(memory_space=pl.ANY)
    links = {"collective_id": collective, "has_side_effects": True} if linked else {}
    gathered = []
    if linked:
        gathered = [jax.ShapeDtypeStruct((dp_count * shards.shape[1], shards.shape[2]), low)]
    return pl.pallas_call(
        functools.partial(attention_forward_kernel, dp_count if linked else 0),
        grid=(groups,),
        out_shape=[full] * 5
        + [
            jax.ShapeDtypeStruct((rows, width), jnp.float32),
            full,
            jax.ShapeDtypeStruct((rows, 128), jnp.float32),
        ]
        + gathered,
        in_specs=[
            whole((rows, width)),
            column(0),
            column(groups),
            column(2 * groups),
            pl.BlockSpec((GROUP, width), lambda j: (j, 3)),
            pl.BlockSpec((width, 256), lambda j: (0, 12)),
            whole((1, rows)),
            whole((rows, 128)),
            whole((rows, 128)),
            whole((rows, 128)),
        ]
        + [anywhere] * linked,
        out_specs=[whole((rows, width))]
        + [out_column] * 4
        + [whole((rows, width)), whole((rows, width)), whole((rows, 128))]
        + [anywhere] * linked,
        scratch_shapes=[pltpu.VMEM((rows, width), jnp.float32)]
        + (gather_semaphores(dp_count) if linked else []),
        compiler_params=pltpu.CompilerParams(
            dimension_semantics=("arbitrary",), vmem_limit_bytes=56 * 2**20, **links
        ),
        cost_estimate=pl.CostEstimate(
            flops=2 * rows * width * 4 * width + 8 * rows * rows * width // 2,
            bytes_accessed=24 * rows * width,
            transcendentals=rows * rows * HEADS // 2,
        ),
        name="attention_forward",
    )(
        tokens, packed, packed, packed, packed, packed, docs_row, cosine, sine, table,
        *([shards] if linked else []),
    )


def attention_backward_kernel(count, *refs):
    (
        grad_middle_ref, q_ref, k_ref, v_ref, attended_ref, normed_ref, tokens_ref,
        wq_ref, wk_ref, wv_ref, wo_ref, small_ref, docs_row_ref, table_ref,
        cosine_ref, sine_ref, small_grad_ref,
    ) = refs[:17]
    sources, refs = refs[17 : 17 + count], refs[17 + count :]
    token_grad_ref, gq_ref, gk_ref, gv_ref, go_ref, small_out_ref = refs[:6]
    totals, refs = refs[6 : 6 + count], refs[6 + count :]
    branch_ref, back_ref, turned_ref, key_acc, value_acc, query_acc = refs[:6]
    step = pl.program_id(0)
    rows, width = tokens_ref.shape
    if count:
        line = line_reduce(sources[0], totals[0], refs[6:], 2)

        @pl.when(step == 0)
        def _():
            greet(line.peers())
            line.each_plane(line.start)

        pl.when(step == 1)(lambda: line.turns([0], []))
        pl.when(step == 2)(lambda: line.turns([1], [0]))

    @pl.when(step == 0)
    def _():
        branch_ref[...] = grad_middle_ref[...].astype(jnp.bfloat16)
        back_ref[...] = jnp.zeros_like(back_ref)

    grad_branch = branch_ref[...]
    grad_attended = nt(grad_branch, wo_ref[...]).astype(jnp.bfloat16)
    go_ref[...] = tn(attended_ref[...], grad_branch).astype(jnp.bfloat16)
    cosine, sine = cosine_ref[...], sine_ref[...]
    docs_row, docs_column = docs_row_ref[...], table_ref[:, 18:19].astype(jnp.int32)
    for pair in range(2):
        lanes = slice(pair * 128, pair * 128 + 128)
        key_acc[...] = jnp.zeros_like(key_acc)
        value_acc[...] = jnp.zeros_like(value_acc)
        for i in range(rows // BLOCK):
            low, high = key_span(i)
            here = slice(i * BLOCK, (i + 1) * BLOCK)
            allowed = mask_of(docs_column, docs_row, i)
            queries = q_ref[here, lanes] * jnp.asarray(0.125, jnp.bfloat16)
            grads = grad_attended[here, lanes]
            keys, values = k_ref[low:high, lanes], v_ref[low:high, lanes]
            left = lane_ids(queries.shape) < 64
            query_grads = []
            key_grad, value_grad = None, None
            for head in range(2):
                own = left if head == 0 else jnp.logical_not(left)
                own_queries = jnp.where(own, queries, jnp.zeros_like(queries))
                own_grads = jnp.where(own, grads, jnp.zeros_like(grads))
                scores = jnp.where(allowed, nt(keys, own_queries), -1e30)
                shifted = jnp.exp(scores - jnp.max(scores, 0, keepdims=True))
                probs = shifted * (1.0 / jnp.sum(shifted, 0, keepdims=True))
                grad_probs = nt(values, own_grads)
                inner = jnp.sum(probs * grad_probs, 0, keepdims=True)
                grad_scores = (probs * (grad_probs - inner)).astype(jnp.bfloat16)
                part_value = nn(probs.astype(jnp.bfloat16), own_grads)
                part_key = nn(grad_scores, own_queries)
                value_grad = part_value if head == 0 else value_grad + part_value
                key_grad = part_key if head == 0 else key_grad + part_key
                query_grads.append(tn(grad_scores, keys))
            value_acc[low:high, :] += value_grad
            key_acc[low:high, :] += key_grad
            query_acc[here, :] = jnp.where(left, query_grads[0], query_grads[1]) * 0.125
        turned_ref[0, :, lanes] = turn(query_acc[...], cosine, -sine).astype(jnp.bfloat16)
        turned_ref[1, :, lanes] = turn(key_acc[...], cosine, -sine).astype(jnp.bfloat16)
        turned_ref[2, :, lanes] = value_acc[...].astype(jnp.bfloat16)
    normed = normed_ref[...]
    for at, (w_ref, out_ref) in enumerate(((wq_ref, gq_ref), (wk_ref, gk_ref), (wv_ref, gv_ref))):
        turned = turned_ref[at]
        out_ref[...] = tn(normed, turned).astype(jnp.bfloat16)
        back_ref[...] += nt(turned, w_ref[...])

    @pl.when(step == pl.num_programs(0) - 1)
    def _():
        gains = jnp.transpose(small_ref[:, :128].astype(jnp.float32))[18:19, :]
        inputs = tokens_ref[...].astype(jnp.float32)
        grads = back_ref[...]
        scale = lax.rsqrt(jnp.mean(inputs * inputs, -1, keepdims=True) + epsilon)
        weighted = grads * gains
        mean = jnp.mean(weighted * inputs, -1, keepdims=True)
        grad_inputs = scale * weighted - inputs * (scale * scale * scale * mean)
        token_grad_ref[...] = (grad_inputs + grad_middle_ref[...]).astype(jnp.bfloat16)
        gain_grad = jnp.sum(grads * inputs * scale, 0, keepdims=True)
        column = jnp.transpose(jnp.broadcast_to(gain_grad, (128, width)))
        small_grad = small_grad_ref[...]
        small_grad = jnp.where(lane_ids(small_grad.shape) == 18, column, small_grad)
        small_out_ref[...] = small_grad.astype(jnp.bfloat16)
        if count:
            line.turns([2, 3], [1, 2, 3])
            line.each_plane(line.finish)


def attention_backward(
    grad_middle, queries, keys, values, attended, normed, tokens, packed, docs_row, table,
    cosine, sine, small_grad, sources=(), collective=None,
):
    rows, width = tokens.shape
    groups = width // GROUP
    low = jnp.bfloat16
    whole = lambda shape: pl.BlockSpec(shape, lambda j: (0, 0))
    column = lambda at: pl.BlockSpec((width, GROUP), lambda j: (0, at + j))
    by_group = pl.BlockSpec((rows, GROUP), lambda j: (0, j))
    weight = jax.ShapeDtypeStruct((width, width), low)
    linked = len(sources) > 0
    links = {"collective_id": collective, "has_side_effects": True} if linked else {}
    sums = []
    for source in sources:
        sums.append((source.shape[-2] // 8, source.shape[0] * source.shape[-1]))
    once = lambda shape: pl.BlockSpec(
        shape, lambda j: (0, 0), pipeline_mode=pl.Buffered(1)
    )
    return pl.pallas_call(
        functools.partial(attention_backward_kernel, len(sources)),
        grid=(groups,),
        out_shape=[jax.ShapeDtypeStruct((rows, width), low)]
        + [weight] * 4
        + [jax.ShapeDtypeStruct((width, 128), low)]
        + [jax.ShapeDtypeStruct(shape, jnp.float32) for shape in sums],
        in_specs=[
            once((rows, width)),
            by_group,
            by_group,
            by_group,
            by_group,
            once((rows, width)),
            once((rows, width)),
            column(0),
            column(groups),
            column(2 * groups),
            pl.BlockSpec((GROUP, width), lambda j: (j, 3)),
            pl.BlockSpec((width, 256), lambda j: (0, 12)),
            once((1, rows)),
            once((rows, 128)),
            once((rows, 128)),
            once((rows, 128)),
            once((width, 128)),
        ]
        + [pl.BlockSpec(memory_space=pl.ANY)] * len(sources),
        out_specs=[
            whole((rows, width)),
            column(0),
            column(0),
            column(0),
            pl.BlockSpec((GROUP, width), lambda j: (j, 0)),
            whole((width, 128)),
        ]
        + [whole(shape) for shape in sums],
        scratch_shapes=[
            pltpu.VMEM((rows, width), low),
            pltpu.VMEM((rows, width), jnp.float32),
            pltpu.VMEM((3, rows, GROUP), low),
            pltpu.VMEM((rows, 128), jnp.float32),
            pltpu.VMEM((rows, 128), jnp.float32),
            pltpu.VMEM((rows, 128), jnp.float32),
        ]
        + (reduce_scratch(sources[0], 2) if linked else []),
        compiler_params=pltpu.CompilerParams(
            dimension_semantics=("arbitrary",), vmem_limit_bytes=61 * 2**20, **links
        ),
        cost_estimate=pl.CostEstimate(
            flops=4 * rows * width * 4 * width + 20 * rows * rows * width // 2,
            bytes_accessed=32 * rows * width,
            transcendentals=rows * rows * HEADS // 2,
        ),
        name="attention_backward",
    )(
        grad_middle, queries, keys, values, attended, normed, tokens, packed, packed, packed,
        packed, packed, docs_row, table, cosine, sine, small_grad, *sources,
    )


def routing_kernel(expert_count, table_ref, columns_ref, rows_ref):
    rows = table_ref.shape[0]
    lanes = lane_ids((rows, 128))
    routes = [table_ref[:, 16 + s : 17 + s].astype(jnp.int32) for s in range(2)]
    first = (lanes == routes[0]).astype(jnp.float32)
    second = (lanes == routes[1]).astype(jnp.float32)
    down = lax.broadcasted_iota(jnp.int32, (rows, rows), 0)
    lower = (down > lane_ids((rows, rows))).astype(jnp.bfloat16)
    before_first = nn(lower, first.astype(jnp.bfloat16))
    before_second = nn(lower, second.astype(jnp.bfloat16)) + jnp.sum(first, 0, keepdims=True)
    spots = []
    for picked, before, at in ((first, before_first, 0), (second, before_second, 1)):
        rank = jnp.sum(picked * before, -1, keepdims=True)
        route = routes[at]
        spot = route.astype(jnp.float32) * CAP + rank
        spots.append(jnp.where(route < expert_count, spot, jnp.full_like(spot, 2.0 * expert_count * CAP)))
    both = jnp.where(lanes == 0, spots[0], jnp.where(lanes == 1, spots[1], 0.0))
    columns_ref[...] = both.astype(jnp.int32)
    rows_ref[...] = jnp.transpose(both)[0:8, :].astype(jnp.int32)


def routing(table, expert_count):
    rows = table.shape[0]
    return pl.pallas_call(
        functools.partial(routing_kernel, expert_count),
        out_shape=[
            jax.ShapeDtypeStruct((rows, 128), jnp.int32),
            jax.ShapeDtypeStruct((8, rows), jnp.int32),
        ],
        compiler_params=pltpu.CompilerParams(vmem_limit_bytes=40 * 2**20),
        name="routing",
    )(table)


def dispatch_kernel(local_count, spots_ref, aux_ref, normed_ref, cot_ref, rows_ref, grads_ref, gates_ref):
    step = pl.program_id(0)

    @pl.when(step == 0)
    def _():
        gates_ref[...] = jnp.transpose(aux_ref[...])[0:8, :]

    owners, width = rows_ref.shape[0], rows_ref.shape[2]
    shape = (owners * CAP, normed_ref.shape[0])
    place_in = lax.broadcasted_iota(jnp.int32, shape, 0)
    first_owner = step // local_count * owners
    slots = (first_owner + place_in // CAP) * (local_count * CAP)
    slots = slots + step % local_count * CAP + place_in % CAP
    first, second = slots == spots_ref[0:1, :], slots == spots_ref[1:2, :]
    gates = jnp.sum(
        jnp.where(first, gates_ref[0:1, :], jnp.where(second, gates_ref[1:2, :], 0.0)), -1, keepdims=True
    )
    chosen = jnp.where(first | second, 1.0, 0.0).astype(jnp.bfloat16)
    rows_ref[...] = nn(chosen, normed_ref[...]).astype(jnp.bfloat16).reshape(owners, CAP, width)
    grads_ref[...] = (
        (nn(chosen, cot_ref[...]) * gates).astype(jnp.bfloat16).reshape(owners, CAP, width)
    )


def dispatch(spots, aux, normed, cot, owner_count, local_count):
    rows, width = normed.shape
    slot_count = owner_count * local_count * CAP
    whole = lambda shape: pl.BlockSpec(shape, lambda j: (0, 0))
    block = pl.BlockSpec(
        (None, 2, CAP, width), lambda j: (j % local_count, j // local_count, 0, 0)
    )
    return pl.pallas_call(
        functools.partial(dispatch_kernel, local_count),
        grid=(slot_count // CAP // 2,),
        out_shape=[jax.ShapeDtypeStruct((local_count, owner_count, CAP, width), jnp.bfloat16)] * 2,
        in_specs=[whole((8, rows)), whole((rows, 128)), whole((rows, width)), whole((rows, width))],
        out_specs=[block, block],
        scratch_shapes=[pltpu.VMEM((8, rows), jnp.float32)],
        compiler_params=pltpu.CompilerParams(
            dimension_semantics=("arbitrary",), vmem_limit_bytes=60 * 2**20
        ),
        cost_estimate=pl.CostEstimate(
            flops=4 * slot_count * rows * width,
            bytes_accessed=4 * (rows + slot_count) * width,
            transcendentals=0,
        ),
        name="dispatch",
    )(spots, aux, normed, cot)


def halves(values):
    high = values.astype(jnp.bfloat16)
    return high, (values - high.astype(jnp.float32)).astype(jnp.bfloat16)


def combine_kernel(
    expert_count, local_count, linked, *refs
):
    parts, refs = refs[:local_count], refs[local_count:]
    spots_ref, table_ref, aux_ref, normed_ref, middle_ref, cot_ref, small_ref = refs[:7]
    refs = refs[7:]
    if linked:
        source_ref, refs = refs[0], refs[1:]
    output_ref, logit_ref, grad_middle_ref, small_out_ref = refs[:4]
    refs = refs[4:]
    if linked:
        total_ref, refs = refs[0], refs[1:]
    vectors_ref, small_grad_ref = refs[:2]
    step = pl.program_id(0)
    if linked:
        line = line_reduce(source_ref, total_ref, refs[2:], 2, (0,))

        @pl.when(step == 0)
        def _():
            greet(line.peers())
            line.each_plane(line.start)

        pl.when(step == 1)(lambda: line.turns([0], []))

    @pl.when(step == 0)
    def _():
        vectors_ref[0:8, :] = jnp.transpose(small_ref[:, :128].astype(jnp.float32))[16:24, :]
        vectors_ref[8:16, :] = jnp.zeros((8, vectors_ref.shape[1]), jnp.float32)
        small_grad_ref[...] = jnp.zeros_like(small_grad_ref)

    rows, width = normed_ref.shape
    normed_low, cot_low = normed_ref[...], cot_ref[...]
    normed, cot = normed_low.astype(jnp.float32), cot_low.astype(jnp.float32)
    total = lambda values: jnp.sum(values, -1, keepdims=True)
    picks, back = [0.0, 0.0], 0.0
    for e in range(local_count):
        count = parts[e].shape[0] * CAP
        slots = lane_ids((rows, count))
        slots = slots // CAP * (local_count * CAP) + e * CAP + slots % CAP
        hits = [slots == spots_ref[:, s : s + 1] for s in range(2)]
        chosen = [jnp.where(hit, 1.0, 0.0).astype(jnp.bfloat16) for hit in hits]
        returned = parts[e][:, 0].reshape(count, width)
        for s in range(2):
            picks[s] = picks[s] + nn(chosen[s], returned)
        back = back + nn(chosen[0] + chosen[1], parts[e][:, 1].reshape(count, width))
    inner = [total(pick * cot) for pick in picks]
    gates = [aux_ref[:, s : s + 1] for s in range(2)]
    routes = [table_ref[:, 16 + s : 17 + s].astype(jnp.int32) for s in range(2)]
    dot_copy = total(cot * normed)

    def weight_of(route):
        return sum(jnp.where(routes[s] == route, gates[s], 0.0) for s in range(2))

    copy_weight = weight_of(expert_count + 1)
    mix = gates[0] * picks[0] + gates[1] * picks[1]
    pass_weight = copy_weight
    gate_grads = [
        inner[s] + jnp.where(routes[s] == expert_count + 1, dot_copy, 0.0) for s in range(2)
    ]
    lanes = lane_ids((rows, 128))
    spread = jnp.zeros((rows, 128), jnp.float32)
    for k in range(2):
        vector = vectors_ref[k : k + 1, :]
        keep, blend = aux_ref[:, 2 + 2 * k : 3 + 2 * k], aux_ref[:, 3 + 2 * k : 4 + 2 * k]
        weight = weight_of(expert_count + 2 + k)
        dot_vector = total(cot * vector)
        pass_weight = pass_weight + weight * keep
        mix = mix + (weight * blend) * vector
        value = keep * dot_copy + blend * dot_vector
        for s in range(2):
            gate_grads[s] = gate_grads[s] + jnp.where(routes[s] == expert_count + 2 + k, value, 0.0)
        term = keep * blend * (weight * dot_copy - weight * dot_vector)
        spread = jnp.where(lanes == 12 + 2 * k, term, spread)
        spread = jnp.where(lanes == 13 + 2 * k, -term, spread)
        spread = jnp.where(lanes == 16 + k, weight * blend, spread)
    mix = mix + pass_weight * normed
    middle, scale = middle_ref[...], aux_ref[:, 6:7]
    output_ref[...] = (middle + mix).astype(jnp.bfloat16)
    mean = gates[0] * gate_grads[0] + gates[1] * gate_grads[1]
    for s in range(2):
        spread = jnp.where(lanes == routes[s], gates[s] * (gate_grads[s] - mean), spread)
    logit_ref[...] = spread[:, : logit_ref.shape[1]].astype(jnp.bfloat16)
    logits = jnp.where(lanes < 16, spread, 0.0)
    high, low = halves(logits)
    small = small_ref[:, :128]
    vector_high, vector_low = halves(spread - logits)
    small_grad_ref[...] += (
        tn(normed_low, high) + tn(normed_low, low) + tn(cot_low, vector_high) + tn(cot_low, vector_low)
    )
    grads = back + pass_weight * cot + nt(high, small) + nt(low, small)
    vectors_ref[8:9, :] += jnp.sum(grads * middle * scale, 0, keepdims=True)
    weighted = grads * vectors_ref[3:4, :]
    mean = jnp.mean(weighted * middle, -1, keepdims=True)
    grad_middle_ref[...] = cot + scale * weighted - middle * (scale * scale * scale * mean)

    @pl.when(step == pl.num_programs(0) - 1)
    def _():
        column = jnp.transpose(jnp.broadcast_to(vectors_ref[8:9, :], (128, width)))
        small_grad = small_grad_ref[...]
        small_out_ref[...] = jnp.where(lane_ids(small_grad.shape) == 19, column, small_grad)
        if linked:
            line.turns([1, 2, 3], [0, 1, 2, 3])
            line.each_plane(line.finish)


def combine(
    parts, spots, table, aux, normed, middle, cot, packed, choice_count, expert_count, source=None,
    collective=None,
):
    rows, width = normed.shape
    local_count = len(parts)
    slot_count = expert_count * CAP
    size = 256
    linked = source is not None
    links = {"collective_id": collective, "has_side_effects": True} if linked else {}
    block = lambda columns: pl.BlockSpec((size, columns), lambda j: (j, 0))
    whole = lambda shape: pl.BlockSpec(shape, lambda j: (0,) * len(shape))
    return pl.pallas_call(
        functools.partial(combine_kernel, expert_count, local_count, linked),
        grid=(rows // size,),
        out_shape=[
            jax.ShapeDtypeStruct((rows, width), jnp.bfloat16),
            jax.ShapeDtypeStruct((rows, choice_count), jnp.bfloat16),
            jax.ShapeDtypeStruct((rows, width), jnp.float32),
            jax.ShapeDtypeStruct((width, 128), jnp.float32),
        ]
        + ([jax.ShapeDtypeStruct((width // 8, source.shape[2]), jnp.float32)] if linked else []),
        in_specs=[whole(part.shape) for part in parts]
        + [
            block(128),
            block(128),
            block(128),
            block(width),
            block(width),
            block(width),
            pl.BlockSpec((width, 256), lambda j: (0, 12)),
        ]
        + [pl.BlockSpec(memory_space=pl.ANY)] * linked,
        out_specs=[block(width), block(choice_count), block(width), whole((width, 128))]
        + ([whole((width // 8, source.shape[2]))] if linked else []),
        scratch_shapes=[pltpu.VMEM((16, width), jnp.float32), pltpu.VMEM((width, 128), jnp.float32)]
        + (reduce_scratch(source, 2, (0,)) if linked else []),
        compiler_params=pltpu.CompilerParams(
            dimension_semantics=("arbitrary",), vmem_limit_bytes=58 * 2**20, **links
        ),
        cost_estimate=pl.CostEstimate(
            flops=6 * slot_count * rows * width,
            bytes_accessed=14 * rows * width + 4 * slot_count * width,
            transcendentals=0,
        ),
        name="combine",
    )(*parts, spots, table, aux, normed, middle, cot, packed, *([source] if linked else []))


def experts_kernel(mode, dp_count, *refs):
    rows_ref, grads_ref, w_gate_ref, w_up_ref, w_down_ref = refs[:5]
    if mode == 0:
        grad_gu_ref, grad_down_ref, both_ref, turned_ref, out_ref, back_ref = refs[5:]
    if mode == 1:
        next_rows, next_grads, shards_ref, grad_gu_ref, grad_down_ref, both_ref = refs[5:11]
        rows_out, grads_out, full_ref, turned_ref, out_ref, back_ref = refs[11:17]
        sems = refs[17:]
    if mode == 2:
        before_ref, source_ref, grad_gu_ref, grad_down_ref, first_in, second_in, total_ref = refs[5:12]
        turned_ref, out_ref, back_ref, both_ref = refs[12:16]
        sems = refs[16:]
    step = pl.program_id(0)
    width = rows_ref.shape[-1]
    rows = rows_ref[...].reshape(-1, width)
    grads = grads_ref[...].reshape(-1, width)
    if mode == 1:
        half = full_ref.shape[1] // 2
        lines = []
        for n in range(2):
            columns = slice(n * half, n * half + half)
            lines.append(
                LineGather(
                    shards_ref.at[1, :, columns], full_ref, dp_count, *sems[3 * n : 3 * n + 3], columns
                )
            )
        trades = [
            Trade(next_rows.at[1], rows_out, *sems[6:8]),
            Trade(next_grads.at[1], grads_out, *sems[8:10]),
        ]

        @pl.when(step == 0)
        def _():
            greet(lines[0].peers() + trades[0].peers())
            for part in lines + trades:
                part.start()

        for hop in range(1, 4):

            @pl.when(step == hop)
            def _(hop=hop):
                for part in lines:
                    part.relay(hop)

    if mode == 2:
        trades = [Trade(before_ref, first_in, *sems[:2]), Trade(both_ref, second_in, *sems[2:4])]
        line = line_reduce(source_ref, total_ref, sems[4:], 2)

        @pl.when(step == 0)
        def _():
            greet(line.peers() + trades[0].peers())
            line.each_plane(line.start)
            trades[0].start()

        pl.when(step == 2)(lambda: line.turns([0], []))
        pl.when(step == 3)(lambda: line.turns([], [0]))

    @pl.when(step == 0)
    def _():
        turned_ref[...] = jnp.transpose(rows)
        out_ref[...] = jnp.zeros_like(out_ref)
        back_ref[...] = jnp.zeros_like(back_ref)

    w_gate, w_up, w_down = w_gate_ref[...], w_up_ref[...], w_down_ref[...]
    gate, up = nn(rows, w_gate), nn(rows, w_up)
    squashed = 1.0 / (1.0 + jnp.exp(-gate))
    silu = gate * squashed
    activated = (silu * up).astype(jnp.bfloat16)
    grad_act = nt(grads, w_down)
    grad_gate = (grad_act * up * (squashed * (1.0 + gate * (1.0 - squashed)))).astype(jnp.bfloat16)
    grad_up = (grad_act * silu).astype(jnp.bfloat16)
    out_ref[...] += nn(activated, w_down)
    grad_down_ref[...] = tn(activated, grads).astype(jnp.bfloat16)
    back_ref[...] += nt(grad_gate, w_gate) + nt(grad_up, w_up)
    grad_gu_ref[0] = nn(turned_ref[...], grad_gate).astype(jnp.bfloat16)
    grad_gu_ref[1] = nn(turned_ref[...], grad_up).astype(jnp.bfloat16)

    @pl.when(step == pl.num_programs(0) - 1)
    def _():
        shape = (both_ref.shape[0],) + both_ref.shape[2:]
        both_ref[:, 0] = out_ref[...].astype(jnp.bfloat16).reshape(shape)
        both_ref[:, 1] = back_ref[...].astype(jnp.bfloat16).reshape(shape)
        if mode == 1:
            for part in lines + trades:
                part.finish()
        if mode == 2:
            trades[1].start()
            line.turns([1, 2, 3], [1, 2, 3])
            line.each_plane(line.finish)
            for trade in trades:
                trade.finish()


def experts(rows, grads, gate, up, down, mode=0, dp_count=0, extras=(), collective=None):
    owners, cap, width = rows.shape
    hidden = down.shape[0]
    count = owners * cap
    block = FF_BLOCK if count <= 1024 else FF_BLOCK // 4
    steps = hidden // block
    low = jnp.bfloat16
    pairs = pl.BlockSpec((owners, cap, width), lambda j: (0, 0, 0), pipeline_mode=pl.Buffered(1))
    anywhere = pl.BlockSpec(memory_space=pl.ANY)
    both = jax.ShapeDtypeStruct((owners, 2, cap, width), low)
    links = {"collective_id": collective, "has_side_effects": True} if mode else {}
    out_shape = [
        jax.ShapeDtypeStruct((2, width, hidden), low),
        jax.ShapeDtypeStruct((hidden, width), low),
    ]
    out_specs = [
        pl.BlockSpec((2, width, block), lambda j: (0, 0, j)),
        pl.BlockSpec((block, width), lambda j: (j, 0)),
    ]
    scratch = [
        pltpu.VMEM((width, count), low),
        pltpu.VMEM((count, width), jnp.float32),
        pltpu.VMEM((count, width), jnp.float32),
    ]
    if mode < 2:
        out_shape.append(both)
        out_specs.append(pl.BlockSpec(both.shape, lambda j: (0, 0, 0, 0)))
    if mode == 1:
        shards = extras[2]
        out_shape += [jax.ShapeDtypeStruct(rows.shape, low)] * 2
        out_shape.append(jax.ShapeDtypeStruct((dp_count * shards.shape[1], shards.shape[2]), low))
        out_specs += [anywhere] * 3
        scratch += gather_semaphores(dp_count) * 2 + trade_semaphores(owners) + trade_semaphores(owners)
    if mode == 2:
        total = (width // 8, 2 * hidden)
        out_shape += [both, both, jax.ShapeDtypeStruct(total, jnp.float32)]
        out_specs += [anywhere] * 2 + [pl.BlockSpec(total, lambda j: (0, 0))]
        scratch.append(pltpu.VMEM(both.shape, low))
        scratch += trade_semaphores(owners) + trade_semaphores(owners) + reduce_scratch(extras[1], 2)
    return pl.pallas_call(
        functools.partial(experts_kernel, mode, dp_count),
        grid=(steps,),
        out_shape=out_shape,
        in_specs=[
            pairs,
            pairs,
            pl.BlockSpec((width, block), lambda j: (0, j)),
            pl.BlockSpec((width, block), lambda j: (0, up.shape[1] // block - steps + j)),
            pl.BlockSpec((block, width), lambda j: (j, 0)),
        ]
        + [anywhere] * len(extras),
        out_specs=out_specs,
        scratch_shapes=scratch,
        compiler_params=pltpu.CompilerParams(
            dimension_semantics=("arbitrary",), vmem_limit_bytes=60 * 2**20, **links
        ),
        cost_estimate=pl.CostEstimate(
            flops=18 * count * width * hidden,
            bytes_accessed=12 * width * hidden + 8 * count * width,
            transcendentals=count * hidden,
        ),
        name="experts",
    )(rows, grads, gate, up, down, *extras)


def dp_grid(dp_count):
    outer = 4 if dp_count % 4 == 0 else 1
    return outer, dp_count // outer


def place():
    me, mine = lax.axis_index("dp"), lax.axis_index("expert")
    return me, mine


def greet(peers):
    barrier = pltpu.get_barrier_semaphore()
    for peer in peers:
        pl.semaphore_signal(barrier, inc=1, device_id=peer, device_id_type=MESH)
    pl.semaphore_wait(barrier, len(peers))


class LineGather:
    def __init__(self, shard, full, dp_count, send_sem, recv_sem, own_sem, columns=None, also=None):
        self.columns = slice(None) if columns is None else columns
        self.also = also or (lambda chunk: None)
        self.shard, self.full, self.dp_count = shard, full, dp_count
        self.send_sem, self.recv_sem, self.own_sem = send_sem, recv_sem, own_sem
        self.outer_count, self.inner_count = dp_grid(dp_count)
        self.me, self.mine = place()
        self.outer, self.inner = self.me // self.inner_count, self.me % self.inner_count
        self.inner_peers = [
            lax.rem(self.inner + k, self.inner_count) for k in range(1, self.inner_count)
        ]
        self.can_up, self.can_down = self.outer < self.outer_count - 1, self.outer > 0

    def peers(self):
        below = lax.rem(self.outer + self.outer_count - 1, self.outer_count)
        above = lax.rem(self.outer + 1, self.outer_count)
        return [(peer * self.inner_count + self.inner, self.mine) for peer in (below, above)] + [
            (self.outer * self.inner_count + peer, self.mine) for peer in self.inner_peers
        ]

    def spot(self, chunk):
        rows = self.shard.shape[0]
        return self.full.at[pl.ds(pl.multiple_of(chunk * rows, 8), rows), self.columns]

    def copy(self, source, chunk, device, way, at):
        return pltpu.make_async_remote_copy(
            src_ref=source,
            dst_ref=self.spot(chunk),
            send_sem=self.send_sem.at[way, at, chunk],
            recv_sem=self.recv_sem.at[chunk],
            device_id=(device, self.mine),
            device_id_type=MESH,
        )

    def up(self, source, chunk):
        return self.copy(source, chunk, (self.outer + 1) * self.inner_count + self.inner, 1, 0)

    def down(self, source, chunk):
        return self.copy(source, chunk, (self.outer - 1) * self.inner_count + self.inner, 2, 0)

    def across(self, source, chunk):
        return [
            self.copy(source, chunk, self.outer * self.inner_count + peer, 0, at)
            for at, peer in enumerate(self.inner_peers)
        ]

    def keep(self):
        return pltpu.make_async_copy(self.shard, self.spot(self.me), self.own_sem)

    def arrived(self, chunk):
        pltpu.make_async_copy(self.spot(chunk), self.spot(chunk), self.recv_sem.at[chunk]).wait()

    def start(self):
        for copy in self.across(self.shard, self.me):
            copy.start()
        pl.when(self.can_up)(lambda: self.up(self.shard, self.me).start())
        pl.when(self.can_down)(lambda: self.down(self.shard, self.me).start())
        self.keep().start()

    def relay(self, step):
        low, high = self.outer - step, self.outer + step

        def pass_on(source, upward):
            chunk = source * self.inner_count + self.inner
            self.arrived(chunk)
            if upward:
                pl.when(self.can_up)(lambda: self.up(self.spot(chunk), chunk).start())
            else:
                pl.when(self.can_down)(lambda: self.down(self.spot(chunk), chunk).start())
            for copy in self.across(self.spot(chunk), chunk):
                copy.start()
            self.also(chunk)

        pl.when(low >= 0)(lambda: pass_on(low, True))
        pl.when(high < self.outer_count)(lambda: pass_on(high, False))

    def finish(self):
        self.keep().wait()
        for peer in self.inner_peers:
            for k in range(self.outer_count):
                chunk = lax.rem(self.outer + k, self.outer_count) * self.inner_count + peer
                self.arrived(chunk)
                self.also(chunk)
        for plane in range(self.outer_count):
            chunk = plane * self.inner_count + self.inner
            for copy in self.across(self.spot(chunk), chunk):
                copy.wait_send()
            pl.when(self.can_up & (self.outer >= plane))(
                lambda chunk=chunk: self.up(self.spot(chunk), chunk).wait_send()
            )
            pl.when(self.can_down & (self.outer <= plane))(
                lambda chunk=chunk: self.down(self.spot(chunk), chunk).wait_send()
            )


def gather_semaphores(dp_count):
    inner_count = dp_grid(dp_count)[1]
    return [
        pltpu.SemaphoreType.DMA((3, max(1, inner_count - 1), dp_count)),
        pltpu.SemaphoreType.DMA((dp_count,)),
        pltpu.SemaphoreType.DMA,
    ]


def by_rows(count, body):
    def step(i, carry):
        body(i * 16)
        return carry

    lax.fori_loop(0, count // 16, step, 0)


class Trade:
    def __init__(self, source, target, send_sem, recv_sem):
        self.source, self.target, self.send_sem, self.recv_sem = source, target, send_sem, recv_sem
        self.me, self.mine = place()
        count = target.shape[0]
        self.partners = [lax.rem(self.mine + k, count) for k in range(1, count)]

    def peers(self):
        return [(self.me, peer) for peer in self.partners]

    def copy(self, k):
        peer = self.partners[k]
        return pltpu.make_async_remote_copy(
            src_ref=self.source.at[peer],
            dst_ref=self.target.at[self.mine],
            send_sem=self.send_sem.at[k + 1],
            recv_sem=self.recv_sem.at[self.mine],
            device_id=(self.me, peer),
            device_id_type=MESH,
        )

    def keep(self):
        return pltpu.make_async_copy(
            self.source.at[self.mine], self.target.at[self.mine], self.send_sem.at[0]
        )

    def start(self):
        for k in range(len(self.partners)):
            self.copy(k).start()
        self.keep().start()

    def finish(self):
        self.keep().wait()
        for k, peer in enumerate(self.partners):
            there = self.target.at[peer]
            pltpu.make_async_copy(there, there, self.recv_sem.at[peer]).wait()
            self.copy(k).wait_send()


def trade_semaphores(owner_count):
    return [pltpu.SemaphoreType.DMA((owner_count,)), pltpu.SemaphoreType.DMA((owner_count,))]


def expert_gather_kernel(
    dp_count, rows_ref, grads_ref, down_ref, gate_up_ref, rows_out, grads_out, full_ref, up_ref, *sems
):
    half = up_ref.shape[1] // 2
    lines = [LineGather(down_ref.at[0], full_ref, dp_count, *sems[:3])]
    for n in range(2):
        columns = slice(n * half, n * half + half)
        shard = gate_up_ref.at[0, :, (2 + n) * half : (3 + n) * half]
        lines.append(LineGather(shard, up_ref, dp_count, *sems[3 * n + 3 : 3 * n + 6], columns))
    trades = [Trade(rows_ref.at[0], rows_out, *sems[9:11]), Trade(grads_ref.at[0], grads_out, *sems[11:13])]
    greet(lines[0].peers() + trades[0].peers())
    for part in lines + trades:
        part.start()
    for hop in range(1, lines[0].outer_count):
        for line in lines:
            line.relay(hop)
    for part in lines + trades:
        part.finish()


def expert_gather(rows, grads, down, gate_up, dp_count, collective):
    anywhere = pl.BlockSpec(memory_space=pl.ANY)
    return pl.pallas_call(
        functools.partial(expert_gather_kernel, dp_count),
        out_shape=[
            jax.ShapeDtypeStruct(rows.shape[1:], rows.dtype),
            jax.ShapeDtypeStruct(grads.shape[1:], grads.dtype),
            jax.ShapeDtypeStruct((dp_count * down.shape[1], down.shape[2]), down.dtype),
            jax.ShapeDtypeStruct((dp_count * gate_up.shape[1], gate_up.shape[2] // 2), gate_up.dtype),
        ],
        in_specs=[anywhere] * 4,
        out_specs=[anywhere] * 4,
        scratch_shapes=gather_semaphores(dp_count) * 3 + trade_semaphores(rows.shape[1]) * 2,
        compiler_params=pltpu.CompilerParams(collective_id=collective, has_side_effects=True),
        name="expert_gather",
    )(rows, grads, down, gate_up)


def small_gather_kernel(
    dp_count, expert_count, shard_ref, routes_ref, docs_ref, resid_ref,
    full_ref, columns_ref, rows_ref, table_ref, pass_sem, mate_sem, all_sem, stack_ref, *sems,
):
    me, mine = place()
    rows, columns = shard_ref.shape
    half = columns // 2
    side = mine % 2
    mate = mine + 1 - 2 * side
    mate_columns = pl.ds(pl.multiple_of((1 - side) * half, 128), half)
    first = half // 256 * 128
    spans = [(0, first), (first, half - first)]

    def there(chunk, lanes):
        return full_ref.at[pl.ds(pl.multiple_of(chunk * rows, 8), rows), lanes]

    def columns_at(n, of):
        start, size = spans[n]
        return pl.ds(pl.multiple_of(of * half + start, 128), size)

    def pass_copy(n, chunk):
        here = there(chunk, columns_at(n, side))
        return pltpu.make_async_remote_copy(
            src_ref=here,
            dst_ref=here,
            send_sem=pass_sem.at[n, chunk],
            recv_sem=mate_sem.at[n, chunk],
            device_id=(me, mate),
            device_id_type=MESH,
        )

    lines = []
    for n in range(2):
        lines.append(
            LineGather(
                shard_ref.at[:, columns_at(n, side)], full_ref, dp_count, *sems[3 * n : 3 * n + 3],
                columns_at(n, side), lambda chunk, n=n: pass_copy(n, chunk).start(),
            )
        )
    greet(lines[0].peers() + [(me, mate)])
    for line in lines:
        line.start()
    other = pltpu.make_async_copy(shard_ref.at[:, mate_columns], there(me, mate_columns), all_sem)
    other.start()
    stack_ref[...] = jnp.zeros_like(stack_ref)
    stack_ref[0 : resid_ref.shape[0], :] = resid_ref[...].astype(jnp.float32)
    stack_ref[16:18, :] = routes_ref[...].astype(jnp.float32)
    stack_ref[18:19, :] = docs_ref[...].astype(jnp.float32)
    table_ref[...] = jnp.transpose(stack_ref[...])
    routing_kernel(expert_count, table_ref, columns_ref, rows_ref)
    for hop in range(1, lines[0].outer_count):
        for line in lines:
            line.relay(hop)
    for line in lines:
        line.finish()
    other.wait()
    for k in range(1, dp_count):
        chunk = lax.rem(me + k, dp_count)
        for n in range(2):
            target = there(chunk, columns_at(n, 1 - side))
            pltpu.make_async_copy(target, target, mate_sem.at[n, chunk]).wait()
            pass_copy(n, chunk).wait_send()


def small_gather(shard, routes, docs, resid, expert_count, dp_count, collective):
    rows, columns = shard.shape
    tokens = routes.shape[1]
    anywhere, in_vmem = pl.BlockSpec(memory_space=pl.ANY), pl.BlockSpec(memory_space=pltpu.VMEM)
    return pl.pallas_call(
        functools.partial(small_gather_kernel, dp_count, expert_count),
        out_shape=[
            jax.ShapeDtypeStruct((dp_count * rows, columns), shard.dtype),
            jax.ShapeDtypeStruct((tokens, 128), jnp.int32),
            jax.ShapeDtypeStruct((8, tokens), jnp.int32),
            jax.ShapeDtypeStruct((tokens, 128), jnp.float32),
        ],
        in_specs=[anywhere] + [in_vmem] * 3,
        out_specs=[anywhere] + [in_vmem] * 3,
        scratch_shapes=[
            pltpu.SemaphoreType.DMA((2, dp_count)),
            pltpu.SemaphoreType.DMA((2, dp_count)),
            pltpu.SemaphoreType.DMA,
            pltpu.VMEM((128, tokens), jnp.float32),
        ]
        + gather_semaphores(dp_count) * 2,
        compiler_params=pltpu.CompilerParams(
            collective_id=collective, has_side_effects=True, vmem_limit_bytes=60 * 2**20
        ),
        name="small_gather",
    )(shard, routes, docs, resid)


class LineReduce:
    def __init__(self, sources, totals, owns, ins, lows, highs, own_sem, in_send, in_recv, line_send, line_recv):
        self.sources, self.totals = sources, totals
        self.owns, self.ins, self.lows, self.highs = owns, ins, lows, highs
        self.own_sem, self.in_send, self.in_recv = own_sem, in_send, in_recv
        self.line_send, self.line_recv = line_send, line_recv
        self.me, self.mine = place()
        self.outer, self.inner = self.me // 2, self.me % 2
        self.every = range(len(sources))

    def peers(self):
        low, high = lax.rem(self.outer + 3, 4), lax.rem(self.outer + 1, 4)
        return [
            (self.me + 1 - 2 * self.inner, self.mine),
            (low * 2 + self.inner, self.mine),
            (high * 2 + self.inner, self.mine),
        ]

    def order(self, o):
        return sorted(range(4), key=lambda plane: (-abs(plane - o), plane))

    def chunk(self, p, at):
        source = self.sources[p]
        rows = self.owns[p].shape[-2]
        here = pl.ds(pl.multiple_of(at * rows, 16), rows)
        return source.at[:, here, :] if len(source.shape) == 3 else source.at[here, :]

    def own_copy(self, p, plane):
        return pltpu.make_async_copy(
            self.chunk(p, plane * 2 + self.inner), self.owns[p].at[plane], self.own_sem.at[p, plane]
        )

    def in_copy(self, p, plane):
        return pltpu.make_async_remote_copy(
            src_ref=self.chunk(p, plane * 2 + 1 - self.inner),
            dst_ref=self.ins[p].at[plane],
            send_sem=self.in_send.at[p, plane],
            recv_sem=self.in_recv.at[p, plane],
            device_id=(self.me + 1 - 2 * self.inner, self.mine),
            device_id_type=MESH,
        )

    def line_copy(self, p, plane, upward, device_plane):
        target = self.lows[p].at[plane - 1] if upward else self.highs[p].at[plane]
        return pltpu.make_async_remote_copy(
            src_ref=self.ins[p].at[plane],
            dst_ref=target,
            send_sem=self.line_send.at[p, 0 if upward else 1, plane],
            recv_sem=self.line_recv.at[p, 0 if upward else 1, plane],
            device_id=(device_plane * 2 + self.inner, self.mine),
            device_id_type=MESH,
        )

    def start(self, o):
        for plane in self.order(o):
            for p in self.every:
                self.in_copy(p, plane).start()
        for plane in self.order(o):
            for p in self.every:
                self.own_copy(p, plane).start()

    def line_start(self, o, p, plane):
        return self.line_copy(p, plane, plane > o, o + 1 if plane > o else o - 1)

    def pass_on(self, o, k):
        plane = self.order(o)[k]
        for p in self.every:
            self.own_copy(p, plane).wait()
            self.in_copy(p, plane).wait_recv()
            terms = [self.owns[p].at[plane]]
            if o > 0 and plane >= o:
                self.line_copy(p, plane, True, o).wait_recv()
                terms.append(self.lows[p].at[plane - 1])
            if o < 3 and plane <= o:
                self.line_copy(p, plane, False, o).wait_recv()
                terms.append(self.highs[p].at[plane])
            held = self.ins[p].at[plane]
            last = plane == o
            sides = held.shape[0] if len(held.shape) == 3 else 0

            def body(at, p=p, terms=terms, held=held, last=last, sides=sides):
                here = pl.ds(pl.multiple_of(at, 16), 16)
                for side in range(max(1, sides)):
                    spot = (side, here) if sides else (here,)
                    total = held[spot].astype(jnp.float32)
                    for term in terms:
                        total = total + term[spot].astype(jnp.float32)
                    if last:
                        size = total.shape[-1]
                        self.totals[p][here, side * size : (side + 1) * size] = total
                    else:
                        held[spot] = total.astype(held.dtype)

            by_rows(held.shape[-2], body)
            if not last:
                self.line_start(o, p, plane).start()

    def finish(self, o):
        for plane in range(4):
            for p in self.every:
                self.in_copy(p, plane).wait_send()
                if plane != o:
                    self.line_start(o, p, plane).wait_send()

    def each_plane(self, body):
        for o in range(4):
            pl.when(self.outer == o)(functools.partial(body, o))

    def turns(self, ends, middles):
        def body(o):
            for k in ends if o in (0, 3) else middles:
                self.pass_on(o, k)

        self.each_plane(body)


def pieces_of(source, cut, sides=None):
    columns = source.shape[-1]
    size = columns // cut
    fronts = [()]
    if len(source.shape) == 3:
        fronts = [(side,) for side in (range(source.shape[0]) if sides is None else sides)]
    return [
        (front, slice(c * size, c * size + size), slice(n * columns + c * size, n * columns + c * size + size))
        for n, front in enumerate(fronts)
        for c in range(cut)
    ]


def reduce_scratch(source, cut, sides=None):
    rows = source.shape[-2] // 8
    size = source.shape[-1] // cut
    count = len(pieces_of(source, cut, sides))
    shapes = []
    for planes in (4, 4, 3, 3):
        shapes += [pltpu.VMEM((planes, rows, size), jnp.bfloat16)] * count
    return shapes + [
        pltpu.SemaphoreType.DMA((count, 4)),
        pltpu.SemaphoreType.DMA((count, 4)),
        pltpu.SemaphoreType.DMA((count, 4)),
        pltpu.SemaphoreType.DMA((count, 2, 4)),
        pltpu.SemaphoreType.DMA((count, 2, 4)),
    ]


def line_reduce(source, total, scratch, cut, sides=None):
    pieces = pieces_of(source, cut, sides)
    count = len(pieces)
    buffers = [scratch[n * count : (n + 1) * count] for n in range(4)]
    sources = [source.at[front + (slice(None), columns)] for front, columns, _ in pieces]
    totals = [total.at[:, columns] for _, _, columns in pieces]
    return LineReduce(sources, totals, *buffers, *scratch[4 * count :])


def final_reduce_kernel(small_count, *refs):
    small_refs, refs = refs[:small_count], refs[small_count:]
    (
        small_out, swap, small_own, small_in, small_low, small_high, final_low, final_in, own_sem,
        swap_send, swap_recv, in_send, in_recv, line_send, line_recv, last_send, last_recv,
    ) = refs
    outer_count, inner_count = 4, 2
    me, mine = place()
    outer, inner = me // inner_count, me % inner_count
    side = mine % 2
    mate, across = mine + 1 - 2 * side, lax.rem(mine + 2, 4)
    beside = me + 1 - 2 * inner
    half_rows = small_refs[0].shape[1] // 2
    starts = [sum(ref.shape[2] for ref in small_refs[:n]) for n in range(small_count + 1)]

    def remote(source, target, device, send_at, recv_at):
        return pltpu.make_async_remote_copy(
            src_ref=source,
            dst_ref=target,
            send_sem=send_at,
            recv_sem=recv_at,
            device_id=device,
            device_id_type=MESH,
        )

    low_peer = lax.rem(outer + outer_count - 1, outer_count) * inner_count + inner
    high_peer = lax.rem(outer + 1, outer_count) * inner_count + inner
    greet([(me, mate), (me, across), (beside, mine), (low_peer, mine), (high_peer, mine)])

    mate_rows = pl.ds(pl.multiple_of((1 - side) * half_rows, 16), half_rows)
    own_rows = pl.ds(pl.multiple_of(side * half_rows, 16), half_rows)

    middle = starts[-1] // 256 * 128
    spans = [slice(0, middle), slice(middle, starts[-1])]

    def swap_copy(n):
        return remote(
            small_refs[n].at[:, mate_rows, :],
            swap.at[:, :, starts[n] : starts[n + 1]],
            (me, mate),
            swap_send.at[n],
            swap_recv.at[n],
        )

    def own_copy(n):
        return pltpu.make_async_copy(
            small_refs[n].at[:, own_rows, :], small_own.at[:, :, starts[n] : starts[n + 1]], own_sem.at[n]
        )

    def inner_copy(p, plane):
        return remote(
            swap.at[plane * inner_count + 1 - inner, :, spans[p]],
            small_in.at[plane, :, spans[p]],
            (beside, mine),
            in_send.at[p, plane],
            in_recv.at[p, plane],
        )

    def line_copy(p, plane, upward, device_plane):
        way = 0 if upward else 1
        return remote(
            small_in.at[plane, :, spans[p]],
            (small_low if upward else small_high).at[plane, :, spans[p]],
            (device_plane * inner_count + inner, mine),
            line_send.at[p, way, plane],
            line_recv.at[p, way, plane],
        )

    def last_copy(p):
        return remote(
            final_low.at[:, spans[p]], final_in.at[:, spans[p]], (me, across), last_send.at[p], last_recv.at[p]
        )

    def wide(values):
        return values.astype(jnp.float32)

    def add_own(chunk, lanes):
        def body(at):
            here = pl.ds(pl.multiple_of(at, 16), 16)
            swap[chunk, here, lanes] = (
                wide(swap[chunk, here, lanes]) + wide(small_own[chunk, here, lanes])
            ).astype(swap.dtype)

        by_rows(half_rows, body)

    def at_plane(o):
        order = sorted(range(outer_count), key=lambda t: (-abs(t - o), t))

        def line_start(p, plane):
            return line_copy(p, plane, plane > o, o + 1 if plane > o else o - 1)

        for n in range(small_count):
            swap_copy(n).start()
            own_copy(n).start()
        for n in range(small_count):
            swap_copy(n).wait_recv()
            own_copy(n).wait()
        for plane in order:
            for p in range(2):
                add_own(plane * inner_count + 1 - inner, spans[p])
                inner_copy(p, plane).start()
        for plane in order:
            for p in range(2):
                add_own(plane * inner_count + inner, spans[p])
                inner_copy(p, plane).wait_recv()
                terms = [swap.at[plane * inner_count + inner]]
                if o > 0 and plane >= o:
                    line_copy(p, plane, True, o).wait_recv()
                    terms.append(small_low.at[plane])
                if o < outer_count - 1 and plane <= o:
                    line_copy(p, plane, False, o).wait_recv()
                    terms.append(small_high.at[plane])
                target = final_low if plane == o else small_in.at[plane]

                def gather(at, plane=plane, terms=terms, target=target, lanes=spans[p]):
                    here = pl.ds(pl.multiple_of(at, 16), 16)
                    total = wide(small_in[plane, here, lanes])
                    for term in terms:
                        total = total + wide(term[here, lanes])
                    target[here, lanes] = total.astype(target.dtype)

                by_rows(half_rows, gather)
                if plane != o:
                    line_start(p, plane).start()
                else:
                    last_copy(p).start()
        for plane in range(outer_count):
            for p in range(2):
                inner_copy(p, plane).wait_send()
                if plane != o:
                    line_start(p, plane).wait_send()
        for n in range(small_count):
            swap_copy(n).wait_send()

    for o in range(outer_count):
        pl.when(outer == o)(functools.partial(at_plane, o))
    for p in range(2):
        last_copy(p).wait()

    def total_body(at):
        here = pl.ds(pl.multiple_of(at, 16), 16)
        there = pl.ds(pl.multiple_of(side * half_rows + at, 16), 16)
        small_out[there, :] = wide(final_low[here, :]) + wide(final_in[here, :])

    by_rows(half_rows, total_body)
    mate_copy = remote(
        small_out.at[own_rows, :], small_out.at[own_rows, :], (me, mate), last_send.at[2], last_recv.at[2]
    )
    mate_copy.start()
    mate_copy.wait()


def final_reduce(smalls, collective):
    chunk_count, small_rows, _ = smalls[0].shape
    small_columns = sum(small.shape[2] for small in smalls)
    low = jnp.bfloat16
    planes = 4
    in_vmem = pl.BlockSpec(memory_space=pltpu.VMEM)
    half = small_rows // 2
    return pl.pallas_call(
        functools.partial(final_reduce_kernel, len(smalls)),
        out_shape=jax.ShapeDtypeStruct((small_rows, small_columns), jnp.float32),
        in_specs=[pl.BlockSpec(memory_space=pl.ANY)] * len(smalls),
        out_specs=in_vmem,
        scratch_shapes=[pltpu.VMEM((chunk_count, half, small_columns), low)] * 2
        + [pltpu.VMEM((planes, half, small_columns), low)] * 3
        + [pltpu.VMEM((half, small_columns), low)] * 2
        + [
            pltpu.SemaphoreType.DMA((len(smalls),)),
            pltpu.SemaphoreType.DMA((len(smalls),)),
            pltpu.SemaphoreType.DMA((len(smalls),)),
            pltpu.SemaphoreType.DMA((2, planes)),
            pltpu.SemaphoreType.DMA((2, planes)),
            pltpu.SemaphoreType.DMA((2, 2, planes)),
            pltpu.SemaphoreType.DMA((2, 2, planes)),
            pltpu.SemaphoreType.DMA((3,)),
            pltpu.SemaphoreType.DMA((3,)),
        ],
        compiler_params=pltpu.CompilerParams(
            collective_id=collective, has_side_effects=True, vmem_limit_bytes=60 * 2**20
        ),
        name="final_reduce",
    )(*smalls)


def shards(
    tokens,
    resid_logits,
    routes,
    doc_ids,
    w_qkv,
    w_out,
    gain_attn,
    gain_ffn,
    w_router,
    w_const,
    v_const,
    w_gate_up,
    w_down,
    out_grad,
):
    dp_count, owner_count = lax.axis_size("dp"), lax.axis_size("expert")
    own_links = dp_count == 8 and owner_count == 4 and w_gate_up.shape[0] == 2
    seq_count, length, width = tokens.shape
    assert seq_count == 1
    rows = seq_count * length
    choice_count = resid_logits.shape[-1]
    local_count = w_gate_up.shape[0]
    expert_count = owner_count * local_count
    hidden_count = w_down.shape[1] * dp_count
    width_qkv, width_out = w_qkv.shape[1], w_out.shape[1]
    small_parts = [w_router, w_const, v_const, gain_attn[:, None], gain_ffn[:, None]]
    small_width = sum(part.shape[1] for part in small_parts)
    pad = jnp.zeros((w_qkv.shape[0], 256 - small_width), jnp.bfloat16)
    packed = jnp.concatenate([w_qkv, w_out] + small_parts + [pad], 1)
    inputs = tokens.reshape(rows, width)
    cot = out_grad.reshape(rows, width)
    route_rows = routes.reshape(rows, 2)
    cosine, sine = rotary_lanes(length, width // HEADS)
    docs_row = doc_ids.reshape(1, rows)
    resid_rows = resid_logits.reshape(rows, choice_count)
    if own_links:
        packed_full, spots, spot_rows, table = small_gather(
            packed, route_rows.T, docs_row, resid_rows.T, expert_count, dp_count, 1
        )
    else:
        columns = [
            resid_rows, jnp.zeros((rows, 16 - choice_count)), route_rows, docs_row.T, jnp.zeros((rows, 109))
        ]
        table = jnp.concatenate([column.astype(jnp.float32) for column in columns], 1)
        spots, spot_rows = routing(table, expert_count)
        packed_full = lax.all_gather(packed, "dp", axis=0, tiled=True)
    gather = functools.partial(lax.all_gather, axis_name="dp", axis=0, tiled=True)
    if own_links:
        first_gate, second_down, packed_full = lax.optimization_barrier(
            (w_gate_up[0, :, :hidden_count], w_down[1], packed_full)
        )
        first_gate, second_down = gather(first_gate), gather(second_down)
    else:
        first_gate_up = gather(w_gate_up[0])
    normed_one, queries, keys, values, attended, middle, normed_two, aux = attention_forward(
        inputs, packed_full, docs_row, cosine, sine, table
    )
    send_rows, send_grads = dispatch(spot_rows, aux, normed_two, cot, owner_count, local_count)
    if own_links:
        rows_in, grads_in, first_down, first_up = expert_gather(
            send_rows, send_grads, w_down, w_gate_up, dp_count, 2
        )
        grad_gu, grad_down, both, next_rows, next_grads, second_gate_up = experts(
            rows_in, grads_in, first_gate, first_up, first_down, 1, dp_count,
            [send_rows, send_grads, w_gate_up], 6,
        )
        down_parts = [lax.psum_scatter(grad_down, "dp", scatter_dimension=0, tiled=True)]
        second_gu, grad_down, *parts, gu_part = experts(
            next_rows, next_grads, second_gate_up, second_gate_up, second_down, 2, dp_count,
            [both, grad_gu], 4,
        )
        down_parts.append(lax.psum_scatter(grad_down, "dp", scatter_dimension=0, tiled=True))
        gu_parts = [gu_part]
    else:
        exchange = functools.partial(
            lax.all_to_all, axis_name="expert", split_axis=0, concat_axis=0, tiled=True
        )
        parts, gu_parts, down_parts = [], [], []
        for e in range(local_count):
            gate_up = first_gate_up if e == 0 else gather(w_gate_up[e])
            grad_gu, grad_down, both = experts(
                exchange(send_rows[e]), exchange(send_grads[e]), gate_up, gate_up, gather(w_down[e])
            )
            parts.append(exchange(both))
            gu_part = lax.psum_scatter(grad_gu, "dp", scatter_dimension=1, tiled=True)
            gu_parts.append(jnp.concatenate([gu_part[0], gu_part[1]], -1).astype(jnp.float32))
            down_parts.append(lax.psum_scatter(grad_down, "dp", scatter_dimension=0, tiled=True))
    down_parts = [part.astype(jnp.float32) for part in down_parts]
    output, logit_grad, grad_middle, small_grad = combine(
        parts, spots, table, aux, normed_two, middle, cot, packed_full, choice_count, expert_count
    )
    if own_links:
        grad_middle, down_parts[0] = lax.optimization_barrier((grad_middle, down_parts[0]))
    backward = functools.partial(
        attention_backward, grad_middle, queries, keys, values, attended, normed_one, inputs,
        packed_full, docs_row, table, cosine, sine, small_grad,
    )
    if own_links:
        token_grad, *weight_grads, gu_part = backward([second_gu], 7)
        gu_parts.append(gu_part)
        packed_part = final_reduce(
            [grad.reshape(dp_count, width // dp_count, grad.shape[1]) for grad in weight_grads], 3
        )
    else:
        token_grad, *weight_grads = backward()
        packed_part = lax.psum_scatter(
            jnp.concatenate(weight_grads, 1), "dp", scatter_dimension=0, tiled=True
        )
        packed_part = lax.psum(packed_part, "expert").astype(jnp.float32)
    part_qkv = packed_part[:, :width_qkv]
    part_out = packed_part[:, width_qkv : width_qkv + width_out]
    small_part = packed_part[:, width_qkv + width_out :]
    return (
        output.reshape(tokens.shape),
        token_grad.reshape(tokens.shape),
        logit_grad.reshape(resid_logits.shape),
        part_qkv,
        part_out,
        small_part[:, 18],
        small_part[:, 19],
        small_part[:, 0:12],
        small_part[:, 12:16],
        small_part[:, 16:18],
        jnp.stack(gu_parts),
        jnp.stack(down_parts),
    )


def solution(mesh):
    placed = (
        P(("dp", "expert"), None, None),
        P(("dp", "expert"), None, None),
        P(("dp", "expert"), None, None),
        P(("dp", "expert"), None),
        P("dp", None),
        P("dp", None),
        P("dp"),
        P("dp"),
        P("dp", None),
        P("dp", None),
        P("dp", None),
        P("expert", "dp", None),
        P("expert", "dp", None),
        P(("dp", "expert"), None, None),
    )
    return jax.shard_map(
        shards,
        mesh=mesh,
        in_specs=placed,
        out_specs=(
            P(("dp", "expert"), None, None),
            P(("dp", "expert"), None, None),
            P(("dp", "expert"), None, None),
            P("dp", None),
            P("dp", None),
            P("dp"),
            P("dp"),
            P("dp", None),
            P("dp", None),
            P("dp", None),
            P("expert", "dp", None),
            P("expert", "dp", None),
        ),
        check_vma=False,
    )
```

```python
import functools

import jax
import jax.numpy as jnp
import numpy as np
from jax import lax
from jax.experimental import pallas as pl
from jax.experimental.pallas import tpu as pltpu
from jax.sharding import PartitionSpec as P

HEADS = 12
BLOCK = 256
CAP = 256
GROUP = 256
FF_BLOCK = 512
MESH = pl.DeviceIdType.MESH
epsilon = 1e-06


def rotary_lanes(length, head_dim):
    half_dim = head_dim // 2
    frequency = (10000.0 ** (-np.arange(half_dim, dtype=np.float32) / half_dim)).astype(np.float32)
    angles = (np.arange(length, dtype=np.float32)[:, None] * frequency[None, :]).astype(np.float64)
    cosine = np.cos(angles).astype(np.float32)
    sine = np.sin(angles).astype(np.float32)
    return (
        np.concatenate([cosine] * 4, 1),
        np.concatenate([-sine, sine, -sine, sine], 1),
    )


def nt(left, right):
    return lax.dot_general(left, right, (((1,), (1,)), ((), ())), preferred_element_type=jnp.float32)


def tn(left, right):
    return lax.dot_general(left, right, (((0,), (0,)), ((), ())), preferred_element_type=jnp.float32)


def nn(left, right):
    return jnp.dot(left, right, preferred_element_type=jnp.float32)


def lane_ids(shape):
    return lax.broadcasted_iota(jnp.int32, shape, len(shape) - 1)


def turn(values, cosine, sine):
    lanes = lane_ids(values.shape)
    ahead, behind = pltpu.roll(values, 96, 1), pltpu.roll(values, 32, 1)
    return values * cosine + jnp.where(lanes % 64 < 32, ahead, behind) * sine


def key_span(i):
    return max(0, i - 2) * BLOCK, (i + 1) * BLOCK


def mask_of(docs_column, docs_row, i):
    low, high = key_span(i)
    return docs_column[low:high, :] == docs_row[:, i * BLOCK : (i + 1) * BLOCK]


def attention_forward_kernel(linked, *refs):
    (
        tokens_ref, wq_ref, wk_ref, wv_ref, wo_ref, small_ref, docs_row_ref,
        cosine_ref, sine_ref, table_ref,
    ) = refs[:10]
    (
        normed_ref, q_ref, k_ref, v_ref, attended_ref, middle_ref, normed_two_ref, aux_ref,
    ) = refs[10 + bool(linked) : 18 + bool(linked)]
    step = pl.program_id(0)
    rows = tokens_ref.shape[0]
    if linked:
        branch_ref = refs[20]
        line = LineGather(refs[10].at[0], refs[19], linked, *refs[21:])

        @pl.when(step == 0)
        def _():
            greet(line.peers())
            line.start()

        @pl.when(step == 2)
        def _():
            line.relay(1)
    else:
        branch_ref = refs[18]

    @pl.when(step == 0)
    def _():
        inputs = tokens_ref[...].astype(jnp.float32)
        gains = jnp.transpose(small_ref[:, :128].astype(jnp.float32))[18:19, :]
        scale = lax.rsqrt(jnp.mean(inputs * inputs, -1, keepdims=True) + epsilon)
        normed_ref[...] = (inputs * scale * gains).astype(jnp.bfloat16)
        branch_ref[...] = jnp.zeros_like(branch_ref)

    normed = normed_ref[...]
    cosine, sine = cosine_ref[...], sine_ref[...]
    for w_ref, out_ref, turned in ((wq_ref, q_ref, True), (wk_ref, k_ref, True), (wv_ref, v_ref, False)):
        projected = nn(normed, w_ref[...])
        for half in range(2):
            part = projected[:, half * 128 : half * 128 + 128]
            if turned:
                part = turn(part, cosine, sine)
            out_ref[:, half * 128 : half * 128 + 128] = part.astype(jnp.bfloat16)

    docs_row, docs_column = docs_row_ref[...], table_ref[:, 18:19].astype(jnp.int32)
    for i in range(rows // BLOCK):
        low, high = key_span(i)
        here = slice(i * BLOCK, (i + 1) * BLOCK)
        allowed = mask_of(docs_column, docs_row, i)
        for pair in range(2):
            lanes = slice(pair * 128, pair * 128 + 128)
            queries = q_ref[here, lanes] * jnp.asarray(0.125, jnp.bfloat16)
            keys, values = k_ref[low:high, lanes], v_ref[low:high, lanes]
            left = lane_ids(queries.shape) < 64
            outs = []
            for head in range(2):
                own = left if head == 0 else jnp.logical_not(left)
                scores = nt(keys, jnp.where(own, queries, jnp.zeros_like(queries)))
                scores = jnp.where(allowed, scores, -1e30)
                shifted = jnp.exp(scores - jnp.max(scores, 0, keepdims=True))
                probs = shifted * (1.0 / jnp.sum(shifted, 0, keepdims=True))
                outs.append(tn(probs.astype(jnp.bfloat16), values))
            attended_ref[here, lanes] = jnp.where(left, outs[0], outs[1]).astype(jnp.bfloat16)
    branch_ref[...] += nn(attended_ref[...], wo_ref[...])

    @pl.when(step == pl.num_programs(0) - 1)
    def _():
        small = small_ref[:, :128]
        gains = jnp.transpose(small.astype(jnp.float32))[19:20, :]
        middle = tokens_ref[...].astype(jnp.float32) + branch_ref[...]
        middle_ref[...] = middle
        scale = lax.rsqrt(jnp.mean(middle * middle, -1, keepdims=True) + epsilon)
        normed_two = (middle * scale * gains).astype(jnp.bfloat16)
        normed_two_ref[...] = normed_two
        logits = nn(normed_two, small) + table_ref[...]
        lanes = lane_ids(logits.shape)

        def lane(at):
            return jnp.sum(jnp.where(lanes == at, logits, 0.0), -1, keepdims=True)

        def two(first, second):
            peak = jnp.maximum(first, second)
            first, second = jnp.exp(first - peak), jnp.exp(second - peak)
            return first / (first + second), second / (first + second)

        columns = list(two(*[lane(table_ref[:, 16 + s : 17 + s].astype(jnp.int32)) for s in range(2)]))
        columns += list(two(lane(12), lane(13))) + list(two(lane(14), lane(15)))
        columns.append(scale)
        aux = jnp.zeros_like(logits)
        for at, column in enumerate(columns):
            aux = jnp.where(lanes == at, column, aux)
        aux_ref[...] = aux
        if linked:
            line.relay(2)
            line.relay(3)
            line.finish()


def attention_forward(
    tokens, packed, docs_row, cosine, sine, table, shards=None,
    dp_count=None, collective=None,
):
    rows, width = tokens.shape
    groups = width // GROUP
    low = jnp.bfloat16
    whole = lambda shape: pl.BlockSpec(shape, lambda j: (0, 0))
    column = lambda at: pl.BlockSpec((width, GROUP), lambda j: (0, at + j))
    out_column = pl.BlockSpec((rows, GROUP), lambda j: (0, j))
    full = jax.ShapeDtypeStruct((rows, width), low)
    linked = shards is not None
    anywhere = pl.BlockSpec(memory_space=pl.ANY)
    links = {"collective_id": collective, "has_side_effects": True} if linked else {}
    gathered = []
    if linked:
        gathered = [jax.ShapeDtypeStruct((dp_count * shards.shape[1], shards.shape[2]), low)]
    return pl.pallas_call(
        functools.partial(attention_forward_kernel, dp_count if linked else 0),
        grid=(groups,),
        out_shape=[full] * 5
        + [
            jax.ShapeDtypeStruct((rows, width), jnp.float32),
            full,
            jax.ShapeDtypeStruct((rows, 128), jnp.float32),
        ]
        + gathered,
        in_specs=[
            whole((rows, width)),
            column(0),
            column(groups),
            column(2 * groups),
            pl.BlockSpec((GROUP, width), lambda j: (j, 3)),
            pl.BlockSpec((width, 256), lambda j: (0, 12)),
            whole((1, rows)),
            whole((rows, 128)),
            whole((rows, 128)),
            whole((rows, 128)),
        ]
        + [anywhere] * linked,
        out_specs=[whole((rows, width))]
        + [out_column] * 4
        + [whole((rows, width)), whole((rows, width)), whole((rows, 128))]
        + [anywhere] * linked,
        scratch_shapes=[pltpu.VMEM((rows, width), jnp.float32)]
        + (gather_semaphores(dp_count) if linked else []),
        compiler_params=pltpu.CompilerParams(
            dimension_semantics=("arbitrary",), vmem_limit_bytes=56 * 2**20, **links
        ),
        cost_estimate=pl.CostEstimate(
            flops=2 * rows * width * 4 * width + 8 * rows * rows * width // 2,
            bytes_accessed=24 * rows * width,
            transcendentals=rows * rows * HEADS // 2,
        ),
        name="attention_forward",
    )(
        tokens, packed, packed, packed, packed, packed, docs_row, cosine, sine, table,
        *([shards] if linked else []),
    )


def attention_backward_kernel(count, *refs):
    (
        grad_middle_ref, q_ref, k_ref, v_ref, attended_ref, normed_ref, tokens_ref,
        wq_ref, wk_ref, wv_ref, wo_ref, small_ref, docs_row_ref, table_ref,
        cosine_ref, sine_ref, small_grad_ref,
    ) = refs[:17]
    sources, refs = refs[17 : 17 + count], refs[17 + count :]
    token_grad_ref, gq_ref, gk_ref, gv_ref, go_ref, small_out_ref = refs[:6]
    totals, refs = refs[6 : 6 + count], refs[6 + count :]
    branch_ref, back_ref, turned_ref, key_acc, value_acc, query_acc = refs[:6]
    step = pl.program_id(0)
    rows, width = tokens_ref.shape
    if count:
        line = line_reduce(sources[0], totals[0], refs[6:], 2)

        @pl.when(step == 0)
        def _():
            greet(line.peers())
            line.each_plane(line.start)

        pl.when(step == 1)(lambda: line.turns([0], []))
        pl.when(step == 2)(lambda: line.turns([1], [0]))

    @pl.when(step == 0)
    def _():
        branch_ref[...] = grad_middle_ref[...].astype(jnp.bfloat16)
        back_ref[...] = jnp.zeros_like(back_ref)

    grad_branch = branch_ref[...]
    grad_attended = nt(grad_branch, wo_ref[...]).astype(jnp.bfloat16)
    go_ref[...] = tn(attended_ref[...], grad_branch).astype(jnp.bfloat16)
    cosine, sine = cosine_ref[...], sine_ref[...]
    docs_row, docs_column = docs_row_ref[...], table_ref[:, 18:19].astype(jnp.int32)
    for pair in range(2):
        lanes = slice(pair * 128, pair * 128 + 128)
        key_acc[...] = jnp.zeros_like(key_acc)
        value_acc[...] = jnp.zeros_like(value_acc)
        for i in range(rows // BLOCK):
            low, high = key_span(i)
            here = slice(i * BLOCK, (i + 1) * BLOCK)
            allowed = mask_of(docs_column, docs_row, i)
            queries = q_ref[here, lanes] * jnp.asarray(0.125, jnp.bfloat16)
            grads = grad_attended[here, lanes]
            keys, values = k_ref[low:high, lanes], v_ref[low:high, lanes]
            left = lane_ids(queries.shape) < 64
            query_grads = []
            key_grad, value_grad = None, None
            for head in range(2):
                own = left if head == 0 else jnp.logical_not(left)
                own_queries = jnp.where(own, queries, jnp.zeros_like(queries))
                own_grads = jnp.where(own, grads, jnp.zeros_like(grads))
                scores = jnp.where(allowed, nt(keys, own_queries), -1e30)
                shifted = jnp.exp(scores - jnp.max(scores, 0, keepdims=True))
                probs = shifted * (1.0 / jnp.sum(shifted, 0, keepdims=True))
                grad_probs = nt(values, own_grads)
                inner = jnp.sum(probs * grad_probs, 0, keepdims=True)
                grad_scores = (probs * (grad_probs - inner)).astype(jnp.bfloat16)
                part_value = nn(probs.astype(jnp.bfloat16), own_grads)
                part_key = nn(grad_scores, own_queries)
                value_grad = part_value if head == 0 else value_grad + part_value
                key_grad = part_key if head == 0 else key_grad + part_key
                query_grads.append(tn(grad_scores, keys))
            value_acc[low:high, :] += value_grad
            key_acc[low:high, :] += key_grad
            query_acc[here, :] = jnp.where(left, query_grads[0], query_grads[1]) * 0.125
        turned_ref[0, :, lanes] = turn(query_acc[...], cosine, -sine).astype(jnp.bfloat16)
        turned_ref[1, :, lanes] = turn(key_acc[...], cosine, -sine).astype(jnp.bfloat16)
        turned_ref[2, :, lanes] = value_acc[...].astype(jnp.bfloat16)
    normed = normed_ref[...]
    for at, (w_ref, out_ref) in enumerate(((wq_ref, gq_ref), (wk_ref, gk_ref), (wv_ref, gv_ref))):
        turned = turned_ref[at]
        out_ref[...] = tn(normed, turned).astype(jnp.bfloat16)
        back_ref[...] += nt(turned, w_ref[...])

    @pl.when(step == pl.num_programs(0) - 1)
    def _():
        gains = jnp.transpose(small_ref[:, :128].astype(jnp.float32))[18:19, :]
        inputs = tokens_ref[...].astype(jnp.float32)
        grads = back_ref[...]
        scale = lax.rsqrt(jnp.mean(inputs * inputs, -1, keepdims=True) + epsilon)
        weighted = grads * gains
        mean = jnp.mean(weighted * inputs, -1, keepdims=True)
        grad_inputs = scale * weighted - inputs * (scale * scale * scale * mean)
        token_grad_ref[...] = (grad_inputs + grad_middle_ref[...]).astype(jnp.bfloat16)
        gain_grad = jnp.sum(grads * inputs * scale, 0, keepdims=True)
        column = jnp.transpose(jnp.broadcast_to(gain_grad, (128, width)))
        small_grad = small_grad_ref[...]
        small_grad = jnp.where(lane_ids(small_grad.shape) == 18, column, small_grad)
        small_out_ref[...] = small_grad.astype(jnp.bfloat16)
        if count:
            line.turns([2, 3], [1, 2, 3])
            line.each_plane(line.finish)


def attention_backward(
    grad_middle, queries, keys, values, attended, normed, tokens, packed, docs_row, table,
    cosine, sine, small_grad, sources=(), collective=None,
):
    rows, width = tokens.shape
    groups = width // GROUP
    low = jnp.bfloat16
    whole = lambda shape: pl.BlockSpec(shape, lambda j: (0, 0))
    column = lambda at: pl.BlockSpec((width, GROUP), lambda j: (0, at + j))
    by_group = pl.BlockSpec((rows, GROUP), lambda j: (0, j))
    weight = jax.ShapeDtypeStruct((width, width), low)
    linked = len(sources) > 0
    links = {"collective_id": collective, "has_side_effects": True} if linked else {}
    sums = []
    for source in sources:
        sums.append((source.shape[-2] // 8, source.shape[0] * source.shape[-1]))
    once = lambda shape: pl.BlockSpec(
        shape, lambda j: (0, 0), pipeline_mode=pl.Buffered(1)
    )
    return pl.pallas_call(
        functools.partial(attention_backward_kernel, len(sources)),
        grid=(groups,),
        out_shape=[jax.ShapeDtypeStruct((rows, width), low)]
        + [weight] * 4
        + [jax.ShapeDtypeStruct((width, 128), low)]
        + [jax.ShapeDtypeStruct(shape, jnp.float32) for shape in sums],
        in_specs=[
            once((rows, width)),
            by_group,
            by_group,
            by_group,
            by_group,
            once((rows, width)),
            once((rows, width)),
            column(0),
            column(groups),
            column(2 * groups),
            pl.BlockSpec((GROUP, width), lambda j: (j, 3)),
            pl.BlockSpec((width, 256), lambda j: (0, 12)),
            once((1, rows)),
            once((rows, 128)),
            once((rows, 128)),
            once((rows, 128)),
            once((width, 128)),
        ]
        + [pl.BlockSpec(memory_space=pl.ANY)] * len(sources),
        out_specs=[
            whole((rows, width)),
            column(0),
            column(0),
            column(0),
            pl.BlockSpec((GROUP, width), lambda j: (j, 0)),
            whole((width, 128)),
        ]
        + [whole(shape) for shape in sums],
        scratch_shapes=[
            pltpu.VMEM((rows, width), low),
            pltpu.VMEM((rows, width), jnp.float32),
            pltpu.VMEM((3, rows, GROUP), low),
            pltpu.VMEM((rows, 128), jnp.float32),
            pltpu.VMEM((rows, 128), jnp.float32),
            pltpu.VMEM((rows, 128), jnp.float32),
        ]
        + (reduce_scratch(sources[0], 2) if linked else []),
        compiler_params=pltpu.CompilerParams(
            dimension_semantics=("arbitrary",), vmem_limit_bytes=61 * 2**20, **links
        ),
        cost_estimate=pl.CostEstimate(
            flops=4 * rows * width * 4 * width + 20 * rows * rows * width // 2,
            bytes_accessed=32 * rows * width,
            transcendentals=rows * rows * HEADS // 2,
        ),
        name="attention_backward",
    )(
        grad_middle, queries, keys, values, attended, normed, tokens, packed, packed, packed,
        packed, packed, docs_row, table, cosine, sine, small_grad, *sources,
    )


def routing_kernel(expert_count, table_ref, columns_ref, rows_ref):
    rows = table_ref.shape[0]
    lanes = lane_ids((rows, 128))
    routes = [table_ref[:, 16 + s : 17 + s].astype(jnp.int32) for s in range(2)]
    first = (lanes == routes[0]).astype(jnp.float32)
    second = (lanes == routes[1]).astype(jnp.float32)
    down = lax.broadcasted_iota(jnp.int32, (rows, rows), 0)
    lower = (down > lane_ids((rows, rows))).astype(jnp.bfloat16)
    before_first = nn(lower, first.astype(jnp.bfloat16))
    before_second = nn(lower, second.astype(jnp.bfloat16)) + jnp.sum(first, 0, keepdims=True)
    spots = []
    for picked, before, at in ((first, before_first, 0), (second, before_second, 1)):
        rank = jnp.sum(picked * before, -1, keepdims=True)
        route = routes[at]
        spot = route.astype(jnp.float32) * CAP + rank
        spots.append(jnp.where(route < expert_count, spot, jnp.full_like(spot, 2.0 * expert_count * CAP)))
    both = jnp.where(lanes == 0, spots[0], jnp.where(lanes == 1, spots[1], 0.0))
    columns_ref[...] = both.astype(jnp.int32)
    rows_ref[...] = jnp.transpose(both)[0:8, :].astype(jnp.int32)


def routing(table, expert_count):
    rows = table.shape[0]
    return pl.pallas_call(
        functools.partial(routing_kernel, expert_count),
        out_shape=[
            jax.ShapeDtypeStruct((rows, 128), jnp.int32),
            jax.ShapeDtypeStruct((8, rows), jnp.int32),
        ],
        compiler_params=pltpu.CompilerParams(vmem_limit_bytes=40 * 2**20),
        name="routing",
    )(table)


def dispatch_kernel(local_count, spots_ref, aux_ref, normed_ref, cot_ref, rows_ref, grads_ref, gates_ref):
    step = pl.program_id(0)

    @pl.when(step == 0)
    def _():
        gates_ref[...] = jnp.transpose(aux_ref[...])[0:8, :]

    owners, width = rows_ref.shape[0], rows_ref.shape[2]
    shape = (owners * CAP, normed_ref.shape[0])
    place_in = lax.broadcasted_iota(jnp.int32, shape, 0)
    first_owner = step // local_count * owners
    slots = (first_owner + place_in // CAP) * (local_count * CAP)
    slots = slots + step % local_count * CAP + place_in % CAP
    first, second = slots == spots_ref[0:1, :], slots == spots_ref[1:2, :]
    gates = jnp.sum(
        jnp.where(first, gates_ref[0:1, :], jnp.where(second, gates_ref[1:2, :], 0.0)), -1, keepdims=True
    )
    chosen = jnp.where(first | second, 1.0, 0.0).astype(jnp.bfloat16)
    rows_ref[...] = nn(chosen, normed_ref[...]).astype(jnp.bfloat16).reshape(owners, CAP, width)
    grads_ref[...] = (
        (nn(chosen, cot_ref[...]) * gates).astype(jnp.bfloat16).reshape(owners, CAP, width)
    )


def dispatch(spots, aux, normed, cot, owner_count, local_count):
    rows, width = normed.shape
    slot_count = owner_count * local_count * CAP
    whole = lambda shape: pl.BlockSpec(shape, lambda j: (0, 0))
    block = pl.BlockSpec(
        (None, 2, CAP, width), lambda j: (j % local_count, j // local_count, 0, 0)
    )
    return pl.pallas_call(
        functools.partial(dispatch_kernel, local_count),
        grid=(slot_count // CAP // 2,),
        out_shape=[jax.ShapeDtypeStruct((local_count, owner_count, CAP, width), jnp.bfloat16)] * 2,
        in_specs=[whole((8, rows)), whole((rows, 128)), whole((rows, width)), whole((rows, width))],
        out_specs=[block, block],
        scratch_shapes=[pltpu.VMEM((8, rows), jnp.float32)],
        compiler_params=pltpu.CompilerParams(
            dimension_semantics=("arbitrary",), vmem_limit_bytes=60 * 2**20
        ),
        cost_estimate=pl.CostEstimate(
            flops=4 * slot_count * rows * width,
            bytes_accessed=4 * (rows + slot_count) * width,
            transcendentals=0,
        ),
        name="dispatch",
    )(spots, aux, normed, cot)


def halves(values):
    high = values.astype(jnp.bfloat16)
    return high, (values - high.astype(jnp.float32)).astype(jnp.bfloat16)


def combine_kernel(
    expert_count, local_count, linked, *refs
):
    parts, refs = refs[:local_count], refs[local_count:]
    spots_ref, table_ref, aux_ref, normed_ref, middle_ref, cot_ref, small_ref = refs[:7]
    refs = refs[7:]
    if linked:
        source_ref, refs = refs[0], refs[1:]
    output_ref, logit_ref, grad_middle_ref, small_out_ref = refs[:4]
    refs = refs[4:]
    if linked:
        total_ref, refs = refs[0], refs[1:]
    vectors_ref, small_grad_ref = refs[:2]
    step = pl.program_id(0)
    if linked:
        line = line_reduce(source_ref, total_ref, refs[2:], 2, (0,))

        @pl.when(step == 0)
        def _():
            greet(line.peers())
            line.each_plane(line.start)

        pl.when(step == 1)(lambda: line.turns([0], []))

    @pl.when(step == 0)
    def _():
        vectors_ref[0:8, :] = jnp.transpose(small_ref[:, :128].astype(jnp.float32))[16:24, :]
        vectors_ref[8:16, :] = jnp.zeros((8, vectors_ref.shape[1]), jnp.float32)
        small_grad_ref[...] = jnp.zeros_like(small_grad_ref)

    rows, width = normed_ref.shape
    normed_low, cot_low = normed_ref[...], cot_ref[...]
    normed, cot = normed_low.astype(jnp.float32), cot_low.astype(jnp.float32)
    total = lambda values: jnp.sum(values, -1, keepdims=True)
    picks, back = [0.0, 0.0], 0.0
    for e in range(local_count):
        count = parts[e].shape[0] * CAP
        slots = lane_ids((rows, count))
        slots = slots // CAP * (local_count * CAP) + e * CAP + slots % CAP
        hits = [slots == spots_ref[:, s : s + 1] for s in range(2)]
        chosen = [jnp.where(hit, 1.0, 0.0).astype(jnp.bfloat16) for hit in hits]
        returned = parts[e][:, 0].reshape(count, width)
        for s in range(2):
            picks[s] = picks[s] + nn(chosen[s], returned)
        back = back + nn(chosen[0] + chosen[1], parts[e][:, 1].reshape(count, width))
    inner = [total(pick * cot) for pick in picks]
    gates = [aux_ref[:, s : s + 1] for s in range(2)]
    routes = [table_ref[:, 16 + s : 17 + s].astype(jnp.int32) for s in range(2)]
    dot_copy = total(cot * normed)

    def weight_of(route):
        return sum(jnp.where(routes[s] == route, gates[s], 0.0) for s in range(2))

    copy_weight = weight_of(expert_count + 1)
    mix = gates[0] * picks[0] + gates[1] * picks[1]
    pass_weight = copy_weight
    gate_grads = [
        inner[s] + jnp.where(routes[s] == expert_count + 1, dot_copy, 0.0) for s in range(2)
    ]
    lanes = lane_ids((rows, 128))
    spread = jnp.zeros((rows, 128), jnp.float32)
    for k in range(2):
        vector = vectors_ref[k : k + 1, :]
        keep, blend = aux_ref[:, 2 + 2 * k : 3 + 2 * k], aux_ref[:, 3 + 2 * k : 4 + 2 * k]
        weight = weight_of(expert_count + 2 + k)
        dot_vector = total(cot * vector)
        pass_weight = pass_weight + weight * keep
        mix = mix + (weight * blend) * vector
        value = keep * dot_copy + blend * dot_vector
        for s in range(2):
            gate_grads[s] = gate_grads[s] + jnp.where(routes[s] == expert_count + 2 + k, value, 0.0)
        term = keep * blend * (weight * dot_copy - weight * dot_vector)
        spread = jnp.where(lanes == 12 + 2 * k, term, spread)
        spread = jnp.where(lanes == 13 + 2 * k, -term, spread)
        spread = jnp.where(lanes == 16 + k, weight * blend, spread)
    mix = mix + pass_weight * normed
    middle, scale = middle_ref[...], aux_ref[:, 6:7]
    output_ref[...] = (middle + mix).astype(jnp.bfloat16)
    mean = gates[0] * gate_grads[0] + gates[1] * gate_grads[1]
    for s in range(2):
        spread = jnp.where(lanes == routes[s], gates[s] * (gate_grads[s] - mean), spread)
    logit_ref[...] = spread[:, : logit_ref.shape[1]].astype(jnp.bfloat16)
    logits = jnp.where(lanes < 16, spread, 0.0)
    high, low = halves(logits)
    small = small_ref[:, :128]
    vector_high, vector_low = halves(spread - logits)
    small_grad_ref[...] += (
        tn(normed_low, high) + tn(normed_low, low) + tn(cot_low, vector_high) + tn(cot_low, vector_low)
    )
    grads = back + pass_weight * cot + nt(high, small) + nt(low, small)
    vectors_ref[8:9, :] += jnp.sum(grads * middle * scale, 0, keepdims=True)
    weighted = grads * vectors_ref[3:4, :]
    mean = jnp.mean(weighted * middle, -1, keepdims=True)
    grad_middle_ref[...] = cot + scale * weighted - middle * (scale * scale * scale * mean)

    @pl.when(step == pl.num_programs(0) - 1)
    def _():
        column = jnp.transpose(jnp.broadcast_to(vectors_ref[8:9, :], (128, width)))
        small_grad = small_grad_ref[...]
        small_out_ref[...] = jnp.where(lane_ids(small_grad.shape) == 19, column, small_grad)
        if linked:
            line.turns([1, 2, 3], [0, 1, 2, 3])
            line.each_plane(line.finish)


def combine(
    parts, spots, table, aux, normed, middle, cot, packed, choice_count, expert_count, source=None,
    collective=None,
):
    rows, width = normed.shape
    local_count = len(parts)
    slot_count = expert_count * CAP
    size = 256
    linked = source is not None
    links = {"collective_id": collective, "has_side_effects": True} if linked else {}
    block = lambda columns: pl.BlockSpec((size, columns), lambda j: (j, 0))
    whole = lambda shape: pl.BlockSpec(shape, lambda j: (0,) * len(shape))
    return pl.pallas_call(
        functools.partial(combine_kernel, expert_count, local_count, linked),
        grid=(rows // size,),
        out_shape=[
            jax.ShapeDtypeStruct((rows, width), jnp.bfloat16),
            jax.ShapeDtypeStruct((rows, choice_count), jnp.bfloat16),
            jax.ShapeDtypeStruct((rows, width), jnp.float32),
            jax.ShapeDtypeStruct((width, 128), jnp.float32),
        ]
        + ([jax.ShapeDtypeStruct((width // 8, source.shape[2]), jnp.float32)] if linked else []),
        in_specs=[whole(part.shape) for part in parts]
        + [
            block(128),
            block(128),
            block(128),
            block(width),
            block(width),
            block(width),
            pl.BlockSpec((width, 256), lambda j: (0, 12)),
        ]
        + [pl.BlockSpec(memory_space=pl.ANY)] * linked,
        out_specs=[block(width), block(choice_count), block(width), whole((width, 128))]
        + ([whole((width // 8, source.shape[2]))] if linked else []),
        scratch_shapes=[pltpu.VMEM((16, width), jnp.float32), pltpu.VMEM((width, 128), jnp.float32)]
        + (reduce_scratch(source, 2, (0,)) if linked else []),
        compiler_params=pltpu.CompilerParams(
            dimension_semantics=("arbitrary",), vmem_limit_bytes=58 * 2**20, **links
        ),
        cost_estimate=pl.CostEstimate(
            flops=6 * slot_count * rows * width,
            bytes_accessed=14 * rows * width + 4 * slot_count * width,
            transcendentals=0,
        ),
        name="combine",
    )(*parts, spots, table, aux, normed, middle, cot, packed, *([source] if linked else []))


def experts_kernel(mode, dp_count, *refs):
    rows_ref, grads_ref, w_gate_ref, w_up_ref, w_down_ref = refs[:5]
    if mode == 0:
        grad_gu_ref, grad_down_ref, both_ref, turned_ref, out_ref, back_ref = refs[5:]
    if mode == 1:
        next_rows, next_grads, shards_ref, grad_gu_ref, grad_down_ref, both_ref = refs[5:11]
        rows_out, grads_out, full_ref, turned_ref, out_ref, back_ref = refs[11:17]
        sems = refs[17:]
    if mode == 2:
        before_ref, source_ref, grad_gu_ref, grad_down_ref, first_in, second_in, total_ref = refs[5:12]
        turned_ref, out_ref, back_ref, both_ref = refs[12:16]
        sems = refs[16:]
    step = pl.program_id(0)
    width = rows_ref.shape[-1]
    rows = rows_ref[...].reshape(-1, width)
    grads = grads_ref[...].reshape(-1, width)
    if mode == 1:
        half = full_ref.shape[1] // 2
        lines = []
        for n in range(2):
            columns = slice(n * half, n * half + half)
            lines.append(
                LineGather(
                    shards_ref.at[1, :, columns], full_ref, dp_count, *sems[3 * n : 3 * n + 3], columns
                )
            )
        trades = [
            Trade(next_rows.at[1], rows_out, *sems[6:8]),
            Trade(next_grads.at[1], grads_out, *sems[8:10]),
        ]

        @pl.when(step == 0)
        def _():
            greet(lines[0].peers() + trades[0].peers())
            for part in lines + trades:
                part.start()

        for hop in range(1, 4):

            @pl.when(step == hop)
            def _(hop=hop):
                for part in lines:
                    part.relay(hop)

    if mode == 2:
        trades = [Trade(before_ref, first_in, *sems[:2]), Trade(both_ref, second_in, *sems[2:4])]
        line = line_reduce(source_ref, total_ref, sems[4:], 2)

        @pl.when(step == 0)
        def _():
            greet(line.peers() + trades[0].peers())
            line.each_plane(line.start)
            trades[0].start()

        pl.when(step == 2)(lambda: line.turns([0], []))
        pl.when(step == 3)(lambda: line.turns([], [0]))

    @pl.when(step == 0)
    def _():
        turned_ref[...] = jnp.transpose(rows)
        out_ref[...] = jnp.zeros_like(out_ref)
        back_ref[...] = jnp.zeros_like(back_ref)

    w_gate, w_up, w_down = w_gate_ref[...], w_up_ref[...], w_down_ref[...]
    gate, up = nn(rows, w_gate), nn(rows, w_up)
    squashed = 1.0 / (1.0 + jnp.exp(-gate))
    silu = gate * squashed
    activated = (silu * up).astype(jnp.bfloat16)
    grad_act = nt(grads, w_down)
    grad_gate = (grad_act * up * (squashed * (1.0 + gate * (1.0 - squashed)))).astype(jnp.bfloat16)
    grad_up = (grad_act * silu).astype(jnp.bfloat16)
    out_ref[...] += nn(activated, w_down)
    grad_down_ref[...] = tn(activated, grads).astype(jnp.bfloat16)
    back_ref[...] += nt(grad_gate, w_gate) + nt(grad_up, w_up)
    grad_gu_ref[0] = nn(turned_ref[...], grad_gate).astype(jnp.bfloat16)
    grad_gu_ref[1] = nn(turned_ref[...], grad_up).astype(jnp.bfloat16)

    @pl.when(step == pl.num_programs(0) - 1)
    def _():
        shape = (both_ref.shape[0],) + both_ref.shape[2:]
        both_ref[:, 0] = out_ref[...].astype(jnp.bfloat16).reshape(shape)
        both_ref[:, 1] = back_ref[...].astype(jnp.bfloat16).reshape(shape)
        if mode == 1:
            for part in lines + trades:
                part.finish()
        if mode == 2:
            trades[1].start()
            line.turns([1, 2, 3], [1, 2, 3])
            line.each_plane(line.finish)
            for trade in trades:
                trade.finish()


def experts(rows, grads, gate, up, down, mode=0, dp_count=0, extras=(), collective=None):
    owners, cap, width = rows.shape
    hidden = down.shape[0]
    count = owners * cap
    block = FF_BLOCK if count <= 1024 else FF_BLOCK // 4
    steps = hidden // block
    low = jnp.bfloat16
    pairs = pl.BlockSpec((owners, cap, width), lambda j: (0, 0, 0), pipeline_mode=pl.Buffered(1))
    anywhere = pl.BlockSpec(memory_space=pl.ANY)
    both = jax.ShapeDtypeStruct((owners, 2, cap, width), low)
    links = {"collective_id": collective, "has_side_effects": True} if mode else {}
    out_shape = [
        jax.ShapeDtypeStruct((2, width, hidden), low),
        jax.ShapeDtypeStruct((hidden, width), low),
    ]
    out_specs = [
        pl.BlockSpec((2, width, block), lambda j: (0, 0, j)),
        pl.BlockSpec((block, width), lambda j: (j, 0)),
    ]
    scratch = [
        pltpu.VMEM((width, count), low),
        pltpu.VMEM((count, width), jnp.float32),
        pltpu.VMEM((count, width), jnp.float32),
    ]
    if mode < 2:
        out_shape.append(both)
        out_specs.append(pl.BlockSpec(both.shape, lambda j: (0, 0, 0, 0)))
    if mode == 1:
        shards = extras[2]
        out_shape += [jax.ShapeDtypeStruct(rows.shape, low)] * 2
        out_shape.append(jax.ShapeDtypeStruct((dp_count * shards.shape[1], shards.shape[2]), low))
        out_specs += [anywhere] * 3
        scratch += gather_semaphores(dp_count) * 2 + trade_semaphores(owners) + trade_semaphores(owners)
    if mode == 2:
        total = (width // 8, 2 * hidden)
        out_shape += [both, both, jax.ShapeDtypeStruct(total, jnp.float32)]
        out_specs += [anywhere] * 2 + [pl.BlockSpec(total, lambda j: (0, 0))]
        scratch.append(pltpu.VMEM(both.shape, low))
        scratch += trade_semaphores(owners) + trade_semaphores(owners) + reduce_scratch(extras[1], 2)
    return pl.pallas_call(
        functools.partial(experts_kernel, mode, dp_count),
        grid=(steps,),
        out_shape=out_shape,
        in_specs=[
            pairs,
            pairs,
            pl.BlockSpec((width, block), lambda j: (0, j)),
            pl.BlockSpec((width, block), lambda j: (0, up.shape[1] // block - steps + j)),
            pl.BlockSpec((block, width), lambda j: (j, 0)),
        ]
        + [anywhere] * len(extras),
        out_specs=out_specs,
        scratch_shapes=scratch,
        compiler_params=pltpu.CompilerParams(
            dimension_semantics=("arbitrary",), vmem_limit_bytes=60 * 2**20, **links
        ),
        cost_estimate=pl.CostEstimate(
            flops=18 * count * width * hidden,
            bytes_accessed=12 * width * hidden + 8 * count * width,
            transcendentals=count * hidden,
        ),
        name="experts",
    )(rows, grads, gate, up, down, *extras)


def dp_grid(dp_count):
    outer = 4 if dp_count % 4 == 0 else 1
    return outer, dp_count // outer


def place():
    me, mine = lax.axis_index("dp"), lax.axis_index("expert")
    return me, mine


def greet(peers):
    barrier = pltpu.get_barrier_semaphore()
    for peer in peers:
        pl.semaphore_signal(barrier, inc=1, device_id=peer, device_id_type=MESH)
    pl.semaphore_wait(barrier, len(peers))


class LineGather:
    def __init__(self, shard, full, dp_count, send_sem, recv_sem, own_sem, columns=None, also=None):
        self.columns = slice(None) if columns is None else columns
        self.also = also or (lambda chunk: None)
        self.shard, self.full, self.dp_count = shard, full, dp_count
        self.send_sem, self.recv_sem, self.own_sem = send_sem, recv_sem, own_sem
        self.outer_count, self.inner_count = dp_grid(dp_count)
        self.me, self.mine = place()
        self.outer, self.inner = self.me // self.inner_count, self.me % self.inner_count
        self.inner_peers = [
            lax.rem(self.inner + k, self.inner_count) for k in range(1, self.inner_count)
        ]
        self.can_up, self.can_down = self.outer < self.outer_count - 1, self.outer > 0

    def peers(self):
        below = lax.rem(self.outer + self.outer_count - 1, self.outer_count)
        above = lax.rem(self.outer + 1, self.outer_count)
        return [(peer * self.inner_count + self.inner, self.mine) for peer in (below, above)] + [
            (self.outer * self.inner_count + peer, self.mine) for peer in self.inner_peers
        ]

    def spot(self, chunk):
        rows = self.shard.shape[0]
        return self.full.at[pl.ds(pl.multiple_of(chunk * rows, 8), rows), self.columns]

    def copy(self, source, chunk, device, way, at):
        return pltpu.make_async_remote_copy(
            src_ref=source,
            dst_ref=self.spot(chunk),
            send_sem=self.send_sem.at[way, at, chunk],
            recv_sem=self.recv_sem.at[chunk],
            device_id=(device, self.mine),
            device_id_type=MESH,
        )

    def up(self, source, chunk):
        return self.copy(source, chunk, (self.outer + 1) * self.inner_count + self.inner, 1, 0)

    def down(self, source, chunk):
        return self.copy(source, chunk, (self.outer - 1) * self.inner_count + self.inner, 2, 0)

    def across(self, source, chunk):
        return [
            self.copy(source, chunk, self.outer * self.inner_count + peer, 0, at)
            for at, peer in enumerate(self.inner_peers)
        ]

    def keep(self):
        return pltpu.make_async_copy(self.shard, self.spot(self.me), self.own_sem)

    def arrived(self, chunk):
        pltpu.make_async_copy(self.spot(chunk), self.spot(chunk), self.recv_sem.at[chunk]).wait()

    def start(self):
        for copy in self.across(self.shard, self.me):
            copy.start()
        pl.when(self.can_up)(lambda: self.up(self.shard, self.me).start())
        pl.when(self.can_down)(lambda: self.down(self.shard, self.me).start())
        self.keep().start()

    def relay(self, step):
        low, high = self.outer - step, self.outer + step

        def pass_on(source, upward):
            chunk = source * self.inner_count + self.inner
            self.arrived(chunk)
            if upward:
                pl.when(self.can_up)(lambda: self.up(self.spot(chunk), chunk).start())
            else:
                pl.when(self.can_down)(lambda: self.down(self.spot(chunk), chunk).start())
            for copy in self.across(self.spot(chunk), chunk):
                copy.start()
            self.also(chunk)

        pl.when(low >= 0)(lambda: pass_on(low, True))
        pl.when(high < self.outer_count)(lambda: pass_on(high, False))

    def finish(self):
        self.keep().wait()
        for peer in self.inner_peers:
            for k in range(self.outer_count):
                chunk = lax.rem(self.outer + k, self.outer_count) * self.inner_count + peer
                self.arrived(chunk)
                self.also(chunk)
        for plane in range(self.outer_count):
            chunk = plane * self.inner_count + self.inner
            for copy in self.across(self.spot(chunk), chunk):
                copy.wait_send()
            pl.when(self.can_up & (self.outer >= plane))(
                lambda chunk=chunk: self.up(self.spot(chunk), chunk).wait_send()
            )
            pl.when(self.can_down & (self.outer <= plane))(
                lambda chunk=chunk: self.down(self.spot(chunk), chunk).wait_send()
            )


def gather_semaphores(dp_count):
    inner_count = dp_grid(dp_count)[1]
    return [
        pltpu.SemaphoreType.DMA((3, max(1, inner_count - 1), dp_count)),
        pltpu.SemaphoreType.DMA((dp_count,)),
        pltpu.SemaphoreType.DMA,
    ]


def by_rows(count, body):
    def step(i, carry):
        body(i * 16)
        return carry

    lax.fori_loop(0, count // 16, step, 0)


class Trade:
    def __init__(self, source, target, send_sem, recv_sem):
        self.source, self.target, self.send_sem, self.recv_sem = source, target, send_sem, recv_sem
        self.me, self.mine = place()
        count = target.shape[0]
        self.partners = [lax.rem(self.mine + k, count) for k in range(1, count)]

    def peers(self):
        return [(self.me, peer) for peer in self.partners]

    def copy(self, k):
        peer = self.partners[k]
        return pltpu.make_async_remote_copy(
            src_ref=self.source.at[peer],
            dst_ref=self.target.at[self.mine],
            send_sem=self.send_sem.at[k + 1],
            recv_sem=self.recv_sem.at[self.mine],
            device_id=(self.me, peer),
            device_id_type=MESH,
        )

    def keep(self):
        return pltpu.make_async_copy(
            self.source.at[self.mine], self.target.at[self.mine], self.send_sem.at[0]
        )

    def start(self):
        for k in range(len(self.partners)):
            self.copy(k).start()
        self.keep().start()

    def finish(self):
        self.keep().wait()
        for k, peer in enumerate(self.partners):
            there = self.target.at[peer]
            pltpu.make_async_copy(there, there, self.recv_sem.at[peer]).wait()
            self.copy(k).wait_send()


def trade_semaphores(owner_count):
    return [pltpu.SemaphoreType.DMA((owner_count,)), pltpu.SemaphoreType.DMA((owner_count,))]


def expert_gather_kernel(
    dp_count, spots_ref, aux_ref, normed_ref, cot_ref, down_ref, gate_up_ref,
    rows_ref, grads_ref, rows_out, grads_out, full_ref, up_ref, *sems
):
    half = up_ref.shape[1] // 2
    lines = [LineGather(down_ref.at[0], full_ref, dp_count, *sems[:3])]
    for n in range(2):
        columns = slice(n * half, n * half + half)
        shard = gate_up_ref.at[0, :, (2 + n) * half : (3 + n) * half]
        lines.append(LineGather(shard, up_ref, dp_count, *sems[3 * n + 3 : 3 * n + 6], columns))
    trades = [Trade(rows_ref.at[0], rows_out, *sems[9:11]), Trade(grads_ref.at[0], grads_out, *sems[11:13])]
    greet(lines[0].peers() + trades[0].peers())
    for part in lines:
        part.start()
    local_count, owner_count, _, width = rows_ref.shape
    gates = jnp.transpose(aux_ref[...])[0:8, :]
    for e in range(local_count):
        for owner in range(0, owner_count, 2):
            shape = (2 * CAP, normed_ref.shape[0])
            within = lax.broadcasted_iota(jnp.int32, shape, 0)
            slots = (owner + within // CAP) * (local_count * CAP) + e * CAP + within % CAP
            first, second = slots == spots_ref[0:1, :], slots == spots_ref[1:2, :]
            weights = jnp.where(first, gates[0:1, :], jnp.where(second, gates[1:2, :], 0.0))
            chosen = jnp.where(first | second, 1.0, 0.0).astype(jnp.bfloat16)
            picked = nn(chosen, normed_ref[...]).astype(jnp.bfloat16)
            scaled = (nn(chosen, cot_ref[...]) * jnp.sum(weights, -1, keepdims=True)).astype(jnp.bfloat16)
            rows_ref[e, owner : owner + 2] = picked.reshape(2, CAP, width)
            grads_ref[e, owner : owner + 2] = scaled.reshape(2, CAP, width)
        if e == 0:
            for part in trades:
                part.start()
    for hop in range(1, lines[0].outer_count):
        for line in lines:
            line.relay(hop)
    for part in lines + trades:
        part.finish()


def expert_gather(spots, aux, normed, cot, down, gate_up, owner_count, dp_count, collective):
    anywhere, in_vmem = pl.BlockSpec(memory_space=pl.ANY), pl.BlockSpec(memory_space=pltpu.VMEM)
    local_count, width = down.shape[0], down.shape[2]
    send = jax.ShapeDtypeStruct((local_count, owner_count, CAP, width), jnp.bfloat16)
    arrive = jax.ShapeDtypeStruct((owner_count, CAP, width), jnp.bfloat16)
    return pl.pallas_call(
        functools.partial(expert_gather_kernel, dp_count),
        out_shape=[
            send,
            send,
            arrive,
            arrive,
            jax.ShapeDtypeStruct((dp_count * down.shape[1], width), down.dtype),
            jax.ShapeDtypeStruct((dp_count * gate_up.shape[1], gate_up.shape[2] // 2), gate_up.dtype),
        ],
        in_specs=[in_vmem] * 4 + [anywhere] * 2,
        out_specs=[in_vmem] * 2 + [anywhere] * 4,
        scratch_shapes=gather_semaphores(dp_count) * 3 + trade_semaphores(owner_count) * 2,
        compiler_params=pltpu.CompilerParams(
            collective_id=collective, has_side_effects=True, vmem_limit_bytes=60 * 2**20
        ),
        name="expert_gather",
    )(spots, aux, normed, cot, down, gate_up)


def small_gather_kernel(
    dp_count, expert_count, shard_ref, routes_ref, docs_ref, resid_ref,
    full_ref, columns_ref, rows_ref, table_ref, pass_sem, mate_sem, all_sem, stack_ref, *sems,
):
    me, mine = place()
    rows, columns = shard_ref.shape
    half = columns // 2
    side = mine % 2
    mate = mine + 1 - 2 * side
    mate_columns = pl.ds(pl.multiple_of((1 - side) * half, 128), half)
    first = half // 256 * 128
    spans = [(0, first), (first, half - first)]

    def there(chunk, lanes):
        return full_ref.at[pl.ds(pl.multiple_of(chunk * rows, 8), rows), lanes]

    def columns_at(n, of):
        start, size = spans[n]
        return pl.ds(pl.multiple_of(of * half + start, 128), size)

    def pass_copy(n, chunk):
        here = there(chunk, columns_at(n, side))
        return pltpu.make_async_remote_copy(
            src_ref=here,
            dst_ref=here,
            send_sem=pass_sem.at[n, chunk],
            recv_sem=mate_sem.at[n, chunk],
            device_id=(me, mate),
            device_id_type=MESH,
        )

    lines = []
    for n in range(2):
        lines.append(
            LineGather(
                shard_ref.at[:, columns_at(n, side)], full_ref, dp_count, *sems[3 * n : 3 * n + 3],
                columns_at(n, side), lambda chunk, n=n: pass_copy(n, chunk).start(),
            )
        )
    greet(lines[0].peers() + [(me, mate)])
    for line in lines:
        line.start()
    other = pltpu.make_async_copy(shard_ref.at[:, mate_columns], there(me, mate_columns), all_sem)
    other.start()
    stack_ref[...] = jnp.zeros_like(stack_ref)
    stack_ref[0 : resid_ref.shape[0], :] = resid_ref[...].astype(jnp.float32)
    stack_ref[16:18, :] = routes_ref[...].astype(jnp.float32)
    stack_ref[18:19, :] = docs_ref[...].astype(jnp.float32)
    table_ref[...] = jnp.transpose(stack_ref[...])
    routing_kernel(expert_count, table_ref, columns_ref, rows_ref)
    for hop in range(1, lines[0].outer_count):
        for line in lines:
            line.relay(hop)
    for line in lines:
        line.finish()
    other.wait()
    for k in range(1, dp_count):
        chunk = lax.rem(me + k, dp_count)
        for n in range(2):
            target = there(chunk, columns_at(n, 1 - side))
            pltpu.make_async_copy(target, target, mate_sem.at[n, chunk]).wait()
            pass_copy(n, chunk).wait_send()


def small_gather(shard, routes, docs, resid, expert_count, dp_count, collective):
    rows, columns = shard.shape
    tokens = routes.shape[1]
    anywhere, in_vmem = pl.BlockSpec(memory_space=pl.ANY), pl.BlockSpec(memory_space=pltpu.VMEM)
    return pl.pallas_call(
        functools.partial(small_gather_kernel, dp_count, expert_count),
        out_shape=[
            jax.ShapeDtypeStruct((dp_count * rows, columns), shard.dtype),
            jax.ShapeDtypeStruct((tokens, 128), jnp.int32),
            jax.ShapeDtypeStruct((8, tokens), jnp.int32),
            jax.ShapeDtypeStruct((tokens, 128), jnp.float32),
        ],
        in_specs=[anywhere] + [in_vmem] * 3,
        out_specs=[anywhere] + [in_vmem] * 3,
        scratch_shapes=[
            pltpu.SemaphoreType.DMA((2, dp_count)),
            pltpu.SemaphoreType.DMA((2, dp_count)),
            pltpu.SemaphoreType.DMA,
            pltpu.VMEM((128, tokens), jnp.float32),
        ]
        + gather_semaphores(dp_count) * 2,
        compiler_params=pltpu.CompilerParams(
            collective_id=collective, has_side_effects=True, vmem_limit_bytes=60 * 2**20
        ),
        name="small_gather",
    )(shard, routes, docs, resid)


class LineReduce:
    def __init__(self, sources, totals, owns, ins, lows, highs, own_sem, in_send, in_recv, line_send, line_recv):
        self.sources, self.totals = sources, totals
        self.owns, self.ins, self.lows, self.highs = owns, ins, lows, highs
        self.own_sem, self.in_send, self.in_recv = own_sem, in_send, in_recv
        self.line_send, self.line_recv = line_send, line_recv
        self.me, self.mine = place()
        self.outer, self.inner = self.me // 2, self.me % 2
        self.every = range(len(sources))

    def peers(self):
        low, high = lax.rem(self.outer + 3, 4), lax.rem(self.outer + 1, 4)
        return [
            (self.me + 1 - 2 * self.inner, self.mine),
            (low * 2 + self.inner, self.mine),
            (high * 2 + self.inner, self.mine),
        ]

    def order(self, o):
        return sorted(range(4), key=lambda plane: (-abs(plane - o), plane))

    def chunk(self, p, at):
        source = self.sources[p]
        rows = self.owns[p].shape[-2]
        here = pl.ds(pl.multiple_of(at * rows, 16), rows)
        return source.at[:, here, :] if len(source.shape) == 3 else source.at[here, :]

    def own_copy(self, p, plane):
        return pltpu.make_async_copy(
            self.chunk(p, plane * 2 + self.inner), self.owns[p].at[plane], self.own_sem.at[p, plane]
        )

    def in_copy(self, p, plane):
        return pltpu.make_async_remote_copy(
            src_ref=self.chunk(p, plane * 2 + 1 - self.inner),
            dst_ref=self.ins[p].at[plane],
            send_sem=self.in_send.at[p, plane],
            recv_sem=self.in_recv.at[p, plane],
            device_id=(self.me + 1 - 2 * self.inner, self.mine),
            device_id_type=MESH,
        )

    def line_copy(self, p, plane, upward, device_plane):
        target = self.lows[p].at[plane - 1] if upward else self.highs[p].at[plane]
        return pltpu.make_async_remote_copy(
            src_ref=self.ins[p].at[plane],
            dst_ref=target,
            send_sem=self.line_send.at[p, 0 if upward else 1, plane],
            recv_sem=self.line_recv.at[p, 0 if upward else 1, plane],
            device_id=(device_plane * 2 + self.inner, self.mine),
            device_id_type=MESH,
        )

    def start(self, o):
        for plane in self.order(o):
            for p in self.every:
                self.in_copy(p, plane).start()
        for plane in self.order(o):
            for p in self.every:
                self.own_copy(p, plane).start()

    def line_start(self, o, p, plane):
        return self.line_copy(p, plane, plane > o, o + 1 if plane > o else o - 1)

    def pass_on(self, o, k):
        plane = self.order(o)[k]
        for p in self.every:
            self.own_copy(p, plane).wait()
            self.in_copy(p, plane).wait_recv()
            terms = [self.owns[p].at[plane]]
            if o > 0 and plane >= o:
                self.line_copy(p, plane, True, o).wait_recv()
                terms.append(self.lows[p].at[plane - 1])
            if o < 3 and plane <= o:
                self.line_copy(p, plane, False, o).wait_recv()
                terms.append(self.highs[p].at[plane])
            held = self.ins[p].at[plane]
            last = plane == o
            sides = held.shape[0] if len(held.shape) == 3 else 0

            def body(at, p=p, terms=terms, held=held, last=last, sides=sides):
                here = pl.ds(pl.multiple_of(at, 16), 16)
                for side in range(max(1, sides)):
                    spot = (side, here) if sides else (here,)
                    total = held[spot].astype(jnp.float32)
                    for term in terms:
                        total = total + term[spot].astype(jnp.float32)
                    if last:
                        size = total.shape[-1]
                        self.totals[p][here, side * size : (side + 1) * size] = total
                    else:
                        held[spot] = total.astype(held.dtype)

            by_rows(held.shape[-2], body)
            if not last:
                self.line_start(o, p, plane).start()

    def finish(self, o):
        for plane in range(4):
            for p in self.every:
                self.in_copy(p, plane).wait_send()
                if plane != o:
                    self.line_start(o, p, plane).wait_send()

    def each_plane(self, body):
        for o in range(4):
            pl.when(self.outer == o)(functools.partial(body, o))

    def turns(self, ends, middles):
        def body(o):
            for k in ends if o in (0, 3) else middles:
                self.pass_on(o, k)

        self.each_plane(body)


def pieces_of(source, cut, sides=None):
    columns = source.shape[-1]
    size = columns // cut
    fronts = [()]
    if len(source.shape) == 3:
        fronts = [(side,) for side in (range(source.shape[0]) if sides is None else sides)]
    return [
        (front, slice(c * size, c * size + size), slice(n * columns + c * size, n * columns + c * size + size))
        for n, front in enumerate(fronts)
        for c in range(cut)
    ]


def reduce_scratch(source, cut, sides=None):
    rows = source.shape[-2] // 8
    size = source.shape[-1] // cut
    count = len(pieces_of(source, cut, sides))
    shapes = []
    for planes in (4, 4, 3, 3):
        shapes += [pltpu.VMEM((planes, rows, size), jnp.bfloat16)] * count
    return shapes + [
        pltpu.SemaphoreType.DMA((count, 4)),
        pltpu.SemaphoreType.DMA((count, 4)),
        pltpu.SemaphoreType.DMA((count, 4)),
        pltpu.SemaphoreType.DMA((count, 2, 4)),
        pltpu.SemaphoreType.DMA((count, 2, 4)),
    ]


def line_reduce(source, total, scratch, cut, sides=None):
    pieces = pieces_of(source, cut, sides)
    count = len(pieces)
    buffers = [scratch[n * count : (n + 1) * count] for n in range(4)]
    sources = [source.at[front + (slice(None), columns)] for front, columns, _ in pieces]
    totals = [total.at[:, columns] for _, _, columns in pieces]
    return LineReduce(sources, totals, *buffers, *scratch[4 * count :])


def final_reduce_kernel(small_count, *refs):
    small_refs, refs = refs[:small_count], refs[small_count:]
    (
        small_out, swap, small_own, small_in, small_low, small_high, final_low, final_in, own_sem,
        swap_send, swap_recv, in_send, in_recv, line_send, line_recv, last_send, last_recv,
    ) = refs
    outer_count, inner_count = 4, 2
    me, mine = place()
    outer, inner = me // inner_count, me % inner_count
    side = mine % 2
    mate, across = mine + 1 - 2 * side, lax.rem(mine + 2, 4)
    beside = me + 1 - 2 * inner
    half_rows = small_refs[0].shape[1] // 2
    starts = [sum(ref.shape[2] for ref in small_refs[:n]) for n in range(small_count + 1)]

    def remote(source, target, device, send_at, recv_at):
        return pltpu.make_async_remote_copy(
            src_ref=source,
            dst_ref=target,
            send_sem=send_at,
            recv_sem=recv_at,
            device_id=device,
            device_id_type=MESH,
        )

    low_peer = lax.rem(outer + outer_count - 1, outer_count) * inner_count + inner
    high_peer = lax.rem(outer + 1, outer_count) * inner_count + inner
    greet([(me, mate), (me, across), (beside, mine), (low_peer, mine), (high_peer, mine)])

    mate_rows = pl.ds(pl.multiple_of((1 - side) * half_rows, 16), half_rows)
    own_rows = pl.ds(pl.multiple_of(side * half_rows, 16), half_rows)

    middle = starts[-1] // 256 * 128
    spans = [slice(0, middle), slice(middle, starts[-1])]

    def swap_copy(n):
        return remote(
            small_refs[n].at[:, mate_rows, :],
            swap.at[:, :, starts[n] : starts[n + 1]],
            (me, mate),
            swap_send.at[n],
            swap_recv.at[n],
        )

    def own_copy(n):
        return pltpu.make_async_copy(
            small_refs[n].at[:, own_rows, :], small_own.at[:, :, starts[n] : starts[n + 1]], own_sem.at[n]
        )

    def inner_copy(p, plane):
        return remote(
            swap.at[plane * inner_count + 1 - inner, :, spans[p]],
            small_in.at[plane, :, spans[p]],
            (beside, mine),
            in_send.at[p, plane],
            in_recv.at[p, plane],
        )

    def line_copy(p, plane, upward, device_plane):
        way = 0 if upward else 1
        return remote(
            small_in.at[plane, :, spans[p]],
            (small_low if upward else small_high).at[plane, :, spans[p]],
            (device_plane * inner_count + inner, mine),
            line_send.at[p, way, plane],
            line_recv.at[p, way, plane],
        )

    def last_copy(p):
        return remote(
            final_low.at[:, spans[p]], final_in.at[:, spans[p]], (me, across), last_send.at[p], last_recv.at[p]
        )

    def wide(values):
        return values.astype(jnp.float32)

    def add_own(chunk, lanes):
        def body(at):
            here = pl.ds(pl.multiple_of(at, 16), 16)
            swap[chunk, here, lanes] = (
                wide(swap[chunk, here, lanes]) + wide(small_own[chunk, here, lanes])
            ).astype(swap.dtype)

        by_rows(half_rows, body)

    def at_plane(o):
        order = sorted(range(outer_count), key=lambda t: (-abs(t - o), t))

        def line_start(p, plane):
            return line_copy(p, plane, plane > o, o + 1 if plane > o else o - 1)

        for n in range(small_count):
            swap_copy(n).start()
            own_copy(n).start()
        for n in range(small_count):
            swap_copy(n).wait_recv()
            own_copy(n).wait()
        for plane in order:
            for p in range(2):
                add_own(plane * inner_count + 1 - inner, spans[p])
                inner_copy(p, plane).start()
        for plane in order:
            for p in range(2):
                add_own(plane * inner_count + inner, spans[p])
                inner_copy(p, plane).wait_recv()
                terms = [swap.at[plane * inner_count + inner]]
                if o > 0 and plane >= o:
                    line_copy(p, plane, True, o).wait_recv()
                    terms.append(small_low.at[plane])
                if o < outer_count - 1 and plane <= o:
                    line_copy(p, plane, False, o).wait_recv()
                    terms.append(small_high.at[plane])
                target = final_low if plane == o else small_in.at[plane]

                def gather(at, plane=plane, terms=terms, target=target, lanes=spans[p]):
                    here = pl.ds(pl.multiple_of(at, 16), 16)
                    total = wide(small_in[plane, here, lanes])
                    for term in terms:
                        total = total + wide(term[here, lanes])
                    target[here, lanes] = total.astype(target.dtype)

                by_rows(half_rows, gather)
                if plane != o:
                    line_start(p, plane).start()
                else:
                    last_copy(p).start()
        for plane in range(outer_count):
            for p in range(2):
                inner_copy(p, plane).wait_send()
                if plane != o:
                    line_start(p, plane).wait_send()
        for n in range(small_count):
            swap_copy(n).wait_send()

    for o in range(outer_count):
        pl.when(outer == o)(functools.partial(at_plane, o))
    for p in range(2):
        last_copy(p).wait()

    def total_body(at):
        here = pl.ds(pl.multiple_of(at, 16), 16)
        there = pl.ds(pl.multiple_of(side * half_rows + at, 16), 16)
        small_out[there, :] = wide(final_low[here, :]) + wide(final_in[here, :])

    by_rows(half_rows, total_body)
    mate_copy = remote(
        small_out.at[own_rows, :], small_out.at[own_rows, :], (me, mate), last_send.at[2], last_recv.at[2]
    )
    mate_copy.start()
    mate_copy.wait()


def final_reduce(smalls, collective):
    chunk_count, small_rows, _ = smalls[0].shape
    small_columns = sum(small.shape[2] for small in smalls)
    low = jnp.bfloat16
    planes = 4
    in_vmem = pl.BlockSpec(memory_space=pltpu.VMEM)
    half = small_rows // 2
    return pl.pallas_call(
        functools.partial(final_reduce_kernel, len(smalls)),
        out_shape=jax.ShapeDtypeStruct((small_rows, small_columns), jnp.float32),
        in_specs=[pl.BlockSpec(memory_space=pl.ANY)] * len(smalls),
        out_specs=in_vmem,
        scratch_shapes=[pltpu.VMEM((chunk_count, half, small_columns), low)] * 2
        + [pltpu.VMEM((planes, half, small_columns), low)] * 3
        + [pltpu.VMEM((half, small_columns), low)] * 2
        + [
            pltpu.SemaphoreType.DMA((len(smalls),)),
            pltpu.SemaphoreType.DMA((len(smalls),)),
            pltpu.SemaphoreType.DMA((len(smalls),)),
            pltpu.SemaphoreType.DMA((2, planes)),
            pltpu.SemaphoreType.DMA((2, planes)),
            pltpu.SemaphoreType.DMA((2, 2, planes)),
            pltpu.SemaphoreType.DMA((2, 2, planes)),
            pltpu.SemaphoreType.DMA((3,)),
            pltpu.SemaphoreType.DMA((3,)),
        ],
        compiler_params=pltpu.CompilerParams(
            collective_id=collective, has_side_effects=True, vmem_limit_bytes=60 * 2**20
        ),
        name="final_reduce",
    )(*smalls)


def shards(
    tokens,
    resid_logits,
    routes,
    doc_ids,
    w_qkv,
    w_out,
    gain_attn,
    gain_ffn,
    w_router,
    w_const,
    v_const,
    w_gate_up,
    w_down,
    out_grad,
):
    dp_count, owner_count = lax.axis_size("dp"), lax.axis_size("expert")
    own_links = dp_count == 8 and owner_count == 4 and w_gate_up.shape[0] == 2
    seq_count, length, width = tokens.shape
    assert seq_count == 1
    rows = seq_count * length
    choice_count = resid_logits.shape[-1]
    local_count = w_gate_up.shape[0]
    expert_count = owner_count * local_count
    hidden_count = w_down.shape[1] * dp_count
    width_qkv, width_out = w_qkv.shape[1], w_out.shape[1]
    small_parts = [w_router, w_const, v_const, gain_attn[:, None], gain_ffn[:, None]]
    small_width = sum(part.shape[1] for part in small_parts)
    pad = jnp.zeros((w_qkv.shape[0], 256 - small_width), jnp.bfloat16)
    packed = jnp.concatenate([w_qkv, w_out] + small_parts + [pad], 1)
    inputs = tokens.reshape(rows, width)
    cot = out_grad.reshape(rows, width)
    route_rows = routes.reshape(rows, 2)
    cosine, sine = rotary_lanes(length, width // HEADS)
    docs_row = doc_ids.reshape(1, rows)
    resid_rows = resid_logits.reshape(rows, choice_count)
    if own_links:
        packed_full, spots, spot_rows, table = small_gather(
            packed, route_rows.T, docs_row, resid_rows.T, expert_count, dp_count, 1
        )
    else:
        columns = [
            resid_rows, jnp.zeros((rows, 16 - choice_count)), route_rows, docs_row.T, jnp.zeros((rows, 109))
        ]
        table = jnp.concatenate([column.astype(jnp.float32) for column in columns], 1)
        spots, spot_rows = routing(table, expert_count)
        packed_full = lax.all_gather(packed, "dp", axis=0, tiled=True)
    gather = functools.partial(lax.all_gather, axis_name="dp", axis=0, tiled=True)
    if own_links:
        first_gate, second_down, packed_full = lax.optimization_barrier(
            (w_gate_up[0, :, :hidden_count], w_down[1], packed_full)
        )
        first_gate, second_down = gather(first_gate), gather(second_down)
    else:
        first_gate_up = gather(w_gate_up[0])
    normed_one, queries, keys, values, attended, middle, normed_two, aux = attention_forward(
        inputs, packed_full, docs_row, cosine, sine, table
    )
    if own_links:
        send_rows, send_grads, rows_in, grads_in, first_down, first_up = expert_gather(
            spot_rows, aux, normed_two, cot, w_down, w_gate_up, owner_count, dp_count, 2
        )
        grad_gu, grad_down, both, next_rows, next_grads, second_gate_up = experts(
            rows_in, grads_in, first_gate, first_up, first_down, 1, dp_count,
            [send_rows, send_grads, w_gate_up], 6,
        )
        down_parts = [lax.psum_scatter(grad_down, "dp", scatter_dimension=0, tiled=True)]
        second_gu, grad_down, *parts, gu_part = experts(
            next_rows, next_grads, second_gate_up, second_gate_up, second_down, 2, dp_count,
            [both, grad_gu], 4,
        )
        down_parts.append(lax.psum_scatter(grad_down, "dp", scatter_dimension=0, tiled=True))
        gu_parts = [gu_part]
    else:
        send_rows, send_grads = dispatch(spot_rows, aux, normed_two, cot, owner_count, local_count)
        exchange = functools.partial(
            lax.all_to_all, axis_name="expert", split_axis=0, concat_axis=0, tiled=True
        )
        parts, gu_parts, down_parts = [], [], []
        for e in range(local_count):
            gate_up = first_gate_up if e == 0 else gather(w_gate_up[e])
            grad_gu, grad_down, both = experts(
                exchange(send_rows[e]), exchange(send_grads[e]), gate_up, gate_up, gather(w_down[e])
            )
            parts.append(exchange(both))
            gu_part = lax.psum_scatter(grad_gu, "dp", scatter_dimension=1, tiled=True)
            gu_parts.append(jnp.concatenate([gu_part[0], gu_part[1]], -1).astype(jnp.float32))
            down_parts.append(lax.psum_scatter(grad_down, "dp", scatter_dimension=0, tiled=True))
    down_parts = [part.astype(jnp.float32) for part in down_parts]
    output, logit_grad, grad_middle, small_grad = combine(
        parts, spots, table, aux, normed_two, middle, cot, packed_full, choice_count, expert_count
    )
    if own_links:
        grad_middle, down_parts[0] = lax.optimization_barrier((grad_middle, down_parts[0]))
    backward = functools.partial(
        attention_backward, grad_middle, queries, keys, values, attended, normed_one, inputs,
        packed_full, docs_row, table, cosine, sine, small_grad,
    )
    if own_links:
        token_grad, *weight_grads, gu_part = backward([second_gu], 7)
        gu_parts.append(gu_part)
        packed_part = final_reduce(
            [grad.reshape(dp_count, width // dp_count, grad.shape[1]) for grad in weight_grads], 3
        )
    else:
        token_grad, *weight_grads = backward()
        packed_part = lax.psum_scatter(
            jnp.concatenate(weight_grads, 1), "dp", scatter_dimension=0, tiled=True
        )
        packed_part = lax.psum(packed_part, "expert").astype(jnp.float32)
    part_qkv = packed_part[:, :width_qkv]
    part_out = packed_part[:, width_qkv : width_qkv + width_out]
    small_part = packed_part[:, width_qkv + width_out :]
    return (
        output.reshape(tokens.shape),
        token_grad.reshape(tokens.shape),
        logit_grad.reshape(resid_logits.shape),
        part_qkv,
        part_out,
        small_part[:, 18],
        small_part[:, 19],
        small_part[:, 0:12],
        small_part[:, 12:16],
        small_part[:, 16:18],
        jnp.stack(gu_parts),
        jnp.stack(down_parts),
    )


def solution(mesh):
    placed = (
        P(("dp", "expert"), None, None),
        P(("dp", "expert"), None, None),
        P(("dp", "expert"), None, None),
        P(("dp", "expert"), None),
        P("dp", None),
        P("dp", None),
        P("dp"),
        P("dp"),
        P("dp", None),
        P("dp", None),
        P("dp", None),
        P("expert", "dp", None),
        P("expert", "dp", None),
        P(("dp", "expert"), None, None),
    )
    return jax.shard_map(
        shards,
        mesh=mesh,
        in_specs=placed,
        out_specs=(
            P(("dp", "expert"), None, None),
            P(("dp", "expert"), None, None),
            P(("dp", "expert"), None, None),
            P("dp", None),
            P("dp", None),
            P("dp"),
            P("dp"),
            P("dp", None),
            P("dp", None),
            P("dp", None),
            P("expert", "dp", None),
            P("expert", "dp", None),
        ),
        check_vma=False,
    )
```
